32 devices in a mesh: batch: 4 (over z), seq: 8 (over y, x, core).
Axes of the slice: x: 2, y: 2, z: 4, core: 2. Of those that a mesh axis runs over, the one named last changes fastest.
Arguments:
- inputs: bfloat16 [4, 2048, 2048], P('batch', 'seq'), may hold values from -6 to 6
- segment_ids: int32 [4, 2048], P('batch'), may hold values from 0 to 3, never falling along the last dimension, each value on 1 to 1024 neighbouring positions
- w_qkv: bfloat16 [6144, 2048], P('seq'), may hold values from -0.125 to 0.125
- w_out: bfloat16 [2048, 2048], P('seq'), may hold values from -0.125 to 0.125
- w_up: bfloat16 [8192, 2048], P('seq'), may hold values from -0.125 to 0.125
- w_down: bfloat16 [2048, 8192], P('seq'), may hold values from -0.0625 to 0.0625
- gain_attn: float32 [2048], replicated, may hold values from 0.5 to 1.5
- gain_mix: float32 [2048], replicated, may hold values from 0.5 to 1.5
- gain_ffn: float32 [2048], replicated, may hold values from 0.5 to 1.5
- gain_hidden: float32 [8192], replicated, may hold values from 0.5 to 1.5
- cotangent: bfloat16 [4, 2048, 2048], P('batch', 'seq'), may hold values from -6 to 6
Outputs:
- outputs: bfloat16 [4, 2048, 2048], P('batch', 'seq')
- grad_inputs: float32 [4, 2048, 2048], P('batch', 'seq')
- grad_w_qkv: float32 [6144, 2048], P('seq')
- grad_w_out: float32 [2048, 2048], P('seq')
- grad_w_up: float32 [8192, 2048], P('seq')
- grad_w_down: float32 [2048, 8192], P('seq')
- grad_gain_attn: float32 [2048], replicated
- grad_gain_mix: float32 [2048], replicated
- grad_gain_ffn: float32 [2048], replicated
- grad_gain_hidden: float32 [8192], replicated
The draws below stay inside these ranges and needn't reach their ends.
Inputs may be any that keep to these rules, and one draw needn't show every extreme that they name: `segment_ids`: along a row the ids never fall and each id from 0 to 3 marks one document of 1 to 1024 tokens.
All inputs are finite; a program needn't handle non-finite values.
Results may differ from the reference program's by a relative error of at most 0.02.
Values may be sent and summed in bfloat16 or wider, within the bound.
A program may use at most 448 MiB of HBM per device.

```python
import math
import jax
import jax.numpy as jnp
import numpy as np
from jax import lax

D = 2048
HEADS = 32
HEAD_DIM = 64
FF = 8192
LENGTH = 2048
QBLOCK = 512
DOCS = 4
XBASE = 512
ROWS = 4


def block_scale(key, shape, cuts, low, top_value):
    factor_of, own = 1.0, jax.random.fold_in(key, 6)
    for dim, shards_of in cuts:
        draws = jnp.exp(jax.random.uniform(jax.random.fold_in(own, dim), (shards_of,), jnp.float32, low / len(cuts), top_value / len(cuts)))
        factor_of = factor_of * jnp.repeat(draws, shape[dim] // shards_of).reshape([-1 if axis == dim else 1 for axis in range(len(shape))])
    return factor_of


def profile(amount, total, limit, lean):
    weights = [(1 << 20) // math.isqrt(rank ** lean) + 1 for rank in range(2, amount + 1)]
    spare, counts = total - limit - (amount - 1), [1] * (amount - 1)
    while spare > 0:
        candidates = [i for i in range(amount - 1) if counts[i] < limit]
        mass, remaining = sum([weights[i] for i in candidates]), spare
        for i in candidates:
            addition = min(limit - counts[i], max(1, remaining * weights[i] // mass), spare)
            counts[i] = counts[i] + addition
            spare = spare - addition
    return np.array([limit] + counts)


def ragged_sizes(stream_key, count, total, most, slope):
    if count == 2:
        one = jax.random.randint(stream_key, (), max(1, total - most), min(most, total - 1) + 1)
        return jnp.stack([one, total - one])
    lengths = jnp.asarray(profile(count, total, most, slope), jnp.int32)
    couples = (count - 1) // 2
    giver, sink = lengths[1:1 + 2 * couples:2], lengths[2:2 + 2 * couples:2]
    room = jnp.minimum(giver - 1, most - sink)
    shifted = jax.random.randint(jax.random.fold_in(stream_key, 1), (couples,), 0, 1 << 20) % (room + 1)
    lengths = lengths.at[1:1 + 2 * couples:2].set(giver - shifted).at[2:2 + 2 * couples:2].set(sink + shifted)
    return lengths[jax.random.permutation(jax.random.fold_in(stream_key, 2), count)]


def centred(own_key, shape, scale, most, cuts=(), kind=jnp.bfloat16):
    drawn = scale * jax.random.normal(own_key, shape, jnp.float32)
    if cuts:
        drawn = drawn * block_scale(own_key, shape, cuts, -0.22, 0.18)
    return jnp.clip(drawn, -most, most).astype(kind)


def setup_inputs(seed: int = 0) -> dict:
    key_list = jax.random.split(jax.random.key(seed), 12)
    return {
        "inputs": centred(key_list[0], (ROWS, LENGTH, D), 1.0, 6.0, ((0, 4), (1, 8))),
        "segment_ids": jax.vmap(lambda own: jnp.searchsorted(jnp.cumsum(ragged_sizes(own, DOCS, LENGTH, LENGTH // 2, 1)), jnp.arange(LENGTH), side="right"))(jax.random.split(key_list[1], ROWS)).reshape((ROWS, LENGTH)).astype(jnp.int32),
        "w_qkv": centred(key_list[2], (3 * D, D), D ** -0.5, 0.125, ((0, 8),)),
        "w_out": centred(key_list[3], (D, D), D ** -0.5, 0.125, ((0, 8),)),
        "w_up": centred(key_list[4], (FF, D), D ** -0.5, 0.125, ((0, 8),)),
        "w_down": centred(key_list[5], (D, FF), FF ** -0.5, 0.0625, ((0, 8),)),
        "gain_attn": jnp.clip(1.0 + 0.1 * jax.random.normal(key_list[6], (D,), jnp.float32), 0.5, 1.5),
        "gain_mix": jnp.clip(1.0 + 0.1 * jax.random.normal(key_list[7], (D,), jnp.float32), 0.5, 1.5),
        "gain_ffn": jnp.clip(1.0 + 0.1 * jax.random.normal(key_list[8], (D,), jnp.float32), 0.5, 1.5),
        "gain_hidden": jnp.clip(1.0 + 0.1 * jax.random.normal(key_list[9], (FF,), jnp.float32), 0.5, 1.5),
        "cotangent": centred(key_list[10], (ROWS, LENGTH, D), 1.0, 6.0, ((0, 4), (1, 8))),
    }


@jax.custom_vjp
def low(v):
    return lax.optimization_barrier(v.astype(jnp.bfloat16)).astype(jnp.float32)

@jax.custom_vjp
def low_back(v):
    return v

def low_keep(v):
    return (low(v), None)

def low_pass(kept, grad):
    return (grad,)

def back_keep(v):
    return (v, None)

def back_low(kept, grad):
    return (low(grad),)
low.defvjp(low_keep, low_pass)
low_back.defvjp(back_keep, back_low)
EPSILON = 1e-05
MASKED = -1e+30
PRECISE = lax.Precision.HIGHEST

def norm_rows(values, gain):
    average = lax.optimization_barrier(jnp.mean(values, axis=-1, keepdims=True))
    centered = values - average
    spread = lax.optimization_barrier(jnp.mean(centered * centered, axis=-1, keepdims=True))
    return centered * lax.rsqrt(spread + EPSILON) * gain

def gelu_norm(upper, gain):
    return norm_rows(jax.nn.gelu(upper, approximate=False), gain)

def doc_positions(seg_row):
    index = jnp.arange(seg_row.shape[0], dtype=jnp.int32)
    change = jnp.concatenate([jnp.ones((1,), dtype=bool), seg_row[1:] != seg_row[:-1]])
    starts = jnp.where(change, index, jnp.zeros_like(index))
    return index - lax.cummax(starts, axis=0)

def xpos_tables(positions):
    half_dim = HEAD_DIM // 2
    channel = jnp.arange(half_dim, dtype=jnp.float32)
    inverse = jnp.exp(channel * (-math.log(10000.0) / half_dim))
    zeta = (channel * (2.0 / HEAD_DIM) + 0.4) / 1.4
    place = positions.astype(jnp.float32)[..., None]
    angle = place * inverse
    growth = jnp.exp((place - 0.5 * LENGTH) * (1.0 / XBASE) * jnp.log(zeta))
    return (jnp.cos(angle), jnp.sin(angle), growth)

def rotate(values, cosine, sine, growth):
    half_dim = values.shape[-1] // 2
    first = values[..., :half_dim]
    second = values[..., half_dim:]
    cosine = cosine[..., None, :]
    sine = sine[..., None, :]
    growth = growth[..., None, :]
    return jnp.concatenate([(first * cosine - second * sine) * growth, (second * cosine + first * sine) * growth], axis=-1)

def allowed_pairs(seg_row, start, count):
    seg_block = lax.dynamic_slice_in_dim(seg_row, start, count, 0)
    query_place = start + jnp.arange(count, dtype=jnp.int32)
    key_place = jnp.arange(seg_row.shape[0], dtype=jnp.int32)
    return (seg_block[:, None] == seg_row[None, :]) & (key_place[None, :] <= query_place[:, None])

def attend_row(query, keys, values, seg_row):
    length = query.shape[0]
    factor = HEAD_DIM ** (-0.5)

    def one_block(start):
        query_block = lax.dynamic_slice_in_dim(query, start, QBLOCK, 0)
        allowed = allowed_pairs(seg_row, start, QBLOCK)
        scores = low_back(jnp.einsum('qhd,khd->hqk', query_block, keys, precision=PRECISE) * factor)
        scores = jnp.where(allowed[None], scores, MASKED)
        peak = lax.optimization_barrier(jnp.max(scores, axis=-1, keepdims=True))
        expo = jnp.exp(scores - peak)
        weights = expo / lax.optimization_barrier(jnp.sum(expo, axis=-1, keepdims=True))
        return jnp.einsum('hqk,khd->qhd', low(weights), values, precision=PRECISE)
    starts = jnp.arange(length // QBLOCK, dtype=jnp.int32) * QBLOCK
    mixed = lax.map(jax.checkpoint(one_block), starts)
    return mixed.reshape(query.shape)

def matmul_rows(activations, matrix):
    return jnp.dot(activations, matrix.T, precision=PRECISE, preferred_element_type=jnp.float32)

def forward_row(seg_row, row, w_qkv, w_out, w_up, w_down, gain_attn, gain_mix, gain_ffn, gain_hidden):
    tokens_here = row.shape[0]
    cosine, sine, growth = xpos_tables(doc_positions(seg_row))
    normed = low(norm_rows(row, gain_attn))
    qkv = low_back(matmul_rows(normed, w_qkv))
    qkv = qkv.reshape(tokens_here, 3, HEADS, HEAD_DIM)
    query = low_back(low(rotate(qkv[:, 0], cosine, sine, growth)))
    keys = low_back(low(rotate(qkv[:, 1], cosine, sine, 1.0 / growth)))
    values = low_back(low(qkv[:, 2]))
    attended = attend_row(query, keys, values, seg_row).reshape(row.shape)
    attended = low_back(low(attended))
    mix_in = low(norm_rows(attended, gain_mix))
    branch = low_back(matmul_rows(mix_in, w_out))
    middle = row + branch
    ffn_in = low(norm_rows(middle, gain_ffn))
    upper = low_back(matmul_rows(ffn_in, w_up))
    hidden = low(gelu_norm(upper, gain_hidden))
    return middle + matmul_rows(hidden, w_down)

def reference(inputs, segment_ids, w_qkv, w_out, w_up, w_down, gain_attn, gain_mix, gain_ffn, gain_hidden, cotangent):
    weights_f32 = tuple((item.astype(jnp.float32) for item in (w_qkv, w_out, w_up, w_down)))
    params = weights_f32 + (gain_attn, gain_mix, gain_ffn, gain_hidden)

    def one_row(totals, pieces):
        row_in, seg_row, row_cot = pieces

        def apply(row_f32, *weights):
            return forward_row(seg_row, row_f32, *weights)
        output, pullback = jax.vjp(apply, row_in.astype(jnp.float32), *params)
        grads = pullback(row_cot.astype(jnp.float32))
        totals = tuple((total + grad_item for total, grad_item in zip(totals, grads[1:])))
        return (totals, (output.astype(jnp.bfloat16), grads[0]))
    zeros = tuple((jnp.zeros(item.shape, jnp.float32) for item in params))
    totals, (outputs, input_grads) = lax.scan(one_row, zeros, (inputs, segment_ids, cotangent))
    return (outputs, input_grads, totals[0], totals[1], totals[2], totals[3], totals[4], totals[5], totals[6], totals[7])
```

```python
import functools
import math

import jax
import jax.numpy as jnp
from jax import lax
from jax.experimental import pallas as pl
from jax.experimental.pallas import tpu as pltpu
from jax.sharding import PartitionSpec as P

HEADS = 32
HEAD_DIM = 64
LENGTH = 2048
XBASE = 512
DOCS = 4
EPSILON = 1e-05
MASKED = -1e30
TILE = 256

MESH = pl.DeviceIdType.MESH
F32 = jnp.float32
BF16 = jnp.bfloat16
ANY = pl.BlockSpec(memory_space=pl.ANY)


def nn(a, b):
    return lax.dot_general(a, b, (((1,), (0,)), ((), ())), preferred_element_type=F32)


def nt(a, b):
    return lax.dot_general(a, b, (((1,), (1,)), ((), ())), preferred_element_type=F32)


def tn(a, b):
    return lax.dot_general(a, b, (((0,), (0,)), ((), ())), preferred_element_type=F32)


def norm_parts(values):
    average = jnp.mean(values, axis=-1, keepdims=True)
    centered = values - average
    spread = jnp.mean(centered * centered, axis=-1, keepdims=True)
    scale = lax.rsqrt(spread + EPSILON)
    return centered * scale, scale


def norm_back(grad, normal, scale, gain):
    part = grad * gain
    inner = (
        part
        - jnp.mean(part, axis=-1, keepdims=True)
        - normal * jnp.mean(part * normal, axis=-1, keepdims=True)
    )
    return scale * inner, jnp.sum(grad * normal, axis=0)


def places():
    me = lax.axis_index("seq")
    core = lax.rem(me, 2)
    along_x = lax.rem(me // 2, 2)
    along_y = me // 4
    twin = 1 - 2 * core
    near_x = me + 2 - 4 * along_x
    near_y = me + 4 - 8 * along_y
    across = near_x + 4 - 8 * along_y
    return me, twin, near_x, near_y, across


def remote(src, dst, send_sem, recv_sem, partner):
    return pltpu.make_async_remote_copy(
        src_ref=src,
        dst_ref=dst,
        send_sem=send_sem,
        recv_sem=recv_sem,
        device_id={"seq": partner},
        device_id_type=MESH,
    )


def meet(partners):
    barrier = pltpu.get_barrier_semaphore()
    for partner in partners:
        pl.semaphore_signal(
            barrier, inc=1, device_id={"seq": partner}, device_id_type=MESH
        )
    pl.semaphore_wait(barrier, len(partners))


def gather_copies(x_ref, o_ref, send_sem, recv_sem):
    me, twin, near_x, near_y, across = places()
    half = x_ref.shape[0] // 2
    low, high = pl.ds(0, half), pl.ds(half, half)

    def copy(k, src, dst, partner):
        return remote(src, dst, send_sem.at[k], recv_sem.at[k], partner)

    def relay(k, owner, rows, partner):
        place = o_ref.at[owner, rows]
        return copy(k, place, place, partner)

    return [
        copy(0, x_ref.at[low], o_ref.at[me, low], near_x),
        copy(1, x_ref.at[high], o_ref.at[me, high], near_y),
        copy(2, x_ref.at[high], o_ref.at[me, high], near_x),
        copy(3, x_ref.at[low], o_ref.at[me, low], near_y),
        copy(4, x_ref, o_ref.at[me], me + twin),
        relay(5, near_x, low, near_y),
        relay(6, near_y, high, near_x),
        relay(7, near_x, low, me + twin),
        relay(8, near_y, high, me + twin),
        relay(9, near_x, high, me + twin),
        relay(10, near_y, low, me + twin),
        relay(11, across, low, me + twin),
        relay(12, across, high, me + twin),
    ]


def gather_run(sends, between=None):
    sends[0].wait_recv()
    sends[5].start()
    sends[7].start()
    sends[1].wait_recv()
    sends[6].start()
    sends[8].start()
    sends[2].wait_recv()
    sends[9].start()
    sends[3].wait_recv()
    sends[10].start()
    if between is not None:
        between()
    sends[5].wait_recv()
    sends[11].start()
    sends[6].wait_recv()
    sends[12].start()
    for k in (4, 7, 8, 9, 10, 11, 12):
        sends[k].wait_recv()
    for send in sends:
        send.wait_send()


def meet_all(n, depth):
    me = lax.axis_index("seq")
    z = lax.axis_index("batch")
    barrier = pltpu.get_barrier_semaphore()
    for k in range(1, n):
        pl.semaphore_signal(
            barrier, inc=1, device_id={"seq": lax.rem(me + k, n)}, device_id_type=MESH
        )
    for sign in (-1, 1):

        @pl.when((z + sign >= 0) & (z + sign < depth))
        def _():
            pl.semaphore_signal(
                barrier, inc=1, device_id={"batch": z + sign}, device_id_type=MESH
            )

    ends = (z == 0).astype(jnp.int32) + (z == depth - 1).astype(jnp.int32)
    pl.semaphore_wait(barrier, n + 1 - ends)


def line_remote(src, dst, send_sem, recv_sem, partner):
    return pltpu.make_async_remote_copy(
        src_ref=src,
        dst_ref=dst,
        send_sem=send_sem,
        recv_sem=recv_sem,
        device_id={"batch": partner},
        device_id_type=MESH,
    )


class Line:
    def __init__(self, depth, source, target, send_sem, recv_sem):
        self.depth, self.source, self.target = depth, source, target
        self.send_sem, self.recv_sem = send_sem, recv_sem
        self.z = lax.axis_index("batch")

    def message(self, side, k):
        sign = 2 * side - 1
        owner = self.z - sign * k
        return line_remote(
            self.source(owner, k),
            self.target(owner),
            self.send_sem.at[side, k],
            self.recv_sem.at[side, k],
            self.z + sign,
        )

    def sends(self, side, k):
        sign = 2 * side - 1
        owner, target = self.z - sign * k, self.z + sign
        inside = (owner >= 0) & (owner < self.depth)
        return inside & (target >= 0) & (target < self.depth)

    def land(self, k):
        for side in (0, 1):
            sign = 2 * side - 1
            owner = self.z - sign * (k + 1)

            @pl.when((owner >= 0) & (owner < self.depth))
            def _():
                place = self.target(owner)
                line_remote(
                    place,
                    place,
                    self.send_sem.at[side, k],
                    self.recv_sem.at[side, k],
                    self.z - sign,
                ).wait_recv()

    def start(self, k):
        for side in (0, 1):

            @pl.when(self.sends(side, k))
            def _():
                self.message(side, k).start()

    def sent(self, k):
        for side in (0, 1):

            @pl.when(self.sends(side, k))
            def _():
                self.message(side, k).wait_send()


def gather_kernel(
    n, depth, x_ref, near_ref, o_ref, all_ref, local_sem, send_sem, recv_sem, line_send, line_recv
):
    me, twin, near_x, near_y, _ = places()
    z = lax.axis_index("batch")
    own = pltpu.make_async_copy(x_ref, o_ref.at[me], local_sem.at[0])
    own.start()

    def keep(shift):
        return pltpu.make_async_copy(
            near_ref.at[:, z + shift], all_ref.at[:, z + shift], local_sem.at[2 + shift]
        )

    def kept(shift):
        return (z + shift >= 0) & (z + shift < depth)

    for shift in (-1, 0, 1):

        @pl.when(kept(shift))
        def _():
            keep(shift).start()

    meet_all(n, depth)
    sends = gather_copies(x_ref, o_ref, send_sem, recv_sem)
    for k in range(5):
        sends[k].start()
    line = Line(
        depth,
        lambda owner, k: (near_ref if k == 1 else all_ref).at[:, owner],
        lambda owner: all_ref.at[:, owner],
        line_send,
        line_recv,
    )
    line.start(1)

    def between():
        for k in range(2, depth - 1):
            line.land(k - 1)
            line.start(k)

    gather_run(sends, between)
    line.land(depth - 2)
    for k in range(1, depth - 1):
        line.sent(k)
    for shift in (-1, 0, 1):

        @pl.when(kept(shift))
        def _():
            keep(shift).wait()

    own.wait()


def gather_seq(block, near, collective_id):
    n, depth = lax.axis_size("seq"), lax.axis_size("batch")
    rows, width = block.shape
    if n != 8:
        return lax.all_gather(block, "seq", axis=0, tiled=True), near
    gathered, every = pl.pallas_call(
        functools.partial(gather_kernel, n, depth),
        out_shape=(
            jax.ShapeDtypeStruct((n, rows, width), block.dtype),
            jax.ShapeDtypeStruct(near.shape, near.dtype),
        ),
        in_specs=[ANY, ANY],
        out_specs=(ANY, ANY),
        scratch_shapes=[
            pltpu.SemaphoreType.DMA((4,)),
            pltpu.SemaphoreType.DMA((13,)),
            pltpu.SemaphoreType.DMA((13,)),
            pltpu.SemaphoreType.DMA((2, depth)),
            pltpu.SemaphoreType.DMA((2, depth)),
        ],
        compiler_params=pltpu.CompilerParams(
            collective_id=collective_id, has_side_effects=True
        ),
        name="gather_seq",
    )(block, near)
    return gathered.reshape(n * rows, width), every.reshape(-1, near.shape[-1])


def lane_tables(place):
    half = HEAD_DIM // 2
    lane = lax.broadcasted_iota(jnp.int32, (1, 128), 1)
    channel = lax.rem(lane, half).astype(F32)
    inverse = jnp.exp(channel * (-math.log(10000.0) / half))
    zeta = (channel * (2.0 / HEAD_DIM) + 0.4) / 1.4
    sign = jnp.where(lax.rem(lane, HEAD_DIM) < half, -1.0, 1.0)
    angle = place * inverse
    growth = jnp.exp((place - 0.5 * LENGTH) * (1.0 / XBASE) * jnp.log(zeta))
    shrink = 1.0 / growth
    cosine = jnp.cos(angle)
    sine = jnp.sin(angle) * sign
    return cosine * growth, sine * growth, cosine * shrink, sine * shrink


def start_kernel(
    n, depth, x_ref, w_ref, wd_ref, pos_ref,
    o_ref, wq_ref, wk_ref, wv_ref, wc_ref, cq_ref, sq_ref, ck_ref, sk_ref,
    local_sem, send_sem, recv_sem, hop_send, hop_recv, col_send, col_recv, line_send, line_recv,
):
    z = lax.axis_index("batch")
    rows_z = wc_ref.shape[2]
    cols = wc_ref.shape[3]
    me, twin, near_x, near_y, _ = places()
    parts = (wq_ref, wk_ref, wv_ref)
    own = pltpu.make_async_copy(x_ref, o_ref.at[me], local_sem.at[0])
    own.start()
    wd_rows = pl.ds(pl.multiple_of(z * rows_z, rows_z), rows_z)

    def column(k):
        return wd_ref.at[wd_rows, pl.ds(pl.multiple_of(k * cols, cols), cols)]

    own_column = pltpu.make_async_copy(column(me), wc_ref.at[me, z], local_sem.at[4])
    own_column.start()
    meet_all(n, depth)
    turns = [
        remote(
            column(lax.rem(me + k, n)),
            wc_ref.at[me, z],
            col_send.at[k],
            col_recv.at[k],
            lax.rem(me + k, n),
        )
        for k in range(1, n)
    ]
    for turn in turns:
        turn.start()
    sends = gather_copies(x_ref, o_ref, send_sem, recv_sem)
    for k in range(5):
        sends[k].start()

    line = Line(
        depth,
        lambda owner, k: wc_ref.at[:, owner],
        lambda owner: wc_ref.at[:, owner],
        line_send,
        line_recv,
    )

    def hop(j, part, target):
        return remote(
            w_ref.at[j], parts[part], hop_send.at[j], hop_recv.at[part], target
        )

    def here(j, part):
        return pltpu.make_async_copy(w_ref.at[j], parts[part], local_sem.at[1 + j])

    for j in range(3):
        block = 3 * me + j
        target = lax.rem(block, n)
        for part in range(3):
            inside = block // n == part

            @pl.when(inside & (target != me))
            def _():
                hop(j, part, target).start()

            @pl.when(inside & (target == me))
            def _():
                here(j, part).start()

    @pl.loop(0, pos_ref.shape[0])
    def _(r):
        at = pl.ds(pl.multiple_of(r * 128, 128), 128)
        places_here = jnp.broadcast_to(pos_ref[pl.ds(r, 1), :], (128, 128)).T
        tables = lane_tables(places_here)
        for ref, table in zip((cq_ref, sq_ref, ck_ref, sk_ref), tables, strict=True):
            ref[at] = table

    own_column.wait()
    for turn in turns:
        turn.wait_recv()
    line.start(0)
    gather_run(sends)
    line.land(0)
    line.sent(0)
    for turn in turns:
        turn.wait_send()
    for j in range(3):
        block = 3 * me + j
        target = lax.rem(block, n)

        for part in range(3):
            inside = block // n == part

            @pl.when(inside & (target != me))
            def _():
                hop(j, part, target).wait_send()

            @pl.when(inside & (target == me))
            def _():
                here(j, part).wait()

    for part in range(3):
        source = (part * n + me) // 3

        @pl.when(source != me)
        def _():
            hop(0, part, source).wait_recv()

    own.wait()


def start_exchange(block, w_qkv, w_down, positions, collective_id):
    n, depth = lax.axis_size("seq"), lax.axis_size("batch")
    rows, width = block.shape
    piece = w_qkv.shape[0] // 3
    w = w_qkv.reshape(3, piece, width)
    if n != 8:
        me = lax.axis_index("seq")
        turned = [
            lax.ppermute(w[j], "seq", [(d, (3 * d + j) % n) for d in range(n)])
            for j in range(3)
        ]
        parts = [pick_part(turned, me, n, part) for part in range(3)]
        place = jnp.broadcast_to(positions[:, None], (positions.shape[0], 128))
        return (
            lax.all_gather(block, "seq", axis=0, tiled=True),
            parts,
            lax.all_to_all(w_down, "seq", split_axis=1, concat_axis=0, tiled=True),
            lane_tables(place),
        )
    rows_z, cols = w_down.shape[0] // depth, w_down.shape[1] // n
    inside = pl.BlockSpec(memory_space=pltpu.VMEM)
    table = jax.ShapeDtypeStruct((n * rows, 128), F32)
    part = jax.ShapeDtypeStruct((piece, width), w.dtype)
    gathered, wq, wk, wv, columns, *tables = pl.pallas_call(
        functools.partial(start_kernel, n, depth),
        out_shape=(
            jax.ShapeDtypeStruct((n, rows, width), block.dtype),
            part,
            part,
            part,
            jax.ShapeDtypeStruct((n, depth, rows_z, cols), w_down.dtype),
            *([table] * 4),
        ),
        in_specs=[ANY, ANY, ANY, inside],
        out_specs=(ANY, ANY, ANY, ANY, ANY, *([inside] * 4)),
        scratch_shapes=[
            pltpu.SemaphoreType.DMA((5,)),
            pltpu.SemaphoreType.DMA((13,)),
            pltpu.SemaphoreType.DMA((13,)),
            pltpu.SemaphoreType.DMA((3,)),
            pltpu.SemaphoreType.DMA((3,)),
            pltpu.SemaphoreType.DMA((n,)),
            pltpu.SemaphoreType.DMA((n,)),
            pltpu.SemaphoreType.DMA((2, depth)),
            pltpu.SemaphoreType.DMA((2, depth)),
        ],
        compiler_params=pltpu.CompilerParams(
            collective_id=collective_id, has_side_effects=True
        ),
        name="start_exchange",
    )(block, w, w_down, positions.reshape(-1, 128))
    return gathered.reshape(n * rows, width), (wq, wk, wv), columns, tables


def scatter_kernel(
    p_ref, o_ref, own, twin_in, held, local_sem, send_sem, recv_sem
):
    me, twin, near_x, near_y, across = places()
    rows = p_ref.shape[1]
    half = rows // 2
    low, high = pl.ds(0, half), pl.ds(half, half)
    mine = (across, near_x, near_y, me)

    loads = [
        pltpu.make_async_copy(p_ref.at[block], own.at[i], local_sem.at[i])
        for i, block in enumerate(mine)
    ]
    for load in loads:
        load.start()
    meet((me + twin, near_x, near_y))

    def copy(k, src, dst, partner):
        return remote(src, dst, send_sem.at[k], recv_sem.at[k], partner)

    twins = [
        copy(i, p_ref.at[block + twin], twin_in.at[i], me + twin)
        for i, block in enumerate(mine)
    ]
    for send in twins:
        send.start()
    sends = [
        copy(4, own.at[0, low], held.at[0], near_x),
        copy(5, own.at[0, high], held.at[1], near_y),
        copy(6, own.at[1, low], held.at[2], near_x),
        copy(7, own.at[2, high], held.at[3], near_y),
        copy(8, own.at[1, high], held.at[4], near_x),
        copy(9, own.at[2, low], held.at[5], near_y),
    ]
    step = 32

    def add_twin(i):
        loads[i].wait()
        twins[i].wait_recv()

        @pl.loop(0, rows // step)
        def _(r):
            at = pl.ds(pl.multiple_of(r * step, step), step)
            own[i, at] = (
                own[i, at].astype(F32) + twin_in[i, at].astype(F32)
            ).astype(own.dtype)

    def add_held(i, base, slot):
        @pl.loop(0, half // step)
        def _(r):
            at = pl.ds(pl.multiple_of(r * step, step), step)
            to = pl.ds(pl.multiple_of(base + r * step, step), step)
            own[i, to] = (
                own[i, to].astype(F32) + held[slot, at].astype(F32)
            ).astype(own.dtype)

    add_twin(0)
    sends[0].start()
    sends[1].start()
    add_twin(1)
    sends[2].start()
    add_twin(2)
    sends[3].start()
    sends[1].wait_recv()
    add_held(1, half, 1)
    sends[4].start()
    sends[0].wait_recv()
    add_held(2, 0, 0)
    sends[5].start()
    loads[3].wait()
    twins[3].wait_recv()
    for k in (2, 3, 4, 5):
        sends[k].wait_recv()

    def final(base, first, second):
        @pl.loop(0, half // step)
        def _(r):
            at = pl.ds(pl.multiple_of(r * step, step), step)
            to = pl.ds(pl.multiple_of(base + r * step, step), step)
            o_ref[to] = (
                own[3, to].astype(F32)
                + twin_in[3, to].astype(F32)
                + held[first, at].astype(F32)
                + held[second, at].astype(F32)
            )

    final(0, 2, 5)
    final(half, 3, 4)
    for send in twins + sends:
        send.wait_send()


def scatter_seq(partial, collective_id):
    n = lax.axis_size("seq")
    rows, width = partial.shape[0] // n, partial.shape[1]
    if n != 8:
        return lax.psum_scatter(
            partial, "seq", scatter_dimension=0, tiled=True
        ).astype(F32)
    return pl.pallas_call(
        scatter_kernel,
        out_shape=jax.ShapeDtypeStruct((rows, width), F32),
        in_specs=[ANY],
        out_specs=pl.BlockSpec(memory_space=pltpu.VMEM),
        scratch_shapes=[
            pltpu.VMEM((4, rows, width), BF16),
            pltpu.VMEM((4, rows, width), BF16),
            pltpu.VMEM((6, rows // 2, width), BF16),
            pltpu.SemaphoreType.DMA((4,)),
            pltpu.SemaphoreType.DMA((10,)),
            pltpu.SemaphoreType.DMA((10,)),
        ],
        compiler_params=pltpu.CompilerParams(
            collective_id=collective_id,
            has_side_effects=True,
            vmem_limit_bytes=32 * 1024 * 1024,
        ),
        name="scatter_seq",
    )(partial.reshape(n, rows, width))


def heads_to_tokens_kernel(n, x_ref, o_ref, local_sem, send_sem, recv_sem):
    me = lax.axis_index("seq")
    rows = o_ref.shape[0]
    cols = x_ref.shape[1]
    exchange(
        n,
        me,
        lambda k: x_ref.at[pl.ds(pl.multiple_of(k * rows, rows), rows)],
        o_ref.at[:, pl.ds(pl.multiple_of(me * cols, cols), cols)],
        local_sem,
        send_sem,
        recv_sem,
    )


def exchange(n, me, source, target, local_sem, send_sem, recv_sem):
    own = pltpu.make_async_copy(source(me), target, local_sem)
    own.start()
    barrier = pltpu.get_barrier_semaphore()
    for k in range(1, n):
        pl.semaphore_signal(
            barrier,
            inc=1,
            device_id={"seq": lax.rem(me + k, n)},
            device_id_type=MESH,
        )
    pl.semaphore_wait(barrier, n - 1)
    copies = []
    for k in range(1, n):
        partner = lax.rem(me + k, n)
        copies.append(
            pltpu.make_async_remote_copy(
                src_ref=source(partner),
                dst_ref=target,
                send_sem=send_sem.at[k],
                recv_sem=recv_sem.at[k],
                device_id={"seq": partner},
                device_id_type=MESH,
            )
        )
        copies[-1].start()
    for copy in copies:
        copy.wait()
    own.wait()


def heads_to_tokens(heads, collective_id):
    n = lax.axis_size("seq")
    total, cols = heads.shape
    rows = total // n
    return pl.pallas_call(
        functools.partial(heads_to_tokens_kernel, n),
        out_shape=jax.ShapeDtypeStruct((rows, n * cols), heads.dtype),
        in_specs=[ANY],
        out_specs=ANY,
        scratch_shapes=[
            pltpu.SemaphoreType.DMA,
            pltpu.SemaphoreType.DMA((n,)),
            pltpu.SemaphoreType.DMA((n,)),
        ],
        compiler_params=pltpu.CompilerParams(
            collective_id=collective_id, has_side_effects=True
        ),
        name="heads_to_tokens",
    )(heads)


def tokens_to_heads_kernel(n, x_ref, o_ref, local_sem, send_sem, recv_sem):
    me = lax.axis_index("seq")
    rows = x_ref.shape[0]
    cols = o_ref.shape[1]
    exchange(
        n,
        me,
        lambda k: x_ref.at[:, pl.ds(pl.multiple_of(k * cols, cols), cols)],
        o_ref.at[pl.ds(pl.multiple_of(me * rows, rows), rows)],
        local_sem,
        send_sem,
        recv_sem,
    )


def tokens_to_heads(tokens, collective_id):
    n = lax.axis_size("seq")
    rows, total = tokens.shape
    return pl.pallas_call(
        functools.partial(tokens_to_heads_kernel, n),
        out_shape=jax.ShapeDtypeStruct((rows * n, total // n), tokens.dtype),
        in_specs=[ANY],
        out_specs=ANY,
        scratch_shapes=[
            pltpu.SemaphoreType.DMA,
            pltpu.SemaphoreType.DMA((n,)),
            pltpu.SemaphoreType.DMA((n,)),
        ],
        compiler_params=pltpu.CompilerParams(
            collective_id=collective_id, has_side_effects=True
        ),
        name="tokens_to_heads",
    )(tokens)


def swap_halves(values):
    width = values.shape[-1]
    half = HEAD_DIM // 2
    lane = lax.broadcasted_iota(jnp.int32, values.shape, 1)
    ahead = pltpu.roll(values, width - half, 1)
    behind = pltpu.roll(values, half, 1)
    return jnp.where(lane % HEAD_DIM < half, ahead, behind)


def spread_lanes(table, width):
    return jnp.concatenate([table] * (width // table.shape[-1]), axis=-1)


def qkv_kernel(
    x_ref, wq_ref, wk_ref, wv_ref, cq_ref, sq_ref, ck_ref, sk_ref,
    q_ref, k_ref, v_ref, kt_ref, vt_ref,
):
    x = x_ref[...]
    width = q_ref.shape[1]
    query = nt(x, wq_ref[...])
    query = query * spread_lanes(cq_ref[...], width) + swap_halves(
        query
    ) * spread_lanes(sq_ref[...], width)
    q_ref[...] = query.astype(BF16) * (HEAD_DIM**-0.5)
    keys = nt(x, wk_ref[...])
    keys = keys * spread_lanes(ck_ref[...], width) + swap_halves(
        keys
    ) * spread_lanes(sk_ref[...], width)
    k_ref[...] = keys.astype(BF16)
    kt_ref[...] = keys.T.astype(BF16)
    values = nt(x, wv_ref[...])
    v_ref[...] = values.astype(BF16)
    vt_ref[...] = values.T.astype(BF16)


def project_qkv(x, wq, wk, wv, tables):
    length, width = x.shape
    cols = wq.shape[0]
    steps = length // TILE
    weight = pl.BlockSpec((cols, width), lambda i: (0, 0))
    table = pl.BlockSpec((TILE, tables[0].shape[1]), lambda i: (i, 0))
    row_out = pl.BlockSpec((TILE, cols), lambda i: (i, 0))
    col_out = pl.BlockSpec((cols, TILE), lambda i: (0, i))
    rows = jax.ShapeDtypeStruct((length, cols), BF16)
    columns = jax.ShapeDtypeStruct((cols, length), BF16)
    return pl.pallas_call(
        qkv_kernel,
        grid=(steps,),
        out_shape=(rows, rows, rows, columns, columns),
        in_specs=[pl.BlockSpec((TILE, width), lambda i: (i, 0))]
        + [weight] * 3
        + [table] * 4,
        out_specs=(row_out, row_out, row_out, col_out, col_out),
        compiler_params=pltpu.CompilerParams(vmem_limit_bytes=40 * 1024 * 1024),
        cost_estimate=pl.CostEstimate(
            flops=6 * length * width * cols,
            bytes_accessed=2 * length * width + 6 * width * cols + 10 * length * cols,
            transcendentals=0,
        ),
        name="project_qkv",
    )(x, wq, wk, wv, *tables)


def pair_mask(start_row, i, j):
    key_place = j * TILE + lax.broadcasted_iota(jnp.int32, (TILE, TILE), 0)
    query_place = i * TILE + lax.broadcasted_iota(jnp.int32, (TILE, TILE), 1)
    return (key_place <= query_place) & (key_place >= start_row)


def head_rows(query, heads):
    lane = lax.broadcasted_iota(jnp.int32, query.shape, 1) // HEAD_DIM
    zero = jnp.zeros_like(query)
    return [jnp.where(lane == h, query, zero) for h in range(heads)]


def attend_kernel(
    heads, first_ref, start_ref, q_ref, k_ref, vt_ref, o_ref, lse_ref, peak, total, mixed
):
    i = pl.program_id(0)
    queries = head_rows(q_ref[...], heads)
    start_row = start_ref[...]

    def block(j, first):
        at = pl.ds(pl.multiple_of(j * TILE, TILE), TILE)
        keys = k_ref[at, :]
        mask = pair_mask(start_row, i, j)
        for h in range(heads):
            here = slice(h * HEAD_DIM, (h + 1) * HEAD_DIM)
            scores = jnp.where(mask, nt(keys, queries[h]), MASKED)
            if first:
                new_peak = jnp.max(scores, axis=0, keepdims=True)
                expo = jnp.exp(scores - new_peak)
                total[h : h + 1] = jnp.sum(expo, axis=0, keepdims=True)
                mixed[here] = nn(vt_ref[here, at], expo.astype(BF16))
            else:
                old_peak = peak[h : h + 1]
                new_peak = jnp.maximum(old_peak, jnp.max(scores, axis=0, keepdims=True))
                expo = jnp.exp(scores - new_peak)
                shrink = jnp.exp(old_peak - new_peak)
                total[h : h + 1] = total[h : h + 1] * shrink + jnp.sum(
                    expo, axis=0, keepdims=True
                )
                mixed[here] = mixed[here] * shrink + nn(
                    vt_ref[here, at], expo.astype(BF16)
                )
            peak[h : h + 1] = new_peak

    block(i, True)

    @pl.loop(0, i - first_ref[i])
    def _(t):
        block(i - 1 - t, False)

    for h in range(heads):
        here = slice(h * HEAD_DIM, (h + 1) * HEAD_DIM)
        mixed[here] = mixed[here] / total[h : h + 1]
    o_ref[...] = mixed[...].T.astype(BF16)
    lse_ref[0] = peak[...] + jnp.log(total[...])


def attend(first, start, q, k, vt):
    length, cols = q.shape
    heads = cols // HEAD_DIM
    steps = length // TILE
    row = pl.BlockSpec((TILE, cols), lambda i, *_: (i, 0))
    return pl.pallas_call(
        functools.partial(attend_kernel, heads),
        out_shape=(
            jax.ShapeDtypeStruct((length, cols), BF16),
            jax.ShapeDtypeStruct((steps, heads, TILE), F32),
        ),
        grid_spec=pltpu.PrefetchScalarGridSpec(
            num_scalar_prefetch=1,
            grid=(steps,),
            in_specs=[
                pl.BlockSpec((1, TILE), lambda i, *_: (0, i)),
                row,
                pl.BlockSpec((length, cols), lambda i, *_: (0, 0)),
                pl.BlockSpec((cols, length), lambda i, *_: (0, 0)),
            ],
            out_specs=(
                row,
                pl.BlockSpec((1, heads, TILE), lambda i, *_: (i, 0, 0)),
            ),
            scratch_shapes=[
                pltpu.VMEM((heads, TILE), F32),
                pltpu.VMEM((heads, TILE), F32),
                pltpu.VMEM((cols, TILE), F32),
            ],
        ),
        compiler_params=pltpu.CompilerParams(vmem_limit_bytes=32 * 1024 * 1024),
        cost_estimate=pl.CostEstimate(
            flops=4 * length * 1024 * cols,
            bytes_accessed=8 * length * cols,
            transcendentals=length * 1024 * heads,
        ),
        name="attend",
    )(first, start, q, k, vt)


def attend_back_kernel(
    heads, first_ref, start_ref, q_ref, k_ref, kt_ref, v_ref, o_ref, lse_ref, do_ref,
    cq_ref, sq_ref, ck_ref, sk_ref, dq_ref, dk_ref, dv_ref, dqt, dk_sum, dv_sum,
):
    i = pl.program_id(0)
    steps = pl.num_programs(0)
    width = q_ref.shape[1]
    queries = head_rows(q_ref[...], heads)
    grads = head_rows(do_ref[...], heads)
    start_row = start_ref[...]
    product = (do_ref[...].astype(F32) * o_ref[...].astype(F32)).T
    inner = [
        jnp.sum(product[h * HEAD_DIM : (h + 1) * HEAD_DIM], axis=0, keepdims=True)
        for h in range(heads)
    ]

    def block(j, first):
        at = pl.ds(pl.multiple_of(j * TILE, TILE), TILE)
        keys = k_ref[at, :]
        values = v_ref[at, :]
        mask = pair_mask(start_row, i, j)
        key_term = None
        value_term = None
        for h in range(heads):
            here = slice(h * HEAD_DIM, (h + 1) * HEAD_DIM)
            scores = nt(keys, queries[h])
            weights = jnp.where(mask, jnp.exp(scores - lse_ref[0, h : h + 1]), 0.0)
            grad_weights = nt(values, grads[h])
            grad_scores = (weights * (grad_weights - inner[h])).astype(BF16)
            term = nn(weights.astype(BF16), grads[h])
            value_term = term if value_term is None else value_term + term
            term = nn(grad_scores, queries[h])
            key_term = term if key_term is None else key_term + term
            term = nn(kt_ref[here, at], grad_scores)
            if first:
                dqt[here] = term
            else:
                dqt[here] = dqt[here] + term
        if first:
            dk_sum[at] = key_term
            dv_sum[at] = value_term
        else:
            dk_sum[at] = dk_sum[at] + key_term
            dv_sum[at] = dv_sum[at] + value_term

    block(i, True)

    @pl.loop(0, i - first_ref[i])
    def _(t):
        block(i - 1 - t, False)

    def unturn(grad, cosine, sine):
        grad = grad.astype(BF16).astype(F32)
        cosine = spread_lanes(cosine, width)
        sine = spread_lanes(sine, width)
        return (grad * cosine - swap_halves(grad) * sine).astype(BF16)

    rows = pl.ds(pl.multiple_of(i * TILE, TILE), TILE)
    dq_ref[...] = unturn(
        dqt[...].T * (HEAD_DIM**-0.5), cq_ref[rows, :], sq_ref[rows, :]
    )

    @pl.when(i == steps - 1)
    def _():
        @pl.loop(0, steps)
        def _(j):
            at = pl.ds(pl.multiple_of(j * TILE, TILE), TILE)
            dk_ref[at] = unturn(dk_sum[at], ck_ref[at, :], sk_ref[at, :])
            dv_ref[at] = dv_sum[at].astype(BF16)


def attend_back(first, start, q, k, kt, v, o, lse, do, tables):
    length, cols = q.shape
    heads = cols // HEAD_DIM
    steps = length // TILE
    row = pl.BlockSpec((TILE, cols), lambda i, *_: (i, 0))
    whole = pl.BlockSpec((length, cols), lambda i, *_: (0, 0))
    table = pl.BlockSpec((length, tables[0].shape[1]), lambda i, *_: (0, 0))
    shape = jax.ShapeDtypeStruct((length, cols), BF16)
    return pl.pallas_call(
        functools.partial(attend_back_kernel, heads),
        out_shape=(shape, shape, shape),
        grid_spec=pltpu.PrefetchScalarGridSpec(
            num_scalar_prefetch=1,
            grid=(steps,),
            in_specs=[
                pl.BlockSpec((1, TILE), lambda i, *_: (0, i)),
                row,
                whole,
                pl.BlockSpec((cols, length), lambda i, *_: (0, 0)),
                whole,
                row,
                pl.BlockSpec((1, heads, TILE), lambda i, *_: (i, 0, 0)),
                row,
            ]
            + [table] * 4,
            out_specs=(row, whole, whole),
            scratch_shapes=[
                pltpu.VMEM((cols, TILE), F32),
                pltpu.VMEM((length, cols), F32),
                pltpu.VMEM((length, cols), F32),
            ],
        ),
        compiler_params=pltpu.CompilerParams(vmem_limit_bytes=48 * 1024 * 1024),
        cost_estimate=pl.CostEstimate(
            flops=10 * length * 1024 * cols,
            bytes_accessed=16 * length * cols,
            transcendentals=length * 1024 * heads,
        ),
        name="attend_back",
    )(first, start, q, k, kt, v, o, lse, do, *tables)


def upper_kernel(
    x_ref, wu_ref, c_ref, wd_ref, gain_ref, act_ref, slope_ref, grad_ref, stat_ref
):
    upper = nt(x_ref[...], wu_ref[...])
    grad = nn(c_ref[...], wd_ref[...])
    below = 0.5 * (1.0 + lax.erf(upper * (0.5**0.5)))
    act = upper * below
    slope = below + upper * (jnp.exp(-0.5 * upper * upper) * ((2.0 * math.pi) ** -0.5))
    act_ref[...] = act
    slope_ref[...] = slope.astype(BF16)
    grad_ref[...] = grad
    part = grad * gain_ref[...]
    average = jnp.mean(act, axis=-1, keepdims=True)
    centered = act - average
    spread = jnp.sum(centered * centered, axis=-1, keepdims=True)
    part_sum = jnp.sum(part, axis=-1, keepdims=True)
    cross = jnp.sum(part * centered, axis=-1, keepdims=True)
    lane = lax.broadcasted_iota(jnp.int32, (x_ref.shape[0], 128), 1)
    columns = jnp.where(
        lane == 0,
        average,
        jnp.where(lane == 1, spread, jnp.where(lane == 2, part_sum, cross)),
    )
    stat_ref[...] = columns.T[:8]


def upper_pass(x, w_up, cot, w_down, gain):
    length, width = x.shape
    feats = w_up.shape[0]
    rows = TILE
    row = pl.BlockSpec((rows, width), lambda i: (i, 0))
    out = pl.BlockSpec((rows, feats), lambda i: (i, 0))
    return pl.pallas_call(
        upper_kernel,
        grid=(length // rows,),
        out_shape=(
            jax.ShapeDtypeStruct((length, feats), F32),
            jax.ShapeDtypeStruct((length, feats), BF16),
            jax.ShapeDtypeStruct((length, feats), F32),
            jax.ShapeDtypeStruct((8, length), F32),
        ),
        in_specs=[
            row,
            pl.BlockSpec((feats, width), lambda i: (0, 0)),
            row,
            pl.BlockSpec((width, feats), lambda i: (0, 0)),
            pl.BlockSpec((1, feats), lambda i: (0, 0)),
        ],
        out_specs=(out, out, out, pl.BlockSpec((8, rows), lambda i: (0, i))),
        compiler_params=pltpu.CompilerParams(vmem_limit_bytes=48 * 1024 * 1024),
        cost_estimate=pl.CostEstimate(
            flops=4 * length * width * feats,
            bytes_accessed=8 * length * width + 8 * length * feats,
            transcendentals=2 * length * feats,
        ),
        name="upper_pass",
    )(x, w_up, cot, w_down, gain)


def hidden_kernel(act_ref, slope_ref, grad_ref, stat_ref, gain_ref, hid_ref, gu_ref, gg_ref):
    i = pl.program_id(0)
    stats = stat_ref[...].T
    average = stats[:, 0:1]
    scale = stats[:, 1:2]
    part_mean = stats[:, 2:3]
    cross_mean = stats[:, 3:4]
    gain = gain_ref[...]
    normal = (act_ref[...] - average) * scale
    grad = grad_ref[...]
    hid_ref[...] = (normal * gain).astype(BF16)
    back = scale * (grad * gain - part_mean - normal * cross_mean)
    gu_ref[...] = (slope_ref[...].astype(F32) * back).astype(BF16)
    term = jnp.sum(grad * normal, axis=0, keepdims=True)

    @pl.when(i == 0)
    def _():
        gg_ref[...] = term

    @pl.when(i > 0)
    def _():
        gg_ref[...] = gg_ref[...] + term


def hidden_pass(act, slope, grad, stats, gain):
    length, feats = act.shape
    out = pl.BlockSpec((TILE, feats), lambda i: (i, 0))
    one = pl.BlockSpec((1, feats), lambda i: (0, 0))
    return pl.pallas_call(
        hidden_kernel,
        grid=(length // TILE,),
        out_shape=(
            jax.ShapeDtypeStruct((length, feats), BF16),
            jax.ShapeDtypeStruct((length, feats), BF16),
            jax.ShapeDtypeStruct((1, feats), F32),
        ),
        in_specs=[out, out, out, pl.BlockSpec((8, TILE), lambda i: (0, i)), one],
        out_specs=(out, out, one),
        compiler_params=pltpu.CompilerParams(vmem_limit_bytes=40 * 1024 * 1024),
        cost_estimate=pl.CostEstimate(
            flops=12 * length * feats,
            bytes_accessed=14 * length * feats,
            transcendentals=0,
        ),
        name="hidden_pass",
    )(act, slope, grad, stats, gain)


def stat_kernel(n, feats, x_ref, o_ref, held, send_sem, recv_sem):
    me = lax.axis_index("seq")
    held[me] = x_ref[...]
    meet([lax.rem(me + k, n) for k in range(1, n)])
    copies = [
        remote(x_ref, held.at[me], send_sem.at[k], recv_sem.at[k], lax.rem(me + k, n))
        for k in range(1, n)
    ]
    for copy in copies:
        copy.start()
    for copy in copies:
        copy.wait()
    average = held[0, 0:1]
    for d in range(1, n):
        average = average + held[d, 0:1]
    average = average * (1.0 / n)
    spread = jnp.zeros_like(average)
    part = jnp.zeros_like(average)
    cross = jnp.zeros_like(average)
    for d in range(n):
        shift = held[d, 0:1] - average
        spread = spread + held[d, 1:2] + feats * (shift * shift)
        part = part + held[d, 2:3]
        cross = cross + held[d, 3:4] + shift * held[d, 2:3]
    whole = 1.0 / (n * feats)
    scale = lax.rsqrt(spread * whole + EPSILON)
    o_ref[0:1] = average
    o_ref[1:2] = scale
    o_ref[2:3] = part * whole
    o_ref[3:4] = cross * scale * whole
    o_ref[4:8] = jnp.zeros((4, average.shape[1]), F32)


def join_stats(stat, feats, collective_id):
    n = lax.axis_size("seq")
    inside = pl.BlockSpec(memory_space=pltpu.VMEM)
    return pl.pallas_call(
        functools.partial(stat_kernel, n, feats),
        out_shape=jax.ShapeDtypeStruct(stat.shape, F32),
        in_specs=[inside],
        out_specs=inside,
        scratch_shapes=[
            pltpu.VMEM((n, *stat.shape), F32),
            pltpu.SemaphoreType.DMA((n,)),
            pltpu.SemaphoreType.DMA((n,)),
        ],
        compiler_params=pltpu.CompilerParams(
            collective_id=collective_id, has_side_effects=True
        ),
        name="join_stats",
    )(stat)


STEP = 32


def mix_kernel(att_ref, x_ref, w_ref, gm_ref, gf_ref, mix_ref, mid_ref, ffn_ref):
    j = pl.program_id(0)
    rows = att_ref.shape[0]
    cols = w_ref.shape[0]

    @pl.when(j == 0)
    def _():
        @pl.loop(0, rows // STEP)
        def _(r):
            at = pl.ds(pl.multiple_of(r * STEP, STEP), STEP)
            normal, _ = norm_parts(att_ref[at].astype(F32))
            mix_ref[at] = (normal * gm_ref[...]).astype(BF16)

    here = pl.ds(pl.multiple_of(j * cols, cols), cols)
    mid_ref[:, here] = x_ref[:, here].astype(F32) + nt(mix_ref[...], w_ref[...])

    @pl.when(j == pl.num_programs(0) - 1)
    def _():
        @pl.loop(0, rows // STEP)
        def _(r):
            at = pl.ds(pl.multiple_of(r * STEP, STEP), STEP)
            normal, _ = norm_parts(mid_ref[at])
            ffn_ref[at] = (normal * gf_ref[...]).astype(BF16)


def mix_pass(attended, x, w_out, gain_mix, gain_ffn):
    rows, width = x.shape
    cols = TILE
    n = width // cols
    whole = pl.BlockSpec((rows, width), lambda j: (0, 0))
    gain = pl.BlockSpec((1, width), lambda j: (0, 0))
    low = jax.ShapeDtypeStruct((rows, width), BF16)
    return pl.pallas_call(
        mix_kernel,
        grid=(n,),
        out_shape=(low, jax.ShapeDtypeStruct((rows, width), F32), low),
        in_specs=[
            whole,
            whole,
            pl.BlockSpec((cols, width), lambda j: (j, 0)),
            gain,
            gain,
        ],
        out_specs=(whole, whole, whole),
        compiler_params=pltpu.CompilerParams(vmem_limit_bytes=32 * 1024 * 1024),
        cost_estimate=pl.CostEstimate(
            flops=2 * rows * width * width,
            bytes_accessed=2 * width * width + 12 * rows * width,
            transcendentals=0,
        ),
        name="mix_pass",
    )(attended, x, w_out, gain_mix[None], gain_ffn[None])


def branch_kernel(
    g_ref, mid_ref, cot_ref, att_ref, w_ref, gm_ref, gf_ref,
    gmid_ref, gbr_ref, gatt_ref, ggf_ref, ggm_ref, total,
):
    j = pl.program_id(0)
    rows = att_ref.shape[0]
    cols = w_ref.shape[0]

    @pl.when(j == 0)
    def _():
        ggf_ref[...] = jnp.zeros_like(ggf_ref)
        total[...] = jnp.zeros_like(total)

        @pl.loop(0, rows // STEP)
        def _(r):
            at = pl.ds(pl.multiple_of(r * STEP, STEP), STEP)
            normal, scale = norm_parts(mid_ref[at])
            part, gain_part = norm_back(g_ref[at], normal, scale, gf_ref[...])
            ggf_ref[...] += gain_part[None]
            grad = cot_ref[at].astype(F32) + part
            gmid_ref[at] = grad
            gbr_ref[at] = grad.astype(BF16)

    here = pl.ds(pl.multiple_of(j * cols, cols), cols)
    total[...] += nn(gbr_ref[:, here], w_ref[...])

    @pl.when(j == pl.num_programs(0) - 1)
    def _():
        ggm_ref[...] = jnp.zeros_like(ggm_ref)

        @pl.loop(0, rows // STEP)
        def _(r):
            at = pl.ds(pl.multiple_of(r * STEP, STEP), STEP)
            normal, scale = norm_parts(att_ref[at].astype(F32))
            part, gain_part = norm_back(total[at], normal, scale, gm_ref[...])
            ggm_ref[...] += gain_part[None]
            gatt_ref[at] = part.astype(BF16)


def branch_pass(grad_ffn_in, middle, cot, attended, w_out, gain_mix, gain_ffn):
    rows, width = cot.shape
    cols = TILE
    n = width // cols
    whole = pl.BlockSpec((rows, width), lambda j: (0, 0))
    gain = pl.BlockSpec((1, width), lambda j: (0, 0))
    low = jax.ShapeDtypeStruct((rows, width), BF16)
    sums = jax.ShapeDtypeStruct((1, width), F32)
    return pl.pallas_call(
        branch_kernel,
        grid=(n,),
        out_shape=(jax.ShapeDtypeStruct((rows, width), F32), low, low, sums, sums),
        in_specs=[
            whole,
            whole,
            whole,
            whole,
            pl.BlockSpec((cols, width), lambda j: (j, 0)),
            gain,
            gain,
        ],
        out_specs=(whole, whole, whole, gain, gain),
        scratch_shapes=[pltpu.VMEM((rows, width), F32)],
        compiler_params=pltpu.CompilerParams(vmem_limit_bytes=40 * 1024 * 1024),
        cost_estimate=pl.CostEstimate(
            flops=2 * rows * width * width,
            bytes_accessed=2 * width * width + 20 * rows * width,
            transcendentals=0,
        ),
        name="branch_pass",
    )(grad_ffn_in, middle, cot, attended, w_out, gain_mix[None], gain_ffn[None])


def finish_kernel(
    n, depth, gq_ref, pw_ref, pn_ref, po_ref, gu_ref, oq_ref, ow_ref, sn_ref, so_ref, ou_ref,
    own, twin_in, held, zown, zin, zfin,
    local_sem, send_sem, recv_sem, keep_sem,
    up_send, up_recv, down_send, down_recv, home_send, home_recv, half_keep, half_send, half_recv,
):
    me, twin, near_x, near_y, across = places()
    z = lax.axis_index("batch")
    rows = pn_ref.shape[1]
    half = rows // 2
    low, high = pl.ds(0, half), pl.ds(half, half)
    mine = (across, near_x, near_y, me)
    chunk = zown.shape[1]
    turned = gq_ref.shape[0]
    chunks = zown.shape[0]
    per_part = turned // 3
    per_side = chunks // 2

    load_q = pltpu.make_async_copy(
        gq_ref, zown.at[pl.ds(0, turned)], local_sem.at[12]
    )
    load_q.start()
    partials = (pw_ref, pn_ref, po_ref)
    loads = [
        [
            pltpu.make_async_copy(p.at[block], own.at[m, i], local_sem.at[4 * m + i])
            for i, block in enumerate(mine)
        ]
        for m, p in enumerate(partials)
    ]
    for part in loads:
        for load in part:
            load.start()
    meet_all(n, depth)

    def copy(m, k, src, dst, partner):
        return remote(src, dst, send_sem.at[m, k], recv_sem.at[m, k], partner)

    twins = [
        [
            copy(m, i, p.at[block + twin], twin_in.at[m, i], me + twin)
            for i, block in enumerate(mine)
        ]
        for m, p in enumerate(partials)
    ]
    sends = [
        [
            copy(m, 4, own.at[m, 0, low], held.at[m, 0], near_x),
            copy(m, 5, own.at[m, 0, high], held.at[m, 1], near_y),
            copy(m, 6, own.at[m, 1, low], held.at[m, 2], near_x),
            copy(m, 7, own.at[m, 2, high], held.at[m, 3], near_y),
            copy(m, 8, own.at[m, 1, high], held.at[m, 4], near_x),
            copy(m, 9, own.at[m, 2, low], held.at[m, 5], near_y),
        ]
        for m in range(3)
    ]
    for part in twins:
        for send in part:
            send.start()

    def add_twin(m, i):
        loads[m][i].wait()
        twins[m][i].wait_recv()

        @pl.loop(0, rows // STEP)
        def _(r):
            at = pl.ds(pl.multiple_of(r * STEP, STEP), STEP)
            own[m, i, at] = (
                own[m, i, at].astype(F32) + twin_in[m, i, at].astype(F32)
            ).astype(BF16)

    def add_held(m, i, base, slot):
        @pl.loop(0, half // STEP)
        def _(r):
            at = pl.ds(pl.multiple_of(r * STEP, STEP), STEP)
            to = pl.ds(pl.multiple_of(base + r * STEP, STEP), STEP)
            own[m, i, to] = (
                own[m, i, to].astype(F32) + held[m, slot, at].astype(F32)
            ).astype(BF16)

    def first(m):
        add_twin(m, 0)
        sends[m][0].start()
        sends[m][1].start()
        add_twin(m, 1)
        sends[m][2].start()
        add_twin(m, 2)
        sends[m][3].start()

    def second(m):
        sends[m][1].wait_recv()
        add_held(m, 1, half, 1)
        sends[m][4].start()
        sends[m][0].wait_recv()
        add_held(m, 2, 0, 0)
        sends[m][5].start()

    def last(m, store):
        loads[m][3].wait()
        twins[m][3].wait_recv()
        for k in (2, 3, 4, 5):
            sends[m][k].wait_recv()
        for base, one, two in ((0, 2, 5), (half, 3, 4)):

            @pl.loop(0, half // STEP)
            def _(r):
                at = pl.ds(pl.multiple_of(r * STEP, STEP), STEP)
                place = base + r * STEP
                to = pl.ds(pl.multiple_of(place, STEP), STEP)
                store(
                    place,
                    own[m, 3, to].astype(F32)
                    + twin_in[m, 3, to].astype(F32)
                    + held[m, one, at].astype(F32)
                    + held[m, two, at].astype(F32),
                )

    def store_line(place, value):
        zown[
            turned + place // chunk,
            pl.ds(pl.multiple_of(lax.rem(place, chunk), STEP), STEP),
        ] = value.astype(BF16)

    def store_into(ref):
        def store(place, value):
            ref[pl.ds(pl.multiple_of(place, STEP), STEP)] = value

        return store

    def home(part):
        block = part * n + me
        return block // 3, lax.rem(block, 3)

    def deliver_far(g):
        target, slot = home(g // per_part)
        piece = lax.rem(g, per_part)
        return remote(
            zfin.at[g],
            oq_ref.at[slot, piece],
            home_send.at[g],
            home_recv.at[slot, piece],
            target,
        )

    def deliver_near(g):
        _, slot = home(g // per_part)
        return pltpu.make_async_copy(
            zfin.at[g], oq_ref.at[slot, lax.rem(g, per_part)], keep_sem.at[g]
        )

    def deliver_out(g):
        return pltpu.make_async_copy(zfin.at[g], ow_ref.at[g - turned], keep_sem.at[g])

    def deliver(g, wait):
        target, _ = home(g // per_part)

        @pl.when((g < turned) & (target != me))
        def _():
            deliver_far(g).wait_send() if wait else deliver_far(g).start()

        @pl.when((g < turned) & (target == me))
        def _():
            deliver_near(g).wait() if wait else deliver_near(g).start()

        @pl.when(g >= turned)
        def _():
            deliver_out(g).wait() if wait else deliver_out(g).start()

    def go_up(g, ahead):
        return line_remote(zown.at[g], zin.at[g], up_send.at[g], up_recv.at[g], ahead)

    def go_down(g, behind):
        return line_remote(
            zfin.at[g], zfin.at[g], down_send.at[g], down_recv.at[g], behind
        )

    def ranks(side):
        if side == 0:
            return z, z + 1, z - 1
        return depth - 1 - z, z - 1, z + 1

    def add_line(g, target):
        @pl.loop(0, chunk // STEP)
        def _(r):
            at = pl.ds(pl.multiple_of(r * STEP, STEP), STEP)
            target[g, at] = (zown[g, at].astype(F32) + zin[g, at].astype(F32)).astype(
                BF16
            )

    def line_step(t):
        half_step(t)
        for side in (0, 1):
            rank, ahead, behind = ranks(side)
            c = t - rank
            g = 2 * c + side
            there = (c >= 0) & (c < per_side)

            @pl.when(there & (rank == 0))
            def _():
                go_up(g, ahead).start()

            @pl.when(there & (rank > 0) & (rank < depth - 1))
            def _():
                go_up(g, behind).wait_recv()
                add_line(g, zown)
                go_up(g, ahead).start()

            @pl.when(there & (rank == depth - 1))
            def _():
                go_up(g, behind).wait_recv()
                add_line(g, zfin)
                go_down(g, behind).start()
                deliver(g, False)

            c_back = t - 2 * (depth - 1) + rank
            g_back = 2 * c_back + side
            there = (c_back >= 0) & (c_back < per_side) & (rank < depth - 1)

            @pl.when(there)
            def _():
                go_down(g_back, ahead).wait_recv()

            @pl.when(there & (rank > 0))
            def _():
                go_down(g_back, behind).start()

            @pl.when(there)
            def _():
                deliver(g_back, False)

    pieces = gu_ref.shape[0]

    def half_rank(side):
        return depth - 1 - z if side == 0 else z

    def half_keeps(side, c):
        return pltpu.make_async_copy(gu_ref.at[c], ou_ref.at[side, c], half_keep.at[c])

    def half_copy(side, c, source):
        return line_remote(
            source,
            ou_ref.at[side, c],
            half_send.at[side, c],
            half_recv.at[side, c],
            z - 1 if side == 0 else z + 1,
        )

    def half_land(side, c):
        place = ou_ref.at[side, c]
        return line_remote(
            place,
            place,
            half_send.at[side, c],
            half_recv.at[side, c],
            z + 1 if side == 0 else z - 1,
        )

    def half_step(t):
        for side in (0, 1):
            rank = half_rank(side)
            c = t - rank
            there = (c >= 0) & (c < pieces)

            @pl.when(there & (rank == 0))
            def _():
                half_keeps(side, c).start()
                half_copy(side, c, gu_ref.at[c]).start()

            @pl.when(there & (rank > 0))
            def _():
                half_land(side, c).wait_recv()

            @pl.when(there & (rank > 0) & (rank < depth - 1))
            def _():
                half_copy(side, c, ou_ref.at[side, c]).start()

    first(0)
    load_q.wait()
    line_step(0)
    line_step(1)
    first(1)
    line_step(2)
    second(0)
    line_step(3)
    last(0, store_line)
    for t in (4, 5, 6):
        line_step(t)
    first(2)
    line_step(7)
    second(1)
    line_step(8)
    last(1, store_into(sn_ref))
    for t in (9, 10):
        line_step(t)
    second(2)
    for t in range(11, per_side + 2 * (depth - 1) - 1):
        line_step(t)
    last(2, store_into(so_ref))
    line_step(per_side + 2 * (depth - 1) - 1)

    for m in range(3):
        for send in twins[m] + sends[m]:
            send.wait_send()
    for side in (0, 1):
        rank = half_rank(side)
        for c in range(pieces):

            @pl.when(rank == 0)
            def _():
                half_keeps(side, c).wait()
                half_copy(side, c, gu_ref.at[c]).wait_send()

            @pl.when((rank > 0) & (rank < depth - 1))
            def _():
                half_copy(side, c, ou_ref.at[side, c]).wait_send()

    for g in range(chunks):
        rank, ahead, behind = ranks(g % 2)

        @pl.when(rank < depth - 1)
        def _():
            go_up(g, ahead).wait_send()

        @pl.when(rank > 0)
        def _():
            go_down(g, behind).wait_send()

        deliver(g, True)
    for slot in range(3):
        block = 3 * me + slot
        source = lax.rem(block, n)

        @pl.when(source != me)
        def _():
            for piece in range(per_part):
                remote(
                    zfin.at[0],
                    oq_ref.at[slot, piece],
                    home_send.at[0],
                    home_recv.at[slot, piece],
                    source,
                ).wait_recv()


CHUNK = 64


def finish(grad_qkv, part_out, part_normed, part_outputs, grad_up, collective_id):
    n, depth = lax.axis_size("seq"), lax.axis_size("batch")
    rows, width = part_out.shape[0] // n, part_out.shape[1]
    cols = grad_qkv.shape[0] // 3
    if n != 8 or depth != 4:
        me = lax.axis_index("seq")
        blocks = lax.psum(grad_qkv, "batch").reshape(3, cols, width)
        back = [
            lax.ppermute(
                give_part(blocks, me, n, j),
                "seq",
                [((3 * d + j) % n, d) for d in range(n)],
            )
            for j in range(3)
        ]
        w_out = lax.psum(scatter_seq(part_out, None).astype(BF16), "batch")
        return (
            jnp.concatenate(back, axis=0),
            w_out,
            scatter_seq(part_normed, None),
            scatter_seq(part_outputs, None),
            grad_up,
        )
    pieces = grad_up.shape[0] // CHUNK
    turned, chunks = 3 * cols // CHUNK, (3 * cols + rows) // CHUNK
    inside = pl.BlockSpec(memory_space=pltpu.VMEM)
    dma = pltpu.SemaphoreType.DMA
    line = pltpu.VMEM((chunks, CHUNK, width), BF16)
    w_qkv, w_out, normed, outputs, w_up = pl.pallas_call(
        functools.partial(finish_kernel, n, depth),
        out_shape=(
            jax.ShapeDtypeStruct((3, cols // CHUNK, CHUNK, width), BF16),
            jax.ShapeDtypeStruct((rows // CHUNK, CHUNK, width), BF16),
            jax.ShapeDtypeStruct((rows, width), F32),
            jax.ShapeDtypeStruct((rows, width), F32),
            jax.ShapeDtypeStruct((2, pieces, CHUNK, width), BF16),
        ),
        in_specs=[ANY] * 5,
        out_specs=(ANY, ANY, inside, inside, ANY),
        scratch_shapes=[
            pltpu.VMEM((3, 4, rows, width), BF16),
            pltpu.VMEM((3, 4, rows, width), BF16),
            pltpu.VMEM((3, 6, rows // 2, width), BF16),
            line,
            line,
            line,
            dma((13,)),
            dma((3, 10)),
            dma((3, 10)),
            dma((chunks,)),
            dma((chunks,)),
            dma((chunks,)),
            dma((chunks,)),
            dma((chunks,)),
            dma((chunks,)),
            dma((3, cols // CHUNK)),
            dma((pieces,)),
            dma((2, pieces)),
            dma((2, pieces)),
        ],
        compiler_params=pltpu.CompilerParams(
            collective_id=collective_id,
            has_side_effects=True,
            vmem_limit_bytes=58 * 1024 * 1024,
        ),
        name="finish",
    )(
        grad_qkv.reshape(turned, CHUNK, width),
        *[p.reshape(n, rows, width) for p in (part_out, part_normed, part_outputs)],
        grad_up.reshape(pieces, CHUNK, width),
    )
    return (
        w_qkv.reshape(3 * cols, width),
        w_out.reshape(rows, width),
        normed,
        outputs,
        w_up.reshape(-1, width),
    )


def half_hop(grad, came, hop):
    n, depth = lax.axis_size("seq"), lax.axis_size("batch")
    if n != 8 or depth != 4:
        return lax.psum(grad, "batch") if hop == 1 else came
    z = lax.axis_index("batch")
    rows = grad.shape[0] // 2
    low, high = grad[:rows], grad[rows:]
    part = jnp.where(z == hop - 1, low, high)
    if hop > 1:
        part = (part.astype(F32) + came.astype(F32)).astype(BF16)
    if hop == depth:
        return part
    pairs = [(hop - 1, hop), (depth - hop, depth - 1 - hop)]
    return lax.ppermute(part, "batch", pairs)


def gains_kernel(
    n, depth, a_ref, b_ref, oa_ref, ob_ref, held_a, held_b, pack, held_c, send_sem, recv_sem, last_send, last_recv
):
    me = lax.axis_index("seq")
    z = lax.axis_index("batch")
    p, q = a_ref.shape[0], b_ref.shape[0]
    barrier = pltpu.get_barrier_semaphore()
    for k in range(1, n):
        pl.semaphore_signal(
            barrier, inc=1, device_id={"seq": lax.rem(me + k, n)}, device_id_type=MESH
        )
    for k in range(1, depth):
        pl.semaphore_signal(
            barrier,
            inc=1,
            device_id={"batch": lax.rem(z + k, depth)},
            device_id_type=MESH,
        )
    pl.semaphore_wait(barrier, n + depth - 2)
    held_a[me] = a_ref[...]
    held_b[me] = b_ref[...]
    copies = []
    for k in range(1, n):
        partner = lax.rem(me + k, n)
        copies.append(
            remote(a_ref, held_a.at[me], send_sem.at[0, k], recv_sem.at[0, k], partner)
        )
        copies.append(
            remote(b_ref, held_b.at[me], send_sem.at[1, k], recv_sem.at[1, k], partner)
        )
    for copy in copies:
        copy.start()
    for copy in copies:
        copy.wait()
    total = held_a[0]
    for d in range(1, n):
        total = total + held_a[d]
    pack[0:p] = total
    for d in range(n):
        pack[p + d * q : p + (d + 1) * q] = held_b[d]
    held_c[z] = pack[...]
    copies = [
        pltpu.make_async_remote_copy(
            src_ref=pack,
            dst_ref=held_c.at[z],
            send_sem=last_send.at[k],
            recv_sem=last_recv.at[k],
            device_id={"batch": lax.rem(z + k, depth)},
            device_id_type=MESH,
        )
        for k in range(1, depth)
    ]
    for copy in copies:
        copy.start()
    for copy in copies:
        copy.wait()
    total = held_c[0]
    for d in range(1, depth):
        total = total + held_c[d]
    oa_ref[...] = total[0:p]
    ob_ref[...] = total[p:]


def sum_gains(shared, mine, collective_id):
    n, depth = lax.axis_size("seq"), lax.axis_size("batch")
    p, q = shared.shape[0], mine.shape[0]
    inside = pl.BlockSpec(memory_space=pltpu.VMEM)
    return pl.pallas_call(
        functools.partial(gains_kernel, n, depth),
        out_shape=(
            jax.ShapeDtypeStruct((p, 128), F32),
            jax.ShapeDtypeStruct((n * q, 128), F32),
        ),
        in_specs=[inside, inside],
        out_specs=(inside, inside),
        scratch_shapes=[
            pltpu.VMEM((n, p, 128), F32),
            pltpu.VMEM((n, q, 128), F32),
            pltpu.VMEM((p + n * q, 128), F32),
            pltpu.VMEM((depth, p + n * q, 128), F32),
            pltpu.SemaphoreType.DMA((2, n)),
            pltpu.SemaphoreType.DMA((2, n)),
            pltpu.SemaphoreType.DMA((depth,)),
            pltpu.SemaphoreType.DMA((depth,)),
        ],
        compiler_params=pltpu.CompilerParams(
            collective_id=collective_id, has_side_effects=True
        ),
        name="sum_gains",
    )(shared, mine)


def body(
    inputs,
    segment_ids,
    w_qkv,
    w_out,
    w_up,
    w_down,
    gain_attn,
    gain_mix,
    gain_ffn,
    gain_hidden,
    cotangent,
):
    _, local, width = inputs.shape
    n, depth = lax.axis_size("seq"), lax.axis_size("batch")
    me = lax.axis_index("seq")
    length = local * n
    feats = w_up.shape[0]
    x_low = inputs[0]
    x = x_low.astype(F32)
    cot = cotangent[0]
    segment = segment_ids[0]

    w_out_full = lax.all_gather(w_out, "seq", axis=0, tiled=True)
    normal_attn, scale_attn = norm_parts(x)
    normed = (normal_attn * gain_attn).astype(BF16)
    before = [jnp.sum((segment < d).astype(jnp.int32)) for d in range(1, DOCS)]
    start = jnp.zeros_like(segment)
    for d in range(1, DOCS):
        start = jnp.where(segment == d, before[d - 1], start)
    positions = jnp.arange(length, dtype=jnp.int32) - start
    first = start[::TILE] // TILE
    start_row = start[None, :]

    normed_full, (wq, wk, wv), w_down_near, tables = start_exchange(
        normed, w_qkv, w_down, positions.astype(F32), 1
    )
    cot_late, _ = lax.optimization_barrier((cot, wq))
    cot_full = lax.all_gather(cot_late, "seq", axis=0, tiled=True)

    q, k, v, kt, vt = project_qkv(normed_full, wq, wk, wv, tables)
    attended_heads, lse = attend(first, start_row, q, k, vt)
    attended = heads_to_tokens(attended_heads, 2)
    mix_in, middle, ffn_in = mix_pass(attended, x_low, w_out_full, gain_mix, gain_ffn)
    ffn_full, w_down_cols = gather_seq(ffn_in, w_down_near, 3)

    gain_here = lax.dynamic_slice_in_dim(gain_hidden, me * feats, feats, 0)[None, :]
    act, slope, grad_hidden, stat = upper_pass(
        ffn_full, w_up, cot_full, w_down_cols, gain_here
    )
    stats = join_stats(stat, feats, 8)
    hidden, grad_upper, grad_gain_here = hidden_pass(act, slope, grad_hidden, stats, gain_here)

    grad_w_down = tn(cot_full, hidden).astype(BF16)
    grad_upper, grad_w_down = lax.optimization_barrier((grad_upper, grad_w_down))
    grad_w_up = tn(grad_upper, ffn_full).astype(BF16)
    grad_upper, grad_w_up = lax.optimization_barrier((grad_upper, grad_w_up))
    down_part = lax.psum_scatter(
        grad_w_down.reshape(n, local, feats), "batch", scatter_dimension=1, tiled=True
    )
    hop_one = half_hop(grad_w_up, None, 1)
    grad_ffn_in = scatter_seq(nn(grad_upper, w_up).astype(BF16), 4)
    hop_one, grad_ffn_in = lax.optimization_barrier((hop_one, grad_ffn_in))
    hop_two = half_hop(grad_w_up, hop_one, 2)
    grad_middle, grad_branch, grad_att, grad_gain_ffn, grad_gain_mix = branch_pass(
        grad_ffn_in, middle, cot, attended, w_out_full, gain_mix, gain_ffn
    )
    grad_heads = tokens_to_heads(grad_att, 5)
    down_part, grad_heads = lax.optimization_barrier((down_part, grad_heads))
    down_part = lax.all_to_all(down_part, "seq", split_axis=0, concat_axis=0, tiled=True)
    down_part = jnp.swapaxes(down_part, 0, 1).reshape(local // depth, n * feats)
    grad_w_down = lax.all_gather(down_part, "batch", axis=0, tiled=True)

    dq, dk, dv = attend_back(
        first, start_row, q, k, kt, v, attended_heads, lse, grad_heads, tables
    )
    hop_two, dq = lax.optimization_barrier((hop_two, dq))
    hop_three = half_hop(grad_w_up, hop_two, 3)
    grads = jnp.concatenate([dq, dk, dv], axis=1)
    weights = jnp.concatenate([wq, wk, wv], axis=0)
    grad_w_qkv, grad_w_out, grad_normed, down_sum, grad_w_up = finish(
        tn(grads, normed_full).astype(BF16),
        tn(grad_branch, mix_in).astype(BF16),
        nn(grads, weights).astype(BF16),
        nt(hidden, w_down_cols).astype(BF16),
        half_hop(grad_w_up, hop_three, depth),
        6,
    )
    grad_part, grad_gain_attn = norm_back(grad_normed, normal_attn, scale_attn, gain_attn)
    grad_inputs = grad_middle + grad_part
    outputs = (middle + down_sum).astype(BF16)
    shared, hidden_gains = sum_gains(
        jnp.concatenate([grad_gain_attn, grad_gain_mix[0], grad_gain_ffn[0]]).reshape(-1, 128),
        grad_gain_here.reshape(-1, 128),
        9,
    )
    shared = shared.reshape(-1)
    return (
        outputs[None],
        grad_inputs[None],
        grad_w_qkv.astype(F32),
        grad_w_out.astype(F32),
        grad_w_up.astype(F32),
        grad_w_down.astype(F32),
        shared[:width],
        shared[width : 2 * width],
        shared[2 * width :],
        hidden_gains.reshape(-1),
    )


def pick_part(turned, me, n, part):
    chosen = turned[0]
    home = part * n + me
    for j in (1, 2):
        chosen = jnp.where(lax.rem(home, 3) == j, turned[j], chosen)
    return chosen


def give_part(blocks, me, n, j):
    chosen = blocks[0]
    for part in (1, 2):
        chosen = jnp.where(lax.rem(part * n + me, 3) == j, blocks[part], chosen)
    return chosen


def solution(mesh):
    in_specs = (
        P("batch", "seq", None),
        P("batch", None),
        P("seq", None),
        P("seq", None),
        P("seq", None),
        P("seq", None),
        P(),
        P(),
        P(),
        P(),
        P("batch", "seq", None),
    )
    out_specs = (
        P("batch", "seq", None),
        P("batch", "seq", None),
        P("seq", None),
        P("seq", None),
        P("seq", None),
        P("seq", None),
        P(),
        P(),
        P(),
        P(),
    )
    return jax.shard_map(body, mesh=mesh, in_specs=in_specs, out_specs=out_specs, check_vma=False)
```

```python
import functools
import math

import jax
import jax.numpy as jnp
from jax import lax
from jax.experimental import pallas as pl
from jax.experimental.pallas import tpu as pltpu
from jax.sharding import PartitionSpec as P

HEADS = 32
HEAD_DIM = 64
LENGTH = 2048
XBASE = 512
DOCS = 4
EPSILON = 1e-05
MASKED = -1e30
TILE = 256

MESH = pl.DeviceIdType.MESH
F32 = jnp.float32
BF16 = jnp.bfloat16
ANY = pl.BlockSpec(memory_space=pl.ANY)
INSIDE = pl.BlockSpec(memory_space=pltpu.VMEM)


def nn(a, b):
    return lax.dot_general(a, b, (((1,), (0,)), ((), ())), preferred_element_type=F32)


def nt(a, b):
    return lax.dot_general(a, b, (((1,), (1,)), ((), ())), preferred_element_type=F32)


def tn(a, b):
    return lax.dot_general(a, b, (((0,), (0,)), ((), ())), preferred_element_type=F32)


def norm_parts(values):
    average = jnp.mean(values, axis=-1, keepdims=True)
    centered = values - average
    spread = jnp.mean(centered * centered, axis=-1, keepdims=True)
    scale = lax.rsqrt(spread + EPSILON)
    return centered * scale, scale


def norm_back(grad, normal, scale, gain):
    part = grad * gain
    inner = (
        part
        - jnp.mean(part, axis=-1, keepdims=True)
        - normal * jnp.mean(part * normal, axis=-1, keepdims=True)
    )
    return scale * inner, jnp.sum(grad * normal, axis=0)


def places():
    me = lax.axis_index("seq")
    core = lax.rem(me, 2)
    along_x = lax.rem(me // 2, 2)
    along_y = me // 4
    twin = 1 - 2 * core
    near_x = me + 2 - 4 * along_x
    near_y = me + 4 - 8 * along_y
    across = near_x + 4 - 8 * along_y
    return me, twin, near_x, near_y, across


def remote(src, dst, send_sem, recv_sem, partner):
    return pltpu.make_async_remote_copy(
        src_ref=src,
        dst_ref=dst,
        send_sem=send_sem,
        recv_sem=recv_sem,
        device_id={"seq": partner},
        device_id_type=MESH,
    )


def meet(partners):
    barrier = pltpu.get_barrier_semaphore()
    for partner in partners:
        pl.semaphore_signal(
            barrier, inc=1, device_id={"seq": partner}, device_id_type=MESH
        )
    pl.semaphore_wait(barrier, len(partners))


def gather_copies(x_ref, o_ref, send_sem, recv_sem):
    me, twin, near_x, near_y, across = places()
    half = x_ref.shape[0] // 2
    low, high = pl.ds(0, half), pl.ds(half, half)

    def copy(k, src, dst, partner):
        return remote(src, dst, send_sem.at[k], recv_sem.at[k], partner)

    def relay(k, owner, rows, partner):
        place = o_ref.at[owner, rows]
        return copy(k, place, place, partner)

    return [
        copy(0, x_ref.at[low], o_ref.at[me, low], near_x),
        copy(1, x_ref.at[high], o_ref.at[me, high], near_y),
        copy(2, x_ref.at[high], o_ref.at[me, high], near_x),
        copy(3, x_ref.at[low], o_ref.at[me, low], near_y),
        copy(4, x_ref, o_ref.at[me], me + twin),
        relay(5, near_x, low, near_y),
        relay(6, near_y, high, near_x),
        relay(7, near_x, low, me + twin),
        relay(8, near_y, high, me + twin),
        relay(9, near_x, high, me + twin),
        relay(10, near_y, low, me + twin),
        relay(11, across, low, me + twin),
        relay(12, across, high, me + twin),
    ]


def gather_run(sends, between=None):
    sends[0].wait_recv()
    sends[5].start()
    sends[7].start()
    sends[1].wait_recv()
    sends[6].start()
    sends[8].start()
    sends[2].wait_recv()
    sends[9].start()
    sends[3].wait_recv()
    sends[10].start()
    if between is not None:
        between()
    sends[5].wait_recv()
    sends[11].start()
    sends[6].wait_recv()
    sends[12].start()
    for k in (4, 7, 8, 9, 10, 11, 12):
        sends[k].wait_recv()
    for send in sends:
        send.wait_send()


def meet_all(n, depth):
    me = lax.axis_index("seq")
    z = lax.axis_index("batch")
    barrier = pltpu.get_barrier_semaphore()
    for k in range(1, n):
        pl.semaphore_signal(
            barrier, inc=1, device_id={"seq": lax.rem(me + k, n)}, device_id_type=MESH
        )
    for sign in (-1, 1):

        @pl.when((z + sign >= 0) & (z + sign < depth))
        def _():
            pl.semaphore_signal(
                barrier, inc=1, device_id={"batch": z + sign}, device_id_type=MESH
            )

    ends = (z == 0).astype(jnp.int32) + (z == depth - 1).astype(jnp.int32)
    pl.semaphore_wait(barrier, n + 1 - ends)


def line_remote(src, dst, send_sem, recv_sem, partner):
    return pltpu.make_async_remote_copy(
        src_ref=src,
        dst_ref=dst,
        send_sem=send_sem,
        recv_sem=recv_sem,
        device_id={"batch": partner},
        device_id_type=MESH,
    )


class Line:
    def __init__(self, depth, source, target, send_sem, recv_sem):
        self.depth, self.source, self.target = depth, source, target
        self.send_sem, self.recv_sem = send_sem, recv_sem
        self.z = lax.axis_index("batch")

    def message(self, side, k):
        sign = 2 * side - 1
        owner = self.z - sign * k
        return line_remote(
            self.source(owner, k),
            self.target(owner),
            self.send_sem.at[side, k],
            self.recv_sem.at[side, k],
            self.z + sign,
        )

    def sends(self, side, k):
        sign = 2 * side - 1
        owner, target = self.z - sign * k, self.z + sign
        inside = (owner >= 0) & (owner < self.depth)
        return inside & (target >= 0) & (target < self.depth)

    def land(self, k):
        for side in (0, 1):
            sign = 2 * side - 1
            owner = self.z - sign * (k + 1)

            @pl.when((owner >= 0) & (owner < self.depth))
            def _():
                place = self.target(owner)
                line_remote(
                    place,
                    place,
                    self.send_sem.at[side, k],
                    self.recv_sem.at[side, k],
                    self.z - sign,
                ).wait_recv()

    def start(self, k):
        for side in (0, 1):

            @pl.when(self.sends(side, k))
            def _():
                self.message(side, k).start()

    def sent(self, k):
        for side in (0, 1):

            @pl.when(self.sends(side, k))
            def _():
                self.message(side, k).wait_send()


def gather_kernel(
    n, depth, x_ref, near_ref, o_ref, all_ref, keep_ref, local_sem, send_sem, recv_sem, line_send, line_recv
):
    me, twin, near_x, near_y, _ = places()
    z = lax.axis_index("batch")
    own = pltpu.make_async_copy(x_ref, o_ref.at[me], local_sem.at[0])
    own.start()

    def load(shift):
        return pltpu.make_async_copy(
            near_ref.at[:, z + shift], keep_ref.at[1 + shift], local_sem.at[2 + shift]
        )

    def keep(shift):
        return pltpu.make_async_copy(
            keep_ref.at[1 + shift], all_ref.at[:, z + shift], local_sem.at[5 + shift]
        )

    def kept(shift):
        return (z + shift >= 0) & (z + shift < depth)

    for shift in (-1, 0, 1):

        @pl.when(kept(shift))
        def _():
            load(shift).start()

    meet_all(n, depth)
    sends = gather_copies(x_ref, o_ref, send_sem, recv_sem)
    for k in range(5):
        sends[k].start()
    line = Line(
        depth,
        lambda owner, k: (near_ref if k == 1 else all_ref).at[:, owner],
        lambda owner: all_ref.at[:, owner],
        line_send,
        line_recv,
    )
    line.start(1)
    for shift in (-1, 0, 1):

        @pl.when(kept(shift))
        def _():
            load(shift).wait()
            keep(shift).start()

    def between():
        for k in range(2, depth - 1):
            line.land(k - 1)
            line.start(k)

    gather_run(sends, between)
    line.land(depth - 2)
    for k in range(1, depth - 1):
        line.sent(k)
    for shift in (-1, 0, 1):

        @pl.when(kept(shift))
        def _():
            keep(shift).wait()

    own.wait()


def gather_seq(block, near, collective_id):
    n, depth = lax.axis_size("seq"), lax.axis_size("batch")
    rows, width = block.shape
    if n != 8:
        return lax.all_gather(block, "seq", axis=0, tiled=True), near
    gathered, every = pl.pallas_call(
        functools.partial(gather_kernel, n, depth),
        out_shape=(
            jax.ShapeDtypeStruct((n, rows, width), block.dtype),
            jax.ShapeDtypeStruct(near.shape, near.dtype),
        ),
        in_specs=[INSIDE, ANY],
        out_specs=(ANY, ANY),
        scratch_shapes=[
            pltpu.VMEM((3, n, *near.shape[2:]), near.dtype),
            pltpu.SemaphoreType.DMA((7,)),
            pltpu.SemaphoreType.DMA((13,)),
            pltpu.SemaphoreType.DMA((13,)),
            pltpu.SemaphoreType.DMA((2, depth)),
            pltpu.SemaphoreType.DMA((2, depth)),
        ],
        compiler_params=pltpu.CompilerParams(
            collective_id=collective_id, has_side_effects=True
        ),
        name="gather_seq",
    )(block, near)
    return gathered.reshape(n * rows, width), every.reshape(-1, near.shape[-1])


def lane_tables(place):
    half = HEAD_DIM // 2
    lane = lax.broadcasted_iota(jnp.int32, (1, 128), 1)
    channel = lax.rem(lane, half).astype(F32)
    inverse = jnp.exp(channel * (-math.log(10000.0) / half))
    zeta = (channel * (2.0 / HEAD_DIM) + 0.4) / 1.4
    sign = jnp.where(lax.rem(lane, HEAD_DIM) < half, -1.0, 1.0)
    angle = place * inverse
    growth = jnp.exp((place - 0.5 * LENGTH) * (1.0 / XBASE) * jnp.log(zeta))
    shrink = 1.0 / growth
    cosine = jnp.cos(angle)
    sine = jnp.sin(angle) * sign
    return cosine * growth, sine * growth, cosine * shrink, sine * shrink


def start_kernel(
    n, depth, x_ref, w_ref, wd_ref, pos_ref,
    o_ref, wq_ref, wk_ref, wv_ref, wc_ref, cq_ref, sq_ref, ck_ref, sk_ref,
    keep_w, keep_c, local_sem, send_sem, recv_sem, hop_send, hop_recv, col_send, col_recv, line_send, line_recv,
):
    z = lax.axis_index("batch")
    rows_z = wc_ref.shape[2]
    cols = wc_ref.shape[3]
    me, twin, near_x, near_y, _ = places()
    parts = (wq_ref, wk_ref, wv_ref)
    own = pltpu.make_async_copy(x_ref, o_ref.at[me], local_sem.at[0])
    own.start()
    wd_rows = pl.ds(pl.multiple_of(z * rows_z, rows_z), rows_z)

    def column(k):
        return wd_ref.at[wd_rows, pl.ds(pl.multiple_of(k * cols, cols), cols)]

    load_column = pltpu.make_async_copy(column(me), keep_c, local_sem.at[4])
    own_column = pltpu.make_async_copy(keep_c, wc_ref.at[me, z], local_sem.at[5])
    load_column.start()
    meet_all(n, depth)
    load_column.wait()
    own_column.start()
    turns = [
        remote(
            column(lax.rem(me + k, n)),
            wc_ref.at[me, z],
            col_send.at[k],
            col_recv.at[k],
            lax.rem(me + k, n),
        )
        for k in range(1, n)
    ]
    for turn in turns:
        turn.start()
    sends = gather_copies(x_ref, o_ref, send_sem, recv_sem)
    for k in range(5):
        sends[k].start()

    line = Line(
        depth,
        lambda owner, k: wc_ref.at[:, owner],
        lambda owner: wc_ref.at[:, owner],
        line_send,
        line_recv,
    )

    def hop(j, part, target):
        return remote(
            w_ref.at[j], parts[part], hop_send.at[j], hop_recv.at[part], target
        )

    def load(j):
        return pltpu.make_async_copy(w_ref.at[j], keep_w, local_sem.at[6])

    def here(j, part):
        return pltpu.make_async_copy(keep_w, parts[part], local_sem.at[1 + j])

    for j in range(3):
        block = 3 * me + j
        target = lax.rem(block, n)
        for part in range(3):
            inside = block // n == part

            @pl.when(inside & (target != me))
            def _():
                hop(j, part, target).start()

            @pl.when(inside & (target == me))
            def _():
                load(j).start()
                load(j).wait()
                here(j, part).start()

    @pl.loop(0, pos_ref.shape[0])
    def _(r):
        at = pl.ds(pl.multiple_of(r * 128, 128), 128)
        places_here = jnp.broadcast_to(pos_ref[pl.ds(r, 1), :], (128, 128)).T
        tables = lane_tables(places_here)
        for ref, table in zip((cq_ref, sq_ref, ck_ref, sk_ref), tables, strict=True):
            ref[at] = table

    own_column.wait()
    for turn in turns:
        turn.wait_recv()
    line.start(0)
    gather_run(sends)
    line.land(0)
    line.sent(0)
    for turn in turns:
        turn.wait_send()
    for j in range(3):
        block = 3 * me + j
        target = lax.rem(block, n)

        for part in range(3):
            inside = block // n == part

            @pl.when(inside & (target != me))
            def _():
                hop(j, part, target).wait_send()

            @pl.when(inside & (target == me))
            def _():
                here(j, part).wait()

    for part in range(3):
        source = (part * n + me) // 3

        @pl.when(source != me)
        def _():
            hop(0, part, source).wait_recv()

    own.wait()


def start_exchange(block, w_qkv, w_down, positions, collective_id):
    n, depth = lax.axis_size("seq"), lax.axis_size("batch")
    rows, width = block.shape
    piece = w_qkv.shape[0] // 3
    w = w_qkv.reshape(3, piece, width)
    if n != 8:
        me = lax.axis_index("seq")
        turned = [
            lax.ppermute(w[j], "seq", [(d, (3 * d + j) % n) for d in range(n)])
            for j in range(3)
        ]
        parts = [pick_part(turned, me, n, part) for part in range(3)]
        place = jnp.broadcast_to(positions[:, None], (positions.shape[0], 128))
        return (
            lax.all_gather(block, "seq", axis=0, tiled=True),
            parts,
            lax.all_to_all(w_down, "seq", split_axis=1, concat_axis=0, tiled=True),
            lane_tables(place),
        )
    rows_z, cols = w_down.shape[0] // depth, w_down.shape[1] // n
    inside = pl.BlockSpec(memory_space=pltpu.VMEM)
    table = jax.ShapeDtypeStruct((n * rows, 128), F32)
    part = jax.ShapeDtypeStruct((piece, width), w.dtype)
    gathered, wq, wk, wv, columns, *tables = pl.pallas_call(
        functools.partial(start_kernel, n, depth),
        out_shape=(
            jax.ShapeDtypeStruct((n, rows, width), block.dtype),
            part,
            part,
            part,
            jax.ShapeDtypeStruct((n, depth, rows_z, cols), w_down.dtype),
            *([table] * 4),
        ),
        in_specs=[INSIDE, ANY, ANY, INSIDE],
        out_specs=(ANY, ANY, ANY, ANY, ANY, *([INSIDE] * 4)),
        scratch_shapes=[
            pltpu.VMEM((piece, width), BF16),
            pltpu.VMEM((rows_z, cols), BF16),
            pltpu.SemaphoreType.DMA((7,)),
            pltpu.SemaphoreType.DMA((13,)),
            pltpu.SemaphoreType.DMA((13,)),
            pltpu.SemaphoreType.DMA((3,)),
            pltpu.SemaphoreType.DMA((3,)),
            pltpu.SemaphoreType.DMA((n,)),
            pltpu.SemaphoreType.DMA((n,)),
            pltpu.SemaphoreType.DMA((2, depth)),
            pltpu.SemaphoreType.DMA((2, depth)),
        ],
        compiler_params=pltpu.CompilerParams(
            collective_id=collective_id, has_side_effects=True
        ),
        name="start_exchange",
    )(block, w, w_down, positions.reshape(-1, 128))
    return gathered.reshape(n * rows, width), (wq, wk, wv), columns, tables


def scatter_kernel(
    p_ref, o_ref, own, twin_in, held, local_sem, send_sem, recv_sem
):
    me, twin, near_x, near_y, across = places()
    rows = p_ref.shape[1]
    half = rows // 2
    low, high = pl.ds(0, half), pl.ds(half, half)
    mine = (across, near_x, near_y, me)

    loads = [
        pltpu.make_async_copy(p_ref.at[block], own.at[i], local_sem.at[i])
        for i, block in enumerate(mine)
    ]
    for load in loads:
        load.start()
    meet((me + twin, near_x, near_y))

    def copy(k, src, dst, partner):
        return remote(src, dst, send_sem.at[k], recv_sem.at[k], partner)

    twins = [
        copy(i, p_ref.at[block + twin], twin_in.at[i], me + twin)
        for i, block in enumerate(mine)
    ]
    for send in twins:
        send.start()
    sends = [
        copy(4, own.at[0, low], held.at[0], near_x),
        copy(5, own.at[0, high], held.at[1], near_y),
        copy(6, own.at[1, low], held.at[2], near_x),
        copy(7, own.at[2, high], held.at[3], near_y),
        copy(8, own.at[1, high], held.at[4], near_x),
        copy(9, own.at[2, low], held.at[5], near_y),
    ]
    step = 32

    def add_twin(i):
        loads[i].wait()
        twins[i].wait_recv()

        @pl.loop(0, rows // step)
        def _(r):
            at = pl.ds(pl.multiple_of(r * step, step), step)
            own[i, at] = (
                own[i, at].astype(F32) + twin_in[i, at].astype(F32)
            ).astype(own.dtype)

    def add_held(i, base, slot):
        @pl.loop(0, half // step)
        def _(r):
            at = pl.ds(pl.multiple_of(r * step, step), step)
            to = pl.ds(pl.multiple_of(base + r * step, step), step)
            own[i, to] = (
                own[i, to].astype(F32) + held[slot, at].astype(F32)
            ).astype(own.dtype)

    add_twin(0)
    sends[0].start()
    sends[1].start()
    add_twin(1)
    sends[2].start()
    add_twin(2)
    sends[3].start()
    sends[1].wait_recv()
    add_held(1, half, 1)
    sends[4].start()
    sends[0].wait_recv()
    add_held(2, 0, 0)
    sends[5].start()
    loads[3].wait()
    twins[3].wait_recv()
    for k in (2, 3, 4, 5):
        sends[k].wait_recv()

    def final(base, first, second):
        @pl.loop(0, half // step)
        def _(r):
            at = pl.ds(pl.multiple_of(r * step, step), step)
            to = pl.ds(pl.multiple_of(base + r * step, step), step)
            o_ref[to] = (
                own[3, to].astype(F32)
                + twin_in[3, to].astype(F32)
                + held[first, at].astype(F32)
                + held[second, at].astype(F32)
            )

    final(0, 2, 5)
    final(half, 3, 4)
    for send in twins + sends:
        send.wait_send()


def scatter_seq(partial, collective_id):
    n = lax.axis_size("seq")
    rows, width = partial.shape[0] // n, partial.shape[1]
    if n != 8:
        return lax.psum_scatter(
            partial, "seq", scatter_dimension=0, tiled=True
        ).astype(F32)
    return pl.pallas_call(
        scatter_kernel,
        out_shape=jax.ShapeDtypeStruct((rows, width), F32),
        in_specs=[ANY],
        out_specs=pl.BlockSpec(memory_space=pltpu.VMEM),
        scratch_shapes=[
            pltpu.VMEM((4, rows, width), BF16),
            pltpu.VMEM((4, rows, width), BF16),
            pltpu.VMEM((6, rows // 2, width), BF16),
            pltpu.SemaphoreType.DMA((4,)),
            pltpu.SemaphoreType.DMA((10,)),
            pltpu.SemaphoreType.DMA((10,)),
        ],
        compiler_params=pltpu.CompilerParams(
            collective_id=collective_id,
            has_side_effects=True,
            vmem_limit_bytes=32 * 1024 * 1024,
        ),
        name="scatter_seq",
    )(partial.reshape(n, rows, width))


def heads_to_tokens_kernel(n, x_ref, o_ref, keep, local_sem, send_sem, recv_sem):
    me = lax.axis_index("seq")
    rows = o_ref.shape[0]
    cols = x_ref.shape[1]
    exchange(
        n,
        me,
        lambda k: x_ref.at[pl.ds(pl.multiple_of(k * rows, rows), rows)],
        o_ref.at[:, pl.ds(pl.multiple_of(me * cols, cols), cols)],
        keep,
        local_sem,
        send_sem,
        recv_sem,
    )


def exchange(n, me, source, target, keep, local_sem, send_sem, recv_sem):
    load = pltpu.make_async_copy(source(me), keep, local_sem.at[0])
    own = pltpu.make_async_copy(keep, target, local_sem.at[1])
    load.start()
    barrier = pltpu.get_barrier_semaphore()
    for k in range(1, n):
        pl.semaphore_signal(
            barrier,
            inc=1,
            device_id={"seq": lax.rem(me + k, n)},
            device_id_type=MESH,
        )
    pl.semaphore_wait(barrier, n - 1)
    copies = []
    for k in range(1, n):
        partner = lax.rem(me + k, n)
        copies.append(
            pltpu.make_async_remote_copy(
                src_ref=source(partner),
                dst_ref=target,
                send_sem=send_sem.at[k],
                recv_sem=recv_sem.at[k],
                device_id={"seq": partner},
                device_id_type=MESH,
            )
        )
        copies[-1].start()
    load.wait()
    own.start()
    for copy in copies:
        copy.wait()
    own.wait()


def heads_to_tokens(heads, collective_id):
    n = lax.axis_size("seq")
    total, cols = heads.shape
    rows = total // n
    return pl.pallas_call(
        functools.partial(heads_to_tokens_kernel, n),
        out_shape=jax.ShapeDtypeStruct((rows, n * cols), heads.dtype),
        in_specs=[ANY],
        out_specs=ANY,
        scratch_shapes=[
            pltpu.VMEM((rows, cols), heads.dtype),
            pltpu.SemaphoreType.DMA((2,)),
            pltpu.SemaphoreType.DMA((n,)),
            pltpu.SemaphoreType.DMA((n,)),
        ],
        compiler_params=pltpu.CompilerParams(
            collective_id=collective_id, has_side_effects=True
        ),
        name="heads_to_tokens",
    )(heads)


def tokens_to_heads_kernel(n, x_ref, o_ref, keep, local_sem, send_sem, recv_sem):
    me = lax.axis_index("seq")
    rows = x_ref.shape[0]
    cols = o_ref.shape[1]
    exchange(
        n,
        me,
        lambda k: x_ref.at[:, pl.ds(pl.multiple_of(k * cols, cols), cols)],
        o_ref.at[pl.ds(pl.multiple_of(me * rows, rows), rows)],
        keep,
        local_sem,
        send_sem,
        recv_sem,
    )


def tokens_to_heads(tokens, collective_id):
    n = lax.axis_size("seq")
    rows, total = tokens.shape
    return pl.pallas_call(
        functools.partial(tokens_to_heads_kernel, n),
        out_shape=jax.ShapeDtypeStruct((rows * n, total // n), tokens.dtype),
        in_specs=[ANY],
        out_specs=ANY,
        scratch_shapes=[
            pltpu.VMEM((rows, total // n), tokens.dtype),
            pltpu.SemaphoreType.DMA((2,)),
            pltpu.SemaphoreType.DMA((n,)),
            pltpu.SemaphoreType.DMA((n,)),
        ],
        compiler_params=pltpu.CompilerParams(
            collective_id=collective_id, has_side_effects=True
        ),
        name="tokens_to_heads",
    )(tokens)


def swap_halves(values):
    width = values.shape[-1]
    half = HEAD_DIM // 2
    lane = lax.broadcasted_iota(jnp.int32, values.shape, 1)
    ahead = pltpu.roll(values, width - half, 1)
    behind = pltpu.roll(values, half, 1)
    return jnp.where(lane % HEAD_DIM < half, ahead, behind)


def spread_lanes(table, width):
    return jnp.concatenate([table] * (width // table.shape[-1]), axis=-1)


def qkv_kernel(
    x_ref, wq_ref, wk_ref, wv_ref, cq_ref, sq_ref, ck_ref, sk_ref,
    q_ref, k_ref, v_ref, kt_ref, vt_ref,
):
    x = x_ref[...]
    width = q_ref.shape[1]
    query = nt(x, wq_ref[...])
    query = query * spread_lanes(cq_ref[...], width) + swap_halves(
        query
    ) * spread_lanes(sq_ref[...], width)
    q_ref[...] = query.astype(BF16) * (HEAD_DIM**-0.5)
    keys = nt(x, wk_ref[...])
    keys = keys * spread_lanes(ck_ref[...], width) + swap_halves(
        keys
    ) * spread_lanes(sk_ref[...], width)
    k_ref[...] = keys.astype(BF16)
    kt_ref[...] = keys.T.astype(BF16)
    values = nt(x, wv_ref[...])
    v_ref[...] = values.astype(BF16)
    vt_ref[...] = values.T.astype(BF16)


def project_qkv(x, wq, wk, wv, tables):
    length, width = x.shape
    cols = wq.shape[0]
    steps = length // TILE
    weight = pl.BlockSpec((cols, width), lambda i: (0, 0))
    table = pl.BlockSpec((TILE, tables[0].shape[1]), lambda i: (i, 0))
    row_out = pl.BlockSpec((TILE, cols), lambda i: (i, 0))
    col_out = pl.BlockSpec((cols, TILE), lambda i: (0, i))
    rows = jax.ShapeDtypeStruct((length, cols), BF16)
    columns = jax.ShapeDtypeStruct((cols, length), BF16)
    return pl.pallas_call(
        qkv_kernel,
        grid=(steps,),
        out_shape=(rows, rows, rows, columns, columns),
        in_specs=[pl.BlockSpec((TILE, width), lambda i: (i, 0))]
        + [weight] * 3
        + [table] * 4,
        out_specs=(row_out, row_out, row_out, col_out, col_out),
        compiler_params=pltpu.CompilerParams(vmem_limit_bytes=40 * 1024 * 1024),
        cost_estimate=pl.CostEstimate(
            flops=6 * length * width * cols,
            bytes_accessed=2 * length * width + 6 * width * cols + 10 * length * cols,
            transcendentals=0,
        ),
        name="project_qkv",
    )(x, wq, wk, wv, *tables)


def pair_mask(start_row, i, j):
    key_place = j * TILE + lax.broadcasted_iota(jnp.int32, (TILE, TILE), 0)
    query_place = i * TILE + lax.broadcasted_iota(jnp.int32, (TILE, TILE), 1)
    return (key_place <= query_place) & (key_place >= start_row)


def head_rows(query, heads):
    lane = lax.broadcasted_iota(jnp.int32, query.shape, 1) // HEAD_DIM
    zero = jnp.zeros_like(query)
    return [jnp.where(lane == h, query, zero) for h in range(heads)]


def attend_kernel(
    heads, first_ref, start_ref, q_ref, k_ref, vt_ref, o_ref, lse_ref, peak, total, mixed
):
    i = pl.program_id(0)
    queries = head_rows(q_ref[...], heads)
    start_row = start_ref[...]

    def block(j, first):
        at = pl.ds(pl.multiple_of(j * TILE, TILE), TILE)
        keys = k_ref[at, :]
        mask = pair_mask(start_row, i, j)
        for h in range(heads):
            here = slice(h * HEAD_DIM, (h + 1) * HEAD_DIM)
            scores = jnp.where(mask, nt(keys, queries[h]), MASKED)
            if first:
                new_peak = jnp.max(scores, axis=0, keepdims=True)
                expo = jnp.exp(scores - new_peak)
                total[h : h + 1] = jnp.sum(expo, axis=0, keepdims=True)
                mixed[here] = nn(vt_ref[here, at], expo.astype(BF16))
            else:
                old_peak = peak[h : h + 1]
                new_peak = jnp.maximum(old_peak, jnp.max(scores, axis=0, keepdims=True))
                expo = jnp.exp(scores - new_peak)
                shrink = jnp.exp(old_peak - new_peak)
                total[h : h + 1] = total[h : h + 1] * shrink + jnp.sum(
                    expo, axis=0, keepdims=True
                )
                mixed[here] = mixed[here] * shrink + nn(
                    vt_ref[here, at], expo.astype(BF16)
                )
            peak[h : h + 1] = new_peak

    block(i, True)

    @pl.loop(0, i - first_ref[i])
    def _(t):
        block(i - 1 - t, False)

    for h in range(heads):
        here = slice(h * HEAD_DIM, (h + 1) * HEAD_DIM)
        mixed[here] = mixed[here] / total[h : h + 1]
    o_ref[...] = mixed[...].T.astype(BF16)
    lse_ref[0] = peak[...] + jnp.log(total[...])


def attend(first, start, q, k, vt):
    length, cols = q.shape
    heads = cols // HEAD_DIM
    steps = length // TILE
    row = pl.BlockSpec((TILE, cols), lambda i, *_: (i, 0))
    return pl.pallas_call(
        functools.partial(attend_kernel, heads),
        out_shape=(
            jax.ShapeDtypeStruct((length, cols), BF16),
            jax.ShapeDtypeStruct((steps, heads, TILE), F32),
        ),
        grid_spec=pltpu.PrefetchScalarGridSpec(
            num_scalar_prefetch=1,
            grid=(steps,),
            in_specs=[
                pl.BlockSpec((1, TILE), lambda i, *_: (0, i)),
                row,
                pl.BlockSpec((length, cols), lambda i, *_: (0, 0)),
                pl.BlockSpec((cols, length), lambda i, *_: (0, 0)),
            ],
            out_specs=(
                row,
                pl.BlockSpec((1, heads, TILE), lambda i, *_: (i, 0, 0)),
            ),
            scratch_shapes=[
                pltpu.VMEM((heads, TILE), F32),
                pltpu.VMEM((heads, TILE), F32),
                pltpu.VMEM((cols, TILE), F32),
            ],
        ),
        compiler_params=pltpu.CompilerParams(vmem_limit_bytes=32 * 1024 * 1024),
        cost_estimate=pl.CostEstimate(
            flops=4 * length * 1024 * cols,
            bytes_accessed=8 * length * cols,
            transcendentals=length * 1024 * heads,
        ),
        name="attend",
    )(first, start, q, k, vt)


def attend_back_kernel(
    heads, first_ref, start_ref, q_ref, k_ref, kt_ref, v_ref, o_ref, lse_ref, do_ref,
    cq_ref, sq_ref, ck_ref, sk_ref, dq_ref, dk_ref, dv_ref, dqt, dk_sum, dv_sum,
):
    i = pl.program_id(0)
    steps = pl.num_programs(0)
    width = q_ref.shape[1]
    queries = head_rows(q_ref[...], heads)
    grads = head_rows(do_ref[...], heads)
    start_row = start_ref[...]
    product = (do_ref[...].astype(F32) * o_ref[...].astype(F32)).T
    inner = [
        jnp.sum(product[h * HEAD_DIM : (h + 1) * HEAD_DIM], axis=0, keepdims=True)
        for h in range(heads)
    ]

    def block(j, first):
        at = pl.ds(pl.multiple_of(j * TILE, TILE), TILE)
        keys = k_ref[at, :]
        values = v_ref[at, :]
        mask = pair_mask(start_row, i, j)
        key_term = None
        value_term = None
        for h in range(heads):
            here = slice(h * HEAD_DIM, (h + 1) * HEAD_DIM)
            scores = nt(keys, queries[h])
            weights = jnp.where(mask, jnp.exp(scores - lse_ref[0, h : h + 1]), 0.0)
            grad_weights = nt(values, grads[h])
            grad_scores = (weights * (grad_weights - inner[h])).astype(BF16)
            term = nn(weights.astype(BF16), grads[h])
            value_term = term if value_term is None else value_term + term
            term = nn(grad_scores, queries[h])
            key_term = term if key_term is None else key_term + term
            term = nn(kt_ref[here, at], grad_scores)
            if first:
                dqt[here] = term
            else:
                dqt[here] = dqt[here] + term
        if first:
            dk_sum[at] = key_term
            dv_sum[at] = value_term
        else:
            dk_sum[at] = dk_sum[at] + key_term
            dv_sum[at] = dv_sum[at] + value_term

    block(i, True)

    @pl.loop(0, i - first_ref[i])
    def _(t):
        block(i - 1 - t, False)

    def unturn(grad, cosine, sine):
        grad = grad.astype(BF16).astype(F32)
        cosine = spread_lanes(cosine, width)
        sine = spread_lanes(sine, width)
        return (grad * cosine - swap_halves(grad) * sine).astype(BF16)

    rows = pl.ds(pl.multiple_of(i * TILE, TILE), TILE)
    dq_ref[...] = unturn(
        dqt[...].T * (HEAD_DIM**-0.5), cq_ref[rows, :], sq_ref[rows, :]
    )

    @pl.when(i == steps - 1)
    def _():
        @pl.loop(0, steps)
        def _(j):
            at = pl.ds(pl.multiple_of(j * TILE, TILE), TILE)
            dk_ref[at] = unturn(dk_sum[at], ck_ref[at, :], sk_ref[at, :])
            dv_ref[at] = dv_sum[at].astype(BF16)


def attend_back(first, start, q, k, kt, v, o, lse, do, tables):
    length, cols = q.shape
    heads = cols // HEAD_DIM
    steps = length // TILE
    row = pl.BlockSpec((TILE, cols), lambda i, *_: (i, 0))
    whole = pl.BlockSpec((length, cols), lambda i, *_: (0, 0))
    table = pl.BlockSpec((length, tables[0].shape[1]), lambda i, *_: (0, 0))
    shape = jax.ShapeDtypeStruct((length, cols), BF16)
    return pl.pallas_call(
        functools.partial(attend_back_kernel, heads),
        out_shape=(shape, shape, shape),
        grid_spec=pltpu.PrefetchScalarGridSpec(
            num_scalar_prefetch=1,
            grid=(steps,),
            in_specs=[
                pl.BlockSpec((1, TILE), lambda i, *_: (0, i)),
                row,
                whole,
                pl.BlockSpec((cols, length), lambda i, *_: (0, 0)),
                whole,
                row,
                pl.BlockSpec((1, heads, TILE), lambda i, *_: (i, 0, 0)),
                row,
            ]
            + [table] * 4,
            out_specs=(row, whole, whole),
            scratch_shapes=[
                pltpu.VMEM((cols, TILE), F32),
                pltpu.VMEM((length, cols), F32),
                pltpu.VMEM((length, cols), F32),
            ],
        ),
        compiler_params=pltpu.CompilerParams(vmem_limit_bytes=48 * 1024 * 1024),
        cost_estimate=pl.CostEstimate(
            flops=10 * length * 1024 * cols,
            bytes_accessed=16 * length * cols,
            transcendentals=length * 1024 * heads,
        ),
        name="attend_back",
    )(first, start, q, k, kt, v, o, lse, do, *tables)


def upper_kernel(
    x_ref, wu_ref, c_ref, wd_ref, gain_ref, act_ref, slope_ref, grad_ref, stat_ref
):
    upper = nt(x_ref[...], wu_ref[...])
    grad = nn(c_ref[...], wd_ref[...])
    below = 0.5 * (1.0 + lax.erf(upper * (0.5**0.5)))
    act = upper * below
    slope = below + upper * (jnp.exp(-0.5 * upper * upper) * ((2.0 * math.pi) ** -0.5))
    act_ref[...] = act
    slope_ref[...] = slope.astype(BF16)
    grad_ref[...] = grad
    part = grad * gain_ref[...]
    average = jnp.mean(act, axis=-1, keepdims=True)
    centered = act - average
    spread = jnp.sum(centered * centered, axis=-1, keepdims=True)
    part_sum = jnp.sum(part, axis=-1, keepdims=True)
    cross = jnp.sum(part * centered, axis=-1, keepdims=True)
    lane = lax.broadcasted_iota(jnp.int32, (x_ref.shape[0], 128), 1)
    columns = jnp.where(
        lane == 0,
        average,
        jnp.where(lane == 1, spread, jnp.where(lane == 2, part_sum, cross)),
    )
    stat_ref[...] = columns.T[:8]


def upper_pass(x, w_up, cot, w_down, gain):
    length, width = x.shape
    feats = w_up.shape[0]
    rows = TILE
    row = pl.BlockSpec((rows, width), lambda i: (i, 0))
    out = pl.BlockSpec((rows, feats), lambda i: (i, 0))
    return pl.pallas_call(
        upper_kernel,
        grid=(length // rows,),
        out_shape=(
            jax.ShapeDtypeStruct((length, feats), F32),
            jax.ShapeDtypeStruct((length, feats), BF16),
            jax.ShapeDtypeStruct((length, feats), F32),
            jax.ShapeDtypeStruct((8, length), F32),
        ),
        in_specs=[
            row,
            pl.BlockSpec((feats, width), lambda i: (0, 0)),
            row,
            pl.BlockSpec((width, feats), lambda i: (0, 0)),
            pl.BlockSpec((1, feats), lambda i: (0, 0)),
        ],
        out_specs=(out, out, out, pl.BlockSpec((8, rows), lambda i: (0, i))),
        compiler_params=pltpu.CompilerParams(vmem_limit_bytes=48 * 1024 * 1024),
        cost_estimate=pl.CostEstimate(
            flops=4 * length * width * feats,
            bytes_accessed=8 * length * width + 8 * length * feats,
            transcendentals=2 * length * feats,
        ),
        name="upper_pass",
    )(x, w_up, cot, w_down, gain)


def hidden_kernel(act_ref, slope_ref, grad_ref, stat_ref, gain_ref, hid_ref, gu_ref, gg_ref):
    i = pl.program_id(0)
    stats = stat_ref[...].T
    average = stats[:, 0:1]
    scale = stats[:, 1:2]
    part_mean = stats[:, 2:3]
    cross_mean = stats[:, 3:4]
    gain = gain_ref[...]
    normal = (act_ref[...] - average) * scale
    grad = grad_ref[...]
    hid_ref[...] = (normal * gain).astype(BF16)
    back = scale * (grad * gain - part_mean - normal * cross_mean)
    gu_ref[...] = (slope_ref[...].astype(F32) * back).astype(BF16)
    term = jnp.sum(grad * normal, axis=0, keepdims=True)

    @pl.when(i == 0)
    def _():
        gg_ref[...] = term

    @pl.when(i > 0)
    def _():
        gg_ref[...] = gg_ref[...] + term


def hidden_pass(act, slope, grad, stats, gain):
    length, feats = act.shape
    out = pl.BlockSpec((TILE, feats), lambda i: (i, 0))
    one = pl.BlockSpec((1, feats), lambda i: (0, 0))
    return pl.pallas_call(
        hidden_kernel,
        grid=(length // TILE,),
        out_shape=(
            jax.ShapeDtypeStruct((length, feats), BF16),
            jax.ShapeDtypeStruct((length, feats), BF16),
            jax.ShapeDtypeStruct((1, feats), F32),
        ),
        in_specs=[out, out, out, pl.BlockSpec((8, TILE), lambda i: (0, i)), one],
        out_specs=(out, out, one),
        compiler_params=pltpu.CompilerParams(vmem_limit_bytes=40 * 1024 * 1024),
        cost_estimate=pl.CostEstimate(
            flops=12 * length * feats,
            bytes_accessed=14 * length * feats,
            transcendentals=0,
        ),
        name="hidden_pass",
    )(act, slope, grad, stats, gain)


def stat_kernel(n, feats, x_ref, o_ref, held, send_sem, recv_sem):
    me = lax.axis_index("seq")
    held[me] = x_ref[...]
    meet([lax.rem(me + k, n) for k in range(1, n)])
    copies = [
        remote(x_ref, held.at[me], send_sem.at[k], recv_sem.at[k], lax.rem(me + k, n))
        for k in range(1, n)
    ]
    for copy in copies:
        copy.start()
    for copy in copies:
        copy.wait()
    average = held[0, 0:1]
    for d in range(1, n):
        average = average + held[d, 0:1]
    average = average * (1.0 / n)
    spread = jnp.zeros_like(average)
    part = jnp.zeros_like(average)
    cross = jnp.zeros_like(average)
    for d in range(n):
        shift = held[d, 0:1] - average
        spread = spread + held[d, 1:2] + feats * (shift * shift)
        part = part + held[d, 2:3]
        cross = cross + held[d, 3:4] + shift * held[d, 2:3]
    whole = 1.0 / (n * feats)
    scale = lax.rsqrt(spread * whole + EPSILON)
    o_ref[0:1] = average
    o_ref[1:2] = scale
    o_ref[2:3] = part * whole
    o_ref[3:4] = cross * scale * whole
    o_ref[4:8] = jnp.zeros((4, average.shape[1]), F32)


def join_stats(stat, feats, collective_id):
    n = lax.axis_size("seq")
    inside = pl.BlockSpec(memory_space=pltpu.VMEM)
    return pl.pallas_call(
        functools.partial(stat_kernel, n, feats),
        out_shape=jax.ShapeDtypeStruct(stat.shape, F32),
        in_specs=[inside],
        out_specs=inside,
        scratch_shapes=[
            pltpu.VMEM((n, *stat.shape), F32),
            pltpu.SemaphoreType.DMA((n,)),
            pltpu.SemaphoreType.DMA((n,)),
        ],
        compiler_params=pltpu.CompilerParams(
            collective_id=collective_id, has_side_effects=True
        ),
        name="join_stats",
    )(stat)


STEP = 32


def mix_kernel(att_ref, x_ref, w_ref, gm_ref, gf_ref, mix_ref, mid_ref, ffn_ref):
    j = pl.program_id(0)
    rows = att_ref.shape[0]
    cols = w_ref.shape[0]

    @pl.when(j == 0)
    def _():
        @pl.loop(0, rows // STEP)
        def _(r):
            at = pl.ds(pl.multiple_of(r * STEP, STEP), STEP)
            normal, _ = norm_parts(att_ref[at].astype(F32))
            mix_ref[at] = (normal * gm_ref[...]).astype(BF16)

    here = pl.ds(pl.multiple_of(j * cols, cols), cols)
    mid_ref[:, here] = x_ref[:, here].astype(F32) + nt(mix_ref[...], w_ref[...])

    @pl.when(j == pl.num_programs(0) - 1)
    def _():
        @pl.loop(0, rows // STEP)
        def _(r):
            at = pl.ds(pl.multiple_of(r * STEP, STEP), STEP)
            normal, _ = norm_parts(mid_ref[at])
            ffn_ref[at] = (normal * gf_ref[...]).astype(BF16)


def mix_pass(attended, x, w_out, gain_mix, gain_ffn):
    rows, width = x.shape
    cols = TILE
    n = width // cols
    whole = pl.BlockSpec((rows, width), lambda j: (0, 0))
    gain = pl.BlockSpec((1, width), lambda j: (0, 0))
    low = jax.ShapeDtypeStruct((rows, width), BF16)
    return pl.pallas_call(
        mix_kernel,
        grid=(n,),
        out_shape=(low, jax.ShapeDtypeStruct((rows, width), F32), low),
        in_specs=[
            whole,
            whole,
            pl.BlockSpec((cols, width), lambda j: (j, 0)),
            gain,
            gain,
        ],
        out_specs=(whole, whole, whole),
        compiler_params=pltpu.CompilerParams(vmem_limit_bytes=32 * 1024 * 1024),
        cost_estimate=pl.CostEstimate(
            flops=2 * rows * width * width,
            bytes_accessed=2 * width * width + 12 * rows * width,
            transcendentals=0,
        ),
        name="mix_pass",
    )(attended, x, w_out, gain_mix[None], gain_ffn[None])


def branch_kernel(
    g_ref, mid_ref, cot_ref, att_ref, w_ref, gm_ref, gf_ref,
    gmid_ref, gbr_ref, gatt_ref, ggf_ref, ggm_ref, total,
):
    j = pl.program_id(0)
    rows = att_ref.shape[0]
    cols = w_ref.shape[0]

    @pl.when(j == 0)
    def _():
        ggf_ref[...] = jnp.zeros_like(ggf_ref)
        total[...] = jnp.zeros_like(total)

        @pl.loop(0, rows // STEP)
        def _(r):
            at = pl.ds(pl.multiple_of(r * STEP, STEP), STEP)
            normal, scale = norm_parts(mid_ref[at])
            part, gain_part = norm_back(g_ref[at], normal, scale, gf_ref[...])
            ggf_ref[...] += gain_part[None]
            grad = cot_ref[at].astype(F32) + part
            gmid_ref[at] = grad
            gbr_ref[at] = grad.astype(BF16)

    here = pl.ds(pl.multiple_of(j * cols, cols), cols)
    total[...] += nn(gbr_ref[:, here], w_ref[...])

    @pl.when(j == pl.num_programs(0) - 1)
    def _():
        ggm_ref[...] = jnp.zeros_like(ggm_ref)

        @pl.loop(0, rows // STEP)
        def _(r):
            at = pl.ds(pl.multiple_of(r * STEP, STEP), STEP)
            normal, scale = norm_parts(att_ref[at].astype(F32))
            part, gain_part = norm_back(total[at], normal, scale, gm_ref[...])
            ggm_ref[...] += gain_part[None]
            gatt_ref[at] = part.astype(BF16)


def branch_pass(grad_ffn_in, middle, cot, attended, w_out, gain_mix, gain_ffn):
    rows, width = cot.shape
    cols = TILE
    n = width // cols
    whole = pl.BlockSpec((rows, width), lambda j: (0, 0))
    gain = pl.BlockSpec((1, width), lambda j: (0, 0))
    low = jax.ShapeDtypeStruct((rows, width), BF16)
    sums = jax.ShapeDtypeStruct((1, width), F32)
    return pl.pallas_call(
        branch_kernel,
        grid=(n,),
        out_shape=(jax.ShapeDtypeStruct((rows, width), F32), low, low, sums, sums),
        in_specs=[
            whole,
            whole,
            whole,
            whole,
            pl.BlockSpec((cols, width), lambda j: (j, 0)),
            gain,
            gain,
        ],
        out_specs=(whole, whole, whole, gain, gain),
        scratch_shapes=[pltpu.VMEM((rows, width), F32)],
        compiler_params=pltpu.CompilerParams(vmem_limit_bytes=40 * 1024 * 1024),
        cost_estimate=pl.CostEstimate(
            flops=2 * rows * width * width,
            bytes_accessed=2 * width * width + 20 * rows * width,
            transcendentals=0,
        ),
        name="branch_pass",
    )(grad_ffn_in, middle, cot, attended, w_out, gain_mix[None], gain_ffn[None])


def finish_kernel(
    n, depth, gq_ref, pw_ref, pn_ref, po_ref, gu_ref, oq_ref, ow_ref, sn_ref, so_ref, ou_ref,
    own, twin_in, held, zown, zin,
    local_sem, send_sem, recv_sem, keep_sem,
    up_send, up_recv, down_send, down_recv, home_send, home_recv,
):
    me, twin, near_x, near_y, across = places()
    z = lax.axis_index("batch")
    rows = pn_ref.shape[1]
    half = rows // 2
    low, high = pl.ds(0, half), pl.ds(half, half)
    mine = (across, near_x, near_y, me)
    chunk = zown.shape[1]
    turned = gq_ref.shape[0]
    upper = turned + gu_ref.shape[0]
    chunks = zown.shape[0]
    per_part = turned // 3
    per_side = chunks // 2

    load_q = pltpu.make_async_copy(
        gq_ref, zown.at[pl.ds(0, turned)], local_sem.at[12]
    )
    load_u = pltpu.make_async_copy(
        gu_ref, zown.at[pl.ds(turned, upper - turned)], local_sem.at[13]
    )
    load_q.start()
    load_u.start()
    partials = (pw_ref, pn_ref, po_ref)
    loads = [
        [
            pltpu.make_async_copy(p.at[block], own.at[m, i], local_sem.at[4 * m + i])
            for i, block in enumerate(mine)
        ]
        for m, p in enumerate(partials)
    ]
    for part in loads:
        for load in part:
            load.start()
    meet_all(n, depth)

    def copy(m, k, src, dst, partner):
        return remote(src, dst, send_sem.at[m, k], recv_sem.at[m, k], partner)

    twins = [
        [
            copy(m, i, p.at[block + twin], twin_in.at[m, i], me + twin)
            for i, block in enumerate(mine)
        ]
        for m, p in enumerate(partials)
    ]
    sends = [
        [
            copy(m, 4, own.at[m, 0, low], held.at[m, 0], near_x),
            copy(m, 5, own.at[m, 0, high], held.at[m, 1], near_y),
            copy(m, 6, own.at[m, 1, low], held.at[m, 2], near_x),
            copy(m, 7, own.at[m, 2, high], held.at[m, 3], near_y),
            copy(m, 8, own.at[m, 1, high], held.at[m, 4], near_x),
            copy(m, 9, own.at[m, 2, low], held.at[m, 5], near_y),
        ]
        for m in range(3)
    ]
    for part in twins:
        for send in part:
            send.start()

    def add_twin(m, i):
        loads[m][i].wait()
        twins[m][i].wait_recv()

        @pl.loop(0, rows // STEP)
        def _(r):
            at = pl.ds(pl.multiple_of(r * STEP, STEP), STEP)
            own[m, i, at] = (
                own[m, i, at].astype(F32) + twin_in[m, i, at].astype(F32)
            ).astype(BF16)

    def add_held(m, i, base, slot):
        @pl.loop(0, half // STEP)
        def _(r):
            at = pl.ds(pl.multiple_of(r * STEP, STEP), STEP)
            to = pl.ds(pl.multiple_of(base + r * STEP, STEP), STEP)
            own[m, i, to] = (
                own[m, i, to].astype(F32) + held[m, slot, at].astype(F32)
            ).astype(BF16)

    def first(m):
        add_twin(m, 0)
        sends[m][0].start()
        sends[m][1].start()
        add_twin(m, 1)
        sends[m][2].start()
        add_twin(m, 2)
        sends[m][3].start()

    def second(m):
        sends[m][1].wait_recv()
        add_held(m, 1, half, 1)
        sends[m][4].start()
        sends[m][0].wait_recv()
        add_held(m, 2, 0, 0)
        sends[m][5].start()

    def last(m, store):
        loads[m][3].wait()
        twins[m][3].wait_recv()
        for k in (2, 3, 4, 5):
            sends[m][k].wait_recv()
        for base, one, two in ((0, 2, 5), (half, 3, 4)):

            @pl.loop(0, half // STEP)
            def _(r):
                at = pl.ds(pl.multiple_of(r * STEP, STEP), STEP)
                place = base + r * STEP
                to = pl.ds(pl.multiple_of(place, STEP), STEP)
                store(
                    place,
                    own[m, 3, to].astype(F32)
                    + twin_in[m, 3, to].astype(F32)
                    + held[m, one, at].astype(F32)
                    + held[m, two, at].astype(F32),
                )

    def store_line(place, value):
        zown[
            upper + place // chunk,
            pl.ds(pl.multiple_of(lax.rem(place, chunk), STEP), STEP),
        ] = value.astype(BF16)

    def store_into(ref):
        def store(place, value):
            ref[pl.ds(pl.multiple_of(place, STEP), STEP)] = value

        return store

    def home(part):
        block = part * n + me
        return block // 3, lax.rem(block, 3)

    def deliver_far(g):
        target, slot = home(g // per_part)
        piece = lax.rem(g, per_part)
        return remote(
            zin.at[g],
            oq_ref.at[slot, piece],
            home_send.at[g],
            home_recv.at[slot, piece],
            target,
        )

    def deliver_near(g):
        _, slot = home(g // per_part)
        return pltpu.make_async_copy(
            zin.at[g], oq_ref.at[slot, lax.rem(g, per_part)], keep_sem.at[g]
        )

    def deliver_up(g):
        return pltpu.make_async_copy(zin.at[g], ou_ref.at[g - turned], keep_sem.at[g])

    def deliver_out(g):
        return pltpu.make_async_copy(zin.at[g], ow_ref.at[g - upper], keep_sem.at[g])

    def deliver(g, wait):
        target, _ = home(g // per_part)

        @pl.when((g < turned) & (target != me))
        def _():
            deliver_far(g).wait_send() if wait else deliver_far(g).start()

        @pl.when((g < turned) & (target == me))
        def _():
            deliver_near(g).wait() if wait else deliver_near(g).start()

        @pl.when((g >= turned) & (g < upper))
        def _():
            deliver_up(g).wait() if wait else deliver_up(g).start()

        @pl.when(g >= upper)
        def _():
            deliver_out(g).wait() if wait else deliver_out(g).start()

    def go_up(g, ahead):
        return line_remote(zown.at[g], zin.at[g], up_send.at[g], up_recv.at[g], ahead)

    def go_down(g, behind):
        return line_remote(
            zin.at[g], zin.at[g], down_send.at[g], down_recv.at[g], behind
        )

    def ranks(side):
        if side == 0:
            return z, z + 1, z - 1
        return depth - 1 - z, z - 1, z + 1

    def add_line(g, target):
        @pl.loop(0, chunk // STEP)
        def _(r):
            at = pl.ds(pl.multiple_of(r * STEP, STEP), STEP)
            target[g, at] = (zown[g, at].astype(F32) + zin[g, at].astype(F32)).astype(
                BF16
            )

    def line_step(t):
        for side in (0, 1):
            rank, ahead, behind = ranks(side)
            c = t - rank
            g = 2 * c + side
            there = (c >= 0) & (c < per_side)

            @pl.when(there & (rank == 0))
            def _():
                go_up(g, ahead).start()

            @pl.when(there & (rank > 0) & (rank < depth - 1))
            def _():
                go_up(g, behind).wait_recv()
                add_line(g, zown)
                go_up(g, ahead).start()

            @pl.when(there & (rank == depth - 1))
            def _():
                go_up(g, behind).wait_recv()
                add_line(g, zin)
                go_down(g, behind).start()
                deliver(g, False)

            c_back = t - 2 * (depth - 1) + rank
            g_back = 2 * c_back + side
            there = (c_back >= 0) & (c_back < per_side) & (rank < depth - 1)

            @pl.when(there)
            def _():
                go_down(g_back, ahead).wait_recv()

            @pl.when(there & (rank > 0))
            def _():
                go_down(g_back, behind).start()

            @pl.when(there)
            def _():
                deliver(g_back, False)

    first(0)
    load_q.wait()
    load_u.wait()
    line_step(0)
    line_step(1)
    first(1)
    line_step(2)
    second(0)
    line_step(3)
    last(0, store_line)
    for t in (4, 5, 6):
        line_step(t)
    first(2)
    for t in (7, 8):
        line_step(t)
    second(1)
    for t in (9, 10):
        line_step(t)
    last(1, store_into(sn_ref))
    for t in (11, 12, 13):
        line_step(t)
    second(2)
    steps = per_side + 2 * (depth - 1)
    for t in range(14, steps - 1):
        line_step(t)
    last(2, store_into(so_ref))
    line_step(steps - 1)

    for m in range(3):
        for send in twins[m] + sends[m]:
            send.wait_send()
    for g in range(chunks):
        rank, ahead, behind = ranks(g % 2)

        @pl.when(rank < depth - 1)
        def _():
            go_up(g, ahead).wait_send()

        @pl.when(rank > 0)
        def _():
            go_down(g, behind).wait_send()

        deliver(g, True)
    for slot in range(3):
        block = 3 * me + slot
        source = lax.rem(block, n)

        @pl.when(source != me)
        def _():
            for piece in range(per_part):
                remote(
                    zin.at[0],
                    oq_ref.at[slot, piece],
                    home_send.at[0],
                    home_recv.at[slot, piece],
                    source,
                ).wait_recv()


CHUNK = 64


def finish(grad_qkv, part_out, part_normed, part_outputs, grad_up, collective_id):
    n, depth = lax.axis_size("seq"), lax.axis_size("batch")
    rows, width = part_out.shape[0] // n, part_out.shape[1]
    cols = grad_qkv.shape[0] // 3
    if n != 8 or depth != 4:
        me = lax.axis_index("seq")
        blocks = lax.psum(grad_qkv, "batch").reshape(3, cols, width)
        back = [
            lax.ppermute(
                give_part(blocks, me, n, j),
                "seq",
                [((3 * d + j) % n, d) for d in range(n)],
            )
            for j in range(3)
        ]
        w_out = lax.psum(scatter_seq(part_out, None).astype(BF16), "batch")
        return (
            jnp.concatenate(back, axis=0),
            w_out,
            scatter_seq(part_normed, None),
            scatter_seq(part_outputs, None),
            lax.psum(grad_up, "batch"),
        )
    pieces = grad_up.shape[0] // CHUNK
    turned = 3 * cols // CHUNK
    chunks = turned + pieces + rows // CHUNK
    inside = pl.BlockSpec(memory_space=pltpu.VMEM)
    dma = pltpu.SemaphoreType.DMA
    line = pltpu.VMEM((chunks, CHUNK, width), BF16)
    w_qkv, w_out, normed, outputs, w_up = pl.pallas_call(
        functools.partial(finish_kernel, n, depth),
        out_shape=(
            jax.ShapeDtypeStruct((3, cols // CHUNK, CHUNK, width), BF16),
            jax.ShapeDtypeStruct((rows // CHUNK, CHUNK, width), BF16),
            jax.ShapeDtypeStruct((rows, width), F32),
            jax.ShapeDtypeStruct((rows, width), F32),
            jax.ShapeDtypeStruct((pieces, CHUNK, width), BF16),
        ),
        in_specs=[ANY] * 5,
        out_specs=(ANY, ANY, inside, inside, ANY),
        scratch_shapes=[
            pltpu.VMEM((3, 4, rows, width), BF16),
            pltpu.VMEM((3, 4, rows, width), BF16),
            pltpu.VMEM((3, 6, rows // 2, width), BF16),
            line,
            line,
            dma((14,)),
            dma((3, 10)),
            dma((3, 10)),
            dma((chunks,)),
            dma((chunks,)),
            dma((chunks,)),
            dma((chunks,)),
            dma((chunks,)),
            dma((chunks,)),
            dma((3, cols // CHUNK)),
        ],
        compiler_params=pltpu.CompilerParams(
            collective_id=collective_id,
            has_side_effects=True,
            vmem_limit_bytes=58 * 1024 * 1024,
        ),
        name="finish",
    )(
        grad_qkv.reshape(turned, CHUNK, width),
        *[p.reshape(n, rows, width) for p in (part_out, part_normed, part_outputs)],
        grad_up.reshape(pieces, CHUNK, width),
    )
    return (
        w_qkv.reshape(3 * cols, width),
        w_out.reshape(rows, width),
        normed,
        outputs,
        w_up.reshape(-1, width),
    )


def gains_kernel(
    n, depth, a_ref, b_ref, oa_ref, ob_ref, held_a, held_b, pack, held_c, send_sem, recv_sem, last_send, last_recv
):
    me = lax.axis_index("seq")
    z = lax.axis_index("batch")
    p, q = a_ref.shape[0], b_ref.shape[0]
    barrier = pltpu.get_barrier_semaphore()
    for k in range(1, n):
        pl.semaphore_signal(
            barrier, inc=1, device_id={"seq": lax.rem(me + k, n)}, device_id_type=MESH
        )
    for k in range(1, depth):
        pl.semaphore_signal(
            barrier,
            inc=1,
            device_id={"batch": lax.rem(z + k, depth)},
            device_id_type=MESH,
        )
    pl.semaphore_wait(barrier, n + depth - 2)
    held_a[me] = a_ref[...]
    held_b[me] = b_ref[...]
    copies = []
    for k in range(1, n):
        partner = lax.rem(me + k, n)
        copies.append(
            remote(a_ref, held_a.at[me], send_sem.at[0, k], recv_sem.at[0, k], partner)
        )
        copies.append(
            remote(b_ref, held_b.at[me], send_sem.at[1, k], recv_sem.at[1, k], partner)
        )
    for copy in copies:
        copy.start()
    for copy in copies:
        copy.wait()
    total = held_a[0]
    for d in range(1, n):
        total = total + held_a[d]
    pack[0:p] = total
    for d in range(n):
        pack[p + d * q : p + (d + 1) * q] = held_b[d]
    held_c[z] = pack[...]
    copies = [
        pltpu.make_async_remote_copy(
            src_ref=pack,
            dst_ref=held_c.at[z],
            send_sem=last_send.at[k],
            recv_sem=last_recv.at[k],
            device_id={"batch": lax.rem(z + k, depth)},
            device_id_type=MESH,
        )
        for k in range(1, depth)
    ]
    for copy in copies:
        copy.start()
    for copy in copies:
        copy.wait()
    total = held_c[0]
    for d in range(1, depth):
        total = total + held_c[d]
    oa_ref[...] = total[0:p]
    ob_ref[...] = total[p:]


def sum_gains(shared, mine, collective_id):
    n, depth = lax.axis_size("seq"), lax.axis_size("batch")
    p, q = shared.shape[0], mine.shape[0]
    inside = pl.BlockSpec(memory_space=pltpu.VMEM)
    return pl.pallas_call(
        functools.partial(gains_kernel, n, depth),
        out_shape=(
            jax.ShapeDtypeStruct((p, 128), F32),
            jax.ShapeDtypeStruct((n * q, 128), F32),
        ),
        in_specs=[inside, inside],
        out_specs=(inside, inside),
        scratch_shapes=[
            pltpu.VMEM((n, p, 128), F32),
            pltpu.VMEM((n, q, 128), F32),
            pltpu.VMEM((p + n * q, 128), F32),
            pltpu.VMEM((depth, p + n * q, 128), F32),
            pltpu.SemaphoreType.DMA((2, n)),
            pltpu.SemaphoreType.DMA((2, n)),
            pltpu.SemaphoreType.DMA((depth,)),
            pltpu.SemaphoreType.DMA((depth,)),
        ],
        compiler_params=pltpu.CompilerParams(
            collective_id=collective_id, has_side_effects=True
        ),
        name="sum_gains",
    )(shared, mine)


def body(
    inputs,
    segment_ids,
    w_qkv,
    w_out,
    w_up,
    w_down,
    gain_attn,
    gain_mix,
    gain_ffn,
    gain_hidden,
    cotangent,
):
    _, local, width = inputs.shape
    n, depth = lax.axis_size("seq"), lax.axis_size("batch")
    me = lax.axis_index("seq")
    length = local * n
    feats = w_up.shape[0]
    x_low = inputs[0]
    x = x_low.astype(F32)
    cot = cotangent[0]
    segment = segment_ids[0]

    w_out_full = lax.all_gather(w_out, "seq", axis=0, tiled=True)
    normal_attn, scale_attn = norm_parts(x)
    normed = (normal_attn * gain_attn).astype(BF16)
    before = [jnp.sum((segment < d).astype(jnp.int32)) for d in range(1, DOCS)]
    start = jnp.zeros_like(segment)
    for d in range(1, DOCS):
        start = jnp.where(segment == d, before[d - 1], start)
    positions = jnp.arange(length, dtype=jnp.int32) - start
    first = start[::TILE] // TILE
    start_row = start[None, :]

    normed_full, (wq, wk, wv), w_down_near, tables = start_exchange(
        normed, w_qkv, w_down, positions.astype(F32), 1
    )
    cot_late, _ = lax.optimization_barrier((cot, wq))
    cot_full = lax.all_gather(cot_late, "seq", axis=0, tiled=True)

    q, k, v, kt, vt = project_qkv(normed_full, wq, wk, wv, tables)
    attended_heads, lse = attend(first, start_row, q, k, vt)
    attended = heads_to_tokens(attended_heads, 2)
    mix_in, middle, ffn_in = mix_pass(attended, x_low, w_out_full, gain_mix, gain_ffn)
    ffn_full, w_down_cols = gather_seq(ffn_in, w_down_near, 3)

    gain_here = lax.dynamic_slice_in_dim(gain_hidden, me * feats, feats, 0)[None, :]
    act, slope, grad_hidden, stat = upper_pass(
        ffn_full, w_up, cot_full, w_down_cols, gain_here
    )
    stats = join_stats(stat, feats, 8)
    hidden, grad_upper, grad_gain_here = hidden_pass(act, slope, grad_hidden, stats, gain_here)

    grad_w_down = tn(cot_full, hidden).astype(BF16)
    grad_upper, grad_w_down = lax.optimization_barrier((grad_upper, grad_w_down))
    grad_w_up = tn(grad_upper, ffn_full).astype(BF16)
    grad_upper, grad_w_up = lax.optimization_barrier((grad_upper, grad_w_up))
    down_part = lax.psum_scatter(
        grad_w_down.reshape(n, local, feats), "batch", scatter_dimension=1, tiled=True
    )
    late = feats // 2
    grad_up_early = lax.psum(grad_w_up[late:], "batch")
    grad_ffn_in = scatter_seq(nn(grad_upper, w_up).astype(BF16), 4)
    grad_middle, grad_branch, grad_att, grad_gain_ffn, grad_gain_mix = branch_pass(
        grad_ffn_in, middle, cot, attended, w_out_full, gain_mix, gain_ffn
    )
    grad_heads = tokens_to_heads(grad_att, 5)
    down_part, grad_heads = lax.optimization_barrier((down_part, grad_heads))
    down_part = lax.all_to_all(down_part, "seq", split_axis=0, concat_axis=0, tiled=True)
    down_part = jnp.swapaxes(down_part, 0, 1).reshape(local // depth, n * feats)
    grad_w_down = lax.all_gather(down_part, "batch", axis=0, tiled=True)

    dq, dk, dv = attend_back(
        first, start_row, q, k, kt, v, attended_heads, lse, grad_heads, tables
    )
    grads = jnp.concatenate([dq, dk, dv], axis=1)
    weights = jnp.concatenate([wq, wk, wv], axis=0)
    grad_w_qkv, grad_w_out, grad_normed, down_sum, grad_up_late = finish(
        tn(grads, normed_full).astype(BF16),
        tn(grad_branch, mix_in).astype(BF16),
        nn(grads, weights).astype(BF16),
        nt(hidden, w_down_cols).astype(BF16),
        grad_w_up[:late],
        6,
    )
    grad_part, grad_gain_attn = norm_back(grad_normed, normal_attn, scale_attn, gain_attn)
    grad_inputs = grad_middle + grad_part
    outputs = (middle + down_sum).astype(BF16)
    shared, hidden_gains = sum_gains(
        jnp.concatenate([grad_gain_attn, grad_gain_mix[0], grad_gain_ffn[0]]).reshape(-1, 128),
        grad_gain_here.reshape(-1, 128),
        9,
    )
    shared = shared.reshape(-1)
    return (
        outputs[None],
        grad_inputs[None],
        grad_w_qkv.astype(F32),
        grad_w_out.astype(F32),
        jnp.concatenate([grad_up_late.astype(F32), grad_up_early.astype(F32)], axis=0),
        grad_w_down.astype(F32),
        shared[:width],
        shared[width : 2 * width],
        shared[2 * width :],
        hidden_gains.reshape(-1),
    )


def pick_part(turned, me, n, part):
    chosen = turned[0]
    home = part * n + me
    for j in (1, 2):
        chosen = jnp.where(lax.rem(home, 3) == j, turned[j], chosen)
    return chosen


def give_part(blocks, me, n, j):
    chosen = blocks[0]
    for part in (1, 2):
        chosen = jnp.where(lax.rem(part * n + me, 3) == j, blocks[part], chosen)
    return chosen


def solution(mesh):
    in_specs = (
        P("batch", "seq", None),
        P("batch", None),
        P("seq", None),
        P("seq", None),
        P("seq", None),
        P("seq", None),
        P(),
        P(),
        P(),
        P(),
        P("batch", "seq", None),
    )
    out_specs = (
        P("batch", "seq", None),
        P("batch", "seq", None),
        P("seq", None),
        P("seq", None),
        P("seq", None),
        P("seq", None),
        P(),
        P(),
        P(),
        P(),
    )
    return jax.shard_map(body, mesh=mesh, in_specs=in_specs, out_specs=out_specs, check_vma=False)
```

```python
import functools
import math

import jax
import jax.numpy as jnp
from jax import lax
from jax.experimental import pallas as pl
from jax.experimental.pallas import tpu as pltpu
from jax.sharding import PartitionSpec as P

HEADS = 32
HEAD_DIM = 64
LENGTH = 2048
XBASE = 512
DOCS = 4
EPSILON = 1e-05
MASKED = -1e30
TILE = 256

MESH = pl.DeviceIdType.MESH
F32 = jnp.float32
BF16 = jnp.bfloat16
ANY = pl.BlockSpec(memory_space=pl.ANY)
INSIDE = pl.BlockSpec(memory_space=pltpu.VMEM)


def nn(a, b):
    return lax.dot_general(a, b, (((1,), (0,)), ((), ())), preferred_element_type=F32)


def nt(a, b):
    return lax.dot_general(a, b, (((1,), (1,)), ((), ())), preferred_element_type=F32)


def tn(a, b):
    return lax.dot_general(a, b, (((0,), (0,)), ((), ())), preferred_element_type=F32)


def norm_parts(values):
    average = jnp.mean(values, axis=-1, keepdims=True)
    centered = values - average
    spread = jnp.mean(centered * centered, axis=-1, keepdims=True)
    scale = lax.rsqrt(spread + EPSILON)
    return centered * scale, scale


def norm_back(grad, normal, scale, gain):
    part = grad * gain
    inner = (
        part
        - jnp.mean(part, axis=-1, keepdims=True)
        - normal * jnp.mean(part * normal, axis=-1, keepdims=True)
    )
    return scale * inner, jnp.sum(grad * normal, axis=0)


def places():
    me = lax.axis_index("seq")
    core = lax.rem(me, 2)
    along_x = lax.rem(me // 2, 2)
    along_y = me // 4
    twin = 1 - 2 * core
    near_x = me + 2 - 4 * along_x
    near_y = me + 4 - 8 * along_y
    across = near_x + 4 - 8 * along_y
    return me, twin, near_x, near_y, across


def remote(src, dst, send_sem, recv_sem, partner):
    return pltpu.make_async_remote_copy(
        src_ref=src,
        dst_ref=dst,
        send_sem=send_sem,
        recv_sem=recv_sem,
        device_id={"seq": partner},
        device_id_type=MESH,
    )


def meet(partners):
    barrier = pltpu.get_barrier_semaphore()
    for partner in partners:
        pl.semaphore_signal(
            barrier, inc=1, device_id={"seq": partner}, device_id_type=MESH
        )
    pl.semaphore_wait(barrier, len(partners))


def gather_copies(x_ref, o_ref, send_sem, recv_sem):
    me, twin, near_x, near_y, across = places()
    half = x_ref.shape[0] // 2
    low, high = pl.ds(0, half), pl.ds(half, half)

    def copy(k, src, dst, partner):
        return remote(src, dst, send_sem.at[k], recv_sem.at[k], partner)

    def relay(k, owner, rows, partner):
        place = o_ref.at[owner, rows]
        return copy(k, place, place, partner)

    return [
        copy(0, x_ref.at[low], o_ref.at[me, low], near_x),
        copy(1, x_ref.at[high], o_ref.at[me, high], near_y),
        copy(2, x_ref.at[high], o_ref.at[me, high], near_x),
        copy(3, x_ref.at[low], o_ref.at[me, low], near_y),
        copy(4, x_ref, o_ref.at[me], me + twin),
        relay(5, near_x, low, near_y),
        relay(6, near_y, high, near_x),
        relay(7, near_x, low, me + twin),
        relay(8, near_y, high, me + twin),
        relay(9, near_x, high, me + twin),
        relay(10, near_y, low, me + twin),
        relay(11, across, low, me + twin),
        relay(12, across, high, me + twin),
    ]


def gather_run(sends, between=None):
    sends[0].wait_recv()
    sends[5].start()
    sends[7].start()
    sends[1].wait_recv()
    sends[6].start()
    sends[8].start()
    sends[2].wait_recv()
    sends[9].start()
    sends[3].wait_recv()
    sends[10].start()
    if between is not None:
        between()
    sends[5].wait_recv()
    sends[11].start()
    sends[6].wait_recv()
    sends[12].start()
    for k in (4, 7, 8, 9, 10, 11, 12):
        sends[k].wait_recv()
    for send in sends:
        send.wait_send()


def meet_all(n, depth):
    me = lax.axis_index("seq")
    z = lax.axis_index("batch")
    barrier = pltpu.get_barrier_semaphore()
    for k in range(1, n):
        pl.semaphore_signal(
            barrier, inc=1, device_id={"seq": lax.rem(me + k, n)}, device_id_type=MESH
        )
    for k in range(1, depth):
        pl.semaphore_signal(
            barrier,
            inc=1,
            device_id={"batch": lax.rem(z + k, depth)},
            device_id_type=MESH,
        )
    pl.semaphore_wait(barrier, n + depth - 2)


def line_remote(src, dst, send_sem, recv_sem, partner):
    return pltpu.make_async_remote_copy(
        src_ref=src,
        dst_ref=dst,
        send_sem=send_sem,
        recv_sem=recv_sem,
        device_id={"batch": partner},
        device_id_type=MESH,
    )


class Line:
    def __init__(self, depth, source, target, send_sem, recv_sem):
        self.depth, self.source, self.target = depth, source, target
        self.send_sem, self.recv_sem = send_sem, recv_sem
        self.z = lax.axis_index("batch")

    def message(self, side, k):
        sign = 2 * side - 1
        owner = self.z - sign * k
        return line_remote(
            self.source(owner, k),
            self.target(owner),
            self.send_sem.at[side, k],
            self.recv_sem.at[side, k],
            self.z + sign,
        )

    def sends(self, side, k):
        sign = 2 * side - 1
        owner, target = self.z - sign * k, self.z + sign
        inside = (owner >= 0) & (owner < self.depth)
        return inside & (target >= 0) & (target < self.depth)

    def land(self, k):
        for side in (0, 1):
            sign = 2 * side - 1
            owner = self.z - sign * (k + 1)

            @pl.when((owner >= 0) & (owner < self.depth))
            def _():
                place = self.target(owner)
                line_remote(
                    place,
                    place,
                    self.send_sem.at[side, k],
                    self.recv_sem.at[side, k],
                    self.z - sign,
                ).wait_recv()

    def start(self, k):
        for side in (0, 1):

            @pl.when(self.sends(side, k))
            def _():
                self.message(side, k).start()

    def sent(self, k):
        for side in (0, 1):

            @pl.when(self.sends(side, k))
            def _():
                self.message(side, k).wait_send()


def gather_kernel(
    n, depth, x_ref, near_ref, o_ref, all_ref, keep_ref, local_sem, send_sem, recv_sem, line_send, line_recv
):
    me, twin, near_x, near_y, _ = places()
    z = lax.axis_index("batch")
    own = pltpu.make_async_copy(x_ref, o_ref.at[me], local_sem.at[0])
    own.start()

    def load(shift):
        return pltpu.make_async_copy(
            near_ref.at[:, z + shift], keep_ref.at[1 + shift], local_sem.at[2 + shift]
        )

    def keep(shift):
        return pltpu.make_async_copy(
            keep_ref.at[1 + shift], all_ref.at[:, z + shift], local_sem.at[5 + shift]
        )

    def kept(shift):
        return (z + shift >= 0) & (z + shift < depth)

    for shift in (-1, 0, 1):

        @pl.when(kept(shift))
        def _():
            load(shift).start()

    meet_all(n, depth)
    sends = gather_copies(x_ref, o_ref, send_sem, recv_sem)
    for k in range(5):
        sends[k].start()
    line = Line(
        depth,
        lambda owner, k: (near_ref if k == 1 else all_ref).at[:, owner],
        lambda owner: all_ref.at[:, owner],
        line_send,
        line_recv,
    )
    line.start(1)
    for shift in (-1, 0, 1):

        @pl.when(kept(shift))
        def _():
            load(shift).wait()
            keep(shift).start()

    def between():
        for k in range(2, depth - 1):
            line.land(k - 1)
            line.start(k)

    gather_run(sends, between)
    line.land(depth - 2)
    for k in range(1, depth - 1):
        line.sent(k)
    for shift in (-1, 0, 1):

        @pl.when(kept(shift))
        def _():
            keep(shift).wait()

    own.wait()


def gather_seq(block, near, collective_id):
    n, depth = lax.axis_size("seq"), lax.axis_size("batch")
    rows, width = block.shape
    if n != 8:
        return lax.all_gather(block, "seq", axis=0, tiled=True), near
    gathered, every = pl.pallas_call(
        functools.partial(gather_kernel, n, depth),
        out_shape=(
            jax.ShapeDtypeStruct((n, rows, width), block.dtype),
            jax.ShapeDtypeStruct(near.shape, near.dtype),
        ),
        in_specs=[INSIDE, ANY],
        out_specs=(ANY, ANY),
        scratch_shapes=[
            pltpu.VMEM((3, n, *near.shape[2:]), near.dtype),
            pltpu.SemaphoreType.DMA((7,)),
            pltpu.SemaphoreType.DMA((13,)),
            pltpu.SemaphoreType.DMA((13,)),
            pltpu.SemaphoreType.DMA((2, depth)),
            pltpu.SemaphoreType.DMA((2, depth)),
        ],
        compiler_params=pltpu.CompilerParams(
            collective_id=collective_id, has_side_effects=True
        ),
        name="gather_seq",
    )(block, near)
    return gathered.reshape(n * rows, width), every.reshape(-1, near.shape[-1])


def lane_tables(place):
    half = HEAD_DIM // 2
    lane = lax.broadcasted_iota(jnp.int32, (1, 128), 1)
    channel = lax.rem(lane, half).astype(F32)
    inverse = jnp.exp(channel * (-math.log(10000.0) / half))
    zeta = (channel * (2.0 / HEAD_DIM) + 0.4) / 1.4
    sign = jnp.where(lax.rem(lane, HEAD_DIM) < half, -1.0, 1.0)
    angle = place * inverse
    growth = jnp.exp((place - 0.5 * LENGTH) * (1.0 / XBASE) * jnp.log(zeta))
    shrink = 1.0 / growth
    cosine = jnp.cos(angle)
    sine = jnp.sin(angle) * sign
    return cosine * growth, sine * growth, cosine * shrink, sine * shrink


def start_kernel(
    n, depth, x_ref, w_ref, wd_ref, pos_ref,
    o_ref, wt_ref, wc_ref, cq_ref, sq_ref, ck_ref, sk_ref,
    keep_w, keep_c, local_sem, send_sem, recv_sem, hop_send, hop_recv, col_send, col_recv, line_send, line_recv,
):
    z = lax.axis_index("batch")
    rows_z = wc_ref.shape[2]
    cols = wc_ref.shape[3]
    me, twin, near_x, near_y, _ = places()
    own = pltpu.make_async_copy(x_ref, o_ref.at[me], local_sem.at[0])
    own.start()
    wd_rows = pl.ds(pl.multiple_of(z * rows_z, rows_z), rows_z)

    def column(k):
        return wd_ref.at[wd_rows, pl.ds(pl.multiple_of(k * cols, cols), cols)]

    load_column = pltpu.make_async_copy(column(me), keep_c, local_sem.at[4])
    own_column = pltpu.make_async_copy(keep_c, wc_ref.at[me, z], local_sem.at[5])
    load_column.start()
    meet_all(n, depth)
    load_column.wait()
    own_column.start()
    turns = [
        remote(
            column(lax.rem(me + k, n)),
            wc_ref.at[me, z],
            col_send.at[k],
            col_recv.at[k],
            lax.rem(me + k, n),
        )
        for k in range(1, n)
    ]
    for turn in turns:
        turn.start()
    sends = gather_copies(x_ref, o_ref, send_sem, recv_sem)
    for k in range(5):
        sends[k].start()

    line = Line(
        depth,
        lambda owner, k: wc_ref.at[:, owner],
        lambda owner: wc_ref.at[:, owner],
        line_send,
        line_recv,
    )

    def hop(j, part, target):
        return remote(
            w_ref.at[j], wt_ref.at[part], hop_send.at[j], hop_recv.at[part], target
        )

    def load(j):
        return pltpu.make_async_copy(w_ref.at[j], keep_w, local_sem.at[6])

    def here(j, part):
        return pltpu.make_async_copy(keep_w, wt_ref.at[part], local_sem.at[1 + j])

    for j in range(3):
        block = 3 * me + j
        target = lax.rem(block, n)
        for part in range(3):
            inside = block // n == part

            @pl.when(inside & (target != me))
            def _():
                hop(j, part, target).start()

            @pl.when(inside & (target == me))
            def _():
                load(j).start()
                load(j).wait()
                here(j, part).start()

    @pl.loop(0, pos_ref.shape[0])
    def _(r):
        at = pl.ds(pl.multiple_of(r * 128, 128), 128)
        places_here = jnp.broadcast_to(pos_ref[pl.ds(r, 1), :], (128, 128)).T
        tables = lane_tables(places_here)
        for ref, table in zip((cq_ref, sq_ref, ck_ref, sk_ref), tables, strict=True):
            ref[at] = table

    own_column.wait()
    for turn in turns:
        turn.wait_recv()
    line.start(0)
    gather_run(sends)
    line.land(0)
    line.sent(0)
    for turn in turns:
        turn.wait_send()
    for j in range(3):
        block = 3 * me + j
        target = lax.rem(block, n)

        for part in range(3):
            inside = block // n == part

            @pl.when(inside & (target != me))
            def _():
                hop(j, part, target).wait_send()

            @pl.when(inside & (target == me))
            def _():
                here(j, part).wait()

    for part in range(3):
        source = (part * n + me) // 3

        @pl.when(source != me)
        def _():
            hop(0, part, source).wait_recv()

    own.wait()


def start_exchange(block, w_qkv, w_down, positions, collective_id):
    n, depth = lax.axis_size("seq"), lax.axis_size("batch")
    rows, width = block.shape
    piece = w_qkv.shape[0] // 3
    w = w_qkv.reshape(3, piece, width)
    if n != 8:
        me = lax.axis_index("seq")
        turned = [
            lax.ppermute(w[j], "seq", [(d, (3 * d + j) % n) for d in range(n)])
            for j in range(3)
        ]
        parts = [pick_part(turned, me, n, part) for part in range(3)]
        place = jnp.broadcast_to(positions[:, None], (positions.shape[0], 128))
        return (
            lax.all_gather(block, "seq", axis=0, tiled=True),
            jnp.concatenate(parts, axis=0),
            lax.all_to_all(w_down, "seq", split_axis=1, concat_axis=0, tiled=True),
            lane_tables(place),
        )
    rows_z, cols = w_down.shape[0] // depth, w_down.shape[1] // n
    inside = pl.BlockSpec(memory_space=pltpu.VMEM)
    table = jax.ShapeDtypeStruct((n * rows, 128), F32)
    gathered, turned, columns, *tables = pl.pallas_call(
        functools.partial(start_kernel, n, depth),
        out_shape=(
            jax.ShapeDtypeStruct((n, rows, width), block.dtype),
            jax.ShapeDtypeStruct((3, piece, width), w.dtype),
            jax.ShapeDtypeStruct((n, depth, rows_z, cols), w_down.dtype),
            *([table] * 4),
        ),
        in_specs=[INSIDE, ANY, ANY, INSIDE],
        out_specs=(ANY, ANY, ANY, *([INSIDE] * 4)),
        scratch_shapes=[
            pltpu.VMEM((piece, width), BF16),
            pltpu.VMEM((rows_z, cols), BF16),
            pltpu.SemaphoreType.DMA((7,)),
            pltpu.SemaphoreType.DMA((13,)),
            pltpu.SemaphoreType.DMA((13,)),
            pltpu.SemaphoreType.DMA((3,)),
            pltpu.SemaphoreType.DMA((3,)),
            pltpu.SemaphoreType.DMA((n,)),
            pltpu.SemaphoreType.DMA((n,)),
            pltpu.SemaphoreType.DMA((2, depth)),
            pltpu.SemaphoreType.DMA((2, depth)),
        ],
        compiler_params=pltpu.CompilerParams(
            collective_id=collective_id, has_side_effects=True
        ),
        name="start_exchange",
    )(block, w, w_down, positions.reshape(-1, 128))
    return (
        gathered.reshape(n * rows, width),
        turned.reshape(3 * piece, width),
        columns,
        tables,
    )


def scatter_kernel(
    p_ref, o_ref, own, twin_in, held, local_sem, send_sem, recv_sem
):
    me, twin, near_x, near_y, across = places()
    rows = p_ref.shape[1]
    half = rows // 2
    low, high = pl.ds(0, half), pl.ds(half, half)
    mine = (across, near_x, near_y, me)

    loads = [
        pltpu.make_async_copy(p_ref.at[block], own.at[i], local_sem.at[i])
        for i, block in enumerate(mine)
    ]
    for load in loads:
        load.start()
    meet((me + twin, near_x, near_y))

    def copy(k, src, dst, partner):
        return remote(src, dst, send_sem.at[k], recv_sem.at[k], partner)

    twins = [
        copy(i, p_ref.at[block + twin], twin_in.at[i], me + twin)
        for i, block in enumerate(mine)
    ]
    for send in twins:
        send.start()
    sends = [
        copy(4, own.at[0, low], held.at[0], near_x),
        copy(5, own.at[0, high], held.at[1], near_y),
        copy(6, own.at[1, low], held.at[2], near_x),
        copy(7, own.at[2, high], held.at[3], near_y),
        copy(8, own.at[1, high], held.at[4], near_x),
        copy(9, own.at[2, low], held.at[5], near_y),
    ]
    step = 32

    def add_twin(i):
        loads[i].wait()
        twins[i].wait_recv()

        @pl.loop(0, rows // step)
        def _(r):
            at = pl.ds(pl.multiple_of(r * step, step), step)
            own[i, at] = (
                own[i, at].astype(F32) + twin_in[i, at].astype(F32)
            ).astype(own.dtype)

    def add_held(i, base, slot):
        @pl.loop(0, half // step)
        def _(r):
            at = pl.ds(pl.multiple_of(r * step, step), step)
            to = pl.ds(pl.multiple_of(base + r * step, step), step)
            own[i, to] = (
                own[i, to].astype(F32) + held[slot, at].astype(F32)
            ).astype(own.dtype)

    add_twin(0)
    sends[0].start()
    sends[1].start()
    add_twin(1)
    sends[2].start()
    add_twin(2)
    sends[3].start()
    sends[1].wait_recv()
    add_held(1, half, 1)
    sends[4].start()
    sends[0].wait_recv()
    add_held(2, 0, 0)
    sends[5].start()
    loads[3].wait()
    twins[3].wait_recv()
    for k in (2, 3, 4, 5):
        sends[k].wait_recv()

    def final(base, first, second):
        @pl.loop(0, half // step)
        def _(r):
            at = pl.ds(pl.multiple_of(r * step, step), step)
            to = pl.ds(pl.multiple_of(base + r * step, step), step)
            o_ref[to] = (
                own[3, to].astype(F32)
                + twin_in[3, to].astype(F32)
                + held[first, at].astype(F32)
                + held[second, at].astype(F32)
            )

    final(0, 2, 5)
    final(half, 3, 4)
    for send in twins + sends:
        send.wait_send()


def scatter_seq(partial, collective_id):
    n = lax.axis_size("seq")
    rows, width = partial.shape[0] // n, partial.shape[1]
    if n != 8:
        return lax.psum_scatter(
            partial, "seq", scatter_dimension=0, tiled=True
        ).astype(F32)
    return pl.pallas_call(
        scatter_kernel,
        out_shape=jax.ShapeDtypeStruct((rows, width), F32),
        in_specs=[ANY],
        out_specs=pl.BlockSpec(memory_space=pltpu.VMEM),
        scratch_shapes=[
            pltpu.VMEM((4, rows, width), BF16),
            pltpu.VMEM((4, rows, width), BF16),
            pltpu.VMEM((6, rows // 2, width), BF16),
            pltpu.SemaphoreType.DMA((4,)),
            pltpu.SemaphoreType.DMA((10,)),
            pltpu.SemaphoreType.DMA((10,)),
        ],
        compiler_params=pltpu.CompilerParams(
            collective_id=collective_id,
            has_side_effects=True,
            vmem_limit_bytes=32 * 1024 * 1024,
        ),
        name="scatter_seq",
    )(partial.reshape(n, rows, width))


def heads_to_tokens_kernel(n, x_ref, o_ref, keep, local_sem, send_sem, recv_sem):
    me = lax.axis_index("seq")
    rows = o_ref.shape[0]
    cols = x_ref.shape[1]
    exchange(
        n,
        me,
        lambda k: x_ref.at[pl.ds(pl.multiple_of(k * rows, rows), rows)],
        o_ref.at[:, pl.ds(pl.multiple_of(me * cols, cols), cols)],
        keep,
        local_sem,
        send_sem,
        recv_sem,
    )


def exchange(n, me, source, target, keep, local_sem, send_sem, recv_sem):
    load = pltpu.make_async_copy(source(me), keep, local_sem.at[0])
    own = pltpu.make_async_copy(keep, target, local_sem.at[1])
    load.start()
    barrier = pltpu.get_barrier_semaphore()
    for k in range(1, n):
        pl.semaphore_signal(
            barrier,
            inc=1,
            device_id={"seq": lax.rem(me + k, n)},
            device_id_type=MESH,
        )
    pl.semaphore_wait(barrier, n - 1)
    copies = []
    for k in range(1, n):
        partner = lax.rem(me + k, n)
        copies.append(
            pltpu.make_async_remote_copy(
                src_ref=source(partner),
                dst_ref=target,
                send_sem=send_sem.at[k],
                recv_sem=recv_sem.at[k],
                device_id={"seq": partner},
                device_id_type=MESH,
            )
        )
        copies[-1].start()
    load.wait()
    own.start()
    for copy in copies:
        copy.wait()
    own.wait()


def heads_to_tokens(heads, collective_id):
    n = lax.axis_size("seq")
    total, cols = heads.shape
    rows = total // n
    return pl.pallas_call(
        functools.partial(heads_to_tokens_kernel, n),
        out_shape=jax.ShapeDtypeStruct((rows, n * cols), heads.dtype),
        in_specs=[ANY],
        out_specs=ANY,
        scratch_shapes=[
            pltpu.VMEM((rows, cols), heads.dtype),
            pltpu.SemaphoreType.DMA((2,)),
            pltpu.SemaphoreType.DMA((n,)),
            pltpu.SemaphoreType.DMA((n,)),
        ],
        compiler_params=pltpu.CompilerParams(
            collective_id=collective_id, has_side_effects=True
        ),
        name="heads_to_tokens",
    )(heads)


def tokens_to_heads_kernel(n, x_ref, o_ref, keep, local_sem, send_sem, recv_sem):
    me = lax.axis_index("seq")
    rows = x_ref.shape[0]
    cols = o_ref.shape[1]
    exchange(
        n,
        me,
        lambda k: x_ref.at[:, pl.ds(pl.multiple_of(k * cols, cols), cols)],
        o_ref.at[pl.ds(pl.multiple_of(me * rows, rows), rows)],
        keep,
        local_sem,
        send_sem,
        recv_sem,
    )


def tokens_to_heads(tokens, collective_id):
    n = lax.axis_size("seq")
    rows, total = tokens.shape
    return pl.pallas_call(
        functools.partial(tokens_to_heads_kernel, n),
        out_shape=jax.ShapeDtypeStruct((rows * n, total // n), tokens.dtype),
        in_specs=[ANY],
        out_specs=ANY,
        scratch_shapes=[
            pltpu.VMEM((rows, total // n), tokens.dtype),
            pltpu.SemaphoreType.DMA((2,)),
            pltpu.SemaphoreType.DMA((n,)),
            pltpu.SemaphoreType.DMA((n,)),
        ],
        compiler_params=pltpu.CompilerParams(
            collective_id=collective_id, has_side_effects=True
        ),
        name="tokens_to_heads",
    )(tokens)


def swap_halves(values):
    width = values.shape[-1]
    half = HEAD_DIM // 2
    lane = lax.broadcasted_iota(jnp.int32, values.shape, 1)
    ahead = pltpu.roll(values, width - half, 1)
    behind = pltpu.roll(values, half, 1)
    return jnp.where(lane % HEAD_DIM < half, ahead, behind)


def spread_lanes(table, width):
    return jnp.concatenate([table] * (width // table.shape[-1]), axis=-1)


def qkv_kernel(
    x_ref, w_ref, cq_ref, sq_ref, ck_ref, sk_ref,
    q_ref, k_ref, v_ref, kt_ref, vt_ref,
):
    x = x_ref[...]
    width = q_ref.shape[1]
    query = nt(x, w_ref[0:width])
    query = query * spread_lanes(cq_ref[...], width) + swap_halves(
        query
    ) * spread_lanes(sq_ref[...], width)
    q_ref[...] = query.astype(BF16) * (HEAD_DIM**-0.5)
    keys = nt(x, w_ref[width : 2 * width])
    keys = keys * spread_lanes(ck_ref[...], width) + swap_halves(
        keys
    ) * spread_lanes(sk_ref[...], width)
    k_ref[...] = keys.astype(BF16)
    kt_ref[...] = keys.T.astype(BF16)
    values = nt(x, w_ref[2 * width :])
    v_ref[...] = values.astype(BF16)
    vt_ref[...] = values.T.astype(BF16)


def project_qkv(x, w, tables):
    length, width = x.shape
    cols = w.shape[0] // 3
    steps = length // TILE
    weight = pl.BlockSpec((3 * cols, width), lambda i: (0, 0))
    table = pl.BlockSpec((TILE, tables[0].shape[1]), lambda i: (i, 0))
    row_out = pl.BlockSpec((TILE, cols), lambda i: (i, 0))
    col_out = pl.BlockSpec((cols, TILE), lambda i: (0, i))
    rows = jax.ShapeDtypeStruct((length, cols), BF16)
    columns = jax.ShapeDtypeStruct((cols, length), BF16)
    return pl.pallas_call(
        qkv_kernel,
        grid=(steps,),
        out_shape=(rows, rows, rows, columns, columns),
        in_specs=[pl.BlockSpec((TILE, width), lambda i: (i, 0))]
        + [weight]
        + [table] * 4,
        out_specs=(row_out, row_out, row_out, col_out, col_out),
        compiler_params=pltpu.CompilerParams(vmem_limit_bytes=40 * 1024 * 1024),
        cost_estimate=pl.CostEstimate(
            flops=6 * length * width * cols,
            bytes_accessed=2 * length * width + 6 * width * cols + 10 * length * cols,
            transcendentals=0,
        ),
        name="project_qkv",
    )(x, w, *tables)


def pair_mask(start_row, i, j):
    key_place = j * TILE + lax.broadcasted_iota(jnp.int32, (TILE, TILE), 0)
    query_place = i * TILE + lax.broadcasted_iota(jnp.int32, (TILE, TILE), 1)
    return (key_place <= query_place) & (key_place >= start_row)


def head_rows(query, heads):
    lane = lax.broadcasted_iota(jnp.int32, query.shape, 1) // HEAD_DIM
    zero = jnp.zeros_like(query)
    return [jnp.where(lane == h, query, zero) for h in range(heads)]


def attend_kernel(
    heads, first_ref, start_ref, q_ref, k_ref, vt_ref, o_ref, lse_ref, peak, total, mixed
):
    i = pl.program_id(0)
    queries = head_rows(q_ref[...], heads)
    start_row = start_ref[...]

    def block(j, first):
        at = pl.ds(pl.multiple_of(j * TILE, TILE), TILE)
        keys = k_ref[at, :]
        mask = pair_mask(start_row, i, j)
        for h in range(heads):
            here = slice(h * HEAD_DIM, (h + 1) * HEAD_DIM)
            scores = jnp.where(mask, nt(keys, queries[h]), MASKED)
            if first:
                new_peak = jnp.max(scores, axis=0, keepdims=True)
                expo = jnp.exp(scores - new_peak)
                total[h : h + 1] = jnp.sum(expo, axis=0, keepdims=True)
                mixed[here] = nn(vt_ref[here, at], expo.astype(BF16))
            else:
                old_peak = peak[h : h + 1]
                new_peak = jnp.maximum(old_peak, jnp.max(scores, axis=0, keepdims=True))
                expo = jnp.exp(scores - new_peak)
                shrink = jnp.exp(old_peak - new_peak)
                total[h : h + 1] = total[h : h + 1] * shrink + jnp.sum(
                    expo, axis=0, keepdims=True
                )
                mixed[here] = mixed[here] * shrink + nn(
                    vt_ref[here, at], expo.astype(BF16)
                )
            peak[h : h + 1] = new_peak

    block(i, True)

    @pl.loop(0, i - first_ref[i])
    def _(t):
        block(i - 1 - t, False)

    for h in range(heads):
        here = slice(h * HEAD_DIM, (h + 1) * HEAD_DIM)
        mixed[here] = mixed[here] / total[h : h + 1]
    o_ref[...] = mixed[...].T.astype(BF16)
    lse_ref[0] = peak[...] + jnp.log(total[...])


def attend(first, start, q, k, vt):
    length, cols = q.shape
    heads = cols // HEAD_DIM
    steps = length // TILE
    row = pl.BlockSpec((TILE, cols), lambda i, *_: (i, 0))
    return pl.pallas_call(
        functools.partial(attend_kernel, heads),
        out_shape=(
            jax.ShapeDtypeStruct((length, cols), BF16),
            jax.ShapeDtypeStruct((steps, heads, TILE), F32),
        ),
        grid_spec=pltpu.PrefetchScalarGridSpec(
            num_scalar_prefetch=1,
            grid=(steps,),
            in_specs=[
                pl.BlockSpec((1, TILE), lambda i, *_: (0, i)),
                row,
                pl.BlockSpec((length, cols), lambda i, *_: (0, 0)),
                pl.BlockSpec((cols, length), lambda i, *_: (0, 0)),
            ],
            out_specs=(
                row,
                pl.BlockSpec((1, heads, TILE), lambda i, *_: (i, 0, 0)),
            ),
            scratch_shapes=[
                pltpu.VMEM((heads, TILE), F32),
                pltpu.VMEM((heads, TILE), F32),
                pltpu.VMEM((cols, TILE), F32),
            ],
        ),
        compiler_params=pltpu.CompilerParams(vmem_limit_bytes=32 * 1024 * 1024),
        cost_estimate=pl.CostEstimate(
            flops=4 * length * 1024 * cols,
            bytes_accessed=8 * length * cols,
            transcendentals=length * 1024 * heads,
        ),
        name="attend",
    )(first, start, q, k, vt)


def attend_back_kernel(
    heads, first_ref, start_ref, q_ref, k_ref, kt_ref, v_ref, o_ref, lse_ref, do_ref,
    cq_ref, sq_ref, ck_ref, sk_ref, grad_ref, dqt, dk_sum, dv_sum,
):
    i = pl.program_id(0)
    steps = pl.num_programs(0)
    width = q_ref.shape[1]
    queries = head_rows(q_ref[...], heads)
    grads = head_rows(do_ref[...], heads)
    start_row = start_ref[...]
    product = (do_ref[...].astype(F32) * o_ref[...].astype(F32)).T
    inner = [
        jnp.sum(product[h * HEAD_DIM : (h + 1) * HEAD_DIM], axis=0, keepdims=True)
        for h in range(heads)
    ]

    def block(j, first):
        at = pl.ds(pl.multiple_of(j * TILE, TILE), TILE)
        keys = k_ref[at, :]
        values = v_ref[at, :]
        mask = pair_mask(start_row, i, j)
        key_term = None
        value_term = None
        for h in range(heads):
            here = slice(h * HEAD_DIM, (h + 1) * HEAD_DIM)
            scores = nt(keys, queries[h])
            weights = jnp.where(mask, jnp.exp(scores - lse_ref[0, h : h + 1]), 0.0)
            grad_weights = nt(values, grads[h])
            grad_scores = (weights * (grad_weights - inner[h])).astype(BF16)
            term = nn(weights.astype(BF16), grads[h])
            value_term = term if value_term is None else value_term + term
            term = nn(grad_scores, queries[h])
            key_term = term if key_term is None else key_term + term
            term = nn(kt_ref[here, at], grad_scores)
            if first:
                dqt[here] = term
            else:
                dqt[here] = dqt[here] + term
        if first:
            dk_sum[at] = key_term
            dv_sum[at] = value_term
        else:
            dk_sum[at] = dk_sum[at] + key_term
            dv_sum[at] = dv_sum[at] + value_term

    block(i, True)

    @pl.loop(0, i - first_ref[i])
    def _(t):
        block(i - 1 - t, False)

    def unturn(grad, cosine, sine):
        grad = grad.astype(BF16).astype(F32)
        cosine = spread_lanes(cosine, width)
        sine = spread_lanes(sine, width)
        return (grad * cosine - swap_halves(grad) * sine).astype(BF16)

    rows = pl.ds(pl.multiple_of(i * TILE, TILE), TILE)
    grad_ref[rows, 0:width] = unturn(
        dqt[...].T * (HEAD_DIM**-0.5), cq_ref[rows, :], sq_ref[rows, :]
    )

    @pl.when(i == steps - 1)
    def _():
        @pl.loop(0, steps)
        def _(j):
            at = pl.ds(pl.multiple_of(j * TILE, TILE), TILE)
            grad_ref[at, width : 2 * width] = unturn(
                dk_sum[at], ck_ref[at, :], sk_ref[at, :]
            )
            grad_ref[at, 2 * width :] = dv_sum[at].astype(BF16)


def attend_back(first, start, q, k, kt, v, o, lse, do, tables):
    length, cols = q.shape
    heads = cols // HEAD_DIM
    steps = length // TILE
    row = pl.BlockSpec((TILE, cols), lambda i, *_: (i, 0))
    whole = pl.BlockSpec((length, cols), lambda i, *_: (0, 0))
    table = pl.BlockSpec((length, tables[0].shape[1]), lambda i, *_: (0, 0))
    return pl.pallas_call(
        functools.partial(attend_back_kernel, heads),
        out_shape=jax.ShapeDtypeStruct((length, 3 * cols), BF16),
        grid_spec=pltpu.PrefetchScalarGridSpec(
            num_scalar_prefetch=1,
            grid=(steps,),
            in_specs=[
                pl.BlockSpec((1, TILE), lambda i, *_: (0, i)),
                row,
                whole,
                pl.BlockSpec((cols, length), lambda i, *_: (0, 0)),
                whole,
                row,
                pl.BlockSpec((1, heads, TILE), lambda i, *_: (i, 0, 0)),
                row,
            ]
            + [table] * 4,
            out_specs=pl.BlockSpec((length, 3 * cols), lambda i, *_: (0, 0)),
            scratch_shapes=[
                pltpu.VMEM((cols, TILE), F32),
                pltpu.VMEM((length, cols), F32),
                pltpu.VMEM((length, cols), F32),
            ],
        ),
        compiler_params=pltpu.CompilerParams(vmem_limit_bytes=48 * 1024 * 1024),
        cost_estimate=pl.CostEstimate(
            flops=10 * length * 1024 * cols,
            bytes_accessed=16 * length * cols,
            transcendentals=length * 1024 * heads,
        ),
        name="attend_back",
    )(first, start, q, k, kt, v, o, lse, do, *tables)


def upper_kernel(
    x_ref, wu_ref, c_ref, wd_ref, gain_ref, act_ref, slope_ref, grad_ref, stat_ref
):
    upper = nt(x_ref[...], wu_ref[...])
    grad = nn(c_ref[...], wd_ref[...])
    below = 0.5 * (1.0 + lax.erf(upper * (0.5**0.5)))
    act = upper * below
    slope = below + upper * (jnp.exp(-0.5 * upper * upper) * ((2.0 * math.pi) ** -0.5))
    act_ref[...] = act
    slope_ref[...] = slope.astype(BF16)
    grad_ref[...] = grad
    part = grad * gain_ref[...]
    average = jnp.mean(act, axis=-1, keepdims=True)
    centered = act - average
    spread = jnp.sum(centered * centered, axis=-1, keepdims=True)
    part_sum = jnp.sum(part, axis=-1, keepdims=True)
    cross = jnp.sum(part * centered, axis=-1, keepdims=True)
    lane = lax.broadcasted_iota(jnp.int32, (x_ref.shape[0], 128), 1)
    columns = jnp.where(
        lane == 0,
        average,
        jnp.where(lane == 1, spread, jnp.where(lane == 2, part_sum, cross)),
    )
    stat_ref[...] = columns.T[:8]


def upper_pass(x, w_up, cot, w_down, gain):
    length, width = x.shape
    feats = w_up.shape[0]
    rows = TILE
    row = pl.BlockSpec((rows, width), lambda i: (i, 0))
    out = pl.BlockSpec((rows, feats), lambda i: (i, 0))
    return pl.pallas_call(
        upper_kernel,
        grid=(length // rows,),
        out_shape=(
            jax.ShapeDtypeStruct((length, feats), F32),
            jax.ShapeDtypeStruct((length, feats), BF16),
            jax.ShapeDtypeStruct((length, feats), F32),
            jax.ShapeDtypeStruct((8, length), F32),
        ),
        in_specs=[
            row,
            pl.BlockSpec((feats, width), lambda i: (0, 0)),
            row,
            pl.BlockSpec((width, feats), lambda i: (0, 0)),
            pl.BlockSpec((1, feats), lambda i: (0, 0)),
        ],
        out_specs=(out, out, out, pl.BlockSpec((8, rows), lambda i: (0, i))),
        compiler_params=pltpu.CompilerParams(vmem_limit_bytes=48 * 1024 * 1024),
        cost_estimate=pl.CostEstimate(
            flops=4 * length * width * feats,
            bytes_accessed=8 * length * width + 8 * length * feats,
            transcendentals=2 * length * feats,
        ),
        name="upper_pass",
    )(x, w_up, cot, w_down, gain)


def hidden_kernel(act_ref, slope_ref, grad_ref, stat_ref, gain_ref, hid_ref, gu_ref, gg_ref):
    i = pl.program_id(0)
    stats = stat_ref[...].T
    average = stats[:, 0:1]
    scale = stats[:, 1:2]
    part_mean = stats[:, 2:3]
    cross_mean = stats[:, 3:4]
    gain = gain_ref[...]
    normal = (act_ref[...] - average) * scale
    grad = grad_ref[...]
    hid_ref[...] = (normal * gain).astype(BF16)
    back = scale * (grad * gain - part_mean - normal * cross_mean)
    gu_ref[...] = (slope_ref[...].astype(F32) * back).astype(BF16)
    term = jnp.sum(grad * normal, axis=0, keepdims=True)

    @pl.when(i == 0)
    def _():
        gg_ref[...] = term

    @pl.when(i > 0)
    def _():
        gg_ref[...] = gg_ref[...] + term


def hidden_pass(act, slope, grad, stats, gain):
    length, feats = act.shape
    out = pl.BlockSpec((TILE, feats), lambda i: (i, 0))
    one = pl.BlockSpec((1, feats), lambda i: (0, 0))
    return pl.pallas_call(
        hidden_kernel,
        grid=(length // TILE,),
        out_shape=(
            jax.ShapeDtypeStruct((length, feats), BF16),
            jax.ShapeDtypeStruct((length, feats), BF16),
            jax.ShapeDtypeStruct((1, feats), F32),
        ),
        in_specs=[out, out, out, pl.BlockSpec((8, TILE), lambda i: (0, i)), one],
        out_specs=(out, out, one),
        compiler_params=pltpu.CompilerParams(vmem_limit_bytes=40 * 1024 * 1024),
        cost_estimate=pl.CostEstimate(
            flops=12 * length * feats,
            bytes_accessed=14 * length * feats,
            transcendentals=0,
        ),
        name="hidden_pass",
    )(act, slope, grad, stats, gain)


def stat_kernel(n, feats, x_ref, o_ref, held, send_sem, recv_sem):
    me = lax.axis_index("seq")
    held[me] = x_ref[...]
    meet([lax.rem(me + k, n) for k in range(1, n)])
    copies = [
        remote(x_ref, held.at[me], send_sem.at[k], recv_sem.at[k], lax.rem(me + k, n))
        for k in range(1, n)
    ]
    for copy in copies:
        copy.start()
    for copy in copies:
        copy.wait()
    average = held[0, 0:1]
    for d in range(1, n):
        average = average + held[d, 0:1]
    average = average * (1.0 / n)
    spread = jnp.zeros_like(average)
    part = jnp.zeros_like(average)
    cross = jnp.zeros_like(average)
    for d in range(n):
        shift = held[d, 0:1] - average
        spread = spread + held[d, 1:2] + feats * (shift * shift)
        part = part + held[d, 2:3]
        cross = cross + held[d, 3:4] + shift * held[d, 2:3]
    whole = 1.0 / (n * feats)
    scale = lax.rsqrt(spread * whole + EPSILON)
    o_ref[0:1] = average
    o_ref[1:2] = scale
    o_ref[2:3] = part * whole
    o_ref[3:4] = cross * scale * whole
    o_ref[4:8] = jnp.zeros((4, average.shape[1]), F32)


def join_stats(stat, feats, collective_id):
    n = lax.axis_size("seq")
    inside = pl.BlockSpec(memory_space=pltpu.VMEM)
    return pl.pallas_call(
        functools.partial(stat_kernel, n, feats),
        out_shape=jax.ShapeDtypeStruct(stat.shape, F32),
        in_specs=[inside],
        out_specs=inside,
        scratch_shapes=[
            pltpu.VMEM((n, *stat.shape), F32),
            pltpu.SemaphoreType.DMA((n,)),
            pltpu.SemaphoreType.DMA((n,)),
        ],
        compiler_params=pltpu.CompilerParams(
            collective_id=collective_id, has_side_effects=True
        ),
        name="join_stats",
    )(stat)


STEP = 32


def mix_kernel(att_ref, x_ref, w_ref, gm_ref, gf_ref, mix_ref, mid_ref, ffn_ref):
    j = pl.program_id(0)
    rows = att_ref.shape[0]
    cols = w_ref.shape[0]

    @pl.when(j == 0)
    def _():
        @pl.loop(0, rows // STEP)
        def _(r):
            at = pl.ds(pl.multiple_of(r * STEP, STEP), STEP)
            normal, _ = norm_parts(att_ref[at].astype(F32))
            mix_ref[at] = (normal * gm_ref[...]).astype(BF16)

    here = pl.ds(pl.multiple_of(j * cols, cols), cols)
    mid_ref[:, here] = x_ref[:, here].astype(F32) + nt(mix_ref[...], w_ref[...])

    @pl.when(j == pl.num_programs(0) - 1)
    def _():
        @pl.loop(0, rows // STEP)
        def _(r):
            at = pl.ds(pl.multiple_of(r * STEP, STEP), STEP)
            normal, _ = norm_parts(mid_ref[at])
            ffn_ref[at] = (normal * gf_ref[...]).astype(BF16)


def mix_pass(attended, x, w_out, gain_mix, gain_ffn):
    rows, width = x.shape
    cols = TILE
    n = width // cols
    whole = pl.BlockSpec((rows, width), lambda j: (0, 0))
    gain = pl.BlockSpec((1, width), lambda j: (0, 0))
    low = jax.ShapeDtypeStruct((rows, width), BF16)
    return pl.pallas_call(
        mix_kernel,
        grid=(n,),
        out_shape=(low, jax.ShapeDtypeStruct((rows, width), F32), low),
        in_specs=[
            whole,
            whole,
            pl.BlockSpec((cols, width), lambda j: (j, 0)),
            gain,
            gain,
        ],
        out_specs=(whole, whole, whole),
        compiler_params=pltpu.CompilerParams(vmem_limit_bytes=32 * 1024 * 1024),
        cost_estimate=pl.CostEstimate(
            flops=2 * rows * width * width,
            bytes_accessed=2 * width * width + 12 * rows * width,
            transcendentals=0,
        ),
        name="mix_pass",
    )(attended, x, w_out, gain_mix[None], gain_ffn[None])


def branch_kernel(
    g_ref, mid_ref, cot_ref, att_ref, w_ref, gm_ref, gf_ref,
    gmid_ref, gbr_ref, gatt_ref, ggf_ref, ggm_ref, total,
):
    j = pl.program_id(0)
    rows = att_ref.shape[0]
    cols = w_ref.shape[0]

    @pl.when(j == 0)
    def _():
        ggf_ref[...] = jnp.zeros_like(ggf_ref)
        total[...] = jnp.zeros_like(total)

        @pl.loop(0, rows // STEP)
        def _(r):
            at = pl.ds(pl.multiple_of(r * STEP, STEP), STEP)
            normal, scale = norm_parts(mid_ref[at])
            part, gain_part = norm_back(g_ref[at], normal, scale, gf_ref[...])
            ggf_ref[...] += gain_part[None]
            grad = cot_ref[at].astype(F32) + part
            gmid_ref[at] = grad
            gbr_ref[at] = grad.astype(BF16)

    here = pl.ds(pl.multiple_of(j * cols, cols), cols)
    total[...] += nn(gbr_ref[:, here], w_ref[...])

    @pl.when(j == pl.num_programs(0) - 1)
    def _():
        ggm_ref[...] = jnp.zeros_like(ggm_ref)

        @pl.loop(0, rows // STEP)
        def _(r):
            at = pl.ds(pl.multiple_of(r * STEP, STEP), STEP)
            normal, scale = norm_parts(att_ref[at].astype(F32))
            part, gain_part = norm_back(total[at], normal, scale, gm_ref[...])
            ggm_ref[...] += gain_part[None]
            gatt_ref[at] = part.astype(BF16)


def branch_pass(grad_ffn_in, middle, cot, attended, w_out, gain_mix, gain_ffn):
    rows, width = cot.shape
    cols = TILE
    n = width // cols
    whole = pl.BlockSpec((rows, width), lambda j: (0, 0))
    gain = pl.BlockSpec((1, width), lambda j: (0, 0))
    low = jax.ShapeDtypeStruct((rows, width), BF16)
    sums = jax.ShapeDtypeStruct((1, width), F32)
    return pl.pallas_call(
        branch_kernel,
        grid=(n,),
        out_shape=(jax.ShapeDtypeStruct((rows, width), F32), low, low, sums, sums),
        in_specs=[
            whole,
            whole,
            whole,
            whole,
            pl.BlockSpec((cols, width), lambda j: (j, 0)),
            gain,
            gain,
        ],
        out_specs=(whole, whole, whole, gain, gain),
        scratch_shapes=[pltpu.VMEM((rows, width), F32)],
        compiler_params=pltpu.CompilerParams(vmem_limit_bytes=40 * 1024 * 1024),
        cost_estimate=pl.CostEstimate(
            flops=2 * rows * width * width,
            bytes_accessed=2 * width * width + 20 * rows * width,
            transcendentals=0,
        ),
        name="branch_pass",
    )(grad_ffn_in, middle, cot, attended, w_out, gain_mix[None], gain_ffn[None])


CHUNK = 128


def finish_kernel(
    n, depth, gq_ref, gd_ref, pw_ref, pn_ref, po_ref, x_ref, grad_ref, mid_ref, ga_ref, gm_ref, gf_ref, gh_ref,
    oq_ref, od_ref, ow_ref, gi_ref, out_ref, sums_ref,
    own, twin_in, held, zown, zin, gain_here, gain_row, gain_pack, gain_line,
    local_sem, load_sem, send_sem, recv_sem, keep_sem,
    up_send, up_recv, down_send, down_recv, home_send, home_recv, gain_send, gain_recv,
):
    me, twin, near_x, near_y, across = places()
    z = lax.axis_index("batch")
    rows, width = pn_ref.shape[1:]
    half = rows // 2
    low, high = pl.ds(0, half), pl.ds(half, half)
    mine = (across, near_x, near_y, me)
    _, chunk, cols = zown.shape
    across_width = width // cols
    per_part = (gq_ref.shape[1] // chunk) * across_width
    turned = gq_ref.shape[0] * per_part
    outer = turned + (rows // chunk) * across_width
    per_source = gd_ref.shape[1] // chunk
    chunks = zown.shape[0]
    per_side = chunks // 2

    def cut(i, size):
        return pl.ds(pl.multiple_of(i * size, size), size)

    def wide(i):
        return cut(i // across_width, chunk), cut(lax.rem(i, across_width), cols)

    line_loads = []
    for g in range(turned):
        source = gq_ref.at[(g // per_part, *wide(g % per_part))]
        line_loads.append(pltpu.make_async_copy(source, zown.at[g], load_sem.at[g]))
    for g in range(outer, chunks):
        source = gd_ref.at[
            (g - outer) // per_source, cut((g - outer) % per_source, chunk)
        ]
        line_loads.append(pltpu.make_async_copy(source, zown.at[g], load_sem.at[g]))
    for load in line_loads:
        load.start()
    partials = (pw_ref, pn_ref, po_ref)
    loads = [
        [
            pltpu.make_async_copy(p.at[block], own.at[m, i], local_sem.at[4 * m + i])
            for i, block in enumerate(mine)
        ]
        for m, p in enumerate(partials)
    ]
    for part in loads:
        for load in part:
            load.start()
    meet_all(n, depth)

    def copy(m, k, src, dst, partner):
        return remote(src, dst, send_sem.at[m, k], recv_sem.at[m, k], partner)

    twins = [
        [
            copy(m, i, p.at[block + twin], twin_in.at[m, i], me + twin)
            for i, block in enumerate(mine)
        ]
        for m, p in enumerate(partials)
    ]
    sends = [
        [
            copy(m, 4, own.at[m, 0, low], held.at[m, 0], near_x),
            copy(m, 5, own.at[m, 0, high], held.at[m, 1], near_y),
            copy(m, 6, own.at[m, 1, low], held.at[m, 2], near_x),
            copy(m, 7, own.at[m, 2, high], held.at[m, 3], near_y),
            copy(m, 8, own.at[m, 1, high], held.at[m, 4], near_x),
            copy(m, 9, own.at[m, 2, low], held.at[m, 5], near_y),
        ]
        for m in range(3)
    ]
    for part in twins:
        for send in part:
            send.start()

    def add_twin(m, i):
        loads[m][i].wait()
        twins[m][i].wait_recv()

        @pl.loop(0, rows // STEP)
        def _(r):
            at = cut(r, STEP)
            own[m, i, at] = (
                own[m, i, at].astype(F32) + twin_in[m, i, at].astype(F32)
            ).astype(BF16)

    def add_held(m, i, base, slot):
        @pl.loop(0, half // STEP)
        def _(r):
            at = cut(r, STEP)
            to = pl.ds(pl.multiple_of(base + r * STEP, STEP), STEP)
            own[m, i, to] = (
                own[m, i, to].astype(F32) + held[m, slot, at].astype(F32)
            ).astype(BF16)

    def first(m):
        add_twin(m, 0)
        sends[m][0].start()
        sends[m][1].start()
        add_twin(m, 1)
        sends[m][2].start()
        add_twin(m, 2)
        sends[m][3].start()

    def second(m):
        sends[m][1].wait_recv()
        add_held(m, 1, half, 1)
        sends[m][4].start()
        sends[m][0].wait_recv()
        add_held(m, 2, 0, 0)
        sends[m][5].start()

    def last(m, store):
        loads[m][3].wait()
        twins[m][3].wait_recv()
        for k in (2, 3, 4, 5):
            sends[m][k].wait_recv()
        for base, one, two in ((0, 2, 5), (half, 3, 4)):

            @pl.loop(0, half // STEP)
            def _(r):
                at = cut(r, STEP)
                place = base + r * STEP
                to = pl.ds(pl.multiple_of(place, STEP), STEP)
                store(
                    place,
                    to,
                    own[m, 3, to].astype(F32)
                    + twin_in[m, 3, to].astype(F32)
                    + held[m, one, at].astype(F32)
                    + held[m, two, at].astype(F32),
                )

    def store_line(place, to, value):
        value = value.astype(BF16)
        for side in range(across_width):
            zown[
                turned + (place // chunk) * across_width + side,
                pl.ds(pl.multiple_of(lax.rem(place, chunk), STEP), STEP),
            ] = value[:, side * cols : (side + 1) * cols]

    def store_inputs(place, to, value):
        normal, scale = norm_parts(x_ref[to].astype(F32))
        part, gain_part = norm_back(value, normal, scale, ga_ref[...])
        gi_ref[to] = grad_ref[to] + part
        gain_here[0:1] = gain_here[0:1] + gain_part[None]

    def store_outputs(place, to, value):
        out_ref[to] = (mid_ref[to] + value).astype(BF16)

    def home(part):
        block = part * n + me
        return block // 3, lax.rem(block, 3)

    def deliver_far(g):
        target, slot = home(g // per_part)
        piece = lax.rem(g, per_part)
        return remote(
            zin.at[g],
            oq_ref.at[(slot, *wide(piece))],
            home_send.at[g],
            home_recv.at[slot, piece],
            target,
        )

    def deliver_near(g):
        _, slot = home(g // per_part)
        return pltpu.make_async_copy(
            zin.at[g], oq_ref.at[(slot, *wide(lax.rem(g, per_part)))], keep_sem.at[g]
        )

    def deliver_out(g):
        return pltpu.make_async_copy(
            zin.at[g], ow_ref.at[wide(g - turned)], keep_sem.at[g]
        )

    def deliver_down(g):
        at = g - outer
        place = cut(lax.rem(at, per_source), chunk), cut(at // per_source, cols)
        return pltpu.make_async_copy(zin.at[g], od_ref.at[place], keep_sem.at[g])

    def deliver(g, wait):
        target, _ = home(g // per_part)

        @pl.when((g < turned) & (target != me))
        def _():
            deliver_far(g).wait_send() if wait else deliver_far(g).start()

        @pl.when((g < turned) & (target == me))
        def _():
            deliver_near(g).wait() if wait else deliver_near(g).start()

        @pl.when((g >= turned) & (g < outer))
        def _():
            deliver_out(g).wait() if wait else deliver_out(g).start()

        @pl.when(g >= outer)
        def _():
            deliver_down(g).wait() if wait else deliver_down(g).start()

    def go_up(g, ahead):
        return line_remote(zown.at[g], zin.at[g], up_send.at[g], up_recv.at[g], ahead)

    def go_down(g, behind):
        return line_remote(
            zin.at[g], zin.at[g], down_send.at[g], down_recv.at[g], behind
        )

    def ranks(side):
        if side == 0:
            return z, z + 1, z - 1
        return depth - 1 - z, z - 1, z + 1

    def add_line(g, target):
        @pl.loop(0, chunk // STEP)
        def _(r):
            at = cut(r, STEP)
            target[g, at] = (zown[g, at].astype(F32) + zin[g, at].astype(F32)).astype(
                BF16
            )

    def line_step(t):
        for side in (0, 1):
            rank, ahead, behind = ranks(side)
            c = t - rank
            g = 2 * c + side
            there = (c >= 0) & (c < per_side)

            @pl.when(there & (rank == 0))
            def _():
                go_up(g, ahead).start()

            @pl.when(there & (rank > 0) & (rank < depth - 1))
            def _():
                go_up(g, behind).wait_recv()
                add_line(g, zown)
                go_up(g, ahead).start()

            @pl.when(there & (rank == depth - 1))
            def _():
                go_up(g, behind).wait_recv()
                add_line(g, zin)
                go_down(g, behind).start()
                deliver(g, False)

            c_back = t - 2 * (depth - 1) + rank
            g_back = 2 * c_back + side
            there = (c_back >= 0) & (c_back < per_side) & (rank < depth - 1)

            @pl.when(there)
            def _():
                go_down(g_back, ahead).wait_recv()

            @pl.when(there & (rank > 0))
            def _():
                go_down(g_back, behind).start()

            @pl.when(there)
            def _():
                deliver(g_back, False)

    gain_here[...] = jnp.zeros_like(gain_here)
    first(0)
    for load in line_loads:
        load.wait()
    line_step(0)
    line_step(1)
    first(1)
    line_step(2)
    second(0)
    line_step(3)
    last(0, store_line)
    for t in (4, 5, 6):
        line_step(t)
    first(2)
    for t in (7, 8):
        line_step(t)
    second(1)
    for t in (9, 10):
        line_step(t)
    last(1, store_inputs)

    gain_here[1:2] = gm_ref[...]
    gain_here[2:3] = gf_ref[...]
    gain_here[3:4, 0 : gh_ref.shape[1]] = gh_ref[...]
    gain_row[me] = gain_here[...]
    rounds = [
        remote(
            gain_here,
            gain_row.at[me],
            gain_send.at[0, k],
            gain_recv.at[0, k],
            lax.rem(me + k, n),
        )
        for k in range(1, n)
    ]
    for send in rounds:
        send.start()
    for t in (11, 12):
        line_step(t)
    second(2)
    for t in (13, 14):
        line_step(t)
    last(2, store_outputs)
    line_step(15)
    for send in rounds:
        send.wait()
    total = gain_row[0]
    for d in range(1, n):
        total = total + gain_row[d]
    gain_pack[0:8] = total
    for d in range(n):
        gain_pack[8 + d : 9 + d] = gain_row[d, 3:4]
    gain_line[z] = gain_pack[...]
    rounds = [
        line_remote(
            gain_pack,
            gain_line.at[z],
            gain_send.at[1, k],
            gain_recv.at[1, k],
            lax.rem(z + k, depth),
        )
        for k in range(1, depth)
    ]
    for send in rounds:
        send.start()
    for t in range(16, per_side + 2 * (depth - 1)):
        line_step(t)
    for send in rounds:
        send.wait()
    total = gain_line[0]
    for d in range(1, depth):
        total = total + gain_line[d]
    sums_ref[...] = total

    for m in range(3):
        for send in twins[m] + sends[m]:
            send.wait_send()
    for g in range(chunks):
        rank, ahead, behind = ranks(g % 2)

        @pl.when(rank < depth - 1)
        def _():
            go_up(g, ahead).wait_send()

        @pl.when(rank > 0)
        def _():
            go_down(g, behind).wait_send()

        deliver(g, True)
    for slot in range(3):
        block = 3 * me + slot
        source = lax.rem(block, n)

        @pl.when(source != me)
        def _():
            for piece in range(per_part):
                remote(
                    zin.at[0],
                    oq_ref.at[(slot, *wide(piece))],
                    home_send.at[0],
                    home_recv.at[slot, piece],
                    source,
                ).wait_recv()


def finish(
    grad_qkv, grad_down, part_out, part_normed, part_outputs, x, grad_middle, middle, gain, gains, collective_id
):
    n, depth = lax.axis_size("seq"), lax.axis_size("batch")
    rows, width = part_out.shape[0] // n, part_out.shape[1]
    cols = grad_qkv.shape[1]
    sources, _, feats = grad_down.shape
    if n != 8 or depth != 4:
        me = lax.axis_index("seq")
        blocks = lax.psum(grad_qkv, "batch")
        back = [
            lax.ppermute(
                give_part(blocks, me, n, j),
                "seq",
                [((3 * d + j) % n, d) for d in range(n)],
            )
            for j in range(3)
        ]
        w_out = lax.psum(scatter_seq(part_out, None).astype(BF16), "batch")
        normal, scale = norm_parts(x.astype(F32))
        part, gain_part = norm_back(scatter_seq(part_normed, None), normal, scale, gain)
        shared = [lax.psum(g, ("batch", "seq")) for g in (gain_part, gains[0][0], gains[1][0])]
        hidden = lax.all_gather(lax.psum(gains[2][0], "batch"), "seq", axis=0, tiled=True)
        down = lax.psum(grad_down, "batch")
        return (
            jnp.concatenate(back, axis=0),
            jnp.swapaxes(down, 0, 1).reshape(rows, sources * feats),
            w_out,
            grad_middle + part,
            (middle + scatter_seq(part_outputs, None)).astype(BF16),
            (*shared, hidden),
        )
    chunks = (
        3 * cols * width + rows * width + sources * rows * feats
    ) // (CHUNK * feats)
    dma = pltpu.SemaphoreType.DMA
    line = pltpu.VMEM((chunks, CHUNK, feats), BF16)
    w_qkv, w_down, w_out, grad_inputs, outputs, sums = pl.pallas_call(
        functools.partial(finish_kernel, n, depth),
        out_shape=(
            jax.ShapeDtypeStruct((3, cols, width), BF16),
            jax.ShapeDtypeStruct((rows, sources * feats), BF16),
            jax.ShapeDtypeStruct((rows, width), BF16),
            jax.ShapeDtypeStruct((rows, width), F32),
            jax.ShapeDtypeStruct((rows, width), BF16),
            jax.ShapeDtypeStruct((16, width), F32),
        ),
        in_specs=[ANY] * 5 + [INSIDE] * 7,
        out_specs=(ANY, ANY, ANY, INSIDE, INSIDE, INSIDE),
        scratch_shapes=[
            pltpu.VMEM((3, 4, rows, width), BF16),
            pltpu.VMEM((3, 4, rows, width), BF16),
            pltpu.VMEM((3, 6, rows // 2, width), BF16),
            line,
            line,
            pltpu.VMEM((8, width), F32),
            pltpu.VMEM((n, 8, width), F32),
            pltpu.VMEM((16, width), F32),
            pltpu.VMEM((depth, 16, width), F32),
            dma((12,)),
            dma((chunks,)),
            dma((3, 10)),
            dma((3, 10)),
            dma((chunks,)),
            dma((chunks,)),
            dma((chunks,)),
            dma((chunks,)),
            dma((chunks,)),
            dma((chunks,)),
            dma((3, cols * width // (CHUNK * feats))),
            dma((2, n)),
            dma((2, n)),
        ],
        compiler_params=pltpu.CompilerParams(
            collective_id=collective_id,
            has_side_effects=True,
            vmem_limit_bytes=60 * 1024 * 1024,
        ),
        name="finish",
    )(
        grad_qkv,
        grad_down,
        *[p.reshape(n, rows, width) for p in (part_out, part_normed, part_outputs)],
        x,
        grad_middle,
        middle,
        gain[None],
        *gains,
    )
    return (
        w_qkv.reshape(3 * cols, width),
        w_down,
        w_out,
        grad_inputs,
        outputs,
        (sums[0], sums[1], sums[2], sums[8:, :feats].reshape(-1)),
    )


def body(
    inputs,
    segment_ids,
    w_qkv,
    w_out,
    w_up,
    w_down,
    gain_attn,
    gain_mix,
    gain_ffn,
    gain_hidden,
    cotangent,
):
    _, local, width = inputs.shape
    n, depth = lax.axis_size("seq"), lax.axis_size("batch")
    me = lax.axis_index("seq")
    length = local * n
    feats = w_up.shape[0]
    x_low = inputs[0]
    x = x_low.astype(F32)
    cot = cotangent[0]
    segment = segment_ids[0]

    w_out_full = lax.all_gather(w_out, "seq", axis=0, tiled=True)
    normed = (norm_parts(x)[0] * gain_attn).astype(BF16)
    before = [jnp.sum((segment < d).astype(jnp.int32)) for d in range(1, DOCS)]
    start = jnp.zeros_like(segment)
    for d in range(1, DOCS):
        start = jnp.where(segment == d, before[d - 1], start)
    positions = jnp.arange(length, dtype=jnp.int32) - start
    first = start[::TILE] // TILE
    start_row = start[None, :]

    normed_full, w_heads, w_down_near, tables = start_exchange(
        normed, w_qkv, w_down, positions.astype(F32), 1
    )
    cot_late, _ = lax.optimization_barrier((cot, w_heads))
    cot_full = lax.all_gather(cot_late, "seq", axis=0, tiled=True)

    q, k, v, kt, vt = project_qkv(normed_full, w_heads, tables)
    attended_heads, lse = attend(first, start_row, q, k, vt)
    attended = heads_to_tokens(attended_heads, 2)
    mix_in, middle, ffn_in = mix_pass(attended, x_low, w_out_full, gain_mix, gain_ffn)
    ffn_full, w_down_cols = gather_seq(ffn_in, w_down_near, 3)

    gain_here = lax.dynamic_slice_in_dim(gain_hidden, me * feats, feats, 0)[None, :]
    act, slope, grad_hidden, stat = upper_pass(
        ffn_full, w_up, cot_full, w_down_cols, gain_here
    )
    stats = join_stats(stat, feats, 8)
    hidden, grad_upper, grad_gain_here = hidden_pass(act, slope, grad_hidden, stats, gain_here)

    grad_w_up = tn(grad_upper, ffn_full).astype(BF16)
    grad_upper, grad_w_up = lax.optimization_barrier((grad_upper, grad_w_up))
    grad_w_up = lax.psum(grad_w_up, "batch")
    grad_w_down = tn(cot_full, hidden).astype(BF16).reshape(n, local, feats)
    grad_upper, grad_w_down = lax.optimization_barrier((grad_upper, grad_w_down))
    grad_ffn_in = scatter_seq(nn(grad_upper, w_up).astype(BF16), 4)
    grad_middle, grad_branch, grad_att, grad_gain_ffn, grad_gain_mix = branch_pass(
        grad_ffn_in, middle, cot, attended, w_out_full, gain_mix, gain_ffn
    )
    grad_heads = tokens_to_heads(grad_att, 5)
    grad_w_down, grad_heads = lax.optimization_barrier((grad_w_down, grad_heads))
    grad_w_down = lax.all_to_all(grad_w_down, "seq", split_axis=0, concat_axis=0, tiled=True)
    grads = attend_back(
        first, start_row, q, k, kt, v, attended_heads, lse, grad_heads, tables
    )
    grad_w_qkv, grad_w_down, grad_w_out, grad_inputs, outputs, gains = finish(
        tn(grads, normed_full).astype(BF16).reshape(3, -1, width),
        grad_w_down,
        tn(grad_branch, mix_in).astype(BF16),
        nn(grads, w_heads).astype(BF16),
        nt(hidden, w_down_cols).astype(BF16),
        x_low,
        grad_middle,
        middle,
        gain_attn,
        (grad_gain_mix, grad_gain_ffn, grad_gain_here),
        6,
    )
    return (
        outputs[None],
        grad_inputs[None],
        grad_w_qkv.astype(F32),
        grad_w_out.astype(F32),
        grad_w_up.astype(F32),
        grad_w_down.astype(F32),
        *gains,
    )


def pick_part(turned, me, n, part):
    chosen = turned[0]
    home = part * n + me
    for j in (1, 2):
        chosen = jnp.where(lax.rem(home, 3) == j, turned[j], chosen)
    return chosen


def give_part(blocks, me, n, j):
    chosen = blocks[0]
    for part in (1, 2):
        chosen = jnp.where(lax.rem(part * n + me, 3) == j, blocks[part], chosen)
    return chosen


def solution(mesh):
    in_specs = (
        P("batch", "seq", None),
        P("batch", None),
        P("seq", None),
        P("seq", None),
        P("seq", None),
        P("seq", None),
        P(),
        P(),
        P(),
        P(),
        P("batch", "seq", None),
    )
    out_specs = (
        P("batch", "seq", None),
        P("batch", "seq", None),
        P("seq", None),
        P("seq", None),
        P("seq", None),
        P("seq", None),
        P(),
        P(),
        P(),
        P(),
    )
    return jax.shard_map(body, mesh=mesh, in_specs=in_specs, out_specs=out_specs, check_vma=False)
```

```python
import functools
import math

import jax
import jax.numpy as jnp
from jax import lax
from jax.experimental import pallas as pl
from jax.experimental.pallas import tpu as pltpu
from jax.sharding import PartitionSpec as P

HEADS = 32
HEAD_DIM = 64
LENGTH = 2048
XBASE = 512
DOCS = 4
EPSILON = 1e-05
MASKED = -1e30
TILE = 256
VMEM_LIMIT = 60 * 1024 * 1024

MESH = pl.DeviceIdType.MESH
F32 = jnp.float32
BF16 = jnp.bfloat16
ANY = pl.BlockSpec(memory_space=pl.ANY)
INSIDE = pl.BlockSpec(memory_space=pltpu.VMEM)


def nn(a, b):
    return lax.dot_general(a, b, (((1,), (0,)), ((), ())), preferred_element_type=F32)


def nt(a, b):
    return lax.dot_general(a, b, (((1,), (1,)), ((), ())), preferred_element_type=F32)


def tn(a, b):
    return lax.dot_general(a, b, (((0,), (0,)), ((), ())), preferred_element_type=F32)


def norm_parts(values):
    average = jnp.mean(values, axis=-1, keepdims=True)
    centered = values - average
    spread = jnp.mean(centered * centered, axis=-1, keepdims=True)
    scale = lax.rsqrt(spread + EPSILON)
    return centered * scale, scale


def norm_back(grad, normal, scale, gain):
    part = grad * gain
    inner = (
        part
        - jnp.mean(part, axis=-1, keepdims=True)
        - normal * jnp.mean(part * normal, axis=-1, keepdims=True)
    )
    return scale * inner, jnp.sum(grad * normal, axis=0)


def places():
    me = lax.axis_index("seq")
    core = lax.rem(me, 2)
    along_x = lax.rem(me // 2, 2)
    along_y = me // 4
    twin = 1 - 2 * core
    near_x = me + 2 - 4 * along_x
    near_y = me + 4 - 8 * along_y
    across = near_x + 4 - 8 * along_y
    return me, twin, near_x, near_y, across


def remote(src, dst, send_sem, recv_sem, partner):
    return pltpu.make_async_remote_copy(
        src_ref=src,
        dst_ref=dst,
        send_sem=send_sem,
        recv_sem=recv_sem,
        device_id={"seq": partner},
        device_id_type=MESH,
    )


def meet(partners):
    barrier = pltpu.get_barrier_semaphore()
    for partner in partners:
        pl.semaphore_signal(
            barrier, inc=1, device_id={"seq": partner}, device_id_type=MESH
        )
    pl.semaphore_wait(barrier, len(partners))


def gather_copies(x_ref, o_ref, send_sem, recv_sem):
    me, twin, near_x, near_y, across = places()
    half = x_ref.shape[0] // 2
    low, high = pl.ds(0, half), pl.ds(half, half)

    def copy(k, src, dst, partner):
        return remote(src, dst, send_sem.at[k], recv_sem.at[k], partner)

    def relay(k, owner, rows, partner):
        place = o_ref.at[owner, rows]
        return copy(k, place, place, partner)

    return [
        copy(0, x_ref.at[low], o_ref.at[me, low], near_x),
        copy(1, x_ref.at[high], o_ref.at[me, high], near_y),
        copy(2, x_ref.at[high], o_ref.at[me, high], near_x),
        copy(3, x_ref.at[low], o_ref.at[me, low], near_y),
        copy(4, x_ref, o_ref.at[me], me + twin),
        relay(5, near_x, low, near_y),
        relay(6, near_y, high, near_x),
        relay(7, near_x, low, me + twin),
        relay(8, near_y, high, me + twin),
        relay(9, near_x, high, me + twin),
        relay(10, near_y, low, me + twin),
        relay(11, across, low, me + twin),
        relay(12, across, high, me + twin),
    ]


def gather_run(sends, between=None, later=None):
    sends[0].wait_recv()
    sends[5].start()
    sends[7].start()
    sends[1].wait_recv()
    sends[6].start()
    sends[8].start()
    sends[2].wait_recv()
    sends[9].start()
    sends[3].wait_recv()
    sends[10].start()
    if between is not None:
        between()
    sends[5].wait_recv()
    sends[11].start()
    sends[6].wait_recv()
    sends[12].start()
    if later is not None:
        later()
    for k in (4, 7, 8, 9, 10, 11, 12):
        sends[k].wait_recv()
    for send in sends:
        send.wait_send()


def meet_all(n, depth):
    me = lax.axis_index("seq")
    z = lax.axis_index("batch")
    barrier = pltpu.get_barrier_semaphore()
    for k in range(1, n):
        pl.semaphore_signal(
            barrier, inc=1, device_id={"seq": lax.rem(me + k, n)}, device_id_type=MESH
        )
    for k in range(1, depth):
        pl.semaphore_signal(
            barrier,
            inc=1,
            device_id={"batch": lax.rem(z + k, depth)},
            device_id_type=MESH,
        )
    pl.semaphore_wait(barrier, n + depth - 2)


def line_remote(src, dst, send_sem, recv_sem, partner):
    return pltpu.make_async_remote_copy(
        src_ref=src,
        dst_ref=dst,
        send_sem=send_sem,
        recv_sem=recv_sem,
        device_id={"batch": partner},
        device_id_type=MESH,
    )


class Line:
    def __init__(self, depth, source, target, send_sem, recv_sem):
        self.depth, self.source, self.target = depth, source, target
        self.send_sem, self.recv_sem = send_sem, recv_sem
        self.z = lax.axis_index("batch")

    def message(self, side, k):
        sign = 2 * side - 1
        owner = self.z - sign * k
        return line_remote(
            self.source(owner, k),
            self.target(owner),
            self.send_sem.at[side, k],
            self.recv_sem.at[side, k],
            self.z + sign,
        )

    def sends(self, side, k):
        sign = 2 * side - 1
        owner, target = self.z - sign * k, self.z + sign
        inside = (owner >= 0) & (owner < self.depth)
        return inside & (target >= 0) & (target < self.depth)

    def land(self, k):
        for side in (0, 1):
            sign = 2 * side - 1
            owner = self.z - sign * (k + 1)

            @pl.when((owner >= 0) & (owner < self.depth))
            def _():
                place = self.target(owner)
                line_remote(
                    place,
                    place,
                    self.send_sem.at[side, k],
                    self.recv_sem.at[side, k],
                    self.z - sign,
                ).wait_recv()

    def start(self, k):
        for side in (0, 1):

            @pl.when(self.sends(side, k))
            def _():
                self.message(side, k).start()

    def sent(self, k):
        for side in (0, 1):

            @pl.when(self.sends(side, k))
            def _():
                self.message(side, k).wait_send()


def gather_kernel(
    n, depth, x_ref, near_ref, o_ref, all_ref, keep_ref, local_sem, send_sem, recv_sem, line_send, line_recv
):
    me, twin, near_x, near_y, _ = places()
    z = lax.axis_index("batch")
    own = pltpu.make_async_copy(x_ref, o_ref.at[me], local_sem.at[0])
    own.start()

    def load(shift):
        return pltpu.make_async_copy(
            near_ref.at[:, z + shift], keep_ref.at[1 + shift], local_sem.at[2 + shift]
        )

    def keep(shift):
        return pltpu.make_async_copy(
            keep_ref.at[1 + shift], all_ref.at[:, z + shift], local_sem.at[5 + shift]
        )

    def kept(shift):
        return (z + shift >= 0) & (z + shift < depth)

    for shift in (-1, 0, 1):

        @pl.when(kept(shift))
        def _():
            load(shift).start()

    meet_all(n, depth)
    sends = gather_copies(x_ref, o_ref, send_sem, recv_sem)
    for k in range(5):
        sends[k].start()
    line = Line(
        depth,
        lambda owner, k: (near_ref if k == 1 else all_ref).at[:, owner],
        lambda owner: all_ref.at[:, owner],
        line_send,
        line_recv,
    )
    line.start(1)
    for shift in (-1, 0, 1):

        @pl.when(kept(shift))
        def _():
            load(shift).wait()
            keep(shift).start()

    def between():
        for k in range(2, depth - 1):
            line.land(k - 1)
            line.start(k)

    gather_run(sends, between)
    line.land(depth - 2)
    for k in range(1, depth - 1):
        line.sent(k)
    for shift in (-1, 0, 1):

        @pl.when(kept(shift))
        def _():
            keep(shift).wait()

    own.wait()


def gather_seq(block, near, collective_id):
    n, depth = lax.axis_size("seq"), lax.axis_size("batch")
    rows, width = block.shape
    if n != 8:
        return lax.all_gather(block, "seq", axis=0, tiled=True), near
    gathered, every = pl.pallas_call(
        functools.partial(gather_kernel, n, depth),
        out_shape=(
            jax.ShapeDtypeStruct((n, rows, width), block.dtype),
            jax.ShapeDtypeStruct(near.shape, near.dtype),
        ),
        in_specs=[INSIDE, ANY],
        out_specs=(ANY, ANY),
        scratch_shapes=[
            pltpu.VMEM((3, n, *near.shape[2:]), near.dtype),
            pltpu.SemaphoreType.DMA((7,)),
            pltpu.SemaphoreType.DMA((13,)),
            pltpu.SemaphoreType.DMA((13,)),
            pltpu.SemaphoreType.DMA((2, depth)),
            pltpu.SemaphoreType.DMA((2, depth)),
        ],
        compiler_params=pltpu.CompilerParams(
            collective_id=collective_id, has_side_effects=True, vmem_limit_bytes=VMEM_LIMIT
        ),
        name="gather_seq",
    )(block, near)
    return gathered.reshape(n * rows, width), every.reshape(-1, near.shape[-1])


def lane_tables(place):
    half = HEAD_DIM // 2
    lane = lax.broadcasted_iota(jnp.int32, (1, 128), 1)
    channel = lax.rem(lane, half).astype(F32)
    inverse = jnp.exp(channel * (-math.log(10000.0) / half))
    zeta = (channel * (2.0 / HEAD_DIM) + 0.4) / 1.4
    sign = jnp.where(lax.rem(lane, HEAD_DIM) < half, -1.0, 1.0)
    angle = place * inverse
    growth = jnp.exp((place - 0.5 * LENGTH) * (1.0 / XBASE) * jnp.log(zeta))
    shrink = 1.0 / growth
    cosine = jnp.cos(angle)
    sine = jnp.sin(angle) * sign
    return cosine * growth, sine * growth, cosine * shrink, sine * shrink


def start_kernel(
    n, depth, x_ref, w_ref, wd_ref, pos_ref,
    o_ref, wt_ref, wc_ref, cq_ref, sq_ref, ck_ref, sk_ref,
    keep_w, keep_c, local_sem, send_sem, recv_sem, hop_send, hop_recv, col_send, col_recv,
    line_send, line_recv, w_send, w_recv,
):
    z = lax.axis_index("batch")
    rows_z = wc_ref.shape[2]
    cols = wc_ref.shape[3]
    me, twin, near_x, near_y, _ = places()
    own = pltpu.make_async_copy(x_ref, o_ref.at[me], local_sem.at[0])
    own.start()
    wd_rows = pl.ds(pl.multiple_of(z * rows_z, rows_z), rows_z)

    def column(k):
        return wd_ref.at[wd_rows, pl.ds(pl.multiple_of(k * cols, cols), cols)]

    load_column = pltpu.make_async_copy(column(me), keep_c, local_sem.at[4])
    own_column = pltpu.make_async_copy(keep_c, wc_ref.at[me, z], local_sem.at[5])
    load_column.start()
    meet_all(n, depth)
    load_column.wait()
    own_column.start()
    w_rows = pl.ds(
        pl.multiple_of(z * wt_ref.shape[2], wt_ref.shape[2]), wt_ref.shape[2]
    )

    def hop(j, part, target):
        return remote(
            w_ref.at[j, w_rows], wt_ref.at[part, z], hop_send.at[j], hop_recv.at[part], target
        )

    def load(j):
        return pltpu.make_async_copy(w_ref.at[j, w_rows], keep_w, local_sem.at[6])

    def here(j, part):
        return pltpu.make_async_copy(keep_w, wt_ref.at[part, z], local_sem.at[1 + j])

    for j in range(3):
        block = 3 * me + j
        target = lax.rem(block, n)
        for part in range(3):
            inside = block // n == part

            @pl.when(inside & (target != me))
            def _():
                hop(j, part, target).start()

            @pl.when(inside & (target == me))
            def _():
                load(j).start()
                load(j).wait()
                here(j, part).start()

    turns = [
        remote(
            column(lax.rem(me + k, n)),
            wc_ref.at[me, z],
            col_send.at[k],
            col_recv.at[k],
            lax.rem(me + k, n),
        )
        for k in range(1, n)
    ]
    for turn in turns:
        turn.start()
    sends = gather_copies(x_ref, o_ref, send_sem, recv_sem)
    for k in range(5):
        sends[k].start()

    line = Line(
        depth,
        lambda owner, k: wc_ref.at[:, owner],
        lambda owner: wc_ref.at[:, owner],
        line_send,
        line_recv,
    )

    line_w = Line(
        depth,
        lambda owner, k: wt_ref.at[:, owner],
        lambda owner: wt_ref.at[:, owner],
        w_send,
        w_recv,
    )
    for j in range(3):
        block = 3 * me + j
        target = lax.rem(block, n)
        for part in range(3):

            @pl.when((block // n == part) & (target == me))
            def _():
                here(j, part).wait()

    for part in range(3):
        source = (part * n + me) // 3

        @pl.when(source != me)
        def _():
            hop(0, part, source).wait_recv()

    line_w.start(0)

    @pl.loop(0, pos_ref.shape[0])
    def _(r):
        at = pl.ds(pl.multiple_of(r * 128, 128), 128)
        places_here = jnp.broadcast_to(pos_ref[pl.ds(r, 1), :], (128, 128)).T
        tables = lane_tables(places_here)
        for ref, table in zip((cq_ref, sq_ref, ck_ref, sk_ref), tables, strict=True):
            ref[at] = table

    own_column.wait()
    for turn in turns:
        turn.wait_recv()

    def between():
        line_w.land(0)
        line_w.start(1)
        line.start(0)

    def later():
        for k in range(2, depth - 1):
            line_w.land(k - 1)
            line_w.start(k)

    gather_run(sends, between, later)
    line_w.land(depth - 2)
    line.land(0)
    for k in range(depth - 1):
        line_w.sent(k)
    line.sent(0)
    for turn in turns:
        turn.wait_send()
    for j in range(3):
        block = 3 * me + j
        target = lax.rem(block, n)
        for part in range(3):

            @pl.when((block // n == part) & (target != me))
            def _():
                hop(j, part, target).wait_send()

    own.wait()


def start_exchange(block, w_qkv, w_down, positions, collective_id):
    n, depth = lax.axis_size("seq"), lax.axis_size("batch")
    rows, width = block.shape
    piece = w_qkv.shape[0] // 3
    w = w_qkv.reshape(3, piece, width)
    if n != 8:
        me = lax.axis_index("seq")
        turned = [
            lax.ppermute(w[j], "seq", [(d, (3 * d + j) % n) for d in range(n)])
            for j in range(3)
        ]
        parts = [pick_part(turned, me, n, part) for part in range(3)]
        place = jnp.broadcast_to(positions[:, None], (positions.shape[0], 128))
        return (
            lax.all_gather(block, "seq", axis=0, tiled=True),
            jnp.concatenate(parts, axis=0),
            lax.all_to_all(w_down, "seq", split_axis=1, concat_axis=0, tiled=True),
            lane_tables(place),
        )
    rows_z, cols = w_down.shape[0] // depth, w_down.shape[1] // n
    inside = pl.BlockSpec(memory_space=pltpu.VMEM)
    table = jax.ShapeDtypeStruct((n * rows, 128), F32)
    gathered, turned, columns, *tables = pl.pallas_call(
        functools.partial(start_kernel, n, depth),
        out_shape=(
            jax.ShapeDtypeStruct((n, rows, width), block.dtype),
            jax.ShapeDtypeStruct((3, depth, piece // depth, width), w.dtype),
            jax.ShapeDtypeStruct((n, depth, rows_z, cols), w_down.dtype),
            *([table] * 4),
        ),
        in_specs=[INSIDE, ANY, ANY, INSIDE],
        out_specs=(ANY, ANY, ANY, *([INSIDE] * 4)),
        scratch_shapes=[
            pltpu.VMEM((piece // depth, width), BF16),
            pltpu.VMEM((rows_z, cols), BF16),
            pltpu.SemaphoreType.DMA((7,)),
            pltpu.SemaphoreType.DMA((13,)),
            pltpu.SemaphoreType.DMA((13,)),
            pltpu.SemaphoreType.DMA((3,)),
            pltpu.SemaphoreType.DMA((3,)),
            pltpu.SemaphoreType.DMA((n,)),
            pltpu.SemaphoreType.DMA((n,)),
            pltpu.SemaphoreType.DMA((2, depth)),
            pltpu.SemaphoreType.DMA((2, depth)),
            pltpu.SemaphoreType.DMA((2, depth)),
            pltpu.SemaphoreType.DMA((2, depth)),
        ],
        compiler_params=pltpu.CompilerParams(
            collective_id=collective_id, has_side_effects=True, vmem_limit_bytes=VMEM_LIMIT
        ),
        name="start_exchange",
    )(block, w, w_down, positions.reshape(-1, 128))
    return (
        gathered.reshape(n * rows, width),
        turned.reshape(3 * piece, width),
        columns,
        tables,
    )


def scatter_kernel(
    p_ref, o_ref, own, twin_in, held, local_sem, send_sem, recv_sem
):
    me, twin, near_x, near_y, across = places()
    rows = p_ref.shape[1]
    half = rows // 2
    low, high = pl.ds(0, half), pl.ds(half, half)
    mine = (across, near_x, near_y, me)

    loads = [
        pltpu.make_async_copy(p_ref.at[block], own.at[i], local_sem.at[i])
        for i, block in enumerate(mine)
    ]
    for load in loads:
        load.start()
    meet((me + twin, near_x, near_y))

    def copy(k, src, dst, partner):
        return remote(src, dst, send_sem.at[k], recv_sem.at[k], partner)

    twins = [
        copy(i, p_ref.at[block + twin], twin_in.at[i], me + twin)
        for i, block in enumerate(mine)
    ]
    for send in twins:
        send.start()
    sends = [
        copy(4, own.at[0, low], held.at[0], near_x),
        copy(5, own.at[0, high], held.at[1], near_y),
        copy(6, own.at[1, low], held.at[2], near_x),
        copy(7, own.at[2, high], held.at[3], near_y),
        copy(8, own.at[1, high], held.at[4], near_x),
        copy(9, own.at[2, low], held.at[5], near_y),
    ]
    step = 32

    def add_twin(i):
        loads[i].wait()
        twins[i].wait_recv()

        @pl.loop(0, rows // step)
        def _(r):
            at = pl.ds(pl.multiple_of(r * step, step), step)
            own[i, at] = (
                own[i, at].astype(F32) + twin_in[i, at].astype(F32)
            ).astype(own.dtype)

    def add_held(i, base, slot):
        @pl.loop(0, half // step)
        def _(r):
            at = pl.ds(pl.multiple_of(r * step, step), step)
            to = pl.ds(pl.multiple_of(base + r * step, step), step)
            own[i, to] = (
                own[i, to].astype(F32) + held[slot, at].astype(F32)
            ).astype(own.dtype)

    add_twin(0)
    sends[0].start()
    sends[1].start()
    add_twin(1)
    sends[2].start()
    add_twin(2)
    sends[3].start()
    sends[1].wait_recv()
    add_held(1, half, 1)
    sends[4].start()
    sends[0].wait_recv()
    add_held(2, 0, 0)
    sends[5].start()
    loads[3].wait()
    twins[3].wait_recv()
    for k in (2, 3, 4, 5):
        sends[k].wait_recv()

    def final(base, first, second):
        @pl.loop(0, half // step)
        def _(r):
            at = pl.ds(pl.multiple_of(r * step, step), step)
            to = pl.ds(pl.multiple_of(base + r * step, step), step)
            o_ref[to] = (
                own[3, to].astype(F32)
                + twin_in[3, to].astype(F32)
                + held[first, at].astype(F32)
                + held[second, at].astype(F32)
            )

    final(0, 2, 5)
    final(half, 3, 4)
    for send in twins + sends:
        send.wait_send()


def scatter_seq(partial, collective_id):
    n = lax.axis_size("seq")
    rows, width = partial.shape[0] // n, partial.shape[1]
    if n != 8:
        return lax.psum_scatter(
            partial, "seq", scatter_dimension=0, tiled=True
        ).astype(F32)
    return pl.pallas_call(
        scatter_kernel,
        out_shape=jax.ShapeDtypeStruct((rows, width), F32),
        in_specs=[ANY],
        out_specs=pl.BlockSpec(memory_space=pltpu.VMEM),
        scratch_shapes=[
            pltpu.VMEM((4, rows, width), BF16),
            pltpu.VMEM((4, rows, width), BF16),
            pltpu.VMEM((6, rows // 2, width), BF16),
            pltpu.SemaphoreType.DMA((4,)),
            pltpu.SemaphoreType.DMA((10,)),
            pltpu.SemaphoreType.DMA((10,)),
        ],
        compiler_params=pltpu.CompilerParams(
            collective_id=collective_id,
            has_side_effects=True,
            vmem_limit_bytes=VMEM_LIMIT,
        ),
        name="scatter_seq",
    )(partial.reshape(n, rows, width))


def heads_to_tokens_kernel(n, x_ref, o_ref, keep, local_sem, send_sem, recv_sem):
    me = lax.axis_index("seq")
    rows = o_ref.shape[0]
    cols = x_ref.shape[1]
    exchange(
        n,
        me,
        lambda k: x_ref.at[pl.ds(pl.multiple_of(k * rows, rows), rows)],
        o_ref.at[:, pl.ds(pl.multiple_of(me * cols, cols), cols)],
        keep,
        local_sem,
        send_sem,
        recv_sem,
    )


def exchange(n, me, source, target, keep, local_sem, send_sem, recv_sem):
    load = pltpu.make_async_copy(source(me), keep, local_sem.at[0])
    own = pltpu.make_async_copy(keep, target, local_sem.at[1])
    load.start()
    barrier = pltpu.get_barrier_semaphore()
    for k in range(1, n):
        pl.semaphore_signal(
            barrier,
            inc=1,
            device_id={"seq": lax.rem(me + k, n)},
            device_id_type=MESH,
        )
    pl.semaphore_wait(barrier, n - 1)
    copies = []
    for k in range(1, n):
        partner = lax.rem(me + k, n)
        copies.append(
            pltpu.make_async_remote_copy(
                src_ref=source(partner),
                dst_ref=target,
                send_sem=send_sem.at[k],
                recv_sem=recv_sem.at[k],
                device_id={"seq": partner},
                device_id_type=MESH,
            )
        )
        copies[-1].start()
    load.wait()
    own.start()
    for copy in copies:
        copy.wait()
    own.wait()


def heads_to_tokens(heads, collective_id):
    n = lax.axis_size("seq")
    total, cols = heads.shape
    rows = total // n
    return pl.pallas_call(
        functools.partial(heads_to_tokens_kernel, n),
        out_shape=jax.ShapeDtypeStruct((rows, n * cols), heads.dtype),
        in_specs=[ANY],
        out_specs=ANY,
        scratch_shapes=[
            pltpu.VMEM((rows, cols), heads.dtype),
            pltpu.SemaphoreType.DMA((2,)),
            pltpu.SemaphoreType.DMA((n,)),
            pltpu.SemaphoreType.DMA((n,)),
        ],
        compiler_params=pltpu.CompilerParams(
            collective_id=collective_id, has_side_effects=True, vmem_limit_bytes=VMEM_LIMIT
        ),
        name="heads_to_tokens",
    )(heads)


def tokens_to_heads_kernel(n, x_ref, o_ref, keep, local_sem, send_sem, recv_sem):
    me = lax.axis_index("seq")
    rows = x_ref.shape[0]
    cols = o_ref.shape[1]
    exchange(
        n,
        me,
        lambda k: x_ref.at[:, pl.ds(pl.multiple_of(k * cols, cols), cols)],
        o_ref.at[pl.ds(pl.multiple_of(me * rows, rows), rows)],
        keep,
        local_sem,
        send_sem,
        recv_sem,
    )


def tokens_to_heads(tokens, collective_id):
    n = lax.axis_size("seq")
    rows, total = tokens.shape
    return pl.pallas_call(
        functools.partial(tokens_to_heads_kernel, n),
        out_shape=jax.ShapeDtypeStruct((rows * n, total // n), tokens.dtype),
        in_specs=[ANY],
        out_specs=ANY,
        scratch_shapes=[
            pltpu.VMEM((rows, total // n), tokens.dtype),
            pltpu.SemaphoreType.DMA((2,)),
            pltpu.SemaphoreType.DMA((n,)),
            pltpu.SemaphoreType.DMA((n,)),
        ],
        compiler_params=pltpu.CompilerParams(
            collective_id=collective_id, has_side_effects=True, vmem_limit_bytes=VMEM_LIMIT
        ),
        name="tokens_to_heads",
    )(tokens)


def swap_halves(values):
    width = values.shape[-1]
    half = HEAD_DIM // 2
    lane = lax.broadcasted_iota(jnp.int32, values.shape, 1)
    ahead = pltpu.roll(values, width - half, 1)
    behind = pltpu.roll(values, half, 1)
    return jnp.where(lane % HEAD_DIM < half, ahead, behind)


def spread_lanes(table, width):
    return jnp.concatenate([table] * (width // table.shape[-1]), axis=-1)


def qkv_kernel(
    x_ref, w_ref, cq_ref, sq_ref, ck_ref, sk_ref,
    q_ref, k_ref, v_ref, kt_ref, vt_ref,
):
    x = x_ref[...]
    width = q_ref.shape[1]
    query = nt(x, w_ref[0:width])
    query = query * spread_lanes(cq_ref[...], width) + swap_halves(
        query
    ) * spread_lanes(sq_ref[...], width)
    q_ref[...] = query.astype(BF16) * (HEAD_DIM**-0.5)
    keys = nt(x, w_ref[width : 2 * width])
    keys = keys * spread_lanes(ck_ref[...], width) + swap_halves(
        keys
    ) * spread_lanes(sk_ref[...], width)
    k_ref[...] = keys.astype(BF16)
    kt_ref[...] = keys.T.astype(BF16)
    values = nt(x, w_ref[2 * width :])
    v_ref[...] = values.astype(BF16)
    vt_ref[...] = values.T.astype(BF16)


def project_qkv(x, w, tables):
    length, width = x.shape
    cols = w.shape[0] // 3
    steps = length // TILE
    weight = pl.BlockSpec((3 * cols, width), lambda i: (0, 0))
    table = pl.BlockSpec((TILE, tables[0].shape[1]), lambda i: (i, 0))
    row_out = pl.BlockSpec((TILE, cols), lambda i: (i, 0))
    col_out = pl.BlockSpec((cols, TILE), lambda i: (0, i))
    rows = jax.ShapeDtypeStruct((length, cols), BF16)
    columns = jax.ShapeDtypeStruct((cols, length), BF16)
    return pl.pallas_call(
        qkv_kernel,
        grid=(steps,),
        out_shape=(rows, rows, rows, columns, columns),
        in_specs=[pl.BlockSpec((TILE, width), lambda i: (i, 0))]
        + [weight]
        + [table] * 4,
        out_specs=(row_out, row_out, row_out, col_out, col_out),
        compiler_params=pltpu.CompilerParams(vmem_limit_bytes=VMEM_LIMIT),
        cost_estimate=pl.CostEstimate(
            flops=6 * length * width * cols,
            bytes_accessed=2 * length * width + 6 * width * cols + 10 * length * cols,
            transcendentals=0,
        ),
        name="project_qkv",
    )(x, w, *tables)


def pair_mask(start_row, i, j):
    key_place = j * TILE + lax.broadcasted_iota(jnp.int32, (TILE, TILE), 0)
    query_place = i * TILE + lax.broadcasted_iota(jnp.int32, (TILE, TILE), 1)
    return (key_place <= query_place) & (key_place >= start_row)


def head_rows(query, heads):
    lane = lax.broadcasted_iota(jnp.int32, query.shape, 1) // HEAD_DIM
    zero = jnp.zeros_like(query)
    return [jnp.where(lane == h, query, zero) for h in range(heads)]


def attend_kernel(
    heads, first_ref, start_ref, q_ref, k_ref, vt_ref, o_ref, lse_ref, peak, total, mixed
):
    i = pl.program_id(0)
    queries = head_rows(q_ref[...], heads)
    start_row = start_ref[...]

    def block(j, first):
        at = pl.ds(pl.multiple_of(j * TILE, TILE), TILE)
        keys = k_ref[at, :]
        mask = pair_mask(start_row, i, j)
        for h in range(heads):
            here = slice(h * HEAD_DIM, (h + 1) * HEAD_DIM)
            scores = jnp.where(mask, nt(keys, queries[h]), MASKED)
            if first:
                new_peak = jnp.max(scores, axis=0, keepdims=True)
                expo = jnp.exp(scores - new_peak)
                total[h : h + 1] = jnp.sum(expo, axis=0, keepdims=True)
                mixed[here] = nn(vt_ref[here, at], expo.astype(BF16))
            else:
                old_peak = peak[h : h + 1]
                new_peak = jnp.maximum(old_peak, jnp.max(scores, axis=0, keepdims=True))
                expo = jnp.exp(scores - new_peak)
                shrink = jnp.exp(old_peak - new_peak)
                total[h : h + 1] = total[h : h + 1] * shrink + jnp.sum(
                    expo, axis=0, keepdims=True
                )
                mixed[here] = mixed[here] * shrink + nn(
                    vt_ref[here, at], expo.astype(BF16)
                )
            peak[h : h + 1] = new_peak

    block(i, True)

    @pl.loop(0, i - first_ref[i])
    def _(t):
        block(i - 1 - t, False)

    for h in range(heads):
        here = slice(h * HEAD_DIM, (h + 1) * HEAD_DIM)
        mixed[here] = mixed[here] / total[h : h + 1]
    o_ref[...] = mixed[...].T.astype(BF16)
    lse_ref[0] = peak[...] + jnp.log(total[...])


def attend(first, start, q, k, vt):
    length, cols = q.shape
    heads = cols // HEAD_DIM
    steps = length // TILE
    row = pl.BlockSpec((TILE, cols), lambda i, *_: (i, 0))
    return pl.pallas_call(
        functools.partial(attend_kernel, heads),
        out_shape=(
            jax.ShapeDtypeStruct((length, cols), BF16),
            jax.ShapeDtypeStruct((steps, heads, TILE), F32),
        ),
        grid_spec=pltpu.PrefetchScalarGridSpec(
            num_scalar_prefetch=1,
            grid=(steps,),
            in_specs=[
                pl.BlockSpec((1, TILE), lambda i, *_: (0, i)),
                row,
                pl.BlockSpec((length, cols), lambda i, *_: (0, 0)),
                pl.BlockSpec((cols, length), lambda i, *_: (0, 0)),
            ],
            out_specs=(
                row,
                pl.BlockSpec((1, heads, TILE), lambda i, *_: (i, 0, 0)),
            ),
            scratch_shapes=[
                pltpu.VMEM((heads, TILE), F32),
                pltpu.VMEM((heads, TILE), F32),
                pltpu.VMEM((cols, TILE), F32),
            ],
        ),
        compiler_params=pltpu.CompilerParams(vmem_limit_bytes=VMEM_LIMIT),
        cost_estimate=pl.CostEstimate(
            flops=4 * length * 1024 * cols,
            bytes_accessed=8 * length * cols,
            transcendentals=length * 1024 * heads,
        ),
        name="attend",
    )(first, start, q, k, vt)


def attend_back_kernel(
    heads, first_ref, start_ref, q_ref, k_ref, kt_ref, v_ref, o_ref, lse_ref, do_ref,
    cq_ref, sq_ref, ck_ref, sk_ref, grad_ref, dqt, dk_sum, dv_sum,
):
    i = pl.program_id(0)
    steps = pl.num_programs(0)
    width = q_ref.shape[1]
    queries = head_rows(q_ref[...], heads)
    grads = head_rows(do_ref[...], heads)
    start_row = start_ref[...]
    product = (do_ref[...].astype(F32) * o_ref[...].astype(F32)).T
    inner = [
        jnp.sum(product[h * HEAD_DIM : (h + 1) * HEAD_DIM], axis=0, keepdims=True)
        for h in range(heads)
    ]

    def block(j, first):
        at = pl.ds(pl.multiple_of(j * TILE, TILE), TILE)
        keys = k_ref[at, :]
        values = v_ref[at, :]
        mask = pair_mask(start_row, i, j)
        key_term = None
        value_term = None
        for h in range(heads):
            here = slice(h * HEAD_DIM, (h + 1) * HEAD_DIM)
            scores = nt(keys, queries[h])
            weights = jnp.where(mask, jnp.exp(scores - lse_ref[0, h : h + 1]), 0.0)
            grad_weights = nt(values, grads[h])
            grad_scores = (weights * (grad_weights - inner[h])).astype(BF16)
            term = nn(weights.astype(BF16), grads[h])
            value_term = term if value_term is None else value_term + term
            term = nn(grad_scores, queries[h])
            key_term = term if key_term is None else key_term + term
            term = nn(kt_ref[here, at], grad_scores)
            if first:
                dqt[here] = term
            else:
                dqt[here] = dqt[here] + term
        if first:
            dk_sum[at] = key_term
            dv_sum[at] = value_term
        else:
            dk_sum[at] = dk_sum[at] + key_term
            dv_sum[at] = dv_sum[at] + value_term

    block(i, True)

    @pl.loop(0, i - first_ref[i])
    def _(t):
        block(i - 1 - t, False)

    def unturn(grad, cosine, sine):
        grad = grad.astype(BF16).astype(F32)
        cosine = spread_lanes(cosine, width)
        sine = spread_lanes(sine, width)
        return (grad * cosine - swap_halves(grad) * sine).astype(BF16)

    rows = pl.ds(pl.multiple_of(i * TILE, TILE), TILE)
    grad_ref[rows, 0:width] = unturn(
        dqt[...].T * (HEAD_DIM**-0.5), cq_ref[rows, :], sq_ref[rows, :]
    )

    @pl.when(i == steps - 1)
    def _():
        @pl.loop(0, steps)
        def _(j):
            at = pl.ds(pl.multiple_of(j * TILE, TILE), TILE)
            grad_ref[at, width : 2 * width] = unturn(
                dk_sum[at], ck_ref[at, :], sk_ref[at, :]
            )
            grad_ref[at, 2 * width :] = dv_sum[at].astype(BF16)


def attend_back(first, start, q, k, kt, v, o, lse, do, tables):
    length, cols = q.shape
    heads = cols // HEAD_DIM
    steps = length // TILE
    row = pl.BlockSpec((TILE, cols), lambda i, *_: (i, 0))
    whole = pl.BlockSpec((length, cols), lambda i, *_: (0, 0))
    table = pl.BlockSpec((length, tables[0].shape[1]), lambda i, *_: (0, 0))
    return pl.pallas_call(
        functools.partial(attend_back_kernel, heads),
        out_shape=jax.ShapeDtypeStruct((length, 3 * cols), BF16),
        grid_spec=pltpu.PrefetchScalarGridSpec(
            num_scalar_prefetch=1,
            grid=(steps,),
            in_specs=[
                pl.BlockSpec((1, TILE), lambda i, *_: (0, i)),
                row,
                whole,
                pl.BlockSpec((cols, length), lambda i, *_: (0, 0)),
                whole,
                row,
                pl.BlockSpec((1, heads, TILE), lambda i, *_: (i, 0, 0)),
                row,
            ]
            + [table] * 4,
            out_specs=pl.BlockSpec((length, 3 * cols), lambda i, *_: (0, 0)),
            scratch_shapes=[
                pltpu.VMEM((cols, TILE), F32),
                pltpu.VMEM((length, cols), F32),
                pltpu.VMEM((length, cols), F32),
            ],
        ),
        compiler_params=pltpu.CompilerParams(vmem_limit_bytes=VMEM_LIMIT),
        cost_estimate=pl.CostEstimate(
            flops=10 * length * 1024 * cols,
            bytes_accessed=16 * length * cols,
            transcendentals=length * 1024 * heads,
        ),
        name="attend_back",
    )(first, start, q, k, kt, v, o, lse, do, *tables)


def upper_kernel(
    x_ref, wu_ref, c_ref, wd_ref, gain_ref, act_ref, slope_ref, grad_ref, stat_ref
):
    upper = nt(x_ref[...], wu_ref[...])
    grad = nn(c_ref[...], wd_ref[...])
    below = 0.5 * (1.0 + lax.erf(upper * (0.5**0.5)))
    act = upper * below
    slope = below + upper * (jnp.exp(-0.5 * upper * upper) * ((2.0 * math.pi) ** -0.5))
    act_ref[...] = act
    slope_ref[...] = slope.astype(BF16)
    grad_ref[...] = grad
    part = grad * gain_ref[...]
    average = jnp.mean(act, axis=-1, keepdims=True)
    centered = act - average
    spread = jnp.sum(centered * centered, axis=-1, keepdims=True)
    part_sum = jnp.sum(part, axis=-1, keepdims=True)
    cross = jnp.sum(part * centered, axis=-1, keepdims=True)
    lane = lax.broadcasted_iota(jnp.int32, (x_ref.shape[0], 128), 1)
    columns = jnp.where(
        lane == 0,
        average,
        jnp.where(lane == 1, spread, jnp.where(lane == 2, part_sum, cross)),
    )
    stat_ref[...] = columns.T[:8]


def upper_pass(x, w_up, cot, w_down, gain):
    length, width = x.shape
    feats = w_up.shape[0]
    rows = TILE
    row = pl.BlockSpec((rows, width), lambda i: (i, 0))
    out = pl.BlockSpec((rows, feats), lambda i: (i, 0))
    return pl.pallas_call(
        upper_kernel,
        grid=(length // rows,),
        out_shape=(
            jax.ShapeDtypeStruct((length, feats), F32),
            jax.ShapeDtypeStruct((length, feats), BF16),
            jax.ShapeDtypeStruct((length, feats), F32),
            jax.ShapeDtypeStruct((8, length), F32),
        ),
        in_specs=[
            row,
            pl.BlockSpec((feats, width), lambda i: (0, 0)),
            row,
            pl.BlockSpec((width, feats), lambda i: (0, 0)),
            pl.BlockSpec((1, feats), lambda i: (0, 0)),
        ],
        out_specs=(out, out, out, pl.BlockSpec((8, rows), lambda i: (0, i))),
        compiler_params=pltpu.CompilerParams(vmem_limit_bytes=VMEM_LIMIT),
        cost_estimate=pl.CostEstimate(
            flops=4 * length * width * feats,
            bytes_accessed=8 * length * width + 8 * length * feats,
            transcendentals=2 * length * feats,
        ),
        name="upper_pass",
    )(x, w_up, cot, w_down, gain)


def hidden_kernel(act_ref, slope_ref, grad_ref, stat_ref, gain_ref, hid_ref, gu_ref, gg_ref):
    i = pl.program_id(0)
    stats = stat_ref[...].T
    average = stats[:, 0:1]
    scale = stats[:, 1:2]
    part_mean = stats[:, 2:3]
    cross_mean = stats[:, 3:4]
    gain = gain_ref[...]
    normal = (act_ref[...] - average) * scale
    grad = grad_ref[...]
    hid_ref[...] = (normal * gain).astype(BF16)
    back = scale * (grad * gain - part_mean - normal * cross_mean)
    gu_ref[...] = (slope_ref[...].astype(F32) * back).astype(BF16)
    term = jnp.sum(grad * normal, axis=0, keepdims=True)

    @pl.when(i == 0)
    def _():
        gg_ref[...] = term

    @pl.when(i > 0)
    def _():
        gg_ref[...] = gg_ref[...] + term


def hidden_pass(act, slope, grad, stats, gain):
    length, feats = act.shape
    out = pl.BlockSpec((TILE, feats), lambda i: (i, 0))
    one = pl.BlockSpec((1, feats), lambda i: (0, 0))
    return pl.pallas_call(
        hidden_kernel,
        grid=(length // TILE,),
        out_shape=(
            jax.ShapeDtypeStruct((length, feats), BF16),
            jax.ShapeDtypeStruct((length, feats), BF16),
            jax.ShapeDtypeStruct((1, feats), F32),
        ),
        in_specs=[out, out, out, pl.BlockSpec((8, TILE), lambda i: (0, i)), one],
        out_specs=(out, out, one),
        compiler_params=pltpu.CompilerParams(vmem_limit_bytes=VMEM_LIMIT),
        cost_estimate=pl.CostEstimate(
            flops=12 * length * feats,
            bytes_accessed=14 * length * feats,
            transcendentals=0,
        ),
        name="hidden_pass",
    )(act, slope, grad, stats, gain)


def stat_kernel(n, feats, x_ref, o_ref, held, send_sem, recv_sem):
    me = lax.axis_index("seq")
    held[me] = x_ref[...]
    meet([lax.rem(me + k, n) for k in range(1, n)])
    copies = [
        remote(x_ref, held.at[me], send_sem.at[k], recv_sem.at[k], lax.rem(me + k, n))
        for k in range(1, n)
    ]
    for copy in copies:
        copy.start()
    for copy in copies:
        copy.wait()
    average = held[0, 0:1]
    for d in range(1, n):
        average = average + held[d, 0:1]
    average = average * (1.0 / n)
    spread = jnp.zeros_like(average)
    part = jnp.zeros_like(average)
    cross = jnp.zeros_like(average)
    for d in range(n):
        shift = held[d, 0:1] - average
        spread = spread + held[d, 1:2] + feats * (shift * shift)
        part = part + held[d, 2:3]
        cross = cross + held[d, 3:4] + shift * held[d, 2:3]
    whole = 1.0 / (n * feats)
    scale = lax.rsqrt(spread * whole + EPSILON)
    o_ref[0:1] = average
    o_ref[1:2] = scale
    o_ref[2:3] = part * whole
    o_ref[3:4] = cross * scale * whole
    o_ref[4:8] = jnp.zeros((4, average.shape[1]), F32)


def join_stats(stat, feats, collective_id):
    n = lax.axis_size("seq")
    inside = pl.BlockSpec(memory_space=pltpu.VMEM)
    return pl.pallas_call(
        functools.partial(stat_kernel, n, feats),
        out_shape=jax.ShapeDtypeStruct(stat.shape, F32),
        in_specs=[inside],
        out_specs=inside,
        scratch_shapes=[
            pltpu.VMEM((n, *stat.shape), F32),
            pltpu.SemaphoreType.DMA((n,)),
            pltpu.SemaphoreType.DMA((n,)),
        ],
        compiler_params=pltpu.CompilerParams(
            collective_id=collective_id, has_side_effects=True, vmem_limit_bytes=VMEM_LIMIT
        ),
        name="join_stats",
    )(stat)


STEP = 32


def mix_kernel(att_ref, x_ref, w_ref, gm_ref, gf_ref, mix_ref, mid_ref, ffn_ref):
    j = pl.program_id(0)
    rows = att_ref.shape[0]
    cols = w_ref.shape[0]

    @pl.when(j == 0)
    def _():
        @pl.loop(0, rows // STEP)
        def _(r):
            at = pl.ds(pl.multiple_of(r * STEP, STEP), STEP)
            normal, _ = norm_parts(att_ref[at].astype(F32))
            mix_ref[at] = (normal * gm_ref[...]).astype(BF16)

    here = pl.ds(pl.multiple_of(j * cols, cols), cols)
    mid_ref[:, here] = x_ref[:, here].astype(F32) + nt(mix_ref[...], w_ref[...])

    @pl.when(j == pl.num_programs(0) - 1)
    def _():
        @pl.loop(0, rows // STEP)
        def _(r):
            at = pl.ds(pl.multiple_of(r * STEP, STEP), STEP)
            normal, _ = norm_parts(mid_ref[at])
            ffn_ref[at] = (normal * gf_ref[...]).astype(BF16)


def mix_pass(attended, x, w_out, gain_mix, gain_ffn):
    rows, width = x.shape
    cols = TILE
    n = width // cols
    whole = pl.BlockSpec((rows, width), lambda j: (0, 0))
    gain = pl.BlockSpec((1, width), lambda j: (0, 0))
    low = jax.ShapeDtypeStruct((rows, width), BF16)
    return pl.pallas_call(
        mix_kernel,
        grid=(n,),
        out_shape=(low, jax.ShapeDtypeStruct((rows, width), F32), low),
        in_specs=[
            whole,
            whole,
            pl.BlockSpec((cols, width), lambda j: (j, 0)),
            gain,
            gain,
        ],
        out_specs=(whole, whole, whole),
        compiler_params=pltpu.CompilerParams(vmem_limit_bytes=VMEM_LIMIT),
        cost_estimate=pl.CostEstimate(
            flops=2 * rows * width * width,
            bytes_accessed=2 * width * width + 12 * rows * width,
            transcendentals=0,
        ),
        name="mix_pass",
    )(attended, x, w_out, gain_mix[None], gain_ffn[None])


def branch_kernel(
    g_ref, mid_ref, cot_ref, att_ref, w_ref, gm_ref, gf_ref,
    gmid_ref, gbr_ref, gatt_ref, ggf_ref, ggm_ref, total,
):
    j = pl.program_id(0)
    rows = att_ref.shape[0]
    cols = w_ref.shape[0]

    @pl.when(j == 0)
    def _():
        ggf_ref[...] = jnp.zeros_like(ggf_ref)
        total[...] = jnp.zeros_like(total)

        @pl.loop(0, rows // STEP)
        def _(r):
            at = pl.ds(pl.multiple_of(r * STEP, STEP), STEP)
            normal, scale = norm_parts(mid_ref[at])
            part, gain_part = norm_back(g_ref[at], normal, scale, gf_ref[...])
            ggf_ref[...] += gain_part[None]
            grad = cot_ref[at].astype(F32) + part
            gmid_ref[at] = grad
            gbr_ref[at] = grad.astype(BF16)

    here = pl.ds(pl.multiple_of(j * cols, cols), cols)
    total[...] += nn(gbr_ref[:, here], w_ref[...])

    @pl.when(j == pl.num_programs(0) - 1)
    def _():
        ggm_ref[...] = jnp.zeros_like(ggm_ref)

        @pl.loop(0, rows // STEP)
        def _(r):
            at = pl.ds(pl.multiple_of(r * STEP, STEP), STEP)
            normal, scale = norm_parts(att_ref[at].astype(F32))
            part, gain_part = norm_back(total[at], normal, scale, gm_ref[...])
            ggm_ref[...] += gain_part[None]
            gatt_ref[at] = part.astype(BF16)


def branch_pass(grad_ffn_in, middle, cot, attended, w_out, gain_mix, gain_ffn):
    rows, width = cot.shape
    cols = TILE
    n = width // cols
    whole = pl.BlockSpec((rows, width), lambda j: (0, 0))
    gain = pl.BlockSpec((1, width), lambda j: (0, 0))
    low = jax.ShapeDtypeStruct((rows, width), BF16)
    sums = jax.ShapeDtypeStruct((1, width), F32)
    return pl.pallas_call(
        branch_kernel,
        grid=(n,),
        out_shape=(jax.ShapeDtypeStruct((rows, width), F32), low, low, sums, sums),
        in_specs=[
            whole,
            whole,
            whole,
            whole,
            pl.BlockSpec((cols, width), lambda j: (j, 0)),
            gain,
            gain,
        ],
        out_specs=(whole, whole, whole, gain, gain),
        scratch_shapes=[pltpu.VMEM((rows, width), F32)],
        compiler_params=pltpu.CompilerParams(vmem_limit_bytes=VMEM_LIMIT),
        cost_estimate=pl.CostEstimate(
            flops=2 * rows * width * width,
            bytes_accessed=2 * width * width + 20 * rows * width,
            transcendentals=0,
        ),
        name="branch_pass",
    )(grad_ffn_in, middle, cot, attended, w_out, gain_mix[None], gain_ffn[None])


CHUNK = 128


def finish_kernel(
    n, depth, gq_ref, gd_ref, pw_ref, pn_ref, po_ref, x_ref, grad_ref, mid_ref, ga_ref, gm_ref, gf_ref, gh_ref,
    oq_ref, od_ref, ow_ref, gi_ref, out_ref, sums_ref,
    own, twin_in, held, zown, zin, stage, gain_here, gain_row, gain_pack, gain_line,
    local_sem, load_sem, stage_sem, send_sem, recv_sem, keep_sem,
    up_send, up_recv, down_send, down_recv, home_send, home_recv, gain_send, gain_recv,
):
    me, twin, near_x, near_y, across = places()
    z = lax.axis_index("batch")
    rows, width = pn_ref.shape[1:]
    half = rows // 2
    low, high = pl.ds(0, half), pl.ds(half, half)
    mine = (across, near_x, near_y, me)
    _, chunk, cols = zown.shape
    across_width = width // cols
    per_part = (gq_ref.shape[1] // chunk) * across_width
    turned = gq_ref.shape[0] * per_part
    per_source = gd_ref.shape[1] // chunk
    outer = turned + gd_ref.shape[0] * per_source
    chunks = zown.shape[0]
    per_side = chunks // 2

    def cut(i, size):
        return pl.ds(pl.multiple_of(i * size, size), size)

    def wide(i):
        return cut(i // across_width, chunk), cut(lax.rem(i, across_width), cols)

    line_loads = []
    for g in range(turned):
        source = gq_ref.at[(g // per_part, *wide(g % per_part))]
        line_loads.append(pltpu.make_async_copy(source, zown.at[g], load_sem.at[g]))
    for g in range(turned, outer):
        source = gd_ref.at[
            (g - turned) // per_source, cut((g - turned) % per_source, chunk)
        ]
        line_loads.append(pltpu.make_async_copy(source, zown.at[g], load_sem.at[g]))
    for load in line_loads:
        load.start()
    partials = (pw_ref, pn_ref, po_ref)
    loads = [
        [
            pltpu.make_async_copy(p.at[block], own.at[m, i], local_sem.at[4 * m + i])
            for i, block in enumerate(mine)
        ]
        for m, p in enumerate(partials)
    ]
    for part in loads:
        for load in part:
            load.start()
    meet_all(n, depth)

    def copy(m, k, src, dst, partner):
        return remote(src, dst, send_sem.at[m, k], recv_sem.at[m, k], partner)

    twins = [
        [
            copy(m, i, p.at[block + twin], twin_in.at[m, i], me + twin)
            for i, block in enumerate(mine)
        ]
        for m, p in enumerate(partials)
    ]
    sends = [
        [
            copy(m, 4, own.at[m, 0, low], held.at[m, 0], near_x),
            copy(m, 5, own.at[m, 0, high], held.at[m, 1], near_y),
            copy(m, 6, own.at[m, 1, low], held.at[m, 2], near_x),
            copy(m, 7, own.at[m, 2, high], held.at[m, 3], near_y),
            copy(m, 8, own.at[m, 1, high], held.at[m, 4], near_x),
            copy(m, 9, own.at[m, 2, low], held.at[m, 5], near_y),
        ]
        for m in range(3)
    ]
    for part in twins:
        for send in part:
            send.start()

    def add_twin(m, i):
        loads[m][i].wait()
        twins[m][i].wait_recv()

        @pl.loop(0, rows // STEP)
        def _(r):
            at = cut(r, STEP)
            own[m, i, at] = (
                own[m, i, at].astype(F32) + twin_in[m, i, at].astype(F32)
            ).astype(BF16)

    def add_held(m, i, base, slot):
        @pl.loop(0, half // STEP)
        def _(r):
            at = cut(r, STEP)
            to = pl.ds(pl.multiple_of(base + r * STEP, STEP), STEP)
            own[m, i, to] = (
                own[m, i, to].astype(F32) + held[m, slot, at].astype(F32)
            ).astype(BF16)

    def first(m):
        add_twin(m, 0)
        sends[m][0].start()
        sends[m][1].start()
        add_twin(m, 1)
        sends[m][2].start()
        add_twin(m, 2)
        sends[m][3].start()

    def second(m):
        sends[m][1].wait_recv()
        add_held(m, 1, half, 1)
        sends[m][4].start()
        sends[m][0].wait_recv()
        add_held(m, 2, 0, 0)
        sends[m][5].start()

    def last(m, store):
        loads[m][3].wait()
        twins[m][3].wait_recv()
        for k in (2, 3, 4, 5):
            sends[m][k].wait_recv()
        for base, one, two in ((0, 2, 5), (half, 3, 4)):

            @pl.loop(0, half // STEP)
            def _(r):
                at = cut(r, STEP)
                place = base + r * STEP
                to = pl.ds(pl.multiple_of(place, STEP), STEP)
                store(
                    place,
                    to,
                    own[m, 3, to].astype(F32)
                    + twin_in[m, 3, to].astype(F32)
                    + held[m, one, at].astype(F32)
                    + held[m, two, at].astype(F32),
                )

    def store_line(place, to, value):
        value = value.astype(BF16)
        for side in range(across_width):
            zown[
                outer + (place // chunk) * across_width + side,
                pl.ds(pl.multiple_of(lax.rem(place, chunk), STEP), STEP),
            ] = value[:, side * cols : (side + 1) * cols]

    def store_inputs(place, to, value):
        normal, scale = norm_parts(x_ref[to].astype(F32))
        part, gain_part = norm_back(value, normal, scale, ga_ref[...])
        gi_ref[to] = grad_ref[to] + part
        gain_here[0:1] = gain_here[0:1] + gain_part[None]

    def store_outputs(place, to, value):
        out_ref[to] = (mid_ref[to] + value).astype(BF16)

    def home(part):
        block = part * n + me
        return block // 3, lax.rem(block, 3)

    def deliver_far(g):
        target, slot = home(g // per_part)
        piece = lax.rem(g, per_part)
        return remote(
            zin.at[g],
            oq_ref.at[(slot, *wide(piece))],
            home_send.at[g],
            home_recv.at[slot, piece],
            target,
        )

    def deliver_near(g):
        _, slot = home(g // per_part)
        return pltpu.make_async_copy(
            zin.at[g], oq_ref.at[(slot, *wide(lax.rem(g, per_part)))], keep_sem.at[g]
        )

    def widen(g):
        @pl.loop(0, chunk // STEP)
        def _(r):
            at = cut(r, STEP)
            stage[at] = zin[g, at].astype(F32)

    def deliver(g):
        target, _ = home(g // per_part)

        @pl.when((g < turned) & (target != me))
        def _():
            deliver_far(g).start()

        @pl.when((g < turned) & (target == me))
        def _():
            deliver_near(g).start()

        @pl.when((g >= turned) & (g < outer))
        def _():
            widen(g)
            at = g - turned
            place = cut(lax.rem(at, per_source), chunk), cut(at // per_source, cols)
            store = pltpu.make_async_copy(stage, od_ref.at[place], stage_sem)
            store.start()
            store.wait()

        @pl.when(g >= outer)
        def _():
            widen(g)
            store = pltpu.make_async_copy(
                stage, ow_ref.at[wide(g - outer)], stage_sem
            )
            store.start()
            store.wait()

    def delivered(g):
        target, _ = home(g // per_part)

        @pl.when(target != me)
        def _():
            deliver_far(g).wait_send()

        @pl.when(target == me)
        def _():
            deliver_near(g).wait()

    def go_up(g, ahead):
        return line_remote(zown.at[g], zin.at[g], up_send.at[g], up_recv.at[g], ahead)

    def go_down(g, behind):
        return line_remote(
            zin.at[g], zin.at[g], down_send.at[g], down_recv.at[g], behind
        )

    def ranks(side):
        if side == 0:
            return z, z + 1, z - 1
        return depth - 1 - z, z - 1, z + 1

    def add_line(g, target):
        @pl.loop(0, chunk // STEP)
        def _(r):
            at = cut(r, STEP)
            target[g, at] = (zown[g, at].astype(F32) + zin[g, at].astype(F32)).astype(
                BF16
            )

    lead = 4

    def line_enter(c):
        for side in (0, 1):
            rank, ahead, _ = ranks(side)

            @pl.when(rank == 0)
            def _():
                go_up(2 * c + side, ahead).start()

    def line_step(t):
        if t + lead < per_side:
            line_enter(t + lead)
        for side in (0, 1):
            rank, ahead, behind = ranks(side)
            c = t - rank
            g = 2 * c + side
            there = (c >= 0) & (c < per_side)

            @pl.when(there & (rank > 0) & (rank < depth - 1))
            def _():
                go_up(g, behind).wait_recv()
                add_line(g, zown)
                go_up(g, ahead).start()

            @pl.when(there & (rank == depth - 1))
            def _():
                go_up(g, behind).wait_recv()
                add_line(g, zin)
                go_down(g, behind).start()
                deliver(g)

            c_back = t - 2 * (depth - 1) + rank
            g_back = 2 * c_back + side
            there = (c_back >= 0) & (c_back < per_side) & (rank < depth - 1)

            @pl.when(there)
            def _():
                go_down(g_back, ahead).wait_recv()

            @pl.when(there & (rank > 0))
            def _():
                go_down(g_back, behind).start()

            @pl.when(there)
            def _():
                deliver(g_back)

    gain_here[...] = jnp.zeros_like(gain_here)
    for load in line_loads:
        load.wait()
    for c in range(lead):
        line_enter(c)
    first(0)
    line_step(0)
    line_step(1)
    first(1)
    line_step(2)
    line_step(3)
    second(0)
    line_step(4)
    first(2)
    line_step(5)
    line_step(6)
    last(0, store_line)
    line_step(7)
    second(1)
    line_step(8)
    line_step(9)
    last(1, store_inputs)

    gain_here[1:2] = gm_ref[...]
    gain_here[2:3] = gf_ref[...]
    gain_here[3:4, 0 : gh_ref.shape[1]] = gh_ref[...]
    gain_row[me] = gain_here[...]
    rounds = [
        remote(
            gain_here,
            gain_row.at[me],
            gain_send.at[0, k],
            gain_recv.at[0, k],
            lax.rem(me + k, n),
        )
        for k in range(1, n)
    ]
    for send in rounds:
        send.start()
    line_step(10)
    second(2)
    line_step(11)
    line_step(12)
    last(2, store_outputs)
    for t in (13, 14, 15):
        line_step(t)
    for send in rounds:
        send.wait()
    total = gain_row[0]
    for d in range(1, n):
        total = total + gain_row[d]
    gain_pack[0:8] = total
    for d in range(n):
        gain_pack[8 + d : 9 + d] = gain_row[d, 3:4]
    gain_line[z] = gain_pack[...]
    rounds = [
        line_remote(
            gain_pack,
            gain_line.at[z],
            gain_send.at[1, k],
            gain_recv.at[1, k],
            lax.rem(z + k, depth),
        )
        for k in range(1, depth)
    ]
    for send in rounds:
        send.start()
    for t in range(16, per_side + 2 * (depth - 1)):
        line_step(t)
    for send in rounds:
        send.wait()
    total = gain_line[0]
    for d in range(1, depth):
        total = total + gain_line[d]
    sums_ref[...] = total

    for m in range(3):
        for send in twins[m] + sends[m]:
            send.wait_send()
    for g in range(chunks):
        rank, ahead, behind = ranks(g % 2)

        @pl.when(rank < depth - 1)
        def _():
            go_up(g, ahead).wait_send()

        @pl.when(rank > 0)
        def _():
            go_down(g, behind).wait_send()

    for g in range(turned):
        delivered(g)
    for slot in range(3):
        block = 3 * me + slot
        source = lax.rem(block, n)

        @pl.when(source != me)
        def _():
            for piece in range(per_part):
                remote(
                    zin.at[0],
                    oq_ref.at[(slot, *wide(piece))],
                    home_send.at[0],
                    home_recv.at[slot, piece],
                    source,
                ).wait_recv()


def finish(
    grad_qkv, grad_down, part_out, part_normed, part_outputs, x, grad_middle, middle, gain, gains, collective_id
):
    n, depth = lax.axis_size("seq"), lax.axis_size("batch")
    rows, width = part_out.shape[0] // n, part_out.shape[1]
    cols = grad_qkv.shape[1]
    sources, _, feats = grad_down.shape
    if n != 8 or depth != 4:
        me = lax.axis_index("seq")
        blocks = lax.psum(grad_qkv, "batch")
        back = [
            lax.ppermute(
                give_part(blocks, me, n, j),
                "seq",
                [((3 * d + j) % n, d) for d in range(n)],
            )
            for j in range(3)
        ]
        w_out = lax.psum(scatter_seq(part_out, None).astype(BF16), "batch")
        normal, scale = norm_parts(x.astype(F32))
        part, gain_part = norm_back(scatter_seq(part_normed, None), normal, scale, gain)
        shared = [lax.psum(g, ("batch", "seq")) for g in (gain_part, gains[0][0], gains[1][0])]
        hidden = lax.all_gather(lax.psum(gains[2][0], "batch"), "seq", axis=0, tiled=True)
        down = lax.psum(grad_down, "batch")
        return (
            jnp.concatenate(back, axis=0),
            jnp.swapaxes(down, 0, 1).reshape(rows, sources * feats).astype(F32),
            w_out.astype(F32),
            grad_middle + part,
            (middle + scatter_seq(part_outputs, None)).astype(BF16),
            (*shared, hidden),
        )
    chunks = (
        3 * cols * width + rows * width + sources * rows * feats
    ) // (CHUNK * feats)
    dma = pltpu.SemaphoreType.DMA
    line = pltpu.VMEM((chunks, CHUNK, feats), BF16)
    w_qkv, w_down, w_out, grad_inputs, outputs, sums = pl.pallas_call(
        functools.partial(finish_kernel, n, depth),
        out_shape=(
            jax.ShapeDtypeStruct((3, cols, width), BF16),
            jax.ShapeDtypeStruct((rows, sources * feats), F32),
            jax.ShapeDtypeStruct((rows, width), F32),
            jax.ShapeDtypeStruct((rows, width), F32),
            jax.ShapeDtypeStruct((rows, width), BF16),
            jax.ShapeDtypeStruct((16, width), F32),
        ),
        in_specs=[ANY] * 5 + [INSIDE] * 7,
        out_specs=(ANY, ANY, ANY, INSIDE, INSIDE, INSIDE),
        scratch_shapes=[
            pltpu.VMEM((3, 4, rows, width), BF16),
            pltpu.VMEM((3, 4, rows, width), BF16),
            pltpu.VMEM((3, 6, rows // 2, width), BF16),
            line,
            line,
            pltpu.VMEM((CHUNK, feats), F32),
            pltpu.VMEM((8, width), F32),
            pltpu.VMEM((n, 8, width), F32),
            pltpu.VMEM((16, width), F32),
            pltpu.VMEM((depth, 16, width), F32),
            dma((12,)),
            dma((chunks,)),
            dma,
            dma((3, 10)),
            dma((3, 10)),
            dma((chunks,)),
            dma((chunks,)),
            dma((chunks,)),
            dma((chunks,)),
            dma((chunks,)),
            dma((chunks,)),
            dma((3, cols * width // (CHUNK * feats))),
            dma((2, n)),
            dma((2, n)),
        ],
        compiler_params=pltpu.CompilerParams(
            collective_id=collective_id,
            has_side_effects=True,
            vmem_limit_bytes=VMEM_LIMIT,
        ),
        name="finish",
    )(
        grad_qkv,
        grad_down,
        *[p.reshape(n, rows, width) for p in (part_out, part_normed, part_outputs)],
        x,
        grad_middle,
        middle,
        gain[None],
        *gains,
    )
    return (
        w_qkv.reshape(3 * cols, width),
        w_down,
        w_out,
        grad_inputs,
        outputs,
        (sums[0], sums[1], sums[2], sums[8:, :feats].reshape(-1)),
    )


def body(
    inputs,
    segment_ids,
    w_qkv,
    w_out,
    w_up,
    w_down,
    gain_attn,
    gain_mix,
    gain_ffn,
    gain_hidden,
    cotangent,
):
    _, local, width = inputs.shape
    n, depth = lax.axis_size("seq"), lax.axis_size("batch")
    me = lax.axis_index("seq")
    length = local * n
    feats = w_up.shape[0]
    x_low = inputs[0]
    x = x_low.astype(F32)
    cot = cotangent[0]
    segment = segment_ids[0]

    w_out_full = lax.all_gather(w_out, "seq", axis=0, tiled=True)
    normed = (norm_parts(x)[0] * gain_attn).astype(BF16)
    before = [jnp.sum((segment < d).astype(jnp.int32)) for d in range(1, DOCS)]
    start = jnp.zeros_like(segment)
    for d in range(1, DOCS):
        start = jnp.where(segment == d, before[d - 1], start)
    positions = jnp.arange(length, dtype=jnp.int32) - start
    first = start[::TILE] // TILE
    start_row = start[None, :]

    normed_full, w_heads, w_down_near, tables = start_exchange(
        normed, w_qkv, w_down, positions.astype(F32), 1
    )
    cot_late, _ = lax.optimization_barrier((cot, w_heads))
    cot_full = lax.all_gather(cot_late, "seq", axis=0, tiled=True)

    q, k, v, kt, vt = project_qkv(normed_full, w_heads, tables)
    attended_heads, lse = attend(first, start_row, q, k, vt)
    attended = heads_to_tokens(attended_heads, 2)
    mix_in, middle, ffn_in = mix_pass(attended, x_low, w_out_full, gain_mix, gain_ffn)
    ffn_full, w_down_cols = gather_seq(ffn_in, w_down_near, 3)

    gain_here = lax.dynamic_slice_in_dim(gain_hidden, me * feats, feats, 0)[None, :]
    act, slope, grad_hidden, stat = upper_pass(
        ffn_full, w_up, cot_full, w_down_cols, gain_here
    )
    stats = join_stats(stat, feats, 8)
    hidden, grad_upper, grad_gain_here = hidden_pass(act, slope, grad_hidden, stats, gain_here)

    grad_w_up = tn(grad_upper, ffn_full).astype(BF16)
    grad_upper, grad_w_up = lax.optimization_barrier((grad_upper, grad_w_up))
    grad_w_up = lax.psum(grad_w_up, "batch")
    grad_w_down = tn(cot_full, hidden).astype(BF16).reshape(n, local, feats)
    grad_upper, grad_w_down = lax.optimization_barrier((grad_upper, grad_w_down))
    grad_ffn_in = scatter_seq(nn(grad_upper, w_up).astype(BF16), 4)
    grad_middle, grad_branch, grad_att, grad_gain_ffn, grad_gain_mix = branch_pass(
        grad_ffn_in, middle, cot, attended, w_out_full, gain_mix, gain_ffn
    )
    grad_heads = tokens_to_heads(grad_att, 5)
    grad_w_down, grad_heads = lax.optimization_barrier((grad_w_down, grad_heads))
    grad_w_down = lax.all_to_all(grad_w_down, "seq", split_axis=0, concat_axis=0, tiled=True)
    grads = attend_back(
        first, start_row, q, k, kt, v, attended_heads, lse, grad_heads, tables
    )
    grad_w_qkv, grad_w_down, grad_w_out, grad_inputs, outputs, gains = finish(
        tn(grads, normed_full).astype(BF16).reshape(3, -1, width),
        grad_w_down,
        tn(grad_branch, mix_in).astype(BF16),
        nn(grads, w_heads).astype(BF16),
        nt(hidden, w_down_cols).astype(BF16),
        x_low,
        grad_middle,
        middle,
        gain_attn,
        (grad_gain_mix, grad_gain_ffn, grad_gain_here),
        6,
    )
    return (
        outputs[None],
        grad_inputs[None],
        grad_w_qkv.astype(F32),
        grad_w_out,
        grad_w_up.astype(F32),
        grad_w_down,
        *gains,
    )


def pick_part(turned, me, n, part):
    chosen = turned[0]
    home = part * n + me
    for j in (1, 2):
        chosen = jnp.where(lax.rem(home, 3) == j, turned[j], chosen)
    return chosen


def give_part(blocks, me, n, j):
    chosen = blocks[0]
    for part in (1, 2):
        chosen = jnp.where(lax.rem(part * n + me, 3) == j, blocks[part], chosen)
    return chosen


def solution(mesh):
    in_specs = (
        P("batch", "seq", None),
        P("batch", None),
        P("seq", None),
        P("seq", None),
        P("seq", None),
        P("seq", None),
        P(),
        P(),
        P(),
        P(),
        P("batch", "seq", None),
    )
    out_specs = (
        P("batch", "seq", None),
        P("batch", "seq", None),
        P("seq", None),
        P("seq", None),
        P("seq", None),
        P("seq", None),
        P(),
        P(),
        P(),
        P(),
    )
    return jax.shard_map(body, mesh=mesh, in_specs=in_specs, out_specs=out_specs, check_vma=False)
```

```python
import functools
import math

import jax
import jax.numpy as jnp
from jax import lax
from jax.experimental import pallas as pl
from jax.experimental.pallas import tpu as pltpu
from jax.sharding import PartitionSpec as P

HEADS = 32
HEAD_DIM = 64
LENGTH = 2048
XBASE = 512
DOCS = 4
EPSILON = 1e-05
MASKED = -1e30
TILE = 256
VMEM_LIMIT = 60 * 1024 * 1024

MESH = pl.DeviceIdType.MESH
F32 = jnp.float32
BF16 = jnp.bfloat16
ANY = pl.BlockSpec(memory_space=pl.ANY)
INSIDE = pl.BlockSpec(memory_space=pltpu.VMEM)


def nn(a, b):
    return lax.dot_general(a, b, (((1,), (0,)), ((), ())), preferred_element_type=F32)


def nt(a, b):
    return lax.dot_general(a, b, (((1,), (1,)), ((), ())), preferred_element_type=F32)


def tn(a, b):
    return lax.dot_general(a, b, (((0,), (0,)), ((), ())), preferred_element_type=F32)


def norm_parts(values):
    average = jnp.mean(values, axis=-1, keepdims=True)
    centered = values - average
    spread = jnp.mean(centered * centered, axis=-1, keepdims=True)
    scale = lax.rsqrt(spread + EPSILON)
    return centered * scale, scale


def norm_back(grad, normal, scale, gain):
    part = grad * gain
    inner = (
        part
        - jnp.mean(part, axis=-1, keepdims=True)
        - normal * jnp.mean(part * normal, axis=-1, keepdims=True)
    )
    return scale * inner, jnp.sum(grad * normal, axis=0)


def places():
    me = lax.axis_index("seq")
    core = lax.rem(me, 2)
    along_x = lax.rem(me // 2, 2)
    along_y = me // 4
    twin = 1 - 2 * core
    near_x = me + 2 - 4 * along_x
    near_y = me + 4 - 8 * along_y
    across = near_x + 4 - 8 * along_y
    return me, twin, near_x, near_y, across


def remote(src, dst, send_sem, recv_sem, partner):
    return pltpu.make_async_remote_copy(
        src_ref=src,
        dst_ref=dst,
        send_sem=send_sem,
        recv_sem=recv_sem,
        device_id={"seq": partner},
        device_id_type=MESH,
    )


def meet(partners):
    barrier = pltpu.get_barrier_semaphore()
    for partner in partners:
        pl.semaphore_signal(
            barrier, inc=1, device_id={"seq": partner}, device_id_type=MESH
        )
    pl.semaphore_wait(barrier, len(partners))


def gather_copies(x_ref, o_ref, send_sem, recv_sem):
    me, twin, near_x, near_y, across = places()
    half = x_ref.shape[0] // 2
    low, high = pl.ds(0, half), pl.ds(half, half)

    def copy(k, src, dst, partner):
        return remote(src, dst, send_sem.at[k], recv_sem.at[k], partner)

    def relay(k, owner, rows, partner):
        place = o_ref.at[owner, rows]
        return copy(k, place, place, partner)

    return [
        copy(0, x_ref.at[low], o_ref.at[me, low], near_x),
        copy(1, x_ref.at[high], o_ref.at[me, high], near_y),
        copy(2, x_ref.at[high], o_ref.at[me, high], near_x),
        copy(3, x_ref.at[low], o_ref.at[me, low], near_y),
        copy(4, x_ref, o_ref.at[me], me + twin),
        relay(5, near_x, low, near_y),
        relay(6, near_y, high, near_x),
        relay(7, near_x, low, me + twin),
        relay(8, near_y, high, me + twin),
        relay(9, near_x, high, me + twin),
        relay(10, near_y, low, me + twin),
        relay(11, across, low, me + twin),
        relay(12, across, high, me + twin),
    ]


def gather_run(sends, *between):
    between = (*between, *([None] * 3))[:3]

    def pause(i):
        if between[i] is not None:
            between[i]()

    sends[0].wait_recv()
    sends[5].start()
    sends[7].start()
    sends[1].wait_recv()
    sends[6].start()
    sends[8].start()
    pause(0)
    sends[2].wait_recv()
    sends[9].start()
    sends[3].wait_recv()
    sends[10].start()
    pause(1)
    sends[5].wait_recv()
    sends[11].start()
    sends[6].wait_recv()
    sends[12].start()
    pause(2)
    for k in (4, 7, 8, 9, 10, 11, 12):
        sends[k].wait_recv()
    for send in sends:
        send.wait_send()


def meet_all(n, depth):
    me = lax.axis_index("seq")
    z = lax.axis_index("batch")
    barrier = pltpu.get_barrier_semaphore()
    for k in range(1, n):
        pl.semaphore_signal(
            barrier, inc=1, device_id={"seq": lax.rem(me + k, n)}, device_id_type=MESH
        )
    for k in range(1, depth):
        pl.semaphore_signal(
            barrier,
            inc=1,
            device_id={"batch": lax.rem(z + k, depth)},
            device_id_type=MESH,
        )
    pl.semaphore_wait(barrier, n + depth - 2)


def line_remote(src, dst, send_sem, recv_sem, partner):
    return pltpu.make_async_remote_copy(
        src_ref=src,
        dst_ref=dst,
        send_sem=send_sem,
        recv_sem=recv_sem,
        device_id={"batch": partner},
        device_id_type=MESH,
    )


class Line:
    def __init__(self, depth, source, target, send_sem, recv_sem):
        self.depth, self.source, self.target = depth, source, target
        self.send_sem, self.recv_sem = send_sem, recv_sem
        self.z = lax.axis_index("batch")

    def message(self, side, k):
        sign = 2 * side - 1
        owner = self.z - sign * k
        return line_remote(
            self.source(owner, k),
            self.target(owner),
            self.send_sem.at[side, k],
            self.recv_sem.at[side, k],
            self.z + sign,
        )

    def sends(self, side, k):
        sign = 2 * side - 1
        owner, target = self.z - sign * k, self.z + sign
        inside = (owner >= 0) & (owner < self.depth)
        return inside & (target >= 0) & (target < self.depth)

    def land(self, k):
        for side in (0, 1):
            sign = 2 * side - 1
            owner = self.z - sign * (k + 1)

            @pl.when((owner >= 0) & (owner < self.depth))
            def _():
                place = self.target(owner)
                line_remote(
                    place,
                    place,
                    self.send_sem.at[side, k],
                    self.recv_sem.at[side, k],
                    self.z - sign,
                ).wait_recv()

    def start(self, k):
        for side in (0, 1):

            @pl.when(self.sends(side, k))
            def _():
                self.message(side, k).start()

    def sent(self, k):
        for side in (0, 1):

            @pl.when(self.sends(side, k))
            def _():
                self.message(side, k).wait_send()


def gather_kernel(
    n, depth, x_ref, near_ref, o_ref, all_ref, keep_ref, local_sem, send_sem, recv_sem, line_send, line_recv
):
    me, twin, near_x, near_y, _ = places()
    z = lax.axis_index("batch")
    own = pltpu.make_async_copy(x_ref, o_ref.at[me], local_sem.at[0])
    own.start()

    def load(shift):
        return pltpu.make_async_copy(
            near_ref.at[:, z + shift], keep_ref.at[1 + shift], local_sem.at[2 + shift]
        )

    def keep(shift):
        return pltpu.make_async_copy(
            keep_ref.at[1 + shift], all_ref.at[:, z + shift], local_sem.at[5 + shift]
        )

    def kept(shift):
        return (z + shift >= 0) & (z + shift < depth)

    for shift in (-1, 0, 1):

        @pl.when(kept(shift))
        def _():
            load(shift).start()

    meet_all(n, depth)
    sends = gather_copies(x_ref, o_ref, send_sem, recv_sem)
    for k in range(5):
        sends[k].start()
    line = Line(
        depth,
        lambda owner, k: (near_ref if k == 1 else all_ref).at[:, owner],
        lambda owner: all_ref.at[:, owner],
        line_send,
        line_recv,
    )
    line.start(1)
    for shift in (-1, 0, 1):

        @pl.when(kept(shift))
        def _():
            load(shift).wait()
            keep(shift).start()

    def between():
        for k in range(2, depth - 1):
            line.land(k - 1)
            line.start(k)

    gather_run(sends, None, between)
    line.land(depth - 2)
    for k in range(1, depth - 1):
        line.sent(k)
    for shift in (-1, 0, 1):

        @pl.when(kept(shift))
        def _():
            keep(shift).wait()

    own.wait()


def gather_seq(block, near, collective_id):
    n, depth = lax.axis_size("seq"), lax.axis_size("batch")
    rows, width = block.shape
    if n != 8:
        return lax.all_gather(block, "seq", axis=0, tiled=True), near
    gathered, every = pl.pallas_call(
        functools.partial(gather_kernel, n, depth),
        out_shape=(
            jax.ShapeDtypeStruct((n, rows, width), block.dtype),
            jax.ShapeDtypeStruct(near.shape, near.dtype),
        ),
        in_specs=[INSIDE, ANY],
        out_specs=(ANY, ANY),
        scratch_shapes=[
            pltpu.VMEM((3, n, *near.shape[2:]), near.dtype),
            pltpu.SemaphoreType.DMA((7,)),
            pltpu.SemaphoreType.DMA((13,)),
            pltpu.SemaphoreType.DMA((13,)),
            pltpu.SemaphoreType.DMA((2, depth)),
            pltpu.SemaphoreType.DMA((2, depth)),
        ],
        compiler_params=pltpu.CompilerParams(
            collective_id=collective_id, has_side_effects=True, vmem_limit_bytes=VMEM_LIMIT
        ),
        name="gather_seq",
    )(block, near)
    return gathered.reshape(n * rows, width), every.reshape(-1, near.shape[-1])


def lane_tables(place):
    half = HEAD_DIM // 2
    lane = lax.broadcasted_iota(jnp.int32, (1, 128), 1)
    channel = lax.rem(lane, half).astype(F32)
    inverse = jnp.exp(channel * (-math.log(10000.0) / half))
    zeta = (channel * (2.0 / HEAD_DIM) + 0.4) / 1.4
    sign = jnp.where(lax.rem(lane, HEAD_DIM) < half, -1.0, 1.0)
    angle = place * inverse
    growth = jnp.exp((place - 0.5 * LENGTH) * (1.0 / XBASE) * jnp.log(zeta))
    shrink = 1.0 / growth
    cosine = jnp.cos(angle)
    sine = jnp.sin(angle) * sign
    return cosine * growth, sine * growth, cosine * shrink, sine * shrink


def start_kernel(
    n, depth, x_ref, w_ref, wd_ref, pos_ref,
    o_ref, wt_ref, wc_ref, cq_ref, sq_ref, ck_ref, sk_ref,
    keep_w, keep_c, local_sem, send_sem, recv_sem, hop_send, hop_recv, col_send, col_recv,
    line_send, line_recv, w_send, w_recv,
):
    z = lax.axis_index("batch")
    rows_z = wc_ref.shape[2]
    cols = wc_ref.shape[3]
    me, twin, near_x, near_y, _ = places()
    own = pltpu.make_async_copy(x_ref, o_ref.at[me], local_sem.at[0])
    own.start()
    wd_rows = pl.ds(pl.multiple_of(z * rows_z, rows_z), rows_z)

    def column(k):
        return wd_ref.at[wd_rows, pl.ds(pl.multiple_of(k * cols, cols), cols)]

    load_column = pltpu.make_async_copy(column(me), keep_c, local_sem.at[4])
    own_column = pltpu.make_async_copy(keep_c, wc_ref.at[me, z], local_sem.at[5])
    load_column.start()
    meet_all(n, depth)
    load_column.wait()
    own_column.start()
    w_rows = pl.ds(
        pl.multiple_of(z * wt_ref.shape[2], wt_ref.shape[2]), wt_ref.shape[2]
    )

    def hop(j, part, target):
        return remote(
            w_ref.at[j, w_rows], wt_ref.at[part, z], hop_send.at[j], hop_recv.at[part], target
        )

    def load(j):
        return pltpu.make_async_copy(w_ref.at[j, w_rows], keep_w, local_sem.at[6])

    def here(j, part):
        return pltpu.make_async_copy(keep_w, wt_ref.at[part, z], local_sem.at[1 + j])

    for j in range(3):
        block = 3 * me + j
        target = lax.rem(block, n)
        for part in range(3):
            inside = block // n == part

            @pl.when(inside & (target != me))
            def _():
                hop(j, part, target).start()

            @pl.when(inside & (target == me))
            def _():
                load(j).start()
                load(j).wait()
                here(j, part).start()

    turns = [
        remote(
            column(lax.rem(me + k, n)),
            wc_ref.at[me, z],
            col_send.at[k],
            col_recv.at[k],
            lax.rem(me + k, n),
        )
        for k in range(1, n)
    ]
    for turn in turns:
        turn.start()
    sends = gather_copies(x_ref, o_ref, send_sem, recv_sem)
    for k in range(5):
        sends[k].start()

    line = Line(
        depth,
        lambda owner, k: wc_ref.at[:, owner],
        lambda owner: wc_ref.at[:, owner],
        line_send,
        line_recv,
    )

    line_w = Line(
        depth,
        lambda owner, k: wt_ref.at[:, owner],
        lambda owner: wt_ref.at[:, owner],
        w_send,
        w_recv,
    )
    for j in range(3):
        block = 3 * me + j
        target = lax.rem(block, n)
        for part in range(3):

            @pl.when((block // n == part) & (target == me))
            def _():
                here(j, part).wait()

    for part in range(3):
        source = (part * n + me) // 3

        @pl.when(source != me)
        def _():
            hop(0, part, source).wait_recv()

    line_w.start(0)

    @pl.loop(0, pos_ref.shape[0])
    def _(r):
        at = pl.ds(pl.multiple_of(r * 128, 128), 128)
        places_here = jnp.broadcast_to(pos_ref[pl.ds(r, 1), :], (128, 128)).T
        tables = lane_tables(places_here)
        for ref, table in zip((cq_ref, sq_ref, ck_ref, sk_ref), tables, strict=True):
            ref[at] = table

    own_column.wait()
    for turn in turns:
        turn.wait_recv()

    def hop_one():
        line_w.land(0)
        line_w.start(1)

    def hop_two():
        for k in range(2, depth - 1):
            line_w.land(k - 1)
            line_w.start(k)
        line.start(0)

    gather_run(sends, hop_one, hop_two)
    line_w.land(depth - 2)
    line.land(0)
    for k in range(depth - 1):
        line_w.sent(k)
    line.sent(0)
    for turn in turns:
        turn.wait_send()
    for j in range(3):
        block = 3 * me + j
        target = lax.rem(block, n)
        for part in range(3):

            @pl.when((block // n == part) & (target != me))
            def _():
                hop(j, part, target).wait_send()

    own.wait()


def start_exchange(block, w_qkv, w_down, positions, collective_id):
    n, depth = lax.axis_size("seq"), lax.axis_size("batch")
    rows, width = block.shape
    piece = w_qkv.shape[0] // 3
    w = w_qkv.reshape(3, piece, width)
    if n != 8:
        me = lax.axis_index("seq")
        turned = [
            lax.ppermute(w[j], "seq", [(d, (3 * d + j) % n) for d in range(n)])
            for j in range(3)
        ]
        parts = [pick_part(turned, me, n, part) for part in range(3)]
        place = jnp.broadcast_to(positions[:, None], (positions.shape[0], 128))
        return (
            lax.all_gather(block, "seq", axis=0, tiled=True),
            jnp.concatenate(parts, axis=0),
            lax.all_to_all(w_down, "seq", split_axis=1, concat_axis=0, tiled=True),
            lane_tables(place),
        )
    rows_z, cols = w_down.shape[0] // depth, w_down.shape[1] // n
    inside = pl.BlockSpec(memory_space=pltpu.VMEM)
    table = jax.ShapeDtypeStruct((n * rows, 128), F32)
    gathered, turned, columns, *tables = pl.pallas_call(
        functools.partial(start_kernel, n, depth),
        out_shape=(
            jax.ShapeDtypeStruct((n, rows, width), block.dtype),
            jax.ShapeDtypeStruct((3, depth, piece // depth, width), w.dtype),
            jax.ShapeDtypeStruct((n, depth, rows_z, cols), w_down.dtype),
            *([table] * 4),
        ),
        in_specs=[INSIDE, ANY, ANY, INSIDE],
        out_specs=(ANY, ANY, ANY, *([INSIDE] * 4)),
        scratch_shapes=[
            pltpu.VMEM((piece // depth, width), BF16),
            pltpu.VMEM((rows_z, cols), BF16),
            pltpu.SemaphoreType.DMA((7,)),
            pltpu.SemaphoreType.DMA((13,)),
            pltpu.SemaphoreType.DMA((13,)),
            pltpu.SemaphoreType.DMA((3,)),
            pltpu.SemaphoreType.DMA((3,)),
            pltpu.SemaphoreType.DMA((n,)),
            pltpu.SemaphoreType.DMA((n,)),
            pltpu.SemaphoreType.DMA((2, depth)),
            pltpu.SemaphoreType.DMA((2, depth)),
            pltpu.SemaphoreType.DMA((2, depth)),
            pltpu.SemaphoreType.DMA((2, depth)),
        ],
        compiler_params=pltpu.CompilerParams(
            collective_id=collective_id, has_side_effects=True, vmem_limit_bytes=VMEM_LIMIT
        ),
        name="start_exchange",
    )(block, w, w_down, positions.reshape(-1, 128))
    return (
        gathered.reshape(n * rows, width),
        turned.reshape(3 * piece, width),
        columns,
        tables,
    )


def scatter_kernel(
    p_ref, o_ref, own, twin_in, held, local_sem, send_sem, recv_sem
):
    me, twin, near_x, near_y, across = places()
    rows = p_ref.shape[1]
    half = rows // 2
    low, high = pl.ds(0, half), pl.ds(half, half)
    mine = (across, near_x, near_y, me)

    loads = [
        pltpu.make_async_copy(p_ref.at[block], own.at[i], local_sem.at[i])
        for i, block in enumerate(mine)
    ]
    for load in loads:
        load.start()
    meet((me + twin, near_x, near_y))

    def copy(k, src, dst, partner):
        return remote(src, dst, send_sem.at[k], recv_sem.at[k], partner)

    twins = [
        copy(i, p_ref.at[block + twin], twin_in.at[i], me + twin)
        for i, block in enumerate(mine)
    ]
    for send in twins:
        send.start()
    sends = [
        copy(4, own.at[0, low], held.at[0], near_x),
        copy(5, own.at[0, high], held.at[1], near_y),
        copy(6, own.at[1, low], held.at[2], near_x),
        copy(7, own.at[2, high], held.at[3], near_y),
        copy(8, own.at[1, high], held.at[4], near_x),
        copy(9, own.at[2, low], held.at[5], near_y),
    ]
    step = 32

    def add_twin(i):
        loads[i].wait()
        twins[i].wait_recv()

        @pl.loop(0, rows // step)
        def _(r):
            at = pl.ds(pl.multiple_of(r * step, step), step)
            own[i, at] = (
                own[i, at].astype(F32) + twin_in[i, at].astype(F32)
            ).astype(own.dtype)

    def add_held(i, base, slot):
        @pl.loop(0, half // step)
        def _(r):
            at = pl.ds(pl.multiple_of(r * step, step), step)
            to = pl.ds(pl.multiple_of(base + r * step, step), step)
            own[i, to] = (
                own[i, to].astype(F32) + held[slot, at].astype(F32)
            ).astype(own.dtype)

    add_twin(0)
    sends[0].start()
    sends[1].start()
    add_twin(1)
    sends[2].start()
    add_twin(2)
    sends[3].start()
    sends[1].wait_recv()
    add_held(1, half, 1)
    sends[4].start()
    sends[0].wait_recv()
    add_held(2, 0, 0)
    sends[5].start()
    loads[3].wait()
    twins[3].wait_recv()
    for k in (2, 3, 4, 5):
        sends[k].wait_recv()

    def final(base, first, second):
        @pl.loop(0, half // step)
        def _(r):
            at = pl.ds(pl.multiple_of(r * step, step), step)
            to = pl.ds(pl.multiple_of(base + r * step, step), step)
            o_ref[to] = (
                own[3, to].astype(F32)
                + twin_in[3, to].astype(F32)
                + held[first, at].astype(F32)
                + held[second, at].astype(F32)
            )

    final(0, 2, 5)
    final(half, 3, 4)
    for send in twins + sends:
        send.wait_send()


def scatter_seq(partial, collective_id):
    n = lax.axis_size("seq")
    rows, width = partial.shape[0] // n, partial.shape[1]
    if n != 8:
        return lax.psum_scatter(
            partial, "seq", scatter_dimension=0, tiled=True
        ).astype(F32)
    return pl.pallas_call(
        scatter_kernel,
        out_shape=jax.ShapeDtypeStruct((rows, width), F32),
        in_specs=[ANY],
        out_specs=pl.BlockSpec(memory_space=pltpu.VMEM),
        scratch_shapes=[
            pltpu.VMEM((4, rows, width), BF16),
            pltpu.VMEM((4, rows, width), BF16),
            pltpu.VMEM((6, rows // 2, width), BF16),
            pltpu.SemaphoreType.DMA((4,)),
            pltpu.SemaphoreType.DMA((10,)),
            pltpu.SemaphoreType.DMA((10,)),
        ],
        compiler_params=pltpu.CompilerParams(
            collective_id=collective_id,
            has_side_effects=True,
            vmem_limit_bytes=VMEM_LIMIT,
        ),
        name="scatter_seq",
    )(partial.reshape(n, rows, width))


def heads_to_tokens_kernel(n, x_ref, o_ref, keep, local_sem, send_sem, recv_sem):
    me = lax.axis_index("seq")
    rows = o_ref.shape[0]
    cols = x_ref.shape[1]
    exchange(
        n,
        me,
        lambda k: x_ref.at[pl.ds(pl.multiple_of(k * rows, rows), rows)],
        o_ref.at[:, pl.ds(pl.multiple_of(me * cols, cols), cols)],
        keep,
        local_sem,
        send_sem,
        recv_sem,
    )


def exchange(n, me, source, target, keep, local_sem, send_sem, recv_sem):
    load = pltpu.make_async_copy(source(me), keep, local_sem.at[0])
    own = pltpu.make_async_copy(keep, target, local_sem.at[1])
    load.start()
    barrier = pltpu.get_barrier_semaphore()
    for k in range(1, n):
        pl.semaphore_signal(
            barrier,
            inc=1,
            device_id={"seq": lax.rem(me + k, n)},
            device_id_type=MESH,
        )
    pl.semaphore_wait(barrier, n - 1)
    copies = []
    for k in range(1, n):
        partner = lax.rem(me + k, n)
        copies.append(
            pltpu.make_async_remote_copy(
                src_ref=source(partner),
                dst_ref=target,
                send_sem=send_sem.at[k],
                recv_sem=recv_sem.at[k],
                device_id={"seq": partner},
                device_id_type=MESH,
            )
        )
        copies[-1].start()
    load.wait()
    own.start()
    for copy in copies:
        copy.wait()
    own.wait()


def heads_to_tokens(heads, collective_id):
    n = lax.axis_size("seq")
    total, cols = heads.shape
    rows = total // n
    return pl.pallas_call(
        functools.partial(heads_to_tokens_kernel, n),
        out_shape=jax.ShapeDtypeStruct((rows, n * cols), heads.dtype),
        in_specs=[ANY],
        out_specs=ANY,
        scratch_shapes=[
            pltpu.VMEM((rows, cols), heads.dtype),
            pltpu.SemaphoreType.DMA((2,)),
            pltpu.SemaphoreType.DMA((n,)),
            pltpu.SemaphoreType.DMA((n,)),
        ],
        compiler_params=pltpu.CompilerParams(
            collective_id=collective_id, has_side_effects=True, vmem_limit_bytes=VMEM_LIMIT
        ),
        name="heads_to_tokens",
    )(heads)


def tokens_to_heads_kernel(n, x_ref, o_ref, keep, local_sem, send_sem, recv_sem):
    me = lax.axis_index("seq")
    rows = x_ref.shape[0]
    cols = o_ref.shape[1]
    exchange(
        n,
        me,
        lambda k: x_ref.at[:, pl.ds(pl.multiple_of(k * cols, cols), cols)],
        o_ref.at[pl.ds(pl.multiple_of(me * rows, rows), rows)],
        keep,
        local_sem,
        send_sem,
        recv_sem,
    )


def tokens_to_heads(tokens, collective_id):
    n = lax.axis_size("seq")
    rows, total = tokens.shape
    return pl.pallas_call(
        functools.partial(tokens_to_heads_kernel, n),
        out_shape=jax.ShapeDtypeStruct((rows * n, total // n), tokens.dtype),
        in_specs=[ANY],
        out_specs=ANY,
        scratch_shapes=[
            pltpu.VMEM((rows, total // n), tokens.dtype),
            pltpu.SemaphoreType.DMA((2,)),
            pltpu.SemaphoreType.DMA((n,)),
            pltpu.SemaphoreType.DMA((n,)),
        ],
        compiler_params=pltpu.CompilerParams(
            collective_id=collective_id, has_side_effects=True, vmem_limit_bytes=VMEM_LIMIT
        ),
        name="tokens_to_heads",
    )(tokens)


def swap_halves(values):
    width = values.shape[-1]
    half = HEAD_DIM // 2
    lane = lax.broadcasted_iota(jnp.int32, values.shape, 1)
    ahead = pltpu.roll(values, width - half, 1)
    behind = pltpu.roll(values, half, 1)
    return jnp.where(lane % HEAD_DIM < half, ahead, behind)


def spread_lanes(table, width):
    return jnp.concatenate([table] * (width // table.shape[-1]), axis=-1)


def qkv_kernel(
    x_ref, w_ref, cq_ref, sq_ref, ck_ref, sk_ref,
    q_ref, k_ref, v_ref, kt_ref, vt_ref,
):
    x = x_ref[...]
    width = q_ref.shape[1]
    query = nt(x, w_ref[0:width])
    query = query * spread_lanes(cq_ref[...], width) + swap_halves(
        query
    ) * spread_lanes(sq_ref[...], width)
    q_ref[...] = query.astype(BF16) * (HEAD_DIM**-0.5)
    keys = nt(x, w_ref[width : 2 * width])
    keys = keys * spread_lanes(ck_ref[...], width) + swap_halves(
        keys
    ) * spread_lanes(sk_ref[...], width)
    k_ref[...] = keys.astype(BF16)
    kt_ref[...] = keys.T.astype(BF16)
    values = nt(x, w_ref[2 * width :])
    v_ref[...] = values.astype(BF16)
    vt_ref[...] = values.T.astype(BF16)


def project_qkv(x, w, tables):
    length, width = x.shape
    cols = w.shape[0] // 3
    steps = length // TILE
    weight = pl.BlockSpec((3 * cols, width), lambda i: (0, 0))
    table = pl.BlockSpec((TILE, tables[0].shape[1]), lambda i: (i, 0))
    row_out = pl.BlockSpec((TILE, cols), lambda i: (i, 0))
    col_out = pl.BlockSpec((cols, TILE), lambda i: (0, i))
    rows = jax.ShapeDtypeStruct((length, cols), BF16)
    columns = jax.ShapeDtypeStruct((cols, length), BF16)
    return pl.pallas_call(
        qkv_kernel,
        grid=(steps,),
        out_shape=(rows, rows, rows, columns, columns),
        in_specs=[pl.BlockSpec((TILE, width), lambda i: (i, 0))]
        + [weight]
        + [table] * 4,
        out_specs=(row_out, row_out, row_out, col_out, col_out),
        compiler_params=pltpu.CompilerParams(vmem_limit_bytes=VMEM_LIMIT),
        cost_estimate=pl.CostEstimate(
            flops=6 * length * width * cols,
            bytes_accessed=2 * length * width + 6 * width * cols + 10 * length * cols,
            transcendentals=0,
        ),
        name="project_qkv",
    )(x, w, *tables)


def pair_mask(start_row, i, j):
    key_place = j * TILE + lax.broadcasted_iota(jnp.int32, (TILE, TILE), 0)
    query_place = i * TILE + lax.broadcasted_iota(jnp.int32, (TILE, TILE), 1)
    return (key_place <= query_place) & (key_place >= start_row)


def head_rows(query, heads):
    lane = lax.broadcasted_iota(jnp.int32, query.shape, 1) // HEAD_DIM
    zero = jnp.zeros_like(query)
    return [jnp.where(lane == h, query, zero) for h in range(heads)]


def attend_kernel(
    heads, first_ref, start_ref, q_ref, k_ref, vt_ref, o_ref, lse_ref, peak, total, mixed
):
    i = pl.program_id(0)
    queries = head_rows(q_ref[...], heads)
    start_row = start_ref[...]

    def block(j, first):
        at = pl.ds(pl.multiple_of(j * TILE, TILE), TILE)
        keys = k_ref[at, :]
        mask = pair_mask(start_row, i, j)
        for h in range(heads):
            here = slice(h * HEAD_DIM, (h + 1) * HEAD_DIM)
            scores = jnp.where(mask, nt(keys, queries[h]), MASKED)
            if first:
                new_peak = jnp.max(scores, axis=0, keepdims=True)
                expo = jnp.exp(scores - new_peak)
                total[h : h + 1] = jnp.sum(expo, axis=0, keepdims=True)
                mixed[here] = nn(vt_ref[here, at], expo.astype(BF16))
            else:
                old_peak = peak[h : h + 1]
                new_peak = jnp.maximum(old_peak, jnp.max(scores, axis=0, keepdims=True))
                expo = jnp.exp(scores - new_peak)
                shrink = jnp.exp(old_peak - new_peak)
                total[h : h + 1] = total[h : h + 1] * shrink + jnp.sum(
                    expo, axis=0, keepdims=True
                )
                mixed[here] = mixed[here] * shrink + nn(
                    vt_ref[here, at], expo.astype(BF16)
                )
            peak[h : h + 1] = new_peak

    block(i, True)

    @pl.loop(0, i - first_ref[i])
    def _(t):
        block(i - 1 - t, False)

    for h in range(heads):
        here = slice(h * HEAD_DIM, (h + 1) * HEAD_DIM)
        mixed[here] = mixed[here] / total[h : h + 1]
    o_ref[...] = mixed[...].T.astype(BF16)
    lse_ref[0] = peak[...] + jnp.log(total[...])


def attend(first, start, q, k, vt):
    length, cols = q.shape
    heads = cols // HEAD_DIM
    steps = length // TILE
    row = pl.BlockSpec((TILE, cols), lambda i, *_: (i, 0))
    return pl.pallas_call(
        functools.partial(attend_kernel, heads),
        out_shape=(
            jax.ShapeDtypeStruct((length, cols), BF16),
            jax.ShapeDtypeStruct((steps, heads, TILE), F32),
        ),
        grid_spec=pltpu.PrefetchScalarGridSpec(
            num_scalar_prefetch=1,
            grid=(steps,),
            in_specs=[
                pl.BlockSpec((1, TILE), lambda i, *_: (0, i)),
                row,
                pl.BlockSpec((length, cols), lambda i, *_: (0, 0)),
                pl.BlockSpec((cols, length), lambda i, *_: (0, 0)),
            ],
            out_specs=(
                row,
                pl.BlockSpec((1, heads, TILE), lambda i, *_: (i, 0, 0)),
            ),
            scratch_shapes=[
                pltpu.VMEM((heads, TILE), F32),
                pltpu.VMEM((heads, TILE), F32),
                pltpu.VMEM((cols, TILE), F32),
            ],
        ),
        compiler_params=pltpu.CompilerParams(vmem_limit_bytes=VMEM_LIMIT),
        cost_estimate=pl.CostEstimate(
            flops=4 * length * 1024 * cols,
            bytes_accessed=8 * length * cols,
            transcendentals=length * 1024 * heads,
        ),
        name="attend",
    )(first, start, q, k, vt)


def attend_back_kernel(
    heads, first_ref, start_ref, q_ref, k_ref, kt_ref, v_ref, o_ref, lse_ref, do_ref,
    cq_ref, sq_ref, ck_ref, sk_ref, grad_ref, dqt, dk_sum, dv_sum,
):
    i = pl.program_id(0)
    steps = pl.num_programs(0)
    width = q_ref.shape[1]
    queries = head_rows(q_ref[...], heads)
    grads = head_rows(do_ref[...], heads)
    start_row = start_ref[...]
    product = (do_ref[...].astype(F32) * o_ref[...].astype(F32)).T
    inner = [
        jnp.sum(product[h * HEAD_DIM : (h + 1) * HEAD_DIM], axis=0, keepdims=True)
        for h in range(heads)
    ]

    def block(j, first):
        at = pl.ds(pl.multiple_of(j * TILE, TILE), TILE)
        keys = k_ref[at, :]
        values = v_ref[at, :]
        mask = pair_mask(start_row, i, j)
        key_term = None
        value_term = None
        for h in range(heads):
            here = slice(h * HEAD_DIM, (h + 1) * HEAD_DIM)
            scores = nt(keys, queries[h])
            weights = jnp.where(mask, jnp.exp(scores - lse_ref[0, h : h + 1]), 0.0)
            grad_weights = nt(values, grads[h])
            grad_scores = (weights * (grad_weights - inner[h])).astype(BF16)
            term = nn(weights.astype(BF16), grads[h])
            value_term = term if value_term is None else value_term + term
            term = nn(grad_scores, queries[h])
            key_term = term if key_term is None else key_term + term
            term = nn(kt_ref[here, at], grad_scores)
            if first:
                dqt[here] = term
            else:
                dqt[here] = dqt[here] + term
        if first:
            dk_sum[at] = key_term
            dv_sum[at] = value_term
        else:
            dk_sum[at] = dk_sum[at] + key_term
            dv_sum[at] = dv_sum[at] + value_term

    block(i, True)

    @pl.loop(0, i - first_ref[i])
    def _(t):
        block(i - 1 - t, False)

    def unturn(grad, cosine, sine):
        grad = grad.astype(BF16).astype(F32)
        cosine = spread_lanes(cosine, width)
        sine = spread_lanes(sine, width)
        return (grad * cosine - swap_halves(grad) * sine).astype(BF16)

    rows = pl.ds(pl.multiple_of(i * TILE, TILE), TILE)
    grad_ref[rows, 0:width] = unturn(
        dqt[...].T * (HEAD_DIM**-0.5), cq_ref[rows, :], sq_ref[rows, :]
    )

    @pl.when(i == steps - 1)
    def _():
        @pl.loop(0, steps)
        def _(j):
            at = pl.ds(pl.multiple_of(j * TILE, TILE), TILE)
            grad_ref[at, width : 2 * width] = unturn(
                dk_sum[at], ck_ref[at, :], sk_ref[at, :]
            )
            grad_ref[at, 2 * width :] = dv_sum[at].astype(BF16)


def attend_back(first, start, q, k, kt, v, o, lse, do, tables):
    length, cols = q.shape
    heads = cols // HEAD_DIM
    steps = length // TILE
    row = pl.BlockSpec((TILE, cols), lambda i, *_: (i, 0))
    whole = pl.BlockSpec((length, cols), lambda i, *_: (0, 0))
    table = pl.BlockSpec((length, tables[0].shape[1]), lambda i, *_: (0, 0))
    return pl.pallas_call(
        functools.partial(attend_back_kernel, heads),
        out_shape=jax.ShapeDtypeStruct((length, 3 * cols), BF16),
        grid_spec=pltpu.PrefetchScalarGridSpec(
            num_scalar_prefetch=1,
            grid=(steps,),
            in_specs=[
                pl.BlockSpec((1, TILE), lambda i, *_: (0, i)),
                row,
                whole,
                pl.BlockSpec((cols, length), lambda i, *_: (0, 0)),
                whole,
                row,
                pl.BlockSpec((1, heads, TILE), lambda i, *_: (i, 0, 0)),
                row,
            ]
            + [table] * 4,
            out_specs=pl.BlockSpec((length, 3 * cols), lambda i, *_: (0, 0)),
            scratch_shapes=[
                pltpu.VMEM((cols, TILE), F32),
                pltpu.VMEM((length, cols), F32),
                pltpu.VMEM((length, cols), F32),
            ],
        ),
        compiler_params=pltpu.CompilerParams(vmem_limit_bytes=VMEM_LIMIT),
        cost_estimate=pl.CostEstimate(
            flops=10 * length * 1024 * cols,
            bytes_accessed=16 * length * cols,
            transcendentals=length * 1024 * heads,
        ),
        name="attend_back",
    )(first, start, q, k, kt, v, o, lse, do, *tables)


def upper_kernel(
    x_ref, wu_ref, c_ref, wd_ref, gain_ref, act_ref, slope_ref, grad_ref, stat_ref
):
    upper = nt(x_ref[...], wu_ref[...])
    grad = nn(c_ref[...], wd_ref[...])
    below = 0.5 * (1.0 + lax.erf(upper * (0.5**0.5)))
    act = upper * below
    slope = below + upper * (jnp.exp(-0.5 * upper * upper) * ((2.0 * math.pi) ** -0.5))
    act_ref[...] = act
    slope_ref[...] = slope.astype(BF16)
    grad_ref[...] = grad
    part = grad * gain_ref[...]
    average = jnp.mean(act, axis=-1, keepdims=True)
    centered = act - average
    spread = jnp.sum(centered * centered, axis=-1, keepdims=True)
    part_sum = jnp.sum(part, axis=-1, keepdims=True)
    cross = jnp.sum(part * centered, axis=-1, keepdims=True)
    lane = lax.broadcasted_iota(jnp.int32, (x_ref.shape[0], 128), 1)
    columns = jnp.where(
        lane == 0,
        average,
        jnp.where(lane == 1, spread, jnp.where(lane == 2, part_sum, cross)),
    )
    stat_ref[...] = columns.T[:8]


def upper_pass(x, w_up, cot, w_down, gain):
    length, width = x.shape
    feats = w_up.shape[0]
    rows = TILE
    row = pl.BlockSpec((rows, width), lambda i: (i, 0))
    out = pl.BlockSpec((rows, feats), lambda i: (i, 0))
    return pl.pallas_call(
        upper_kernel,
        grid=(length // rows,),
        out_shape=(
            jax.ShapeDtypeStruct((length, feats), F32),
            jax.ShapeDtypeStruct((length, feats), BF16),
            jax.ShapeDtypeStruct((length, feats), F32),
            jax.ShapeDtypeStruct((8, length), F32),
        ),
        in_specs=[
            row,
            pl.BlockSpec((feats, width), lambda i: (0, 0)),
            row,
            pl.BlockSpec((width, feats), lambda i: (0, 0)),
            pl.BlockSpec((1, feats), lambda i: (0, 0)),
        ],
        out_specs=(out, out, out, pl.BlockSpec((8, rows), lambda i: (0, i))),
        compiler_params=pltpu.CompilerParams(vmem_limit_bytes=VMEM_LIMIT),
        cost_estimate=pl.CostEstimate(
            flops=4 * length * width * feats,
            bytes_accessed=8 * length * width + 8 * length * feats,
            transcendentals=2 * length * feats,
        ),
        name="upper_pass",
    )(x, w_up, cot, w_down, gain)


def hidden_kernel(act_ref, slope_ref, grad_ref, stat_ref, gain_ref, hid_ref, gu_ref, gg_ref):
    i = pl.program_id(0)
    stats = stat_ref[...].T
    average = stats[:, 0:1]
    scale = stats[:, 1:2]
    part_mean = stats[:, 2:3]
    cross_mean = stats[:, 3:4]
    gain = gain_ref[...]
    normal = (act_ref[...] - average) * scale
    grad = grad_ref[...]
    hid_ref[...] = (normal * gain).astype(BF16)
    back = scale * (grad * gain - part_mean - normal * cross_mean)
    gu_ref[...] = (slope_ref[...].astype(F32) * back).astype(BF16)
    term = jnp.sum(grad * normal, axis=0, keepdims=True)

    @pl.when(i == 0)
    def _():
        gg_ref[...] = term

    @pl.when(i > 0)
    def _():
        gg_ref[...] = gg_ref[...] + term


def hidden_pass(act, slope, grad, stats, gain):
    length, feats = act.shape
    out = pl.BlockSpec((TILE, feats), lambda i: (i, 0))
    one = pl.BlockSpec((1, feats), lambda i: (0, 0))
    return pl.pallas_call(
        hidden_kernel,
        grid=(length // TILE,),
        out_shape=(
            jax.ShapeDtypeStruct((length, feats), BF16),
            jax.ShapeDtypeStruct((length, feats), BF16),
            jax.ShapeDtypeStruct((1, feats), F32),
        ),
        in_specs=[out, out, out, pl.BlockSpec((8, TILE), lambda i: (0, i)), one],
        out_specs=(out, out, one),
        compiler_params=pltpu.CompilerParams(vmem_limit_bytes=VMEM_LIMIT),
        cost_estimate=pl.CostEstimate(
            flops=12 * length * feats,
            bytes_accessed=14 * length * feats,
            transcendentals=0,
        ),
        name="hidden_pass",
    )(act, slope, grad, stats, gain)


def stat_kernel(n, feats, x_ref, o_ref, held, send_sem, recv_sem):
    me = lax.axis_index("seq")
    held[me] = x_ref[...]
    meet([lax.rem(me + k, n) for k in range(1, n)])
    copies = [
        remote(x_ref, held.at[me], send_sem.at[k], recv_sem.at[k], lax.rem(me + k, n))
        for k in range(1, n)
    ]
    for copy in copies:
        copy.start()
    for copy in copies:
        copy.wait()
    average = held[0, 0:1]
    for d in range(1, n):
        average = average + held[d, 0:1]
    average = average * (1.0 / n)
    spread = jnp.zeros_like(average)
    part = jnp.zeros_like(average)
    cross = jnp.zeros_like(average)
    for d in range(n):
        shift = held[d, 0:1] - average
        spread = spread + held[d, 1:2] + feats * (shift * shift)
        part = part + held[d, 2:3]
        cross = cross + held[d, 3:4] + shift * held[d, 2:3]
    whole = 1.0 / (n * feats)
    scale = lax.rsqrt(spread * whole + EPSILON)
    o_ref[0:1] = average
    o_ref[1:2] = scale
    o_ref[2:3] = part * whole
    o_ref[3:4] = cross * scale * whole
    o_ref[4:8] = jnp.zeros((4, average.shape[1]), F32)


def join_stats(stat, feats, collective_id):
    n = lax.axis_size("seq")
    inside = pl.BlockSpec(memory_space=pltpu.VMEM)
    return pl.pallas_call(
        functools.partial(stat_kernel, n, feats),
        out_shape=jax.ShapeDtypeStruct(stat.shape, F32),
        in_specs=[inside],
        out_specs=inside,
        scratch_shapes=[
            pltpu.VMEM((n, *stat.shape), F32),
            pltpu.SemaphoreType.DMA((n,)),
            pltpu.SemaphoreType.DMA((n,)),
        ],
        compiler_params=pltpu.CompilerParams(
            collective_id=collective_id, has_side_effects=True, vmem_limit_bytes=VMEM_LIMIT
        ),
        name="join_stats",
    )(stat)


STEP = 32


def mix_kernel(att_ref, x_ref, w_ref, gm_ref, gf_ref, mix_ref, mid_ref, ffn_ref):
    j = pl.program_id(0)
    rows = att_ref.shape[0]
    cols = w_ref.shape[0]

    @pl.when(j == 0)
    def _():
        @pl.loop(0, rows // STEP)
        def _(r):
            at = pl.ds(pl.multiple_of(r * STEP, STEP), STEP)
            normal, _ = norm_parts(att_ref[at].astype(F32))
            mix_ref[at] = (normal * gm_ref[...]).astype(BF16)

    here = pl.ds(pl.multiple_of(j * cols, cols), cols)
    mid_ref[:, here] = x_ref[:, here].astype(F32) + nt(mix_ref[...], w_ref[...])

    @pl.when(j == pl.num_programs(0) - 1)
    def _():
        @pl.loop(0, rows // STEP)
        def _(r):
            at = pl.ds(pl.multiple_of(r * STEP, STEP), STEP)
            normal, _ = norm_parts(mid_ref[at])
            ffn_ref[at] = (normal * gf_ref[...]).astype(BF16)


def mix_pass(attended, x, w_out, gain_mix, gain_ffn):
    rows, width = x.shape
    cols = TILE
    n = width // cols
    whole = pl.BlockSpec((rows, width), lambda j: (0, 0))
    gain = pl.BlockSpec((1, width), lambda j: (0, 0))
    low = jax.ShapeDtypeStruct((rows, width), BF16)
    return pl.pallas_call(
        mix_kernel,
        grid=(n,),
        out_shape=(low, jax.ShapeDtypeStruct((rows, width), F32), low),
        in_specs=[
            whole,
            whole,
            pl.BlockSpec((cols, width), lambda j: (j, 0)),
            gain,
            gain,
        ],
        out_specs=(whole, whole, whole),
        compiler_params=pltpu.CompilerParams(vmem_limit_bytes=VMEM_LIMIT),
        cost_estimate=pl.CostEstimate(
            flops=2 * rows * width * width,
            bytes_accessed=2 * width * width + 12 * rows * width,
            transcendentals=0,
        ),
        name="mix_pass",
    )(attended, x, w_out, gain_mix[None], gain_ffn[None])


def branch_kernel(
    g_ref, mid_ref, cot_ref, att_ref, w_ref, gm_ref, gf_ref,
    gmid_ref, gbr_ref, gatt_ref, ggf_ref, ggm_ref, total,
):
    j = pl.program_id(0)
    rows = att_ref.shape[0]
    cols = w_ref.shape[0]

    @pl.when(j == 0)
    def _():
        ggf_ref[...] = jnp.zeros_like(ggf_ref)
        total[...] = jnp.zeros_like(total)

        @pl.loop(0, rows // STEP)
        def _(r):
            at = pl.ds(pl.multiple_of(r * STEP, STEP), STEP)
            normal, scale = norm_parts(mid_ref[at])
            part, gain_part = norm_back(g_ref[at], normal, scale, gf_ref[...])
            ggf_ref[...] += gain_part[None]
            grad = cot_ref[at].astype(F32) + part
            gmid_ref[at] = grad
            gbr_ref[at] = grad.astype(BF16)

    here = pl.ds(pl.multiple_of(j * cols, cols), cols)
    total[...] += nn(gbr_ref[:, here], w_ref[...])

    @pl.when(j == pl.num_programs(0) - 1)
    def _():
        ggm_ref[...] = jnp.zeros_like(ggm_ref)

        @pl.loop(0, rows // STEP)
        def _(r):
            at = pl.ds(pl.multiple_of(r * STEP, STEP), STEP)
            normal, scale = norm_parts(att_ref[at].astype(F32))
            part, gain_part = norm_back(total[at], normal, scale, gm_ref[...])
            ggm_ref[...] += gain_part[None]
            gatt_ref[at] = part.astype(BF16)


def branch_pass(grad_ffn_in, middle, cot, attended, w_out, gain_mix, gain_ffn):
    rows, width = cot.shape
    cols = TILE
    n = width // cols
    whole = pl.BlockSpec((rows, width), lambda j: (0, 0))
    gain = pl.BlockSpec((1, width), lambda j: (0, 0))
    low = jax.ShapeDtypeStruct((rows, width), BF16)
    sums = jax.ShapeDtypeStruct((1, width), F32)
    return pl.pallas_call(
        branch_kernel,
        grid=(n,),
        out_shape=(jax.ShapeDtypeStruct((rows, width), F32), low, low, sums, sums),
        in_specs=[
            whole,
            whole,
            whole,
            whole,
            pl.BlockSpec((cols, width), lambda j: (j, 0)),
            gain,
            gain,
        ],
        out_specs=(whole, whole, whole, gain, gain),
        scratch_shapes=[pltpu.VMEM((rows, width), F32)],
        compiler_params=pltpu.CompilerParams(vmem_limit_bytes=VMEM_LIMIT),
        cost_estimate=pl.CostEstimate(
            flops=2 * rows * width * width,
            bytes_accessed=2 * width * width + 20 * rows * width,
            transcendentals=0,
        ),
        name="branch_pass",
    )(grad_ffn_in, middle, cot, attended, w_out, gain_mix[None], gain_ffn[None])


CHUNK = 64


def finish_kernel(
    n, depth, gq_ref, gd_ref, pw_ref, pn_ref, po_ref, x_ref, grad_ref, mid_ref, ga_ref, gm_ref, gf_ref, gh_ref,
    oq_ref, od_ref, ow_ref, gi_ref, out_ref, sums_ref,
    own, twin_in, held, zown, zin, stage, gain_here, gain_row, gain_pack, gain_line,
    local_sem, load_sem, stage_sem, send_sem, recv_sem, keep_sem,
    up_send, up_recv, down_send, down_recv, home_send, home_recv, gain_send, gain_recv,
):
    me, twin, near_x, near_y, across = places()
    z = lax.axis_index("batch")
    rows, width = pn_ref.shape[1:]
    half = rows // 2
    low, high = pl.ds(0, half), pl.ds(half, half)
    mine = (across, near_x, near_y, me)
    _, chunk, cols = zown.shape
    across_width = width // cols
    per_part = (gq_ref.shape[1] // chunk) * across_width
    turned = gq_ref.shape[0] * per_part
    per_source = gd_ref.shape[1] // chunk
    outer = turned + gd_ref.shape[0] * per_source
    chunks = zown.shape[0]
    per_side = chunks // 2

    def cut(i, size):
        return pl.ds(pl.multiple_of(i * size, size), size)

    def wide(i):
        return cut(i // across_width, chunk), cut(lax.rem(i, across_width), cols)

    line_loads = []
    for g in range(turned):
        source = gq_ref.at[(g // per_part, *wide(g % per_part))]
        line_loads.append(pltpu.make_async_copy(source, zown.at[g], load_sem.at[g]))
    for g in range(turned, outer):
        source = gd_ref.at[
            (g - turned) // per_source, cut((g - turned) % per_source, chunk)
        ]
        line_loads.append(pltpu.make_async_copy(source, zown.at[g], load_sem.at[g]))
    for load in line_loads:
        load.start()
    partials = (pw_ref, pn_ref, po_ref)
    loads = [
        [
            pltpu.make_async_copy(p.at[block], own.at[m, i], local_sem.at[4 * m + i])
            for i, block in enumerate(mine)
        ]
        for m, p in enumerate(partials)
    ]
    for part in loads:
        for load in part:
            load.start()
    meet_all(n, depth)

    def copy(m, k, src, dst, partner):
        return remote(src, dst, send_sem.at[m, k], recv_sem.at[m, k], partner)

    twins = [
        [
            copy(m, i, p.at[block + twin], twin_in.at[m, i], me + twin)
            for i, block in enumerate(mine)
        ]
        for m, p in enumerate(partials)
    ]
    sends = [
        [
            copy(m, 4, own.at[m, 0, low], held.at[m, 0], near_x),
            copy(m, 5, own.at[m, 0, high], held.at[m, 1], near_y),
            copy(m, 6, own.at[m, 1, low], held.at[m, 2], near_x),
            copy(m, 7, own.at[m, 2, high], held.at[m, 3], near_y),
            copy(m, 8, own.at[m, 1, high], held.at[m, 4], near_x),
            copy(m, 9, own.at[m, 2, low], held.at[m, 5], near_y),
        ]
        for m in range(3)
    ]
    for part in twins:
        for send in part:
            send.start()

    def add_twin(m, i):
        loads[m][i].wait()
        twins[m][i].wait_recv()

        @pl.loop(0, rows // STEP)
        def _(r):
            at = cut(r, STEP)
            own[m, i, at] = (
                own[m, i, at].astype(F32) + twin_in[m, i, at].astype(F32)
            ).astype(BF16)

    def add_held(m, i, base, slot):
        @pl.loop(0, half // STEP)
        def _(r):
            at = cut(r, STEP)
            to = pl.ds(pl.multiple_of(base + r * STEP, STEP), STEP)
            own[m, i, to] = (
                own[m, i, to].astype(F32) + held[m, slot, at].astype(F32)
            ).astype(BF16)

    def first(m):
        add_twin(m, 0)
        sends[m][0].start()
        sends[m][1].start()
        add_twin(m, 1)
        sends[m][2].start()
        add_twin(m, 2)
        sends[m][3].start()

    def second(m):
        sends[m][1].wait_recv()
        add_held(m, 1, half, 1)
        sends[m][4].start()
        sends[m][0].wait_recv()
        add_held(m, 2, 0, 0)
        sends[m][5].start()

    def last(m, store):
        loads[m][3].wait()
        twins[m][3].wait_recv()
        for k in (2, 3, 4, 5):
            sends[m][k].wait_recv()
        for base, one, two in ((0, 2, 5), (half, 3, 4)):

            @pl.loop(0, half // STEP)
            def _(r):
                at = cut(r, STEP)
                place = base + r * STEP
                to = pl.ds(pl.multiple_of(place, STEP), STEP)
                store(
                    place,
                    to,
                    own[m, 3, to].astype(F32)
                    + twin_in[m, 3, to].astype(F32)
                    + held[m, one, at].astype(F32)
                    + held[m, two, at].astype(F32),
                )

    def store_line(place, to, value):
        value = value.astype(BF16)
        for side in range(across_width):
            zown[
                outer + (place // chunk) * across_width + side,
                pl.ds(pl.multiple_of(lax.rem(place, chunk), STEP), STEP),
            ] = value[:, side * cols : (side + 1) * cols]

    def store_inputs(place, to, value):
        normal, scale = norm_parts(x_ref[to].astype(F32))
        part, gain_part = norm_back(value, normal, scale, ga_ref[...])
        gi_ref[to] = grad_ref[to] + part
        gain_here[0:1] = gain_here[0:1] + gain_part[None]

    def store_outputs(place, to, value):
        out_ref[to] = (mid_ref[to] + value).astype(BF16)

    def home(part):
        block = part * n + me
        return block // 3, lax.rem(block, 3)

    def deliver_far(g):
        target, slot = home(g // per_part)
        piece = lax.rem(g, per_part)
        return remote(
            zin.at[g],
            oq_ref.at[(slot, *wide(piece))],
            home_send.at[g],
            home_recv.at[slot, piece],
            target,
        )

    def deliver_near(g):
        _, slot = home(g // per_part)
        return pltpu.make_async_copy(
            zin.at[g], oq_ref.at[(slot, *wide(lax.rem(g, per_part)))], keep_sem.at[g]
        )

    def widen(g):
        @pl.loop(0, chunk // STEP)
        def _(r):
            at = cut(r, STEP)
            stage[at] = zin[g, at].astype(F32)

    def deliver(g):
        target, _ = home(g // per_part)

        @pl.when((g < turned) & (target != me))
        def _():
            deliver_far(g).start()

        @pl.when((g < turned) & (target == me))
        def _():
            deliver_near(g).start()

        @pl.when((g >= turned) & (g < outer))
        def _():
            widen(g)
            at = g - turned
            place = cut(lax.rem(at, per_source), chunk), cut(at // per_source, cols)
            store = pltpu.make_async_copy(stage, od_ref.at[place], stage_sem)
            store.start()
            store.wait()

        @pl.when(g >= outer)
        def _():
            widen(g)
            store = pltpu.make_async_copy(
                stage, ow_ref.at[wide(g - outer)], stage_sem
            )
            store.start()
            store.wait()

    def delivered(g):
        target, _ = home(g // per_part)

        @pl.when(target != me)
        def _():
            deliver_far(g).wait_send()

        @pl.when(target == me)
        def _():
            deliver_near(g).wait()

    def go_up(g, ahead):
        return line_remote(zown.at[g], zin.at[g], up_send.at[g], up_recv.at[g], ahead)

    def go_down(g, behind):
        return line_remote(
            zin.at[g], zin.at[g], down_send.at[g], down_recv.at[g], behind
        )

    def ranks(side):
        if side == 0:
            return z, z + 1, z - 1
        return depth - 1 - z, z - 1, z + 1

    def add_line(g, target):
        @pl.loop(0, chunk // STEP)
        def _(r):
            at = cut(r, STEP)
            target[g, at] = (zown[g, at].astype(F32) + zin[g, at].astype(F32)).astype(
                BF16
            )

    lead = 2
    far = 2 * (depth - 1)
    steps = per_side + 2 * far

    def line_enter(c):
        for side in (0, 1):
            rank, ahead, _ = ranks(side)

            @pl.when(rank == 0)
            def _():
                go_up(2 * c + side, ahead).start()

    def line_step(t):
        @pl.when(t + lead < per_side)
        def _():
            line_enter(t + lead)

        back = []
        for side in (0, 1):
            rank, ahead, behind = ranks(side)
            c_back = t - 2 * far + 2 * rank
            g_back = 2 * c_back + side
            there = (c_back >= 0) & (c_back < per_side) & (rank < depth - 1)
            back.append((there, g_back))

            @pl.when(there)
            def _():
                go_down(g_back, ahead).wait_recv()

            @pl.when(there & (rank > 0))
            def _():
                go_down(g_back, behind).start()

        for side in (0, 1):
            rank, ahead, behind = ranks(side)
            c = t - 2 * rank
            g = 2 * c + side
            there = (c >= 0) & (c < per_side)

            @pl.when(there & (rank > 0) & (rank < depth - 1))
            def _():
                go_up(g, behind).wait_recv()
                add_line(g, zown)
                go_up(g, ahead).start()

            @pl.when(there & (rank == depth - 1))
            def _():
                go_up(g, behind).wait_recv()
                add_line(g, zin)
                go_down(g, behind).start()
                deliver(g)

        for there, g_back in back:

            @pl.when(there)
            def _():
                deliver(g_back)

    def line_steps(first_step, last_step):
        @pl.loop(first_step, last_step)
        def _(t):
            line_step(t)

    gain_here[...] = jnp.zeros_like(gain_here)
    for load in line_loads:
        load.wait()
    for c in range(lead):
        line_enter(c)
    first(0)
    line_steps(0, 8)
    second(0)
    line_steps(8, 9)
    first(1)
    line_steps(9, 18)
    last(0, store_line)
    line_steps(18, 20)
    second(1)
    line_steps(20, 21)
    first(2)
    line_steps(21, 28)
    last(1, store_inputs)

    gain_here[1:2] = gm_ref[...]
    gain_here[2:3] = gf_ref[...]
    gain_here[3:4, 0 : gh_ref.shape[1]] = gh_ref[...]
    gain_row[me] = gain_here[...]
    rounds = [
        remote(
            gain_here,
            gain_row.at[me],
            gain_send.at[0, k],
            gain_recv.at[0, k],
            lax.rem(me + k, n),
        )
        for k in range(1, n)
    ]
    for send in rounds:
        send.start()
    line_steps(28, 32)
    second(2)
    line_steps(32, 40)
    last(2, store_outputs)
    line_steps(40, 42)
    for send in rounds:
        send.wait()
    total = gain_row[0]
    for d in range(1, n):
        total = total + gain_row[d]
    gain_pack[0:8] = total
    for d in range(n):
        gain_pack[8 + d : 9 + d] = gain_row[d, 3:4]
    gain_line[z] = gain_pack[...]
    rounds = [
        line_remote(
            gain_pack,
            gain_line.at[z],
            gain_send.at[1, k],
            gain_recv.at[1, k],
            lax.rem(z + k, depth),
        )
        for k in range(1, depth)
    ]
    for send in rounds:
        send.start()
    line_steps(42, steps)
    for send in rounds:
        send.wait()
    total = gain_line[0]
    for d in range(1, depth):
        total = total + gain_line[d]
    sums_ref[...] = total

    for m in range(3):
        for send in twins[m] + sends[m]:
            send.wait_send()
    for g in range(chunks):
        rank, ahead, behind = ranks(g % 2)

        @pl.when(rank < depth - 1)
        def _():
            go_up(g, ahead).wait_send()

        @pl.when(rank > 0)
        def _():
            go_down(g, behind).wait_send()

    for g in range(turned):
        delivered(g)
    for slot in range(3):
        block = 3 * me + slot
        source = lax.rem(block, n)

        @pl.when(source != me)
        def _():
            for piece in range(per_part):
                remote(
                    zin.at[0],
                    oq_ref.at[(slot, *wide(piece))],
                    home_send.at[0],
                    home_recv.at[slot, piece],
                    source,
                ).wait_recv()


def finish(
    grad_qkv, grad_down, part_out, part_normed, part_outputs, x, grad_middle, middle, gain, gains, collective_id
):
    n, depth = lax.axis_size("seq"), lax.axis_size("batch")
    rows, width = part_out.shape[0] // n, part_out.shape[1]
    cols = grad_qkv.shape[1]
    sources, _, feats = grad_down.shape
    if n != 8 or depth != 4:
        me = lax.axis_index("seq")
        blocks = lax.psum(grad_qkv, "batch")
        back = [
            lax.ppermute(
                give_part(blocks, me, n, j),
                "seq",
                [((3 * d + j) % n, d) for d in range(n)],
            )
            for j in range(3)
        ]
        w_out = lax.psum(scatter_seq(part_out, None).astype(BF16), "batch")
        normal, scale = norm_parts(x.astype(F32))
        part, gain_part = norm_back(scatter_seq(part_normed, None), normal, scale, gain)
        shared = [lax.psum(g, ("batch", "seq")) for g in (gain_part, gains[0][0], gains[1][0])]
        hidden = lax.all_gather(lax.psum(gains[2][0], "batch"), "seq", axis=0, tiled=True)
        down = lax.psum(grad_down, "batch")
        return (
            jnp.concatenate(back, axis=0),
            jnp.swapaxes(down, 0, 1).reshape(rows, sources * feats).astype(F32),
            w_out.astype(F32),
            grad_middle + part,
            (middle + scatter_seq(part_outputs, None)).astype(BF16),
            (*shared, hidden),
        )
    chunks = (
        3 * cols * width + rows * width + sources * rows * feats
    ) // (CHUNK * feats)
    dma = pltpu.SemaphoreType.DMA
    line = pltpu.VMEM((chunks, CHUNK, feats), BF16)
    w_qkv, w_down, w_out, grad_inputs, outputs, sums = pl.pallas_call(
        functools.partial(finish_kernel, n, depth),
        out_shape=(
            jax.ShapeDtypeStruct((3, cols, width), BF16),
            jax.ShapeDtypeStruct((rows, sources * feats), F32),
            jax.ShapeDtypeStruct((rows, width), F32),
            jax.ShapeDtypeStruct((rows, width), F32),
            jax.ShapeDtypeStruct((rows, width), BF16),
            jax.ShapeDtypeStruct((16, width), F32),
        ),
        in_specs=[ANY] * 5 + [INSIDE] * 7,
        out_specs=(ANY, ANY, ANY, INSIDE, INSIDE, INSIDE),
        scratch_shapes=[
            pltpu.VMEM((3, 4, rows, width), BF16),
            pltpu.VMEM((3, 4, rows, width), BF16),
            pltpu.VMEM((3, 6, rows // 2, width), BF16),
            line,
            line,
            pltpu.VMEM((CHUNK, feats), F32),
            pltpu.VMEM((8, width), F32),
            pltpu.VMEM((n, 8, width), F32),
            pltpu.VMEM((16, width), F32),
            pltpu.VMEM((depth, 16, width), F32),
            dma((12,)),
            dma((chunks,)),
            dma,
            dma((3, 10)),
            dma((3, 10)),
            dma((chunks,)),
            dma((chunks,)),
            dma((chunks,)),
            dma((chunks,)),
            dma((chunks,)),
            dma((chunks,)),
            dma((3, cols * width // (CHUNK * feats))),
            dma((2, n)),
            dma((2, n)),
        ],
        compiler_params=pltpu.CompilerParams(
            collective_id=collective_id,
            has_side_effects=True,
            vmem_limit_bytes=VMEM_LIMIT,
        ),
        name="finish",
    )(
        grad_qkv,
        grad_down,
        *[p.reshape(n, rows, width) for p in (part_out, part_normed, part_outputs)],
        x,
        grad_middle,
        middle,
        gain[None],
        *gains,
    )
    return (
        w_qkv.reshape(3 * cols, width),
        w_down,
        w_out,
        grad_inputs,
        outputs,
        (sums[0], sums[1], sums[2], sums[8:, :feats].reshape(-1)),
    )


def body(
    inputs,
    segment_ids,
    w_qkv,
    w_out,
    w_up,
    w_down,
    gain_attn,
    gain_mix,
    gain_ffn,
    gain_hidden,
    cotangent,
):
    _, local, width = inputs.shape
    n, depth = lax.axis_size("seq"), lax.axis_size("batch")
    me = lax.axis_index("seq")
    length = local * n
    feats = w_up.shape[0]
    x_low = inputs[0]
    x = x_low.astype(F32)
    cot = cotangent[0]
    segment = segment_ids[0]

    w_out_full = lax.all_gather(w_out, "seq", axis=0, tiled=True)
    normed = (norm_parts(x)[0] * gain_attn).astype(BF16)
    before = [jnp.sum((segment < d).astype(jnp.int32)) for d in range(1, DOCS)]
    start = jnp.zeros_like(segment)
    for d in range(1, DOCS):
        start = jnp.where(segment == d, before[d - 1], start)
    positions = jnp.arange(length, dtype=jnp.int32) - start
    first = start[::TILE] // TILE
    start_row = start[None, :]

    normed_full, w_heads, w_down_near, tables = start_exchange(
        normed, w_qkv, w_down, positions.astype(F32), 1
    )
    cot_late, _ = lax.optimization_barrier((cot, w_heads))
    cot_full = lax.all_gather(cot_late, "seq", axis=0, tiled=True)

    q, k, v, kt, vt = project_qkv(normed_full, w_heads, tables)
    attended_heads, lse = attend(first, start_row, q, k, vt)
    attended = heads_to_tokens(attended_heads, 2)
    mix_in, middle, ffn_in = mix_pass(attended, x_low, w_out_full, gain_mix, gain_ffn)
    ffn_full, w_down_cols = gather_seq(ffn_in, w_down_near, 3)

    gain_here = lax.dynamic_slice_in_dim(gain_hidden, me * feats, feats, 0)[None, :]
    act, slope, grad_hidden, stat = upper_pass(
        ffn_full, w_up, cot_full, w_down_cols, gain_here
    )
    stats = join_stats(stat, feats, 8)
    hidden, grad_upper, grad_gain_here = hidden_pass(act, slope, grad_hidden, stats, gain_here)

    grad_w_up = tn(grad_upper, ffn_full).astype(BF16)
    grad_upper, grad_w_up = lax.optimization_barrier((grad_upper, grad_w_up))
    grad_w_up = lax.psum(grad_w_up, "batch")
    grad_w_down = tn(cot_full, hidden).astype(BF16).reshape(n, local, feats)
    grad_upper, grad_w_down = lax.optimization_barrier((grad_upper, grad_w_down))
    grad_ffn_in = scatter_seq(nn(grad_upper, w_up).astype(BF16), 4)
    grad_middle, grad_branch, grad_att, grad_gain_ffn, grad_gain_mix = branch_pass(
        grad_ffn_in, middle, cot, attended, w_out_full, gain_mix, gain_ffn
    )
    grad_heads = tokens_to_heads(grad_att, 5)
    grad_w_down, grad_heads = lax.optimization_barrier((grad_w_down, grad_heads))
    grad_w_down = lax.all_to_all(grad_w_down, "seq", split_axis=0, concat_axis=0, tiled=True)
    grads = attend_back(
        first, start_row, q, k, kt, v, attended_heads, lse, grad_heads, tables
    )
    grad_w_qkv, grad_w_down, grad_w_out, grad_inputs, outputs, gains = finish(
        tn(grads, normed_full).astype(BF16).reshape(3, -1, width),
        grad_w_down,
        tn(grad_branch, mix_in).astype(BF16),
        nn(grads, w_heads).astype(BF16),
        nt(hidden, w_down_cols).astype(BF16),
        x_low,
        grad_middle,
        middle,
        gain_attn,
        (grad_gain_mix, grad_gain_ffn, grad_gain_here),
        6,
    )
    return (
        outputs[None],
        grad_inputs[None],
        grad_w_qkv.astype(F32),
        grad_w_out,
        grad_w_up.astype(F32),
        grad_w_down,
        *gains,
    )


def pick_part(turned, me, n, part):
    chosen = turned[0]
    home = part * n + me
    for j in (1, 2):
        chosen = jnp.where(lax.rem(home, 3) == j, turned[j], chosen)
    return chosen


def give_part(blocks, me, n, j):
    chosen = blocks[0]
    for part in (1, 2):
        chosen = jnp.where(lax.rem(part * n + me, 3) == j, blocks[part], chosen)
    return chosen


def solution(mesh):
    in_specs = (
        P("batch", "seq", None),
        P("batch", None),
        P("seq", None),
        P("seq", None),
        P("seq", None),
        P("seq", None),
        P(),
        P(),
        P(),
        P(),
        P("batch", "seq", None),
    )
    out_specs = (
        P("batch", "seq", None),
        P("batch", "seq", None),
        P("seq", None),
        P("seq", None),
        P("seq", None),
        P("seq", None),
        P(),
        P(),
        P(),
        P(),
    )
    return jax.shard_map(body, mesh=mesh, in_specs=in_specs, out_specs=out_specs, check_vma=False)
```

```python
import functools
import math

import jax
import jax.numpy as jnp
from jax import lax
from jax.experimental import pallas as pl
from jax.experimental.pallas import tpu as pltpu
from jax.sharding import PartitionSpec as P

HEADS = 32
HEAD_DIM = 64
LENGTH = 2048
XBASE = 512
DOCS = 4
EPSILON = 1e-05
MASKED = -1e30
TILE = 256
VMEM_LIMIT = 60 * 1024 * 1024

MESH = pl.DeviceIdType.MESH
F32 = jnp.float32
BF16 = jnp.bfloat16
ANY = pl.BlockSpec(memory_space=pl.ANY)
INSIDE = pl.BlockSpec(memory_space=pltpu.VMEM)


def nn(a, b):
    return lax.dot_general(a, b, (((1,), (0,)), ((), ())), preferred_element_type=F32)


def nt(a, b):
    return lax.dot_general(a, b, (((1,), (1,)), ((), ())), preferred_element_type=F32)


def tn(a, b):
    return lax.dot_general(a, b, (((0,), (0,)), ((), ())), preferred_element_type=F32)


def norm_parts(values):
    average = jnp.mean(values, axis=-1, keepdims=True)
    centered = values - average
    spread = jnp.mean(centered * centered, axis=-1, keepdims=True)
    scale = lax.rsqrt(spread + EPSILON)
    return centered * scale, scale


def norm_back(grad, normal, scale, gain):
    part = grad * gain
    inner = (
        part
        - jnp.mean(part, axis=-1, keepdims=True)
        - normal * jnp.mean(part * normal, axis=-1, keepdims=True)
    )
    return scale * inner, jnp.sum(grad * normal, axis=0)


def places():
    me = lax.axis_index("seq")
    core = lax.rem(me, 2)
    along_x = lax.rem(me // 2, 2)
    along_y = me // 4
    twin = 1 - 2 * core
    near_x = me + 2 - 4 * along_x
    near_y = me + 4 - 8 * along_y
    across = near_x + 4 - 8 * along_y
    return me, twin, near_x, near_y, across


def remote(src, dst, send_sem, recv_sem, partner):
    return pltpu.make_async_remote_copy(
        src_ref=src,
        dst_ref=dst,
        send_sem=send_sem,
        recv_sem=recv_sem,
        device_id={"seq": partner},
        device_id_type=MESH,
    )


def meet(partners):
    barrier = pltpu.get_barrier_semaphore()
    for partner in partners:
        pl.semaphore_signal(
            barrier, inc=1, device_id={"seq": partner}, device_id_type=MESH
        )
    pl.semaphore_wait(barrier, len(partners))


def gather_copies(x_ref, o_ref, send_sem, recv_sem):
    me, twin, near_x, near_y, across = places()
    half = x_ref.shape[0] // 2
    low, high = pl.ds(0, half), pl.ds(half, half)

    def copy(k, src, dst, partner):
        return remote(src, dst, send_sem.at[k], recv_sem.at[k], partner)

    def relay(k, owner, rows, partner):
        place = o_ref.at[owner, rows]
        return copy(k, place, place, partner)

    return [
        copy(0, x_ref.at[low], o_ref.at[me, low], near_x),
        copy(1, x_ref.at[high], o_ref.at[me, high], near_y),
        copy(2, x_ref.at[high], o_ref.at[me, high], near_x),
        copy(3, x_ref.at[low], o_ref.at[me, low], near_y),
        copy(4, x_ref, o_ref.at[me], me + twin),
        relay(5, near_x, low, near_y),
        relay(6, near_y, high, near_x),
        relay(7, near_x, low, me + twin),
        relay(8, near_y, high, me + twin),
        relay(9, near_x, high, me + twin),
        relay(10, near_y, low, me + twin),
        relay(11, across, low, me + twin),
        relay(12, across, high, me + twin),
    ]


def gather_run(sends, *between):
    between = (*between, *([None] * 3))[:3]

    def pause(i):
        if between[i] is not None:
            between[i]()

    sends[0].wait_recv()
    sends[5].start()
    sends[7].start()
    sends[1].wait_recv()
    sends[6].start()
    sends[8].start()
    pause(0)
    sends[2].wait_recv()
    sends[9].start()
    sends[3].wait_recv()
    sends[10].start()
    pause(1)
    sends[5].wait_recv()
    sends[11].start()
    sends[6].wait_recv()
    sends[12].start()
    pause(2)
    for k in (4, 7, 8, 9, 10, 11, 12):
        sends[k].wait_recv()
    for send in sends:
        send.wait_send()


def meet_all(n, depth):
    me = lax.axis_index("seq")
    z = lax.axis_index("batch")
    barrier = pltpu.get_barrier_semaphore()
    for k in range(1, n):
        pl.semaphore_signal(
            barrier, inc=1, device_id={"seq": lax.rem(me + k, n)}, device_id_type=MESH
        )
    for k in range(1, depth):
        pl.semaphore_signal(
            barrier,
            inc=1,
            device_id={"batch": lax.rem(z + k, depth)},
            device_id_type=MESH,
        )
    pl.semaphore_wait(barrier, n + depth - 2)


def line_remote(src, dst, send_sem, recv_sem, partner):
    return pltpu.make_async_remote_copy(
        src_ref=src,
        dst_ref=dst,
        send_sem=send_sem,
        recv_sem=recv_sem,
        device_id={"batch": partner},
        device_id_type=MESH,
    )


class Line:
    def __init__(self, depth, source, target, send_sem, recv_sem):
        self.depth, self.source, self.target = depth, source, target
        self.send_sem, self.recv_sem = send_sem, recv_sem
        self.z = lax.axis_index("batch")

    def message(self, side, k):
        sign = 2 * side - 1
        owner = self.z - sign * k
        return line_remote(
            self.source(owner, k),
            self.target(owner),
            self.send_sem.at[side, k],
            self.recv_sem.at[side, k],
            self.z + sign,
        )

    def sends(self, side, k):
        sign = 2 * side - 1
        owner, target = self.z - sign * k, self.z + sign
        inside = (owner >= 0) & (owner < self.depth)
        return inside & (target >= 0) & (target < self.depth)

    def land(self, k):
        for side in (0, 1):
            sign = 2 * side - 1
            owner = self.z - sign * (k + 1)

            @pl.when((owner >= 0) & (owner < self.depth))
            def _():
                place = self.target(owner)
                line_remote(
                    place,
                    place,
                    self.send_sem.at[side, k],
                    self.recv_sem.at[side, k],
                    self.z - sign,
                ).wait_recv()

    def start(self, k):
        for side in (0, 1):

            @pl.when(self.sends(side, k))
            def _():
                self.message(side, k).start()

    def sent(self, k):
        for side in (0, 1):

            @pl.when(self.sends(side, k))
            def _():
                self.message(side, k).wait_send()


def lane_tables(place):
    half = HEAD_DIM // 2
    lane = lax.broadcasted_iota(jnp.int32, (1, 128), 1)
    channel = lax.rem(lane, half).astype(F32)
    inverse = jnp.exp(channel * (-math.log(10000.0) / half))
    zeta = (channel * (2.0 / HEAD_DIM) + 0.4) / 1.4
    sign = jnp.where(lax.rem(lane, HEAD_DIM) < half, -1.0, 1.0)
    angle = place * inverse
    growth = jnp.exp((place - 0.5 * LENGTH) * (1.0 / XBASE) * jnp.log(zeta))
    shrink = 1.0 / growth
    cosine = jnp.cos(angle)
    sine = jnp.sin(angle) * sign
    return cosine * growth, sine * growth, cosine * shrink, sine * shrink


def start_kernel(
    n, depth, x_ref, w_ref, wd_ref, pos_ref,
    o_ref, wt_ref, wc_ref, cq_ref, sq_ref, ck_ref, sk_ref,
    keep_w, keep_c, local_sem, send_sem, recv_sem, hop_send, hop_recv, col_send, col_recv,
    line_send, line_recv, w_send, w_recv,
):
    z = lax.axis_index("batch")
    rows_z = wc_ref.shape[2]
    cols = wc_ref.shape[3]
    me, twin, near_x, near_y, _ = places()
    own = pltpu.make_async_copy(x_ref, o_ref.at[me], local_sem.at[0])
    own.start()
    wd_rows = pl.ds(pl.multiple_of(z * rows_z, rows_z), rows_z)

    def column(k):
        return wd_ref.at[wd_rows, pl.ds(pl.multiple_of(k * cols, cols), cols)]

    load_column = pltpu.make_async_copy(column(me), keep_c, local_sem.at[4])
    own_column = pltpu.make_async_copy(keep_c, wc_ref.at[me, z], local_sem.at[5])
    load_column.start()
    meet_all(n, depth)
    load_column.wait()
    own_column.start()
    w_rows = pl.ds(
        pl.multiple_of(z * wt_ref.shape[2], wt_ref.shape[2]), wt_ref.shape[2]
    )

    def hop(j, part, target):
        return remote(
            w_ref.at[j, w_rows], wt_ref.at[part, z], hop_send.at[j], hop_recv.at[part], target
        )

    def load(j):
        return pltpu.make_async_copy(w_ref.at[j, w_rows], keep_w, local_sem.at[6])

    def here(j, part):
        return pltpu.make_async_copy(keep_w, wt_ref.at[part, z], local_sem.at[1 + j])

    for j in range(3):
        block = 3 * me + j
        target = lax.rem(block, n)
        for part in range(3):
            inside = block // n == part

            @pl.when(inside & (target != me))
            def _():
                hop(j, part, target).start()

            @pl.when(inside & (target == me))
            def _():
                load(j).start()
                load(j).wait()
                here(j, part).start()

    turns = [
        remote(
            column(lax.rem(me + k, n)),
            wc_ref.at[me, z],
            col_send.at[k],
            col_recv.at[k],
            lax.rem(me + k, n),
        )
        for k in range(1, n)
    ]
    for turn in turns:
        turn.start()
    sends = gather_copies(x_ref, o_ref, send_sem, recv_sem)
    for k in range(5):
        sends[k].start()

    line = Line(
        depth,
        lambda owner, k: wc_ref.at[:, owner],
        lambda owner: wc_ref.at[:, owner],
        line_send,
        line_recv,
    )

    line_w = Line(
        depth,
        lambda owner, k: wt_ref.at[:, owner],
        lambda owner: wt_ref.at[:, owner],
        w_send,
        w_recv,
    )
    for j in range(3):
        block = 3 * me + j
        target = lax.rem(block, n)
        for part in range(3):

            @pl.when((block // n == part) & (target == me))
            def _():
                here(j, part).wait()

    for part in range(3):
        source = (part * n + me) // 3

        @pl.when(source != me)
        def _():
            hop(0, part, source).wait_recv()

    line_w.start(0)

    @pl.loop(0, pos_ref.shape[0])
    def _(r):
        at = pl.ds(pl.multiple_of(r * 128, 128), 128)
        places_here = jnp.broadcast_to(pos_ref[pl.ds(r, 1), :], (128, 128)).T
        tables = lane_tables(places_here)
        for ref, table in zip((cq_ref, sq_ref, ck_ref, sk_ref), tables, strict=True):
            ref[at] = table

    own_column.wait()
    for turn in turns:
        turn.wait_recv()

    def hop_one():
        line_w.land(0)
        line_w.start(1)

    def hop_two():
        for k in range(2, depth - 1):
            line_w.land(k - 1)
            line_w.start(k)
        line.start(0)

    gather_run(sends, hop_one, hop_two)
    line.land(0)
    line.start(1)
    line_w.land(depth - 2)
    for k in range(depth - 1):
        line_w.sent(k)
    line.land(1)
    line.sent(0)
    line.sent(1)
    for turn in turns:
        turn.wait_send()
    for j in range(3):
        block = 3 * me + j
        target = lax.rem(block, n)
        for part in range(3):

            @pl.when((block // n == part) & (target != me))
            def _():
                hop(j, part, target).wait_send()

    own.wait()


def start_exchange(block, w_qkv, w_down, positions, collective_id):
    n, depth = lax.axis_size("seq"), lax.axis_size("batch")
    rows, width = block.shape
    piece = w_qkv.shape[0] // 3
    w = w_qkv.reshape(3, piece, width)
    if n != 8:
        me = lax.axis_index("seq")
        turned = [
            lax.ppermute(w[j], "seq", [(d, (3 * d + j) % n) for d in range(n)])
            for j in range(3)
        ]
        parts = [pick_part(turned, me, n, part) for part in range(3)]
        place = jnp.broadcast_to(positions[:, None], (positions.shape[0], 128))
        return (
            lax.all_gather(block, "seq", axis=0, tiled=True),
            jnp.concatenate(parts, axis=0),
            lax.all_to_all(w_down, "seq", split_axis=1, concat_axis=0, tiled=True),
            lane_tables(place),
        )
    rows_z, cols = w_down.shape[0] // depth, w_down.shape[1] // n
    inside = pl.BlockSpec(memory_space=pltpu.VMEM)
    table = jax.ShapeDtypeStruct((n * rows, 128), F32)
    gathered, turned, columns, *tables = pl.pallas_call(
        functools.partial(start_kernel, n, depth),
        out_shape=(
            jax.ShapeDtypeStruct((n, rows, width), block.dtype),
            jax.ShapeDtypeStruct((3, depth, piece // depth, width), w.dtype),
            jax.ShapeDtypeStruct((n, depth, rows_z, cols), w_down.dtype),
            *([table] * 4),
        ),
        in_specs=[INSIDE, ANY, ANY, INSIDE],
        out_specs=(ANY, ANY, ANY, *([INSIDE] * 4)),
        scratch_shapes=[
            pltpu.VMEM((piece // depth, width), BF16),
            pltpu.VMEM((rows_z, cols), BF16),
            pltpu.SemaphoreType.DMA((7,)),
            pltpu.SemaphoreType.DMA((13,)),
            pltpu.SemaphoreType.DMA((13,)),
            pltpu.SemaphoreType.DMA((3,)),
            pltpu.SemaphoreType.DMA((3,)),
            pltpu.SemaphoreType.DMA((n,)),
            pltpu.SemaphoreType.DMA((n,)),
            pltpu.SemaphoreType.DMA((2, depth)),
            pltpu.SemaphoreType.DMA((2, depth)),
            pltpu.SemaphoreType.DMA((2, depth)),
            pltpu.SemaphoreType.DMA((2, depth)),
        ],
        compiler_params=pltpu.CompilerParams(
            collective_id=collective_id, has_side_effects=True, vmem_limit_bytes=VMEM_LIMIT
        ),
        name="start_exchange",
    )(block, w, w_down, positions.reshape(-1, 128))
    return (
        gathered.reshape(n * rows, width),
        turned.reshape(3 * piece, width),
        columns,
        tables,
    )


def scatter_kernel(
    p_ref, o_ref, own, twin_in, held, local_sem, send_sem, recv_sem
):
    me, twin, near_x, near_y, across = places()
    rows = p_ref.shape[1]
    half = rows // 2
    low, high = pl.ds(0, half), pl.ds(half, half)
    mine = (across, near_x, near_y, me)

    loads = [
        pltpu.make_async_copy(p_ref.at[block], own.at[i], local_sem.at[i])
        for i, block in enumerate(mine)
    ]
    for load in loads:
        load.start()
    meet((me + twin, near_x, near_y))

    def copy(k, src, dst, partner):
        return remote(src, dst, send_sem.at[k], recv_sem.at[k], partner)

    twins = [
        copy(i, p_ref.at[block + twin], twin_in.at[i], me + twin)
        for i, block in enumerate(mine)
    ]
    for send in twins:
        send.start()
    sends = [
        copy(4, own.at[0, low], held.at[0], near_x),
        copy(5, own.at[0, high], held.at[1], near_y),
        copy(6, own.at[1, low], held.at[2], near_x),
        copy(7, own.at[2, high], held.at[3], near_y),
        copy(8, own.at[1, high], held.at[4], near_x),
        copy(9, own.at[2, low], held.at[5], near_y),
    ]
    step = 32

    def add_twin(i):
        loads[i].wait()
        twins[i].wait_recv()

        @pl.loop(0, rows // step)
        def _(r):
            at = pl.ds(pl.multiple_of(r * step, step), step)
            own[i, at] = (
                own[i, at].astype(F32) + twin_in[i, at].astype(F32)
            ).astype(own.dtype)

    def add_held(i, base, slot):
        @pl.loop(0, half // step)
        def _(r):
            at = pl.ds(pl.multiple_of(r * step, step), step)
            to = pl.ds(pl.multiple_of(base + r * step, step), step)
            own[i, to] = (
                own[i, to].astype(F32) + held[slot, at].astype(F32)
            ).astype(own.dtype)

    add_twin(0)
    sends[0].start()
    sends[1].start()
    add_twin(1)
    sends[2].start()
    add_twin(2)
    sends[3].start()
    sends[1].wait_recv()
    add_held(1, half, 1)
    sends[4].start()
    sends[0].wait_recv()
    add_held(2, 0, 0)
    sends[5].start()
    loads[3].wait()
    twins[3].wait_recv()
    for k in (2, 3, 4, 5):
        sends[k].wait_recv()

    def final(base, first, second):
        @pl.loop(0, half // step)
        def _(r):
            at = pl.ds(pl.multiple_of(r * step, step), step)
            to = pl.ds(pl.multiple_of(base + r * step, step), step)
            o_ref[to] = (
                own[3, to].astype(F32)
                + twin_in[3, to].astype(F32)
                + held[first, at].astype(F32)
                + held[second, at].astype(F32)
            )

    final(0, 2, 5)
    final(half, 3, 4)
    for send in twins + sends:
        send.wait_send()


def scatter_seq(partial, collective_id):
    n = lax.axis_size("seq")
    rows, width = partial.shape[0] // n, partial.shape[1]
    if n != 8:
        return lax.psum_scatter(
            partial, "seq", scatter_dimension=0, tiled=True
        ).astype(F32)
    return pl.pallas_call(
        scatter_kernel,
        out_shape=jax.ShapeDtypeStruct((rows, width), F32),
        in_specs=[ANY],
        out_specs=pl.BlockSpec(memory_space=pltpu.VMEM),
        scratch_shapes=[
            pltpu.VMEM((4, rows, width), BF16),
            pltpu.VMEM((4, rows, width), BF16),
            pltpu.VMEM((6, rows // 2, width), BF16),
            pltpu.SemaphoreType.DMA((4,)),
            pltpu.SemaphoreType.DMA((10,)),
            pltpu.SemaphoreType.DMA((10,)),
        ],
        compiler_params=pltpu.CompilerParams(
            collective_id=collective_id,
            has_side_effects=True,
            vmem_limit_bytes=VMEM_LIMIT,
        ),
        name="scatter_seq",
    )(partial.reshape(n, rows, width))


def heads_to_tokens_kernel(
    n, depth, x_ref, near_ref, o_ref, extra_ref, keep, local_sem, send_sem, recv_sem, line_send, line_recv
):
    me = lax.axis_index("seq")
    z = lax.axis_index("batch")
    rows = o_ref.shape[0]
    cols = x_ref.shape[1]
    load = pltpu.make_async_copy(
        x_ref.at[pl.ds(pl.multiple_of(me * rows, rows), rows)], keep, local_sem.at[0]
    )
    target = o_ref.at[:, pl.ds(pl.multiple_of(me * cols, cols), cols)]
    own = pltpu.make_async_copy(keep, target, local_sem.at[1])
    load.start()
    meet_all(n, depth)
    copies = [
        remote(
            x_ref.at[pl.ds(pl.multiple_of(lax.rem(me + k, n) * rows, rows), rows)],
            target,
            send_sem.at[k],
            recv_sem.at[k],
            lax.rem(me + k, n),
        )
        for k in range(1, n)
    ]
    for copy in copies:
        copy.start()

    def last_hop(side):
        owner, end = (depth - 1, 0) if side == 0 else (0, depth - 1)
        return line_remote(
            near_ref.at[:, owner],
            extra_ref,
            line_send.at[side],
            line_recv.at[side],
            end,
        )

    for side, sender in ((0, 1), (1, depth - 2)):

        @pl.when(z == sender)
        def _():
            last_hop(side).start()

    load.wait()
    own.start()
    for copy in copies:
        copy.wait()
    own.wait()
    for side, sender, end in ((0, 1, 0), (1, depth - 2, depth - 1)):

        @pl.when(z == sender)
        def _():
            last_hop(side).wait_send()

        @pl.when(z == end)
        def _():
            line_remote(
                extra_ref, extra_ref, line_send.at[side], line_recv.at[side], sender
            ).wait_recv()


def exchange(n, me, source, target, keep, local_sem, send_sem, recv_sem):
    load = pltpu.make_async_copy(source(me), keep, local_sem.at[0])
    own = pltpu.make_async_copy(keep, target, local_sem.at[1])
    load.start()
    barrier = pltpu.get_barrier_semaphore()
    for k in range(1, n):
        pl.semaphore_signal(
            barrier,
            inc=1,
            device_id={"seq": lax.rem(me + k, n)},
            device_id_type=MESH,
        )
    pl.semaphore_wait(barrier, n - 1)
    copies = []
    for k in range(1, n):
        partner = lax.rem(me + k, n)
        copies.append(
            pltpu.make_async_remote_copy(
                src_ref=source(partner),
                dst_ref=target,
                send_sem=send_sem.at[k],
                recv_sem=recv_sem.at[k],
                device_id={"seq": partner},
                device_id_type=MESH,
            )
        )
        copies[-1].start()
    load.wait()
    own.start()
    for copy in copies:
        copy.wait()
    own.wait()


def heads_to_tokens(heads, near, collective_id):
    n, depth = lax.axis_size("seq"), lax.axis_size("batch")
    total, cols = heads.shape
    rows = total // n
    if n != 8 or depth != 4:
        tokens = lax.all_to_all(heads, "seq", split_axis=0, concat_axis=1, tiled=True)
        return tokens, None
    return pl.pallas_call(
        functools.partial(heads_to_tokens_kernel, n, depth),
        out_shape=(
            jax.ShapeDtypeStruct((rows, n * cols), heads.dtype),
            jax.ShapeDtypeStruct((n, *near.shape[2:]), near.dtype),
        ),
        in_specs=[ANY, ANY],
        out_specs=(ANY, ANY),
        scratch_shapes=[
            pltpu.VMEM((rows, cols), heads.dtype),
            pltpu.SemaphoreType.DMA((2,)),
            pltpu.SemaphoreType.DMA((n,)),
            pltpu.SemaphoreType.DMA((n,)),
            pltpu.SemaphoreType.DMA((2,)),
            pltpu.SemaphoreType.DMA((2,)),
        ],
        compiler_params=pltpu.CompilerParams(
            collective_id=collective_id, has_side_effects=True, vmem_limit_bytes=VMEM_LIMIT
        ),
        name="heads_to_tokens",
    )(heads, near)


def tokens_to_heads_kernel(n, x_ref, o_ref, keep, local_sem, send_sem, recv_sem):
    me = lax.axis_index("seq")
    rows = x_ref.shape[0]
    cols = o_ref.shape[1]
    exchange(
        n,
        me,
        lambda k: x_ref.at[:, pl.ds(pl.multiple_of(k * cols, cols), cols)],
        o_ref.at[pl.ds(pl.multiple_of(me * rows, rows), rows)],
        keep,
        local_sem,
        send_sem,
        recv_sem,
    )


def tokens_to_heads(tokens, collective_id):
    n = lax.axis_size("seq")
    rows, total = tokens.shape
    return pl.pallas_call(
        functools.partial(tokens_to_heads_kernel, n),
        out_shape=jax.ShapeDtypeStruct((rows * n, total // n), tokens.dtype),
        in_specs=[ANY],
        out_specs=ANY,
        scratch_shapes=[
            pltpu.VMEM((rows, total // n), tokens.dtype),
            pltpu.SemaphoreType.DMA((2,)),
            pltpu.SemaphoreType.DMA((n,)),
            pltpu.SemaphoreType.DMA((n,)),
        ],
        compiler_params=pltpu.CompilerParams(
            collective_id=collective_id, has_side_effects=True, vmem_limit_bytes=VMEM_LIMIT
        ),
        name="tokens_to_heads",
    )(tokens)


def swap_halves(values):
    width = values.shape[-1]
    half = HEAD_DIM // 2
    lane = lax.broadcasted_iota(jnp.int32, values.shape, 1)
    ahead = pltpu.roll(values, width - half, 1)
    behind = pltpu.roll(values, half, 1)
    return jnp.where(lane % HEAD_DIM < half, ahead, behind)


def spread_lanes(table, width):
    return jnp.concatenate([table] * (width // table.shape[-1]), axis=-1)


def qkv_kernel(
    x_ref, w_ref, cq_ref, sq_ref, ck_ref, sk_ref,
    q_ref, k_ref, v_ref, kt_ref, vt_ref,
):
    x = x_ref[...]
    width = q_ref.shape[1]
    query = nt(x, w_ref[0:width])
    query = query * spread_lanes(cq_ref[...], width) + swap_halves(
        query
    ) * spread_lanes(sq_ref[...], width)
    q_ref[...] = query.astype(BF16) * (HEAD_DIM**-0.5)
    keys = nt(x, w_ref[width : 2 * width])
    keys = keys * spread_lanes(ck_ref[...], width) + swap_halves(
        keys
    ) * spread_lanes(sk_ref[...], width)
    k_ref[...] = keys.astype(BF16)
    kt_ref[...] = keys.T.astype(BF16)
    values = nt(x, w_ref[2 * width :])
    v_ref[...] = values.astype(BF16)
    vt_ref[...] = values.T.astype(BF16)


def project_qkv(x, w, tables):
    length, width = x.shape
    cols = w.shape[0] // 3
    steps = length // TILE
    weight = pl.BlockSpec((3 * cols, width), lambda i: (0, 0))
    table = pl.BlockSpec((TILE, tables[0].shape[1]), lambda i: (i, 0))
    row_out = pl.BlockSpec((TILE, cols), lambda i: (i, 0))
    col_out = pl.BlockSpec((cols, TILE), lambda i: (0, i))
    rows = jax.ShapeDtypeStruct((length, cols), BF16)
    columns = jax.ShapeDtypeStruct((cols, length), BF16)
    return pl.pallas_call(
        qkv_kernel,
        grid=(steps,),
        out_shape=(rows, rows, rows, columns, columns),
        in_specs=[pl.BlockSpec((TILE, width), lambda i: (i, 0))]
        + [weight]
        + [table] * 4,
        out_specs=(row_out, row_out, row_out, col_out, col_out),
        compiler_params=pltpu.CompilerParams(vmem_limit_bytes=VMEM_LIMIT),
        cost_estimate=pl.CostEstimate(
            flops=6 * length * width * cols,
            bytes_accessed=2 * length * width + 6 * width * cols + 10 * length * cols,
            transcendentals=0,
        ),
        name="project_qkv",
    )(x, w, *tables)


def pair_mask(start_row, i, j):
    key_place = j * TILE + lax.broadcasted_iota(jnp.int32, (TILE, TILE), 0)
    query_place = i * TILE + lax.broadcasted_iota(jnp.int32, (TILE, TILE), 1)
    return (key_place <= query_place) & (key_place >= start_row)


def head_rows(query, heads):
    lane = lax.broadcasted_iota(jnp.int32, query.shape, 1) // HEAD_DIM
    zero = jnp.zeros_like(query)
    return [jnp.where(lane == h, query, zero) for h in range(heads)]


def attend_kernel(
    heads, first_ref, start_ref, q_ref, k_ref, vt_ref, o_ref, lse_ref, peak, total, mixed
):
    i = pl.program_id(0)
    queries = head_rows(q_ref[...], heads)
    start_row = start_ref[...]

    def block(j, first):
        at = pl.ds(pl.multiple_of(j * TILE, TILE), TILE)
        keys = k_ref[at, :]
        mask = pair_mask(start_row, i, j)
        for h in range(heads):
            here = slice(h * HEAD_DIM, (h + 1) * HEAD_DIM)
            scores = jnp.where(mask, nt(keys, queries[h]), MASKED)
            if first:
                new_peak = jnp.max(scores, axis=0, keepdims=True)
                expo = jnp.exp(scores - new_peak)
                total[h : h + 1] = jnp.sum(expo, axis=0, keepdims=True)
                mixed[here] = nn(vt_ref[here, at], expo.astype(BF16))
            else:
                old_peak = peak[h : h + 1]
                new_peak = jnp.maximum(old_peak, jnp.max(scores, axis=0, keepdims=True))
                expo = jnp.exp(scores - new_peak)
                shrink = jnp.exp(old_peak - new_peak)
                total[h : h + 1] = total[h : h + 1] * shrink + jnp.sum(
                    expo, axis=0, keepdims=True
                )
                mixed[here] = mixed[here] * shrink + nn(
                    vt_ref[here, at], expo.astype(BF16)
                )
            peak[h : h + 1] = new_peak

    block(i, True)

    @pl.loop(0, i - first_ref[i])
    def _(t):
        block(i - 1 - t, False)

    for h in range(heads):
        here = slice(h * HEAD_DIM, (h + 1) * HEAD_DIM)
        mixed[here] = mixed[here] / total[h : h + 1]
    o_ref[...] = mixed[...].T.astype(BF16)
    lse_ref[0] = peak[...] + jnp.log(total[...])


def attend(first, start, q, k, vt):
    length, cols = q.shape
    heads = cols // HEAD_DIM
    steps = length // TILE
    row = pl.BlockSpec((TILE, cols), lambda i, *_: (i, 0))
    return pl.pallas_call(
        functools.partial(attend_kernel, heads),
        out_shape=(
            jax.ShapeDtypeStruct((length, cols), BF16),
            jax.ShapeDtypeStruct((steps, heads, TILE), F32),
        ),
        grid_spec=pltpu.PrefetchScalarGridSpec(
            num_scalar_prefetch=1,
            grid=(steps,),
            in_specs=[
                pl.BlockSpec((1, TILE), lambda i, *_: (0, i)),
                row,
                pl.BlockSpec((length, cols), lambda i, *_: (0, 0)),
                pl.BlockSpec((cols, length), lambda i, *_: (0, 0)),
            ],
            out_specs=(
                row,
                pl.BlockSpec((1, heads, TILE), lambda i, *_: (i, 0, 0)),
            ),
            scratch_shapes=[
                pltpu.VMEM((heads, TILE), F32),
                pltpu.VMEM((heads, TILE), F32),
                pltpu.VMEM((cols, TILE), F32),
            ],
        ),
        compiler_params=pltpu.CompilerParams(vmem_limit_bytes=VMEM_LIMIT),
        cost_estimate=pl.CostEstimate(
            flops=4 * length * 1024 * cols,
            bytes_accessed=8 * length * cols,
            transcendentals=length * 1024 * heads,
        ),
        name="attend",
    )(first, start, q, k, vt)


def attend_back_kernel(
    heads, first_ref, start_ref, q_ref, k_ref, kt_ref, v_ref, o_ref, lse_ref, do_ref,
    cq_ref, sq_ref, ck_ref, sk_ref, grad_ref, dqt, dk_sum, dv_sum,
):
    i = pl.program_id(0)
    steps = pl.num_programs(0)
    width = q_ref.shape[1]
    queries = head_rows(q_ref[...], heads)
    grads = head_rows(do_ref[...], heads)
    start_row = start_ref[...]
    product = (do_ref[...].astype(F32) * o_ref[...].astype(F32)).T
    inner = [
        jnp.sum(product[h * HEAD_DIM : (h + 1) * HEAD_DIM], axis=0, keepdims=True)
        for h in range(heads)
    ]

    def block(j, first):
        at = pl.ds(pl.multiple_of(j * TILE, TILE), TILE)
        keys = k_ref[at, :]
        values = v_ref[at, :]
        mask = pair_mask(start_row, i, j)
        key_term = None
        value_term = None
        for h in range(heads):
            here = slice(h * HEAD_DIM, (h + 1) * HEAD_DIM)
            scores = nt(keys, queries[h])
            weights = jnp.where(mask, jnp.exp(scores - lse_ref[0, h : h + 1]), 0.0)
            grad_weights = nt(values, grads[h])
            grad_scores = (weights * (grad_weights - inner[h])).astype(BF16)
            term = nn(weights.astype(BF16), grads[h])
            value_term = term if value_term is None else value_term + term
            term = nn(grad_scores, queries[h])
            key_term = term if key_term is None else key_term + term
            term = nn(kt_ref[here, at], grad_scores)
            if first:
                dqt[here] = term
            else:
                dqt[here] = dqt[here] + term
        if first:
            dk_sum[at] = key_term
            dv_sum[at] = value_term
        else:
            dk_sum[at] = dk_sum[at] + key_term
            dv_sum[at] = dv_sum[at] + value_term

    block(i, True)

    @pl.loop(0, i - first_ref[i])
    def _(t):
        block(i - 1 - t, False)

    def unturn(grad, cosine, sine):
        grad = grad.astype(BF16).astype(F32)
        cosine = spread_lanes(cosine, width)
        sine = spread_lanes(sine, width)
        return (grad * cosine - swap_halves(grad) * sine).astype(BF16)

    rows = pl.ds(pl.multiple_of(i * TILE, TILE), TILE)
    grad_ref[rows, 0:width] = unturn(
        dqt[...].T * (HEAD_DIM**-0.5), cq_ref[rows, :], sq_ref[rows, :]
    )

    @pl.when(i == steps - 1)
    def _():
        @pl.loop(0, steps)
        def _(j):
            at = pl.ds(pl.multiple_of(j * TILE, TILE), TILE)
            grad_ref[at, width : 2 * width] = unturn(
                dk_sum[at], ck_ref[at, :], sk_ref[at, :]
            )
            grad_ref[at, 2 * width :] = dv_sum[at].astype(BF16)


def attend_back(first, start, q, k, kt, v, o, lse, do, tables):
    length, cols = q.shape
    heads = cols // HEAD_DIM
    steps = length // TILE
    row = pl.BlockSpec((TILE, cols), lambda i, *_: (i, 0))
    whole = pl.BlockSpec((length, cols), lambda i, *_: (0, 0))
    table = pl.BlockSpec((length, tables[0].shape[1]), lambda i, *_: (0, 0))
    return pl.pallas_call(
        functools.partial(attend_back_kernel, heads),
        out_shape=jax.ShapeDtypeStruct((length, 3 * cols), BF16),
        grid_spec=pltpu.PrefetchScalarGridSpec(
            num_scalar_prefetch=1,
            grid=(steps,),
            in_specs=[
                pl.BlockSpec((1, TILE), lambda i, *_: (0, i)),
                row,
                whole,
                pl.BlockSpec((cols, length), lambda i, *_: (0, 0)),
                whole,
                row,
                pl.BlockSpec((1, heads, TILE), lambda i, *_: (i, 0, 0)),
                row,
            ]
            + [table] * 4,
            out_specs=pl.BlockSpec((length, 3 * cols), lambda i, *_: (0, 0)),
            scratch_shapes=[
                pltpu.VMEM((cols, TILE), F32),
                pltpu.VMEM((length, cols), F32),
                pltpu.VMEM((length, cols), F32),
            ],
        ),
        compiler_params=pltpu.CompilerParams(vmem_limit_bytes=VMEM_LIMIT),
        cost_estimate=pl.CostEstimate(
            flops=10 * length * 1024 * cols,
            bytes_accessed=16 * length * cols,
            transcendentals=length * 1024 * heads,
        ),
        name="attend_back",
    )(first, start, q, k, kt, v, o, lse, do, *tables)


def upper_kernel(
    x_ref, wu_ref, c_ref, wd_ref, gain_ref, act_ref, slope_ref, grad_ref, stat_ref
):
    upper = nt(x_ref[...], wu_ref[...])
    grad = nn(c_ref[...], wd_ref[...])
    below = 0.5 * (1.0 + lax.erf(upper * (0.5**0.5)))
    act = upper * below
    slope = below + upper * (jnp.exp(-0.5 * upper * upper) * ((2.0 * math.pi) ** -0.5))
    act_ref[...] = act
    slope_ref[...] = slope.astype(BF16)
    grad_ref[...] = grad
    part = grad * gain_ref[...]
    average = jnp.mean(act, axis=-1, keepdims=True)
    centered = act - average
    spread = jnp.sum(centered * centered, axis=-1, keepdims=True)
    part_sum = jnp.sum(part, axis=-1, keepdims=True)
    cross = jnp.sum(part * centered, axis=-1, keepdims=True)
    lane = lax.broadcasted_iota(jnp.int32, (x_ref.shape[0], 128), 1)
    columns = jnp.where(
        lane == 0,
        average,
        jnp.where(lane == 1, spread, jnp.where(lane == 2, part_sum, cross)),
    )
    stat_ref[...] = columns.T[:8]


def upper_pass(x, w_up, cot, w_down, gain):
    length, width = x.shape
    feats = w_up.shape[0]
    rows = TILE
    row = pl.BlockSpec((rows, width), lambda i: (i, 0))
    out = pl.BlockSpec((rows, feats), lambda i: (i, 0))
    return pl.pallas_call(
        upper_kernel,
        grid=(length // rows,),
        out_shape=(
            jax.ShapeDtypeStruct((length, feats), F32),
            jax.ShapeDtypeStruct((length, feats), BF16),
            jax.ShapeDtypeStruct((length, feats), F32),
            jax.ShapeDtypeStruct((8, length), F32),
        ),
        in_specs=[
            row,
            pl.BlockSpec((feats, width), lambda i: (0, 0)),
            row,
            pl.BlockSpec((width, feats), lambda i: (0, 0)),
            pl.BlockSpec((1, feats), lambda i: (0, 0)),
        ],
        out_specs=(out, out, out, pl.BlockSpec((8, rows), lambda i: (0, i))),
        compiler_params=pltpu.CompilerParams(vmem_limit_bytes=VMEM_LIMIT),
        cost_estimate=pl.CostEstimate(
            flops=4 * length * width * feats,
            bytes_accessed=8 * length * width + 8 * length * feats,
            transcendentals=2 * length * feats,
        ),
        name="upper_pass",
    )(x, w_up, cot, w_down, gain)


def hidden_kernel(act_ref, slope_ref, grad_ref, stat_ref, gain_ref, hid_ref, gu_ref, gg_ref):
    i = pl.program_id(0)
    stats = stat_ref[...].T
    average = stats[:, 0:1]
    scale = stats[:, 1:2]
    part_mean = stats[:, 2:3]
    cross_mean = stats[:, 3:4]
    gain = gain_ref[...]
    normal = (act_ref[...] - average) * scale
    grad = grad_ref[...]
    hid_ref[...] = (normal * gain).astype(BF16)
    back = scale * (grad * gain - part_mean - normal * cross_mean)
    gu_ref[...] = (slope_ref[...].astype(F32) * back).astype(BF16)
    term = jnp.sum(grad * normal, axis=0, keepdims=True)

    @pl.when(i == 0)
    def _():
        gg_ref[...] = term

    @pl.when(i > 0)
    def _():
        gg_ref[...] = gg_ref[...] + term


def hidden_pass(act, slope, grad, stats, gain):
    length, feats = act.shape
    out = pl.BlockSpec((TILE, feats), lambda i: (i, 0))
    one = pl.BlockSpec((1, feats), lambda i: (0, 0))
    return pl.pallas_call(
        hidden_kernel,
        grid=(length // TILE,),
        out_shape=(
            jax.ShapeDtypeStruct((length, feats), BF16),
            jax.ShapeDtypeStruct((length, feats), BF16),
            jax.ShapeDtypeStruct((1, feats), F32),
        ),
        in_specs=[out, out, out, pl.BlockSpec((8, TILE), lambda i: (0, i)), one],
        out_specs=(out, out, one),
        compiler_params=pltpu.CompilerParams(vmem_limit_bytes=VMEM_LIMIT),
        cost_estimate=pl.CostEstimate(
            flops=12 * length * feats,
            bytes_accessed=14 * length * feats,
            transcendentals=0,
        ),
        name="hidden_pass",
    )(act, slope, grad, stats, gain)


def ffn_kernel(
    n, depth, x_ref, wu_ref, cot_ref, near_ref, extra_ref, gain_ref,
    full_ref, wd_out_ref, hid_ref, gu_ref, gg_ref,
    rows_in, wd, cot_in, act, slope, grad, stat, held, results,
    local_sem, cot_sem, out_sem, full_sem, send_sem, recv_sem, stat_send, stat_recv,
):
    me, twin, near_x, near_y, across = places()
    z = lax.axis_index("batch")
    rows = x_ref.shape[0]
    feats = wu_ref.shape[0]
    quarter = extra_ref.shape[1]

    def cut(i, size=rows):
        return pl.ds(pl.multiple_of(i * size, size), size)

    own = pltpu.make_async_copy(x_ref, rows_in.at[me], local_sem.at[0])
    own.start()
    load_wd = pltpu.make_async_copy(near_ref, wd, local_sem.at[1])
    load_wd.start()

    def load_cot(i, slot):
        return pltpu.make_async_copy(
            cot_ref.at[cut(i)], cot_in.at[slot], cot_sem.at[slot]
        )

    load_cot(0, 0).start()
    meet([lax.rem(me + k, n) for k in range(1, n)])
    sends = gather_copies(x_ref, rows_in, send_sem, recv_sem)
    for k in range(5):
        sends[k].start()

    load_wd.wait()
    for end, owner in ((0, depth - 1), (depth - 1, 0)):

        @pl.when(z == end)
        def _():
            fills = [
                pltpu.make_async_copy(
                    extra_ref.at[d],
                    wd.at[pl.ds((d * depth + owner) * quarter, quarter)],
                    full_sem.at[d],
                )
                for d in range(n)
            ]
            for fill in fills:
                fill.start()
            for fill in fills:
                fill.wait()

    keep_wd = pltpu.make_async_copy(wd, wd_out_ref, local_sem.at[2])
    keep_wd.start()

    def incoming(first, last):
        @pl.loop(first, last)
        def _(i):
            slot = lax.rem(i, 2)

            @pl.when(i + 1 < n)
            def _():
                load_cot(i + 1, 1 - slot).start()

            load_cot(i, slot).wait()
            grad[cut(i)] = nn(cot_in[slot], wd[...])

    incoming(0, n - 2)
    sends[0].wait_recv()
    sends[5].start()
    sends[7].start()
    sends[1].wait_recv()
    sends[6].start()
    sends[8].start()
    incoming(n - 2, n)
    own.wait()

    def keep(b):
        return pltpu.make_async_copy(rows_in.at[b], full_ref.at[b], full_sem.at[b])

    @pl.loop(0, n)
    def _(i):
        @pl.when(i == 1)
        def _():
            sends[4].wait_recv()

        @pl.when(i == 2)
        def _():
            sends[2].wait_recv()
            sends[9].start()
            sends[3].wait_recv()
            sends[10].start()

        @pl.when(i == 4)
        def _():
            sends[7].wait_recv()
            sends[9].wait_recv()

        @pl.when(i == 5)
        def _():
            sends[8].wait_recv()
            sends[10].wait_recv()
            sends[5].wait_recv()
            sends[11].start()
            sends[6].wait_recv()
            sends[12].start()

        @pl.when(i == 7)
        def _():
            sends[11].wait_recv()
            sends[12].wait_recv()

        other = jnp.where((i == 1) | (i == 4) | (i == 5) | (i == 7), twin, 0)
        place = jnp.where(i < 2, me, jnp.where(i >= 6, across, jnp.where(lax.rem(i, 2) == 0, near_x, near_y)))
        b = place + other
        keep(b).start()
        at = cut(b)
        upper = nt(rows_in[b], wu_ref[...])
        below = 0.5 * (1.0 + lax.erf(upper * (0.5**0.5)))
        value = upper * below
        act[at] = value
        slope[at] = (
            below + upper * (jnp.exp(-0.5 * upper * upper) * ((2.0 * math.pi) ** -0.5))
        ).astype(BF16)
        part = grad[at] * gain_ref[...]
        average = jnp.mean(value, axis=-1, keepdims=True)
        centered = value - average
        spread = jnp.sum(centered * centered, axis=-1, keepdims=True)
        part_sum = jnp.sum(part, axis=-1, keepdims=True)
        cross = jnp.sum(part * centered, axis=-1, keepdims=True)
        lane = lax.broadcasted_iota(jnp.int32, (rows, 128), 1)
        columns = jnp.where(
            lane == 0,
            average,
            jnp.where(lane == 1, spread, jnp.where(lane == 2, part_sum, cross)),
        )
        stat[:, at] = columns.T[:8]

    held[me] = stat[...]
    rounds = [
        remote(
            stat, held.at[me], stat_send.at[k], stat_recv.at[k], lax.rem(me + k, n)
        )
        for k in range(1, n)
    ]
    for send in rounds:
        send.start()
    for send in rounds:
        send.wait()
    join_rows(n, feats, held, stat)

    def store(i, slot):
        return [
            pltpu.make_async_copy(
                results.at[slot, j], ref.at[cut(i)], out_sem.at[slot, j]
            )
            for j, ref in enumerate((hid_ref, gu_ref))
        ]

    gg_ref[...] = jnp.zeros_like(gg_ref)

    @pl.loop(0, n)
    def _(i):
        slot = lax.rem(i, 2)

        @pl.when(i >= 2)
        def _():
            for copy in store(i - 2, slot):
                copy.wait()

        at = cut(i)
        stats = stat[:, at].T
        gain = gain_ref[...]
        scale = stats[:, 1:2]
        normal = (act[at] - stats[:, 0:1]) * scale
        coming = grad[at]
        results[slot, 0] = (normal * gain).astype(BF16)
        back = scale * (coming * gain - stats[:, 2:3] - normal * stats[:, 3:4])
        results[slot, 1] = (slope[at].astype(F32) * back).astype(BF16)
        gg_ref[...] = gg_ref[...] + jnp.sum(coming * normal, axis=0, keepdims=True)
        for copy in store(i, slot):
            copy.start()

    for i in (n - 2, n - 1):
        for copy in store(i, i % 2):
            copy.wait()
    for b in range(n):
        keep(b).wait()
    keep_wd.wait()
    for send in sends:
        send.wait_send()


def ffn_pass(ffn_in, w_up, cot, near, extra, gain, collective_id):
    n, depth = lax.axis_size("seq"), lax.axis_size("batch")
    rows, width = ffn_in.shape
    feats = w_up.shape[0]
    if n != 8 or depth != 4:
        full = lax.all_gather(ffn_in, "seq", axis=0, tiled=True)
        act, slope, grad, stat = upper_pass(full, w_up, cot, near, gain)
        stats = join_stats(stat, feats, collective_id)
        return (full, near, *hidden_pass(act, slope, grad, stats, gain))
    length = n * rows
    dma = pltpu.SemaphoreType.DMA
    low = jax.ShapeDtypeStruct((length, feats), BF16)
    full, w_down, hidden, grad_upper, gain_grad = pl.pallas_call(
        functools.partial(ffn_kernel, n, depth),
        out_shape=(
            jax.ShapeDtypeStruct((n, rows, width), BF16),
            jax.ShapeDtypeStruct((width, feats), BF16),
            low,
            low,
            jax.ShapeDtypeStruct((1, feats), F32),
        ),
        in_specs=[INSIDE, INSIDE, ANY, ANY, ANY, INSIDE],
        out_specs=(ANY, ANY, ANY, ANY, INSIDE),
        scratch_shapes=[
            pltpu.VMEM((n, rows, width), BF16),
            pltpu.VMEM((width, feats), BF16),
            pltpu.VMEM((2, rows, width), BF16),
            pltpu.VMEM((length, feats), F32),
            pltpu.VMEM((length, feats), BF16),
            pltpu.VMEM((length, feats), F32),
            pltpu.VMEM((8, length), F32),
            pltpu.VMEM((n, 8, length), F32),
            pltpu.VMEM((2, 2, rows, feats), BF16),
            dma((3,)),
            dma((2,)),
            dma((2, 2)),
            dma((n,)),
            dma((13,)),
            dma((13,)),
            dma((n,)),
            dma((n,)),
        ],
        compiler_params=pltpu.CompilerParams(
            collective_id=collective_id, has_side_effects=True, vmem_limit_bytes=VMEM_LIMIT
        ),
        name="ffn_pass",
    )(ffn_in, w_up, cot, near.reshape(width, feats), extra, gain)
    return full.reshape(length, width), w_down, hidden, grad_upper, gain_grad


def join_rows(n, feats, held, o_ref):
    average = held[0, 0:1]
    for d in range(1, n):
        average = average + held[d, 0:1]
    average = average * (1.0 / n)
    spread = jnp.zeros_like(average)
    part = jnp.zeros_like(average)
    cross = jnp.zeros_like(average)
    for d in range(n):
        shift = held[d, 0:1] - average
        spread = spread + held[d, 1:2] + feats * (shift * shift)
        part = part + held[d, 2:3]
        cross = cross + held[d, 3:4] + shift * held[d, 2:3]
    whole = 1.0 / (n * feats)
    scale = lax.rsqrt(spread * whole + EPSILON)
    o_ref[0:1] = average
    o_ref[1:2] = scale
    o_ref[2:3] = part * whole
    o_ref[3:4] = cross * scale * whole
    o_ref[4:8] = jnp.zeros((4, average.shape[1]), F32)


def stat_kernel(n, feats, x_ref, o_ref, held, send_sem, recv_sem):
    me = lax.axis_index("seq")
    held[me] = x_ref[...]
    meet([lax.rem(me + k, n) for k in range(1, n)])
    copies = [
        remote(x_ref, held.at[me], send_sem.at[k], recv_sem.at[k], lax.rem(me + k, n))
        for k in range(1, n)
    ]
    for copy in copies:
        copy.start()
    for copy in copies:
        copy.wait()
    join_rows(n, feats, held, o_ref)


def join_stats(stat, feats, collective_id):
    n = lax.axis_size("seq")
    inside = pl.BlockSpec(memory_space=pltpu.VMEM)
    return pl.pallas_call(
        functools.partial(stat_kernel, n, feats),
        out_shape=jax.ShapeDtypeStruct(stat.shape, F32),
        in_specs=[inside],
        out_specs=inside,
        scratch_shapes=[
            pltpu.VMEM((n, *stat.shape), F32),
            pltpu.SemaphoreType.DMA((n,)),
            pltpu.SemaphoreType.DMA((n,)),
        ],
        compiler_params=pltpu.CompilerParams(
            collective_id=collective_id, has_side_effects=True, vmem_limit_bytes=VMEM_LIMIT
        ),
        name="join_stats",
    )(stat)


STEP = 32


def mix_kernel(att_ref, x_ref, w_ref, gm_ref, gf_ref, mix_ref, mid_ref, ffn_ref):
    j = pl.program_id(0)
    rows = att_ref.shape[0]
    cols = w_ref.shape[0]

    @pl.when(j == 0)
    def _():
        @pl.loop(0, rows // STEP)
        def _(r):
            at = pl.ds(pl.multiple_of(r * STEP, STEP), STEP)
            normal, _ = norm_parts(att_ref[at].astype(F32))
            mix_ref[at] = (normal * gm_ref[...]).astype(BF16)

    here = pl.ds(pl.multiple_of(j * cols, cols), cols)
    mid_ref[:, here] = x_ref[:, here].astype(F32) + nt(mix_ref[...], w_ref[...])

    @pl.when(j == pl.num_programs(0) - 1)
    def _():
        @pl.loop(0, rows // STEP)
        def _(r):
            at = pl.ds(pl.multiple_of(r * STEP, STEP), STEP)
            normal, _ = norm_parts(mid_ref[at])
            ffn_ref[at] = (normal * gf_ref[...]).astype(BF16)


def mix_pass(attended, x, w_out, gain_mix, gain_ffn):
    rows, width = x.shape
    cols = TILE
    n = width // cols
    whole = pl.BlockSpec((rows, width), lambda j: (0, 0))
    gain = pl.BlockSpec((1, width), lambda j: (0, 0))
    low = jax.ShapeDtypeStruct((rows, width), BF16)
    return pl.pallas_call(
        mix_kernel,
        grid=(n,),
        out_shape=(low, jax.ShapeDtypeStruct((rows, width), F32), low),
        in_specs=[
            whole,
            whole,
            pl.BlockSpec((cols, width), lambda j: (j, 0)),
            gain,
            gain,
        ],
        out_specs=(whole, whole, whole),
        compiler_params=pltpu.CompilerParams(vmem_limit_bytes=VMEM_LIMIT),
        cost_estimate=pl.CostEstimate(
            flops=2 * rows * width * width,
            bytes_accessed=2 * width * width + 12 * rows * width,
            transcendentals=0,
        ),
        name="mix_pass",
    )(attended, x, w_out, gain_mix[None], gain_ffn[None])


def branch_kernel(
    g_ref, mid_ref, cot_ref, att_ref, w_ref, gm_ref, gf_ref,
    gmid_ref, gbr_ref, gatt_ref, ggf_ref, ggm_ref, total,
):
    j = pl.program_id(0)
    rows = att_ref.shape[0]
    cols = w_ref.shape[0]

    @pl.when(j == 0)
    def _():
        ggf_ref[...] = jnp.zeros_like(ggf_ref)
        total[...] = jnp.zeros_like(total)

        @pl.loop(0, rows // STEP)
        def _(r):
            at = pl.ds(pl.multiple_of(r * STEP, STEP), STEP)
            normal, scale = norm_parts(mid_ref[at])
            part, gain_part = norm_back(g_ref[at], normal, scale, gf_ref[...])
            ggf_ref[...] += gain_part[None]
            grad = cot_ref[at].astype(F32) + part
            gmid_ref[at] = grad
            gbr_ref[at] = grad.astype(BF16)

    here = pl.ds(pl.multiple_of(j * cols, cols), cols)
    total[...] += nn(gbr_ref[:, here], w_ref[...])

    @pl.when(j == pl.num_programs(0) - 1)
    def _():
        ggm_ref[...] = jnp.zeros_like(ggm_ref)

        @pl.loop(0, rows // STEP)
        def _(r):
            at = pl.ds(pl.multiple_of(r * STEP, STEP), STEP)
            normal, scale = norm_parts(att_ref[at].astype(F32))
            part, gain_part = norm_back(total[at], normal, scale, gm_ref[...])
            ggm_ref[...] += gain_part[None]
            gatt_ref[at] = part.astype(BF16)


def branch_pass(grad_ffn_in, middle, cot, attended, w_out, gain_mix, gain_ffn):
    rows, width = cot.shape
    cols = TILE
    n = width // cols
    whole = pl.BlockSpec((rows, width), lambda j: (0, 0))
    gain = pl.BlockSpec((1, width), lambda j: (0, 0))
    low = jax.ShapeDtypeStruct((rows, width), BF16)
    sums = jax.ShapeDtypeStruct((1, width), F32)
    return pl.pallas_call(
        branch_kernel,
        grid=(n,),
        out_shape=(jax.ShapeDtypeStruct((rows, width), F32), low, low, sums, sums),
        in_specs=[
            whole,
            whole,
            whole,
            whole,
            pl.BlockSpec((cols, width), lambda j: (j, 0)),
            gain,
            gain,
        ],
        out_specs=(whole, whole, whole, gain, gain),
        scratch_shapes=[pltpu.VMEM((rows, width), F32)],
        compiler_params=pltpu.CompilerParams(vmem_limit_bytes=VMEM_LIMIT),
        cost_estimate=pl.CostEstimate(
            flops=2 * rows * width * width,
            bytes_accessed=2 * width * width + 20 * rows * width,
            transcendentals=0,
        ),
        name="branch_pass",
    )(grad_ffn_in, middle, cot, attended, w_out, gain_mix[None], gain_ffn[None])


CHUNK = 64


def finish_kernel(
    n, depth, gq_ref, gd_ref, pw_ref, pn_ref, po_ref, x_ref, grad_ref, mid_ref, ga_ref, gm_ref, gf_ref, gh_ref,
    oq_ref, od_ref, ow_ref, gi_ref, out_ref, sums_ref,
    own, twin_in, held, zown, zin, stage, gain_here, gain_row, gain_pack, gain_line,
    local_sem, load_sem, stage_sem, send_sem, recv_sem, keep_sem,
    up_send, up_recv, down_send, down_recv, home_send, home_recv, gain_send, gain_recv,
):
    me, twin, near_x, near_y, across = places()
    z = lax.axis_index("batch")
    rows, width = pn_ref.shape[1:]
    half = rows // 2
    low, high = pl.ds(0, half), pl.ds(half, half)
    mine = (across, near_x, near_y, me)
    _, chunk, cols = zown.shape
    across_width = width // cols
    per_part = (gq_ref.shape[1] // chunk) * across_width
    turned = gq_ref.shape[0] * per_part
    per_source = gd_ref.shape[1] // chunk
    outer = turned + gd_ref.shape[0] * per_source
    chunks = zown.shape[0]
    per_side = chunks // 2

    def cut(i, size):
        return pl.ds(pl.multiple_of(i * size, size), size)

    def wide(i):
        return cut(i // across_width, chunk), cut(lax.rem(i, across_width), cols)

    line_loads = []
    for g in range(turned):
        source = gq_ref.at[(g // per_part, *wide(g % per_part))]
        line_loads.append(pltpu.make_async_copy(source, zown.at[g], load_sem.at[g]))
    for g in range(turned, outer):
        source = gd_ref.at[
            (g - turned) // per_source, cut((g - turned) % per_source, chunk)
        ]
        line_loads.append(pltpu.make_async_copy(source, zown.at[g], load_sem.at[g]))
    for load in line_loads:
        load.start()
    partials = (pw_ref, pn_ref, po_ref)
    loads = [
        [
            pltpu.make_async_copy(p.at[block], own.at[m, i], local_sem.at[4 * m + i])
            for i, block in enumerate(mine)
        ]
        for m, p in enumerate(partials)
    ]
    for part in loads:
        for load in part:
            load.start()
    meet_all(n, depth)

    def copy(m, k, src, dst, partner):
        return remote(src, dst, send_sem.at[m, k], recv_sem.at[m, k], partner)

    twins = [
        [
            copy(m, i, p.at[block + twin], twin_in.at[m, i], me + twin)
            for i, block in enumerate(mine)
        ]
        for m, p in enumerate(partials)
    ]
    sends = [
        [
            copy(m, 4, own.at[m, 0, low], held.at[m, 0], near_x),
            copy(m, 5, own.at[m, 0, high], held.at[m, 1], near_y),
            copy(m, 6, own.at[m, 1, low], held.at[m, 2], near_x),
            copy(m, 7, own.at[m, 2, high], held.at[m, 3], near_y),
            copy(m, 8, own.at[m, 1, high], held.at[m, 4], near_x),
            copy(m, 9, own.at[m, 2, low], held.at[m, 5], near_y),
        ]
        for m in range(3)
    ]
    for part in twins:
        for send in part:
            send.start()

    def add_twin(m, i):
        loads[m][i].wait()
        twins[m][i].wait_recv()

        @pl.loop(0, rows // STEP)
        def _(r):
            at = cut(r, STEP)
            own[m, i, at] = (
                own[m, i, at].astype(F32) + twin_in[m, i, at].astype(F32)
            ).astype(BF16)

    def add_held(m, i, base, slot):
        @pl.loop(0, half // STEP)
        def _(r):
            at = cut(r, STEP)
            to = pl.ds(pl.multiple_of(base + r * STEP, STEP), STEP)
            own[m, i, to] = (
                own[m, i, to].astype(F32) + held[m, slot, at].astype(F32)
            ).astype(BF16)

    def first(m):
        add_twin(m, 0)
        sends[m][0].start()
        sends[m][1].start()
        add_twin(m, 1)
        sends[m][2].start()
        add_twin(m, 2)
        sends[m][3].start()

    def second(m):
        sends[m][1].wait_recv()
        add_held(m, 1, half, 1)
        sends[m][4].start()
        sends[m][0].wait_recv()
        add_held(m, 2, 0, 0)
        sends[m][5].start()

    def last(m, store):
        loads[m][3].wait()
        twins[m][3].wait_recv()
        for k in (2, 3, 4, 5):
            sends[m][k].wait_recv()
        for base, one, two in ((0, 2, 5), (half, 3, 4)):

            @pl.loop(0, half // STEP)
            def _(r):
                at = cut(r, STEP)
                place = base + r * STEP
                to = pl.ds(pl.multiple_of(place, STEP), STEP)
                store(
                    place,
                    to,
                    own[m, 3, to].astype(F32)
                    + twin_in[m, 3, to].astype(F32)
                    + held[m, one, at].astype(F32)
                    + held[m, two, at].astype(F32),
                )

    def store_line(place, to, value):
        value = value.astype(BF16)
        for side in range(across_width):
            zown[
                outer + (place // chunk) * across_width + side,
                pl.ds(pl.multiple_of(lax.rem(place, chunk), STEP), STEP),
            ] = value[:, side * cols : (side + 1) * cols]

    def store_inputs(place, to, value):
        normal, scale = norm_parts(x_ref[to].astype(F32))
        part, gain_part = norm_back(value, normal, scale, ga_ref[...])
        gi_ref[to] = grad_ref[to] + part
        gain_here[0:1] = gain_here[0:1] + gain_part[None]

    def store_outputs(place, to, value):
        out_ref[to] = (mid_ref[to] + value).astype(BF16)

    def home(part):
        block = part * n + me
        return block // 3, lax.rem(block, 3)

    def deliver_far(g):
        target, slot = home(g // per_part)
        piece = lax.rem(g, per_part)
        return remote(
            zin.at[g],
            oq_ref.at[(slot, *wide(piece))],
            home_send.at[g],
            home_recv.at[slot, piece],
            target,
        )

    def deliver_near(g):
        _, slot = home(g // per_part)
        return pltpu.make_async_copy(
            zin.at[g], oq_ref.at[(slot, *wide(lax.rem(g, per_part)))], keep_sem.at[g]
        )

    def widen(g):
        @pl.loop(0, chunk // STEP)
        def _(r):
            at = cut(r, STEP)
            stage[at] = zin[g, at].astype(F32)

    def deliver(g):
        target, _ = home(g // per_part)

        @pl.when((g < turned) & (target != me))
        def _():
            deliver_far(g).start()

        @pl.when((g < turned) & (target == me))
        def _():
            deliver_near(g).start()

        @pl.when((g >= turned) & (g < outer))
        def _():
            widen(g)
            at = g - turned
            place = cut(lax.rem(at, per_source), chunk), cut(at // per_source, cols)
            store = pltpu.make_async_copy(stage, od_ref.at[place], stage_sem)
            store.start()
            store.wait()

        @pl.when(g >= outer)
        def _():
            widen(g)
            store = pltpu.make_async_copy(
                stage, ow_ref.at[wide(g - outer)], stage_sem
            )
            store.start()
            store.wait()

    def delivered(g):
        target, _ = home(g // per_part)

        @pl.when(target != me)
        def _():
            deliver_far(g).wait_send()

        @pl.when(target == me)
        def _():
            deliver_near(g).wait()

    def go_up(g, ahead):
        return line_remote(zown.at[g], zin.at[g], up_send.at[g], up_recv.at[g], ahead)

    def go_down(g, behind):
        return line_remote(
            zin.at[g], zin.at[g], down_send.at[g], down_recv.at[g], behind
        )

    def ranks(side):
        if side == 0:
            return z, z + 1, z - 1
        return depth - 1 - z, z - 1, z + 1

    def add_line(g, target):
        @pl.loop(0, chunk // STEP)
        def _(r):
            at = cut(r, STEP)
            target[g, at] = (zown[g, at].astype(F32) + zin[g, at].astype(F32)).astype(
                BF16
            )

    lead = 2
    far = 2 * (depth - 1)
    steps = per_side + 2 * far

    def line_enter(c):
        for side in (0, 1):
            rank, ahead, _ = ranks(side)

            @pl.when(rank == 0)
            def _():
                go_up(2 * c + side, ahead).start()

    def line_step(t):
        @pl.when(t + lead < per_side)
        def _():
            line_enter(t + lead)

        back = []
        for side in (0, 1):
            rank, ahead, behind = ranks(side)
            c_back = t - 2 * far + 2 * rank
            g_back = 2 * c_back + side
            there = (c_back >= 0) & (c_back < per_side) & (rank < depth - 1)
            back.append((there, g_back))

            @pl.when(there)
            def _():
                go_down(g_back, ahead).wait_recv()

            @pl.when(there & (rank > 0))
            def _():
                go_down(g_back, behind).start()

        for side in (0, 1):
            rank, ahead, behind = ranks(side)
            c = t - 2 * rank
            g = 2 * c + side
            there = (c >= 0) & (c < per_side)

            @pl.when(there & (rank > 0) & (rank < depth - 1))
            def _():
                go_up(g, behind).wait_recv()
                add_line(g, zown)
                go_up(g, ahead).start()

            @pl.when(there & (rank == depth - 1))
            def _():
                go_up(g, behind).wait_recv()
                add_line(g, zin)
                go_down(g, behind).start()
                deliver(g)

        for there, g_back in back:

            @pl.when(there)
            def _():
                deliver(g_back)

    def line_steps(first_step, last_step):
        @pl.loop(first_step, last_step)
        def _(t):
            line_step(t)

    gain_here[...] = jnp.zeros_like(gain_here)
    for load in line_loads:
        load.wait()
    for c in range(lead):
        line_enter(c)
    first(0)
    line_steps(0, 8)
    second(0)
    line_steps(8, 9)
    first(1)
    line_steps(9, 18)
    last(0, store_line)
    line_steps(18, 20)
    second(1)
    line_steps(20, 21)
    first(2)
    line_steps(21, 28)
    last(1, store_inputs)

    gain_here[1:2] = gm_ref[...]
    gain_here[2:3] = gf_ref[...]
    gain_here[3:4, 0 : gh_ref.shape[1]] = gh_ref[...]
    gain_row[me] = gain_here[...]
    rounds = [
        remote(
            gain_here,
            gain_row.at[me],
            gain_send.at[0, k],
            gain_recv.at[0, k],
            lax.rem(me + k, n),
        )
        for k in range(1, n)
    ]
    for send in rounds:
        send.start()
    line_steps(28, 32)
    second(2)
    line_steps(32, 40)
    last(2, store_outputs)
    line_steps(40, 42)
    for send in rounds:
        send.wait()
    total = gain_row[0]
    for d in range(1, n):
        total = total + gain_row[d]
    gain_pack[0:8] = total
    for d in range(n):
        gain_pack[8 + d : 9 + d] = gain_row[d, 3:4]
    gain_line[z] = gain_pack[...]
    rounds = [
        line_remote(
            gain_pack,
            gain_line.at[z],
            gain_send.at[1, k],
            gain_recv.at[1, k],
            lax.rem(z + k, depth),
        )
        for k in range(1, depth)
    ]
    for send in rounds:
        send.start()
    line_steps(42, steps)
    for send in rounds:
        send.wait()
    total = gain_line[0]
    for d in range(1, depth):
        total = total + gain_line[d]
    sums_ref[...] = total

    for m in range(3):
        for send in twins[m] + sends[m]:
            send.wait_send()
    for g in range(chunks):
        rank, ahead, behind = ranks(g % 2)

        @pl.when(rank < depth - 1)
        def _():
            go_up(g, ahead).wait_send()

        @pl.when(rank > 0)
        def _():
            go_down(g, behind).wait_send()

    for g in range(turned):
        delivered(g)
    for slot in range(3):
        block = 3 * me + slot
        source = lax.rem(block, n)

        @pl.when(source != me)
        def _():
            for piece in range(per_part):
                remote(
                    zin.at[0],
                    oq_ref.at[(slot, *wide(piece))],
                    home_send.at[0],
                    home_recv.at[slot, piece],
                    source,
                ).wait_recv()


def finish(
    grad_qkv, grad_down, part_out, part_normed, part_outputs, x, grad_middle, middle, gain, gains, collective_id
):
    n, depth = lax.axis_size("seq"), lax.axis_size("batch")
    rows, width = part_out.shape[0] // n, part_out.shape[1]
    cols = grad_qkv.shape[1]
    sources, _, feats = grad_down.shape
    if n != 8 or depth != 4:
        me = lax.axis_index("seq")
        blocks = lax.psum(grad_qkv, "batch")
        back = [
            lax.ppermute(
                give_part(blocks, me, n, j),
                "seq",
                [((3 * d + j) % n, d) for d in range(n)],
            )
            for j in range(3)
        ]
        w_out = lax.psum(scatter_seq(part_out, None).astype(BF16), "batch")
        normal, scale = norm_parts(x.astype(F32))
        part, gain_part = norm_back(scatter_seq(part_normed, None), normal, scale, gain)
        shared = [lax.psum(g, ("batch", "seq")) for g in (gain_part, gains[0][0], gains[1][0])]
        hidden = lax.all_gather(lax.psum(gains[2][0], "batch"), "seq", axis=0, tiled=True)
        down = lax.psum(grad_down, "batch")
        return (
            jnp.concatenate(back, axis=0),
            jnp.swapaxes(down, 0, 1).reshape(rows, sources * feats).astype(F32),
            w_out.astype(F32),
            grad_middle + part,
            (middle + scatter_seq(part_outputs, None)).astype(BF16),
            (*shared, hidden),
        )
    chunks = (
        3 * cols * width + rows * width + sources * rows * feats
    ) // (CHUNK * feats)
    dma = pltpu.SemaphoreType.DMA
    line = pltpu.VMEM((chunks, CHUNK, feats), BF16)
    w_qkv, w_down, w_out, grad_inputs, outputs, sums = pl.pallas_call(
        functools.partial(finish_kernel, n, depth),
        out_shape=(
            jax.ShapeDtypeStruct((3, cols, width), BF16),
            jax.ShapeDtypeStruct((rows, sources * feats), F32),
            jax.ShapeDtypeStruct((rows, width), F32),
            jax.ShapeDtypeStruct((rows, width), F32),
            jax.ShapeDtypeStruct((rows, width), BF16),
            jax.ShapeDtypeStruct((16, width), F32),
        ),
        in_specs=[ANY] * 5 + [INSIDE] * 7,
        out_specs=(ANY, ANY, ANY, INSIDE, INSIDE, INSIDE),
        scratch_shapes=[
            pltpu.VMEM((3, 4, rows, width), BF16),
            pltpu.VMEM((3, 4, rows, width), BF16),
            pltpu.VMEM((3, 6, rows // 2, width), BF16),
            line,
            line,
            pltpu.VMEM((CHUNK, feats), F32),
            pltpu.VMEM((8, width), F32),
            pltpu.VMEM((n, 8, width), F32),
            pltpu.VMEM((16, width), F32),
            pltpu.VMEM((depth, 16, width), F32),
            dma((12,)),
            dma((chunks,)),
            dma,
            dma((3, 10)),
            dma((3, 10)),
            dma((chunks,)),
            dma((chunks,)),
            dma((chunks,)),
            dma((chunks,)),
            dma((chunks,)),
            dma((chunks,)),
            dma((3, cols * width // (CHUNK * feats))),
            dma((2, n)),
            dma((2, n)),
        ],
        compiler_params=pltpu.CompilerParams(
            collective_id=collective_id,
            has_side_effects=True,
            vmem_limit_bytes=VMEM_LIMIT,
        ),
        name="finish",
    )(
        grad_qkv,
        grad_down,
        *[p.reshape(n, rows, width) for p in (part_out, part_normed, part_outputs)],
        x,
        grad_middle,
        middle,
        gain[None],
        *gains,
    )
    return (
        w_qkv.reshape(3 * cols, width),
        w_down,
        w_out,
        grad_inputs,
        outputs,
        (sums[0], sums[1], sums[2], sums[8:, :feats].reshape(-1)),
    )


def body(
    inputs,
    segment_ids,
    w_qkv,
    w_out,
    w_up,
    w_down,
    gain_attn,
    gain_mix,
    gain_ffn,
    gain_hidden,
    cotangent,
):
    _, local, width = inputs.shape
    n, depth = lax.axis_size("seq"), lax.axis_size("batch")
    me = lax.axis_index("seq")
    length = local * n
    feats = w_up.shape[0]
    x_low = inputs[0]
    x = x_low.astype(F32)
    cot = cotangent[0]
    segment = segment_ids[0]

    w_out_full = lax.all_gather(w_out, "seq", axis=0, tiled=True)
    normed = (norm_parts(x)[0] * gain_attn).astype(BF16)
    before = [jnp.sum((segment < d).astype(jnp.int32)) for d in range(1, DOCS)]
    start = jnp.zeros_like(segment)
    for d in range(1, DOCS):
        start = jnp.where(segment == d, before[d - 1], start)
    positions = jnp.arange(length, dtype=jnp.int32) - start
    first = start[::TILE] // TILE
    start_row = start[None, :]

    normed_full, w_heads, w_down_near, tables = start_exchange(
        normed, w_qkv, w_down, positions.astype(F32), 1
    )
    cot_late, _ = lax.optimization_barrier((cot, w_heads))
    cot_full = lax.all_gather(cot_late, "seq", axis=0, tiled=True)

    q, k, v, kt, vt = project_qkv(normed_full, w_heads, tables)
    attended_heads, lse = attend(first, start_row, q, k, vt)
    attended, w_down_extra = heads_to_tokens(attended_heads, w_down_near, 2)
    mix_in, middle, ffn_in = mix_pass(attended, x_low, w_out_full, gain_mix, gain_ffn)
    gain_here = lax.dynamic_slice_in_dim(gain_hidden, me * feats, feats, 0)[None, :]
    ffn_full, w_down_cols, hidden, grad_upper, grad_gain_here = ffn_pass(
        ffn_in, w_up, cot_full, w_down_near, w_down_extra, gain_here, 3
    )

    grad_w_up = tn(grad_upper, ffn_full).astype(BF16)
    grad_upper, grad_w_up = lax.optimization_barrier((grad_upper, grad_w_up))
    grad_w_up = lax.psum(grad_w_up, "batch")
    grad_w_down = tn(cot_full, hidden).astype(BF16).reshape(n, local, feats)
    grad_upper, grad_w_down = lax.optimization_barrier((grad_upper, grad_w_down))
    grad_ffn_in = scatter_seq(nn(grad_upper, w_up).astype(BF16), 4)
    grad_middle, grad_branch, grad_att, grad_gain_ffn, grad_gain_mix = branch_pass(
        grad_ffn_in, middle, cot, attended, w_out_full, gain_mix, gain_ffn
    )
    grad_heads = tokens_to_heads(grad_att, 5)
    grad_w_down, grad_heads = lax.optimization_barrier((grad_w_down, grad_heads))
    grad_w_down = lax.all_to_all(grad_w_down, "seq", split_axis=0, concat_axis=0, tiled=True)
    grads = attend_back(
        first, start_row, q, k, kt, v, attended_heads, lse, grad_heads, tables
    )
    grad_w_qkv, grad_w_down, grad_w_out, grad_inputs, outputs, gains = finish(
        tn(grads, normed_full).astype(BF16).reshape(3, -1, width),
        grad_w_down,
        tn(grad_branch, mix_in).astype(BF16),
        nn(grads, w_heads).astype(BF16),
        nt(hidden, w_down_cols).astype(BF16),
        x_low,
        grad_middle,
        middle,
        gain_attn,
        (grad_gain_mix, grad_gain_ffn, grad_gain_here),
        6,
    )
    return (
        outputs[None],
        grad_inputs[None],
        grad_w_qkv.astype(F32),
        grad_w_out,
        grad_w_up.astype(F32),
        grad_w_down,
        *gains,
    )


def pick_part(turned, me, n, part):
    chosen = turned[0]
    home = part * n + me
    for j in (1, 2):
        chosen = jnp.where(lax.rem(home, 3) == j, turned[j], chosen)
    return chosen


def give_part(blocks, me, n, j):
    chosen = blocks[0]
    for part in (1, 2):
        chosen = jnp.where(lax.rem(part * n + me, 3) == j, blocks[part], chosen)
    return chosen


def solution(mesh):
    in_specs = (
        P("batch", "seq", None),
        P("batch", None),
        P("seq", None),
        P("seq", None),
        P("seq", None),
        P("seq", None),
        P(),
        P(),
        P(),
        P(),
        P("batch", "seq", None),
    )
    out_specs = (
        P("batch", "seq", None),
        P("batch", "seq", None),
        P("seq", None),
        P("seq", None),
        P("seq", None),
        P("seq", None),
        P(),
        P(),
        P(),
        P(),
    )
    return jax.shard_map(body, mesh=mesh, in_specs=in_specs, out_specs=out_specs, check_vma=False)
```

```python
import functools
import math

import jax
import jax.numpy as jnp
from jax import lax
from jax.experimental import pallas as pl
from jax.experimental.pallas import tpu as pltpu
from jax.sharding import PartitionSpec as P

HEADS = 32
HEAD_DIM = 64
LENGTH = 2048
XBASE = 512
DOCS = 4
EPSILON = 1e-05
MASKED = -1e30
TILE = 256
VMEM_LIMIT = 60 * 1024 * 1024

MESH = pl.DeviceIdType.MESH
F32 = jnp.float32
BF16 = jnp.bfloat16
ANY = pl.BlockSpec(memory_space=pl.ANY)
INSIDE = pl.BlockSpec(memory_space=pltpu.VMEM)


def nn(a, b):
    return lax.dot_general(a, b, (((1,), (0,)), ((), ())), preferred_element_type=F32)


def nt(a, b):
    return lax.dot_general(a, b, (((1,), (1,)), ((), ())), preferred_element_type=F32)


def tn(a, b):
    return lax.dot_general(a, b, (((0,), (0,)), ((), ())), preferred_element_type=F32)


def norm_parts(values):
    average = jnp.mean(values, axis=-1, keepdims=True)
    centered = values - average
    spread = jnp.mean(centered * centered, axis=-1, keepdims=True)
    scale = lax.rsqrt(spread + EPSILON)
    return centered * scale, scale


def norm_back(grad, normal, scale, gain):
    part = grad * gain
    inner = (
        part
        - jnp.mean(part, axis=-1, keepdims=True)
        - normal * jnp.mean(part * normal, axis=-1, keepdims=True)
    )
    return scale * inner, jnp.sum(grad * normal, axis=0)


def places():
    me = lax.axis_index("seq")
    core = lax.rem(me, 2)
    along_x = lax.rem(me // 2, 2)
    along_y = me // 4
    twin = 1 - 2 * core
    near_x = me + 2 - 4 * along_x
    near_y = me + 4 - 8 * along_y
    across = near_x + 4 - 8 * along_y
    return me, twin, near_x, near_y, across


def remote(src, dst, send_sem, recv_sem, partner):
    return pltpu.make_async_remote_copy(
        src_ref=src,
        dst_ref=dst,
        send_sem=send_sem,
        recv_sem=recv_sem,
        device_id={"seq": partner},
        device_id_type=MESH,
    )


def meet(partners):
    barrier = pltpu.get_barrier_semaphore()
    for partner in partners:
        pl.semaphore_signal(
            barrier, inc=1, device_id={"seq": partner}, device_id_type=MESH
        )
    pl.semaphore_wait(barrier, len(partners))


def gather_copies(x_ref, o_ref, send_sem, recv_sem):
    me, twin, near_x, near_y, across = places()
    half = x_ref.shape[0] // 2
    low, high = pl.ds(0, half), pl.ds(half, half)

    def copy(k, src, dst, partner):
        return remote(src, dst, send_sem.at[k], recv_sem.at[k], partner)

    def relay(k, owner, rows, partner):
        place = o_ref.at[owner, rows]
        return copy(k, place, place, partner)

    return [
        copy(0, x_ref.at[low], o_ref.at[me, low], near_x),
        copy(1, x_ref.at[high], o_ref.at[me, high], near_y),
        copy(2, x_ref.at[high], o_ref.at[me, high], near_x),
        copy(3, x_ref.at[low], o_ref.at[me, low], near_y),
        copy(4, x_ref, o_ref.at[me], me + twin),
        relay(5, near_x, low, near_y),
        relay(6, near_y, high, near_x),
        relay(7, near_x, low, me + twin),
        relay(8, near_y, high, me + twin),
        relay(9, near_x, high, me + twin),
        relay(10, near_y, low, me + twin),
        relay(11, across, low, me + twin),
        relay(12, across, high, me + twin),
    ]


def gather_run(sends, *between):
    between = (*between, *([None] * 3))[:3]

    def pause(i):
        if between[i] is not None:
            between[i]()

    sends[0].wait_recv()
    sends[5].start()
    sends[7].start()
    sends[1].wait_recv()
    sends[6].start()
    sends[8].start()
    pause(0)
    sends[2].wait_recv()
    sends[9].start()
    sends[3].wait_recv()
    sends[10].start()
    pause(1)
    sends[5].wait_recv()
    sends[11].start()
    sends[6].wait_recv()
    sends[12].start()
    pause(2)
    for k in (4, 7, 8, 9, 10, 11, 12):
        sends[k].wait_recv()
    for send in sends:
        send.wait_send()


def meet_all(n, depth):
    me = lax.axis_index("seq")
    z = lax.axis_index("batch")
    barrier = pltpu.get_barrier_semaphore()
    for k in range(1, n):
        pl.semaphore_signal(
            barrier, inc=1, device_id={"seq": lax.rem(me + k, n)}, device_id_type=MESH
        )
    for k in range(1, depth):
        pl.semaphore_signal(
            barrier,
            inc=1,
            device_id={"batch": lax.rem(z + k, depth)},
            device_id_type=MESH,
        )
    pl.semaphore_wait(barrier, n + depth - 2)


def line_remote(src, dst, send_sem, recv_sem, partner):
    return pltpu.make_async_remote_copy(
        src_ref=src,
        dst_ref=dst,
        send_sem=send_sem,
        recv_sem=recv_sem,
        device_id={"batch": partner},
        device_id_type=MESH,
    )


class Line:
    def __init__(self, depth, source, target, send_sem, recv_sem):
        self.depth, self.source, self.target = depth, source, target
        self.send_sem, self.recv_sem = send_sem, recv_sem
        self.z = lax.axis_index("batch")

    def message(self, side, k):
        sign = 2 * side - 1
        owner = self.z - sign * k
        return line_remote(
            self.source(owner, k),
            self.target(owner),
            self.send_sem.at[side, k],
            self.recv_sem.at[side, k],
            self.z + sign,
        )

    def sends(self, side, k):
        sign = 2 * side - 1
        owner, target = self.z - sign * k, self.z + sign
        inside = (owner >= 0) & (owner < self.depth)
        return inside & (target >= 0) & (target < self.depth)

    def land(self, k):
        for side in (0, 1):
            sign = 2 * side - 1
            owner = self.z - sign * (k + 1)

            @pl.when((owner >= 0) & (owner < self.depth))
            def _():
                place = self.target(owner)
                line_remote(
                    place,
                    place,
                    self.send_sem.at[side, k],
                    self.recv_sem.at[side, k],
                    self.z - sign,
                ).wait_recv()

    def start(self, k):
        for side in (0, 1):

            @pl.when(self.sends(side, k))
            def _():
                self.message(side, k).start()

    def sent(self, k):
        for side in (0, 1):

            @pl.when(self.sends(side, k))
            def _():
                self.message(side, k).wait_send()


def lane_tables(place):
    half = HEAD_DIM // 2
    lane = lax.broadcasted_iota(jnp.int32, (1, 128), 1)
    channel = lax.rem(lane, half).astype(F32)
    inverse = jnp.exp(channel * (-math.log(10000.0) / half))
    zeta = (channel * (2.0 / HEAD_DIM) + 0.4) / 1.4
    sign = jnp.where(lax.rem(lane, HEAD_DIM) < half, -1.0, 1.0)
    angle = place * inverse
    growth = jnp.exp((place - 0.5 * LENGTH) * (1.0 / XBASE) * jnp.log(zeta))
    shrink = 1.0 / growth
    cosine = jnp.cos(angle)
    sine = jnp.sin(angle) * sign
    return cosine * growth, sine * growth, cosine * shrink, sine * shrink


def start_kernel(
    n, depth, x_ref, w_ref, wd_ref, pos_ref,
    o_ref, wt_ref, wc_ref, cq_ref, sq_ref, ck_ref, sk_ref,
    keep_w, keep_c, local_sem, send_sem, recv_sem, hop_send, hop_recv, col_send, col_recv,
    line_send, line_recv,
):
    z = lax.axis_index("batch")
    rows_z = wc_ref.shape[2]
    cols = wc_ref.shape[3]
    me, twin, near_x, near_y, _ = places()
    own = pltpu.make_async_copy(x_ref, o_ref.at[me], local_sem.at[0])
    own.start()
    wd_rows = pl.ds(pl.multiple_of(z * rows_z, rows_z), rows_z)

    def column(k):
        return wd_ref.at[wd_rows, pl.ds(pl.multiple_of(k * cols, cols), cols)]

    load_column = pltpu.make_async_copy(column(me), keep_c, local_sem.at[4])
    own_column = pltpu.make_async_copy(keep_c, wc_ref.at[me, z], local_sem.at[5])
    load_column.start()
    meet_all(n, depth)
    load_column.wait()
    own_column.start()
    def hop(j, part, target):
        return remote(
            w_ref.at[j], wt_ref.at[part], hop_send.at[j], hop_recv.at[part], target
        )

    def load(j):
        return pltpu.make_async_copy(w_ref.at[j], keep_w, local_sem.at[6])

    def here(j, part):
        return pltpu.make_async_copy(keep_w, wt_ref.at[part], local_sem.at[1 + j])

    turns = [
        remote(
            column(lax.rem(me + k, n)),
            wc_ref.at[me, z],
            col_send.at[k],
            col_recv.at[k],
            lax.rem(me + k, n),
        )
        for k in range(1, n)
    ]
    for turn in turns:
        turn.start()
    for j in range(3):
        block = 3 * me + j
        target = lax.rem(block, n)
        for part in range(3):
            inside = block // n == part

            @pl.when(inside & (target != me))
            def _():
                hop(j, part, target).start()

            @pl.when(inside & (target == me))
            def _():
                load(j).start()

    sends = gather_copies(x_ref, o_ref, send_sem, recv_sem)
    for k in range(5):
        sends[k].start()

    line = Line(
        depth,
        lambda owner, k: wc_ref.at[:, owner],
        lambda owner: wc_ref.at[:, owner],
        line_send,
        line_recv,
    )

    own_column.wait()
    for turn in turns:
        turn.wait_recv()
    line.start(0)
    for j in range(3):
        block = 3 * me + j
        target = lax.rem(block, n)
        for part in range(3):

            @pl.when((block // n == part) & (target == me))
            def _():
                load(j).wait()
                here(j, part).start()

    @pl.loop(0, pos_ref.shape[0])
    def _(r):
        at = pl.ds(pl.multiple_of(r * 128, 128), 128)
        places_here = jnp.broadcast_to(pos_ref[pl.ds(r, 1), :], (128, 128)).T
        tables = lane_tables(places_here)
        for ref, table in zip((cq_ref, sq_ref, ck_ref, sk_ref), tables, strict=True):
            ref[at] = table

    def hand_on(k):
        def step():
            line.land(k - 1)
            line.start(k)

        return step

    gather_run(sends, *[hand_on(k) for k in range(1, depth - 1)])
    line.land(depth - 2)
    for k in range(depth - 1):
        line.sent(k)
    for turn in turns:
        turn.wait_send()
    for j in range(3):
        block = 3 * me + j
        target = lax.rem(block, n)
        for part in range(3):
            inside = block // n == part

            @pl.when(inside & (target != me))
            def _():
                hop(j, part, target).wait_send()

            @pl.when(inside & (target == me))
            def _():
                here(j, part).wait()

    for part in range(3):
        source = (part * n + me) // 3

        @pl.when(source != me)
        def _():
            hop(0, part, source).wait_recv()

    own.wait()


def start_exchange(block, w_qkv, w_down, positions, collective_id):
    n, depth = lax.axis_size("seq"), lax.axis_size("batch")
    rows, width = block.shape
    piece = w_qkv.shape[0] // 3
    w = w_qkv.reshape(3, piece, width)
    if n != 8:
        me = lax.axis_index("seq")
        turned = [
            lax.ppermute(w[j], "seq", [(d, (3 * d + j) % n) for d in range(n)])
            for j in range(3)
        ]
        parts = [pick_part(turned, me, n, part) for part in range(3)]
        place = jnp.broadcast_to(positions[:, None], (positions.shape[0], 128))
        return (
            lax.all_gather(block, "seq", axis=0, tiled=True),
            jnp.concatenate(parts, axis=0),
            lax.all_to_all(w_down, "seq", split_axis=1, concat_axis=0, tiled=True),
            lane_tables(place),
        )
    rows_z, cols = w_down.shape[0] // depth, w_down.shape[1] // n
    inside = pl.BlockSpec(memory_space=pltpu.VMEM)
    table = jax.ShapeDtypeStruct((n * rows, 128), F32)
    gathered, turned, columns, *tables = pl.pallas_call(
        functools.partial(start_kernel, n, depth),
        out_shape=(
            jax.ShapeDtypeStruct((n, rows, width), block.dtype),
            jax.ShapeDtypeStruct((3, piece, width), w.dtype),
            jax.ShapeDtypeStruct((n, depth, rows_z, cols), w_down.dtype),
            *([table] * 4),
        ),
        in_specs=[INSIDE, ANY, ANY, INSIDE],
        out_specs=(ANY, ANY, ANY, *([INSIDE] * 4)),
        scratch_shapes=[
            pltpu.VMEM((piece, width), BF16),
            pltpu.VMEM((rows_z, cols), BF16),
            pltpu.SemaphoreType.DMA((7,)),
            pltpu.SemaphoreType.DMA((13,)),
            pltpu.SemaphoreType.DMA((13,)),
            pltpu.SemaphoreType.DMA((3,)),
            pltpu.SemaphoreType.DMA((3,)),
            pltpu.SemaphoreType.DMA((n,)),
            pltpu.SemaphoreType.DMA((n,)),
            pltpu.SemaphoreType.DMA((2, depth)),
            pltpu.SemaphoreType.DMA((2, depth)),
        ],
        compiler_params=pltpu.CompilerParams(
            collective_id=collective_id, has_side_effects=True, vmem_limit_bytes=VMEM_LIMIT
        ),
        name="start_exchange",
    )(block, w, w_down, positions.reshape(-1, 128))
    return (
        gathered.reshape(n * rows, width),
        turned.reshape(3 * piece, width),
        columns.reshape(-1, cols),
        tables,
    )


def scatter_kernel(
    p_ref, o_ref, own, twin_in, held, local_sem, send_sem, recv_sem
):
    me, twin, near_x, near_y, across = places()
    rows = p_ref.shape[1]
    half = rows // 2
    low, high = pl.ds(0, half), pl.ds(half, half)
    mine = (across, near_x, near_y, me)

    loads = [
        pltpu.make_async_copy(p_ref.at[block], own.at[i], local_sem.at[i])
        for i, block in enumerate(mine)
    ]
    for load in loads:
        load.start()
    meet((me + twin, near_x, near_y))

    def copy(k, src, dst, partner):
        return remote(src, dst, send_sem.at[k], recv_sem.at[k], partner)

    twins = [
        copy(i, p_ref.at[block + twin], twin_in.at[i], me + twin)
        for i, block in enumerate(mine)
    ]
    for send in twins:
        send.start()
    sends = [
        copy(4, own.at[0, low], held.at[0], near_x),
        copy(5, own.at[0, high], held.at[1], near_y),
        copy(6, own.at[1, low], held.at[2], near_x),
        copy(7, own.at[2, high], held.at[3], near_y),
        copy(8, own.at[1, high], held.at[4], near_x),
        copy(9, own.at[2, low], held.at[5], near_y),
    ]
    step = 32

    def add_twin(i):
        loads[i].wait()
        twins[i].wait_recv()

        @pl.loop(0, rows // step)
        def _(r):
            at = pl.ds(pl.multiple_of(r * step, step), step)
            own[i, at] = (
                own[i, at].astype(F32) + twin_in[i, at].astype(F32)
            ).astype(own.dtype)

    def add_held(i, base, slot):
        @pl.loop(0, half // step)
        def _(r):
            at = pl.ds(pl.multiple_of(r * step, step), step)
            to = pl.ds(pl.multiple_of(base + r * step, step), step)
            own[i, to] = (
                own[i, to].astype(F32) + held[slot, at].astype(F32)
            ).astype(own.dtype)

    add_twin(0)
    sends[0].start()
    sends[1].start()
    add_twin(1)
    sends[2].start()
    add_twin(2)
    sends[3].start()
    sends[1].wait_recv()
    add_held(1, half, 1)
    sends[4].start()
    sends[0].wait_recv()
    add_held(2, 0, 0)
    sends[5].start()
    loads[3].wait()
    twins[3].wait_recv()
    for k in (2, 3, 4, 5):
        sends[k].wait_recv()

    def final(base, first, second):
        @pl.loop(0, half // step)
        def _(r):
            at = pl.ds(pl.multiple_of(r * step, step), step)
            to = pl.ds(pl.multiple_of(base + r * step, step), step)
            o_ref[to] = (
                own[3, to].astype(F32)
                + twin_in[3, to].astype(F32)
                + held[first, at].astype(F32)
                + held[second, at].astype(F32)
            )

    final(0, 2, 5)
    final(half, 3, 4)
    for send in twins + sends:
        send.wait_send()


def scatter_seq(partial, collective_id):
    n = lax.axis_size("seq")
    rows, width = partial.shape[0] // n, partial.shape[1]
    if n != 8:
        return lax.psum_scatter(
            partial, "seq", scatter_dimension=0, tiled=True
        ).astype(F32)
    return pl.pallas_call(
        scatter_kernel,
        out_shape=jax.ShapeDtypeStruct((rows, width), F32),
        in_specs=[ANY],
        out_specs=pl.BlockSpec(memory_space=pltpu.VMEM),
        scratch_shapes=[
            pltpu.VMEM((4, rows, width), BF16),
            pltpu.VMEM((4, rows, width), BF16),
            pltpu.VMEM((6, rows // 2, width), BF16),
            pltpu.SemaphoreType.DMA((4,)),
            pltpu.SemaphoreType.DMA((10,)),
            pltpu.SemaphoreType.DMA((10,)),
        ],
        compiler_params=pltpu.CompilerParams(
            collective_id=collective_id,
            has_side_effects=True,
            vmem_limit_bytes=VMEM_LIMIT,
        ),
        name="scatter_seq",
    )(partial.reshape(n, rows, width))


def heads_to_tokens_kernel(n, x_ref, o_ref, keep, local_sem, send_sem, recv_sem):
    me = lax.axis_index("seq")
    rows = o_ref.shape[0]
    cols = x_ref.shape[1]
    exchange(
        n,
        me,
        lambda k: x_ref.at[pl.ds(pl.multiple_of(k * rows, rows), rows)],
        o_ref.at[:, pl.ds(pl.multiple_of(me * cols, cols), cols)],
        keep,
        local_sem,
        send_sem,
        recv_sem,
    )


def exchange(n, me, source, target, keep, local_sem, send_sem, recv_sem):
    load = pltpu.make_async_copy(source(me), keep, local_sem.at[0])
    own = pltpu.make_async_copy(keep, target, local_sem.at[1])
    load.start()
    barrier = pltpu.get_barrier_semaphore()
    for k in range(1, n):
        pl.semaphore_signal(
            barrier,
            inc=1,
            device_id={"seq": lax.rem(me + k, n)},
            device_id_type=MESH,
        )
    pl.semaphore_wait(barrier, n - 1)
    copies = []
    for k in range(1, n):
        partner = lax.rem(me + k, n)
        copies.append(
            pltpu.make_async_remote_copy(
                src_ref=source(partner),
                dst_ref=target,
                send_sem=send_sem.at[k],
                recv_sem=recv_sem.at[k],
                device_id={"seq": partner},
                device_id_type=MESH,
            )
        )
        copies[-1].start()
    load.wait()
    own.start()
    for copy in copies:
        copy.wait()
    own.wait()


def heads_to_tokens(heads, collective_id):
    n = lax.axis_size("seq")
    total, cols = heads.shape
    rows = total // n
    return pl.pallas_call(
        functools.partial(heads_to_tokens_kernel, n),
        out_shape=jax.ShapeDtypeStruct((rows, n * cols), heads.dtype),
        in_specs=[ANY],
        out_specs=ANY,
        scratch_shapes=[
            pltpu.VMEM((rows, cols), heads.dtype),
            pltpu.SemaphoreType.DMA((2,)),
            pltpu.SemaphoreType.DMA((n,)),
            pltpu.SemaphoreType.DMA((n,)),
        ],
        compiler_params=pltpu.CompilerParams(
            collective_id=collective_id, has_side_effects=True, vmem_limit_bytes=VMEM_LIMIT
        ),
        name="heads_to_tokens",
    )(heads)


def tokens_to_heads_kernel(n, x_ref, o_ref, keep, local_sem, send_sem, recv_sem):
    me = lax.axis_index("seq")
    rows = x_ref.shape[0]
    cols = o_ref.shape[1]
    exchange(
        n,
        me,
        lambda k: x_ref.at[:, pl.ds(pl.multiple_of(k * cols, cols), cols)],
        o_ref.at[pl.ds(pl.multiple_of(me * rows, rows), rows)],
        keep,
        local_sem,
        send_sem,
        recv_sem,
    )


def tokens_to_heads(tokens, collective_id):
    n = lax.axis_size("seq")
    rows, total = tokens.shape
    return pl.pallas_call(
        functools.partial(tokens_to_heads_kernel, n),
        out_shape=jax.ShapeDtypeStruct((rows * n, total // n), tokens.dtype),
        in_specs=[ANY],
        out_specs=ANY,
        scratch_shapes=[
            pltpu.VMEM((rows, total // n), tokens.dtype),
            pltpu.SemaphoreType.DMA((2,)),
            pltpu.SemaphoreType.DMA((n,)),
            pltpu.SemaphoreType.DMA((n,)),
        ],
        compiler_params=pltpu.CompilerParams(
            collective_id=collective_id, has_side_effects=True, vmem_limit_bytes=VMEM_LIMIT
        ),
        name="tokens_to_heads",
    )(tokens)


def swap_halves(values):
    width = values.shape[-1]
    half = HEAD_DIM // 2
    lane = lax.broadcasted_iota(jnp.int32, values.shape, 1)
    ahead = pltpu.roll(values, width - half, 1)
    behind = pltpu.roll(values, half, 1)
    return jnp.where(lane % HEAD_DIM < half, ahead, behind)


def spread_lanes(table, width):
    return jnp.concatenate([table] * (width // table.shape[-1]), axis=-1)


def qkv_kernel(
    x_ref, w_ref, cq_ref, sq_ref, ck_ref, sk_ref,
    q_ref, k_ref, v_ref, kt_ref, vt_ref,
):
    x = x_ref[...]
    width = q_ref.shape[1]
    query = nt(x, w_ref[0:width])
    query = query * spread_lanes(cq_ref[...], width) + swap_halves(
        query
    ) * spread_lanes(sq_ref[...], width)
    q_ref[...] = query.astype(BF16) * (HEAD_DIM**-0.5)
    keys = nt(x, w_ref[width : 2 * width])
    keys = keys * spread_lanes(ck_ref[...], width) + swap_halves(
        keys
    ) * spread_lanes(sk_ref[...], width)
    k_ref[...] = keys.astype(BF16)
    kt_ref[...] = keys.T.astype(BF16)
    values = nt(x, w_ref[2 * width :])
    v_ref[...] = values.astype(BF16)
    vt_ref[...] = values.T.astype(BF16)


def project_qkv(x, w, tables):
    length, width = x.shape
    cols = w.shape[0] // 3
    steps = length // TILE
    weight = pl.BlockSpec((3 * cols, width), lambda i: (0, 0))
    table = pl.BlockSpec((TILE, tables[0].shape[1]), lambda i: (i, 0))
    row_out = pl.BlockSpec((TILE, cols), lambda i: (i, 0))
    col_out = pl.BlockSpec((cols, TILE), lambda i: (0, i))
    rows = jax.ShapeDtypeStruct((length, cols), BF16)
    columns = jax.ShapeDtypeStruct((cols, length), BF16)
    return pl.pallas_call(
        qkv_kernel,
        grid=(steps,),
        out_shape=(rows, rows, rows, columns, columns),
        in_specs=[pl.BlockSpec((TILE, width), lambda i: (i, 0))]
        + [weight]
        + [table] * 4,
        out_specs=(row_out, row_out, row_out, col_out, col_out),
        compiler_params=pltpu.CompilerParams(vmem_limit_bytes=VMEM_LIMIT),
        cost_estimate=pl.CostEstimate(
            flops=6 * length * width * cols,
            bytes_accessed=2 * length * width + 6 * width * cols + 10 * length * cols,
            transcendentals=0,
        ),
        name="project_qkv",
    )(x, w, *tables)


def pair_mask(start_row, i, j):
    key_place = j * TILE + lax.broadcasted_iota(jnp.int32, (TILE, TILE), 0)
    query_place = i * TILE + lax.broadcasted_iota(jnp.int32, (TILE, TILE), 1)
    return (key_place <= query_place) & (key_place >= start_row)


def head_rows(query, heads):
    lane = lax.broadcasted_iota(jnp.int32, query.shape, 1) // HEAD_DIM
    zero = jnp.zeros_like(query)
    return [jnp.where(lane == h, query, zero) for h in range(heads)]


def attend_kernel(
    heads, first_ref, start_ref, q_ref, k_ref, vt_ref, o_ref, lse_ref, peak, total, mixed
):
    i = pl.program_id(0)
    queries = head_rows(q_ref[...], heads)
    start_row = start_ref[...]

    def block(j, first):
        at = pl.ds(pl.multiple_of(j * TILE, TILE), TILE)
        keys = k_ref[at, :]
        mask = pair_mask(start_row, i, j)
        for h in range(heads):
            here = slice(h * HEAD_DIM, (h + 1) * HEAD_DIM)
            scores = jnp.where(mask, nt(keys, queries[h]), MASKED)
            if first:
                new_peak = jnp.max(scores, axis=0, keepdims=True)
                expo = jnp.exp(scores - new_peak)
                total[h : h + 1] = jnp.sum(expo, axis=0, keepdims=True)
                mixed[here] = nn(vt_ref[here, at], expo.astype(BF16))
            else:
                old_peak = peak[h : h + 1]
                new_peak = jnp.maximum(old_peak, jnp.max(scores, axis=0, keepdims=True))
                expo = jnp.exp(scores - new_peak)
                shrink = jnp.exp(old_peak - new_peak)
                total[h : h + 1] = total[h : h + 1] * shrink + jnp.sum(
                    expo, axis=0, keepdims=True
                )
                mixed[here] = mixed[here] * shrink + nn(
                    vt_ref[here, at], expo.astype(BF16)
                )
            peak[h : h + 1] = new_peak

    block(i, True)

    @pl.loop(0, i - first_ref[i])
    def _(t):
        block(i - 1 - t, False)

    for h in range(heads):
        here = slice(h * HEAD_DIM, (h + 1) * HEAD_DIM)
        mixed[here] = mixed[here] / total[h : h + 1]
    o_ref[...] = mixed[...].T.astype(BF16)
    lse_ref[0] = peak[...] + jnp.log(total[...])


def attend(first, start, q, k, vt):
    length, cols = q.shape
    heads = cols // HEAD_DIM
    steps = length // TILE
    row = pl.BlockSpec((TILE, cols), lambda i, *_: (i, 0))
    return pl.pallas_call(
        functools.partial(attend_kernel, heads),
        out_shape=(
            jax.ShapeDtypeStruct((length, cols), BF16),
            jax.ShapeDtypeStruct((steps, heads, TILE), F32),
        ),
        grid_spec=pltpu.PrefetchScalarGridSpec(
            num_scalar_prefetch=1,
            grid=(steps,),
            in_specs=[
                pl.BlockSpec((1, TILE), lambda i, *_: (0, i)),
                row,
                pl.BlockSpec((length, cols), lambda i, *_: (0, 0)),
                pl.BlockSpec((cols, length), lambda i, *_: (0, 0)),
            ],
            out_specs=(
                row,
                pl.BlockSpec((1, heads, TILE), lambda i, *_: (i, 0, 0)),
            ),
            scratch_shapes=[
                pltpu.VMEM((heads, TILE), F32),
                pltpu.VMEM((heads, TILE), F32),
                pltpu.VMEM((cols, TILE), F32),
            ],
        ),
        compiler_params=pltpu.CompilerParams(vmem_limit_bytes=VMEM_LIMIT),
        cost_estimate=pl.CostEstimate(
            flops=4 * length * 1024 * cols,
            bytes_accessed=8 * length * cols,
            transcendentals=length * 1024 * heads,
        ),
        name="attend",
    )(first, start, q, k, vt)


def attend_back_kernel(
    heads, first_ref, start_ref, q_ref, k_ref, kt_ref, v_ref, o_ref, lse_ref, do_ref,
    cq_ref, sq_ref, ck_ref, sk_ref, grad_ref, dqt, dk_sum, dv_sum,
):
    i = pl.program_id(0)
    steps = pl.num_programs(0)
    width = q_ref.shape[1]
    queries = head_rows(q_ref[...], heads)
    grads = head_rows(do_ref[...], heads)
    start_row = start_ref[...]
    product = (do_ref[...].astype(F32) * o_ref[...].astype(F32)).T
    inner = [
        jnp.sum(product[h * HEAD_DIM : (h + 1) * HEAD_DIM], axis=0, keepdims=True)
        for h in range(heads)
    ]

    def block(j, first):
        at = pl.ds(pl.multiple_of(j * TILE, TILE), TILE)
        keys = k_ref[at, :]
        values = v_ref[at, :]
        mask = pair_mask(start_row, i, j)
        key_term = None
        value_term = None
        for h in range(heads):
            here = slice(h * HEAD_DIM, (h + 1) * HEAD_DIM)
            scores = nt(keys, queries[h])
            weights = jnp.where(mask, jnp.exp(scores - lse_ref[0, h : h + 1]), 0.0)
            grad_weights = nt(values, grads[h])
            grad_scores = (weights * (grad_weights - inner[h])).astype(BF16)
            term = nn(weights.astype(BF16), grads[h])
            value_term = term if value_term is None else value_term + term
            term = nn(grad_scores, queries[h])
            key_term = term if key_term is None else key_term + term
            term = nn(kt_ref[here, at], grad_scores)
            if first:
                dqt[here] = term
            else:
                dqt[here] = dqt[here] + term
        if first:
            dk_sum[at] = key_term
            dv_sum[at] = value_term
        else:
            dk_sum[at] = dk_sum[at] + key_term
            dv_sum[at] = dv_sum[at] + value_term

    block(i, True)

    @pl.loop(0, i - first_ref[i])
    def _(t):
        block(i - 1 - t, False)

    def unturn(grad, cosine, sine):
        grad = grad.astype(BF16).astype(F32)
        cosine = spread_lanes(cosine, width)
        sine = spread_lanes(sine, width)
        return (grad * cosine - swap_halves(grad) * sine).astype(BF16)

    rows = pl.ds(pl.multiple_of(i * TILE, TILE), TILE)
    grad_ref[rows, 0:width] = unturn(
        dqt[...].T * (HEAD_DIM**-0.5), cq_ref[rows, :], sq_ref[rows, :]
    )

    @pl.when(i == steps - 1)
    def _():
        @pl.loop(0, steps)
        def _(j):
            at = pl.ds(pl.multiple_of(j * TILE, TILE), TILE)
            grad_ref[at, width : 2 * width] = unturn(
                dk_sum[at], ck_ref[at, :], sk_ref[at, :]
            )
            grad_ref[at, 2 * width :] = dv_sum[at].astype(BF16)


def attend_back(first, start, q, k, kt, v, o, lse, do, tables):
    length, cols = q.shape
    heads = cols // HEAD_DIM
    steps = length // TILE
    row = pl.BlockSpec((TILE, cols), lambda i, *_: (i, 0))
    whole = pl.BlockSpec((length, cols), lambda i, *_: (0, 0))
    table = pl.BlockSpec((length, tables[0].shape[1]), lambda i, *_: (0, 0))
    return pl.pallas_call(
        functools.partial(attend_back_kernel, heads),
        out_shape=jax.ShapeDtypeStruct((length, 3 * cols), BF16),
        grid_spec=pltpu.PrefetchScalarGridSpec(
            num_scalar_prefetch=1,
            grid=(steps,),
            in_specs=[
                pl.BlockSpec((1, TILE), lambda i, *_: (0, i)),
                row,
                whole,
                pl.BlockSpec((cols, length), lambda i, *_: (0, 0)),
                whole,
                row,
                pl.BlockSpec((1, heads, TILE), lambda i, *_: (i, 0, 0)),
                row,
            ]
            + [table] * 4,
            out_specs=pl.BlockSpec((length, 3 * cols), lambda i, *_: (0, 0)),
            scratch_shapes=[
                pltpu.VMEM((cols, TILE), F32),
                pltpu.VMEM((length, cols), F32),
                pltpu.VMEM((length, cols), F32),
            ],
        ),
        compiler_params=pltpu.CompilerParams(vmem_limit_bytes=VMEM_LIMIT),
        cost_estimate=pl.CostEstimate(
            flops=10 * length * 1024 * cols,
            bytes_accessed=16 * length * cols,
            transcendentals=length * 1024 * heads,
        ),
        name="attend_back",
    )(first, start, q, k, kt, v, o, lse, do, *tables)


def upper_kernel(
    x_ref, wu_ref, c_ref, wd_ref, gain_ref, act_ref, slope_ref, grad_ref, stat_ref
):
    upper = nt(x_ref[...], wu_ref[...])
    grad = nn(c_ref[...], wd_ref[...])
    below = 0.5 * (1.0 + lax.erf(upper * (0.5**0.5)))
    act = upper * below
    slope = below + upper * (jnp.exp(-0.5 * upper * upper) * ((2.0 * math.pi) ** -0.5))
    act_ref[...] = act
    slope_ref[...] = slope.astype(BF16)
    grad_ref[...] = grad
    part = grad * gain_ref[...]
    average = jnp.mean(act, axis=-1, keepdims=True)
    centered = act - average
    spread = jnp.sum(centered * centered, axis=-1, keepdims=True)
    part_sum = jnp.sum(part, axis=-1, keepdims=True)
    cross = jnp.sum(part * centered, axis=-1, keepdims=True)
    lane = lax.broadcasted_iota(jnp.int32, (x_ref.shape[0], 128), 1)
    columns = jnp.where(
        lane == 0,
        average,
        jnp.where(lane == 1, spread, jnp.where(lane == 2, part_sum, cross)),
    )
    stat_ref[...] = columns.T[:8]


def upper_pass(x, w_up, cot, w_down, gain):
    length, width = x.shape
    feats = w_up.shape[0]
    rows = TILE
    row = pl.BlockSpec((rows, width), lambda i: (i, 0))
    out = pl.BlockSpec((rows, feats), lambda i: (i, 0))
    return pl.pallas_call(
        upper_kernel,
        grid=(length // rows,),
        out_shape=(
            jax.ShapeDtypeStruct((length, feats), F32),
            jax.ShapeDtypeStruct((length, feats), BF16),
            jax.ShapeDtypeStruct((length, feats), F32),
            jax.ShapeDtypeStruct((8, length), F32),
        ),
        in_specs=[
            row,
            pl.BlockSpec((feats, width), lambda i: (0, 0)),
            row,
            pl.BlockSpec((width, feats), lambda i: (0, 0)),
            pl.BlockSpec((1, feats), lambda i: (0, 0)),
        ],
        out_specs=(out, out, out, pl.BlockSpec((8, rows), lambda i: (0, i))),
        compiler_params=pltpu.CompilerParams(vmem_limit_bytes=VMEM_LIMIT),
        cost_estimate=pl.CostEstimate(
            flops=4 * length * width * feats,
            bytes_accessed=8 * length * width + 8 * length * feats,
            transcendentals=2 * length * feats,
        ),
        name="upper_pass",
    )(x, w_up, cot, w_down, gain)


def hidden_kernel(act_ref, slope_ref, grad_ref, stat_ref, gain_ref, hid_ref, gu_ref, gg_ref):
    i = pl.program_id(0)
    stats = stat_ref[...].T
    average = stats[:, 0:1]
    scale = stats[:, 1:2]
    part_mean = stats[:, 2:3]
    cross_mean = stats[:, 3:4]
    gain = gain_ref[...]
    normal = (act_ref[...] - average) * scale
    grad = grad_ref[...]
    hid_ref[...] = (normal * gain).astype(BF16)
    back = scale * (grad * gain - part_mean - normal * cross_mean)
    gu_ref[...] = (slope_ref[...].astype(F32) * back).astype(BF16)
    term = jnp.sum(grad * normal, axis=0, keepdims=True)

    @pl.when(i == 0)
    def _():
        gg_ref[...] = term

    @pl.when(i > 0)
    def _():
        gg_ref[...] = gg_ref[...] + term


def hidden_pass(act, slope, grad, stats, gain):
    length, feats = act.shape
    out = pl.BlockSpec((TILE, feats), lambda i: (i, 0))
    one = pl.BlockSpec((1, feats), lambda i: (0, 0))
    return pl.pallas_call(
        hidden_kernel,
        grid=(length // TILE,),
        out_shape=(
            jax.ShapeDtypeStruct((length, feats), BF16),
            jax.ShapeDtypeStruct((length, feats), BF16),
            jax.ShapeDtypeStruct((1, feats), F32),
        ),
        in_specs=[out, out, out, pl.BlockSpec((8, TILE), lambda i: (0, i)), one],
        out_specs=(out, out, one),
        compiler_params=pltpu.CompilerParams(vmem_limit_bytes=VMEM_LIMIT),
        cost_estimate=pl.CostEstimate(
            flops=12 * length * feats,
            bytes_accessed=14 * length * feats,
            transcendentals=0,
        ),
        name="hidden_pass",
    )(act, slope, grad, stats, gain)


def ffn_kernel(
    n, x_ref, wu_ref, cot_ref, wd_ref, gain_ref,
    full_ref, hid_ref, gu_ref, gg_ref,
    rows_in, wd, cot_in, act, slope, grad, stat, held, results,
    local_sem, cot_sem, out_sem, full_sem, send_sem, recv_sem, stat_send, stat_recv,
):
    me, twin, near_x, near_y, across = places()
    rows = x_ref.shape[0]
    feats = wu_ref.shape[0]

    def cut(i, size=rows):
        return pl.ds(pl.multiple_of(i * size, size), size)

    own = pltpu.make_async_copy(x_ref, rows_in.at[me], local_sem.at[0])
    own.start()
    load_wd = pltpu.make_async_copy(wd_ref, wd, local_sem.at[1])
    load_wd.start()

    def load_cot(i, slot):
        return pltpu.make_async_copy(
            cot_ref.at[cut(i)], cot_in.at[slot], cot_sem.at[slot]
        )

    load_cot(0, 0).start()
    meet([lax.rem(me + k, n) for k in range(1, n)])
    sends = gather_copies(x_ref, rows_in, send_sem, recv_sem)
    for k in range(5):
        sends[k].start()

    load_wd.wait()
    def incoming(first, last):
        @pl.loop(first, last)
        def _(i):
            slot = lax.rem(i, 2)

            @pl.when(i + 1 < n)
            def _():
                load_cot(i + 1, 1 - slot).start()

            load_cot(i, slot).wait()
            grad[cut(i)] = nn(cot_in[slot], wd[...])

    incoming(0, n - 2)
    sends[0].wait_recv()
    sends[5].start()
    sends[7].start()
    sends[1].wait_recv()
    sends[6].start()
    sends[8].start()
    incoming(n - 2, n)
    own.wait()

    def keep(b):
        return pltpu.make_async_copy(rows_in.at[b], full_ref.at[b], full_sem.at[b])

    @pl.loop(0, n)
    def _(i):
        @pl.when(i == 1)
        def _():
            sends[4].wait_recv()

        @pl.when(i == 2)
        def _():
            sends[2].wait_recv()
            sends[9].start()
            sends[3].wait_recv()
            sends[10].start()

        @pl.when(i == 4)
        def _():
            sends[7].wait_recv()
            sends[9].wait_recv()

        @pl.when(i == 5)
        def _():
            sends[8].wait_recv()
            sends[10].wait_recv()
            sends[5].wait_recv()
            sends[11].start()
            sends[6].wait_recv()
            sends[12].start()

        @pl.when(i == 7)
        def _():
            sends[11].wait_recv()
            sends[12].wait_recv()

        other = jnp.where((i == 1) | (i == 4) | (i == 5) | (i == 7), twin, 0)
        place = jnp.where(i < 2, me, jnp.where(i >= 6, across, jnp.where(lax.rem(i, 2) == 0, near_x, near_y)))
        b = place + other
        keep(b).start()
        at = cut(b)
        upper = nt(rows_in[b], wu_ref[...])
        below = 0.5 * (1.0 + lax.erf(upper * (0.5**0.5)))
        value = upper * below
        act[at] = value
        slope[at] = (
            below + upper * (jnp.exp(-0.5 * upper * upper) * ((2.0 * math.pi) ** -0.5))
        ).astype(BF16)
        part = grad[at] * gain_ref[...]
        average = jnp.mean(value, axis=-1, keepdims=True)
        centered = value - average
        spread = jnp.sum(centered * centered, axis=-1, keepdims=True)
        part_sum = jnp.sum(part, axis=-1, keepdims=True)
        cross = jnp.sum(part * centered, axis=-1, keepdims=True)
        lane = lax.broadcasted_iota(jnp.int32, (rows, 128), 1)
        columns = jnp.where(
            lane == 0,
            average,
            jnp.where(lane == 1, spread, jnp.where(lane == 2, part_sum, cross)),
        )
        stat[:, at] = columns.T[:8]

    held[me] = stat[...]
    rounds = [
        remote(
            stat, held.at[me], stat_send.at[k], stat_recv.at[k], lax.rem(me + k, n)
        )
        for k in range(1, n)
    ]
    for send in rounds:
        send.start()
    for send in rounds:
        send.wait()
    join_rows(n, feats, held, stat)

    def store(i, slot):
        return [
            pltpu.make_async_copy(
                results.at[slot, j], ref.at[cut(i)], out_sem.at[slot, j]
            )
            for j, ref in enumerate((hid_ref, gu_ref))
        ]

    gg_ref[...] = jnp.zeros_like(gg_ref)

    @pl.loop(0, n)
    def _(i):
        slot = lax.rem(i, 2)

        @pl.when(i >= 2)
        def _():
            for copy in store(i - 2, slot):
                copy.wait()

        at = cut(i)
        stats = stat[:, at].T
        gain = gain_ref[...]
        scale = stats[:, 1:2]
        normal = (act[at] - stats[:, 0:1]) * scale
        coming = grad[at]
        results[slot, 0] = (normal * gain).astype(BF16)
        back = scale * (coming * gain - stats[:, 2:3] - normal * stats[:, 3:4])
        results[slot, 1] = (slope[at].astype(F32) * back).astype(BF16)
        gg_ref[...] = gg_ref[...] + jnp.sum(coming * normal, axis=0, keepdims=True)
        for copy in store(i, slot):
            copy.start()

    for i in (n - 2, n - 1):
        for copy in store(i, i % 2):
            copy.wait()
    for b in range(n):
        keep(b).wait()
    for send in sends:
        send.wait_send()


def ffn_pass(ffn_in, w_up, cot, w_down, gain, collective_id):
    n = lax.axis_size("seq")
    rows, width = ffn_in.shape
    feats = w_up.shape[0]
    if n != 8:
        full = lax.all_gather(ffn_in, "seq", axis=0, tiled=True)
        act, slope, grad, stat = upper_pass(full, w_up, cot, w_down, gain)
        stats = join_stats(stat, feats, collective_id)
        return (full, *hidden_pass(act, slope, grad, stats, gain))
    length = n * rows
    dma = pltpu.SemaphoreType.DMA
    low = jax.ShapeDtypeStruct((length, feats), BF16)
    full, hidden, grad_upper, gain_grad = pl.pallas_call(
        functools.partial(ffn_kernel, n),
        out_shape=(
            jax.ShapeDtypeStruct((n, rows, width), BF16),
            low,
            low,
            jax.ShapeDtypeStruct((1, feats), F32),
        ),
        in_specs=[INSIDE, INSIDE, ANY, ANY, INSIDE],
        out_specs=(ANY, ANY, ANY, INSIDE),
        scratch_shapes=[
            pltpu.VMEM((n, rows, width), BF16),
            pltpu.VMEM((width, feats), BF16),
            pltpu.VMEM((2, rows, width), BF16),
            pltpu.VMEM((length, feats), F32),
            pltpu.VMEM((length, feats), BF16),
            pltpu.VMEM((length, feats), F32),
            pltpu.VMEM((8, length), F32),
            pltpu.VMEM((n, 8, length), F32),
            pltpu.VMEM((2, 2, rows, feats), BF16),
            dma((2,)),
            dma((2,)),
            dma((2, 2)),
            dma((n,)),
            dma((13,)),
            dma((13,)),
            dma((n,)),
            dma((n,)),
        ],
        compiler_params=pltpu.CompilerParams(
            collective_id=collective_id, has_side_effects=True, vmem_limit_bytes=VMEM_LIMIT
        ),
        name="ffn_pass",
    )(ffn_in, w_up, cot, w_down, gain)
    return full.reshape(length, width), hidden, grad_upper, gain_grad


def join_rows(n, feats, held, o_ref):
    average = held[0, 0:1]
    for d in range(1, n):
        average = average + held[d, 0:1]
    average = average * (1.0 / n)
    spread = jnp.zeros_like(average)
    part = jnp.zeros_like(average)
    cross = jnp.zeros_like(average)
    for d in range(n):
        shift = held[d, 0:1] - average
        spread = spread + held[d, 1:2] + feats * (shift * shift)
        part = part + held[d, 2:3]
        cross = cross + held[d, 3:4] + shift * held[d, 2:3]
    whole = 1.0 / (n * feats)
    scale = lax.rsqrt(spread * whole + EPSILON)
    o_ref[0:1] = average
    o_ref[1:2] = scale
    o_ref[2:3] = part * whole
    o_ref[3:4] = cross * scale * whole
    o_ref[4:8] = jnp.zeros((4, average.shape[1]), F32)


def stat_kernel(n, feats, x_ref, o_ref, held, send_sem, recv_sem):
    me = lax.axis_index("seq")
    held[me] = x_ref[...]
    meet([lax.rem(me + k, n) for k in range(1, n)])
    copies = [
        remote(x_ref, held.at[me], send_sem.at[k], recv_sem.at[k], lax.rem(me + k, n))
        for k in range(1, n)
    ]
    for copy in copies:
        copy.start()
    for copy in copies:
        copy.wait()
    join_rows(n, feats, held, o_ref)


def join_stats(stat, feats, collective_id):
    n = lax.axis_size("seq")
    inside = pl.BlockSpec(memory_space=pltpu.VMEM)
    return pl.pallas_call(
        functools.partial(stat_kernel, n, feats),
        out_shape=jax.ShapeDtypeStruct(stat.shape, F32),
        in_specs=[inside],
        out_specs=inside,
        scratch_shapes=[
            pltpu.VMEM((n, *stat.shape), F32),
            pltpu.SemaphoreType.DMA((n,)),
            pltpu.SemaphoreType.DMA((n,)),
        ],
        compiler_params=pltpu.CompilerParams(
            collective_id=collective_id, has_side_effects=True, vmem_limit_bytes=VMEM_LIMIT
        ),
        name="join_stats",
    )(stat)


def weight_kernel(a_ref, b_ref, o_ref):
    o_ref[...] = tn(a_ref[...], b_ref[...]).astype(BF16)


def weight_grad(a, b):
    length, outs = a.shape
    cols = b.shape[1]
    block = 2 * TILE
    return pl.pallas_call(
        weight_kernel,
        grid=(outs // block,),
        out_shape=jax.ShapeDtypeStruct((outs, cols), BF16),
        in_specs=[
            pl.BlockSpec((length, block), lambda i: (0, i)),
            pl.BlockSpec((length, cols), lambda i: (0, 0)),
        ],
        out_specs=pl.BlockSpec((block, cols), lambda i: (i, 0)),
        compiler_params=pltpu.CompilerParams(vmem_limit_bytes=VMEM_LIMIT),
        cost_estimate=pl.CostEstimate(
            flops=2 * length * outs * cols,
            bytes_accessed=2 * (length * outs + length * cols + outs * cols),
            transcendentals=0,
        ),
        name="weight_grad",
    )(a, b)


STEP = 32


def mix_kernel(att_ref, x_ref, w_ref, gm_ref, gf_ref, mix_ref, mid_ref, ffn_ref):
    j = pl.program_id(0)
    rows = att_ref.shape[0]
    cols = w_ref.shape[0]

    @pl.when(j == 0)
    def _():
        @pl.loop(0, rows // STEP)
        def _(r):
            at = pl.ds(pl.multiple_of(r * STEP, STEP), STEP)
            normal, _ = norm_parts(att_ref[at].astype(F32))
            mix_ref[at] = (normal * gm_ref[...]).astype(BF16)

    here = pl.ds(pl.multiple_of(j * cols, cols), cols)
    mid_ref[:, here] = x_ref[:, here].astype(F32) + nt(mix_ref[...], w_ref[...])

    @pl.when(j == pl.num_programs(0) - 1)
    def _():
        @pl.loop(0, rows // STEP)
        def _(r):
            at = pl.ds(pl.multiple_of(r * STEP, STEP), STEP)
            normal, _ = norm_parts(mid_ref[at])
            ffn_ref[at] = (normal * gf_ref[...]).astype(BF16)


def mix_pass(attended, x, w_out, gain_mix, gain_ffn):
    rows, width = x.shape
    cols = TILE
    n = width // cols
    whole = pl.BlockSpec((rows, width), lambda j: (0, 0))
    gain = pl.BlockSpec((1, width), lambda j: (0, 0))
    low = jax.ShapeDtypeStruct((rows, width), BF16)
    return pl.pallas_call(
        mix_kernel,
        grid=(n,),
        out_shape=(low, jax.ShapeDtypeStruct((rows, width), F32), low),
        in_specs=[
            whole,
            whole,
            pl.BlockSpec((cols, width), lambda j: (j, 0)),
            gain,
            gain,
        ],
        out_specs=(whole, whole, whole),
        compiler_params=pltpu.CompilerParams(vmem_limit_bytes=VMEM_LIMIT),
        cost_estimate=pl.CostEstimate(
            flops=2 * rows * width * width,
            bytes_accessed=2 * width * width + 12 * rows * width,
            transcendentals=0,
        ),
        name="mix_pass",
    )(attended, x, w_out, gain_mix[None], gain_ffn[None])


def branch_kernel(
    g_ref, mid_ref, cot_ref, att_ref, w_ref, gm_ref, gf_ref,
    gmid_ref, gbr_ref, gatt_ref, ggf_ref, ggm_ref, total,
):
    j = pl.program_id(0)
    rows = att_ref.shape[0]
    cols = w_ref.shape[0]

    @pl.when(j == 0)
    def _():
        ggf_ref[...] = jnp.zeros_like(ggf_ref)
        total[...] = jnp.zeros_like(total)

        @pl.loop(0, rows // STEP)
        def _(r):
            at = pl.ds(pl.multiple_of(r * STEP, STEP), STEP)
            normal, scale = norm_parts(mid_ref[at])
            part, gain_part = norm_back(g_ref[at], normal, scale, gf_ref[...])
            ggf_ref[...] += gain_part[None]
            grad = cot_ref[at].astype(F32) + part
            gmid_ref[at] = grad
            gbr_ref[at] = grad.astype(BF16)

    here = pl.ds(pl.multiple_of(j * cols, cols), cols)
    total[...] += nn(gbr_ref[:, here], w_ref[...])

    @pl.when(j == pl.num_programs(0) - 1)
    def _():
        ggm_ref[...] = jnp.zeros_like(ggm_ref)

        @pl.loop(0, rows // STEP)
        def _(r):
            at = pl.ds(pl.multiple_of(r * STEP, STEP), STEP)
            normal, scale = norm_parts(att_ref[at].astype(F32))
            part, gain_part = norm_back(total[at], normal, scale, gm_ref[...])
            ggm_ref[...] += gain_part[None]
            gatt_ref[at] = part.astype(BF16)


def branch_pass(grad_ffn_in, middle, cot, attended, w_out, gain_mix, gain_ffn):
    rows, width = cot.shape
    cols = TILE
    n = width // cols
    whole = pl.BlockSpec((rows, width), lambda j: (0, 0))
    gain = pl.BlockSpec((1, width), lambda j: (0, 0))
    low = jax.ShapeDtypeStruct((rows, width), BF16)
    sums = jax.ShapeDtypeStruct((1, width), F32)
    return pl.pallas_call(
        branch_kernel,
        grid=(n,),
        out_shape=(jax.ShapeDtypeStruct((rows, width), F32), low, low, sums, sums),
        in_specs=[
            whole,
            whole,
            whole,
            whole,
            pl.BlockSpec((cols, width), lambda j: (j, 0)),
            gain,
            gain,
        ],
        out_specs=(whole, whole, whole, gain, gain),
        scratch_shapes=[pltpu.VMEM((rows, width), F32)],
        compiler_params=pltpu.CompilerParams(vmem_limit_bytes=VMEM_LIMIT),
        cost_estimate=pl.CostEstimate(
            flops=2 * rows * width * width,
            bytes_accessed=2 * width * width + 20 * rows * width,
            transcendentals=0,
        ),
        name="branch_pass",
    )(grad_ffn_in, middle, cot, attended, w_out, gain_mix[None], gain_ffn[None])


CHUNK = 64


def finish_kernel(
    n, depth, gq_ref, gd_ref, pw_ref, pn_ref, po_ref, x_ref, grad_ref, mid_ref, ga_ref, gm_ref, gf_ref, gh_ref,
    oq_ref, od_ref, ow_ref, gi_ref, out_ref, sums_ref,
    own, twin_in, held, zown, zin, stage, gain_here, gain_row, gain_pack, gain_line,
    local_sem, load_sem, stage_sem, send_sem, recv_sem, keep_sem,
    up_send, up_recv, down_send, down_recv, home_send, home_recv, gain_send, gain_recv,
):
    me, twin, near_x, near_y, across = places()
    z = lax.axis_index("batch")
    rows, width = pn_ref.shape[1:]
    half = rows // 2
    low, high = pl.ds(0, half), pl.ds(half, half)
    mine = (across, near_x, near_y, me)
    _, chunk, cols = zown.shape
    across_width = width // cols
    per_part = (gq_ref.shape[1] // chunk) * across_width
    turned = gq_ref.shape[0] * per_part
    per_source = gd_ref.shape[1] // chunk
    outer = turned + gd_ref.shape[0] * per_source
    chunks = zown.shape[0]
    per_side = chunks // 2

    def cut(i, size):
        return pl.ds(pl.multiple_of(i * size, size), size)

    def wide(i):
        return cut(i // across_width, chunk), cut(lax.rem(i, across_width), cols)

    line_loads = []
    for g in range(turned):
        source = gq_ref.at[(g // per_part, *wide(g % per_part))]
        line_loads.append(pltpu.make_async_copy(source, zown.at[g], load_sem.at[g]))
    for g in range(turned, outer):
        source = gd_ref.at[
            (g - turned) // per_source, cut((g - turned) % per_source, chunk)
        ]
        line_loads.append(pltpu.make_async_copy(source, zown.at[g], load_sem.at[g]))
    for load in line_loads:
        load.start()
    partials = (pw_ref, pn_ref, po_ref)
    loads = [
        [
            pltpu.make_async_copy(p.at[block], own.at[m, i], local_sem.at[4 * m + i])
            for i, block in enumerate(mine)
        ]
        for m, p in enumerate(partials)
    ]
    for part in loads:
        for load in part:
            load.start()
    meet_all(n, depth)

    def copy(m, k, src, dst, partner):
        return remote(src, dst, send_sem.at[m, k], recv_sem.at[m, k], partner)

    twins = [
        [
            copy(m, i, p.at[block + twin], twin_in.at[m, i], me + twin)
            for i, block in enumerate(mine)
        ]
        for m, p in enumerate(partials)
    ]
    sends = [
        [
            copy(m, 4, own.at[m, 0, low], held.at[m, 0], near_x),
            copy(m, 5, own.at[m, 0, high], held.at[m, 1], near_y),
            copy(m, 6, own.at[m, 1, low], held.at[m, 2], near_x),
            copy(m, 7, own.at[m, 2, high], held.at[m, 3], near_y),
            copy(m, 8, own.at[m, 1, high], held.at[m, 4], near_x),
            copy(m, 9, own.at[m, 2, low], held.at[m, 5], near_y),
        ]
        for m in range(3)
    ]
    for part in twins:
        for send in part:
            send.start()

    def add_twin(m, i):
        loads[m][i].wait()
        twins[m][i].wait_recv()

        @pl.loop(0, rows // STEP)
        def _(r):
            at = cut(r, STEP)
            own[m, i, at] = (
                own[m, i, at].astype(F32) + twin_in[m, i, at].astype(F32)
            ).astype(BF16)

    def add_held(m, i, base, slot):
        @pl.loop(0, half // STEP)
        def _(r):
            at = cut(r, STEP)
            to = pl.ds(pl.multiple_of(base + r * STEP, STEP), STEP)
            own[m, i, to] = (
                own[m, i, to].astype(F32) + held[m, slot, at].astype(F32)
            ).astype(BF16)

    def first(m):
        add_twin(m, 0)
        sends[m][0].start()
        sends[m][1].start()
        add_twin(m, 1)
        sends[m][2].start()
        add_twin(m, 2)
        sends[m][3].start()

    def second(m):
        sends[m][1].wait_recv()
        add_held(m, 1, half, 1)
        sends[m][4].start()
        sends[m][0].wait_recv()
        add_held(m, 2, 0, 0)
        sends[m][5].start()

    def last(m, store):
        loads[m][3].wait()
        twins[m][3].wait_recv()
        for k in (2, 3, 4, 5):
            sends[m][k].wait_recv()
        for base, one, two in ((0, 2, 5), (half, 3, 4)):

            @pl.loop(0, half // STEP)
            def _(r):
                at = cut(r, STEP)
                place = base + r * STEP
                to = pl.ds(pl.multiple_of(place, STEP), STEP)
                store(
                    place,
                    to,
                    own[m, 3, to].astype(F32)
                    + twin_in[m, 3, to].astype(F32)
                    + held[m, one, at].astype(F32)
                    + held[m, two, at].astype(F32),
                )

    def store_line(place, to, value):
        value = value.astype(BF16)
        for side in range(across_width):
            zown[
                outer + (place // chunk) * across_width + side,
                pl.ds(pl.multiple_of(lax.rem(place, chunk), STEP), STEP),
            ] = value[:, side * cols : (side + 1) * cols]

    def store_inputs(place, to, value):
        normal, scale = norm_parts(x_ref[to].astype(F32))
        part, gain_part = norm_back(value, normal, scale, ga_ref[...])
        gi_ref[to] = grad_ref[to] + part
        gain_here[0:1] = gain_here[0:1] + gain_part[None]

    def store_outputs(place, to, value):
        out_ref[to] = (mid_ref[to] + value).astype(BF16)

    def home(part):
        block = part * n + me
        return block // 3, lax.rem(block, 3)

    def deliver_far(g):
        target, slot = home(g // per_part)
        piece = lax.rem(g, per_part)
        return remote(
            zin.at[g],
            oq_ref.at[(slot, *wide(piece))],
            home_send.at[g],
            home_recv.at[slot, piece],
            target,
        )

    def deliver_near(g):
        _, slot = home(g // per_part)
        return pltpu.make_async_copy(
            zin.at[g], oq_ref.at[(slot, *wide(lax.rem(g, per_part)))], keep_sem.at[g]
        )

    def widen(g):
        @pl.loop(0, chunk // STEP)
        def _(r):
            at = cut(r, STEP)
            stage[at] = zin[g, at].astype(F32)

    def deliver(g):
        target, _ = home(g // per_part)

        @pl.when((g < turned) & (target != me))
        def _():
            deliver_far(g).start()

        @pl.when((g < turned) & (target == me))
        def _():
            deliver_near(g).start()

        @pl.when((g >= turned) & (g < outer))
        def _():
            widen(g)
            at = g - turned
            place = cut(lax.rem(at, per_source), chunk), cut(at // per_source, cols)
            store = pltpu.make_async_copy(stage, od_ref.at[place], stage_sem)
            store.start()
            store.wait()

        @pl.when(g >= outer)
        def _():
            widen(g)
            store = pltpu.make_async_copy(
                stage, ow_ref.at[wide(g - outer)], stage_sem
            )
            store.start()
            store.wait()

    def delivered(g):
        target, _ = home(g // per_part)

        @pl.when(target != me)
        def _():
            deliver_far(g).wait_send()

        @pl.when(target == me)
        def _():
            deliver_near(g).wait()

    def go_up(g, ahead):
        return line_remote(zown.at[g], zin.at[g], up_send.at[g], up_recv.at[g], ahead)

    def go_down(g, behind):
        return line_remote(
            zin.at[g], zin.at[g], down_send.at[g], down_recv.at[g], behind
        )

    def ranks(side):
        if side == 0:
            return z, z + 1, z - 1
        return depth - 1 - z, z - 1, z + 1

    def add_line(g, target):
        @pl.loop(0, chunk // STEP)
        def _(r):
            at = cut(r, STEP)
            target[g, at] = (zown[g, at].astype(F32) + zin[g, at].astype(F32)).astype(
                BF16
            )

    lead = 2
    far = 2 * (depth - 1)
    steps = per_side + 2 * far

    def line_enter(c):
        for side in (0, 1):
            rank, ahead, _ = ranks(side)

            @pl.when(rank == 0)
            def _():
                go_up(2 * c + side, ahead).start()

    def line_step(t):
        @pl.when(t + lead < per_side)
        def _():
            line_enter(t + lead)

        back = []
        for side in (0, 1):
            rank, ahead, behind = ranks(side)
            c_back = t - 2 * far + 2 * rank
            g_back = 2 * c_back + side
            there = (c_back >= 0) & (c_back < per_side) & (rank < depth - 1)
            back.append((there, g_back))

            @pl.when(there)
            def _():
                go_down(g_back, ahead).wait_recv()

            @pl.when(there & (rank > 0))
            def _():
                go_down(g_back, behind).start()

        for side in (0, 1):
            rank, ahead, behind = ranks(side)
            c = t - 2 * rank
            g = 2 * c + side
            there = (c >= 0) & (c < per_side)

            @pl.when(there & (rank > 0) & (rank < depth - 1))
            def _():
                go_up(g, behind).wait_recv()
                add_line(g, zown)
                go_up(g, ahead).start()

            @pl.when(there & (rank == depth - 1))
            def _():
                go_up(g, behind).wait_recv()
                add_line(g, zin)
                go_down(g, behind).start()
                deliver(g)

        for there, g_back in back:

            @pl.when(there)
            def _():
                deliver(g_back)

    def line_steps(first_step, last_step):
        @pl.loop(first_step, last_step)
        def _(t):
            line_step(t)

    gain_here[...] = jnp.zeros_like(gain_here)
    for load in line_loads:
        load.wait()
    for c in range(lead):
        line_enter(c)
    first(0)
    line_steps(0, 8)
    second(0)
    line_steps(8, 9)
    first(1)
    line_steps(9, 18)
    last(0, store_line)
    line_steps(18, 20)
    second(1)
    line_steps(20, 21)
    first(2)
    line_steps(21, 28)
    last(1, store_inputs)

    gain_here[1:2] = gm_ref[...]
    gain_here[2:3] = gf_ref[...]
    gain_here[3:4, 0 : gh_ref.shape[1]] = gh_ref[...]
    gain_row[me] = gain_here[...]
    rounds = [
        remote(
            gain_here,
            gain_row.at[me],
            gain_send.at[0, k],
            gain_recv.at[0, k],
            lax.rem(me + k, n),
        )
        for k in range(1, n)
    ]
    for send in rounds:
        send.start()
    line_steps(28, 32)
    second(2)
    line_steps(32, 40)
    last(2, store_outputs)
    line_steps(40, 42)
    for send in rounds:
        send.wait()
    total = gain_row[0]
    for d in range(1, n):
        total = total + gain_row[d]
    gain_pack[0:8] = total
    for d in range(n):
        gain_pack[8 + d : 9 + d] = gain_row[d, 3:4]
    gain_line[z] = gain_pack[...]
    rounds = [
        line_remote(
            gain_pack,
            gain_line.at[z],
            gain_send.at[1, k],
            gain_recv.at[1, k],
            lax.rem(z + k, depth),
        )
        for k in range(1, depth)
    ]
    for send in rounds:
        send.start()
    line_steps(42, steps)
    for send in rounds:
        send.wait()
    total = gain_line[0]
    for d in range(1, depth):
        total = total + gain_line[d]
    sums_ref[...] = total

    for m in range(3):
        for send in twins[m] + sends[m]:
            send.wait_send()
    for g in range(chunks):
        rank, ahead, behind = ranks(g % 2)

        @pl.when(rank < depth - 1)
        def _():
            go_up(g, ahead).wait_send()

        @pl.when(rank > 0)
        def _():
            go_down(g, behind).wait_send()

    for g in range(turned):
        delivered(g)
    for slot in range(3):
        block = 3 * me + slot
        source = lax.rem(block, n)

        @pl.when(source != me)
        def _():
            for piece in range(per_part):
                remote(
                    zin.at[0],
                    oq_ref.at[(slot, *wide(piece))],
                    home_send.at[0],
                    home_recv.at[slot, piece],
                    source,
                ).wait_recv()


def finish(
    grad_qkv, grad_down, part_out, part_normed, part_outputs, x, grad_middle, middle, gain, gains, collective_id
):
    n, depth = lax.axis_size("seq"), lax.axis_size("batch")
    rows, width = part_out.shape[0] // n, part_out.shape[1]
    cols = grad_qkv.shape[1]
    sources, _, feats = grad_down.shape
    if n != 8 or depth != 4:
        me = lax.axis_index("seq")
        blocks = lax.psum(grad_qkv, "batch")
        back = [
            lax.ppermute(
                give_part(blocks, me, n, j),
                "seq",
                [((3 * d + j) % n, d) for d in range(n)],
            )
            for j in range(3)
        ]
        w_out = lax.psum(scatter_seq(part_out, None).astype(BF16), "batch")
        normal, scale = norm_parts(x.astype(F32))
        part, gain_part = norm_back(scatter_seq(part_normed, None), normal, scale, gain)
        shared = [lax.psum(g, ("batch", "seq")) for g in (gain_part, gains[0][0], gains[1][0])]
        hidden = lax.all_gather(lax.psum(gains[2][0], "batch"), "seq", axis=0, tiled=True)
        down = lax.psum(grad_down, "batch")
        return (
            jnp.concatenate(back, axis=0),
            jnp.swapaxes(down, 0, 1).reshape(rows, sources * feats).astype(F32),
            w_out.astype(F32),
            grad_middle + part,
            (middle + scatter_seq(part_outputs, None)).astype(BF16),
            (*shared, hidden),
        )
    chunks = (
        3 * cols * width + rows * width + sources * rows * feats
    ) // (CHUNK * feats)
    dma = pltpu.SemaphoreType.DMA
    line = pltpu.VMEM((chunks, CHUNK, feats), BF16)
    w_qkv, w_down, w_out, grad_inputs, outputs, sums = pl.pallas_call(
        functools.partial(finish_kernel, n, depth),
        out_shape=(
            jax.ShapeDtypeStruct((3, cols, width), BF16),
            jax.ShapeDtypeStruct((rows, sources * feats), F32),
            jax.ShapeDtypeStruct((rows, width), F32),
            jax.ShapeDtypeStruct((rows, width), F32),
            jax.ShapeDtypeStruct((rows, width), BF16),
            jax.ShapeDtypeStruct((16, width), F32),
        ),
        in_specs=[ANY] * 5 + [INSIDE] * 7,
        out_specs=(ANY, ANY, ANY, INSIDE, INSIDE, INSIDE),
        scratch_shapes=[
            pltpu.VMEM((3, 4, rows, width), BF16),
            pltpu.VMEM((3, 4, rows, width), BF16),
            pltpu.VMEM((3, 6, rows // 2, width), BF16),
            line,
            line,
            pltpu.VMEM((CHUNK, feats), F32),
            pltpu.VMEM((8, width), F32),
            pltpu.VMEM((n, 8, width), F32),
            pltpu.VMEM((16, width), F32),
            pltpu.VMEM((depth, 16, width), F32),
            dma((12,)),
            dma((chunks,)),
            dma,
            dma((3, 10)),
            dma((3, 10)),
            dma((chunks,)),
            dma((chunks,)),
            dma((chunks,)),
            dma((chunks,)),
            dma((chunks,)),
            dma((chunks,)),
            dma((3, cols * width // (CHUNK * feats))),
            dma((2, n)),
            dma((2, n)),
        ],
        compiler_params=pltpu.CompilerParams(
            collective_id=collective_id,
            has_side_effects=True,
            vmem_limit_bytes=VMEM_LIMIT,
        ),
        name="finish",
    )(
        grad_qkv,
        grad_down,
        *[p.reshape(n, rows, width) for p in (part_out, part_normed, part_outputs)],
        x,
        grad_middle,
        middle,
        gain[None],
        *gains,
    )
    return (
        w_qkv.reshape(3 * cols, width),
        w_down,
        w_out,
        grad_inputs,
        outputs,
        (sums[0], sums[1], sums[2], sums[8:, :feats].reshape(-1)),
    )


def body(
    inputs,
    segment_ids,
    w_qkv,
    w_out,
    w_up,
    w_down,
    gain_attn,
    gain_mix,
    gain_ffn,
    gain_hidden,
    cotangent,
):
    _, local, width = inputs.shape
    n, depth = lax.axis_size("seq"), lax.axis_size("batch")
    me = lax.axis_index("seq")
    length = local * n
    feats = w_up.shape[0]
    x_low = inputs[0]
    x = x_low.astype(F32)
    cot = cotangent[0]
    segment = segment_ids[0]

    w_out_full = lax.all_gather(w_out, "seq", axis=0, tiled=True)
    normed = (norm_parts(x)[0] * gain_attn).astype(BF16)
    before = [jnp.sum((segment < d).astype(jnp.int32)) for d in range(1, DOCS)]
    start = jnp.zeros_like(segment)
    for d in range(1, DOCS):
        start = jnp.where(segment == d, before[d - 1], start)
    positions = jnp.arange(length, dtype=jnp.int32) - start
    first = start[::TILE] // TILE
    start_row = start[None, :]

    normed_full, w_heads, w_down_cols, tables = start_exchange(
        normed, w_qkv, w_down, positions.astype(F32), 1
    )
    cot_full = lax.all_gather(lax.optimization_barrier(cot), "seq", axis=0, tiled=True)

    q, k, v, kt, vt = project_qkv(normed_full, w_heads, tables)
    attended_heads, lse = attend(first, start_row, q, k, vt)
    attended = heads_to_tokens(attended_heads, 2)
    mix_in, middle, ffn_in = mix_pass(attended, x_low, w_out_full, gain_mix, gain_ffn)
    gain_here = lax.dynamic_slice_in_dim(gain_hidden, me * feats, feats, 0)[None, :]
    ffn_full, hidden, grad_upper, grad_gain_here = ffn_pass(
        ffn_in, w_up, cot_full, w_down_cols, gain_here, 3
    )

    grad_w_up = tn(grad_upper, ffn_full).astype(BF16)
    grad_upper, grad_w_up = lax.optimization_barrier((grad_upper, grad_w_up))
    grad_w_up = lax.psum(grad_w_up, "batch")
    grad_w_down = weight_grad(cot_full, hidden).reshape(n, local, feats)
    grad_upper, grad_w_down = lax.optimization_barrier((grad_upper, grad_w_down))
    grad_ffn_in = scatter_seq(nn(grad_upper, w_up).astype(BF16), 4)
    grad_middle, grad_branch, grad_att, grad_gain_ffn, grad_gain_mix = branch_pass(
        grad_ffn_in, middle, cot, attended, w_out_full, gain_mix, gain_ffn
    )
    grad_heads = tokens_to_heads(grad_att, 5)
    grad_w_down, grad_heads = lax.optimization_barrier((grad_w_down, grad_heads))
    grad_w_down = lax.all_to_all(grad_w_down, "seq", split_axis=0, concat_axis=0, tiled=True)
    grads = attend_back(
        first, start_row, q, k, kt, v, attended_heads, lse, grad_heads, tables
    )
    grad_w_qkv, grad_w_down, grad_w_out, grad_inputs, outputs, gains = finish(
        tn(grads, normed_full).astype(BF16).reshape(3, -1, width),
        grad_w_down,
        tn(grad_branch, mix_in).astype(BF16),
        nn(grads, w_heads).astype(BF16),
        nt(hidden, w_down_cols).astype(BF16),
        x_low,
        grad_middle,
        middle,
        gain_attn,
        (grad_gain_mix, grad_gain_ffn, grad_gain_here),
        6,
    )
    return (
        outputs[None],
        grad_inputs[None],
        grad_w_qkv.astype(F32),
        grad_w_out,
        grad_w_up.astype(F32),
        grad_w_down,
        *gains,
    )


def pick_part(turned, me, n, part):
    chosen = turned[0]
    home = part * n + me
    for j in (1, 2):
        chosen = jnp.where(lax.rem(home, 3) == j, turned[j], chosen)
    return chosen


def give_part(blocks, me, n, j):
    chosen = blocks[0]
    for part in (1, 2):
        chosen = jnp.where(lax.rem(part * n + me, 3) == j, blocks[part], chosen)
    return chosen


def solution(mesh):
    in_specs = (
        P("batch", "seq", None),
        P("batch", None),
        P("seq", None),
        P("seq", None),
        P("seq", None),
        P("seq", None),
        P(),
        P(),
        P(),
        P(),
        P("batch", "seq", None),
    )
    out_specs = (
        P("batch", "seq", None),
        P("batch", "seq", None),
        P("seq", None),
        P("seq", None),
        P("seq", None),
        P("seq", None),
        P(),
        P(),
        P(),
        P(),
    )
    return jax.shard_map(body, mesh=mesh, in_specs=in_specs, out_specs=out_specs, check_vma=False)
```

```python
import functools
import math

import jax
import jax.numpy as jnp
from jax import lax
from jax.experimental import pallas as pl
from jax.experimental.pallas import tpu as pltpu
from jax.sharding import PartitionSpec as P

HEADS = 32
HEAD_DIM = 64
LENGTH = 2048
XBASE = 512
DOCS = 4
EPSILON = 1e-05
MASKED = -1e30
TILE = 256
VMEM_LIMIT = 60 * 1024 * 1024

MESH = pl.DeviceIdType.MESH
F32 = jnp.float32
BF16 = jnp.bfloat16
ANY = pl.BlockSpec(memory_space=pl.ANY)
INSIDE = pl.BlockSpec(memory_space=pltpu.VMEM)


def nn(a, b):
    return lax.dot_general(a, b, (((1,), (0,)), ((), ())), preferred_element_type=F32)


def nt(a, b):
    return lax.dot_general(a, b, (((1,), (1,)), ((), ())), preferred_element_type=F32)


def tn(a, b):
    return lax.dot_general(a, b, (((0,), (0,)), ((), ())), preferred_element_type=F32)


def norm_parts(values):
    average = jnp.mean(values, axis=-1, keepdims=True)
    centered = values - average
    spread = jnp.mean(centered * centered, axis=-1, keepdims=True)
    scale = lax.rsqrt(spread + EPSILON)
    return centered * scale, scale


def norm_back(grad, normal, scale, gain):
    part = grad * gain
    inner = (
        part
        - jnp.mean(part, axis=-1, keepdims=True)
        - normal * jnp.mean(part * normal, axis=-1, keepdims=True)
    )
    return scale * inner, jnp.sum(grad * normal, axis=0)


def places():
    me = lax.axis_index("seq")
    core = lax.rem(me, 2)
    along_x = lax.rem(me // 2, 2)
    along_y = me // 4
    twin = 1 - 2 * core
    near_x = me + 2 - 4 * along_x
    near_y = me + 4 - 8 * along_y
    across = near_x + 4 - 8 * along_y
    return me, twin, near_x, near_y, across


def remote(src, dst, send_sem, recv_sem, partner):
    return pltpu.make_async_remote_copy(
        src_ref=src,
        dst_ref=dst,
        send_sem=send_sem,
        recv_sem=recv_sem,
        device_id={"seq": partner},
        device_id_type=MESH,
    )


def meet(partners):
    barrier = pltpu.get_barrier_semaphore()
    for partner in partners:
        pl.semaphore_signal(
            barrier, inc=1, device_id={"seq": partner}, device_id_type=MESH
        )
    pl.semaphore_wait(barrier, len(partners))


def gather_copies(x_ref, o_ref, send_sem, recv_sem):
    me, twin, near_x, near_y, across = places()
    half = x_ref.shape[0] // 2
    low, high = pl.ds(0, half), pl.ds(half, half)

    def copy(k, src, dst, partner):
        return remote(src, dst, send_sem.at[k], recv_sem.at[k], partner)

    def relay(k, owner, rows, partner):
        place = o_ref.at[owner, rows]
        return copy(k, place, place, partner)

    return [
        copy(0, x_ref.at[low], o_ref.at[me, low], near_x),
        copy(1, x_ref.at[high], o_ref.at[me, high], near_y),
        copy(2, x_ref.at[high], o_ref.at[me, high], near_x),
        copy(3, x_ref.at[low], o_ref.at[me, low], near_y),
        copy(4, x_ref, o_ref.at[me], me + twin),
        relay(5, near_x, low, near_y),
        relay(6, near_y, high, near_x),
        relay(7, near_x, low, me + twin),
        relay(8, near_y, high, me + twin),
        relay(9, near_x, high, me + twin),
        relay(10, near_y, low, me + twin),
        relay(11, across, low, me + twin),
        relay(12, across, high, me + twin),
    ]


def gather_run(sends, *between):
    between = (*between, *([None] * 3))[:3]

    def pause(i):
        if between[i] is not None:
            between[i]()

    sends[0].wait_recv()
    sends[5].start()
    sends[7].start()
    sends[1].wait_recv()
    sends[6].start()
    sends[8].start()
    pause(0)
    sends[2].wait_recv()
    sends[9].start()
    sends[3].wait_recv()
    sends[10].start()
    pause(1)
    sends[5].wait_recv()
    sends[11].start()
    sends[6].wait_recv()
    sends[12].start()
    pause(2)
    for k in (4, 7, 8, 9, 10, 11, 12):
        sends[k].wait_recv()
    for send in sends:
        send.wait_send()


def meet_all(n, depth):
    me = lax.axis_index("seq")
    z = lax.axis_index("batch")
    barrier = pltpu.get_barrier_semaphore()
    for k in range(1, n):
        pl.semaphore_signal(
            barrier, inc=1, device_id={"seq": lax.rem(me + k, n)}, device_id_type=MESH
        )
    for k in range(1, depth):
        pl.semaphore_signal(
            barrier,
            inc=1,
            device_id={"batch": lax.rem(z + k, depth)},
            device_id_type=MESH,
        )
    pl.semaphore_wait(barrier, n + depth - 2)


def line_remote(src, dst, send_sem, recv_sem, partner):
    return pltpu.make_async_remote_copy(
        src_ref=src,
        dst_ref=dst,
        send_sem=send_sem,
        recv_sem=recv_sem,
        device_id={"batch": partner},
        device_id_type=MESH,
    )


class Line:
    def __init__(self, depth, source, target, send_sem, recv_sem):
        self.depth, self.source, self.target = depth, source, target
        self.send_sem, self.recv_sem = send_sem, recv_sem
        self.z = lax.axis_index("batch")

    def message(self, side, k):
        sign = 2 * side - 1
        owner = self.z - sign * k
        return line_remote(
            self.source(owner, k),
            self.target(owner),
            self.send_sem.at[side, k],
            self.recv_sem.at[side, k],
            self.z + sign,
        )

    def sends(self, side, k):
        sign = 2 * side - 1
        owner, target = self.z - sign * k, self.z + sign
        inside = (owner >= 0) & (owner < self.depth)
        return inside & (target >= 0) & (target < self.depth)

    def land(self, k):
        for side in (0, 1):
            sign = 2 * side - 1
            owner = self.z - sign * (k + 1)

            @pl.when((owner >= 0) & (owner < self.depth))
            def _():
                place = self.target(owner)
                line_remote(
                    place,
                    place,
                    self.send_sem.at[side, k],
                    self.recv_sem.at[side, k],
                    self.z - sign,
                ).wait_recv()

    def start(self, k):
        for side in (0, 1):

            @pl.when(self.sends(side, k))
            def _():
                self.message(side, k).start()

    def sent(self, k):
        for side in (0, 1):

            @pl.when(self.sends(side, k))
            def _():
                self.message(side, k).wait_send()


def lane_tables(place):
    half = HEAD_DIM // 2
    lane = lax.broadcasted_iota(jnp.int32, (1, 128), 1)
    channel = lax.rem(lane, half).astype(F32)
    inverse = jnp.exp(channel * (-math.log(10000.0) / half))
    zeta = (channel * (2.0 / HEAD_DIM) + 0.4) / 1.4
    sign = jnp.where(lax.rem(lane, HEAD_DIM) < half, -1.0, 1.0)
    angle = place * inverse
    growth = jnp.exp((place - 0.5 * LENGTH) * (1.0 / XBASE) * jnp.log(zeta))
    shrink = 1.0 / growth
    cosine = jnp.cos(angle)
    sine = jnp.sin(angle) * sign
    return cosine * growth, sine * growth, cosine * shrink, sine * shrink


def start_kernel(
    n, depth, x_ref, w_ref, wd_ref, pos_ref,
    o_ref, wt_ref, wc_ref, cq_ref, sq_ref, ck_ref, sk_ref,
    keep_w, keep_c, local_sem, send_sem, recv_sem, hop_send, hop_recv, col_send, col_recv,
    line_send, line_recv,
):
    z = lax.axis_index("batch")
    rows_z = wc_ref.shape[2]
    cols = wc_ref.shape[3]
    me, twin, near_x, near_y, _ = places()
    own = pltpu.make_async_copy(x_ref, o_ref.at[me], local_sem.at[0])
    own.start()
    wd_rows = pl.ds(pl.multiple_of(z * rows_z, rows_z), rows_z)

    def column(k):
        return wd_ref.at[wd_rows, pl.ds(pl.multiple_of(k * cols, cols), cols)]

    load_column = pltpu.make_async_copy(column(me), keep_c, local_sem.at[4])
    own_column = pltpu.make_async_copy(keep_c, wc_ref.at[me, z], local_sem.at[5])
    load_column.start()
    meet_all(n, depth)
    load_column.wait()
    own_column.start()
    def hop(j, part, target):
        return remote(
            w_ref.at[j], wt_ref.at[part], hop_send.at[j], hop_recv.at[part], target
        )

    def load(j):
        return pltpu.make_async_copy(w_ref.at[j], keep_w, local_sem.at[6])

    def here(j, part):
        return pltpu.make_async_copy(keep_w, wt_ref.at[part], local_sem.at[1 + j])

    turns = [
        remote(
            column(lax.rem(me + k, n)),
            wc_ref.at[me, z],
            col_send.at[k],
            col_recv.at[k],
            lax.rem(me + k, n),
        )
        for k in range(1, n)
    ]
    for turn in turns:
        turn.start()
    for j in range(3):
        block = 3 * me + j
        target = lax.rem(block, n)
        for part in range(3):
            inside = block // n == part

            @pl.when(inside & (target != me))
            def _():
                hop(j, part, target).start()

            @pl.when(inside & (target == me))
            def _():
                load(j).start()

    sends = gather_copies(x_ref, o_ref, send_sem, recv_sem)
    for k in range(5):
        sends[k].start()

    line = Line(
        depth,
        lambda owner, k: wc_ref.at[:, owner],
        lambda owner: wc_ref.at[:, owner],
        line_send,
        line_recv,
    )

    own_column.wait()
    for turn in turns:
        turn.wait_recv()
    line.start(0)
    for j in range(3):
        block = 3 * me + j
        target = lax.rem(block, n)
        for part in range(3):

            @pl.when((block // n == part) & (target == me))
            def _():
                load(j).wait()
                here(j, part).start()

    @pl.loop(0, pos_ref.shape[0])
    def _(r):
        at = pl.ds(pl.multiple_of(r * 128, 128), 128)
        places_here = jnp.broadcast_to(pos_ref[pl.ds(r, 1), :], (128, 128)).T
        tables = lane_tables(places_here)
        for ref, table in zip((cq_ref, sq_ref, ck_ref, sk_ref), tables, strict=True):
            ref[at] = table

    def hand_on(k):
        def step():
            line.land(k - 1)
            line.start(k)

        return step

    gather_run(sends, *[hand_on(k) for k in range(1, depth - 1)])
    line.land(depth - 2)
    for k in range(depth - 1):
        line.sent(k)
    for turn in turns:
        turn.wait_send()
    for j in range(3):
        block = 3 * me + j
        target = lax.rem(block, n)
        for part in range(3):
            inside = block // n == part

            @pl.when(inside & (target != me))
            def _():
                hop(j, part, target).wait_send()

            @pl.when(inside & (target == me))
            def _():
                here(j, part).wait()

    for part in range(3):
        source = (part * n + me) // 3

        @pl.when(source != me)
        def _():
            hop(0, part, source).wait_recv()

    own.wait()


def start_exchange(block, w_qkv, w_down, positions, collective_id):
    n, depth = lax.axis_size("seq"), lax.axis_size("batch")
    rows, width = block.shape
    piece = w_qkv.shape[0] // 3
    w = w_qkv.reshape(3, piece, width)
    if n != 8:
        me = lax.axis_index("seq")
        turned = [
            lax.ppermute(w[j], "seq", [(d, (3 * d + j) % n) for d in range(n)])
            for j in range(3)
        ]
        parts = [pick_part(turned, me, n, part) for part in range(3)]
        place = jnp.broadcast_to(positions[:, None], (positions.shape[0], 128))
        return (
            lax.all_gather(block, "seq", axis=0, tiled=True),
            jnp.concatenate(parts, axis=0),
            lax.all_to_all(w_down, "seq", split_axis=1, concat_axis=0, tiled=True),
            lane_tables(place),
        )
    rows_z, cols = w_down.shape[0] // depth, w_down.shape[1] // n
    inside = pl.BlockSpec(memory_space=pltpu.VMEM)
    table = jax.ShapeDtypeStruct((n * rows, 128), F32)
    gathered, turned, columns, *tables = pl.pallas_call(
        functools.partial(start_kernel, n, depth),
        out_shape=(
            jax.ShapeDtypeStruct((n, rows, width), block.dtype),
            jax.ShapeDtypeStruct((3, piece, width), w.dtype),
            jax.ShapeDtypeStruct((n, depth, rows_z, cols), w_down.dtype),
            *([table] * 4),
        ),
        in_specs=[INSIDE, ANY, ANY, INSIDE],
        out_specs=(ANY, ANY, ANY, *([INSIDE] * 4)),
        scratch_shapes=[
            pltpu.VMEM((piece, width), BF16),
            pltpu.VMEM((rows_z, cols), BF16),
            pltpu.SemaphoreType.DMA((7,)),
            pltpu.SemaphoreType.DMA((13,)),
            pltpu.SemaphoreType.DMA((13,)),
            pltpu.SemaphoreType.DMA((3,)),
            pltpu.SemaphoreType.DMA((3,)),
            pltpu.SemaphoreType.DMA((n,)),
            pltpu.SemaphoreType.DMA((n,)),
            pltpu.SemaphoreType.DMA((2, depth)),
            pltpu.SemaphoreType.DMA((2, depth)),
        ],
        compiler_params=pltpu.CompilerParams(
            collective_id=collective_id, has_side_effects=True, vmem_limit_bytes=VMEM_LIMIT
        ),
        name="start_exchange",
    )(block, w, w_down, positions.reshape(-1, 128))
    return (
        gathered.reshape(n * rows, width),
        turned.reshape(3 * piece, width),
        columns.reshape(-1, cols),
        tables,
    )


def scatter_seq(partial):
    return lax.psum_scatter(partial, "seq", scatter_dimension=0, tiled=True).astype(F32)


def heads_to_tokens_kernel(n, x_ref, o_ref, keep, local_sem, send_sem, recv_sem):
    me = lax.axis_index("seq")
    rows = o_ref.shape[0]
    cols = x_ref.shape[1]
    exchange(
        n,
        me,
        lambda k: x_ref.at[pl.ds(pl.multiple_of(k * rows, rows), rows)],
        o_ref.at[:, pl.ds(pl.multiple_of(me * cols, cols), cols)],
        keep,
        local_sem,
        send_sem,
        recv_sem,
    )


def exchange(n, me, source, target, keep, local_sem, send_sem, recv_sem):
    load = pltpu.make_async_copy(source(me), keep, local_sem.at[0])
    own = pltpu.make_async_copy(keep, target, local_sem.at[1])
    load.start()
    barrier = pltpu.get_barrier_semaphore()
    for k in range(1, n):
        pl.semaphore_signal(
            barrier,
            inc=1,
            device_id={"seq": lax.rem(me + k, n)},
            device_id_type=MESH,
        )
    pl.semaphore_wait(barrier, n - 1)
    copies = []
    for k in range(1, n):
        partner = lax.rem(me + k, n)
        copies.append(
            pltpu.make_async_remote_copy(
                src_ref=source(partner),
                dst_ref=target,
                send_sem=send_sem.at[k],
                recv_sem=recv_sem.at[k],
                device_id={"seq": partner},
                device_id_type=MESH,
            )
        )
        copies[-1].start()
    load.wait()
    own.start()
    for copy in copies:
        copy.wait()
    own.wait()


def heads_to_tokens(heads, collective_id):
    n = lax.axis_size("seq")
    total, cols = heads.shape
    rows = total // n
    return pl.pallas_call(
        functools.partial(heads_to_tokens_kernel, n),
        out_shape=jax.ShapeDtypeStruct((rows, n * cols), heads.dtype),
        in_specs=[ANY],
        out_specs=ANY,
        scratch_shapes=[
            pltpu.VMEM((rows, cols), heads.dtype),
            pltpu.SemaphoreType.DMA((2,)),
            pltpu.SemaphoreType.DMA((n,)),
            pltpu.SemaphoreType.DMA((n,)),
        ],
        compiler_params=pltpu.CompilerParams(
            collective_id=collective_id, has_side_effects=True, vmem_limit_bytes=VMEM_LIMIT
        ),
        name="heads_to_tokens",
    )(heads)


def tokens_to_heads_kernel(n, x_ref, o_ref, keep, local_sem, send_sem, recv_sem):
    me = lax.axis_index("seq")
    rows = x_ref.shape[0]
    cols = o_ref.shape[1]
    exchange(
        n,
        me,
        lambda k: x_ref.at[:, pl.ds(pl.multiple_of(k * cols, cols), cols)],
        o_ref.at[pl.ds(pl.multiple_of(me * rows, rows), rows)],
        keep,
        local_sem,
        send_sem,
        recv_sem,
    )


def tokens_to_heads(tokens, collective_id):
    n = lax.axis_size("seq")
    rows, total = tokens.shape
    return pl.pallas_call(
        functools.partial(tokens_to_heads_kernel, n),
        out_shape=jax.ShapeDtypeStruct((rows * n, total // n), tokens.dtype),
        in_specs=[ANY],
        out_specs=ANY,
        scratch_shapes=[
            pltpu.VMEM((rows, total // n), tokens.dtype),
            pltpu.SemaphoreType.DMA((2,)),
            pltpu.SemaphoreType.DMA((n,)),
            pltpu.SemaphoreType.DMA((n,)),
        ],
        compiler_params=pltpu.CompilerParams(
            collective_id=collective_id, has_side_effects=True, vmem_limit_bytes=VMEM_LIMIT
        ),
        name="tokens_to_heads",
    )(tokens)


def swap_halves(values):
    width = values.shape[-1]
    half = HEAD_DIM // 2
    lane = lax.broadcasted_iota(jnp.int32, values.shape, 1)
    ahead = pltpu.roll(values, width - half, 1)
    behind = pltpu.roll(values, half, 1)
    return jnp.where(lane % HEAD_DIM < half, ahead, behind)


def spread_lanes(table, width):
    return jnp.concatenate([table] * (width // table.shape[-1]), axis=-1)


def qkv_kernel(
    x_ref, w_ref, cq_ref, sq_ref, ck_ref, sk_ref,
    q_ref, k_ref, v_ref, kt_ref, vt_ref,
):
    x = x_ref[...]
    width = q_ref.shape[1]
    query = nt(x, w_ref[0:width])
    query = query * spread_lanes(cq_ref[...], width) + swap_halves(
        query
    ) * spread_lanes(sq_ref[...], width)
    q_ref[...] = query.astype(BF16) * (HEAD_DIM**-0.5)
    keys = nt(x, w_ref[width : 2 * width])
    keys = keys * spread_lanes(ck_ref[...], width) + swap_halves(
        keys
    ) * spread_lanes(sk_ref[...], width)
    k_ref[...] = keys.astype(BF16)
    kt_ref[...] = keys.T.astype(BF16)
    values = nt(x, w_ref[2 * width :])
    v_ref[...] = values.astype(BF16)
    vt_ref[...] = values.T.astype(BF16)


def project_qkv(x, w, tables):
    length, width = x.shape
    cols = w.shape[0] // 3
    steps = length // TILE
    weight = pl.BlockSpec((3 * cols, width), lambda i: (0, 0))
    table = pl.BlockSpec((TILE, tables[0].shape[1]), lambda i: (i, 0))
    row_out = pl.BlockSpec((TILE, cols), lambda i: (i, 0))
    col_out = pl.BlockSpec((cols, TILE), lambda i: (0, i))
    rows = jax.ShapeDtypeStruct((length, cols), BF16)
    columns = jax.ShapeDtypeStruct((cols, length), BF16)
    return pl.pallas_call(
        qkv_kernel,
        grid=(steps,),
        out_shape=(rows, rows, rows, columns, columns),
        in_specs=[pl.BlockSpec((TILE, width), lambda i: (i, 0))]
        + [weight]
        + [table] * 4,
        out_specs=(row_out, row_out, row_out, col_out, col_out),
        compiler_params=pltpu.CompilerParams(vmem_limit_bytes=VMEM_LIMIT),
        cost_estimate=pl.CostEstimate(
            flops=6 * length * width * cols,
            bytes_accessed=2 * length * width + 6 * width * cols + 10 * length * cols,
            transcendentals=0,
        ),
        name="project_qkv",
    )(x, w, *tables)


def pair_mask(start_row, i, j):
    key_place = j * TILE + lax.broadcasted_iota(jnp.int32, (TILE, TILE), 0)
    query_place = i * TILE + lax.broadcasted_iota(jnp.int32, (TILE, TILE), 1)
    return (key_place <= query_place) & (key_place >= start_row)


def head_rows(query, heads):
    lane = lax.broadcasted_iota(jnp.int32, query.shape, 1) // HEAD_DIM
    zero = jnp.zeros_like(query)
    return [jnp.where(lane == h, query, zero) for h in range(heads)]


def attend_kernel(
    heads, first_ref, start_ref, q_ref, k_ref, vt_ref, o_ref, lse_ref, peak, total, mixed
):
    i = pl.program_id(0)
    queries = head_rows(q_ref[...], heads)
    start_row = start_ref[...]

    def block(j, first):
        at = pl.ds(pl.multiple_of(j * TILE, TILE), TILE)
        keys = k_ref[at, :]
        mask = pair_mask(start_row, i, j)
        for h in range(heads):
            here = slice(h * HEAD_DIM, (h + 1) * HEAD_DIM)
            scores = jnp.where(mask, nt(keys, queries[h]), MASKED)
            if first:
                new_peak = jnp.max(scores, axis=0, keepdims=True)
                expo = jnp.exp(scores - new_peak)
                total[h : h + 1] = jnp.sum(expo, axis=0, keepdims=True)
                mixed[here] = nn(vt_ref[here, at], expo.astype(BF16))
            else:
                old_peak = peak[h : h + 1]
                new_peak = jnp.maximum(old_peak, jnp.max(scores, axis=0, keepdims=True))
                expo = jnp.exp(scores - new_peak)
                shrink = jnp.exp(old_peak - new_peak)
                total[h : h + 1] = total[h : h + 1] * shrink + jnp.sum(
                    expo, axis=0, keepdims=True
                )
                mixed[here] = mixed[here] * shrink + nn(
                    vt_ref[here, at], expo.astype(BF16)
                )
            peak[h : h + 1] = new_peak

    block(i, True)

    @pl.loop(0, i - first_ref[i])
    def _(t):
        block(i - 1 - t, False)

    for h in range(heads):
        here = slice(h * HEAD_DIM, (h + 1) * HEAD_DIM)
        mixed[here] = mixed[here] / total[h : h + 1]
    o_ref[...] = mixed[...].T.astype(BF16)
    lse_ref[0] = peak[...] + jnp.log(total[...])


def attend(first, start, q, k, vt):
    length, cols = q.shape
    heads = cols // HEAD_DIM
    steps = length // TILE
    row = pl.BlockSpec((TILE, cols), lambda i, *_: (i, 0))
    return pl.pallas_call(
        functools.partial(attend_kernel, heads),
        out_shape=(
            jax.ShapeDtypeStruct((length, cols), BF16),
            jax.ShapeDtypeStruct((steps, heads, TILE), F32),
        ),
        grid_spec=pltpu.PrefetchScalarGridSpec(
            num_scalar_prefetch=1,
            grid=(steps,),
            in_specs=[
                pl.BlockSpec((1, TILE), lambda i, *_: (0, i)),
                row,
                pl.BlockSpec((length, cols), lambda i, *_: (0, 0)),
                pl.BlockSpec((cols, length), lambda i, *_: (0, 0)),
            ],
            out_specs=(
                row,
                pl.BlockSpec((1, heads, TILE), lambda i, *_: (i, 0, 0)),
            ),
            scratch_shapes=[
                pltpu.VMEM((heads, TILE), F32),
                pltpu.VMEM((heads, TILE), F32),
                pltpu.VMEM((cols, TILE), F32),
            ],
        ),
        compiler_params=pltpu.CompilerParams(vmem_limit_bytes=VMEM_LIMIT),
        cost_estimate=pl.CostEstimate(
            flops=4 * length * 1024 * cols,
            bytes_accessed=8 * length * cols,
            transcendentals=length * 1024 * heads,
        ),
        name="attend",
    )(first, start, q, k, vt)


def attend_back_kernel(
    heads, first_ref, start_ref, q_ref, k_ref, kt_ref, v_ref, o_ref, lse_ref, do_ref,
    cq_ref, sq_ref, ck_ref, sk_ref, grad_ref, dqt, dk_sum, dv_sum,
):
    i = pl.program_id(0)
    steps = pl.num_programs(0)
    width = q_ref.shape[1]
    queries = head_rows(q_ref[...], heads)
    grads = head_rows(do_ref[...], heads)
    start_row = start_ref[...]
    product = (do_ref[...].astype(F32) * o_ref[...].astype(F32)).T
    inner = [
        jnp.sum(product[h * HEAD_DIM : (h + 1) * HEAD_DIM], axis=0, keepdims=True)
        for h in range(heads)
    ]

    def block(j, first):
        at = pl.ds(pl.multiple_of(j * TILE, TILE), TILE)
        keys = k_ref[at, :]
        values = v_ref[at, :]
        mask = pair_mask(start_row, i, j)
        key_term = None
        value_term = None
        for h in range(heads):
            here = slice(h * HEAD_DIM, (h + 1) * HEAD_DIM)
            scores = nt(keys, queries[h])
            weights = jnp.where(mask, jnp.exp(scores - lse_ref[0, h : h + 1]), 0.0)
            grad_weights = nt(values, grads[h])
            grad_scores = (weights * (grad_weights - inner[h])).astype(BF16)
            term = nn(weights.astype(BF16), grads[h])
            value_term = term if value_term is None else value_term + term
            term = nn(grad_scores, queries[h])
            key_term = term if key_term is None else key_term + term
            term = nn(kt_ref[here, at], grad_scores)
            if first:
                dqt[here] = term
            else:
                dqt[here] = dqt[here] + term
        if first:
            dk_sum[at] = key_term
            dv_sum[at] = value_term
        else:
            dk_sum[at] = dk_sum[at] + key_term
            dv_sum[at] = dv_sum[at] + value_term

    block(i, True)

    @pl.loop(0, i - first_ref[i])
    def _(t):
        block(i - 1 - t, False)

    def unturn(grad, cosine, sine):
        grad = grad.astype(BF16).astype(F32)
        cosine = spread_lanes(cosine, width)
        sine = spread_lanes(sine, width)
        return (grad * cosine - swap_halves(grad) * sine).astype(BF16)

    rows = pl.ds(pl.multiple_of(i * TILE, TILE), TILE)
    grad_ref[rows, 0:width] = unturn(
        dqt[...].T * (HEAD_DIM**-0.5), cq_ref[rows, :], sq_ref[rows, :]
    )

    @pl.when(i == steps - 1)
    def _():
        @pl.loop(0, steps)
        def _(j):
            at = pl.ds(pl.multiple_of(j * TILE, TILE), TILE)
            grad_ref[at, width : 2 * width] = unturn(
                dk_sum[at], ck_ref[at, :], sk_ref[at, :]
            )
            grad_ref[at, 2 * width :] = dv_sum[at].astype(BF16)


def attend_back(first, start, q, k, kt, v, o, lse, do, tables):
    length, cols = q.shape
    heads = cols // HEAD_DIM
    steps = length // TILE
    row = pl.BlockSpec((TILE, cols), lambda i, *_: (i, 0))
    whole = pl.BlockSpec((length, cols), lambda i, *_: (0, 0))
    table = pl.BlockSpec((length, tables[0].shape[1]), lambda i, *_: (0, 0))
    return pl.pallas_call(
        functools.partial(attend_back_kernel, heads),
        out_shape=jax.ShapeDtypeStruct((length, 3 * cols), BF16),
        grid_spec=pltpu.PrefetchScalarGridSpec(
            num_scalar_prefetch=1,
            grid=(steps,),
            in_specs=[
                pl.BlockSpec((1, TILE), lambda i, *_: (0, i)),
                row,
                whole,
                pl.BlockSpec((cols, length), lambda i, *_: (0, 0)),
                whole,
                row,
                pl.BlockSpec((1, heads, TILE), lambda i, *_: (i, 0, 0)),
                row,
            ]
            + [table] * 4,
            out_specs=pl.BlockSpec((length, 3 * cols), lambda i, *_: (0, 0)),
            scratch_shapes=[
                pltpu.VMEM((cols, TILE), F32),
                pltpu.VMEM((length, cols), F32),
                pltpu.VMEM((length, cols), F32),
            ],
        ),
        compiler_params=pltpu.CompilerParams(vmem_limit_bytes=VMEM_LIMIT),
        cost_estimate=pl.CostEstimate(
            flops=10 * length * 1024 * cols,
            bytes_accessed=16 * length * cols,
            transcendentals=length * 1024 * heads,
        ),
        name="attend_back",
    )(first, start, q, k, kt, v, o, lse, do, *tables)


def upper_kernel(
    x_ref, wu_ref, c_ref, wd_ref, gain_ref, act_ref, slope_ref, grad_ref, stat_ref
):
    upper = nt(x_ref[...], wu_ref[...])
    grad = nn(c_ref[...], wd_ref[...])
    below = 0.5 * (1.0 + lax.erf(upper * (0.5**0.5)))
    act = upper * below
    slope = below + upper * (jnp.exp(-0.5 * upper * upper) * ((2.0 * math.pi) ** -0.5))
    act_ref[...] = act
    slope_ref[...] = slope.astype(BF16)
    grad_ref[...] = grad
    part = grad * gain_ref[...]
    average = jnp.mean(act, axis=-1, keepdims=True)
    centered = act - average
    spread = jnp.sum(centered * centered, axis=-1, keepdims=True)
    part_sum = jnp.sum(part, axis=-1, keepdims=True)
    cross = jnp.sum(part * centered, axis=-1, keepdims=True)
    lane = lax.broadcasted_iota(jnp.int32, (x_ref.shape[0], 128), 1)
    columns = jnp.where(
        lane == 0,
        average,
        jnp.where(lane == 1, spread, jnp.where(lane == 2, part_sum, cross)),
    )
    stat_ref[...] = columns.T[:8]


def upper_pass(x, w_up, cot, w_down, gain):
    length, width = x.shape
    feats = w_up.shape[0]
    rows = TILE
    row = pl.BlockSpec((rows, width), lambda i: (i, 0))
    out = pl.BlockSpec((rows, feats), lambda i: (i, 0))
    return pl.pallas_call(
        upper_kernel,
        grid=(length // rows,),
        out_shape=(
            jax.ShapeDtypeStruct((length, feats), F32),
            jax.ShapeDtypeStruct((length, feats), BF16),
            jax.ShapeDtypeStruct((length, feats), F32),
            jax.ShapeDtypeStruct((8, length), F32),
        ),
        in_specs=[
            row,
            pl.BlockSpec((feats, width), lambda i: (0, 0)),
            row,
            pl.BlockSpec((width, feats), lambda i: (0, 0)),
            pl.BlockSpec((1, feats), lambda i: (0, 0)),
        ],
        out_specs=(out, out, out, pl.BlockSpec((8, rows), lambda i: (0, i))),
        compiler_params=pltpu.CompilerParams(vmem_limit_bytes=VMEM_LIMIT),
        cost_estimate=pl.CostEstimate(
            flops=4 * length * width * feats,
            bytes_accessed=8 * length * width + 8 * length * feats,
            transcendentals=2 * length * feats,
        ),
        name="upper_pass",
    )(x, w_up, cot, w_down, gain)


def hidden_kernel(act_ref, slope_ref, grad_ref, stat_ref, gain_ref, hid_ref, gu_ref, gg_ref):
    i = pl.program_id(0)
    stats = stat_ref[...].T
    average = stats[:, 0:1]
    scale = stats[:, 1:2]
    part_mean = stats[:, 2:3]
    cross_mean = stats[:, 3:4]
    gain = gain_ref[...]
    normal = (act_ref[...] - average) * scale
    grad = grad_ref[...]
    hid_ref[...] = (normal * gain).astype(BF16)
    back = scale * (grad * gain - part_mean - normal * cross_mean)
    gu_ref[...] = (slope_ref[...].astype(F32) * back).astype(BF16)
    term = jnp.sum(grad * normal, axis=0, keepdims=True)

    @pl.when(i == 0)
    def _():
        gg_ref[...] = term

    @pl.when(i > 0)
    def _():
        gg_ref[...] = gg_ref[...] + term


def hidden_pass(act, slope, grad, stats, gain):
    length, feats = act.shape
    out = pl.BlockSpec((TILE, feats), lambda i: (i, 0))
    one = pl.BlockSpec((1, feats), lambda i: (0, 0))
    return pl.pallas_call(
        hidden_kernel,
        grid=(length // TILE,),
        out_shape=(
            jax.ShapeDtypeStruct((length, feats), BF16),
            jax.ShapeDtypeStruct((length, feats), BF16),
            jax.ShapeDtypeStruct((1, feats), F32),
        ),
        in_specs=[out, out, out, pl.BlockSpec((8, TILE), lambda i: (0, i)), one],
        out_specs=(out, out, one),
        compiler_params=pltpu.CompilerParams(vmem_limit_bytes=VMEM_LIMIT),
        cost_estimate=pl.CostEstimate(
            flops=12 * length * feats,
            bytes_accessed=14 * length * feats,
            transcendentals=0,
        ),
        name="hidden_pass",
    )(act, slope, grad, stats, gain)


def ffn_kernel(
    n, x_ref, wu_ref, cot_ref, wd_ref, gain_ref,
    full_ref, hid_ref, gu_ref, gg_ref,
    rows_in, wd, cot_in, act, slope, grad, stat, held, results,
    local_sem, cot_sem, out_sem, full_sem, send_sem, recv_sem, stat_send, stat_recv,
):
    me, twin, near_x, near_y, across = places()
    rows = x_ref.shape[0]
    feats = wu_ref.shape[0]

    def cut(i, size=rows):
        return pl.ds(pl.multiple_of(i * size, size), size)

    own = pltpu.make_async_copy(x_ref, rows_in.at[me], local_sem.at[0])
    own.start()
    load_wd = pltpu.make_async_copy(wd_ref, wd, local_sem.at[1])
    load_wd.start()

    def load_cot(i, slot):
        return pltpu.make_async_copy(
            cot_ref.at[cut(i)], cot_in.at[slot], cot_sem.at[slot]
        )

    load_cot(0, 0).start()
    meet([lax.rem(me + k, n) for k in range(1, n)])
    sends = gather_copies(x_ref, rows_in, send_sem, recv_sem)
    for k in range(5):
        sends[k].start()

    load_wd.wait()
    def incoming(first, last):
        @pl.loop(first, last)
        def _(i):
            slot = lax.rem(i, 2)

            @pl.when(i + 1 < n)
            def _():
                load_cot(i + 1, 1 - slot).start()

            load_cot(i, slot).wait()
            grad[cut(i)] = nn(cot_in[slot], wd[...])

    incoming(0, n - 2)
    sends[0].wait_recv()
    sends[5].start()
    sends[7].start()
    sends[1].wait_recv()
    sends[6].start()
    sends[8].start()
    incoming(n - 2, n)
    own.wait()

    def keep(b):
        return pltpu.make_async_copy(rows_in.at[b], full_ref.at[b], full_sem.at[b])

    @pl.loop(0, n)
    def _(i):
        @pl.when(i == 1)
        def _():
            sends[4].wait_recv()

        @pl.when(i == 2)
        def _():
            sends[2].wait_recv()
            sends[9].start()
            sends[3].wait_recv()
            sends[10].start()

        @pl.when(i == 4)
        def _():
            sends[7].wait_recv()
            sends[9].wait_recv()

        @pl.when(i == 5)
        def _():
            sends[8].wait_recv()
            sends[10].wait_recv()
            sends[5].wait_recv()
            sends[11].start()
            sends[6].wait_recv()
            sends[12].start()

        @pl.when(i == 7)
        def _():
            sends[11].wait_recv()
            sends[12].wait_recv()

        other = jnp.where((i == 1) | (i == 4) | (i == 5) | (i == 7), twin, 0)
        place = jnp.where(i < 2, me, jnp.where(i >= 6, across, jnp.where(lax.rem(i, 2) == 0, near_x, near_y)))
        b = place + other
        keep(b).start()
        at = cut(b)
        upper = nt(rows_in[b], wu_ref[...])
        below = 0.5 * (1.0 + lax.erf(upper * (0.5**0.5)))
        value = upper * below
        act[at] = value
        slope[at] = (
            below + upper * (jnp.exp(-0.5 * upper * upper) * ((2.0 * math.pi) ** -0.5))
        ).astype(BF16)
        part = grad[at] * gain_ref[...]
        average = jnp.mean(value, axis=-1, keepdims=True)
        centered = value - average
        spread = jnp.sum(centered * centered, axis=-1, keepdims=True)
        part_sum = jnp.sum(part, axis=-1, keepdims=True)
        cross = jnp.sum(part * centered, axis=-1, keepdims=True)
        lane = lax.broadcasted_iota(jnp.int32, (rows, 128), 1)
        columns = jnp.where(
            lane == 0,
            average,
            jnp.where(lane == 1, spread, jnp.where(lane == 2, part_sum, cross)),
        )
        stat[:, at] = columns.T[:8]

    held[me] = stat[...]
    rounds = [
        remote(
            stat, held.at[me], stat_send.at[k], stat_recv.at[k], lax.rem(me + k, n)
        )
        for k in range(1, n)
    ]
    for send in rounds:
        send.start()
    for send in rounds:
        send.wait()
    join_rows(n, feats, held, stat)

    def store(i, slot):
        return [
            pltpu.make_async_copy(
                results.at[slot, j], ref.at[cut(i)], out_sem.at[slot, j]
            )
            for j, ref in enumerate((hid_ref, gu_ref))
        ]

    gg_ref[...] = jnp.zeros_like(gg_ref)

    @pl.loop(0, n)
    def _(i):
        slot = lax.rem(i, 2)

        @pl.when(i >= 2)
        def _():
            for copy in store(i - 2, slot):
                copy.wait()

        at = cut(i)
        stats = stat[:, at].T
        gain = gain_ref[...]
        scale = stats[:, 1:2]
        normal = (act[at] - stats[:, 0:1]) * scale
        coming = grad[at]
        results[slot, 0] = (normal * gain).astype(BF16)
        back = scale * (coming * gain - stats[:, 2:3] - normal * stats[:, 3:4])
        results[slot, 1] = (slope[at].astype(F32) * back).astype(BF16)
        gg_ref[...] = gg_ref[...] + jnp.sum(coming * normal, axis=0, keepdims=True)
        for copy in store(i, slot):
            copy.start()

    for i in (n - 2, n - 1):
        for copy in store(i, i % 2):
            copy.wait()
    for b in range(n):
        keep(b).wait()
    for send in sends:
        send.wait_send()


def ffn_pass(ffn_in, w_up, cot, w_down, gain, collective_id):
    n = lax.axis_size("seq")
    rows, width = ffn_in.shape
    feats = w_up.shape[0]
    if n != 8:
        full = lax.all_gather(ffn_in, "seq", axis=0, tiled=True)
        act, slope, grad, stat = upper_pass(full, w_up, cot, w_down, gain)
        stats = join_stats(stat, feats, collective_id)
        return (full, *hidden_pass(act, slope, grad, stats, gain))
    length = n * rows
    dma = pltpu.SemaphoreType.DMA
    low = jax.ShapeDtypeStruct((length, feats), BF16)
    full, hidden, grad_upper, gain_grad = pl.pallas_call(
        functools.partial(ffn_kernel, n),
        out_shape=(
            jax.ShapeDtypeStruct((n, rows, width), BF16),
            low,
            low,
            jax.ShapeDtypeStruct((1, feats), F32),
        ),
        in_specs=[INSIDE, INSIDE, ANY, ANY, INSIDE],
        out_specs=(ANY, ANY, ANY, INSIDE),
        scratch_shapes=[
            pltpu.VMEM((n, rows, width), BF16),
            pltpu.VMEM((width, feats), BF16),
            pltpu.VMEM((2, rows, width), BF16),
            pltpu.VMEM((length, feats), F32),
            pltpu.VMEM((length, feats), BF16),
            pltpu.VMEM((length, feats), F32),
            pltpu.VMEM((8, length), F32),
            pltpu.VMEM((n, 8, length), F32),
            pltpu.VMEM((2, 2, rows, feats), BF16),
            dma((2,)),
            dma((2,)),
            dma((2, 2)),
            dma((n,)),
            dma((13,)),
            dma((13,)),
            dma((n,)),
            dma((n,)),
        ],
        compiler_params=pltpu.CompilerParams(
            collective_id=collective_id, has_side_effects=True, vmem_limit_bytes=VMEM_LIMIT
        ),
        name="ffn_pass",
    )(ffn_in, w_up, cot, w_down, gain)
    return full.reshape(length, width), hidden, grad_upper, gain_grad


def join_rows(n, feats, held, o_ref):
    average = held[0, 0:1]
    for d in range(1, n):
        average = average + held[d, 0:1]
    average = average * (1.0 / n)
    spread = jnp.zeros_like(average)
    part = jnp.zeros_like(average)
    cross = jnp.zeros_like(average)
    for d in range(n):
        shift = held[d, 0:1] - average
        spread = spread + held[d, 1:2] + feats * (shift * shift)
        part = part + held[d, 2:3]
        cross = cross + held[d, 3:4] + shift * held[d, 2:3]
    whole = 1.0 / (n * feats)
    scale = lax.rsqrt(spread * whole + EPSILON)
    o_ref[0:1] = average
    o_ref[1:2] = scale
    o_ref[2:3] = part * whole
    o_ref[3:4] = cross * scale * whole
    o_ref[4:8] = jnp.zeros((4, average.shape[1]), F32)


def stat_kernel(n, feats, x_ref, o_ref, held, send_sem, recv_sem):
    me = lax.axis_index("seq")
    held[me] = x_ref[...]
    meet([lax.rem(me + k, n) for k in range(1, n)])
    copies = [
        remote(x_ref, held.at[me], send_sem.at[k], recv_sem.at[k], lax.rem(me + k, n))
        for k in range(1, n)
    ]
    for copy in copies:
        copy.start()
    for copy in copies:
        copy.wait()
    join_rows(n, feats, held, o_ref)


def join_stats(stat, feats, collective_id):
    n = lax.axis_size("seq")
    inside = pl.BlockSpec(memory_space=pltpu.VMEM)
    return pl.pallas_call(
        functools.partial(stat_kernel, n, feats),
        out_shape=jax.ShapeDtypeStruct(stat.shape, F32),
        in_specs=[inside],
        out_specs=inside,
        scratch_shapes=[
            pltpu.VMEM((n, *stat.shape), F32),
            pltpu.SemaphoreType.DMA((n,)),
            pltpu.SemaphoreType.DMA((n,)),
        ],
        compiler_params=pltpu.CompilerParams(
            collective_id=collective_id, has_side_effects=True, vmem_limit_bytes=VMEM_LIMIT
        ),
        name="join_stats",
    )(stat)


def weight_kernel(a_ref, b_ref, o_ref):
    o_ref[...] = tn(a_ref[...], b_ref[...]).astype(BF16)


def weight_grad(a, b):
    length, outs = a.shape
    cols = b.shape[1]
    block = 2 * TILE
    return pl.pallas_call(
        weight_kernel,
        grid=(outs // block,),
        out_shape=jax.ShapeDtypeStruct((outs, cols), BF16),
        in_specs=[
            pl.BlockSpec((length, block), lambda i: (0, i)),
            pl.BlockSpec((length, cols), lambda i: (0, 0)),
        ],
        out_specs=pl.BlockSpec((block, cols), lambda i: (i, 0)),
        compiler_params=pltpu.CompilerParams(vmem_limit_bytes=VMEM_LIMIT),
        cost_estimate=pl.CostEstimate(
            flops=2 * length * outs * cols,
            bytes_accessed=2 * (length * outs + length * cols + outs * cols),
            transcendentals=0,
        ),
        name="weight_grad",
    )(a, b)


STEP = 32


def mix_kernel(att_ref, x_ref, w_ref, gm_ref, gf_ref, mix_ref, mid_ref, ffn_ref):
    j = pl.program_id(0)
    rows = att_ref.shape[0]
    cols = w_ref.shape[0]

    @pl.when(j == 0)
    def _():
        @pl.loop(0, rows // STEP)
        def _(r):
            at = pl.ds(pl.multiple_of(r * STEP, STEP), STEP)
            normal, _ = norm_parts(att_ref[at].astype(F32))
            mix_ref[at] = (normal * gm_ref[...]).astype(BF16)

    here = pl.ds(pl.multiple_of(j * cols, cols), cols)
    mid_ref[:, here] = x_ref[:, here].astype(F32) + nt(mix_ref[...], w_ref[...])

    @pl.when(j == pl.num_programs(0) - 1)
    def _():
        @pl.loop(0, rows // STEP)
        def _(r):
            at = pl.ds(pl.multiple_of(r * STEP, STEP), STEP)
            normal, _ = norm_parts(mid_ref[at])
            ffn_ref[at] = (normal * gf_ref[...]).astype(BF16)


def mix_pass(attended, x, w_out, gain_mix, gain_ffn):
    rows, width = x.shape
    cols = TILE
    n = width // cols
    whole = pl.BlockSpec((rows, width), lambda j: (0, 0))
    gain = pl.BlockSpec((1, width), lambda j: (0, 0))
    low = jax.ShapeDtypeStruct((rows, width), BF16)
    return pl.pallas_call(
        mix_kernel,
        grid=(n,),
        out_shape=(low, jax.ShapeDtypeStruct((rows, width), F32), low),
        in_specs=[
            whole,
            whole,
            pl.BlockSpec((cols, width), lambda j: (j, 0)),
            gain,
            gain,
        ],
        out_specs=(whole, whole, whole),
        compiler_params=pltpu.CompilerParams(vmem_limit_bytes=VMEM_LIMIT),
        cost_estimate=pl.CostEstimate(
            flops=2 * rows * width * width,
            bytes_accessed=2 * width * width + 12 * rows * width,
            transcendentals=0,
        ),
        name="mix_pass",
    )(attended, x, w_out, gain_mix[None], gain_ffn[None])


def branch_kernel(gbr_ref, att_ref, w_ref, gm_ref, gatt_ref, ggm_ref, total):
    j = pl.program_id(0)
    rows = att_ref.shape[0]
    cols = w_ref.shape[0]
    here = pl.ds(pl.multiple_of(j * cols, cols), cols)
    term = nn(gbr_ref[:, here], w_ref[...])

    @pl.when(j == 0)
    def _():
        total[...] = term

    @pl.when(j > 0)
    def _():
        total[...] = total[...] + term

    @pl.when(j == pl.num_programs(0) - 1)
    def _():
        ggm_ref[...] = jnp.zeros_like(ggm_ref)

        @pl.loop(0, rows // STEP)
        def _(r):
            at = pl.ds(pl.multiple_of(r * STEP, STEP), STEP)
            normal, scale = norm_parts(att_ref[at].astype(F32))
            part, gain_part = norm_back(total[at], normal, scale, gm_ref[...])
            ggm_ref[...] += gain_part[None]
            gatt_ref[at] = part.astype(BF16)


def branch_pass(grad_branch, attended, w_out, gain_mix):
    rows, width = grad_branch.shape
    cols = TILE
    n = width // cols
    whole = pl.BlockSpec((rows, width), lambda j: (0, 0))
    gain = pl.BlockSpec((1, width), lambda j: (0, 0))
    return pl.pallas_call(
        branch_kernel,
        grid=(n,),
        out_shape=(
            jax.ShapeDtypeStruct((rows, width), BF16),
            jax.ShapeDtypeStruct((1, width), F32),
        ),
        in_specs=[whole, whole, pl.BlockSpec((cols, width), lambda j: (j, 0)), gain],
        out_specs=(whole, gain),
        scratch_shapes=[pltpu.VMEM((rows, width), F32)],
        compiler_params=pltpu.CompilerParams(vmem_limit_bytes=VMEM_LIMIT),
        cost_estimate=pl.CostEstimate(
            flops=2 * rows * width * width,
            bytes_accessed=2 * width * width + 8 * rows * width,
            transcendentals=0,
        ),
        name="branch_pass",
    )(grad_branch, attended, w_out, gain_mix[None])


def ffn_back_kernel(
    n, gu_ref, wu_ref, hid_ref, wd_ref, mid_ref, cot_ref, gf_ref,
    po_ref, gmid_ref, gbr_ref, ggf_ref,
    gu, hid, own, far, twin_in, held, made,
    local_sem, hid_sem, made_sem, send_sem, recv_sem,
):
    me, twin, near_x, near_y, across = places()
    rows, width = mid_ref.shape
    half = rows // 2
    low, high = pl.ds(0, half), pl.ds(half, half)
    mine = (across, near_x, near_y, me)

    def cut(i, size=rows):
        return pl.ds(pl.multiple_of(i * size, size), size)

    def load_hid(i, slot):
        return pltpu.make_async_copy(hid_ref.at[cut(i)], hid.at[slot], hid_sem.at[slot])

    load_gu = pltpu.make_async_copy(gu_ref, gu, local_sem)
    load_gu.start()
    load_hid(0, 0).start()
    meet((me + twin, near_x, near_y))
    load_gu.wait()

    def copy(k, src, dst, partner):
        return remote(src, dst, send_sem.at[k], recv_sem.at[k], partner)

    twins = [copy(i, far.at[i], twin_in.at[i], me + twin) for i in range(4)]
    sends = [
        copy(4, own.at[0, low], held.at[0], near_x),
        copy(5, own.at[0, high], held.at[1], near_y),
        copy(6, own.at[1, low], held.at[2], near_x),
        copy(7, own.at[2, high], held.at[3], near_y),
        copy(8, own.at[1, high], held.at[4], near_x),
        copy(9, own.at[2, low], held.at[5], near_y),
    ]

    def add(i, base, count, source):
        @pl.loop(0, count // STEP)
        def _(r):
            at = cut(r, STEP)
            to = pl.ds(pl.multiple_of(base + r * STEP, STEP), STEP)
            own[i, to] = (own[i, to].astype(F32) + source[at].astype(F32)).astype(BF16)

    for i, block in enumerate(mine):
        far[i] = nn(gu[cut(block + twin)], wu_ref[...]).astype(BF16)
        twins[i].start()
        own[i] = nn(gu[cut(block)], wu_ref[...]).astype(BF16)
        if i < 3:
            twins[i].wait_recv()
            add(i, 0, rows, twin_in.at[i])
        if i == 0:
            sends[0].start()
            sends[1].start()
        elif i < 3:
            sends[i + 1].start()

    def store(i, slot):
        return pltpu.make_async_copy(made.at[slot], po_ref.at[cut(i)], made_sem.at[slot])

    def outputs(first, last):
        @pl.loop(first, last)
        def _(i):
            slot = lax.rem(i, 2)

            @pl.when(i + 1 < n)
            def _():
                load_hid(i + 1, 1 - slot).start()

            load_hid(i, slot).wait()

            @pl.when(i >= 2)
            def _():
                store(i - 2, slot).wait()

            made[slot] = nt(hid[slot], wd_ref[...]).astype(BF16)
            store(i, slot).start()

    outputs(0, n // 2)
    sends[1].wait_recv()
    add(1, half, half, held.at[1])
    sends[4].start()
    sends[0].wait_recv()
    add(2, 0, half, held.at[0])
    sends[5].start()
    outputs(n // 2, n)
    twins[3].wait_recv()
    for k in (2, 3, 4, 5):
        sends[k].wait_recv()
    ggf_ref[...] = jnp.zeros_like(ggf_ref)
    for base, one, two in ((0, 2, 5), (half, 3, 4)):

        @pl.loop(0, half // STEP)
        def _(r):
            at = cut(r, STEP)
            to = pl.ds(pl.multiple_of(base + r * STEP, STEP), STEP)
            value = (
                own[3, to].astype(F32)
                + twin_in[3, to].astype(F32)
                + held[one, at].astype(F32)
                + held[two, at].astype(F32)
            )
            normal, scale = norm_parts(mid_ref[to])
            part, gain_part = norm_back(value, normal, scale, gf_ref[...])
            ggf_ref[...] = ggf_ref[...] + gain_part[None]
            grad = cot_ref[to].astype(F32) + part
            gmid_ref[to] = grad
            gbr_ref[to] = grad.astype(BF16)

    for i in (n - 2, n - 1):
        store(i, i % 2).wait()
    for send in twins + sends:
        send.wait_send()


def ffn_back(grad_upper, w_up, hidden, w_down, middle, cot, gain, collective_id):
    n = lax.axis_size("seq")
    rows, width = middle.shape
    feats = w_up.shape[0]
    if n != 8:
        normal, scale = norm_parts(middle)
        value = scatter_seq(nn(grad_upper, w_up).astype(BF16))
        part, gain_part = norm_back(value, normal, scale, gain)
        grad = cot.astype(F32) + part
        return nt(hidden, w_down).astype(BF16), grad, grad.astype(BF16), gain_part[None]
    dma = pltpu.SemaphoreType.DMA
    block = pltpu.VMEM((4, rows, width), BF16)
    return pl.pallas_call(
        functools.partial(ffn_back_kernel, n),
        out_shape=(
            jax.ShapeDtypeStruct((n * rows, width), BF16),
            jax.ShapeDtypeStruct((rows, width), F32),
            jax.ShapeDtypeStruct((rows, width), BF16),
            jax.ShapeDtypeStruct((1, width), F32),
        ),
        in_specs=[ANY, INSIDE, ANY, INSIDE, INSIDE, INSIDE, INSIDE],
        out_specs=(ANY, INSIDE, INSIDE, INSIDE),
        scratch_shapes=[
            pltpu.VMEM((n * rows, feats), BF16),
            pltpu.VMEM((2, rows, feats), BF16),
            block,
            block,
            block,
            pltpu.VMEM((6, rows // 2, width), BF16),
            pltpu.VMEM((2, rows, width), BF16),
            dma,
            dma((2,)),
            dma((2,)),
            dma((10,)),
            dma((10,)),
        ],
        compiler_params=pltpu.CompilerParams(
            collective_id=collective_id, has_side_effects=True, vmem_limit_bytes=VMEM_LIMIT
        ),
        name="ffn_back",
    )(grad_upper, w_up, hidden, w_down, middle, cot, gain[None])


CHUNK = 64


def finish_kernel(
    n, depth, gq_ref, gd_ref, pw_ref, pn_ref, po_ref, x_ref, grad_ref, mid_ref, ga_ref, gm_ref, gf_ref, gh_ref,
    oq_ref, od_ref, ow_ref, gi_ref, out_ref, sums_ref,
    own, twin_in, held, zown, zin, stage, gain_here, gain_row, gain_pack, gain_line,
    local_sem, load_sem, stage_sem, send_sem, recv_sem, keep_sem,
    up_send, up_recv, down_send, down_recv, home_send, home_recv, gain_send, gain_recv,
):
    me, twin, near_x, near_y, across = places()
    z = lax.axis_index("batch")
    rows, width = pn_ref.shape[1:]
    half = rows // 2
    low, high = pl.ds(0, half), pl.ds(half, half)
    mine = (across, near_x, near_y, me)
    _, chunk, cols = zown.shape
    across_width = width // cols
    per_part = (gq_ref.shape[1] // chunk) * across_width
    turned = gq_ref.shape[0] * per_part
    per_source = gd_ref.shape[1] // chunk
    outer = turned + gd_ref.shape[0] * per_source
    chunks = zown.shape[0]
    per_side = chunks // 2

    def cut(i, size):
        return pl.ds(pl.multiple_of(i * size, size), size)

    def wide(i):
        return cut(i // across_width, chunk), cut(lax.rem(i, across_width), cols)

    line_loads = []
    for g in range(turned):
        source = gq_ref.at[(g // per_part, *wide(g % per_part))]
        line_loads.append(pltpu.make_async_copy(source, zown.at[g], load_sem.at[g]))
    for g in range(turned, outer):
        source = gd_ref.at[
            (g - turned) // per_source, cut((g - turned) % per_source, chunk)
        ]
        line_loads.append(pltpu.make_async_copy(source, zown.at[g], load_sem.at[g]))
    for load in line_loads:
        load.start()
    partials = (pw_ref, pn_ref, po_ref)
    loads = [
        [
            pltpu.make_async_copy(p.at[block], own.at[m, i], local_sem.at[4 * m + i])
            for i, block in enumerate(mine)
        ]
        for m, p in enumerate(partials)
    ]
    for part in loads:
        for load in part:
            load.start()
    meet_all(n, depth)

    def copy(m, k, src, dst, partner):
        return remote(src, dst, send_sem.at[m, k], recv_sem.at[m, k], partner)

    twins = [
        [
            copy(m, i, p.at[block + twin], twin_in.at[m, i], me + twin)
            for i, block in enumerate(mine)
        ]
        for m, p in enumerate(partials)
    ]
    sends = [
        [
            copy(m, 4, own.at[m, 0, low], held.at[m, 0], near_x),
            copy(m, 5, own.at[m, 0, high], held.at[m, 1], near_y),
            copy(m, 6, own.at[m, 1, low], held.at[m, 2], near_x),
            copy(m, 7, own.at[m, 2, high], held.at[m, 3], near_y),
            copy(m, 8, own.at[m, 1, high], held.at[m, 4], near_x),
            copy(m, 9, own.at[m, 2, low], held.at[m, 5], near_y),
        ]
        for m in range(3)
    ]
    for part in twins:
        for send in part:
            send.start()

    def add_twin(m, i):
        loads[m][i].wait()
        twins[m][i].wait_recv()

        @pl.loop(0, rows // STEP)
        def _(r):
            at = cut(r, STEP)
            own[m, i, at] = (
                own[m, i, at].astype(F32) + twin_in[m, i, at].astype(F32)
            ).astype(BF16)

    def add_held(m, i, base, slot):
        @pl.loop(0, half // STEP)
        def _(r):
            at = cut(r, STEP)
            to = pl.ds(pl.multiple_of(base + r * STEP, STEP), STEP)
            own[m, i, to] = (
                own[m, i, to].astype(F32) + held[m, slot, at].astype(F32)
            ).astype(BF16)

    def first(m):
        add_twin(m, 0)
        sends[m][0].start()
        sends[m][1].start()
        add_twin(m, 1)
        sends[m][2].start()
        add_twin(m, 2)
        sends[m][3].start()

    def second(m):
        sends[m][1].wait_recv()
        add_held(m, 1, half, 1)
        sends[m][4].start()
        sends[m][0].wait_recv()
        add_held(m, 2, 0, 0)
        sends[m][5].start()

    def last(m, store):
        loads[m][3].wait()
        twins[m][3].wait_recv()
        for k in (2, 3, 4, 5):
            sends[m][k].wait_recv()
        for base, one, two in ((0, 2, 5), (half, 3, 4)):

            @pl.loop(0, half // STEP)
            def _(r):
                at = cut(r, STEP)
                place = base + r * STEP
                to = pl.ds(pl.multiple_of(place, STEP), STEP)
                store(
                    place,
                    to,
                    own[m, 3, to].astype(F32)
                    + twin_in[m, 3, to].astype(F32)
                    + held[m, one, at].astype(F32)
                    + held[m, two, at].astype(F32),
                )

    def store_line(place, to, value):
        value = value.astype(BF16)
        for side in range(across_width):
            zown[
                outer + (place // chunk) * across_width + side,
                pl.ds(pl.multiple_of(lax.rem(place, chunk), STEP), STEP),
            ] = value[:, side * cols : (side + 1) * cols]

    def store_inputs(place, to, value):
        normal, scale = norm_parts(x_ref[to].astype(F32))
        part, gain_part = norm_back(value, normal, scale, ga_ref[...])
        gi_ref[to] = grad_ref[to] + part
        gain_here[0:1] = gain_here[0:1] + gain_part[None]

    def store_outputs(place, to, value):
        out_ref[to] = (mid_ref[to] + value).astype(BF16)

    def home(part):
        block = part * n + me
        return block // 3, lax.rem(block, 3)

    def deliver_far(g):
        target, slot = home(g // per_part)
        piece = lax.rem(g, per_part)
        return remote(
            zin.at[g],
            oq_ref.at[(slot, *wide(piece))],
            home_send.at[g],
            home_recv.at[slot, piece],
            target,
        )

    def deliver_near(g):
        _, slot = home(g // per_part)
        return pltpu.make_async_copy(
            zin.at[g], oq_ref.at[(slot, *wide(lax.rem(g, per_part)))], keep_sem.at[g]
        )

    def widen(g):
        @pl.loop(0, chunk // STEP)
        def _(r):
            at = cut(r, STEP)
            stage[at] = zin[g, at].astype(F32)

    def deliver(g):
        target, _ = home(g // per_part)

        @pl.when((g < turned) & (target != me))
        def _():
            deliver_far(g).start()

        @pl.when((g < turned) & (target == me))
        def _():
            deliver_near(g).start()

        @pl.when((g >= turned) & (g < outer))
        def _():
            widen(g)
            at = g - turned
            place = cut(lax.rem(at, per_source), chunk), cut(at // per_source, cols)
            store = pltpu.make_async_copy(stage, od_ref.at[place], stage_sem)
            store.start()
            store.wait()

        @pl.when(g >= outer)
        def _():
            widen(g)
            store = pltpu.make_async_copy(
                stage, ow_ref.at[wide(g - outer)], stage_sem
            )
            store.start()
            store.wait()

    def delivered(g):
        target, _ = home(g // per_part)

        @pl.when(target != me)
        def _():
            deliver_far(g).wait_send()

        @pl.when(target == me)
        def _():
            deliver_near(g).wait()

    def go_up(g, ahead):
        return line_remote(zown.at[g], zin.at[g], up_send.at[g], up_recv.at[g], ahead)

    def go_down(g, behind):
        return line_remote(
            zin.at[g], zin.at[g], down_send.at[g], down_recv.at[g], behind
        )

    def ranks(side):
        if side == 0:
            return z, z + 1, z - 1
        return depth - 1 - z, z - 1, z + 1

    def add_line(g, target):
        @pl.loop(0, chunk // STEP)
        def _(r):
            at = cut(r, STEP)
            target[g, at] = (zown[g, at].astype(F32) + zin[g, at].astype(F32)).astype(
                BF16
            )

    lead = 2
    far = 2 * (depth - 1)
    steps = per_side + 2 * far

    def line_enter(c):
        for side in (0, 1):
            rank, ahead, _ = ranks(side)

            @pl.when(rank == 0)
            def _():
                go_up(2 * c + side, ahead).start()

    def line_step(t):
        @pl.when(t + lead < per_side)
        def _():
            line_enter(t + lead)

        back = []
        for side in (0, 1):
            rank, ahead, behind = ranks(side)
            c_back = t - 2 * far + 2 * rank
            g_back = 2 * c_back + side
            there = (c_back >= 0) & (c_back < per_side) & (rank < depth - 1)
            back.append((there, g_back))

            @pl.when(there)
            def _():
                go_down(g_back, ahead).wait_recv()

            @pl.when(there & (rank > 0))
            def _():
                go_down(g_back, behind).start()

        for side in (0, 1):
            rank, ahead, behind = ranks(side)
            c = t - 2 * rank
            g = 2 * c + side
            there = (c >= 0) & (c < per_side)

            @pl.when(there & (rank > 0) & (rank < depth - 1))
            def _():
                go_up(g, behind).wait_recv()
                add_line(g, zown)
                go_up(g, ahead).start()

            @pl.when(there & (rank == depth - 1))
            def _():
                go_up(g, behind).wait_recv()
                add_line(g, zin)
                go_down(g, behind).start()
                deliver(g)

        for there, g_back in back:

            @pl.when(there)
            def _():
                deliver(g_back)

    def line_steps(first_step, last_step):
        @pl.loop(first_step, last_step)
        def _(t):
            line_step(t)

    gain_here[...] = jnp.zeros_like(gain_here)
    for load in line_loads:
        load.wait()
    for c in range(lead):
        line_enter(c)
    first(0)
    line_steps(0, 8)
    second(0)
    line_steps(8, 9)
    first(1)
    line_steps(9, 18)
    last(0, store_line)
    line_steps(18, 20)
    second(1)
    line_steps(20, 21)
    first(2)
    line_steps(21, 28)
    last(1, store_inputs)

    gain_here[1:2] = gm_ref[...]
    gain_here[2:3] = gf_ref[...]
    gain_here[3:4, 0 : gh_ref.shape[1]] = gh_ref[...]
    gain_row[me] = gain_here[...]
    rounds = [
        remote(
            gain_here,
            gain_row.at[me],
            gain_send.at[0, k],
            gain_recv.at[0, k],
            lax.rem(me + k, n),
        )
        for k in range(1, n)
    ]
    for send in rounds:
        send.start()
    line_steps(28, 32)
    second(2)
    line_steps(32, 40)
    last(2, store_outputs)
    line_steps(40, 42)
    for send in rounds:
        send.wait()
    total = gain_row[0]
    for d in range(1, n):
        total = total + gain_row[d]
    gain_pack[0:8] = total
    for d in range(n):
        gain_pack[8 + d : 9 + d] = gain_row[d, 3:4]
    gain_line[z] = gain_pack[...]
    rounds = [
        line_remote(
            gain_pack,
            gain_line.at[z],
            gain_send.at[1, k],
            gain_recv.at[1, k],
            lax.rem(z + k, depth),
        )
        for k in range(1, depth)
    ]
    for send in rounds:
        send.start()
    line_steps(42, steps)
    for send in rounds:
        send.wait()
    total = gain_line[0]
    for d in range(1, depth):
        total = total + gain_line[d]
    sums_ref[...] = total

    for m in range(3):
        for send in twins[m] + sends[m]:
            send.wait_send()
    for g in range(chunks):
        rank, ahead, behind = ranks(g % 2)

        @pl.when(rank < depth - 1)
        def _():
            go_up(g, ahead).wait_send()

        @pl.when(rank > 0)
        def _():
            go_down(g, behind).wait_send()

    for g in range(turned):
        delivered(g)
    for slot in range(3):
        block = 3 * me + slot
        source = lax.rem(block, n)

        @pl.when(source != me)
        def _():
            for piece in range(per_part):
                remote(
                    zin.at[0],
                    oq_ref.at[(slot, *wide(piece))],
                    home_send.at[0],
                    home_recv.at[slot, piece],
                    source,
                ).wait_recv()


def finish(
    grad_qkv, grad_down, part_out, part_normed, part_outputs, x, grad_middle, middle, gain, gains, collective_id
):
    n, depth = lax.axis_size("seq"), lax.axis_size("batch")
    rows, width = part_out.shape[0] // n, part_out.shape[1]
    cols = grad_qkv.shape[1]
    sources, _, feats = grad_down.shape
    if n != 8 or depth != 4:
        me = lax.axis_index("seq")
        blocks = lax.psum(grad_qkv, "batch")
        back = [
            lax.ppermute(
                give_part(blocks, me, n, j),
                "seq",
                [((3 * d + j) % n, d) for d in range(n)],
            )
            for j in range(3)
        ]
        w_out = lax.psum(scatter_seq(part_out).astype(BF16), "batch")
        normal, scale = norm_parts(x.astype(F32))
        part, gain_part = norm_back(scatter_seq(part_normed), normal, scale, gain)
        shared = [lax.psum(g, ("batch", "seq")) for g in (gain_part, gains[0][0], gains[1][0])]
        hidden = lax.all_gather(lax.psum(gains[2][0], "batch"), "seq", axis=0, tiled=True)
        down = lax.psum(grad_down, "batch")
        return (
            jnp.concatenate(back, axis=0),
            jnp.swapaxes(down, 0, 1).reshape(rows, sources * feats).astype(F32),
            w_out.astype(F32),
            grad_middle + part,
            (middle + scatter_seq(part_outputs)).astype(BF16),
            (*shared, hidden),
        )
    chunks = (
        3 * cols * width + rows * width + sources * rows * feats
    ) // (CHUNK * feats)
    dma = pltpu.SemaphoreType.DMA
    line = pltpu.VMEM((chunks, CHUNK, feats), BF16)
    w_qkv, w_down, w_out, grad_inputs, outputs, sums = pl.pallas_call(
        functools.partial(finish_kernel, n, depth),
        out_shape=(
            jax.ShapeDtypeStruct((3, cols, width), BF16),
            jax.ShapeDtypeStruct((rows, sources * feats), F32),
            jax.ShapeDtypeStruct((rows, width), F32),
            jax.ShapeDtypeStruct((rows, width), F32),
            jax.ShapeDtypeStruct((rows, width), BF16),
            jax.ShapeDtypeStruct((16, width), F32),
        ),
        in_specs=[ANY] * 5 + [INSIDE] * 7,
        out_specs=(ANY, ANY, ANY, INSIDE, INSIDE, INSIDE),
        scratch_shapes=[
            pltpu.VMEM((3, 4, rows, width), BF16),
            pltpu.VMEM((3, 4, rows, width), BF16),
            pltpu.VMEM((3, 6, rows // 2, width), BF16),
            line,
            line,
            pltpu.VMEM((CHUNK, feats), F32),
            pltpu.VMEM((8, width), F32),
            pltpu.VMEM((n, 8, width), F32),
            pltpu.VMEM((16, width), F32),
            pltpu.VMEM((depth, 16, width), F32),
            dma((12,)),
            dma((chunks,)),
            dma,
            dma((3, 10)),
            dma((3, 10)),
            dma((chunks,)),
            dma((chunks,)),
            dma((chunks,)),
            dma((chunks,)),
            dma((chunks,)),
            dma((chunks,)),
            dma((3, cols * width // (CHUNK * feats))),
            dma((2, n)),
            dma((2, n)),
        ],
        compiler_params=pltpu.CompilerParams(
            collective_id=collective_id,
            has_side_effects=True,
            vmem_limit_bytes=VMEM_LIMIT,
        ),
        name="finish",
    )(
        grad_qkv,
        grad_down,
        *[p.reshape(n, rows, width) for p in (part_out, part_normed, part_outputs)],
        x,
        grad_middle,
        middle,
        gain[None],
        *gains,
    )
    return (
        w_qkv.reshape(3 * cols, width),
        w_down,
        w_out,
        grad_inputs,
        outputs,
        (sums[0], sums[1], sums[2], sums[8:, :feats].reshape(-1)),
    )


def body(
    inputs,
    segment_ids,
    w_qkv,
    w_out,
    w_up,
    w_down,
    gain_attn,
    gain_mix,
    gain_ffn,
    gain_hidden,
    cotangent,
):
    _, local, width = inputs.shape
    n, depth = lax.axis_size("seq"), lax.axis_size("batch")
    me = lax.axis_index("seq")
    length = local * n
    feats = w_up.shape[0]
    x_low = inputs[0]
    x = x_low.astype(F32)
    cot = cotangent[0]
    segment = segment_ids[0]

    w_out_full = lax.all_gather(w_out, "seq", axis=0, tiled=True)
    normed = (norm_parts(x)[0] * gain_attn).astype(BF16)
    before = [jnp.sum((segment < d).astype(jnp.int32)) for d in range(1, DOCS)]
    start = jnp.zeros_like(segment)
    for d in range(1, DOCS):
        start = jnp.where(segment == d, before[d - 1], start)
    positions = jnp.arange(length, dtype=jnp.int32) - start
    first = start[::TILE] // TILE
    start_row = start[None, :]

    normed_full, w_heads, w_down_cols, tables = start_exchange(
        normed, w_qkv, w_down, positions.astype(F32), 1
    )
    cot_full = lax.all_gather(lax.optimization_barrier(cot), "seq", axis=0, tiled=True)

    q, k, v, kt, vt = project_qkv(normed_full, w_heads, tables)
    attended_heads, lse = attend(first, start_row, q, k, vt)
    attended = heads_to_tokens(attended_heads, 2)
    mix_in, middle, ffn_in = mix_pass(attended, x_low, w_out_full, gain_mix, gain_ffn)
    gain_here = lax.dynamic_slice_in_dim(gain_hidden, me * feats, feats, 0)[None, :]
    ffn_full, hidden, grad_upper, grad_gain_here = ffn_pass(
        ffn_in, w_up, cot_full, w_down_cols, gain_here, 3
    )

    grad_w_up = tn(grad_upper, ffn_full).astype(BF16)
    grad_upper, grad_w_up = lax.optimization_barrier((grad_upper, grad_w_up))
    grad_w_up = lax.psum(grad_w_up, "batch")
    grad_w_down = weight_grad(cot_full, hidden).reshape(n, local, feats)
    grad_upper, grad_w_down = lax.optimization_barrier((grad_upper, grad_w_down))
    part_outputs, grad_middle, grad_branch, grad_gain_ffn = ffn_back(
        grad_upper, w_up, hidden, w_down_cols, middle, cot, gain_ffn, 4
    )
    grad_att, grad_gain_mix = branch_pass(grad_branch, attended, w_out_full, gain_mix)
    grad_heads = tokens_to_heads(grad_att, 5)
    grad_w_down, grad_heads = lax.optimization_barrier((grad_w_down, grad_heads))
    grad_w_down = lax.all_to_all(grad_w_down, "seq", split_axis=0, concat_axis=0, tiled=True)
    grads = attend_back(
        first, start_row, q, k, kt, v, attended_heads, lse, grad_heads, tables
    )
    grad_w_qkv, grad_w_down, grad_w_out, grad_inputs, outputs, gains = finish(
        tn(grads, normed_full).astype(BF16).reshape(3, -1, width),
        grad_w_down,
        tn(grad_branch, mix_in).astype(BF16),
        nn(grads, w_heads).astype(BF16),
        part_outputs,
        x_low,
        grad_middle,
        middle,
        gain_attn,
        (grad_gain_mix, grad_gain_ffn, grad_gain_here),
        6,
    )
    return (
        outputs[None],
        grad_inputs[None],
        grad_w_qkv.astype(F32),
        grad_w_out,
        grad_w_up.astype(F32),
        grad_w_down,
        *gains,
    )


def pick_part(turned, me, n, part):
    chosen = turned[0]
    home = part * n + me
    for j in (1, 2):
        chosen = jnp.where(lax.rem(home, 3) == j, turned[j], chosen)
    return chosen


def give_part(blocks, me, n, j):
    chosen = blocks[0]
    for part in (1, 2):
        chosen = jnp.where(lax.rem(part * n + me, 3) == j, blocks[part], chosen)
    return chosen


def solution(mesh):
    in_specs = (
        P("batch", "seq", None),
        P("batch", None),
        P("seq", None),
        P("seq", None),
        P("seq", None),
        P("seq", None),
        P(),
        P(),
        P(),
        P(),
        P("batch", "seq", None),
    )
    out_specs = (
        P("batch", "seq", None),
        P("batch", "seq", None),
        P("seq", None),
        P("seq", None),
        P("seq", None),
        P("seq", None),
        P(),
        P(),
        P(),
        P(),
    )
    return jax.shard_map(body, mesh=mesh, in_specs=in_specs, out_specs=out_specs, check_vma=False)
```

```python
import functools
import math

import jax
import jax.numpy as jnp
from jax import lax
from jax.experimental import pallas as pl
from jax.experimental.pallas import tpu as pltpu
from jax.sharding import PartitionSpec as P

HEADS = 32
HEAD_DIM = 64
LENGTH = 2048
XBASE = 512
DOCS = 4
EPSILON = 1e-05
MASKED = -1e30
TILE = 256
STEP = 32
VMEM_LIMIT = 60 * 1024 * 1024

MESH = pl.DeviceIdType.MESH
F32 = jnp.float32
BF16 = jnp.bfloat16
ANY = pl.BlockSpec(memory_space=pl.ANY)
INSIDE = pl.BlockSpec(memory_space=pltpu.VMEM)


def nn(a, b):
    return lax.dot_general(a, b, (((1,), (0,)), ((), ())), preferred_element_type=F32)


def nt(a, b):
    return lax.dot_general(a, b, (((1,), (1,)), ((), ())), preferred_element_type=F32)


def tn(a, b):
    return lax.dot_general(a, b, (((0,), (0,)), ((), ())), preferred_element_type=F32)


def norm_parts(values):
    average = jnp.mean(values, axis=-1, keepdims=True)
    centered = values - average
    spread = jnp.mean(centered * centered, axis=-1, keepdims=True)
    scale = lax.rsqrt(spread + EPSILON)
    return centered * scale, scale


def norm_back(grad, normal, scale, gain):
    part = grad * gain
    inner = (
        part
        - jnp.mean(part, axis=-1, keepdims=True)
        - normal * jnp.mean(part * normal, axis=-1, keepdims=True)
    )
    return scale * inner, jnp.sum(grad * normal, axis=0)


def places():
    me = lax.axis_index("seq")
    core = lax.rem(me, 2)
    along_x = lax.rem(me // 2, 2)
    along_y = me // 4
    twin = 1 - 2 * core
    near_x = me + 2 - 4 * along_x
    near_y = me + 4 - 8 * along_y
    across = near_x + 4 - 8 * along_y
    return me, twin, near_x, near_y, across


def remote(src, dst, send_sem, recv_sem, partner):
    return pltpu.make_async_remote_copy(
        src_ref=src,
        dst_ref=dst,
        send_sem=send_sem,
        recv_sem=recv_sem,
        device_id={"seq": partner},
        device_id_type=MESH,
    )


def meet(partners):
    barrier = pltpu.get_barrier_semaphore()
    for partner in partners:
        pl.semaphore_signal(
            barrier, inc=1, device_id={"seq": partner}, device_id_type=MESH
        )
    pl.semaphore_wait(barrier, len(partners))


def gather_copies(x_ref, o_ref, send_sem, recv_sem):
    me, twin, near_x, near_y, across = places()
    half = x_ref.shape[0] // 2
    low, high = pl.ds(0, half), pl.ds(half, half)

    def copy(k, src, dst, partner):
        return remote(src, dst, send_sem.at[k], recv_sem.at[k], partner)

    def relay(k, owner, rows, partner):
        place = o_ref.at[owner, rows]
        return copy(k, place, place, partner)

    return [
        copy(0, x_ref.at[low], o_ref.at[me, low], near_x),
        copy(1, x_ref.at[high], o_ref.at[me, high], near_y),
        copy(2, x_ref.at[high], o_ref.at[me, high], near_x),
        copy(3, x_ref.at[low], o_ref.at[me, low], near_y),
        copy(4, x_ref, o_ref.at[me], me + twin),
        relay(5, near_x, low, near_y),
        relay(6, near_y, high, near_x),
        relay(7, near_x, low, me + twin),
        relay(8, near_y, high, me + twin),
        relay(9, near_x, high, me + twin),
        relay(10, near_y, low, me + twin),
        relay(11, across, low, me + twin),
        relay(12, across, high, me + twin),
    ]


def gather_run(sends, *between):
    between = (*between, *([None] * 3))[:3]

    def pause(i):
        if between[i] is not None:
            between[i]()

    sends[0].wait_recv()
    sends[5].start()
    sends[7].start()
    sends[1].wait_recv()
    sends[6].start()
    sends[8].start()
    pause(0)
    sends[2].wait_recv()
    sends[9].start()
    sends[3].wait_recv()
    sends[10].start()
    pause(1)
    sends[5].wait_recv()
    sends[11].start()
    sends[6].wait_recv()
    sends[12].start()
    pause(2)
    for k in (4, 7, 8, 9, 10, 11, 12):
        sends[k].wait_recv()
    for send in sends:
        send.wait_send()


def meet_all(n, depth):
    me = lax.axis_index("seq")
    z = lax.axis_index("batch")
    barrier = pltpu.get_barrier_semaphore()
    for k in range(1, n):
        pl.semaphore_signal(
            barrier, inc=1, device_id={"seq": lax.rem(me + k, n)}, device_id_type=MESH
        )
    for k in range(1, depth):
        pl.semaphore_signal(
            barrier,
            inc=1,
            device_id={"batch": lax.rem(z + k, depth)},
            device_id_type=MESH,
        )
    pl.semaphore_wait(barrier, n + depth - 2)


def line_remote(src, dst, send_sem, recv_sem, partner):
    return pltpu.make_async_remote_copy(
        src_ref=src,
        dst_ref=dst,
        send_sem=send_sem,
        recv_sem=recv_sem,
        device_id={"batch": partner},
        device_id_type=MESH,
    )


class Line:
    def __init__(self, depth, source, target, send_sem, recv_sem):
        self.depth, self.source, self.target = depth, source, target
        self.send_sem, self.recv_sem = send_sem, recv_sem
        self.z = lax.axis_index("batch")

    def message(self, side, k):
        sign = 2 * side - 1
        owner = self.z - sign * k
        return line_remote(
            self.source(owner, k),
            self.target(owner),
            self.send_sem.at[side, k],
            self.recv_sem.at[side, k],
            self.z + sign,
        )

    def sends(self, side, k):
        sign = 2 * side - 1
        owner, target = self.z - sign * k, self.z + sign
        inside = (owner >= 0) & (owner < self.depth)
        return inside & (target >= 0) & (target < self.depth)

    def land(self, k):
        for side in (0, 1):
            sign = 2 * side - 1
            owner = self.z - sign * (k + 1)

            @pl.when((owner >= 0) & (owner < self.depth))
            def _():
                place = self.target(owner)
                line_remote(
                    place,
                    place,
                    self.send_sem.at[side, k],
                    self.recv_sem.at[side, k],
                    self.z - sign,
                ).wait_recv()

    def start(self, k):
        for side in (0, 1):

            @pl.when(self.sends(side, k))
            def _():
                self.message(side, k).start()

    def sent(self, k):
        for side in (0, 1):

            @pl.when(self.sends(side, k))
            def _():
                self.message(side, k).wait_send()


def lane_tables(place):
    half = HEAD_DIM // 2
    lane = lax.broadcasted_iota(jnp.int32, (1, 128), 1)
    channel = lax.rem(lane, half).astype(F32)
    inverse = jnp.exp(channel * (-math.log(10000.0) / half))
    zeta = (channel * (2.0 / HEAD_DIM) + 0.4) / 1.4
    sign = jnp.where(lax.rem(lane, HEAD_DIM) < half, -1.0, 1.0)
    angle = place * inverse
    growth = jnp.exp((place - 0.5 * LENGTH) * (1.0 / XBASE) * jnp.log(zeta))
    shrink = 1.0 / growth
    cosine = jnp.cos(angle)
    sine = jnp.sin(angle) * sign
    return cosine * growth, sine * growth, cosine * shrink, sine * shrink


def start_kernel(
    n, depth, x_ref, gain_ref, w_ref, wd_ref, pos_ref,
    o_ref, wt_ref, wc_ref, cq_ref, sq_ref, ck_ref, sk_ref,
    normed, keep_w, keep_c, local_sem, send_sem, recv_sem, hop_send, hop_recv, col_send, col_recv,
    line_send, line_recv,
):
    z = lax.axis_index("batch")
    rows_z = wc_ref.shape[2]
    cols = wc_ref.shape[3]
    me, twin, near_x, near_y, _ = places()
    own = pltpu.make_async_copy(normed, o_ref.at[me], local_sem.at[0])
    wd_rows = pl.ds(pl.multiple_of(z * rows_z, rows_z), rows_z)

    def column(k):
        return wd_ref.at[wd_rows, pl.ds(pl.multiple_of(k * cols, cols), cols)]

    load_column = pltpu.make_async_copy(column(me), keep_c, local_sem.at[4])
    own_column = pltpu.make_async_copy(keep_c, wc_ref.at[me, z], local_sem.at[5])
    load_column.start()
    meet_all(n, depth)
    load_column.wait()
    own_column.start()

    def hop(j, part, target):
        return remote(
            w_ref.at[j], wt_ref.at[part], hop_send.at[j], hop_recv.at[part], target
        )

    def load(j):
        return pltpu.make_async_copy(w_ref.at[j], keep_w, local_sem.at[6])

    def here(j, part):
        return pltpu.make_async_copy(keep_w, wt_ref.at[part], local_sem.at[1 + j])

    turns = [
        remote(
            column(lax.rem(me + k, n)),
            wc_ref.at[me, z],
            col_send.at[k],
            col_recv.at[k],
            lax.rem(me + k, n),
        )
        for k in range(1, n)
    ]
    for turn in turns:
        turn.start()
    for j in range(3):
        block = 3 * me + j
        target = lax.rem(block, n)
        for part in range(3):
            inside = block // n == part

            @pl.when(inside & (target != me))
            def _():
                hop(j, part, target).start()

            @pl.when(inside & (target == me))
            def _():
                load(j).start()

    @pl.loop(0, x_ref.shape[0] // STEP)
    def _(r):
        at = pl.ds(pl.multiple_of(r * STEP, STEP), STEP)
        normal, _ = norm_parts(x_ref[at].astype(F32))
        normed[at] = (normal * gain_ref[...]).astype(BF16)

    own.start()
    sends = gather_copies(normed, o_ref, send_sem, recv_sem)
    for k in range(5):
        sends[k].start()

    line = Line(
        depth,
        lambda owner, k: wc_ref.at[:, owner],
        lambda owner: wc_ref.at[:, owner],
        line_send,
        line_recv,
    )

    own_column.wait()
    for turn in turns:
        turn.wait_recv()
    line.start(0)
    for j in range(3):
        block = 3 * me + j
        target = lax.rem(block, n)
        for part in range(3):

            @pl.when((block // n == part) & (target == me))
            def _():
                load(j).wait()
                here(j, part).start()

    @pl.loop(0, pos_ref.shape[0])
    def _(r):
        at = pl.ds(pl.multiple_of(r * 128, 128), 128)
        places_here = jnp.broadcast_to(pos_ref[pl.ds(r, 1), :], (128, 128)).T
        tables = lane_tables(places_here)
        for ref, table in zip((cq_ref, sq_ref, ck_ref, sk_ref), tables, strict=True):
            ref[at] = table

    def hand_on(k):
        def step():
            line.land(k - 1)
            line.start(k)

        return step

    gather_run(sends, *[hand_on(k) for k in range(1, depth - 1)])
    line.land(depth - 2)
    for k in range(depth - 1):
        line.sent(k)
    for turn in turns:
        turn.wait_send()
    for j in range(3):
        block = 3 * me + j
        target = lax.rem(block, n)
        for part in range(3):
            inside = block // n == part

            @pl.when(inside & (target != me))
            def _():
                hop(j, part, target).wait_send()

            @pl.when(inside & (target == me))
            def _():
                here(j, part).wait()

    for part in range(3):
        source = (part * n + me) // 3

        @pl.when(source != me)
        def _():
            hop(0, part, source).wait_recv()

    own.wait()


def start_exchange(block, gain, w_qkv, w_down, positions, collective_id):
    n, depth = lax.axis_size("seq"), lax.axis_size("batch")
    rows, width = block.shape
    piece = w_qkv.shape[0] // 3
    w = w_qkv.reshape(3, piece, width)
    if n != 8:
        me = lax.axis_index("seq")
        turned = [
            lax.ppermute(w[j], "seq", [(d, (3 * d + j) % n) for d in range(n)])
            for j in range(3)
        ]
        parts = [pick_part(turned, me, n, part) for part in range(3)]
        place = jnp.broadcast_to(positions[:, None], (positions.shape[0], 128))
        normed = (norm_parts(block.astype(F32))[0] * gain).astype(BF16)
        return (
            lax.all_gather(normed, "seq", axis=0, tiled=True),
            jnp.concatenate(parts, axis=0),
            lax.all_to_all(w_down, "seq", split_axis=1, concat_axis=0, tiled=True),
            lane_tables(place),
        )
    rows_z, cols = w_down.shape[0] // depth, w_down.shape[1] // n
    inside = pl.BlockSpec(memory_space=pltpu.VMEM)
    table = jax.ShapeDtypeStruct((n * rows, 128), F32)
    gathered, turned, columns, *tables = pl.pallas_call(
        functools.partial(start_kernel, n, depth),
        out_shape=(
            jax.ShapeDtypeStruct((n, rows, width), block.dtype),
            jax.ShapeDtypeStruct((3, piece, width), w.dtype),
            jax.ShapeDtypeStruct((n, depth, rows_z, cols), w_down.dtype),
            *([table] * 4),
        ),
        in_specs=[INSIDE, INSIDE, ANY, ANY, INSIDE],
        out_specs=(ANY, ANY, ANY, *([INSIDE] * 4)),
        scratch_shapes=[
            pltpu.VMEM((rows, width), BF16),
            pltpu.VMEM((piece, width), BF16),
            pltpu.VMEM((rows_z, cols), BF16),
            pltpu.SemaphoreType.DMA((7,)),
            pltpu.SemaphoreType.DMA((13,)),
            pltpu.SemaphoreType.DMA((13,)),
            pltpu.SemaphoreType.DMA((3,)),
            pltpu.SemaphoreType.DMA((3,)),
            pltpu.SemaphoreType.DMA((n,)),
            pltpu.SemaphoreType.DMA((n,)),
            pltpu.SemaphoreType.DMA((2, depth)),
            pltpu.SemaphoreType.DMA((2, depth)),
        ],
        compiler_params=pltpu.CompilerParams(
            collective_id=collective_id, has_side_effects=True, vmem_limit_bytes=VMEM_LIMIT
        ),
        name="start_exchange",
    )(block, gain[None], w, w_down, positions.reshape(-1, 128))
    return (
        gathered.reshape(n * rows, width),
        turned.reshape(3 * piece, width),
        columns.reshape(-1, cols),
        tables,
    )


def scatter_seq(partial):
    return lax.psum_scatter(partial, "seq", scatter_dimension=0, tiled=True).astype(F32)


def heads_to_tokens_kernel(n, x_ref, o_ref, keep, local_sem, send_sem, recv_sem):
    me = lax.axis_index("seq")
    rows = o_ref.shape[0]
    cols = x_ref.shape[1]
    exchange(
        n,
        me,
        lambda k: x_ref.at[pl.ds(pl.multiple_of(k * rows, rows), rows)],
        o_ref.at[:, pl.ds(pl.multiple_of(me * cols, cols), cols)],
        keep,
        local_sem,
        send_sem,
        recv_sem,
    )


def exchange(n, me, source, target, keep, local_sem, send_sem, recv_sem):
    load = pltpu.make_async_copy(source(me), keep, local_sem.at[0])
    own = pltpu.make_async_copy(keep, target, local_sem.at[1])
    load.start()
    barrier = pltpu.get_barrier_semaphore()
    for k in range(1, n):
        pl.semaphore_signal(
            barrier,
            inc=1,
            device_id={"seq": lax.rem(me + k, n)},
            device_id_type=MESH,
        )
    pl.semaphore_wait(barrier, n - 1)
    copies = []
    for k in range(1, n):
        partner = lax.rem(me + k, n)
        copies.append(
            pltpu.make_async_remote_copy(
                src_ref=source(partner),
                dst_ref=target,
                send_sem=send_sem.at[k],
                recv_sem=recv_sem.at[k],
                device_id={"seq": partner},
                device_id_type=MESH,
            )
        )
        copies[-1].start()
    load.wait()
    own.start()
    for copy in copies:
        copy.wait()
    own.wait()


def heads_to_tokens(heads, collective_id):
    n = lax.axis_size("seq")
    total, cols = heads.shape
    rows = total // n
    return pl.pallas_call(
        functools.partial(heads_to_tokens_kernel, n),
        out_shape=jax.ShapeDtypeStruct((rows, n * cols), heads.dtype),
        in_specs=[ANY],
        out_specs=ANY,
        scratch_shapes=[
            pltpu.VMEM((rows, cols), heads.dtype),
            pltpu.SemaphoreType.DMA((2,)),
            pltpu.SemaphoreType.DMA((n,)),
            pltpu.SemaphoreType.DMA((n,)),
        ],
        compiler_params=pltpu.CompilerParams(
            collective_id=collective_id, has_side_effects=True, vmem_limit_bytes=VMEM_LIMIT
        ),
        name="heads_to_tokens",
    )(heads)


def tokens_to_heads_kernel(n, x_ref, o_ref, keep, local_sem, send_sem, recv_sem):
    me = lax.axis_index("seq")
    rows = x_ref.shape[0]
    cols = o_ref.shape[1]
    exchange(
        n,
        me,
        lambda k: x_ref.at[:, pl.ds(pl.multiple_of(k * cols, cols), cols)],
        o_ref.at[pl.ds(pl.multiple_of(me * rows, rows), rows)],
        keep,
        local_sem,
        send_sem,
        recv_sem,
    )


def tokens_to_heads(tokens, collective_id):
    n = lax.axis_size("seq")
    rows, total = tokens.shape
    return pl.pallas_call(
        functools.partial(tokens_to_heads_kernel, n),
        out_shape=jax.ShapeDtypeStruct((rows * n, total // n), tokens.dtype),
        in_specs=[ANY],
        out_specs=ANY,
        scratch_shapes=[
            pltpu.VMEM((rows, total // n), tokens.dtype),
            pltpu.SemaphoreType.DMA((2,)),
            pltpu.SemaphoreType.DMA((n,)),
            pltpu.SemaphoreType.DMA((n,)),
        ],
        compiler_params=pltpu.CompilerParams(
            collective_id=collective_id, has_side_effects=True, vmem_limit_bytes=VMEM_LIMIT
        ),
        name="tokens_to_heads",
    )(tokens)


def swap_halves(values):
    width = values.shape[-1]
    half = HEAD_DIM // 2
    lane = lax.broadcasted_iota(jnp.int32, values.shape, 1)
    ahead = pltpu.roll(values, width - half, 1)
    behind = pltpu.roll(values, half, 1)
    return jnp.where(lane % HEAD_DIM < half, ahead, behind)


def spread_lanes(table, width):
    return jnp.concatenate([table] * (width // table.shape[-1]), axis=-1)


def qkv_kernel(
    x_ref, w_ref, cq_ref, sq_ref, ck_ref, sk_ref,
    q_ref, k_ref, v_ref, kt_ref, vt_ref,
):
    x = x_ref[...]
    width = q_ref.shape[1]
    query = nt(x, w_ref[0:width])
    query = query * spread_lanes(cq_ref[...], width) + swap_halves(
        query
    ) * spread_lanes(sq_ref[...], width)
    q_ref[...] = query.astype(BF16) * (HEAD_DIM**-0.5)
    keys = nt(x, w_ref[width : 2 * width])
    keys = keys * spread_lanes(ck_ref[...], width) + swap_halves(
        keys
    ) * spread_lanes(sk_ref[...], width)
    k_ref[...] = keys.astype(BF16)
    kt_ref[...] = keys.T.astype(BF16)
    values = nt(x, w_ref[2 * width :])
    v_ref[...] = values.astype(BF16)
    vt_ref[...] = values.T.astype(BF16)


def project_qkv(x, w, tables):
    length, width = x.shape
    cols = w.shape[0] // 3
    steps = length // TILE
    weight = pl.BlockSpec((3 * cols, width), lambda i: (0, 0))
    table = pl.BlockSpec((TILE, tables[0].shape[1]), lambda i: (i, 0))
    row_out = pl.BlockSpec((TILE, cols), lambda i: (i, 0))
    col_out = pl.BlockSpec((cols, TILE), lambda i: (0, i))
    rows = jax.ShapeDtypeStruct((length, cols), BF16)
    columns = jax.ShapeDtypeStruct((cols, length), BF16)
    return pl.pallas_call(
        qkv_kernel,
        grid=(steps,),
        out_shape=(rows, rows, rows, columns, columns),
        in_specs=[pl.BlockSpec((TILE, width), lambda i: (i, 0))]
        + [weight]
        + [table] * 4,
        out_specs=(row_out, row_out, row_out, col_out, col_out),
        compiler_params=pltpu.CompilerParams(vmem_limit_bytes=VMEM_LIMIT),
        cost_estimate=pl.CostEstimate(
            flops=6 * length * width * cols,
            bytes_accessed=2 * length * width + 6 * width * cols + 10 * length * cols,
            transcendentals=0,
        ),
        name="project_qkv",
    )(x, w, *tables)


def pair_mask(start_row, i, j):
    key_place = j * TILE + lax.broadcasted_iota(jnp.int32, (TILE, TILE), 0)
    query_place = i * TILE + lax.broadcasted_iota(jnp.int32, (TILE, TILE), 1)
    return (key_place <= query_place) & (key_place >= start_row)


def head_rows(query, heads):
    lane = lax.broadcasted_iota(jnp.int32, query.shape, 1) // HEAD_DIM
    zero = jnp.zeros_like(query)
    return [jnp.where(lane == h, query, zero) for h in range(heads)]


def attend_kernel(
    heads, first_ref, start_ref, q_ref, k_ref, vt_ref, o_ref, lse_ref, peak, total, mixed
):
    i = pl.program_id(0)
    queries = head_rows(q_ref[...], heads)
    start_row = start_ref[...]

    def block(j, first):
        at = pl.ds(pl.multiple_of(j * TILE, TILE), TILE)
        keys = k_ref[at, :]
        mask = pair_mask(start_row, i, j)
        for h in range(heads):
            here = slice(h * HEAD_DIM, (h + 1) * HEAD_DIM)
            scores = jnp.where(mask, nt(keys, queries[h]), MASKED)
            if first:
                new_peak = jnp.max(scores, axis=0, keepdims=True)
                expo = jnp.exp(scores - new_peak)
                total[h : h + 1] = jnp.sum(expo, axis=0, keepdims=True)
                mixed[here] = nn(vt_ref[here, at], expo.astype(BF16))
            else:
                old_peak = peak[h : h + 1]
                new_peak = jnp.maximum(old_peak, jnp.max(scores, axis=0, keepdims=True))
                expo = jnp.exp(scores - new_peak)
                shrink = jnp.exp(old_peak - new_peak)
                total[h : h + 1] = total[h : h + 1] * shrink + jnp.sum(
                    expo, axis=0, keepdims=True
                )
                mixed[here] = mixed[here] * shrink + nn(
                    vt_ref[here, at], expo.astype(BF16)
                )
            peak[h : h + 1] = new_peak

    block(i, True)

    @pl.loop(0, i - first_ref[i])
    def _(t):
        block(i - 1 - t, False)

    for h in range(heads):
        here = slice(h * HEAD_DIM, (h + 1) * HEAD_DIM)
        mixed[here] = mixed[here] / total[h : h + 1]
    o_ref[...] = mixed[...].T.astype(BF16)
    lse_ref[0] = peak[...] + jnp.log(total[...])


def attend(first, start, q, k, vt):
    length, cols = q.shape
    heads = cols // HEAD_DIM
    steps = length // TILE
    row = pl.BlockSpec((TILE, cols), lambda i, *_: (i, 0))
    return pl.pallas_call(
        functools.partial(attend_kernel, heads),
        out_shape=(
            jax.ShapeDtypeStruct((length, cols), BF16),
            jax.ShapeDtypeStruct((steps, heads, TILE), F32),
        ),
        grid_spec=pltpu.PrefetchScalarGridSpec(
            num_scalar_prefetch=1,
            grid=(steps,),
            in_specs=[
                pl.BlockSpec((1, TILE), lambda i, *_: (0, i)),
                row,
                pl.BlockSpec((length, cols), lambda i, *_: (0, 0)),
                pl.BlockSpec((cols, length), lambda i, *_: (0, 0)),
            ],
            out_specs=(
                row,
                pl.BlockSpec((1, heads, TILE), lambda i, *_: (i, 0, 0)),
            ),
            scratch_shapes=[
                pltpu.VMEM((heads, TILE), F32),
                pltpu.VMEM((heads, TILE), F32),
                pltpu.VMEM((cols, TILE), F32),
            ],
        ),
        compiler_params=pltpu.CompilerParams(vmem_limit_bytes=VMEM_LIMIT),
        cost_estimate=pl.CostEstimate(
            flops=4 * length * 1024 * cols,
            bytes_accessed=8 * length * cols,
            transcendentals=length * 1024 * heads,
        ),
        name="attend",
    )(first, start, q, k, vt)


def attend_back_kernel(
    heads, first_ref, start_ref, q_ref, k_ref, kt_ref, v_ref, o_ref, lse_ref, do_ref,
    cq_ref, sq_ref, ck_ref, sk_ref, grad_ref, dqt, dk_sum, dv_sum,
):
    i = pl.program_id(0)
    steps = pl.num_programs(0)
    width = q_ref.shape[1]
    queries = head_rows(q_ref[...], heads)
    grads = head_rows(do_ref[...], heads)
    start_row = start_ref[...]
    product = (do_ref[...].astype(F32) * o_ref[...].astype(F32)).T
    inner = [
        jnp.sum(product[h * HEAD_DIM : (h + 1) * HEAD_DIM], axis=0, keepdims=True)
        for h in range(heads)
    ]

    def block(j, first):
        at = pl.ds(pl.multiple_of(j * TILE, TILE), TILE)
        keys = k_ref[at, :]
        values = v_ref[at, :]
        mask = pair_mask(start_row, i, j)
        key_term = None
        value_term = None
        for h in range(heads):
            here = slice(h * HEAD_DIM, (h + 1) * HEAD_DIM)
            scores = nt(keys, queries[h])
            weights = jnp.where(mask, jnp.exp(scores - lse_ref[0, h : h + 1]), 0.0)
            grad_weights = nt(values, grads[h])
            grad_scores = (weights * (grad_weights - inner[h])).astype(BF16)
            term = nn(weights.astype(BF16), grads[h])
            value_term = term if value_term is None else value_term + term
            term = nn(grad_scores, queries[h])
            key_term = term if key_term is None else key_term + term
            term = nn(kt_ref[here, at], grad_scores)
            if first:
                dqt[here] = term
            else:
                dqt[here] = dqt[here] + term
        if first:
            dk_sum[at] = key_term
            dv_sum[at] = value_term
        else:
            dk_sum[at] = dk_sum[at] + key_term
            dv_sum[at] = dv_sum[at] + value_term

    block(i, True)

    @pl.loop(0, i - first_ref[i])
    def _(t):
        block(i - 1 - t, False)

    def unturn(grad, cosine, sine):
        grad = grad.astype(BF16).astype(F32)
        cosine = spread_lanes(cosine, width)
        sine = spread_lanes(sine, width)
        return (grad * cosine - swap_halves(grad) * sine).astype(BF16)

    rows = pl.ds(pl.multiple_of(i * TILE, TILE), TILE)
    grad_ref[rows, 0:width] = unturn(
        dqt[...].T * (HEAD_DIM**-0.5), cq_ref[rows, :], sq_ref[rows, :]
    )

    @pl.when(i == steps - 1)
    def _():
        @pl.loop(0, steps)
        def _(j):
            at = pl.ds(pl.multiple_of(j * TILE, TILE), TILE)
            grad_ref[at, width : 2 * width] = unturn(
                dk_sum[at], ck_ref[at, :], sk_ref[at, :]
            )
            grad_ref[at, 2 * width :] = dv_sum[at].astype(BF16)


def attend_back(first, start, q, k, kt, v, o, lse, do, tables):
    length, cols = q.shape
    heads = cols // HEAD_DIM
    steps = length // TILE
    row = pl.BlockSpec((TILE, cols), lambda i, *_: (i, 0))
    whole = pl.BlockSpec((length, cols), lambda i, *_: (0, 0))
    table = pl.BlockSpec((length, tables[0].shape[1]), lambda i, *_: (0, 0))
    return pl.pallas_call(
        functools.partial(attend_back_kernel, heads),
        out_shape=jax.ShapeDtypeStruct((length, 3 * cols), BF16),
        grid_spec=pltpu.PrefetchScalarGridSpec(
            num_scalar_prefetch=1,
            grid=(steps,),
            in_specs=[
                pl.BlockSpec((1, TILE), lambda i, *_: (0, i)),
                row,
                whole,
                pl.BlockSpec((cols, length), lambda i, *_: (0, 0)),
                whole,
                row,
                pl.BlockSpec((1, heads, TILE), lambda i, *_: (i, 0, 0)),
                row,
            ]
            + [table] * 4,
            out_specs=pl.BlockSpec((length, 3 * cols), lambda i, *_: (0, 0)),
            scratch_shapes=[
                pltpu.VMEM((cols, TILE), F32),
                pltpu.VMEM((length, cols), F32),
                pltpu.VMEM((length, cols), F32),
            ],
        ),
        compiler_params=pltpu.CompilerParams(vmem_limit_bytes=VMEM_LIMIT),
        name="attend_back",
    )(first, start, q, k, kt, v, o, lse, do, *tables)


def upper_kernel(
    x_ref, wu_ref, c_ref, wd_ref, gain_ref, act_ref, slope_ref, grad_ref, stat_ref
):
    upper = nt(x_ref[...], wu_ref[...])
    grad = nn(c_ref[...], wd_ref[...])
    below = 0.5 * (1.0 + lax.erf(upper * (0.5**0.5)))
    act = upper * below
    slope = below + upper * (jnp.exp(-0.5 * upper * upper) * ((2.0 * math.pi) ** -0.5))
    act_ref[...] = act
    slope_ref[...] = slope.astype(BF16)
    grad_ref[...] = grad
    part = grad * gain_ref[...]
    average = jnp.mean(act, axis=-1, keepdims=True)
    centered = act - average
    spread = jnp.sum(centered * centered, axis=-1, keepdims=True)
    part_sum = jnp.sum(part, axis=-1, keepdims=True)
    cross = jnp.sum(part * centered, axis=-1, keepdims=True)
    lane = lax.broadcasted_iota(jnp.int32, (x_ref.shape[0], 128), 1)
    columns = jnp.where(
        lane == 0,
        average,
        jnp.where(lane == 1, spread, jnp.where(lane == 2, part_sum, cross)),
    )
    stat_ref[...] = columns.T[:8]


def upper_pass(x, w_up, cot, w_down, gain):
    length, width = x.shape
    feats = w_up.shape[0]
    rows = TILE
    row = pl.BlockSpec((rows, width), lambda i: (i, 0))
    out = pl.BlockSpec((rows, feats), lambda i: (i, 0))
    return pl.pallas_call(
        upper_kernel,
        grid=(length // rows,),
        out_shape=(
            jax.ShapeDtypeStruct((length, feats), F32),
            jax.ShapeDtypeStruct((length, feats), BF16),
            jax.ShapeDtypeStruct((length, feats), F32),
            jax.ShapeDtypeStruct((8, length), F32),
        ),
        in_specs=[
            row,
            pl.BlockSpec((feats, width), lambda i: (0, 0)),
            row,
            pl.BlockSpec((width, feats), lambda i: (0, 0)),
            pl.BlockSpec((1, feats), lambda i: (0, 0)),
        ],
        out_specs=(out, out, out, pl.BlockSpec((8, rows), lambda i: (0, i))),
        compiler_params=pltpu.CompilerParams(vmem_limit_bytes=VMEM_LIMIT),
        cost_estimate=pl.CostEstimate(
            flops=4 * length * width * feats,
            bytes_accessed=8 * length * width + 8 * length * feats,
            transcendentals=2 * length * feats,
        ),
        name="upper_pass",
    )(x, w_up, cot, w_down, gain)


def hidden_kernel(act_ref, slope_ref, grad_ref, stat_ref, gain_ref, hid_ref, gu_ref, gg_ref):
    i = pl.program_id(0)
    stats = stat_ref[...].T
    average = stats[:, 0:1]
    scale = stats[:, 1:2]
    part_mean = stats[:, 2:3]
    cross_mean = stats[:, 3:4]
    gain = gain_ref[...]
    normal = (act_ref[...] - average) * scale
    grad = grad_ref[...]
    hid_ref[...] = (normal * gain).astype(BF16)
    back = scale * (grad * gain - part_mean - normal * cross_mean)
    gu_ref[...] = (slope_ref[...].astype(F32) * back).astype(BF16)
    term = jnp.sum(grad * normal, axis=0, keepdims=True)

    @pl.when(i == 0)
    def _():
        gg_ref[...] = term

    @pl.when(i > 0)
    def _():
        gg_ref[...] = gg_ref[...] + term


def hidden_pass(act, slope, grad, stats, gain):
    length, feats = act.shape
    out = pl.BlockSpec((TILE, feats), lambda i: (i, 0))
    one = pl.BlockSpec((1, feats), lambda i: (0, 0))
    return pl.pallas_call(
        hidden_kernel,
        grid=(length // TILE,),
        out_shape=(
            jax.ShapeDtypeStruct((length, feats), BF16),
            jax.ShapeDtypeStruct((length, feats), BF16),
            jax.ShapeDtypeStruct((1, feats), F32),
        ),
        in_specs=[out, out, out, pl.BlockSpec((8, TILE), lambda i: (0, i)), one],
        out_specs=(out, out, one),
        compiler_params=pltpu.CompilerParams(vmem_limit_bytes=VMEM_LIMIT),
        cost_estimate=pl.CostEstimate(
            flops=12 * length * feats,
            bytes_accessed=14 * length * feats,
            transcendentals=0,
        ),
        name="hidden_pass",
    )(act, slope, grad, stats, gain)


def ffn_kernel(
    n, x_ref, wu_ref, cot_ref, wd_ref, gain_ref,
    full_ref, hid_ref, gu_ref, gg_ref,
    rows_in, wd, cot_in, act, slope, grad, stat, held, results,
    local_sem, cot_sem, out_sem, full_sem, send_sem, recv_sem, stat_send, stat_recv,
):
    me, twin, near_x, near_y, across = places()
    rows = x_ref.shape[0]
    feats = wu_ref.shape[0]

    def cut(i, size=rows):
        return pl.ds(pl.multiple_of(i * size, size), size)

    own = pltpu.make_async_copy(x_ref, rows_in.at[me], local_sem.at[0])
    own.start()
    load_wd = pltpu.make_async_copy(wd_ref, wd, local_sem.at[1])
    load_wd.start()

    def load_cot(i, slot):
        return pltpu.make_async_copy(
            cot_ref.at[cut(i)], cot_in.at[slot], cot_sem.at[slot]
        )

    load_cot(0, 0).start()
    meet([lax.rem(me + k, n) for k in range(1, n)])
    sends = gather_copies(x_ref, rows_in, send_sem, recv_sem)
    for k in range(5):
        sends[k].start()

    load_wd.wait()
    def incoming(first, last):
        @pl.loop(first, last)
        def _(i):
            slot = lax.rem(i, 2)

            @pl.when(i + 1 < n)
            def _():
                load_cot(i + 1, 1 - slot).start()

            load_cot(i, slot).wait()
            grad[cut(i)] = nn(cot_in[slot], wd[...])

    incoming(0, n - 2)
    sends[0].wait_recv()
    sends[5].start()
    sends[7].start()
    sends[1].wait_recv()
    sends[6].start()
    sends[8].start()
    incoming(n - 2, n)
    own.wait()

    def keep(b):
        return pltpu.make_async_copy(rows_in.at[b], full_ref.at[b], full_sem.at[b])

    @pl.loop(0, n)
    def _(i):
        @pl.when(i == 1)
        def _():
            sends[4].wait_recv()

        @pl.when(i == 2)
        def _():
            sends[2].wait_recv()
            sends[9].start()
            sends[3].wait_recv()
            sends[10].start()

        @pl.when(i == 4)
        def _():
            sends[7].wait_recv()
            sends[9].wait_recv()

        @pl.when(i == 5)
        def _():
            sends[8].wait_recv()
            sends[10].wait_recv()
            sends[5].wait_recv()
            sends[11].start()
            sends[6].wait_recv()
            sends[12].start()

        @pl.when(i == 7)
        def _():
            sends[11].wait_recv()
            sends[12].wait_recv()

        other = jnp.where((i == 1) | (i == 4) | (i == 5) | (i == 7), twin, 0)
        place = jnp.where(i < 2, me, jnp.where(i >= 6, across, jnp.where(lax.rem(i, 2) == 0, near_x, near_y)))
        b = place + other
        keep(b).start()
        at = cut(b)
        upper = nt(rows_in[b], wu_ref[...])
        below = 0.5 * (1.0 + lax.erf(upper * (0.5**0.5)))
        value = upper * below
        act[at] = value
        slope[at] = (
            below + upper * (jnp.exp(-0.5 * upper * upper) * ((2.0 * math.pi) ** -0.5))
        ).astype(BF16)
        part = grad[at] * gain_ref[...]
        average = jnp.mean(value, axis=-1, keepdims=True)
        centered = value - average
        spread = jnp.sum(centered * centered, axis=-1, keepdims=True)
        part_sum = jnp.sum(part, axis=-1, keepdims=True)
        cross = jnp.sum(part * centered, axis=-1, keepdims=True)
        lane = lax.broadcasted_iota(jnp.int32, (rows, 128), 1)
        columns = jnp.where(
            lane == 0,
            average,
            jnp.where(lane == 1, spread, jnp.where(lane == 2, part_sum, cross)),
        )
        stat[:, at] = columns.T[:8]

    held[me] = stat[...]
    rounds = [
        remote(
            stat, held.at[me], stat_send.at[k], stat_recv.at[k], lax.rem(me + k, n)
        )
        for k in range(1, n)
    ]
    for send in rounds:
        send.start()
    for send in rounds:
        send.wait()
    join_rows(n, feats, held, stat)

    def store(i, slot):
        return [
            pltpu.make_async_copy(
                results.at[slot, j], ref.at[cut(i)], out_sem.at[slot, j]
            )
            for j, ref in enumerate((hid_ref, gu_ref))
        ]

    gg_ref[...] = jnp.zeros_like(gg_ref)

    @pl.loop(0, n)
    def _(i):
        slot = lax.rem(i, 2)

        @pl.when(i >= 2)
        def _():
            for copy in store(i - 2, slot):
                copy.wait()

        at = cut(i)
        stats = stat[:, at].T
        gain = gain_ref[...]
        scale = stats[:, 1:2]
        normal = (act[at] - stats[:, 0:1]) * scale
        coming = grad[at]
        results[slot, 0] = (normal * gain).astype(BF16)
        back = scale * (coming * gain - stats[:, 2:3] - normal * stats[:, 3:4])
        results[slot, 1] = (slope[at].astype(F32) * back).astype(BF16)
        gg_ref[...] = gg_ref[...] + jnp.sum(coming * normal, axis=0, keepdims=True)
        for copy in store(i, slot):
            copy.start()

    for i in (n - 2, n - 1):
        for copy in store(i, i % 2):
            copy.wait()
    for b in range(n):
        keep(b).wait()
    for send in sends:
        send.wait_send()


def ffn_pass(ffn_in, w_up, cot, w_down, gain, collective_id):
    n = lax.axis_size("seq")
    rows, width = ffn_in.shape
    feats = w_up.shape[0]
    if n != 8:
        full = lax.all_gather(ffn_in, "seq", axis=0, tiled=True)
        act, slope, grad, stat = upper_pass(full, w_up, cot, w_down, gain)
        stats = join_stats(stat, feats, collective_id)
        return (full, *hidden_pass(act, slope, grad, stats, gain))
    length = n * rows
    dma = pltpu.SemaphoreType.DMA
    low = jax.ShapeDtypeStruct((length, feats), BF16)
    full, hidden, grad_upper, gain_grad = pl.pallas_call(
        functools.partial(ffn_kernel, n),
        out_shape=(
            jax.ShapeDtypeStruct((n, rows, width), BF16),
            low,
            low,
            jax.ShapeDtypeStruct((1, feats), F32),
        ),
        in_specs=[INSIDE, INSIDE, ANY, ANY, INSIDE],
        out_specs=(ANY, ANY, ANY, INSIDE),
        scratch_shapes=[
            pltpu.VMEM((n, rows, width), BF16),
            pltpu.VMEM((width, feats), BF16),
            pltpu.VMEM((2, rows, width), BF16),
            pltpu.VMEM((length, feats), F32),
            pltpu.VMEM((length, feats), BF16),
            pltpu.VMEM((length, feats), F32),
            pltpu.VMEM((8, length), F32),
            pltpu.VMEM((n, 8, length), F32),
            pltpu.VMEM((2, 2, rows, feats), BF16),
            dma((2,)),
            dma((2,)),
            dma((2, 2)),
            dma((n,)),
            dma((13,)),
            dma((13,)),
            dma((n,)),
            dma((n,)),
        ],
        compiler_params=pltpu.CompilerParams(
            collective_id=collective_id, has_side_effects=True, vmem_limit_bytes=VMEM_LIMIT
        ),
        name="ffn_pass",
    )(ffn_in, w_up, cot, w_down, gain)
    return full.reshape(length, width), hidden, grad_upper, gain_grad


def join_rows(n, feats, held, o_ref):
    average = held[0, 0:1]
    for d in range(1, n):
        average = average + held[d, 0:1]
    average = average * (1.0 / n)
    spread = jnp.zeros_like(average)
    part = jnp.zeros_like(average)
    cross = jnp.zeros_like(average)
    for d in range(n):
        shift = held[d, 0:1] - average
        spread = spread + held[d, 1:2] + feats * (shift * shift)
        part = part + held[d, 2:3]
        cross = cross + held[d, 3:4] + shift * held[d, 2:3]
    whole = 1.0 / (n * feats)
    scale = lax.rsqrt(spread * whole + EPSILON)
    o_ref[0:1] = average
    o_ref[1:2] = scale
    o_ref[2:3] = part * whole
    o_ref[3:4] = cross * scale * whole
    o_ref[4:8] = jnp.zeros((4, average.shape[1]), F32)


def stat_kernel(n, feats, x_ref, o_ref, held, send_sem, recv_sem):
    me = lax.axis_index("seq")
    held[me] = x_ref[...]
    meet([lax.rem(me + k, n) for k in range(1, n)])
    copies = [
        remote(x_ref, held.at[me], send_sem.at[k], recv_sem.at[k], lax.rem(me + k, n))
        for k in range(1, n)
    ]
    for copy in copies:
        copy.start()
    for copy in copies:
        copy.wait()
    join_rows(n, feats, held, o_ref)


def join_stats(stat, feats, collective_id):
    n = lax.axis_size("seq")
    inside = pl.BlockSpec(memory_space=pltpu.VMEM)
    return pl.pallas_call(
        functools.partial(stat_kernel, n, feats),
        out_shape=jax.ShapeDtypeStruct(stat.shape, F32),
        in_specs=[inside],
        out_specs=inside,
        scratch_shapes=[
            pltpu.VMEM((n, *stat.shape), F32),
            pltpu.SemaphoreType.DMA((n,)),
            pltpu.SemaphoreType.DMA((n,)),
        ],
        compiler_params=pltpu.CompilerParams(
            collective_id=collective_id, has_side_effects=True, vmem_limit_bytes=VMEM_LIMIT
        ),
        name="join_stats",
    )(stat)


def mix_kernel(att_ref, x_ref, w_ref, gm_ref, gf_ref, mix_ref, mid_ref, ffn_ref):
    j = pl.program_id(0)
    rows = att_ref.shape[0]
    cols = w_ref.shape[0]

    @pl.when(j == 0)
    def _():
        @pl.loop(0, rows // STEP)
        def _(r):
            at = pl.ds(pl.multiple_of(r * STEP, STEP), STEP)
            normal, _ = norm_parts(att_ref[at].astype(F32))
            mix_ref[at] = (normal * gm_ref[...]).astype(BF16)

    here = pl.ds(pl.multiple_of(j * cols, cols), cols)
    mid_ref[:, here] = x_ref[:, here].astype(F32) + nt(mix_ref[...], w_ref[...])

    @pl.when(j == pl.num_programs(0) - 1)
    def _():
        @pl.loop(0, rows // STEP)
        def _(r):
            at = pl.ds(pl.multiple_of(r * STEP, STEP), STEP)
            normal, _ = norm_parts(mid_ref[at])
            ffn_ref[at] = (normal * gf_ref[...]).astype(BF16)


def mix_pass(attended, x, w_out, gain_mix, gain_ffn):
    rows, width = x.shape
    cols = TILE
    n = width // cols
    whole = pl.BlockSpec((rows, width), lambda j: (0, 0))
    gain = pl.BlockSpec((1, width), lambda j: (0, 0))
    low = jax.ShapeDtypeStruct((rows, width), BF16)
    return pl.pallas_call(
        mix_kernel,
        grid=(n,),
        out_shape=(low, jax.ShapeDtypeStruct((rows, width), F32), low),
        in_specs=[
            whole,
            whole,
            pl.BlockSpec((cols, width), lambda j: (j, 0)),
            gain,
            gain,
        ],
        out_specs=(whole, whole, whole),
        compiler_params=pltpu.CompilerParams(vmem_limit_bytes=VMEM_LIMIT),
        cost_estimate=pl.CostEstimate(
            flops=2 * rows * width * width,
            bytes_accessed=2 * width * width + 12 * rows * width,
            transcendentals=0,
        ),
        name="mix_pass",
    )(attended, x, w_out, gain_mix[None], gain_ffn[None])


def branch_kernel(gbr_ref, att_ref, w_ref, gm_ref, gatt_ref, ggm_ref, total):
    j = pl.program_id(0)
    rows = att_ref.shape[0]
    cols = w_ref.shape[0]
    here = pl.ds(pl.multiple_of(j * cols, cols), cols)
    term = nn(gbr_ref[:, here], w_ref[...])

    @pl.when(j == 0)
    def _():
        total[...] = term

    @pl.when(j > 0)
    def _():
        total[...] = total[...] + term

    @pl.when(j == pl.num_programs(0) - 1)
    def _():
        ggm_ref[...] = jnp.zeros_like(ggm_ref)

        @pl.loop(0, rows // STEP)
        def _(r):
            at = pl.ds(pl.multiple_of(r * STEP, STEP), STEP)
            normal, scale = norm_parts(att_ref[at].astype(F32))
            part, gain_part = norm_back(total[at], normal, scale, gm_ref[...])
            ggm_ref[...] += gain_part[None]
            gatt_ref[at] = part.astype(BF16)


def branch_pass(grad_branch, attended, w_out, gain_mix):
    rows, width = grad_branch.shape
    cols = TILE
    n = width // cols
    whole = pl.BlockSpec((rows, width), lambda j: (0, 0))
    gain = pl.BlockSpec((1, width), lambda j: (0, 0))
    return pl.pallas_call(
        branch_kernel,
        grid=(n,),
        out_shape=(
            jax.ShapeDtypeStruct((rows, width), BF16),
            jax.ShapeDtypeStruct((1, width), F32),
        ),
        in_specs=[whole, whole, pl.BlockSpec((cols, width), lambda j: (j, 0)), gain],
        out_specs=(whole, gain),
        scratch_shapes=[pltpu.VMEM((rows, width), F32)],
        compiler_params=pltpu.CompilerParams(vmem_limit_bytes=VMEM_LIMIT),
        name="branch_pass",
    )(grad_branch, attended, w_out, gain_mix[None])


def ffn_back_kernel(
    n, gu_ref, wu_ref, hid_ref, wd_ref, all_ref, mid_ref, cot_ref, gf_ref,
    po_ref, gd_ref, gmid_ref, gbr_ref, ggf_ref,
    gu, hid, every, own, far, twin_in, held, made, made_grad,
    local_sem, made_sem, grad_sem, send_sem, recv_sem,
):
    me, twin, near_x, near_y, across = places()
    rows, width = mid_ref.shape
    half = rows // 2
    low, high = pl.ds(0, half), pl.ds(half, half)
    mine = (across, near_x, near_y, me)

    def cut(i, size=rows):
        return pl.ds(pl.multiple_of(i * size, size), size)

    load_gu = pltpu.make_async_copy(gu_ref, gu, local_sem.at[0])
    load_hid = pltpu.make_async_copy(hid_ref, hid, local_sem.at[1])
    load_all = pltpu.make_async_copy(all_ref, every, local_sem.at[2])
    for load in (load_gu, load_hid, load_all):
        load.start()
    meet((me + twin, near_x, near_y))
    load_gu.wait()

    def copy(k, src, dst, partner):
        return remote(src, dst, send_sem.at[k], recv_sem.at[k], partner)

    twins = [copy(i, far.at[i], twin_in.at[i], me + twin) for i in range(4)]
    sends = [
        copy(4, own.at[0, low], held.at[0], near_x),
        copy(5, own.at[0, high], held.at[1], near_y),
        copy(6, own.at[1, low], held.at[2], near_x),
        copy(7, own.at[2, high], held.at[3], near_y),
        copy(8, own.at[1, high], held.at[4], near_x),
        copy(9, own.at[2, low], held.at[5], near_y),
    ]

    def add(i, base, count, source):
        @pl.loop(0, count // STEP)
        def _(r):
            at = cut(r, STEP)
            to = pl.ds(pl.multiple_of(base + r * STEP, STEP), STEP)
            own[i, to] = (own[i, to].astype(F32) + source[at].astype(F32)).astype(BF16)

    for i, block in enumerate(mine):
        far[i] = nn(gu[cut(block + twin)], wu_ref[...]).astype(BF16)
        twins[i].start()
        own[i] = nn(gu[cut(block)], wu_ref[...]).astype(BF16)
        if i < 3:
            twins[i].wait_recv()
            add(i, 0, rows, twin_in.at[i])
        if i == 0:
            sends[0].start()
            sends[1].start()
        elif i < 3:
            sends[i + 1].start()

    def store(i, slot):
        return pltpu.make_async_copy(made.at[slot], po_ref.at[cut(i)], made_sem.at[slot])

    def outputs(first, last):
        @pl.loop(first, last)
        def _(i):
            slot = lax.rem(i, 2)

            @pl.when(i >= 2)
            def _():
                store(i - 2, slot).wait()

            made[slot] = nt(hid[cut(i)], wd_ref[...]).astype(BF16)
            store(i, slot).start()

    def store_grad(i, slot):
        return pltpu.make_async_copy(
            made_grad.at[slot], gd_ref.at[i], grad_sem.at[slot]
        )

    def weight_grads(first, last):
        for i in range(first, last):
            slot = i % 2
            if i >= 2:
                store_grad(i - 2, slot).wait()
            made_grad[slot] = tn(
                every[:, i * rows : (i + 1) * rows], hid[...]
            ).astype(BF16)
            store_grad(i, slot).start()

    load_hid.wait()
    load_all.wait()
    weight_grads(0, n // 2)
    sends[1].wait_recv()
    add(1, half, half, held.at[1])
    sends[4].start()
    sends[0].wait_recv()
    add(2, 0, half, held.at[0])
    sends[5].start()
    weight_grads(n // 2, n)
    outputs(0, n)
    twins[3].wait_recv()
    for k in (2, 3, 4, 5):
        sends[k].wait_recv()
    ggf_ref[...] = jnp.zeros_like(ggf_ref)
    for base, one, two in ((0, 2, 5), (half, 3, 4)):

        @pl.loop(0, half // STEP)
        def _(r):
            at = cut(r, STEP)
            to = pl.ds(pl.multiple_of(base + r * STEP, STEP), STEP)
            value = (
                own[3, to].astype(F32)
                + twin_in[3, to].astype(F32)
                + held[one, at].astype(F32)
                + held[two, at].astype(F32)
            )
            normal, scale = norm_parts(mid_ref[to])
            part, gain_part = norm_back(value, normal, scale, gf_ref[...])
            ggf_ref[...] = ggf_ref[...] + gain_part[None]
            grad = cot_ref[to].astype(F32) + part
            gmid_ref[to] = grad
            gbr_ref[to] = grad.astype(BF16)

    for i in (n - 2, n - 1):
        store(i, i % 2).wait()
        store_grad(i, i % 2).wait()
    for send in twins + sends:
        send.wait_send()


def ffn_back(grad_upper, w_up, hidden, w_down, cot_full, middle, cot, gain, collective_id):
    n = lax.axis_size("seq")
    rows, width = middle.shape
    feats = w_up.shape[0]
    if n != 8:
        normal, scale = norm_parts(middle)
        value = scatter_seq(nn(grad_upper, w_up).astype(BF16))
        part, gain_part = norm_back(value, normal, scale, gain)
        grad = cot.astype(F32) + part
        down = tn(cot_full, hidden).astype(BF16).reshape(n, rows, feats)
        outputs = nt(hidden, w_down).astype(BF16)
        return outputs, down, grad, grad.astype(BF16), gain_part[None]
    dma = pltpu.SemaphoreType.DMA
    block = pltpu.VMEM((4, rows, width), BF16)
    return pl.pallas_call(
        functools.partial(ffn_back_kernel, n),
        out_shape=(
            jax.ShapeDtypeStruct((n * rows, width), BF16),
            jax.ShapeDtypeStruct((n, rows, feats), BF16),
            jax.ShapeDtypeStruct((rows, width), F32),
            jax.ShapeDtypeStruct((rows, width), BF16),
            jax.ShapeDtypeStruct((1, width), F32),
        ),
        in_specs=[ANY, INSIDE, ANY, INSIDE, ANY, INSIDE, INSIDE, INSIDE],
        out_specs=(ANY, ANY, INSIDE, INSIDE, INSIDE),
        scratch_shapes=[
            pltpu.VMEM((n * rows, feats), BF16),
            pltpu.VMEM((n * rows, feats), BF16),
            pltpu.VMEM((n * rows, width), BF16),
            block,
            block,
            block,
            pltpu.VMEM((6, rows // 2, width), BF16),
            pltpu.VMEM((2, rows, width), BF16),
            pltpu.VMEM((2, rows, feats), BF16),
            dma((3,)),
            dma((2,)),
            dma((2,)),
            dma((10,)),
            dma((10,)),
        ],
        compiler_params=pltpu.CompilerParams(
            collective_id=collective_id, has_side_effects=True, vmem_limit_bytes=VMEM_LIMIT
        ),
        name="ffn_back",
    )(grad_upper, w_up, hidden, w_down, cot_full, middle, cot, gain[None])


CHUNK = 64


def finish_kernel(
    n, depth, gq_ref, gd_ref, pw_ref, pn_ref, po_ref, x_ref, grad_ref, mid_ref, ga_ref, gm_ref, gf_ref, gh_ref,
    oq_ref, od_ref, ow_ref, gi_ref, out_ref, sums_ref,
    own, twin_in, held, zown, zin, stage, gain_here, gain_row, gain_pack, gain_line,
    local_sem, load_sem, stage_sem, send_sem, recv_sem, keep_sem,
    up_send, up_recv, down_send, down_recv, home_send, home_recv, gain_send, gain_recv,
):
    me, twin, near_x, near_y, across = places()
    z = lax.axis_index("batch")
    rows, width = pn_ref.shape[1:]
    half = rows // 2
    low, high = pl.ds(0, half), pl.ds(half, half)
    mine = (across, near_x, near_y, me)
    _, chunk, cols = zown.shape
    across_width = width // cols
    per_part = (gq_ref.shape[1] // chunk) * across_width
    turned = gq_ref.shape[0] * per_part
    per_source = gd_ref.shape[1] // chunk
    outer = turned + gd_ref.shape[0] * per_source
    chunks = zown.shape[0]
    per_side = chunks // 2

    def cut(i, size):
        return pl.ds(pl.multiple_of(i * size, size), size)

    def wide(i):
        return cut(i // across_width, chunk), cut(lax.rem(i, across_width), cols)

    line_loads = []
    for g in range(turned):
        source = gq_ref.at[(g // per_part, *wide(g % per_part))]
        line_loads.append(pltpu.make_async_copy(source, zown.at[g], load_sem.at[g]))
    for g in range(turned, outer):
        source = gd_ref.at[
            (g - turned) // per_source, cut((g - turned) % per_source, chunk)
        ]
        line_loads.append(pltpu.make_async_copy(source, zown.at[g], load_sem.at[g]))
    for load in line_loads:
        load.start()
    partials = (pw_ref, pn_ref, po_ref)
    loads = [
        [
            pltpu.make_async_copy(p.at[block], own.at[m, i], local_sem.at[4 * m + i])
            for i, block in enumerate(mine)
        ]
        for m, p in enumerate(partials)
    ]
    for part in loads:
        for load in part:
            load.start()
    meet_all(n, depth)

    def copy(m, k, src, dst, partner):
        return remote(src, dst, send_sem.at[m, k], recv_sem.at[m, k], partner)

    twins = [
        [
            copy(m, i, p.at[block + twin], twin_in.at[m, i], me + twin)
            for i, block in enumerate(mine)
        ]
        for m, p in enumerate(partials)
    ]
    sends = [
        [
            copy(m, 4, own.at[m, 0, low], held.at[m, 0], near_x),
            copy(m, 5, own.at[m, 0, high], held.at[m, 1], near_y),
            copy(m, 6, own.at[m, 1, low], held.at[m, 2], near_x),
            copy(m, 7, own.at[m, 2, high], held.at[m, 3], near_y),
            copy(m, 8, own.at[m, 1, high], held.at[m, 4], near_x),
            copy(m, 9, own.at[m, 2, low], held.at[m, 5], near_y),
        ]
        for m in range(3)
    ]
    for part in twins:
        for send in part:
            send.start()

    def add_twin(m, i):
        loads[m][i].wait()
        twins[m][i].wait_recv()

        @pl.loop(0, rows // STEP)
        def _(r):
            at = cut(r, STEP)
            own[m, i, at] = (
                own[m, i, at].astype(F32) + twin_in[m, i, at].astype(F32)
            ).astype(BF16)

    def add_held(m, i, base, slot):
        @pl.loop(0, half // STEP)
        def _(r):
            at = cut(r, STEP)
            to = pl.ds(pl.multiple_of(base + r * STEP, STEP), STEP)
            own[m, i, to] = (
                own[m, i, to].astype(F32) + held[m, slot, at].astype(F32)
            ).astype(BF16)

    def first(m):
        add_twin(m, 0)
        sends[m][0].start()
        sends[m][1].start()
        add_twin(m, 1)
        sends[m][2].start()
        add_twin(m, 2)
        sends[m][3].start()

    def second(m):
        sends[m][1].wait_recv()
        add_held(m, 1, half, 1)
        sends[m][4].start()
        sends[m][0].wait_recv()
        add_held(m, 2, 0, 0)
        sends[m][5].start()

    def last(m, store):
        loads[m][3].wait()
        twins[m][3].wait_recv()
        for k in (2, 3, 4, 5):
            sends[m][k].wait_recv()
        for base, one, two in ((0, 2, 5), (half, 3, 4)):

            @pl.loop(0, half // STEP)
            def _(r):
                at = cut(r, STEP)
                place = base + r * STEP
                to = pl.ds(pl.multiple_of(place, STEP), STEP)
                store(
                    place,
                    to,
                    own[m, 3, to].astype(F32)
                    + twin_in[m, 3, to].astype(F32)
                    + held[m, one, at].astype(F32)
                    + held[m, two, at].astype(F32),
                )

    def store_line(place, to, value):
        value = value.astype(BF16)
        for side in range(across_width):
            zown[
                outer + (place // chunk) * across_width + side,
                pl.ds(pl.multiple_of(lax.rem(place, chunk), STEP), STEP),
            ] = value[:, side * cols : (side + 1) * cols]

    def store_inputs(place, to, value):
        normal, scale = norm_parts(x_ref[to].astype(F32))
        part, gain_part = norm_back(value, normal, scale, ga_ref[...])
        gi_ref[to] = grad_ref[to] + part
        gain_here[0:1] = gain_here[0:1] + gain_part[None]

    def store_outputs(place, to, value):
        out_ref[to] = (mid_ref[to] + value).astype(BF16)

    def home(part):
        block = part * n + me
        return block // 3, lax.rem(block, 3)

    def deliver_far(g):
        target, slot = home(g // per_part)
        piece = lax.rem(g, per_part)
        return remote(
            zin.at[g],
            oq_ref.at[(slot, *wide(piece))],
            home_send.at[g],
            home_recv.at[slot, piece],
            target,
        )

    def deliver_near(g):
        _, slot = home(g // per_part)
        return pltpu.make_async_copy(
            zin.at[g], oq_ref.at[(slot, *wide(lax.rem(g, per_part)))], keep_sem.at[g]
        )

    def widen(g):
        @pl.loop(0, chunk // STEP)
        def _(r):
            at = cut(r, STEP)
            stage[at] = zin[g, at].astype(F32)

    def deliver(g):
        target, _ = home(g // per_part)

        @pl.when((g < turned) & (target != me))
        def _():
            deliver_far(g).start()

        @pl.when((g < turned) & (target == me))
        def _():
            deliver_near(g).start()

        @pl.when((g >= turned) & (g < outer))
        def _():
            widen(g)
            at = g - turned
            place = cut(lax.rem(at, per_source), chunk), cut(at // per_source, cols)
            store = pltpu.make_async_copy(stage, od_ref.at[place], stage_sem)
            store.start()
            store.wait()

        @pl.when(g >= outer)
        def _():
            widen(g)
            store = pltpu.make_async_copy(
                stage, ow_ref.at[wide(g - outer)], stage_sem
            )
            store.start()
            store.wait()

    def delivered(g):
        target, _ = home(g // per_part)

        @pl.when(target != me)
        def _():
            deliver_far(g).wait_send()

        @pl.when(target == me)
        def _():
            deliver_near(g).wait()

    def go_up(g, ahead):
        return line_remote(zown.at[g], zin.at[g], up_send.at[g], up_recv.at[g], ahead)

    def go_down(g, behind):
        return line_remote(
            zin.at[g], zin.at[g], down_send.at[g], down_recv.at[g], behind
        )

    def ranks(side):
        if side == 0:
            return z, z + 1, z - 1
        return depth - 1 - z, z - 1, z + 1

    def add_line(g, target):
        @pl.loop(0, chunk // STEP)
        def _(r):
            at = cut(r, STEP)
            target[g, at] = (zown[g, at].astype(F32) + zin[g, at].astype(F32)).astype(
                BF16
            )

    lead = 2
    far = 2 * (depth - 1)
    steps = per_side + 2 * far

    def line_enter(c):
        for side in (0, 1):
            rank, ahead, _ = ranks(side)

            @pl.when(rank == 0)
            def _():
                go_up(2 * c + side, ahead).start()

    def line_step(t):
        @pl.when(t + lead < per_side)
        def _():
            line_enter(t + lead)

        back = []
        for side in (0, 1):
            rank, ahead, behind = ranks(side)
            c_back = t - 2 * far + 2 * rank
            g_back = 2 * c_back + side
            there = (c_back >= 0) & (c_back < per_side) & (rank < depth - 1)
            back.append((there, g_back))

            @pl.when(there)
            def _():
                go_down(g_back, ahead).wait_recv()

            @pl.when(there & (rank > 0))
            def _():
                go_down(g_back, behind).start()

        for side in (0, 1):
            rank, ahead, behind = ranks(side)
            c = t - 2 * rank
            g = 2 * c + side
            there = (c >= 0) & (c < per_side)

            @pl.when(there & (rank > 0) & (rank < depth - 1))
            def _():
                go_up(g, behind).wait_recv()
                add_line(g, zown)
                go_up(g, ahead).start()

            @pl.when(there & (rank == depth - 1))
            def _():
                go_up(g, behind).wait_recv()
                add_line(g, zin)
                go_down(g, behind).start()
                deliver(g)

        for there, g_back in back:

            @pl.when(there)
            def _():
                deliver(g_back)

    def line_steps(first_step, last_step):
        @pl.loop(first_step, last_step)
        def _(t):
            line_step(t)

    gain_here[...] = jnp.zeros_like(gain_here)
    for load in line_loads:
        load.wait()
    for c in range(lead):
        line_enter(c)
    first(0)
    line_steps(0, 8)
    second(0)
    line_steps(8, 9)
    first(1)
    line_steps(9, 18)
    last(0, store_line)
    line_steps(18, 20)
    second(1)
    line_steps(20, 21)
    first(2)
    line_steps(21, 28)
    last(1, store_inputs)

    gain_here[1:2] = gm_ref[...]
    gain_here[2:3] = gf_ref[...]
    gain_here[3:4, 0 : gh_ref.shape[1]] = gh_ref[...]
    gain_row[me] = gain_here[...]
    rounds = [
        remote(
            gain_here,
            gain_row.at[me],
            gain_send.at[0, k],
            gain_recv.at[0, k],
            lax.rem(me + k, n),
        )
        for k in range(1, n)
    ]
    for send in rounds:
        send.start()
    line_steps(28, 32)
    second(2)
    line_steps(32, 40)
    last(2, store_outputs)
    line_steps(40, 42)
    for send in rounds:
        send.wait()
    total = gain_row[0]
    for d in range(1, n):
        total = total + gain_row[d]
    gain_pack[0:8] = total
    for d in range(n):
        gain_pack[8 + d : 9 + d] = gain_row[d, 3:4]
    gain_line[z] = gain_pack[...]
    rounds = [
        line_remote(
            gain_pack,
            gain_line.at[z],
            gain_send.at[1, k],
            gain_recv.at[1, k],
            lax.rem(z + k, depth),
        )
        for k in range(1, depth)
    ]
    for send in rounds:
        send.start()
    line_steps(42, steps)
    for send in rounds:
        send.wait()
    total = gain_line[0]
    for d in range(1, depth):
        total = total + gain_line[d]
    sums_ref[...] = total

    for m in range(3):
        for send in twins[m] + sends[m]:
            send.wait_send()
    for g in range(chunks):
        rank, ahead, behind = ranks(g % 2)

        @pl.when(rank < depth - 1)
        def _():
            go_up(g, ahead).wait_send()

        @pl.when(rank > 0)
        def _():
            go_down(g, behind).wait_send()

    for g in range(turned):
        delivered(g)
    for slot in range(3):
        block = 3 * me + slot
        source = lax.rem(block, n)

        @pl.when(source != me)
        def _():
            for piece in range(per_part):
                remote(
                    zin.at[0],
                    oq_ref.at[(slot, *wide(piece))],
                    home_send.at[0],
                    home_recv.at[slot, piece],
                    source,
                ).wait_recv()


def finish(
    grad_qkv, grad_down, part_out, part_normed, part_outputs, x, grad_middle, middle, gain, gains, collective_id
):
    n, depth = lax.axis_size("seq"), lax.axis_size("batch")
    rows, width = part_out.shape[0] // n, part_out.shape[1]
    cols = grad_qkv.shape[1]
    sources, _, feats = grad_down.shape
    if n != 8 or depth != 4:
        me = lax.axis_index("seq")
        blocks = lax.psum(grad_qkv, "batch")
        back = [
            lax.ppermute(
                give_part(blocks, me, n, j),
                "seq",
                [((3 * d + j) % n, d) for d in range(n)],
            )
            for j in range(3)
        ]
        w_out = lax.psum(scatter_seq(part_out).astype(BF16), "batch")
        normal, scale = norm_parts(x.astype(F32))
        part, gain_part = norm_back(scatter_seq(part_normed), normal, scale, gain)
        shared = [lax.psum(g, ("batch", "seq")) for g in (gain_part, gains[0][0], gains[1][0])]
        hidden = lax.all_gather(lax.psum(gains[2][0], "batch"), "seq", axis=0, tiled=True)
        down = lax.psum(grad_down, "batch")
        return (
            jnp.concatenate(back, axis=0),
            jnp.swapaxes(down, 0, 1).reshape(rows, sources * feats).astype(F32),
            w_out.astype(F32),
            grad_middle + part,
            (middle + scatter_seq(part_outputs)).astype(BF16),
            (*shared, hidden),
        )
    chunks = (
        3 * cols * width + rows * width + sources * rows * feats
    ) // (CHUNK * feats)
    dma = pltpu.SemaphoreType.DMA
    line = pltpu.VMEM((chunks, CHUNK, feats), BF16)
    w_qkv, w_down, w_out, grad_inputs, outputs, sums = pl.pallas_call(
        functools.partial(finish_kernel, n, depth),
        out_shape=(
            jax.ShapeDtypeStruct((3, cols, width), BF16),
            jax.ShapeDtypeStruct((rows, sources * feats), F32),
            jax.ShapeDtypeStruct((rows, width), F32),
            jax.ShapeDtypeStruct((rows, width), F32),
            jax.ShapeDtypeStruct((rows, width), BF16),
            jax.ShapeDtypeStruct((16, width), F32),
        ),
        in_specs=[ANY] * 5 + [INSIDE] * 7,
        out_specs=(ANY, ANY, ANY, INSIDE, INSIDE, INSIDE),
        scratch_shapes=[
            pltpu.VMEM((3, 4, rows, width), BF16),
            pltpu.VMEM((3, 4, rows, width), BF16),
            pltpu.VMEM((3, 6, rows // 2, width), BF16),
            line,
            line,
            pltpu.VMEM((CHUNK, feats), F32),
            pltpu.VMEM((8, width), F32),
            pltpu.VMEM((n, 8, width), F32),
            pltpu.VMEM((16, width), F32),
            pltpu.VMEM((depth, 16, width), F32),
            dma((12,)),
            dma((chunks,)),
            dma,
            dma((3, 10)),
            dma((3, 10)),
            dma((chunks,)),
            dma((chunks,)),
            dma((chunks,)),
            dma((chunks,)),
            dma((chunks,)),
            dma((chunks,)),
            dma((3, cols * width // (CHUNK * feats))),
            dma((2, n)),
            dma((2, n)),
        ],
        compiler_params=pltpu.CompilerParams(
            collective_id=collective_id,
            has_side_effects=True,
            vmem_limit_bytes=VMEM_LIMIT,
        ),
        name="finish",
    )(
        grad_qkv,
        grad_down,
        *[p.reshape(n, rows, width) for p in (part_out, part_normed, part_outputs)],
        x,
        grad_middle,
        middle,
        gain[None],
        *gains,
    )
    return (
        w_qkv.reshape(3 * cols, width),
        w_down,
        w_out,
        grad_inputs,
        outputs,
        (sums[0], sums[1], sums[2], sums[8:, :feats].reshape(-1)),
    )


def widen_kernel(*refs):
    half = len(refs) // 2
    for source, target in zip(refs[:half], refs[half:], strict=True):
        target[...] = source[...].astype(F32)


def widen(arrays):
    steps = 8
    specs = [pl.BlockSpec((x.shape[0] // steps, x.shape[1]), lambda i: (i, 0)) for x in arrays]
    return pl.pallas_call(
        widen_kernel,
        grid=(steps,),
        out_shape=[jax.ShapeDtypeStruct(x.shape, F32) for x in arrays],
        in_specs=specs,
        out_specs=specs,
        compiler_params=pltpu.CompilerParams(vmem_limit_bytes=VMEM_LIMIT),
        name="widen",
    )(*arrays)


def body(
    inputs,
    segment_ids,
    w_qkv,
    w_out,
    w_up,
    w_down,
    gain_attn,
    gain_mix,
    gain_ffn,
    gain_hidden,
    cotangent,
):
    _, local, width = inputs.shape
    n, depth = lax.axis_size("seq"), lax.axis_size("batch")
    me = lax.axis_index("seq")
    length = local * n
    feats = w_up.shape[0]
    x_low = inputs[0]
    cot = cotangent[0]
    segment = segment_ids[0]

    w_out_full = lax.all_gather(w_out, "seq", axis=0, tiled=True)
    before = [jnp.sum((segment < d).astype(jnp.int32)) for d in range(1, DOCS)]
    start = jnp.zeros_like(segment)
    for d in range(1, DOCS):
        start = jnp.where(segment == d, before[d - 1], start)
    positions = jnp.arange(length, dtype=jnp.int32) - start
    first = start[::TILE] // TILE
    start_row = start[None, :]

    normed_full, w_heads, w_down_cols, tables = start_exchange(
        x_low, gain_attn, w_qkv, w_down, positions.astype(F32), 1
    )
    cot_full = lax.all_gather(lax.optimization_barrier(cot), "seq", axis=0, tiled=True)

    q, k, v, kt, vt = project_qkv(normed_full, w_heads, tables)
    attended_heads, lse = attend(first, start_row, q, k, vt)
    attended = heads_to_tokens(attended_heads, 2)
    mix_in, middle, ffn_in = mix_pass(attended, x_low, w_out_full, gain_mix, gain_ffn)
    gain_here = lax.dynamic_slice_in_dim(gain_hidden, me * feats, feats, 0)[None, :]
    ffn_full, hidden, grad_upper, grad_gain_here = ffn_pass(
        ffn_in, w_up, cot_full, w_down_cols, gain_here, 3
    )

    grad_w_up = tn(grad_upper, ffn_full).astype(BF16)
    grad_upper, grad_w_up = lax.optimization_barrier((grad_upper, grad_w_up))
    grad_w_up = lax.psum(grad_w_up, "batch")
    part_outputs, grad_w_down, grad_middle, grad_branch, grad_gain_ffn = ffn_back(
        grad_upper, w_up, hidden, w_down_cols, cot_full, middle, cot, gain_ffn, 4
    )
    grad_att, grad_gain_mix = branch_pass(grad_branch, attended, w_out_full, gain_mix)
    grad_heads = tokens_to_heads(grad_att, 5)
    grad_w_down, grad_heads = lax.optimization_barrier((grad_w_down, grad_heads))
    grad_w_down = lax.all_to_all(grad_w_down, "seq", split_axis=0, concat_axis=0, tiled=True)
    grads = attend_back(
        first, start_row, q, k, kt, v, attended_heads, lse, grad_heads, tables
    )
    grad_w_qkv = tn(grads, normed_full).astype(BF16).reshape(3, -1, width)
    grad_w_qkv, grad_w_up = lax.optimization_barrier((grad_w_qkv, grad_w_up))
    grad_w_qkv, grad_w_down, grad_w_out, grad_inputs, outputs, gains = finish(
        grad_w_qkv,
        grad_w_down,
        tn(grad_branch, mix_in).astype(BF16),
        nn(grads, w_heads).astype(BF16),
        part_outputs,
        x_low,
        grad_middle,
        middle,
        gain_attn,
        (grad_gain_mix, grad_gain_ffn, grad_gain_here),
        6,
    )
    grad_w_qkv, grad_w_up = widen([grad_w_qkv, grad_w_up])
    return (
        outputs[None],
        grad_inputs[None],
        grad_w_qkv,
        grad_w_out,
        grad_w_up,
        grad_w_down,
        *gains,
    )


def pick_part(turned, me, n, part):
    chosen = turned[0]
    home = part * n + me
    for j in (1, 2):
        chosen = jnp.where(lax.rem(home, 3) == j, turned[j], chosen)
    return chosen


def give_part(blocks, me, n, j):
    chosen = blocks[0]
    for part in (1, 2):
        chosen = jnp.where(lax.rem(part * n + me, 3) == j, blocks[part], chosen)
    return chosen


def solution(mesh):
    in_specs = (
        P("batch", "seq", None),
        P("batch", None),
        P("seq", None),
        P("seq", None),
        P("seq", None),
        P("seq", None),
        P(),
        P(),
        P(),
        P(),
        P("batch", "seq", None),
    )
    out_specs = (
        P("batch", "seq", None),
        P("batch", "seq", None),
        P("seq", None),
        P("seq", None),
        P("seq", None),
        P("seq", None),
        P(),
        P(),
        P(),
        P(),
    )
    return jax.shard_map(body, mesh=mesh, in_specs=in_specs, out_specs=out_specs, check_vma=False)
```

```python
import functools
import math

import jax
import jax.numpy as jnp
from jax import lax
from jax.experimental import pallas as pl
from jax.experimental.pallas import tpu as pltpu
from jax.sharding import PartitionSpec as P

HEADS = 32
HEAD_DIM = 64
LENGTH = 2048
XBASE = 512
DOCS = 4
EPSILON = 1e-05
MASKED = -1e30
TILE = 256
STEP = 32
VMEM_LIMIT = 60 * 1024 * 1024

MESH = pl.DeviceIdType.MESH
F32 = jnp.float32
BF16 = jnp.bfloat16
ANY = pl.BlockSpec(memory_space=pl.ANY)
INSIDE = pl.BlockSpec(memory_space=pltpu.VMEM)


def nn(a, b):
    return lax.dot_general(a, b, (((1,), (0,)), ((), ())), preferred_element_type=F32)


def nt(a, b):
    return lax.dot_general(a, b, (((1,), (1,)), ((), ())), preferred_element_type=F32)


def tn(a, b):
    return lax.dot_general(a, b, (((0,), (0,)), ((), ())), preferred_element_type=F32)


def norm_parts(values):
    average = jnp.mean(values, axis=-1, keepdims=True)
    centered = values - average
    spread = jnp.mean(centered * centered, axis=-1, keepdims=True)
    scale = lax.rsqrt(spread + EPSILON)
    return centered * scale, scale


def norm_back(grad, normal, scale, gain):
    part = grad * gain
    inner = (
        part
        - jnp.mean(part, axis=-1, keepdims=True)
        - normal * jnp.mean(part * normal, axis=-1, keepdims=True)
    )
    return scale * inner, jnp.sum(grad * normal, axis=0)


def places():
    me = lax.axis_index("seq")
    core = lax.rem(me, 2)
    along_x = lax.rem(me // 2, 2)
    along_y = me // 4
    twin = 1 - 2 * core
    near_x = me + 2 - 4 * along_x
    near_y = me + 4 - 8 * along_y
    across = near_x + 4 - 8 * along_y
    return me, twin, near_x, near_y, across


def remote(src, dst, send_sem, recv_sem, partner):
    return pltpu.make_async_remote_copy(
        src_ref=src,
        dst_ref=dst,
        send_sem=send_sem,
        recv_sem=recv_sem,
        device_id={"seq": partner},
        device_id_type=MESH,
    )


def meet(partners):
    barrier = pltpu.get_barrier_semaphore()
    for partner in partners:
        pl.semaphore_signal(
            barrier, inc=1, device_id={"seq": partner}, device_id_type=MESH
        )
    pl.semaphore_wait(barrier, len(partners))


def gather_copies(x_ref, o_ref, send_sem, recv_sem):
    me, twin, near_x, near_y, across = places()
    half = x_ref.shape[0] // 2
    low, high = pl.ds(0, half), pl.ds(half, half)

    def copy(k, src, dst, partner):
        return remote(src, dst, send_sem.at[k], recv_sem.at[k], partner)

    def relay(k, owner, rows, partner):
        place = o_ref.at[owner, rows]
        return copy(k, place, place, partner)

    return [
        copy(0, x_ref.at[low], o_ref.at[me, low], near_x),
        copy(1, x_ref.at[high], o_ref.at[me, high], near_y),
        copy(2, x_ref.at[high], o_ref.at[me, high], near_x),
        copy(3, x_ref.at[low], o_ref.at[me, low], near_y),
        copy(4, x_ref, o_ref.at[me], me + twin),
        relay(5, near_x, low, near_y),
        relay(6, near_y, high, near_x),
        relay(7, near_x, low, me + twin),
        relay(8, near_y, high, me + twin),
        relay(9, near_x, high, me + twin),
        relay(10, near_y, low, me + twin),
        relay(11, across, low, me + twin),
        relay(12, across, high, me + twin),
    ]


def gather_run(sends, *between):
    between = (*between, *([None] * 3))[:3]

    def pause(i):
        if between[i] is not None:
            between[i]()

    sends[0].wait_recv()
    sends[5].start()
    sends[7].start()
    sends[1].wait_recv()
    sends[6].start()
    sends[8].start()
    pause(0)
    sends[2].wait_recv()
    sends[9].start()
    sends[3].wait_recv()
    sends[10].start()
    pause(1)
    sends[5].wait_recv()
    sends[11].start()
    sends[6].wait_recv()
    sends[12].start()
    pause(2)
    for k in (4, 7, 8, 9, 10, 11, 12):
        sends[k].wait_recv()
    for send in sends:
        send.wait_send()


def meet_all(n, depth):
    me = lax.axis_index("seq")
    z = lax.axis_index("batch")
    barrier = pltpu.get_barrier_semaphore()
    for k in range(1, n):
        pl.semaphore_signal(
            barrier, inc=1, device_id={"seq": lax.rem(me + k, n)}, device_id_type=MESH
        )
    for k in range(1, depth):
        pl.semaphore_signal(
            barrier,
            inc=1,
            device_id={"batch": lax.rem(z + k, depth)},
            device_id_type=MESH,
        )
    pl.semaphore_wait(barrier, n + depth - 2)


def line_remote(src, dst, send_sem, recv_sem, partner):
    return pltpu.make_async_remote_copy(
        src_ref=src,
        dst_ref=dst,
        send_sem=send_sem,
        recv_sem=recv_sem,
        device_id={"batch": partner},
        device_id_type=MESH,
    )


class Line:
    def __init__(self, depth, source, target, send_sem, recv_sem):
        self.depth, self.source, self.target = depth, source, target
        self.send_sem, self.recv_sem = send_sem, recv_sem
        self.z = lax.axis_index("batch")

    def message(self, side, k):
        sign = 2 * side - 1
        owner = self.z - sign * k
        return line_remote(
            self.source(owner, k),
            self.target(owner),
            self.send_sem.at[side, k],
            self.recv_sem.at[side, k],
            self.z + sign,
        )

    def sends(self, side, k):
        sign = 2 * side - 1
        owner, target = self.z - sign * k, self.z + sign
        inside = (owner >= 0) & (owner < self.depth)
        return inside & (target >= 0) & (target < self.depth)

    def land(self, k):
        for side in (0, 1):
            sign = 2 * side - 1
            owner = self.z - sign * (k + 1)

            @pl.when((owner >= 0) & (owner < self.depth))
            def _():
                place = self.target(owner)
                line_remote(
                    place,
                    place,
                    self.send_sem.at[side, k],
                    self.recv_sem.at[side, k],
                    self.z - sign,
                ).wait_recv()

    def start(self, k):
        for side in (0, 1):

            @pl.when(self.sends(side, k))
            def _():
                self.message(side, k).start()

    def sent(self, k):
        for side in (0, 1):

            @pl.when(self.sends(side, k))
            def _():
                self.message(side, k).wait_send()


def lane_tables(place):
    half = HEAD_DIM // 2
    lane = lax.broadcasted_iota(jnp.int32, (1, 128), 1)
    channel = lax.rem(lane, half).astype(F32)
    inverse = jnp.exp(channel * (-math.log(10000.0) / half))
    zeta = (channel * (2.0 / HEAD_DIM) + 0.4) / 1.4
    sign = jnp.where(lax.rem(lane, HEAD_DIM) < half, -1.0, 1.0)
    angle = place * inverse
    growth = jnp.exp((place - 0.5 * LENGTH) * (1.0 / XBASE) * jnp.log(zeta))
    shrink = 1.0 / growth
    cosine = jnp.cos(angle)
    sine = jnp.sin(angle) * sign
    return cosine * growth, sine * growth, cosine * shrink, sine * shrink


def start_kernel(
    n, depth, x_ref, gain_ref, w_ref, wd_ref, pos_ref,
    o_ref, wt_ref, wc_ref, cq_ref, sq_ref, ck_ref, sk_ref,
    normed, keep_w, keep_c, local_sem, send_sem, recv_sem, hop_send, hop_recv, col_send, col_recv,
    line_send, line_recv,
):
    z = lax.axis_index("batch")
    rows_z = wc_ref.shape[2]
    cols = wc_ref.shape[3]
    me, twin, near_x, near_y, _ = places()
    own = pltpu.make_async_copy(normed, o_ref.at[me], local_sem.at[0])
    wd_rows = pl.ds(pl.multiple_of(z * rows_z, rows_z), rows_z)

    def column(k):
        return wd_ref.at[wd_rows, pl.ds(pl.multiple_of(k * cols, cols), cols)]

    load_column = pltpu.make_async_copy(column(me), keep_c, local_sem.at[4])
    own_column = pltpu.make_async_copy(keep_c, wc_ref.at[me, z], local_sem.at[5])
    load_column.start()
    meet_all(n, depth)
    load_column.wait()
    own_column.start()

    def hop(j, part, target):
        return remote(
            w_ref.at[j], wt_ref.at[part], hop_send.at[j], hop_recv.at[part], target
        )

    def load(j):
        return pltpu.make_async_copy(w_ref.at[j], keep_w, local_sem.at[6])

    def here(j, part):
        return pltpu.make_async_copy(keep_w, wt_ref.at[part], local_sem.at[1 + j])

    turns = [
        remote(
            column(lax.rem(me + k, n)),
            wc_ref.at[me, z],
            col_send.at[k],
            col_recv.at[k],
            lax.rem(me + k, n),
        )
        for k in range(1, n)
    ]
    for turn in turns:
        turn.start()
    for j in range(3):
        block = 3 * me + j
        target = lax.rem(block, n)
        for part in range(3):
            inside = block // n == part

            @pl.when(inside & (target != me))
            def _():
                hop(j, part, target).start()

            @pl.when(inside & (target == me))
            def _():
                load(j).start()

    @pl.loop(0, x_ref.shape[0] // STEP)
    def _(r):
        at = pl.ds(pl.multiple_of(r * STEP, STEP), STEP)
        normal, _ = norm_parts(x_ref[at].astype(F32))
        normed[at] = (normal * gain_ref[...]).astype(BF16)

    own.start()
    sends = gather_copies(normed, o_ref, send_sem, recv_sem)
    for k in range(5):
        sends[k].start()

    line = Line(
        depth,
        lambda owner, k: wc_ref.at[:, owner],
        lambda owner: wc_ref.at[:, owner],
        line_send,
        line_recv,
    )

    own_column.wait()
    for turn in turns:
        turn.wait_recv()
    line.start(0)
    for j in range(3):
        block = 3 * me + j
        target = lax.rem(block, n)
        for part in range(3):

            @pl.when((block // n == part) & (target == me))
            def _():
                load(j).wait()
                here(j, part).start()

    @pl.loop(0, pos_ref.shape[0])
    def _(r):
        at = pl.ds(pl.multiple_of(r * 128, 128), 128)
        places_here = jnp.broadcast_to(pos_ref[pl.ds(r, 1), :], (128, 128)).T
        tables = lane_tables(places_here)
        for ref, table in zip((cq_ref, sq_ref, ck_ref, sk_ref), tables, strict=True):
            ref[at] = table

    def hand_on(k):
        def step():
            line.land(k - 1)
            line.start(k)

        return step

    gather_run(sends, *[hand_on(k) for k in range(1, depth - 1)])
    line.land(depth - 2)
    for k in range(depth - 1):
        line.sent(k)
    for turn in turns:
        turn.wait_send()
    for j in range(3):
        block = 3 * me + j
        target = lax.rem(block, n)
        for part in range(3):
            inside = block // n == part

            @pl.when(inside & (target != me))
            def _():
                hop(j, part, target).wait_send()

            @pl.when(inside & (target == me))
            def _():
                here(j, part).wait()

    for part in range(3):
        source = (part * n + me) // 3

        @pl.when(source != me)
        def _():
            hop(0, part, source).wait_recv()

    own.wait()


def start_exchange(block, gain, w_qkv, w_down, positions, collective_id):
    n, depth = lax.axis_size("seq"), lax.axis_size("batch")
    rows, width = block.shape
    piece = w_qkv.shape[0] // 3
    w = w_qkv.reshape(3, piece, width)
    if n != 8:
        me = lax.axis_index("seq")
        turned = [
            lax.ppermute(w[j], "seq", [(d, (3 * d + j) % n) for d in range(n)])
            for j in range(3)
        ]
        parts = [pick_part(turned, me, n, part) for part in range(3)]
        place = jnp.broadcast_to(positions[:, None], (positions.shape[0], 128))
        normed = (norm_parts(block.astype(F32))[0] * gain).astype(BF16)
        return (
            lax.all_gather(normed, "seq", axis=0, tiled=True),
            jnp.concatenate(parts, axis=0),
            lax.all_to_all(w_down, "seq", split_axis=1, concat_axis=0, tiled=True),
            lane_tables(place),
        )
    rows_z, cols = w_down.shape[0] // depth, w_down.shape[1] // n
    inside = pl.BlockSpec(memory_space=pltpu.VMEM)
    table = jax.ShapeDtypeStruct((n * rows, 128), F32)
    gathered, turned, columns, *tables = pl.pallas_call(
        functools.partial(start_kernel, n, depth),
        out_shape=(
            jax.ShapeDtypeStruct((n, rows, width), block.dtype),
            jax.ShapeDtypeStruct((3, piece, width), w.dtype),
            jax.ShapeDtypeStruct((n, depth, rows_z, cols), w_down.dtype),
            *([table] * 4),
        ),
        in_specs=[INSIDE, INSIDE, ANY, ANY, INSIDE],
        out_specs=(ANY, ANY, ANY, *([INSIDE] * 4)),
        scratch_shapes=[
            pltpu.VMEM((rows, width), BF16),
            pltpu.VMEM((piece, width), BF16),
            pltpu.VMEM((rows_z, cols), BF16),
            pltpu.SemaphoreType.DMA((7,)),
            pltpu.SemaphoreType.DMA((13,)),
            pltpu.SemaphoreType.DMA((13,)),
            pltpu.SemaphoreType.DMA((3,)),
            pltpu.SemaphoreType.DMA((3,)),
            pltpu.SemaphoreType.DMA((n,)),
            pltpu.SemaphoreType.DMA((n,)),
            pltpu.SemaphoreType.DMA((2, depth)),
            pltpu.SemaphoreType.DMA((2, depth)),
        ],
        compiler_params=pltpu.CompilerParams(
            collective_id=collective_id, has_side_effects=True, vmem_limit_bytes=VMEM_LIMIT
        ),
        name="start_exchange",
    )(block, gain[None], w, w_down, positions.reshape(-1, 128))
    return (
        gathered.reshape(n * rows, width),
        turned.reshape(3 * piece, width),
        columns.reshape(-1, cols),
        tables,
    )


def scatter_seq(partial):
    return lax.psum_scatter(partial, "seq", scatter_dimension=0, tiled=True).astype(F32)


def heads_to_tokens_kernel(n, x_ref, o_ref, keep, local_sem, send_sem, recv_sem):
    me = lax.axis_index("seq")
    rows = o_ref.shape[0]
    cols = x_ref.shape[1]
    exchange(
        n,
        me,
        lambda k: x_ref.at[pl.ds(pl.multiple_of(k * rows, rows), rows)],
        o_ref.at[:, pl.ds(pl.multiple_of(me * cols, cols), cols)],
        keep,
        local_sem,
        send_sem,
        recv_sem,
    )


def exchange(n, me, source, target, keep, local_sem, send_sem, recv_sem):
    load = pltpu.make_async_copy(source(me), keep, local_sem.at[0])
    own = pltpu.make_async_copy(keep, target, local_sem.at[1])
    load.start()
    barrier = pltpu.get_barrier_semaphore()
    for k in range(1, n):
        pl.semaphore_signal(
            barrier,
            inc=1,
            device_id={"seq": lax.rem(me + k, n)},
            device_id_type=MESH,
        )
    pl.semaphore_wait(barrier, n - 1)
    copies = []
    for k in range(1, n):
        partner = lax.rem(me + k, n)
        copies.append(
            pltpu.make_async_remote_copy(
                src_ref=source(partner),
                dst_ref=target,
                send_sem=send_sem.at[k],
                recv_sem=recv_sem.at[k],
                device_id={"seq": partner},
                device_id_type=MESH,
            )
        )
        copies[-1].start()
    load.wait()
    own.start()
    for copy in copies:
        copy.wait()
    own.wait()


def heads_to_tokens(heads, collective_id):
    n = lax.axis_size("seq")
    total, cols = heads.shape
    rows = total // n
    return pl.pallas_call(
        functools.partial(heads_to_tokens_kernel, n),
        out_shape=jax.ShapeDtypeStruct((rows, n * cols), heads.dtype),
        in_specs=[ANY],
        out_specs=ANY,
        scratch_shapes=[
            pltpu.VMEM((rows, cols), heads.dtype),
            pltpu.SemaphoreType.DMA((2,)),
            pltpu.SemaphoreType.DMA((n,)),
            pltpu.SemaphoreType.DMA((n,)),
        ],
        compiler_params=pltpu.CompilerParams(
            collective_id=collective_id, has_side_effects=True, vmem_limit_bytes=VMEM_LIMIT
        ),
        name="heads_to_tokens",
    )(heads)


def tokens_to_heads_kernel(n, x_ref, o_ref, keep, local_sem, send_sem, recv_sem):
    me = lax.axis_index("seq")
    rows = x_ref.shape[0]
    cols = o_ref.shape[1]
    exchange(
        n,
        me,
        lambda k: x_ref.at[:, pl.ds(pl.multiple_of(k * cols, cols), cols)],
        o_ref.at[pl.ds(pl.multiple_of(me * rows, rows), rows)],
        keep,
        local_sem,
        send_sem,
        recv_sem,
    )


def tokens_to_heads(tokens, collective_id):
    n = lax.axis_size("seq")
    rows, total = tokens.shape
    return pl.pallas_call(
        functools.partial(tokens_to_heads_kernel, n),
        out_shape=jax.ShapeDtypeStruct((rows * n, total // n), tokens.dtype),
        in_specs=[ANY],
        out_specs=ANY,
        scratch_shapes=[
            pltpu.VMEM((rows, total // n), tokens.dtype),
            pltpu.SemaphoreType.DMA((2,)),
            pltpu.SemaphoreType.DMA((n,)),
            pltpu.SemaphoreType.DMA((n,)),
        ],
        compiler_params=pltpu.CompilerParams(
            collective_id=collective_id, has_side_effects=True, vmem_limit_bytes=VMEM_LIMIT
        ),
        name="tokens_to_heads",
    )(tokens)


def swap_halves(values):
    width = values.shape[-1]
    half = HEAD_DIM // 2
    lane = lax.broadcasted_iota(jnp.int32, values.shape, 1)
    ahead = pltpu.roll(values, width - half, 1)
    behind = pltpu.roll(values, half, 1)
    return jnp.where(lane % HEAD_DIM < half, ahead, behind)


def spread_lanes(table, width):
    return jnp.concatenate([table] * (width // table.shape[-1]), axis=-1)


def qkv_kernel(
    x_ref, w_ref, cq_ref, sq_ref, ck_ref, sk_ref,
    q_ref, k_ref, v_ref, kt_ref, vt_ref,
):
    x = x_ref[...]
    width = q_ref.shape[1]
    query = nt(x, w_ref[0:width])
    query = query * spread_lanes(cq_ref[...], width) + swap_halves(
        query
    ) * spread_lanes(sq_ref[...], width)
    q_ref[...] = query.astype(BF16) * (HEAD_DIM**-0.5)
    keys = nt(x, w_ref[width : 2 * width])
    keys = keys * spread_lanes(ck_ref[...], width) + swap_halves(
        keys
    ) * spread_lanes(sk_ref[...], width)
    k_ref[...] = keys.astype(BF16)
    kt_ref[...] = keys.T.astype(BF16)
    values = nt(x, w_ref[2 * width :])
    v_ref[...] = values.astype(BF16)
    vt_ref[...] = values.T.astype(BF16)


def project_qkv(x, w, tables):
    length, width = x.shape
    cols = w.shape[0] // 3
    steps = length // TILE
    weight = pl.BlockSpec((3 * cols, width), lambda i: (0, 0))
    table = pl.BlockSpec((TILE, tables[0].shape[1]), lambda i: (i, 0))
    row_out = pl.BlockSpec((TILE, cols), lambda i: (i, 0))
    col_out = pl.BlockSpec((cols, TILE), lambda i: (0, i))
    rows = jax.ShapeDtypeStruct((length, cols), BF16)
    columns = jax.ShapeDtypeStruct((cols, length), BF16)
    return pl.pallas_call(
        qkv_kernel,
        grid=(steps,),
        out_shape=(rows, rows, rows, columns, columns),
        in_specs=[pl.BlockSpec((TILE, width), lambda i: (i, 0))]
        + [weight]
        + [table] * 4,
        out_specs=(row_out, row_out, row_out, col_out, col_out),
        compiler_params=pltpu.CompilerParams(vmem_limit_bytes=VMEM_LIMIT),
        cost_estimate=pl.CostEstimate(
            flops=6 * length * width * cols,
            bytes_accessed=2 * length * width + 6 * width * cols + 10 * length * cols,
            transcendentals=0,
        ),
        name="project_qkv",
    )(x, w, *tables)


def pair_mask(start_row, i, j):
    key_place = j * TILE + lax.broadcasted_iota(jnp.int32, (TILE, TILE), 0)
    query_place = i * TILE + lax.broadcasted_iota(jnp.int32, (TILE, TILE), 1)
    return (key_place <= query_place) & (key_place >= start_row)


def head_rows(query, heads):
    lane = lax.broadcasted_iota(jnp.int32, query.shape, 1) // HEAD_DIM
    zero = jnp.zeros_like(query)
    return [jnp.where(lane == h, query, zero) for h in range(heads)]


def attend_kernel(
    heads, first_ref, start_ref, q_ref, k_ref, vt_ref, o_ref, lse_ref, peak, total, mixed
):
    i = pl.program_id(0)
    queries = head_rows(q_ref[...], heads)
    start_row = start_ref[...]

    def block(j, first):
        at = pl.ds(pl.multiple_of(j * TILE, TILE), TILE)
        keys = k_ref[at, :]
        mask = pair_mask(start_row, i, j)
        for h in range(heads):
            here = slice(h * HEAD_DIM, (h + 1) * HEAD_DIM)
            scores = jnp.where(mask, nt(keys, queries[h]), MASKED)
            if first:
                new_peak = jnp.max(scores, axis=0, keepdims=True)
                expo = jnp.exp(scores - new_peak)
                total[h : h + 1] = jnp.sum(expo, axis=0, keepdims=True)
                mixed[here] = nn(vt_ref[here, at], expo.astype(BF16))
            else:
                old_peak = peak[h : h + 1]
                new_peak = jnp.maximum(old_peak, jnp.max(scores, axis=0, keepdims=True))
                expo = jnp.exp(scores - new_peak)
                shrink = jnp.exp(old_peak - new_peak)
                total[h : h + 1] = total[h : h + 1] * shrink + jnp.sum(
                    expo, axis=0, keepdims=True
                )
                mixed[here] = mixed[here] * shrink + nn(
                    vt_ref[here, at], expo.astype(BF16)
                )
            peak[h : h + 1] = new_peak

    block(i, True)

    @pl.loop(0, i - first_ref[i])
    def _(t):
        block(i - 1 - t, False)

    for h in range(heads):
        here = slice(h * HEAD_DIM, (h + 1) * HEAD_DIM)
        mixed[here] = mixed[here] / total[h : h + 1]
    o_ref[...] = mixed[...].T.astype(BF16)
    lse_ref[0] = peak[...] + jnp.log(total[...])


def attend(first, start, q, k, vt):
    length, cols = q.shape
    heads = cols // HEAD_DIM
    steps = length // TILE
    row = pl.BlockSpec((TILE, cols), lambda i, *_: (i, 0))
    return pl.pallas_call(
        functools.partial(attend_kernel, heads),
        out_shape=(
            jax.ShapeDtypeStruct((length, cols), BF16),
            jax.ShapeDtypeStruct((steps, heads, TILE), F32),
        ),
        grid_spec=pltpu.PrefetchScalarGridSpec(
            num_scalar_prefetch=1,
            grid=(steps,),
            in_specs=[
                pl.BlockSpec((1, TILE), lambda i, *_: (0, i)),
                row,
                pl.BlockSpec((length, cols), lambda i, *_: (0, 0)),
                pl.BlockSpec((cols, length), lambda i, *_: (0, 0)),
            ],
            out_specs=(
                row,
                pl.BlockSpec((1, heads, TILE), lambda i, *_: (i, 0, 0)),
            ),
            scratch_shapes=[
                pltpu.VMEM((heads, TILE), F32),
                pltpu.VMEM((heads, TILE), F32),
                pltpu.VMEM((cols, TILE), F32),
            ],
        ),
        compiler_params=pltpu.CompilerParams(vmem_limit_bytes=VMEM_LIMIT),
        cost_estimate=pl.CostEstimate(
            flops=4 * length * 1024 * cols,
            bytes_accessed=8 * length * cols,
            transcendentals=length * 1024 * heads,
        ),
        name="attend",
    )(first, start, q, k, vt)


def attend_back_kernel(
    heads, first_ref, start_ref, q_ref, k_ref, kt_ref, v_ref, o_ref, lse_ref, do_ref,
    cq_ref, sq_ref, ck_ref, sk_ref, grad_ref, dqt, dk_sum, dv_sum,
):
    i = pl.program_id(0)
    steps = pl.num_programs(0)
    width = q_ref.shape[1]
    queries = head_rows(q_ref[...], heads)
    grads = head_rows(do_ref[...], heads)
    start_row = start_ref[...]
    product = (do_ref[...].astype(F32) * o_ref[...].astype(F32)).T
    inner = [
        jnp.sum(product[h * HEAD_DIM : (h + 1) * HEAD_DIM], axis=0, keepdims=True)
        for h in range(heads)
    ]

    def block(j, first):
        at = pl.ds(pl.multiple_of(j * TILE, TILE), TILE)
        keys = k_ref[at, :]
        values = v_ref[at, :]
        mask = pair_mask(start_row, i, j)
        key_term = None
        value_term = None
        for h in range(heads):
            here = slice(h * HEAD_DIM, (h + 1) * HEAD_DIM)
            scores = nt(keys, queries[h])
            weights = jnp.where(mask, jnp.exp(scores - lse_ref[0, h : h + 1]), 0.0)
            grad_weights = nt(values, grads[h])
            grad_scores = (weights * (grad_weights - inner[h])).astype(BF16)
            term = nn(weights.astype(BF16), grads[h])
            value_term = term if value_term is None else value_term + term
            term = nn(grad_scores, queries[h])
            key_term = term if key_term is None else key_term + term
            term = nn(kt_ref[here, at], grad_scores)
            if first:
                dqt[here] = term
            else:
                dqt[here] = dqt[here] + term
        if first:
            dk_sum[at] = key_term
            dv_sum[at] = value_term
        else:
            dk_sum[at] = dk_sum[at] + key_term
            dv_sum[at] = dv_sum[at] + value_term

    block(i, True)

    @pl.loop(0, i - first_ref[i])
    def _(t):
        block(i - 1 - t, False)

    def unturn(grad, cosine, sine):
        grad = grad.astype(BF16).astype(F32)
        cosine = spread_lanes(cosine, width)
        sine = spread_lanes(sine, width)
        return (grad * cosine - swap_halves(grad) * sine).astype(BF16)

    rows = pl.ds(pl.multiple_of(i * TILE, TILE), TILE)
    grad_ref[rows, 0:width] = unturn(
        dqt[...].T * (HEAD_DIM**-0.5), cq_ref[rows, :], sq_ref[rows, :]
    )

    @pl.when(i == steps - 1)
    def _():
        @pl.loop(0, steps)
        def _(j):
            at = pl.ds(pl.multiple_of(j * TILE, TILE), TILE)
            grad_ref[at, width : 2 * width] = unturn(
                dk_sum[at], ck_ref[at, :], sk_ref[at, :]
            )
            grad_ref[at, 2 * width :] = dv_sum[at].astype(BF16)


def attend_back(first, start, q, k, kt, v, o, lse, do, tables):
    length, cols = q.shape
    heads = cols // HEAD_DIM
    steps = length // TILE
    row = pl.BlockSpec((TILE, cols), lambda i, *_: (i, 0))
    whole = pl.BlockSpec((length, cols), lambda i, *_: (0, 0))
    table = pl.BlockSpec((length, tables[0].shape[1]), lambda i, *_: (0, 0))
    return pl.pallas_call(
        functools.partial(attend_back_kernel, heads),
        out_shape=jax.ShapeDtypeStruct((length, 3 * cols), BF16),
        grid_spec=pltpu.PrefetchScalarGridSpec(
            num_scalar_prefetch=1,
            grid=(steps,),
            in_specs=[
                pl.BlockSpec((1, TILE), lambda i, *_: (0, i)),
                row,
                whole,
                pl.BlockSpec((cols, length), lambda i, *_: (0, 0)),
                whole,
                row,
                pl.BlockSpec((1, heads, TILE), lambda i, *_: (i, 0, 0)),
                row,
            ]
            + [table] * 4,
            out_specs=pl.BlockSpec((length, 3 * cols), lambda i, *_: (0, 0)),
            scratch_shapes=[
                pltpu.VMEM((cols, TILE), F32),
                pltpu.VMEM((length, cols), F32),
                pltpu.VMEM((length, cols), F32),
            ],
        ),
        compiler_params=pltpu.CompilerParams(vmem_limit_bytes=VMEM_LIMIT),
        name="attend_back",
    )(first, start, q, k, kt, v, o, lse, do, *tables)


def upper_kernel(
    x_ref, wu_ref, c_ref, wd_ref, gain_ref, act_ref, slope_ref, grad_ref, stat_ref
):
    upper = nt(x_ref[...], wu_ref[...])
    grad = nn(c_ref[...], wd_ref[...])
    below = 0.5 * (1.0 + lax.erf(upper * (0.5**0.5)))
    act = upper * below
    slope = below + upper * (jnp.exp(-0.5 * upper * upper) * ((2.0 * math.pi) ** -0.5))
    act_ref[...] = act
    slope_ref[...] = slope.astype(BF16)
    grad_ref[...] = grad
    part = grad * gain_ref[...]
    average = jnp.mean(act, axis=-1, keepdims=True)
    centered = act - average
    spread = jnp.sum(centered * centered, axis=-1, keepdims=True)
    part_sum = jnp.sum(part, axis=-1, keepdims=True)
    cross = jnp.sum(part * centered, axis=-1, keepdims=True)
    lane = lax.broadcasted_iota(jnp.int32, (x_ref.shape[0], 128), 1)
    columns = jnp.where(
        lane == 0,
        average,
        jnp.where(lane == 1, spread, jnp.where(lane == 2, part_sum, cross)),
    )
    stat_ref[...] = columns.T[:8]


def upper_pass(x, w_up, cot, w_down, gain):
    length, width = x.shape
    feats = w_up.shape[0]
    rows = TILE
    row = pl.BlockSpec((rows, width), lambda i: (i, 0))
    out = pl.BlockSpec((rows, feats), lambda i: (i, 0))
    return pl.pallas_call(
        upper_kernel,
        grid=(length // rows,),
        out_shape=(
            jax.ShapeDtypeStruct((length, feats), F32),
            jax.ShapeDtypeStruct((length, feats), BF16),
            jax.ShapeDtypeStruct((length, feats), F32),
            jax.ShapeDtypeStruct((8, length), F32),
        ),
        in_specs=[
            row,
            pl.BlockSpec((feats, width), lambda i: (0, 0)),
            row,
            pl.BlockSpec((width, feats), lambda i: (0, 0)),
            pl.BlockSpec((1, feats), lambda i: (0, 0)),
        ],
        out_specs=(out, out, out, pl.BlockSpec((8, rows), lambda i: (0, i))),
        compiler_params=pltpu.CompilerParams(vmem_limit_bytes=VMEM_LIMIT),
        cost_estimate=pl.CostEstimate(
            flops=4 * length * width * feats,
            bytes_accessed=8 * length * width + 8 * length * feats,
            transcendentals=2 * length * feats,
        ),
        name="upper_pass",
    )(x, w_up, cot, w_down, gain)


def hidden_kernel(act_ref, slope_ref, grad_ref, stat_ref, gain_ref, hid_ref, gu_ref, gg_ref):
    i = pl.program_id(0)
    stats = stat_ref[...].T
    average = stats[:, 0:1]
    scale = stats[:, 1:2]
    part_mean = stats[:, 2:3]
    cross_mean = stats[:, 3:4]
    gain = gain_ref[...]
    normal = (act_ref[...] - average) * scale
    grad = grad_ref[...]
    hid_ref[...] = (normal * gain).astype(BF16)
    back = scale * (grad * gain - part_mean - normal * cross_mean)
    gu_ref[...] = (slope_ref[...].astype(F32) * back).astype(BF16)
    term = jnp.sum(grad * normal, axis=0, keepdims=True)

    @pl.when(i == 0)
    def _():
        gg_ref[...] = term

    @pl.when(i > 0)
    def _():
        gg_ref[...] = gg_ref[...] + term


def hidden_pass(act, slope, grad, stats, gain):
    length, feats = act.shape
    out = pl.BlockSpec((TILE, feats), lambda i: (i, 0))
    one = pl.BlockSpec((1, feats), lambda i: (0, 0))
    return pl.pallas_call(
        hidden_kernel,
        grid=(length // TILE,),
        out_shape=(
            jax.ShapeDtypeStruct((length, feats), BF16),
            jax.ShapeDtypeStruct((length, feats), BF16),
            jax.ShapeDtypeStruct((1, feats), F32),
        ),
        in_specs=[out, out, out, pl.BlockSpec((8, TILE), lambda i: (0, i)), one],
        out_specs=(out, out, one),
        compiler_params=pltpu.CompilerParams(vmem_limit_bytes=VMEM_LIMIT),
        cost_estimate=pl.CostEstimate(
            flops=12 * length * feats,
            bytes_accessed=14 * length * feats,
            transcendentals=0,
        ),
        name="hidden_pass",
    )(act, slope, grad, stats, gain)


def ffn_kernel(
    n, x_ref, wu_ref, cot_ref, wd_ref, gain_ref,
    full_ref, hid_ref, gu_ref, gg_ref,
    rows_in, wd, cot_in, act, slope, grad, stat, held, results,
    local_sem, cot_sem, out_sem, full_sem, send_sem, recv_sem, stat_send, stat_recv,
):
    me, twin, near_x, near_y, across = places()
    rows = x_ref.shape[0]
    feats = wu_ref.shape[0]

    def cut(i, size=rows):
        return pl.ds(pl.multiple_of(i * size, size), size)

    own = pltpu.make_async_copy(x_ref, rows_in.at[me], local_sem.at[0])
    own.start()
    load_wd = pltpu.make_async_copy(wd_ref, wd, local_sem.at[1])
    load_wd.start()

    def load_cot(i, slot):
        return pltpu.make_async_copy(
            cot_ref.at[cut(i)], cot_in.at[slot], cot_sem.at[slot]
        )

    load_cot(0, 0).start()
    meet([lax.rem(me + k, n) for k in range(1, n)])
    sends = gather_copies(x_ref, rows_in, send_sem, recv_sem)
    for k in range(5):
        sends[k].start()

    load_wd.wait()
    def incoming(first, last):
        @pl.loop(first, last)
        def _(i):
            slot = lax.rem(i, 2)

            @pl.when(i + 1 < n)
            def _():
                load_cot(i + 1, 1 - slot).start()

            load_cot(i, slot).wait()
            grad[cut(i)] = nn(cot_in[slot], wd[...])

    incoming(0, n - 2)
    sends[0].wait_recv()
    sends[5].start()
    sends[7].start()
    sends[1].wait_recv()
    sends[6].start()
    sends[8].start()
    incoming(n - 2, n)
    own.wait()

    def keep(b):
        return pltpu.make_async_copy(rows_in.at[b], full_ref.at[b], full_sem.at[b])

    @pl.loop(0, n)
    def _(i):
        @pl.when(i == 1)
        def _():
            sends[4].wait_recv()

        @pl.when(i == 2)
        def _():
            sends[2].wait_recv()
            sends[9].start()
            sends[3].wait_recv()
            sends[10].start()

        @pl.when(i == 4)
        def _():
            sends[7].wait_recv()
            sends[9].wait_recv()

        @pl.when(i == 5)
        def _():
            sends[8].wait_recv()
            sends[10].wait_recv()
            sends[5].wait_recv()
            sends[11].start()
            sends[6].wait_recv()
            sends[12].start()

        @pl.when(i == 7)
        def _():
            sends[11].wait_recv()
            sends[12].wait_recv()

        other = jnp.where((i == 1) | (i == 4) | (i == 5) | (i == 7), twin, 0)
        place = jnp.where(i < 2, me, jnp.where(i >= 6, across, jnp.where(lax.rem(i, 2) == 0, near_x, near_y)))
        b = place + other
        keep(b).start()
        at = cut(b)
        upper = nt(rows_in[b], wu_ref[...])
        below = 0.5 * (1.0 + lax.erf(upper * (0.5**0.5)))
        value = upper * below
        act[at] = value
        slope[at] = (
            below + upper * (jnp.exp(-0.5 * upper * upper) * ((2.0 * math.pi) ** -0.5))
        ).astype(BF16)
        part = grad[at] * gain_ref[...]
        average = jnp.mean(value, axis=-1, keepdims=True)
        centered = value - average
        spread = jnp.sum(centered * centered, axis=-1, keepdims=True)
        part_sum = jnp.sum(part, axis=-1, keepdims=True)
        cross = jnp.sum(part * centered, axis=-1, keepdims=True)
        lane = lax.broadcasted_iota(jnp.int32, (rows, 128), 1)
        columns = jnp.where(
            lane == 0,
            average,
            jnp.where(lane == 1, spread, jnp.where(lane == 2, part_sum, cross)),
        )
        stat[:, at] = columns.T[:8]

    held[me] = stat[...]
    rounds = [
        remote(
            stat, held.at[me], stat_send.at[k], stat_recv.at[k], lax.rem(me + k, n)
        )
        for k in range(1, n)
    ]
    for send in rounds:
        send.start()
    for send in rounds:
        send.wait()
    join_rows(n, feats, held, stat)

    def store(i, slot):
        return [
            pltpu.make_async_copy(
                results.at[slot, j], ref.at[cut(i)], out_sem.at[slot, j]
            )
            for j, ref in enumerate((hid_ref, gu_ref))
        ]

    gg_ref[...] = jnp.zeros_like(gg_ref)

    @pl.loop(0, n)
    def _(i):
        slot = lax.rem(i, 2)

        @pl.when(i >= 2)
        def _():
            for copy in store(i - 2, slot):
                copy.wait()

        at = cut(i)
        stats = stat[:, at].T
        gain = gain_ref[...]
        scale = stats[:, 1:2]
        normal = (act[at] - stats[:, 0:1]) * scale
        coming = grad[at]
        results[slot, 0] = (normal * gain).astype(BF16)
        back = scale * (coming * gain - stats[:, 2:3] - normal * stats[:, 3:4])
        results[slot, 1] = (slope[at].astype(F32) * back).astype(BF16)
        gg_ref[...] = gg_ref[...] + jnp.sum(coming * normal, axis=0, keepdims=True)
        for copy in store(i, slot):
            copy.start()

    for i in (n - 2, n - 1):
        for copy in store(i, i % 2):
            copy.wait()
    for b in range(n):
        keep(b).wait()
    for send in sends:
        send.wait_send()


def ffn_pass(ffn_in, w_up, cot, w_down, gain, collective_id):
    n = lax.axis_size("seq")
    rows, width = ffn_in.shape
    feats = w_up.shape[0]
    if n != 8:
        full = lax.all_gather(ffn_in, "seq", axis=0, tiled=True)
        act, slope, grad, stat = upper_pass(full, w_up, cot, w_down, gain)
        stats = join_stats(stat, feats, collective_id)
        return (full, *hidden_pass(act, slope, grad, stats, gain))
    length = n * rows
    dma = pltpu.SemaphoreType.DMA
    low = jax.ShapeDtypeStruct((length, feats), BF16)
    full, hidden, grad_upper, gain_grad = pl.pallas_call(
        functools.partial(ffn_kernel, n),
        out_shape=(
            jax.ShapeDtypeStruct((n, rows, width), BF16),
            low,
            low,
            jax.ShapeDtypeStruct((1, feats), F32),
        ),
        in_specs=[INSIDE, INSIDE, ANY, ANY, INSIDE],
        out_specs=(ANY, ANY, ANY, INSIDE),
        scratch_shapes=[
            pltpu.VMEM((n, rows, width), BF16),
            pltpu.VMEM((width, feats), BF16),
            pltpu.VMEM((2, rows, width), BF16),
            pltpu.VMEM((length, feats), F32),
            pltpu.VMEM((length, feats), BF16),
            pltpu.VMEM((length, feats), F32),
            pltpu.VMEM((8, length), F32),
            pltpu.VMEM((n, 8, length), F32),
            pltpu.VMEM((2, 2, rows, feats), BF16),
            dma((2,)),
            dma((2,)),
            dma((2, 2)),
            dma((n,)),
            dma((13,)),
            dma((13,)),
            dma((n,)),
            dma((n,)),
        ],
        compiler_params=pltpu.CompilerParams(
            collective_id=collective_id, has_side_effects=True, vmem_limit_bytes=VMEM_LIMIT
        ),
        name="ffn_pass",
    )(ffn_in, w_up, cot, w_down, gain)
    return full.reshape(length, width), hidden, grad_upper, gain_grad


def join_rows(n, feats, held, o_ref):
    average = held[0, 0:1]
    for d in range(1, n):
        average = average + held[d, 0:1]
    average = average * (1.0 / n)
    spread = jnp.zeros_like(average)
    part = jnp.zeros_like(average)
    cross = jnp.zeros_like(average)
    for d in range(n):
        shift = held[d, 0:1] - average
        spread = spread + held[d, 1:2] + feats * (shift * shift)
        part = part + held[d, 2:3]
        cross = cross + held[d, 3:4] + shift * held[d, 2:3]
    whole = 1.0 / (n * feats)
    scale = lax.rsqrt(spread * whole + EPSILON)
    o_ref[0:1] = average
    o_ref[1:2] = scale
    o_ref[2:3] = part * whole
    o_ref[3:4] = cross * scale * whole
    o_ref[4:8] = jnp.zeros((4, average.shape[1]), F32)


def stat_kernel(n, feats, x_ref, o_ref, held, send_sem, recv_sem):
    me = lax.axis_index("seq")
    held[me] = x_ref[...]
    meet([lax.rem(me + k, n) for k in range(1, n)])
    copies = [
        remote(x_ref, held.at[me], send_sem.at[k], recv_sem.at[k], lax.rem(me + k, n))
        for k in range(1, n)
    ]
    for copy in copies:
        copy.start()
    for copy in copies:
        copy.wait()
    join_rows(n, feats, held, o_ref)


def join_stats(stat, feats, collective_id):
    n = lax.axis_size("seq")
    inside = pl.BlockSpec(memory_space=pltpu.VMEM)
    return pl.pallas_call(
        functools.partial(stat_kernel, n, feats),
        out_shape=jax.ShapeDtypeStruct(stat.shape, F32),
        in_specs=[inside],
        out_specs=inside,
        scratch_shapes=[
            pltpu.VMEM((n, *stat.shape), F32),
            pltpu.SemaphoreType.DMA((n,)),
            pltpu.SemaphoreType.DMA((n,)),
        ],
        compiler_params=pltpu.CompilerParams(
            collective_id=collective_id, has_side_effects=True, vmem_limit_bytes=VMEM_LIMIT
        ),
        name="join_stats",
    )(stat)


def mix_kernel(att_ref, x_ref, w_ref, gm_ref, gf_ref, mix_ref, mid_ref, ffn_ref):
    j = pl.program_id(0)
    rows = att_ref.shape[0]
    cols = w_ref.shape[0]

    @pl.when(j == 0)
    def _():
        @pl.loop(0, rows // STEP)
        def _(r):
            at = pl.ds(pl.multiple_of(r * STEP, STEP), STEP)
            normal, _ = norm_parts(att_ref[at].astype(F32))
            mix_ref[at] = (normal * gm_ref[...]).astype(BF16)

    here = pl.ds(pl.multiple_of(j * cols, cols), cols)
    mid_ref[:, here] = x_ref[:, here].astype(F32) + nt(mix_ref[...], w_ref[...])

    @pl.when(j == pl.num_programs(0) - 1)
    def _():
        @pl.loop(0, rows // STEP)
        def _(r):
            at = pl.ds(pl.multiple_of(r * STEP, STEP), STEP)
            normal, _ = norm_parts(mid_ref[at])
            ffn_ref[at] = (normal * gf_ref[...]).astype(BF16)


def mix_pass(attended, x, w_out, gain_mix, gain_ffn):
    rows, width = x.shape
    cols = TILE
    n = width // cols
    whole = pl.BlockSpec((rows, width), lambda j: (0, 0))
    gain = pl.BlockSpec((1, width), lambda j: (0, 0))
    low = jax.ShapeDtypeStruct((rows, width), BF16)
    return pl.pallas_call(
        mix_kernel,
        grid=(n,),
        out_shape=(low, jax.ShapeDtypeStruct((rows, width), F32), low),
        in_specs=[
            whole,
            whole,
            pl.BlockSpec((cols, width), lambda j: (j, 0)),
            gain,
            gain,
        ],
        out_specs=(whole, whole, whole),
        compiler_params=pltpu.CompilerParams(vmem_limit_bytes=VMEM_LIMIT),
        cost_estimate=pl.CostEstimate(
            flops=2 * rows * width * width,
            bytes_accessed=2 * width * width + 12 * rows * width,
            transcendentals=0,
        ),
        name="mix_pass",
    )(attended, x, w_out, gain_mix[None], gain_ffn[None])


def branch_kernel(gbr_ref, att_ref, w_ref, gm_ref, gatt_ref, ggm_ref, total):
    j = pl.program_id(0)
    rows = att_ref.shape[0]
    cols = w_ref.shape[0]
    here = pl.ds(pl.multiple_of(j * cols, cols), cols)
    term = nn(gbr_ref[:, here], w_ref[...])

    @pl.when(j == 0)
    def _():
        total[...] = term

    @pl.when(j > 0)
    def _():
        total[...] = total[...] + term

    @pl.when(j == pl.num_programs(0) - 1)
    def _():
        ggm_ref[...] = jnp.zeros_like(ggm_ref)

        @pl.loop(0, rows // STEP)
        def _(r):
            at = pl.ds(pl.multiple_of(r * STEP, STEP), STEP)
            normal, scale = norm_parts(att_ref[at].astype(F32))
            part, gain_part = norm_back(total[at], normal, scale, gm_ref[...])
            ggm_ref[...] += gain_part[None]
            gatt_ref[at] = part.astype(BF16)


def branch_pass(grad_branch, attended, w_out, gain_mix):
    rows, width = grad_branch.shape
    cols = TILE
    n = width // cols
    whole = pl.BlockSpec((rows, width), lambda j: (0, 0))
    gain = pl.BlockSpec((1, width), lambda j: (0, 0))
    return pl.pallas_call(
        branch_kernel,
        grid=(n,),
        out_shape=(
            jax.ShapeDtypeStruct((rows, width), BF16),
            jax.ShapeDtypeStruct((1, width), F32),
        ),
        in_specs=[whole, whole, pl.BlockSpec((cols, width), lambda j: (j, 0)), gain],
        out_specs=(whole, gain),
        scratch_shapes=[pltpu.VMEM((rows, width), F32)],
        compiler_params=pltpu.CompilerParams(vmem_limit_bytes=VMEM_LIMIT),
        name="branch_pass",
    )(grad_branch, attended, w_out, gain_mix[None])


def ffn_back_kernel(
    n, gu_ref, wu_ref, hid_ref, wd_ref, all_ref, mid_ref, cot_ref, gf_ref,
    po_ref, gd_ref, gmid_ref, gbr_ref, ggf_ref,
    gu, hid, every, own, far, twin_in, held, made, made_grad,
    local_sem, made_sem, grad_sem, send_sem, recv_sem,
):
    me, twin, near_x, near_y, across = places()
    rows, width = mid_ref.shape
    half = rows // 2
    low, high = pl.ds(0, half), pl.ds(half, half)
    mine = (across, near_x, near_y, me)

    def cut(i, size=rows):
        return pl.ds(pl.multiple_of(i * size, size), size)

    load_gu = pltpu.make_async_copy(gu_ref, gu, local_sem.at[0])
    load_hid = pltpu.make_async_copy(hid_ref, hid, local_sem.at[1])
    load_all = pltpu.make_async_copy(all_ref, every, local_sem.at[2])
    for load in (load_gu, load_hid, load_all):
        load.start()
    meet((me + twin, near_x, near_y))
    load_gu.wait()

    def copy(k, src, dst, partner):
        return remote(src, dst, send_sem.at[k], recv_sem.at[k], partner)

    twins = [copy(i, far.at[i], twin_in.at[i], me + twin) for i in range(4)]
    sends = [
        copy(4, own.at[0, low], held.at[0], near_x),
        copy(5, own.at[0, high], held.at[1], near_y),
        copy(6, own.at[1, low], held.at[2], near_x),
        copy(7, own.at[2, high], held.at[3], near_y),
        copy(8, own.at[1, high], held.at[4], near_x),
        copy(9, own.at[2, low], held.at[5], near_y),
    ]

    def add(i, base, count, source):
        @pl.loop(0, count // STEP)
        def _(r):
            at = cut(r, STEP)
            to = pl.ds(pl.multiple_of(base + r * STEP, STEP), STEP)
            own[i, to] = (own[i, to].astype(F32) + source[at].astype(F32)).astype(BF16)

    for i, block in enumerate(mine):
        far[i] = nn(gu[cut(block + twin)], wu_ref[...]).astype(BF16)
        twins[i].start()
        own[i] = nn(gu[cut(block)], wu_ref[...]).astype(BF16)
        if i < 3:
            twins[i].wait_recv()
            add(i, 0, rows, twin_in.at[i])
        if i == 0:
            sends[0].start()
            sends[1].start()
        elif i < 3:
            sends[i + 1].start()

    def store(i, slot):
        return pltpu.make_async_copy(made.at[slot], po_ref.at[cut(i)], made_sem.at[slot])

    def outputs(first, last):
        @pl.loop(first, last)
        def _(i):
            slot = lax.rem(i, 2)

            @pl.when(i >= 2)
            def _():
                store(i - 2, slot).wait()

            made[slot] = nt(hid[cut(i)], wd_ref[...]).astype(BF16)
            store(i, slot).start()

    def store_grad(i, slot):
        return pltpu.make_async_copy(
            made_grad.at[slot], gd_ref.at[i], grad_sem.at[slot]
        )

    def weight_grads(first, last):
        for i in range(first, last):
            slot = i % 2
            if i >= 2:
                store_grad(i - 2, slot).wait()
            made_grad[slot] = tn(
                every[:, i * rows : (i + 1) * rows], hid[...]
            ).astype(BF16)
            store_grad(i, slot).start()

    load_hid.wait()
    load_all.wait()
    weight_grads(0, n // 2)
    sends[1].wait_recv()
    add(1, half, half, held.at[1])
    sends[4].start()
    sends[0].wait_recv()
    add(2, 0, half, held.at[0])
    sends[5].start()
    weight_grads(n // 2, n)
    outputs(0, n)
    twins[3].wait_recv()
    for k in (2, 3, 4, 5):
        sends[k].wait_recv()
    ggf_ref[...] = jnp.zeros_like(ggf_ref)
    for base, one, two in ((0, 2, 5), (half, 3, 4)):

        @pl.loop(0, half // STEP)
        def _(r):
            at = cut(r, STEP)
            to = pl.ds(pl.multiple_of(base + r * STEP, STEP), STEP)
            value = (
                own[3, to].astype(F32)
                + twin_in[3, to].astype(F32)
                + held[one, at].astype(F32)
                + held[two, at].astype(F32)
            )
            normal, scale = norm_parts(mid_ref[to])
            part, gain_part = norm_back(value, normal, scale, gf_ref[...])
            ggf_ref[...] = ggf_ref[...] + gain_part[None]
            grad = cot_ref[to].astype(F32) + part
            gmid_ref[to] = grad
            gbr_ref[to] = grad.astype(BF16)

    for i in (n - 2, n - 1):
        store(i, i % 2).wait()
        store_grad(i, i % 2).wait()
    for send in twins + sends:
        send.wait_send()


def ffn_back(grad_upper, w_up, hidden, w_down, cot_full, middle, cot, gain, collective_id):
    n = lax.axis_size("seq")
    rows, width = middle.shape
    feats = w_up.shape[0]
    if n != 8:
        normal, scale = norm_parts(middle)
        value = scatter_seq(nn(grad_upper, w_up).astype(BF16))
        part, gain_part = norm_back(value, normal, scale, gain)
        grad = cot.astype(F32) + part
        down = tn(cot_full, hidden).astype(BF16).reshape(n, rows, feats)
        outputs = nt(hidden, w_down).astype(BF16)
        return outputs, down, grad, grad.astype(BF16), gain_part[None]
    dma = pltpu.SemaphoreType.DMA
    block = pltpu.VMEM((4, rows, width), BF16)
    return pl.pallas_call(
        functools.partial(ffn_back_kernel, n),
        out_shape=(
            jax.ShapeDtypeStruct((n * rows, width), BF16),
            jax.ShapeDtypeStruct((n, rows, feats), BF16),
            jax.ShapeDtypeStruct((rows, width), F32),
            jax.ShapeDtypeStruct((rows, width), BF16),
            jax.ShapeDtypeStruct((1, width), F32),
        ),
        in_specs=[ANY, INSIDE, ANY, INSIDE, ANY, INSIDE, INSIDE, INSIDE],
        out_specs=(ANY, ANY, INSIDE, INSIDE, INSIDE),
        scratch_shapes=[
            pltpu.VMEM((n * rows, feats), BF16),
            pltpu.VMEM((n * rows, feats), BF16),
            pltpu.VMEM((n * rows, width), BF16),
            block,
            block,
            block,
            pltpu.VMEM((6, rows // 2, width), BF16),
            pltpu.VMEM((2, rows, width), BF16),
            pltpu.VMEM((2, rows, feats), BF16),
            dma((3,)),
            dma((2,)),
            dma((2,)),
            dma((10,)),
            dma((10,)),
        ],
        compiler_params=pltpu.CompilerParams(
            collective_id=collective_id, has_side_effects=True, vmem_limit_bytes=VMEM_LIMIT
        ),
        name="ffn_back",
    )(grad_upper, w_up, hidden, w_down, cot_full, middle, cot, gain[None])


CHUNK = 64


def finish_kernel(
    n, depth, gq_ref, gd_ref, pw_ref, pn_ref, po_ref, x_ref, grad_ref, mid_ref, ga_ref, gm_ref, gf_ref, gh_ref,
    oq_ref, od_ref, ow_ref, gi_ref, out_ref, sums_ref,
    own, twin_in, held, zown, zin, stage, gain_here, gain_row, gain_pack, gain_line,
    local_sem, load_sem, stage_sem, send_sem, recv_sem, keep_sem,
    up_send, up_recv, down_send, down_recv, home_send, home_recv, gain_send, gain_recv,
):
    me, twin, near_x, near_y, across = places()
    z = lax.axis_index("batch")
    rows, width = pn_ref.shape[1:]
    half = rows // 2
    low, high = pl.ds(0, half), pl.ds(half, half)
    mine = (across, near_x, near_y, me)
    _, chunk, cols = zown.shape
    across_width = width // cols
    per_part = (gq_ref.shape[1] // chunk) * across_width
    turned = gq_ref.shape[0] * per_part
    per_source = gd_ref.shape[1] // chunk
    outer = turned + gd_ref.shape[0] * per_source
    chunks = zown.shape[0]
    per_side = chunks // 2

    def cut(i, size):
        return pl.ds(pl.multiple_of(i * size, size), size)

    def wide(i):
        return cut(i // across_width, chunk), cut(lax.rem(i, across_width), cols)

    line_loads = []
    for g in range(turned):
        source = gq_ref.at[(g // per_part, *wide(g % per_part))]
        line_loads.append(pltpu.make_async_copy(source, zown.at[g], load_sem.at[g]))
    for g in range(turned, outer):
        source = gd_ref.at[
            (g - turned) // per_source, cut((g - turned) % per_source, chunk)
        ]
        line_loads.append(pltpu.make_async_copy(source, zown.at[g], load_sem.at[g]))
    for load in line_loads:
        load.start()
    partials = (pw_ref, pn_ref, po_ref)
    loads = [
        [
            pltpu.make_async_copy(p.at[block], own.at[m, i], local_sem.at[4 * m + i])
            for i, block in enumerate(mine)
        ]
        for m, p in enumerate(partials)
    ]
    for part in loads:
        for load in part:
            load.start()
    meet_all(n, depth)

    def copy(m, k, src, dst, partner):
        return remote(src, dst, send_sem.at[m, k], recv_sem.at[m, k], partner)

    twins = [
        [
            copy(m, i, p.at[block + twin], twin_in.at[m, i], me + twin)
            for i, block in enumerate(mine)
        ]
        for m, p in enumerate(partials)
    ]
    sends = [
        [
            copy(m, 4, own.at[m, 0, low], held.at[m, 0], near_x),
            copy(m, 5, own.at[m, 0, high], held.at[m, 1], near_y),
            copy(m, 6, own.at[m, 1, low], held.at[m, 2], near_x),
            copy(m, 7, own.at[m, 2, high], held.at[m, 3], near_y),
            copy(m, 8, own.at[m, 1, high], held.at[m, 4], near_x),
            copy(m, 9, own.at[m, 2, low], held.at[m, 5], near_y),
        ]
        for m in range(3)
    ]
    for part in twins:
        for send in part:
            send.start()

    def add_twin(m, i):
        loads[m][i].wait()
        twins[m][i].wait_recv()

        @pl.loop(0, rows // STEP)
        def _(r):
            at = cut(r, STEP)
            own[m, i, at] = (
                own[m, i, at].astype(F32) + twin_in[m, i, at].astype(F32)
            ).astype(BF16)

    def add_held(m, i, base, slot):
        @pl.loop(0, half // STEP)
        def _(r):
            at = cut(r, STEP)
            to = pl.ds(pl.multiple_of(base + r * STEP, STEP), STEP)
            own[m, i, to] = (
                own[m, i, to].astype(F32) + held[m, slot, at].astype(F32)
            ).astype(BF16)

    def first(m):
        add_twin(m, 0)
        sends[m][0].start()
        sends[m][1].start()
        add_twin(m, 1)
        sends[m][2].start()
        add_twin(m, 2)
        sends[m][3].start()

    def second(m):
        sends[m][1].wait_recv()
        add_held(m, 1, half, 1)
        sends[m][4].start()
        sends[m][0].wait_recv()
        add_held(m, 2, 0, 0)
        sends[m][5].start()

    def last(m, store):
        loads[m][3].wait()
        twins[m][3].wait_recv()
        for k in (2, 3, 4, 5):
            sends[m][k].wait_recv()
        for base, one, two in ((0, 2, 5), (half, 3, 4)):

            @pl.loop(0, half // STEP)
            def _(r):
                at = cut(r, STEP)
                place = base + r * STEP
                to = pl.ds(pl.multiple_of(place, STEP), STEP)
                store(
                    place,
                    to,
                    own[m, 3, to].astype(F32)
                    + twin_in[m, 3, to].astype(F32)
                    + held[m, one, at].astype(F32)
                    + held[m, two, at].astype(F32),
                )

    def store_line(place, to, value):
        value = value.astype(BF16)
        for side in range(across_width):
            zown[
                outer + (place // chunk) * across_width + side,
                pl.ds(pl.multiple_of(lax.rem(place, chunk), STEP), STEP),
            ] = value[:, side * cols : (side + 1) * cols]

    def store_inputs(place, to, value):
        normal, scale = norm_parts(x_ref[to].astype(F32))
        part, gain_part = norm_back(value, normal, scale, ga_ref[...])
        gi_ref[to] = grad_ref[to] + part
        gain_here[0:1] = gain_here[0:1] + gain_part[None]

    def store_outputs(place, to, value):
        out_ref[to] = (mid_ref[to] + value).astype(BF16)

    def home(part):
        block = part * n + me
        return block // 3, lax.rem(block, 3)

    def deliver_far(g):
        target, slot = home(g // per_part)
        piece = lax.rem(g, per_part)
        return remote(
            zin.at[g],
            oq_ref.at[(slot, *wide(piece))],
            home_send.at[g],
            home_recv.at[slot, piece],
            target,
        )

    def deliver_near(g):
        _, slot = home(g // per_part)
        return pltpu.make_async_copy(
            zin.at[g], oq_ref.at[(slot, *wide(lax.rem(g, per_part)))], keep_sem.at[g]
        )

    def widen(g):
        @pl.loop(0, chunk // STEP)
        def _(r):
            at = cut(r, STEP)
            stage[at] = zin[g, at].astype(F32)

    def deliver(g):
        target, _ = home(g // per_part)

        @pl.when((g < turned) & (target != me))
        def _():
            deliver_far(g).start()

        @pl.when((g < turned) & (target == me))
        def _():
            deliver_near(g).start()

        @pl.when((g >= turned) & (g < outer))
        def _():
            widen(g)
            at = g - turned
            place = cut(lax.rem(at, per_source), chunk), cut(at // per_source, cols)
            store = pltpu.make_async_copy(stage, od_ref.at[place], stage_sem)
            store.start()
            store.wait()

        @pl.when(g >= outer)
        def _():
            widen(g)
            store = pltpu.make_async_copy(
                stage, ow_ref.at[wide(g - outer)], stage_sem
            )
            store.start()
            store.wait()

    def delivered(g):
        target, _ = home(g // per_part)

        @pl.when(target != me)
        def _():
            deliver_far(g).wait_send()

        @pl.when(target == me)
        def _():
            deliver_near(g).wait()

    def go_up(g, ahead):
        return line_remote(zown.at[g], zin.at[g], up_send.at[g], up_recv.at[g], ahead)

    def go_down(g, behind):
        return line_remote(
            zin.at[g], zin.at[g], down_send.at[g], down_recv.at[g], behind
        )

    def ranks(side):
        if side == 0:
            return z, z + 1, z - 1
        return depth - 1 - z, z - 1, z + 1

    def add_line(g, target):
        @pl.loop(0, chunk // STEP)
        def _(r):
            at = cut(r, STEP)
            target[g, at] = (zown[g, at].astype(F32) + zin[g, at].astype(F32)).astype(
                BF16
            )

    lead = 2
    far = 2 * (depth - 1)
    steps = per_side + 2 * far

    def line_enter(c):
        for side in (0, 1):
            rank, ahead, _ = ranks(side)

            @pl.when(rank == 0)
            def _():
                go_up(2 * c + side, ahead).start()

    def line_step(t):
        @pl.when(t + lead < per_side)
        def _():
            line_enter(t + lead)

        back = []
        for side in (0, 1):
            rank, ahead, behind = ranks(side)
            c_back = t - 2 * far + 2 * rank
            g_back = 2 * c_back + side
            there = (c_back >= 0) & (c_back < per_side) & (rank < depth - 1)
            back.append((there, g_back))

            @pl.when(there)
            def _():
                go_down(g_back, ahead).wait_recv()

            @pl.when(there & (rank > 0))
            def _():
                go_down(g_back, behind).start()

        for side in (0, 1):
            rank, ahead, behind = ranks(side)
            c = t - 2 * rank
            g = 2 * c + side
            there = (c >= 0) & (c < per_side)

            @pl.when(there & (rank > 0) & (rank < depth - 1))
            def _():
                go_up(g, behind).wait_recv()
                add_line(g, zown)
                go_up(g, ahead).start()

            @pl.when(there & (rank == depth - 1))
            def _():
                go_up(g, behind).wait_recv()
                add_line(g, zin)
                go_down(g, behind).start()
                deliver(g)

        for there, g_back in back:

            @pl.when(there)
            def _():
                deliver(g_back)

    def line_steps(first_step, last_step):
        @pl.loop(first_step, last_step)
        def _(t):
            line_step(t)

    gain_here[...] = jnp.zeros_like(gain_here)
    for load in line_loads:
        load.wait()
    for c in range(lead):
        line_enter(c)
    first(0)
    line_steps(0, 8)
    second(0)
    line_steps(8, 9)
    first(1)
    line_steps(9, 18)
    last(0, store_line)
    line_steps(18, 20)
    second(1)
    line_steps(20, 21)
    first(2)
    line_steps(21, 28)
    last(1, store_inputs)

    gain_here[1:2] = gm_ref[...]
    gain_here[2:3] = gf_ref[...]
    gain_here[3:4, 0 : gh_ref.shape[1]] = gh_ref[...]
    gain_row[me] = gain_here[...]
    rounds = [
        remote(
            gain_here,
            gain_row.at[me],
            gain_send.at[0, k],
            gain_recv.at[0, k],
            lax.rem(me + k, n),
        )
        for k in range(1, n)
    ]
    for send in rounds:
        send.start()
    line_steps(28, 32)
    second(2)
    line_steps(32, 40)
    last(2, store_outputs)
    line_steps(40, 42)
    for send in rounds:
        send.wait()
    total = gain_row[0]
    for d in range(1, n):
        total = total + gain_row[d]
    gain_pack[0:8] = total
    for d in range(n):
        gain_pack[8 + d : 9 + d] = gain_row[d, 3:4]
    gain_line[z] = gain_pack[...]
    rounds = [
        line_remote(
            gain_pack,
            gain_line.at[z],
            gain_send.at[1, k],
            gain_recv.at[1, k],
            lax.rem(z + k, depth),
        )
        for k in range(1, depth)
    ]
    for send in rounds:
        send.start()
    line_steps(42, steps)
    for send in rounds:
        send.wait()
    total = gain_line[0]
    for d in range(1, depth):
        total = total + gain_line[d]
    sums_ref[...] = total

    for m in range(3):
        for send in twins[m] + sends[m]:
            send.wait_send()
    for g in range(chunks):
        rank, ahead, behind = ranks(g % 2)

        @pl.when(rank < depth - 1)
        def _():
            go_up(g, ahead).wait_send()

        @pl.when(rank > 0)
        def _():
            go_down(g, behind).wait_send()

    for g in range(turned):
        delivered(g)
    for slot in range(3):
        block = 3 * me + slot
        source = lax.rem(block, n)

        @pl.when(source != me)
        def _():
            for piece in range(per_part):
                remote(
                    zin.at[0],
                    oq_ref.at[(slot, *wide(piece))],
                    home_send.at[0],
                    home_recv.at[slot, piece],
                    source,
                ).wait_recv()


def finish(
    grad_qkv, grad_down, part_out, part_normed, part_outputs, x, grad_middle, middle, gain, gains, collective_id
):
    n, depth = lax.axis_size("seq"), lax.axis_size("batch")
    rows, width = part_out.shape[0] // n, part_out.shape[1]
    cols = grad_qkv.shape[1]
    sources, _, feats = grad_down.shape
    if n != 8 or depth != 4:
        me = lax.axis_index("seq")
        blocks = lax.psum(grad_qkv, "batch")
        back = [
            lax.ppermute(
                give_part(blocks, me, n, j),
                "seq",
                [((3 * d + j) % n, d) for d in range(n)],
            )
            for j in range(3)
        ]
        w_out = lax.psum(scatter_seq(part_out).astype(BF16), "batch")
        normal, scale = norm_parts(x.astype(F32))
        part, gain_part = norm_back(scatter_seq(part_normed), normal, scale, gain)
        shared = [lax.psum(g, ("batch", "seq")) for g in (gain_part, gains[0][0], gains[1][0])]
        hidden = lax.all_gather(lax.psum(gains[2][0], "batch"), "seq", axis=0, tiled=True)
        down = lax.psum(grad_down, "batch")
        return (
            jnp.concatenate(back, axis=0),
            jnp.swapaxes(down, 0, 1).reshape(rows, sources * feats).astype(F32),
            w_out.astype(F32),
            grad_middle + part,
            (middle + scatter_seq(part_outputs)).astype(BF16),
            (*shared, hidden),
        )
    chunks = (
        3 * cols * width + rows * width + sources * rows * feats
    ) // (CHUNK * feats)
    dma = pltpu.SemaphoreType.DMA
    line = pltpu.VMEM((chunks, CHUNK, feats), BF16)
    w_qkv, w_down, w_out, grad_inputs, outputs, sums = pl.pallas_call(
        functools.partial(finish_kernel, n, depth),
        out_shape=(
            jax.ShapeDtypeStruct((3, cols, width), BF16),
            jax.ShapeDtypeStruct((rows, sources * feats), F32),
            jax.ShapeDtypeStruct((rows, width), F32),
            jax.ShapeDtypeStruct((rows, width), F32),
            jax.ShapeDtypeStruct((rows, width), BF16),
            jax.ShapeDtypeStruct((16, width), F32),
        ),
        in_specs=[ANY] * 5 + [INSIDE] * 7,
        out_specs=(ANY, ANY, ANY, INSIDE, INSIDE, INSIDE),
        scratch_shapes=[
            pltpu.VMEM((3, 4, rows, width), BF16),
            pltpu.VMEM((3, 4, rows, width), BF16),
            pltpu.VMEM((3, 6, rows // 2, width), BF16),
            line,
            line,
            pltpu.VMEM((CHUNK, feats), F32),
            pltpu.VMEM((8, width), F32),
            pltpu.VMEM((n, 8, width), F32),
            pltpu.VMEM((16, width), F32),
            pltpu.VMEM((depth, 16, width), F32),
            dma((12,)),
            dma((chunks,)),
            dma,
            dma((3, 10)),
            dma((3, 10)),
            dma((chunks,)),
            dma((chunks,)),
            dma((chunks,)),
            dma((chunks,)),
            dma((chunks,)),
            dma((chunks,)),
            dma((3, cols * width // (CHUNK * feats))),
            dma((2, n)),
            dma((2, n)),
        ],
        compiler_params=pltpu.CompilerParams(
            collective_id=collective_id,
            has_side_effects=True,
            vmem_limit_bytes=VMEM_LIMIT,
        ),
        name="finish",
    )(
        grad_qkv,
        grad_down,
        *[p.reshape(n, rows, width) for p in (part_out, part_normed, part_outputs)],
        x,
        grad_middle,
        middle,
        gain[None],
        *gains,
    )
    return (
        w_qkv.reshape(3 * cols, width),
        w_down,
        w_out,
        grad_inputs,
        outputs,
        (sums[0], sums[1], sums[2], sums[8:, :feats].reshape(-1)),
    )


def widen_kernel(*refs):
    half = len(refs) // 2
    for source, target in zip(refs[:half], refs[half:], strict=True):
        target[...] = source[...].astype(F32)


def widen(arrays):
    steps = 8
    specs = [pl.BlockSpec((x.shape[0] // steps, x.shape[1]), lambda i: (i, 0)) for x in arrays]
    return pl.pallas_call(
        widen_kernel,
        grid=(steps,),
        out_shape=[jax.ShapeDtypeStruct(x.shape, F32) for x in arrays],
        in_specs=specs,
        out_specs=specs,
        compiler_params=pltpu.CompilerParams(vmem_limit_bytes=VMEM_LIMIT),
        name="widen",
    )(*arrays)


def body(
    inputs,
    segment_ids,
    w_qkv,
    w_out,
    w_up,
    w_down,
    gain_attn,
    gain_mix,
    gain_ffn,
    gain_hidden,
    cotangent,
):
    _, local, width = inputs.shape
    n, depth = lax.axis_size("seq"), lax.axis_size("batch")
    me = lax.axis_index("seq")
    length = local * n
    feats = w_up.shape[0]
    x_low = inputs[0]
    cot = cotangent[0]
    segment = segment_ids[0]

    w_out_full = lax.all_gather(w_out, "seq", axis=0, tiled=True)
    before = [jnp.sum((segment < d).astype(jnp.int32)) for d in range(1, DOCS)]
    start = jnp.zeros_like(segment)
    for d in range(1, DOCS):
        start = jnp.where(segment == d, before[d - 1], start)
    positions = jnp.arange(length, dtype=jnp.int32) - start
    first = start[::TILE] // TILE
    start_row = start[None, :]

    normed_full, w_heads, w_down_cols, tables = start_exchange(
        x_low, gain_attn, w_qkv, w_down, positions.astype(F32), 1
    )
    cot_late, _ = lax.optimization_barrier((cot, w_heads))
    cot_full = lax.all_gather(cot_late, "seq", axis=0, tiled=True)

    q, k, v, kt, vt = project_qkv(normed_full, w_heads, tables)
    attended_heads, lse = attend(first, start_row, q, k, vt)
    attended = heads_to_tokens(attended_heads, 2)
    mix_in, middle, ffn_in = mix_pass(attended, x_low, w_out_full, gain_mix, gain_ffn)
    gain_here = lax.dynamic_slice_in_dim(gain_hidden, me * feats, feats, 0)[None, :]
    ffn_full, hidden, grad_upper, grad_gain_here = ffn_pass(
        ffn_in, w_up, cot_full, w_down_cols, gain_here, 3
    )

    grad_w_up = tn(grad_upper, ffn_full).astype(BF16)
    grad_upper, grad_w_up = lax.optimization_barrier((grad_upper, grad_w_up))
    grad_w_up = lax.psum(grad_w_up, "batch")
    part_outputs, grad_w_down, grad_middle, grad_branch, grad_gain_ffn = ffn_back(
        grad_upper, w_up, hidden, w_down_cols, cot_full, middle, cot, gain_ffn, 4
    )
    grad_att, grad_gain_mix = branch_pass(grad_branch, attended, w_out_full, gain_mix)
    grad_heads = tokens_to_heads(grad_att, 5)
    grad_w_down, grad_heads = lax.optimization_barrier((grad_w_down, grad_heads))
    grad_w_down = lax.all_to_all(grad_w_down, "seq", split_axis=0, concat_axis=0, tiled=True)
    grads = attend_back(
        first, start_row, q, k, kt, v, attended_heads, lse, grad_heads, tables
    )
    grad_w_qkv = tn(grads, normed_full).astype(BF16).reshape(3, -1, width)
    grad_w_qkv, grad_w_up = lax.optimization_barrier((grad_w_qkv, grad_w_up))
    grad_w_qkv, grad_w_down, grad_w_out, grad_inputs, outputs, gains = finish(
        grad_w_qkv,
        grad_w_down,
        tn(grad_branch, mix_in).astype(BF16),
        nn(grads, w_heads).astype(BF16),
        part_outputs,
        x_low,
        grad_middle,
        middle,
        gain_attn,
        (grad_gain_mix, grad_gain_ffn, grad_gain_here),
        6,
    )
    grad_w_qkv, grad_w_up = widen([grad_w_qkv, grad_w_up])
    return (
        outputs[None],
        grad_inputs[None],
        grad_w_qkv,
        grad_w_out,
        grad_w_up,
        grad_w_down,
        *gains,
    )


def pick_part(turned, me, n, part):
    chosen = turned[0]
    home = part * n + me
    for j in (1, 2):
        chosen = jnp.where(lax.rem(home, 3) == j, turned[j], chosen)
    return chosen


def give_part(blocks, me, n, j):
    chosen = blocks[0]
    for part in (1, 2):
        chosen = jnp.where(lax.rem(part * n + me, 3) == j, blocks[part], chosen)
    return chosen


def solution(mesh):
    in_specs = (
        P("batch", "seq", None),
        P("batch", None),
        P("seq", None),
        P("seq", None),
        P("seq", None),
        P("seq", None),
        P(),
        P(),
        P(),
        P(),
        P("batch", "seq", None),
    )
    out_specs = (
        P("batch", "seq", None),
        P("batch", "seq", None),
        P("seq", None),
        P("seq", None),
        P("seq", None),
        P("seq", None),
        P(),
        P(),
        P(),
        P(),
    )
    return jax.shard_map(body, mesh=mesh, in_specs=in_specs, out_specs=out_specs, check_vma=False)
```

```python
import functools
import math

import jax
import jax.numpy as jnp
from jax import lax
from jax.experimental import pallas as pl
from jax.experimental.pallas import tpu as pltpu
from jax.sharding import PartitionSpec as P

HEADS = 32
HEAD_DIM = 64
LENGTH = 2048
XBASE = 512
DOCS = 4
EPSILON = 1e-05
MASKED = -1e30
TILE = 256
STEP = 32
VMEM_LIMIT = 60 * 1024 * 1024

MESH = pl.DeviceIdType.MESH
F32 = jnp.float32
BF16 = jnp.bfloat16
ANY = pl.BlockSpec(memory_space=pl.ANY)
INSIDE = pl.BlockSpec(memory_space=pltpu.VMEM)


def nn(a, b):
    return lax.dot_general(a, b, (((1,), (0,)), ((), ())), preferred_element_type=F32)


def nt(a, b):
    return lax.dot_general(a, b, (((1,), (1,)), ((), ())), preferred_element_type=F32)


def tn(a, b):
    return lax.dot_general(a, b, (((0,), (0,)), ((), ())), preferred_element_type=F32)


def norm_parts(values):
    average = jnp.mean(values, axis=-1, keepdims=True)
    centered = values - average
    spread = jnp.mean(centered * centered, axis=-1, keepdims=True)
    scale = lax.rsqrt(spread + EPSILON)
    return centered * scale, scale


def norm_back(grad, normal, scale, gain):
    part = grad * gain
    inner = (
        part
        - jnp.mean(part, axis=-1, keepdims=True)
        - normal * jnp.mean(part * normal, axis=-1, keepdims=True)
    )
    return scale * inner, jnp.sum(grad * normal, axis=0)


def places():
    me = lax.axis_index("seq")
    core = lax.rem(me, 2)
    along_x = lax.rem(me // 2, 2)
    along_y = me // 4
    twin = 1 - 2 * core
    near_x = me + 2 - 4 * along_x
    near_y = me + 4 - 8 * along_y
    across = near_x + 4 - 8 * along_y
    return me, twin, near_x, near_y, across


def remote(src, dst, send_sem, recv_sem, partner):
    return pltpu.make_async_remote_copy(
        src_ref=src,
        dst_ref=dst,
        send_sem=send_sem,
        recv_sem=recv_sem,
        device_id={"seq": partner},
        device_id_type=MESH,
    )


def meet(partners):
    barrier = pltpu.get_barrier_semaphore()
    for partner in partners:
        pl.semaphore_signal(
            barrier, inc=1, device_id={"seq": partner}, device_id_type=MESH
        )
    pl.semaphore_wait(barrier, len(partners))


def gather_copies(x_ref, o_ref, send_sem, recv_sem):
    me, twin, near_x, near_y, across = places()
    half = x_ref.shape[0] // 2
    low, high = pl.ds(0, half), pl.ds(half, half)

    def copy(k, src, dst, partner):
        return remote(src, dst, send_sem.at[k], recv_sem.at[k], partner)

    def relay(k, owner, rows, partner):
        place = o_ref.at[owner, rows]
        return copy(k, place, place, partner)

    return [
        copy(0, x_ref.at[low], o_ref.at[me, low], near_x),
        copy(1, x_ref.at[high], o_ref.at[me, high], near_y),
        copy(2, x_ref.at[high], o_ref.at[me, high], near_x),
        copy(3, x_ref.at[low], o_ref.at[me, low], near_y),
        copy(4, x_ref, o_ref.at[me], me + twin),
        relay(5, near_x, low, near_y),
        relay(6, near_y, high, near_x),
        relay(7, near_x, low, me + twin),
        relay(8, near_y, high, me + twin),
        relay(9, near_x, high, me + twin),
        relay(10, near_y, low, me + twin),
        relay(11, across, low, me + twin),
        relay(12, across, high, me + twin),
    ]


def gather_run(sends, *between):
    between = (*between, *([None] * 3))[:3]

    def pause(i):
        if between[i] is not None:
            between[i]()

    sends[0].wait_recv()
    sends[5].start()
    sends[7].start()
    sends[1].wait_recv()
    sends[6].start()
    sends[8].start()
    pause(0)
    sends[2].wait_recv()
    sends[9].start()
    sends[3].wait_recv()
    sends[10].start()
    pause(1)
    sends[5].wait_recv()
    sends[11].start()
    sends[6].wait_recv()
    sends[12].start()
    pause(2)
    for k in (4, 7, 8, 9, 10, 11, 12):
        sends[k].wait_recv()
    for send in sends:
        send.wait_send()


def meet_all(n, depth):
    me = lax.axis_index("seq")
    z = lax.axis_index("batch")
    barrier = pltpu.get_barrier_semaphore()
    for k in range(1, n):
        pl.semaphore_signal(
            barrier, inc=1, device_id={"seq": lax.rem(me + k, n)}, device_id_type=MESH
        )
    for k in range(1, depth):
        pl.semaphore_signal(
            barrier,
            inc=1,
            device_id={"batch": lax.rem(z + k, depth)},
            device_id_type=MESH,
        )
    pl.semaphore_wait(barrier, n + depth - 2)


def line_remote(src, dst, send_sem, recv_sem, partner):
    return pltpu.make_async_remote_copy(
        src_ref=src,
        dst_ref=dst,
        send_sem=send_sem,
        recv_sem=recv_sem,
        device_id={"batch": partner},
        device_id_type=MESH,
    )


class Line:
    def __init__(self, depth, source, target, send_sem, recv_sem):
        self.depth, self.source, self.target = depth, source, target
        self.send_sem, self.recv_sem = send_sem, recv_sem
        self.z = lax.axis_index("batch")

    def message(self, side, k):
        sign = 2 * side - 1
        owner = self.z - sign * k
        return line_remote(
            self.source(owner, k),
            self.target(owner),
            self.send_sem.at[side, k],
            self.recv_sem.at[side, k],
            self.z + sign,
        )

    def sends(self, side, k):
        sign = 2 * side - 1
        owner, target = self.z - sign * k, self.z + sign
        inside = (owner >= 0) & (owner < self.depth)
        return inside & (target >= 0) & (target < self.depth)

    def land(self, k):
        for side in (0, 1):
            sign = 2 * side - 1
            owner = self.z - sign * (k + 1)

            @pl.when((owner >= 0) & (owner < self.depth))
            def _():
                place = self.target(owner)
                line_remote(
                    place,
                    place,
                    self.send_sem.at[side, k],
                    self.recv_sem.at[side, k],
                    self.z - sign,
                ).wait_recv()

    def start(self, k):
        for side in (0, 1):

            @pl.when(self.sends(side, k))
            def _():
                self.message(side, k).start()

    def sent(self, k):
        for side in (0, 1):

            @pl.when(self.sends(side, k))
            def _():
                self.message(side, k).wait_send()


def lane_tables(place):
    half = HEAD_DIM // 2
    lane = lax.broadcasted_iota(jnp.int32, (1, 128), 1)
    channel = lax.rem(lane, half).astype(F32)
    inverse = jnp.exp(channel * (-math.log(10000.0) / half))
    zeta = (channel * (2.0 / HEAD_DIM) + 0.4) / 1.4
    sign = jnp.where(lax.rem(lane, HEAD_DIM) < half, -1.0, 1.0)
    angle = place * inverse
    growth = jnp.exp((place - 0.5 * LENGTH) * (1.0 / XBASE) * jnp.log(zeta))
    shrink = 1.0 / growth
    cosine = jnp.cos(angle)
    sine = jnp.sin(angle) * sign
    return cosine * growth, sine * growth, cosine * shrink, sine * shrink


def start_kernel(
    n, depth, x_ref, gain_ref, w_ref, wd_ref, pos_ref,
    o_ref, wt_ref, wc_ref, cq_ref, sq_ref, ck_ref, sk_ref,
    normed, keep_w, keep_c, local_sem, send_sem, recv_sem, hop_send, hop_recv, col_send, col_recv,
    line_send, line_recv,
):
    z = lax.axis_index("batch")
    rows_z = wc_ref.shape[2]
    cols = wc_ref.shape[3]
    me, twin, near_x, near_y, _ = places()
    own = pltpu.make_async_copy(normed, o_ref.at[me], local_sem.at[0])
    wd_rows = pl.ds(pl.multiple_of(z * rows_z, rows_z), rows_z)

    def column(k):
        return wd_ref.at[wd_rows, pl.ds(pl.multiple_of(k * cols, cols), cols)]

    load_column = pltpu.make_async_copy(column(me), keep_c, local_sem.at[4])
    own_column = pltpu.make_async_copy(keep_c, wc_ref.at[me, z], local_sem.at[5])
    load_column.start()
    meet_all(n, depth)
    load_column.wait()
    own_column.start()

    def hop(j, part, target):
        return remote(
            w_ref.at[j], wt_ref.at[part], hop_send.at[j], hop_recv.at[part], target
        )

    def load(j):
        return pltpu.make_async_copy(w_ref.at[j], keep_w, local_sem.at[6])

    def here(j, part):
        return pltpu.make_async_copy(keep_w, wt_ref.at[part], local_sem.at[1 + j])

    turns = [
        remote(
            column(lax.rem(me + k, n)),
            wc_ref.at[me, z],
            col_send.at[k],
            col_recv.at[k],
            lax.rem(me + k, n),
        )
        for k in range(1, n)
    ]
    for turn in turns:
        turn.start()

    @pl.loop(0, x_ref.shape[0] // STEP)
    def _(r):
        at = pl.ds(pl.multiple_of(r * STEP, STEP), STEP)
        normal, _ = norm_parts(x_ref[at].astype(F32))
        normed[at] = (normal * gain_ref[...]).astype(BF16)

    own.start()
    sends = gather_copies(normed, o_ref, send_sem, recv_sem)
    for k in range(5):
        sends[k].start()
    for j in range(3):
        block = 3 * me + j
        target = lax.rem(block, n)
        for part in range(3):
            inside = block // n == part

            @pl.when(inside & (target != me))
            def _():
                hop(j, part, target).start()

            @pl.when(inside & (target == me))
            def _():
                load(j).start()

    line = Line(
        depth,
        lambda owner, k: wc_ref.at[:, owner],
        lambda owner: wc_ref.at[:, owner],
        line_send,
        line_recv,
    )

    own_column.wait()
    for turn in turns:
        turn.wait_recv()
    line.start(0)
    for j in range(3):
        block = 3 * me + j
        target = lax.rem(block, n)
        for part in range(3):

            @pl.when((block // n == part) & (target == me))
            def _():
                load(j).wait()
                here(j, part).start()

    @pl.loop(0, pos_ref.shape[0])
    def _(r):
        at = pl.ds(pl.multiple_of(r * 128, 128), 128)
        places_here = jnp.broadcast_to(pos_ref[pl.ds(r, 1), :], (128, 128)).T
        tables = lane_tables(places_here)
        for ref, table in zip((cq_ref, sq_ref, ck_ref, sk_ref), tables, strict=True):
            ref[at] = table

    def hand_on(k):
        def step():
            line.land(k - 1)
            line.start(k)

        return step

    hand_on(1)()
    gather_run(sends, *[hand_on(k) for k in range(2, depth - 1)])
    line.land(depth - 2)
    for k in range(depth - 1):
        line.sent(k)
    for turn in turns:
        turn.wait_send()
    for j in range(3):
        block = 3 * me + j
        target = lax.rem(block, n)
        for part in range(3):
            inside = block // n == part

            @pl.when(inside & (target != me))
            def _():
                hop(j, part, target).wait_send()

            @pl.when(inside & (target == me))
            def _():
                here(j, part).wait()

    for part in range(3):
        source = (part * n + me) // 3

        @pl.when(source != me)
        def _():
            hop(0, part, source).wait_recv()

    own.wait()


def start_exchange(block, gain, w_qkv, w_down, positions, collective_id):
    n, depth = lax.axis_size("seq"), lax.axis_size("batch")
    rows, width = block.shape
    piece = w_qkv.shape[0] // 3
    w = w_qkv.reshape(3, piece, width)
    if n != 8:
        me = lax.axis_index("seq")
        turned = [
            lax.ppermute(w[j], "seq", [(d, (3 * d + j) % n) for d in range(n)])
            for j in range(3)
        ]
        parts = [pick_part(turned, me, n, part) for part in range(3)]
        place = jnp.broadcast_to(positions[:, None], (positions.shape[0], 128))
        normed = (norm_parts(block.astype(F32))[0] * gain).astype(BF16)
        return (
            lax.all_gather(normed, "seq", axis=0, tiled=True),
            jnp.concatenate(parts, axis=0),
            lax.all_to_all(w_down, "seq", split_axis=1, concat_axis=0, tiled=True),
            lane_tables(place),
        )
    rows_z, cols = w_down.shape[0] // depth, w_down.shape[1] // n
    inside = pl.BlockSpec(memory_space=pltpu.VMEM)
    table = jax.ShapeDtypeStruct((n * rows, 128), F32)
    gathered, turned, columns, *tables = pl.pallas_call(
        functools.partial(start_kernel, n, depth),
        out_shape=(
            jax.ShapeDtypeStruct((n, rows, width), block.dtype),
            jax.ShapeDtypeStruct((3, piece, width), w.dtype),
            jax.ShapeDtypeStruct((n, depth, rows_z, cols), w_down.dtype),
            *([table] * 4),
        ),
        in_specs=[INSIDE, INSIDE, ANY, ANY, INSIDE],
        out_specs=(ANY, ANY, ANY, *([INSIDE] * 4)),
        scratch_shapes=[
            pltpu.VMEM((rows, width), BF16),
            pltpu.VMEM((piece, width), BF16),
            pltpu.VMEM((rows_z, cols), BF16),
            pltpu.SemaphoreType.DMA((7,)),
            pltpu.SemaphoreType.DMA((13,)),
            pltpu.SemaphoreType.DMA((13,)),
            pltpu.SemaphoreType.DMA((3,)),
            pltpu.SemaphoreType.DMA((3,)),
            pltpu.SemaphoreType.DMA((n,)),
            pltpu.SemaphoreType.DMA((n,)),
            pltpu.SemaphoreType.DMA((2, depth)),
            pltpu.SemaphoreType.DMA((2, depth)),
        ],
        compiler_params=pltpu.CompilerParams(
            collective_id=collective_id, has_side_effects=True, vmem_limit_bytes=VMEM_LIMIT
        ),
        name="start_exchange",
    )(block, gain[None], w, w_down, positions.reshape(-1, 128))
    return (
        gathered.reshape(n * rows, width),
        turned.reshape(3 * piece, width),
        columns.reshape(-1, cols),
        tables,
    )


def scatter_seq(partial):
    return lax.psum_scatter(partial, "seq", scatter_dimension=0, tiled=True).astype(F32)


def heads_to_tokens_kernel(n, x_ref, o_ref, keep, local_sem, send_sem, recv_sem):
    me = lax.axis_index("seq")
    rows = o_ref.shape[0]
    cols = x_ref.shape[1]
    exchange(
        n,
        me,
        lambda k: x_ref.at[pl.ds(pl.multiple_of(k * rows, rows), rows)],
        o_ref.at[:, pl.ds(pl.multiple_of(me * cols, cols), cols)],
        keep,
        local_sem,
        send_sem,
        recv_sem,
    )


def exchange(n, me, source, target, keep, local_sem, send_sem, recv_sem):
    load = pltpu.make_async_copy(source(me), keep, local_sem.at[0])
    own = pltpu.make_async_copy(keep, target, local_sem.at[1])
    load.start()
    barrier = pltpu.get_barrier_semaphore()
    for k in range(1, n):
        pl.semaphore_signal(
            barrier,
            inc=1,
            device_id={"seq": lax.rem(me + k, n)},
            device_id_type=MESH,
        )
    pl.semaphore_wait(barrier, n - 1)
    copies = []
    for k in range(1, n):
        partner = lax.rem(me + k, n)
        copies.append(
            pltpu.make_async_remote_copy(
                src_ref=source(partner),
                dst_ref=target,
                send_sem=send_sem.at[k],
                recv_sem=recv_sem.at[k],
                device_id={"seq": partner},
                device_id_type=MESH,
            )
        )
        copies[-1].start()
    load.wait()
    own.start()
    for copy in copies:
        copy.wait()
    own.wait()


def heads_to_tokens(heads, collective_id):
    n = lax.axis_size("seq")
    total, cols = heads.shape
    rows = total // n
    return pl.pallas_call(
        functools.partial(heads_to_tokens_kernel, n),
        out_shape=jax.ShapeDtypeStruct((rows, n * cols), heads.dtype),
        in_specs=[ANY],
        out_specs=ANY,
        scratch_shapes=[
            pltpu.VMEM((rows, cols), heads.dtype),
            pltpu.SemaphoreType.DMA((2,)),
            pltpu.SemaphoreType.DMA((n,)),
            pltpu.SemaphoreType.DMA((n,)),
        ],
        compiler_params=pltpu.CompilerParams(
            collective_id=collective_id, has_side_effects=True, vmem_limit_bytes=VMEM_LIMIT
        ),
        name="heads_to_tokens",
    )(heads)


def tokens_to_heads_kernel(n, x_ref, o_ref, keep, local_sem, send_sem, recv_sem):
    me = lax.axis_index("seq")
    rows = x_ref.shape[0]
    cols = o_ref.shape[1]
    exchange(
        n,
        me,
        lambda k: x_ref.at[:, pl.ds(pl.multiple_of(k * cols, cols), cols)],
        o_ref.at[pl.ds(pl.multiple_of(me * rows, rows), rows)],
        keep,
        local_sem,
        send_sem,
        recv_sem,
    )


def tokens_to_heads(tokens, collective_id):
    n = lax.axis_size("seq")
    rows, total = tokens.shape
    return pl.pallas_call(
        functools.partial(tokens_to_heads_kernel, n),
        out_shape=jax.ShapeDtypeStruct((rows * n, total // n), tokens.dtype),
        in_specs=[ANY],
        out_specs=ANY,
        scratch_shapes=[
            pltpu.VMEM((rows, total // n), tokens.dtype),
            pltpu.SemaphoreType.DMA((2,)),
            pltpu.SemaphoreType.DMA((n,)),
            pltpu.SemaphoreType.DMA((n,)),
        ],
        compiler_params=pltpu.CompilerParams(
            collective_id=collective_id, has_side_effects=True, vmem_limit_bytes=VMEM_LIMIT
        ),
        name="tokens_to_heads",
    )(tokens)


def swap_halves(values):
    width = values.shape[-1]
    half = HEAD_DIM // 2
    lane = lax.broadcasted_iota(jnp.int32, values.shape, 1)
    ahead = pltpu.roll(values, width - half, 1)
    behind = pltpu.roll(values, half, 1)
    return jnp.where(lane % HEAD_DIM < half, ahead, behind)


def spread_lanes(table, width):
    return jnp.concatenate([table] * (width // table.shape[-1]), axis=-1)


def qkv_kernel(
    x_ref, w_ref, cq_ref, sq_ref, ck_ref, sk_ref,
    q_ref, k_ref, v_ref, kt_ref, vt_ref,
):
    x = x_ref[...]
    width = q_ref.shape[1]
    query = nt(x, w_ref[0:width])
    query = query * spread_lanes(cq_ref[...], width) + swap_halves(
        query
    ) * spread_lanes(sq_ref[...], width)
    q_ref[...] = query.astype(BF16) * (HEAD_DIM**-0.5)
    keys = nt(x, w_ref[width : 2 * width])
    keys = keys * spread_lanes(ck_ref[...], width) + swap_halves(
        keys
    ) * spread_lanes(sk_ref[...], width)
    k_ref[...] = keys.astype(BF16)
    kt_ref[...] = keys.T.astype(BF16)
    values = nt(x, w_ref[2 * width :])
    v_ref[...] = values.astype(BF16)
    vt_ref[...] = values.T.astype(BF16)


def project_qkv(x, w, tables):
    length, width = x.shape
    cols = w.shape[0] // 3
    steps = length // TILE
    weight = pl.BlockSpec((3 * cols, width), lambda i: (0, 0))
    table = pl.BlockSpec((TILE, tables[0].shape[1]), lambda i: (i, 0))
    row_out = pl.BlockSpec((TILE, cols), lambda i: (i, 0))
    col_out = pl.BlockSpec((cols, TILE), lambda i: (0, i))
    rows = jax.ShapeDtypeStruct((length, cols), BF16)
    columns = jax.ShapeDtypeStruct((cols, length), BF16)
    return pl.pallas_call(
        qkv_kernel,
        grid=(steps,),
        out_shape=(rows, rows, rows, columns, columns),
        in_specs=[pl.BlockSpec((TILE, width), lambda i: (i, 0))]
        + [weight]
        + [table] * 4,
        out_specs=(row_out, row_out, row_out, col_out, col_out),
        compiler_params=pltpu.CompilerParams(vmem_limit_bytes=VMEM_LIMIT),
        cost_estimate=pl.CostEstimate(
            flops=6 * length * width * cols,
            bytes_accessed=2 * length * width + 6 * width * cols + 10 * length * cols,
            transcendentals=0,
        ),
        name="project_qkv",
    )(x, w, *tables)


def pair_mask(start_row, i, j):
    key_place = j * TILE + lax.broadcasted_iota(jnp.int32, (TILE, TILE), 0)
    query_place = i * TILE + lax.broadcasted_iota(jnp.int32, (TILE, TILE), 1)
    return (key_place <= query_place) & (key_place >= start_row)


def head_rows(query, heads):
    lane = lax.broadcasted_iota(jnp.int32, query.shape, 1) // HEAD_DIM
    zero = jnp.zeros_like(query)
    return [jnp.where(lane == h, query, zero) for h in range(heads)]


def attend_kernel(
    heads, first_ref, start_ref, q_ref, k_ref, vt_ref, o_ref, lse_ref, peak, total, mixed
):
    i = pl.program_id(0)
    queries = head_rows(q_ref[...], heads)
    start_row = start_ref[...]

    def block(j, first):
        at = pl.ds(pl.multiple_of(j * TILE, TILE), TILE)
        keys = k_ref[at, :]
        mask = pair_mask(start_row, i, j)
        for h in range(heads):
            here = slice(h * HEAD_DIM, (h + 1) * HEAD_DIM)
            scores = jnp.where(mask, nt(keys, queries[h]), MASKED)
            if first:
                new_peak = jnp.max(scores, axis=0, keepdims=True)
                expo = jnp.exp(scores - new_peak)
                total[h : h + 1] = jnp.sum(expo, axis=0, keepdims=True)
                mixed[here] = nn(vt_ref[here, at], expo.astype(BF16))
            else:
                old_peak = peak[h : h + 1]
                new_peak = jnp.maximum(old_peak, jnp.max(scores, axis=0, keepdims=True))
                expo = jnp.exp(scores - new_peak)
                shrink = jnp.exp(old_peak - new_peak)
                total[h : h + 1] = total[h : h + 1] * shrink + jnp.sum(
                    expo, axis=0, keepdims=True
                )
                mixed[here] = mixed[here] * shrink + nn(
                    vt_ref[here, at], expo.astype(BF16)
                )
            peak[h : h + 1] = new_peak

    block(i, True)

    @pl.loop(0, i - first_ref[i])
    def _(t):
        block(i - 1 - t, False)

    for h in range(heads):
        here = slice(h * HEAD_DIM, (h + 1) * HEAD_DIM)
        mixed[here] = mixed[here] / total[h : h + 1]
    o_ref[...] = mixed[...].T.astype(BF16)
    lse_ref[0] = peak[...] + jnp.log(total[...])


def attend(first, start, q, k, vt):
    length, cols = q.shape
    heads = cols // HEAD_DIM
    steps = length // TILE
    row = pl.BlockSpec((TILE, cols), lambda i, *_: (i, 0))
    return pl.pallas_call(
        functools.partial(attend_kernel, heads),
        out_shape=(
            jax.ShapeDtypeStruct((length, cols), BF16),
            jax.ShapeDtypeStruct((steps, heads, TILE), F32),
        ),
        grid_spec=pltpu.PrefetchScalarGridSpec(
            num_scalar_prefetch=1,
            grid=(steps,),
            in_specs=[
                pl.BlockSpec((1, TILE), lambda i, *_: (0, i)),
                row,
                pl.BlockSpec((length, cols), lambda i, *_: (0, 0)),
                pl.BlockSpec((cols, length), lambda i, *_: (0, 0)),
            ],
            out_specs=(
                row,
                pl.BlockSpec((1, heads, TILE), lambda i, *_: (i, 0, 0)),
            ),
            scratch_shapes=[
                pltpu.VMEM((heads, TILE), F32),
                pltpu.VMEM((heads, TILE), F32),
                pltpu.VMEM((cols, TILE), F32),
            ],
        ),
        compiler_params=pltpu.CompilerParams(vmem_limit_bytes=VMEM_LIMIT),
        cost_estimate=pl.CostEstimate(
            flops=4 * length * 1024 * cols,
            bytes_accessed=8 * length * cols,
            transcendentals=length * 1024 * heads,
        ),
        name="attend",
    )(first, start, q, k, vt)


def attend_back_kernel(
    heads, first_ref, start_ref, q_ref, k_ref, kt_ref, v_ref, o_ref, lse_ref, do_ref,
    cq_ref, sq_ref, ck_ref, sk_ref, grad_ref, dqt, dk_sum, dv_sum,
):
    i = pl.program_id(0)
    steps = pl.num_programs(0)
    width = q_ref.shape[1]
    queries = head_rows(q_ref[...], heads)
    grads = head_rows(do_ref[...], heads)
    start_row = start_ref[...]
    product = (do_ref[...].astype(F32) * o_ref[...].astype(F32)).T
    inner = [
        jnp.sum(product[h * HEAD_DIM : (h + 1) * HEAD_DIM], axis=0, keepdims=True)
        for h in range(heads)
    ]

    def block(j, first):
        at = pl.ds(pl.multiple_of(j * TILE, TILE), TILE)
        keys = k_ref[at, :]
        values = v_ref[at, :]
        mask = pair_mask(start_row, i, j)
        key_term = None
        value_term = None
        for h in range(heads):
            here = slice(h * HEAD_DIM, (h + 1) * HEAD_DIM)
            scores = nt(keys, queries[h])
            weights = jnp.where(mask, jnp.exp(scores - lse_ref[0, h : h + 1]), 0.0)
            grad_weights = nt(values, grads[h])
            grad_scores = (weights * (grad_weights - inner[h])).astype(BF16)
            term = nn(weights.astype(BF16), grads[h])
            value_term = term if value_term is None else value_term + term
            term = nn(grad_scores, queries[h])
            key_term = term if key_term is None else key_term + term
            term = nn(kt_ref[here, at], grad_scores)
            if first:
                dqt[here] = term
            else:
                dqt[here] = dqt[here] + term
        if first:
            dk_sum[at] = key_term
            dv_sum[at] = value_term
        else:
            dk_sum[at] = dk_sum[at] + key_term
            dv_sum[at] = dv_sum[at] + value_term

    block(i, True)

    @pl.loop(0, i - first_ref[i])
    def _(t):
        block(i - 1 - t, False)

    def unturn(grad, cosine, sine):
        grad = grad.astype(BF16).astype(F32)
        cosine = spread_lanes(cosine, width)
        sine = spread_lanes(sine, width)
        return (grad * cosine - swap_halves(grad) * sine).astype(BF16)

    rows = pl.ds(pl.multiple_of(i * TILE, TILE), TILE)
    grad_ref[rows, 0:width] = unturn(
        dqt[...].T * (HEAD_DIM**-0.5), cq_ref[rows, :], sq_ref[rows, :]
    )

    @pl.when(i == steps - 1)
    def _():
        @pl.loop(0, steps)
        def _(j):
            at = pl.ds(pl.multiple_of(j * TILE, TILE), TILE)
            grad_ref[at, width : 2 * width] = unturn(
                dk_sum[at], ck_ref[at, :], sk_ref[at, :]
            )
            grad_ref[at, 2 * width :] = dv_sum[at].astype(BF16)


def attend_back(first, start, q, k, kt, v, o, lse, do, tables):
    length, cols = q.shape
    heads = cols // HEAD_DIM
    steps = length // TILE
    row = pl.BlockSpec((TILE, cols), lambda i, *_: (i, 0))
    whole = pl.BlockSpec((length, cols), lambda i, *_: (0, 0))
    table = pl.BlockSpec((length, tables[0].shape[1]), lambda i, *_: (0, 0))
    return pl.pallas_call(
        functools.partial(attend_back_kernel, heads),
        out_shape=jax.ShapeDtypeStruct((length, 3 * cols), BF16),
        grid_spec=pltpu.PrefetchScalarGridSpec(
            num_scalar_prefetch=1,
            grid=(steps,),
            in_specs=[
                pl.BlockSpec((1, TILE), lambda i, *_: (0, i)),
                row,
                whole,
                pl.BlockSpec((cols, length), lambda i, *_: (0, 0)),
                whole,
                row,
                pl.BlockSpec((1, heads, TILE), lambda i, *_: (i, 0, 0)),
                row,
            ]
            + [table] * 4,
            out_specs=pl.BlockSpec((length, 3 * cols), lambda i, *_: (0, 0)),
            scratch_shapes=[
                pltpu.VMEM((cols, TILE), F32),
                pltpu.VMEM((length, cols), F32),
                pltpu.VMEM((length, cols), F32),
            ],
        ),
        compiler_params=pltpu.CompilerParams(vmem_limit_bytes=VMEM_LIMIT),
        name="attend_back",
    )(first, start, q, k, kt, v, o, lse, do, *tables)


def upper_kernel(
    x_ref, wu_ref, c_ref, wd_ref, gain_ref, act_ref, slope_ref, grad_ref, stat_ref
):
    upper = nt(x_ref[...], wu_ref[...])
    grad = nn(c_ref[...], wd_ref[...])
    below = 0.5 * (1.0 + lax.erf(upper * (0.5**0.5)))
    act = upper * below
    slope = below + upper * (jnp.exp(-0.5 * upper * upper) * ((2.0 * math.pi) ** -0.5))
    act_ref[...] = act
    slope_ref[...] = slope.astype(BF16)
    grad_ref[...] = grad
    part = grad * gain_ref[...]
    average = jnp.mean(act, axis=-1, keepdims=True)
    centered = act - average
    spread = jnp.sum(centered * centered, axis=-1, keepdims=True)
    part_sum = jnp.sum(part, axis=-1, keepdims=True)
    cross = jnp.sum(part * centered, axis=-1, keepdims=True)
    lane = lax.broadcasted_iota(jnp.int32, (x_ref.shape[0], 128), 1)
    columns = jnp.where(
        lane == 0,
        average,
        jnp.where(lane == 1, spread, jnp.where(lane == 2, part_sum, cross)),
    )
    stat_ref[...] = columns.T[:8]


def upper_pass(x, w_up, cot, w_down, gain):
    length, width = x.shape
    feats = w_up.shape[0]
    rows = TILE
    row = pl.BlockSpec((rows, width), lambda i: (i, 0))
    out = pl.BlockSpec((rows, feats), lambda i: (i, 0))
    return pl.pallas_call(
        upper_kernel,
        grid=(length // rows,),
        out_shape=(
            jax.ShapeDtypeStruct((length, feats), F32),
            jax.ShapeDtypeStruct((length, feats), BF16),
            jax.ShapeDtypeStruct((length, feats), F32),
            jax.ShapeDtypeStruct((8, length), F32),
        ),
        in_specs=[
            row,
            pl.BlockSpec((feats, width), lambda i: (0, 0)),
            row,
            pl.BlockSpec((width, feats), lambda i: (0, 0)),
            pl.BlockSpec((1, feats), lambda i: (0, 0)),
        ],
        out_specs=(out, out, out, pl.BlockSpec((8, rows), lambda i: (0, i))),
        compiler_params=pltpu.CompilerParams(vmem_limit_bytes=VMEM_LIMIT),
        cost_estimate=pl.CostEstimate(
            flops=4 * length * width * feats,
            bytes_accessed=8 * length * width + 8 * length * feats,
            transcendentals=2 * length * feats,
        ),
        name="upper_pass",
    )(x, w_up, cot, w_down, gain)


def hidden_kernel(act_ref, slope_ref, grad_ref, stat_ref, gain_ref, hid_ref, gu_ref, gg_ref):
    i = pl.program_id(0)
    stats = stat_ref[...].T
    average = stats[:, 0:1]
    scale = stats[:, 1:2]
    part_mean = stats[:, 2:3]
    cross_mean = stats[:, 3:4]
    gain = gain_ref[...]
    normal = (act_ref[...] - average) * scale
    grad = grad_ref[...]
    hid_ref[...] = (normal * gain).astype(BF16)
    back = scale * (grad * gain - part_mean - normal * cross_mean)
    gu_ref[...] = (slope_ref[...].astype(F32) * back).astype(BF16)
    term = jnp.sum(grad * normal, axis=0, keepdims=True)

    @pl.when(i == 0)
    def _():
        gg_ref[...] = term

    @pl.when(i > 0)
    def _():
        gg_ref[...] = gg_ref[...] + term


def hidden_pass(act, slope, grad, stats, gain):
    length, feats = act.shape
    out = pl.BlockSpec((TILE, feats), lambda i: (i, 0))
    one = pl.BlockSpec((1, feats), lambda i: (0, 0))
    return pl.pallas_call(
        hidden_kernel,
        grid=(length // TILE,),
        out_shape=(
            jax.ShapeDtypeStruct((length, feats), BF16),
            jax.ShapeDtypeStruct((length, feats), BF16),
            jax.ShapeDtypeStruct((1, feats), F32),
        ),
        in_specs=[out, out, out, pl.BlockSpec((8, TILE), lambda i: (0, i)), one],
        out_specs=(out, out, one),
        compiler_params=pltpu.CompilerParams(vmem_limit_bytes=VMEM_LIMIT),
        cost_estimate=pl.CostEstimate(
            flops=12 * length * feats,
            bytes_accessed=14 * length * feats,
            transcendentals=0,
        ),
        name="hidden_pass",
    )(act, slope, grad, stats, gain)


def ffn_kernel(
    n, x_ref, wu_ref, cot_ref, wd_ref, gain_ref,
    full_ref, hid_ref, gu_ref, gg_ref,
    rows_in, wd, cot_in, act, slope, grad, stat, held, results,
    local_sem, cot_sem, out_sem, full_sem, send_sem, recv_sem, stat_send, stat_recv,
):
    me, twin, near_x, near_y, across = places()
    rows = x_ref.shape[0]
    feats = wu_ref.shape[0]

    def cut(i, size=rows):
        return pl.ds(pl.multiple_of(i * size, size), size)

    own = pltpu.make_async_copy(x_ref, rows_in.at[me], local_sem.at[0])
    own.start()
    load_wd = pltpu.make_async_copy(wd_ref, wd, local_sem.at[1])
    load_wd.start()

    def load_cot(i, slot):
        return pltpu.make_async_copy(
            cot_ref.at[cut(i)], cot_in.at[slot], cot_sem.at[slot]
        )

    load_cot(0, 0).start()
    meet([lax.rem(me + k, n) for k in range(1, n)])
    sends = gather_copies(x_ref, rows_in, send_sem, recv_sem)
    for k in range(5):
        sends[k].start()

    load_wd.wait()
    def incoming(first, last):
        @pl.loop(first, last)
        def _(i):
            slot = lax.rem(i, 2)

            @pl.when(i + 1 < n)
            def _():
                load_cot(i + 1, 1 - slot).start()

            load_cot(i, slot).wait()
            grad[cut(i)] = nn(cot_in[slot], wd[...])

    incoming(0, n - 2)
    sends[0].wait_recv()
    sends[5].start()
    sends[7].start()
    sends[1].wait_recv()
    sends[6].start()
    sends[8].start()
    incoming(n - 2, n)
    own.wait()

    def keep(b):
        return pltpu.make_async_copy(rows_in.at[b], full_ref.at[b], full_sem.at[b])

    @pl.loop(0, n)
    def _(i):
        @pl.when(i == 1)
        def _():
            sends[4].wait_recv()

        @pl.when(i == 2)
        def _():
            sends[2].wait_recv()
            sends[9].start()
            sends[3].wait_recv()
            sends[10].start()

        @pl.when(i == 4)
        def _():
            sends[7].wait_recv()
            sends[9].wait_recv()

        @pl.when(i == 5)
        def _():
            sends[8].wait_recv()
            sends[10].wait_recv()
            sends[5].wait_recv()
            sends[11].start()
            sends[6].wait_recv()
            sends[12].start()

        @pl.when(i == 7)
        def _():
            sends[11].wait_recv()
            sends[12].wait_recv()

        other = jnp.where((i == 1) | (i == 4) | (i == 5) | (i == 7), twin, 0)
        place = jnp.where(i < 2, me, jnp.where(i >= 6, across, jnp.where(lax.rem(i, 2) == 0, near_x, near_y)))
        b = place + other
        keep(b).start()
        at = cut(b)
        upper = nt(rows_in[b], wu_ref[...])
        below = 0.5 * (1.0 + lax.erf(upper * (0.5**0.5)))
        value = upper * below
        act[at] = value
        slope[at] = (
            below + upper * (jnp.exp(-0.5 * upper * upper) * ((2.0 * math.pi) ** -0.5))
        ).astype(BF16)
        part = grad[at] * gain_ref[...]
        average = jnp.mean(value, axis=-1, keepdims=True)
        centered = value - average
        spread = jnp.sum(centered * centered, axis=-1, keepdims=True)
        part_sum = jnp.sum(part, axis=-1, keepdims=True)
        cross = jnp.sum(part * centered, axis=-1, keepdims=True)
        lane = lax.broadcasted_iota(jnp.int32, (rows, 128), 1)
        columns = jnp.where(
            lane == 0,
            average,
            jnp.where(lane == 1, spread, jnp.where(lane == 2, part_sum, cross)),
        )
        stat[:, at] = columns.T[:8]

    held[me] = stat[...]
    rounds = [
        remote(
            stat, held.at[me], stat_send.at[k], stat_recv.at[k], lax.rem(me + k, n)
        )
        for k in range(1, n)
    ]
    for send in rounds:
        send.start()
    for send in rounds:
        send.wait()
    join_rows(n, feats, held, stat)

    def store(i, slot):
        return [
            pltpu.make_async_copy(
                results.at[slot, j], ref.at[cut(i)], out_sem.at[slot, j]
            )
            for j, ref in enumerate((hid_ref, gu_ref))
        ]

    gg_ref[...] = jnp.zeros_like(gg_ref)

    @pl.loop(0, n)
    def _(i):
        slot = lax.rem(i, 2)

        @pl.when(i >= 2)
        def _():
            for copy in store(i - 2, slot):
                copy.wait()

        at = cut(i)
        stats = stat[:, at].T
        gain = gain_ref[...]
        scale = stats[:, 1:2]
        normal = (act[at] - stats[:, 0:1]) * scale
        coming = grad[at]
        results[slot, 0] = (normal * gain).astype(BF16)
        back = scale * (coming * gain - stats[:, 2:3] - normal * stats[:, 3:4])
        results[slot, 1] = (slope[at].astype(F32) * back).astype(BF16)
        gg_ref[...] = gg_ref[...] + jnp.sum(coming * normal, axis=0, keepdims=True)
        for copy in store(i, slot):
            copy.start()

    for i in (n - 2, n - 1):
        for copy in store(i, i % 2):
            copy.wait()
    for b in range(n):
        keep(b).wait()
    for send in sends:
        send.wait_send()


def ffn_pass(ffn_in, w_up, cot, w_down, gain, collective_id):
    n = lax.axis_size("seq")
    rows, width = ffn_in.shape
    feats = w_up.shape[0]
    if n != 8:
        full = lax.all_gather(ffn_in, "seq", axis=0, tiled=True)
        act, slope, grad, stat = upper_pass(full, w_up, cot, w_down, gain)
        stats = join_stats(stat, feats, collective_id)
        return (full, *hidden_pass(act, slope, grad, stats, gain))
    length = n * rows
    dma = pltpu.SemaphoreType.DMA
    low = jax.ShapeDtypeStruct((length, feats), BF16)
    full, hidden, grad_upper, gain_grad = pl.pallas_call(
        functools.partial(ffn_kernel, n),
        out_shape=(
            jax.ShapeDtypeStruct((n, rows, width), BF16),
            low,
            low,
            jax.ShapeDtypeStruct((1, feats), F32),
        ),
        in_specs=[INSIDE, INSIDE, ANY, ANY, INSIDE],
        out_specs=(ANY, ANY, ANY, INSIDE),
        scratch_shapes=[
            pltpu.VMEM((n, rows, width), BF16),
            pltpu.VMEM((width, feats), BF16),
            pltpu.VMEM((2, rows, width), BF16),
            pltpu.VMEM((length, feats), F32),
            pltpu.VMEM((length, feats), BF16),
            pltpu.VMEM((length, feats), F32),
            pltpu.VMEM((8, length), F32),
            pltpu.VMEM((n, 8, length), F32),
            pltpu.VMEM((2, 2, rows, feats), BF16),
            dma((2,)),
            dma((2,)),
            dma((2, 2)),
            dma((n,)),
            dma((13,)),
            dma((13,)),
            dma((n,)),
            dma((n,)),
        ],
        compiler_params=pltpu.CompilerParams(
            collective_id=collective_id, has_side_effects=True, vmem_limit_bytes=VMEM_LIMIT
        ),
        name="ffn_pass",
    )(ffn_in, w_up, cot, w_down, gain)
    return full.reshape(length, width), hidden, grad_upper, gain_grad


def join_rows(n, feats, held, o_ref):
    average = held[0, 0:1]
    for d in range(1, n):
        average = average + held[d, 0:1]
    average = average * (1.0 / n)
    spread = jnp.zeros_like(average)
    part = jnp.zeros_like(average)
    cross = jnp.zeros_like(average)
    for d in range(n):
        shift = held[d, 0:1] - average
        spread = spread + held[d, 1:2] + feats * (shift * shift)
        part = part + held[d, 2:3]
        cross = cross + held[d, 3:4] + shift * held[d, 2:3]
    whole = 1.0 / (n * feats)
    scale = lax.rsqrt(spread * whole + EPSILON)
    o_ref[0:1] = average
    o_ref[1:2] = scale
    o_ref[2:3] = part * whole
    o_ref[3:4] = cross * scale * whole
    o_ref[4:8] = jnp.zeros((4, average.shape[1]), F32)


def stat_kernel(n, feats, x_ref, o_ref, held, send_sem, recv_sem):
    me = lax.axis_index("seq")
    held[me] = x_ref[...]
    meet([lax.rem(me + k, n) for k in range(1, n)])
    copies = [
        remote(x_ref, held.at[me], send_sem.at[k], recv_sem.at[k], lax.rem(me + k, n))
        for k in range(1, n)
    ]
    for copy in copies:
        copy.start()
    for copy in copies:
        copy.wait()
    join_rows(n, feats, held, o_ref)


def join_stats(stat, feats, collective_id):
    n = lax.axis_size("seq")
    inside = pl.BlockSpec(memory_space=pltpu.VMEM)
    return pl.pallas_call(
        functools.partial(stat_kernel, n, feats),
        out_shape=jax.ShapeDtypeStruct(stat.shape, F32),
        in_specs=[inside],
        out_specs=inside,
        scratch_shapes=[
            pltpu.VMEM((n, *stat.shape), F32),
            pltpu.SemaphoreType.DMA((n,)),
            pltpu.SemaphoreType.DMA((n,)),
        ],
        compiler_params=pltpu.CompilerParams(
            collective_id=collective_id, has_side_effects=True, vmem_limit_bytes=VMEM_LIMIT
        ),
        name="join_stats",
    )(stat)


def mix_kernel(att_ref, x_ref, w_ref, gm_ref, gf_ref, mix_ref, mid_ref, ffn_ref):
    j = pl.program_id(0)
    rows = att_ref.shape[0]
    cols = w_ref.shape[0]

    @pl.when(j == 0)
    def _():
        @pl.loop(0, rows // STEP)
        def _(r):
            at = pl.ds(pl.multiple_of(r * STEP, STEP), STEP)
            normal, _ = norm_parts(att_ref[at].astype(F32))
            mix_ref[at] = (normal * gm_ref[...]).astype(BF16)

    here = pl.ds(pl.multiple_of(j * cols, cols), cols)
    mid_ref[:, here] = x_ref[:, here].astype(F32) + nt(mix_ref[...], w_ref[...])

    @pl.when(j == pl.num_programs(0) - 1)
    def _():
        @pl.loop(0, rows // STEP)
        def _(r):
            at = pl.ds(pl.multiple_of(r * STEP, STEP), STEP)
            normal, _ = norm_parts(mid_ref[at])
            ffn_ref[at] = (normal * gf_ref[...]).astype(BF16)


def mix_pass(attended, x, w_out, gain_mix, gain_ffn):
    rows, width = x.shape
    cols = TILE
    n = width // cols
    whole = pl.BlockSpec((rows, width), lambda j: (0, 0))
    gain = pl.BlockSpec((1, width), lambda j: (0, 0))
    low = jax.ShapeDtypeStruct((rows, width), BF16)
    return pl.pallas_call(
        mix_kernel,
        grid=(n,),
        out_shape=(low, jax.ShapeDtypeStruct((rows, width), F32), low),
        in_specs=[
            whole,
            whole,
            pl.BlockSpec((cols, width), lambda j: (j, 0)),
            gain,
            gain,
        ],
        out_specs=(whole, whole, whole),
        compiler_params=pltpu.CompilerParams(vmem_limit_bytes=VMEM_LIMIT),
        cost_estimate=pl.CostEstimate(
            flops=2 * rows * width * width,
            bytes_accessed=2 * width * width + 12 * rows * width,
            transcendentals=0,
        ),
        name="mix_pass",
    )(attended, x, w_out, gain_mix[None], gain_ffn[None])


def branch_kernel(gbr_ref, att_ref, w_ref, gm_ref, gatt_ref, ggm_ref, total):
    j = pl.program_id(0)
    rows = att_ref.shape[0]
    cols = w_ref.shape[0]
    here = pl.ds(pl.multiple_of(j * cols, cols), cols)
    term = nn(gbr_ref[:, here], w_ref[...])

    @pl.when(j == 0)
    def _():
        total[...] = term

    @pl.when(j > 0)
    def _():
        total[...] = total[...] + term

    @pl.when(j == pl.num_programs(0) - 1)
    def _():
        ggm_ref[...] = jnp.zeros_like(ggm_ref)

        @pl.loop(0, rows // STEP)
        def _(r):
            at = pl.ds(pl.multiple_of(r * STEP, STEP), STEP)
            normal, scale = norm_parts(att_ref[at].astype(F32))
            part, gain_part = norm_back(total[at], normal, scale, gm_ref[...])
            ggm_ref[...] += gain_part[None]
            gatt_ref[at] = part.astype(BF16)


def branch_pass(grad_branch, attended, w_out, gain_mix):
    rows, width = grad_branch.shape
    cols = TILE
    n = width // cols
    whole = pl.BlockSpec((rows, width), lambda j: (0, 0))
    gain = pl.BlockSpec((1, width), lambda j: (0, 0))
    return pl.pallas_call(
        branch_kernel,
        grid=(n,),
        out_shape=(
            jax.ShapeDtypeStruct((rows, width), BF16),
            jax.ShapeDtypeStruct((1, width), F32),
        ),
        in_specs=[whole, whole, pl.BlockSpec((cols, width), lambda j: (j, 0)), gain],
        out_specs=(whole, gain),
        scratch_shapes=[pltpu.VMEM((rows, width), F32)],
        compiler_params=pltpu.CompilerParams(vmem_limit_bytes=VMEM_LIMIT),
        name="branch_pass",
    )(grad_branch, attended, w_out, gain_mix[None])


def ffn_back_kernel(
    n, gu_ref, wu_ref, hid_ref, wd_ref, all_ref, mid_ref, cot_ref, gf_ref,
    po_ref, gd_ref, gmid_ref, gbr_ref, ggf_ref,
    gu, hid, every, own, far, twin_in, held, made, made_grad,
    local_sem, made_sem, grad_sem, send_sem, recv_sem,
):
    me, twin, near_x, near_y, across = places()
    rows, width = mid_ref.shape
    half = rows // 2
    low, high = pl.ds(0, half), pl.ds(half, half)
    mine = (across, near_x, near_y, me)

    def cut(i, size=rows):
        return pl.ds(pl.multiple_of(i * size, size), size)

    load_gu = pltpu.make_async_copy(gu_ref, gu, local_sem.at[0])
    load_hid = pltpu.make_async_copy(hid_ref, hid, local_sem.at[1])
    load_all = pltpu.make_async_copy(all_ref, every, local_sem.at[2])
    for load in (load_gu, load_hid, load_all):
        load.start()
    meet((me + twin, near_x, near_y))
    load_gu.wait()

    def copy(k, src, dst, partner):
        return remote(src, dst, send_sem.at[k], recv_sem.at[k], partner)

    twins = [copy(i, far.at[i], twin_in.at[i], me + twin) for i in range(4)]
    sends = [
        copy(4, own.at[0, low], held.at[0], near_x),
        copy(5, own.at[0, high], held.at[1], near_y),
        copy(6, own.at[1, low], held.at[2], near_x),
        copy(7, own.at[2, high], held.at[3], near_y),
        copy(8, own.at[1, high], held.at[4], near_x),
        copy(9, own.at[2, low], held.at[5], near_y),
    ]

    def add(i, base, count, source):
        @pl.loop(0, count // STEP)
        def _(r):
            at = cut(r, STEP)
            to = pl.ds(pl.multiple_of(base + r * STEP, STEP), STEP)
            own[i, to] = (own[i, to].astype(F32) + source[at].astype(F32)).astype(BF16)

    for i, block in enumerate(mine):
        far[i] = nn(gu[cut(block + twin)], wu_ref[...]).astype(BF16)
        twins[i].start()
        own[i] = nn(gu[cut(block)], wu_ref[...]).astype(BF16)
        if i < 3:
            twins[i].wait_recv()
            add(i, 0, rows, twin_in.at[i])
        if i == 0:
            sends[0].start()
            sends[1].start()
        elif i < 3:
            sends[i + 1].start()

    def store(i, slot):
        return pltpu.make_async_copy(made.at[slot], po_ref.at[cut(i)], made_sem.at[slot])

    def outputs(first, last):
        @pl.loop(first, last)
        def _(i):
            slot = lax.rem(i, 2)

            @pl.when(i >= 2)
            def _():
                store(i - 2, slot).wait()

            made[slot] = nt(hid[cut(i)], wd_ref[...]).astype(BF16)
            store(i, slot).start()

    def store_grad(i, slot):
        return pltpu.make_async_copy(
            made_grad.at[slot], gd_ref.at[i], grad_sem.at[slot]
        )

    def weight_grads(first, last):
        for i in range(first, last):
            slot = i % 2
            if i >= 2:
                store_grad(i - 2, slot).wait()
            made_grad[slot] = tn(
                every[:, i * rows : (i + 1) * rows], hid[...]
            ).astype(BF16)
            store_grad(i, slot).start()

    load_hid.wait()
    load_all.wait()
    weight_grads(0, n // 2)
    sends[1].wait_recv()
    add(1, half, half, held.at[1])
    sends[4].start()
    sends[0].wait_recv()
    add(2, 0, half, held.at[0])
    sends[5].start()
    weight_grads(n // 2, n)
    outputs(0, n)
    twins[3].wait_recv()
    for k in (2, 3, 4, 5):
        sends[k].wait_recv()
    ggf_ref[...] = jnp.zeros_like(ggf_ref)
    for base, one, two in ((0, 2, 5), (half, 3, 4)):

        @pl.loop(0, half // STEP)
        def _(r):
            at = cut(r, STEP)
            to = pl.ds(pl.multiple_of(base + r * STEP, STEP), STEP)
            value = (
                own[3, to].astype(F32)
                + twin_in[3, to].astype(F32)
                + held[one, at].astype(F32)
                + held[two, at].astype(F32)
            )
            normal, scale = norm_parts(mid_ref[to])
            part, gain_part = norm_back(value, normal, scale, gf_ref[...])
            ggf_ref[...] = ggf_ref[...] + gain_part[None]
            grad = cot_ref[to].astype(F32) + part
            gmid_ref[to] = grad
            gbr_ref[to] = grad.astype(BF16)

    for i in (n - 2, n - 1):
        store(i, i % 2).wait()
        store_grad(i, i % 2).wait()
    for send in twins + sends:
        send.wait_send()


def ffn_back(grad_upper, w_up, hidden, w_down, cot_full, middle, cot, gain, collective_id):
    n = lax.axis_size("seq")
    rows, width = middle.shape
    feats = w_up.shape[0]
    if n != 8:
        normal, scale = norm_parts(middle)
        value = scatter_seq(nn(grad_upper, w_up).astype(BF16))
        part, gain_part = norm_back(value, normal, scale, gain)
        grad = cot.astype(F32) + part
        down = tn(cot_full, hidden).astype(BF16).reshape(n, rows, feats)
        outputs = nt(hidden, w_down).astype(BF16)
        return outputs, down, grad, grad.astype(BF16), gain_part[None]
    dma = pltpu.SemaphoreType.DMA
    block = pltpu.VMEM((4, rows, width), BF16)
    return pl.pallas_call(
        functools.partial(ffn_back_kernel, n),
        out_shape=(
            jax.ShapeDtypeStruct((n * rows, width), BF16),
            jax.ShapeDtypeStruct((n, rows, feats), BF16),
            jax.ShapeDtypeStruct((rows, width), F32),
            jax.ShapeDtypeStruct((rows, width), BF16),
            jax.ShapeDtypeStruct((1, width), F32),
        ),
        in_specs=[ANY, INSIDE, ANY, INSIDE, ANY, INSIDE, INSIDE, INSIDE],
        out_specs=(ANY, ANY, INSIDE, INSIDE, INSIDE),
        scratch_shapes=[
            pltpu.VMEM((n * rows, feats), BF16),
            pltpu.VMEM((n * rows, feats), BF16),
            pltpu.VMEM((n * rows, width), BF16),
            block,
            block,
            block,
            pltpu.VMEM((6, rows // 2, width), BF16),
            pltpu.VMEM((2, rows, width), BF16),
            pltpu.VMEM((2, rows, feats), BF16),
            dma((3,)),
            dma((2,)),
            dma((2,)),
            dma((10,)),
            dma((10,)),
        ],
        compiler_params=pltpu.CompilerParams(
            collective_id=collective_id, has_side_effects=True, vmem_limit_bytes=VMEM_LIMIT
        ),
        name="ffn_back",
    )(grad_upper, w_up, hidden, w_down, cot_full, middle, cot, gain[None])


CHUNK = 64


def finish_kernel(
    n, depth, gq_ref, gd_ref, pw_ref, pn_ref, po_ref, x_ref, grad_ref, mid_ref, ga_ref, gm_ref, gf_ref, gh_ref,
    oq_ref, od_ref, ow_ref, gi_ref, out_ref, sums_ref,
    own, twin_in, held, zown, zin, stage, gain_here, gain_row, gain_pack, gain_line,
    local_sem, load_sem, stage_sem, send_sem, recv_sem, keep_sem,
    up_send, up_recv, down_send, down_recv, home_send, home_recv, gain_send, gain_recv,
):
    me, twin, near_x, near_y, across = places()
    z = lax.axis_index("batch")
    rows, width = pn_ref.shape[1:]
    half = rows // 2
    low, high = pl.ds(0, half), pl.ds(half, half)
    mine = (across, near_x, near_y, me)
    _, chunk, cols = zown.shape
    across_width = width // cols
    per_part = (gq_ref.shape[1] // chunk) * across_width
    turned = gq_ref.shape[0] * per_part
    per_source = gd_ref.shape[1] // chunk
    outer = turned + gd_ref.shape[0] * per_source
    chunks = zown.shape[0]
    per_side = chunks // 2

    def cut(i, size):
        return pl.ds(pl.multiple_of(i * size, size), size)

    def wide(i):
        return cut(i // across_width, chunk), cut(lax.rem(i, across_width), cols)

    line_loads = []
    for g in range(turned):
        source = gq_ref.at[(g // per_part, *wide(g % per_part))]
        line_loads.append(pltpu.make_async_copy(source, zown.at[g], load_sem.at[g]))
    for g in range(turned, outer):
        source = gd_ref.at[
            (g - turned) // per_source, cut((g - turned) % per_source, chunk)
        ]
        line_loads.append(pltpu.make_async_copy(source, zown.at[g], load_sem.at[g]))
    for load in line_loads:
        load.start()
    partials = (pw_ref, pn_ref, po_ref)
    loads = [
        [
            pltpu.make_async_copy(p.at[block], own.at[m, i], local_sem.at[4 * m + i])
            for i, block in enumerate(mine)
        ]
        for m, p in enumerate(partials)
    ]
    for part in loads:
        for load in part:
            load.start()
    meet_all(n, depth)

    def copy(m, k, src, dst, partner):
        return remote(src, dst, send_sem.at[m, k], recv_sem.at[m, k], partner)

    twins = [
        [
            copy(m, i, p.at[block + twin], twin_in.at[m, i], me + twin)
            for i, block in enumerate(mine)
        ]
        for m, p in enumerate(partials)
    ]
    sends = [
        [
            copy(m, 4, own.at[m, 0, low], held.at[m, 0], near_x),
            copy(m, 5, own.at[m, 0, high], held.at[m, 1], near_y),
            copy(m, 6, own.at[m, 1, low], held.at[m, 2], near_x),
            copy(m, 7, own.at[m, 2, high], held.at[m, 3], near_y),
            copy(m, 8, own.at[m, 1, high], held.at[m, 4], near_x),
            copy(m, 9, own.at[m, 2, low], held.at[m, 5], near_y),
        ]
        for m in range(3)
    ]
    for part in twins:
        for send in part:
            send.start()

    def add_twin(m, i):
        loads[m][i].wait()
        twins[m][i].wait_recv()

        @pl.loop(0, rows // STEP)
        def _(r):
            at = cut(r, STEP)
            own[m, i, at] = (
                own[m, i, at].astype(F32) + twin_in[m, i, at].astype(F32)
            ).astype(BF16)

    def add_held(m, i, base, slot):
        @pl.loop(0, half // STEP)
        def _(r):
            at = cut(r, STEP)
            to = pl.ds(pl.multiple_of(base + r * STEP, STEP), STEP)
            own[m, i, to] = (
                own[m, i, to].astype(F32) + held[m, slot, at].astype(F32)
            ).astype(BF16)

    def first(m):
        add_twin(m, 0)
        sends[m][0].start()
        sends[m][1].start()
        add_twin(m, 1)
        sends[m][2].start()
        add_twin(m, 2)
        sends[m][3].start()

    def second(m):
        sends[m][1].wait_recv()
        add_held(m, 1, half, 1)
        sends[m][4].start()
        sends[m][0].wait_recv()
        add_held(m, 2, 0, 0)
        sends[m][5].start()

    def last(m, store):
        loads[m][3].wait()
        twins[m][3].wait_recv()
        for k in (2, 3, 4, 5):
            sends[m][k].wait_recv()
        for base, one, two in ((0, 2, 5), (half, 3, 4)):

            @pl.loop(0, half // STEP)
            def _(r):
                at = cut(r, STEP)
                place = base + r * STEP
                to = pl.ds(pl.multiple_of(place, STEP), STEP)
                store(
                    place,
                    to,
                    own[m, 3, to].astype(F32)
                    + twin_in[m, 3, to].astype(F32)
                    + held[m, one, at].astype(F32)
                    + held[m, two, at].astype(F32),
                )

    def store_line(place, to, value):
        value = value.astype(BF16)
        for side in range(across_width):
            zown[
                outer + (place // chunk) * across_width + side,
                pl.ds(pl.multiple_of(lax.rem(place, chunk), STEP), STEP),
            ] = value[:, side * cols : (side + 1) * cols]

    def store_inputs(place, to, value):
        normal, scale = norm_parts(x_ref[to].astype(F32))
        part, gain_part = norm_back(value, normal, scale, ga_ref[...])
        gi_ref[to] = grad_ref[to] + part
        gain_here[0:1] = gain_here[0:1] + gain_part[None]

    def store_outputs(place, to, value):
        out_ref[to] = (mid_ref[to] + value).astype(BF16)

    def home(part):
        block = part * n + me
        return block // 3, lax.rem(block, 3)

    def deliver_far(g):
        target, slot = home(g // per_part)
        piece = lax.rem(g, per_part)
        return remote(
            zin.at[g],
            oq_ref.at[(slot, *wide(piece))],
            home_send.at[g],
            home_recv.at[slot, piece],
            target,
        )

    def deliver_near(g):
        _, slot = home(g // per_part)
        return pltpu.make_async_copy(
            zin.at[g], oq_ref.at[(slot, *wide(lax.rem(g, per_part)))], keep_sem.at[g]
        )

    def widen(g):
        @pl.loop(0, chunk // STEP)
        def _(r):
            at = cut(r, STEP)
            stage[at] = zin[g, at].astype(F32)

    def deliver(g):
        target, _ = home(g // per_part)

        @pl.when((g < turned) & (target != me))
        def _():
            deliver_far(g).start()

        @pl.when((g < turned) & (target == me))
        def _():
            deliver_near(g).start()

        @pl.when((g >= turned) & (g < outer))
        def _():
            widen(g)
            at = g - turned
            place = cut(lax.rem(at, per_source), chunk), cut(at // per_source, cols)
            store = pltpu.make_async_copy(stage, od_ref.at[place], stage_sem)
            store.start()
            store.wait()

        @pl.when(g >= outer)
        def _():
            widen(g)
            store = pltpu.make_async_copy(
                stage, ow_ref.at[wide(g - outer)], stage_sem
            )
            store.start()
            store.wait()

    def delivered(g):
        target, _ = home(g // per_part)

        @pl.when(target != me)
        def _():
            deliver_far(g).wait_send()

        @pl.when(target == me)
        def _():
            deliver_near(g).wait()

    def go_up(g, ahead):
        return line_remote(zown.at[g], zin.at[g], up_send.at[g], up_recv.at[g], ahead)

    def go_down(g, behind):
        return line_remote(
            zin.at[g], zin.at[g], down_send.at[g], down_recv.at[g], behind
        )

    def ranks(side):
        if side == 0:
            return z, z + 1, z - 1
        return depth - 1 - z, z - 1, z + 1

    def add_line(g, target):
        @pl.loop(0, chunk // STEP)
        def _(r):
            at = cut(r, STEP)
            target[g, at] = (zown[g, at].astype(F32) + zin[g, at].astype(F32)).astype(
                BF16
            )

    lead = 1
    far = 2 * (depth - 1)
    steps = per_side + 2 * far

    def line_enter(c):
        for side in (0, 1):
            rank, ahead, _ = ranks(side)

            @pl.when(rank == 0)
            def _():
                go_up(2 * c + side, ahead).start()

    def line_step(t):
        @pl.when(t + lead < per_side)
        def _():
            line_enter(t + lead)

        back = []
        for side in (0, 1):
            rank, ahead, behind = ranks(side)
            c_back = t - 2 * far + 2 * rank
            g_back = 2 * c_back + side
            there = (c_back >= 0) & (c_back < per_side) & (rank < depth - 1)
            back.append((there, g_back))

            @pl.when(there)
            def _():
                go_down(g_back, ahead).wait_recv()

            @pl.when(there & (rank > 0))
            def _():
                go_down(g_back, behind).start()

        for side in (0, 1):
            rank, ahead, behind = ranks(side)
            c = t - 2 * rank
            g = 2 * c + side
            there = (c >= 0) & (c < per_side)

            @pl.when(there & (rank > 0) & (rank < depth - 1))
            def _():
                go_up(g, behind).wait_recv()
                add_line(g, zown)
                go_up(g, ahead).start()

            @pl.when(there & (rank == depth - 1))
            def _():
                go_up(g, behind).wait_recv()
                add_line(g, zin)
                go_down(g, behind).start()
                deliver(g)

        for there, g_back in back:

            @pl.when(there)
            def _():
                deliver(g_back)

    def line_steps(first_step, last_step):
        @pl.loop(first_step, last_step)
        def _(t):
            line_step(t)

    gain_here[...] = jnp.zeros_like(gain_here)
    for load in line_loads[:turned]:
        load.wait()
    for c in range(lead):
        line_enter(c)
    line_steps(0, 3)
    first(0)
    for load in line_loads[turned:]:
        load.wait()
    line_steps(3, 10)
    second(0)
    line_steps(10, 11)
    first(1)
    line_steps(11, 20)
    last(0, store_line)
    line_steps(20, 22)
    second(1)
    line_steps(22, 23)
    first(2)
    line_steps(23, 29)
    last(1, store_inputs)

    gain_here[1:2] = gm_ref[...]
    gain_here[2:3] = gf_ref[...]
    gain_here[3:4, 0 : gh_ref.shape[1]] = gh_ref[...]
    gain_row[me] = gain_here[...]
    rounds = [
        remote(
            gain_here,
            gain_row.at[me],
            gain_send.at[0, k],
            gain_recv.at[0, k],
            lax.rem(me + k, n),
        )
        for k in range(1, n)
    ]
    for send in rounds:
        send.start()
    line_steps(29, 33)
    second(2)
    line_steps(33, 41)
    last(2, store_outputs)
    line_steps(41, 42)
    for send in rounds:
        send.wait()
    total = gain_row[0]
    for d in range(1, n):
        total = total + gain_row[d]
    gain_pack[0:8] = total
    for d in range(n):
        gain_pack[8 + d : 9 + d] = gain_row[d, 3:4]
    gain_line[z] = gain_pack[...]
    rounds = [
        line_remote(
            gain_pack,
            gain_line.at[z],
            gain_send.at[1, k],
            gain_recv.at[1, k],
            lax.rem(z + k, depth),
        )
        for k in range(1, depth)
    ]
    for send in rounds:
        send.start()
    line_steps(42, steps)
    for send in rounds:
        send.wait()
    total = gain_line[0]
    for d in range(1, depth):
        total = total + gain_line[d]
    sums_ref[...] = total

    for m in range(3):
        for send in twins[m] + sends[m]:
            send.wait_send()
    for g in range(chunks):
        rank, ahead, behind = ranks(g % 2)

        @pl.when(rank < depth - 1)
        def _():
            go_up(g, ahead).wait_send()

        @pl.when(rank > 0)
        def _():
            go_down(g, behind).wait_send()

    for g in range(turned):
        delivered(g)
    for slot in range(3):
        block = 3 * me + slot
        source = lax.rem(block, n)

        @pl.when(source != me)
        def _():
            for piece in range(per_part):
                remote(
                    zin.at[0],
                    oq_ref.at[(slot, *wide(piece))],
                    home_send.at[0],
                    home_recv.at[slot, piece],
                    source,
                ).wait_recv()


def finish(
    grad_qkv, grad_down, part_out, part_normed, part_outputs, x, grad_middle, middle, gain, gains, collective_id
):
    n, depth = lax.axis_size("seq"), lax.axis_size("batch")
    rows, width = part_out.shape[0] // n, part_out.shape[1]
    cols = grad_qkv.shape[1]
    sources, _, feats = grad_down.shape
    if n != 8 or depth != 4:
        me = lax.axis_index("seq")
        blocks = lax.psum(grad_qkv, "batch")
        back = [
            lax.ppermute(
                give_part(blocks, me, n, j),
                "seq",
                [((3 * d + j) % n, d) for d in range(n)],
            )
            for j in range(3)
        ]
        w_out = lax.psum(scatter_seq(part_out).astype(BF16), "batch")
        normal, scale = norm_parts(x.astype(F32))
        part, gain_part = norm_back(scatter_seq(part_normed), normal, scale, gain)
        shared = [lax.psum(g, ("batch", "seq")) for g in (gain_part, gains[0][0], gains[1][0])]
        hidden = lax.all_gather(lax.psum(gains[2][0], "batch"), "seq", axis=0, tiled=True)
        down = lax.psum(grad_down, "batch")
        return (
            jnp.concatenate(back, axis=0),
            jnp.swapaxes(down, 0, 1).reshape(rows, sources * feats).astype(F32),
            w_out.astype(F32),
            grad_middle + part,
            (middle + scatter_seq(part_outputs)).astype(BF16),
            (*shared, hidden),
        )
    chunks = (
        3 * cols * width + rows * width + sources * rows * feats
    ) // (CHUNK * feats)
    dma = pltpu.SemaphoreType.DMA
    line = pltpu.VMEM((chunks, CHUNK, feats), BF16)
    w_qkv, w_down, w_out, grad_inputs, outputs, sums = pl.pallas_call(
        functools.partial(finish_kernel, n, depth),
        out_shape=(
            jax.ShapeDtypeStruct((3, cols, width), BF16),
            jax.ShapeDtypeStruct((rows, sources * feats), F32),
            jax.ShapeDtypeStruct((rows, width), F32),
            jax.ShapeDtypeStruct((rows, width), F32),
            jax.ShapeDtypeStruct((rows, width), BF16),
            jax.ShapeDtypeStruct((16, width), F32),
        ),
        in_specs=[ANY] * 5 + [INSIDE] * 7,
        out_specs=(ANY, ANY, ANY, INSIDE, INSIDE, INSIDE),
        scratch_shapes=[
            pltpu.VMEM((3, 4, rows, width), BF16),
            pltpu.VMEM((3, 4, rows, width), BF16),
            pltpu.VMEM((3, 6, rows // 2, width), BF16),
            line,
            line,
            pltpu.VMEM((CHUNK, feats), F32),
            pltpu.VMEM((8, width), F32),
            pltpu.VMEM((n, 8, width), F32),
            pltpu.VMEM((16, width), F32),
            pltpu.VMEM((depth, 16, width), F32),
            dma((12,)),
            dma((chunks,)),
            dma,
            dma((3, 10)),
            dma((3, 10)),
            dma((chunks,)),
            dma((chunks,)),
            dma((chunks,)),
            dma((chunks,)),
            dma((chunks,)),
            dma((chunks,)),
            dma((3, cols * width // (CHUNK * feats))),
            dma((2, n)),
            dma((2, n)),
        ],
        compiler_params=pltpu.CompilerParams(
            collective_id=collective_id,
            has_side_effects=True,
            vmem_limit_bytes=VMEM_LIMIT,
        ),
        name="finish",
    )(
        grad_qkv,
        grad_down,
        *[p.reshape(n, rows, width) for p in (part_out, part_normed, part_outputs)],
        x,
        grad_middle,
        middle,
        gain[None],
        *gains,
    )
    return (
        w_qkv.reshape(3 * cols, width),
        w_down,
        w_out,
        grad_inputs,
        outputs,
        (sums[0], sums[1], sums[2], sums[8:, :feats].reshape(-1)),
    )


def widen_kernel(*refs):
    half = len(refs) // 2
    for source, target in zip(refs[:half], refs[half:], strict=True):
        target[...] = source[...].astype(F32)


def widen(arrays):
    steps = 8
    specs = [pl.BlockSpec((x.shape[0] // steps, x.shape[1]), lambda i: (i, 0)) for x in arrays]
    return pl.pallas_call(
        widen_kernel,
        grid=(steps,),
        out_shape=[jax.ShapeDtypeStruct(x.shape, F32) for x in arrays],
        in_specs=specs,
        out_specs=specs,
        compiler_params=pltpu.CompilerParams(vmem_limit_bytes=VMEM_LIMIT),
        name="widen",
    )(*arrays)


def body(
    inputs,
    segment_ids,
    w_qkv,
    w_out,
    w_up,
    w_down,
    gain_attn,
    gain_mix,
    gain_ffn,
    gain_hidden,
    cotangent,
):
    _, local, width = inputs.shape
    n, depth = lax.axis_size("seq"), lax.axis_size("batch")
    me = lax.axis_index("seq")
    length = local * n
    feats = w_up.shape[0]
    x_low = inputs[0]
    cot = cotangent[0]
    segment = segment_ids[0]

    w_out_full = lax.all_gather(w_out, "seq", axis=0, tiled=True)
    before = [jnp.sum((segment < d).astype(jnp.int32)) for d in range(1, DOCS)]
    start = jnp.zeros_like(segment)
    for d in range(1, DOCS):
        start = jnp.where(segment == d, before[d - 1], start)
    positions = jnp.arange(length, dtype=jnp.int32) - start
    first = start[::TILE] // TILE
    start_row = start[None, :]

    normed_full, w_heads, w_down_cols, tables = start_exchange(
        x_low, gain_attn, w_qkv, w_down, positions.astype(F32), 1
    )
    cot_late, _ = lax.optimization_barrier((cot, w_heads))
    cot_full = lax.all_gather(cot_late, "seq", axis=0, tiled=True)

    q, k, v, kt, vt = project_qkv(normed_full, w_heads, tables)
    attended_heads, lse = attend(first, start_row, q, k, vt)
    attended = heads_to_tokens(attended_heads, 2)
    mix_in, middle, ffn_in = mix_pass(attended, x_low, w_out_full, gain_mix, gain_ffn)
    gain_here = lax.dynamic_slice_in_dim(gain_hidden, me * feats, feats, 0)[None, :]
    ffn_full, hidden, grad_upper, grad_gain_here = ffn_pass(
        ffn_in, w_up, cot_full, w_down_cols, gain_here, 3
    )

    grad_w_up = tn(grad_upper, ffn_full).astype(BF16)
    grad_upper, grad_w_up = lax.optimization_barrier((grad_upper, grad_w_up))
    grad_w_up = lax.psum(grad_w_up, "batch")
    part_outputs, grad_w_down, grad_middle, grad_branch, grad_gain_ffn = ffn_back(
        grad_upper, w_up, hidden, w_down_cols, cot_full, middle, cot, gain_ffn, 4
    )
    grad_att, grad_gain_mix = branch_pass(grad_branch, attended, w_out_full, gain_mix)
    grad_heads = tokens_to_heads(grad_att, 5)
    grad_w_down, grad_heads = lax.optimization_barrier((grad_w_down, grad_heads))
    grad_w_down = lax.all_to_all(grad_w_down, "seq", split_axis=0, concat_axis=0, tiled=True)
    grads = attend_back(
        first, start_row, q, k, kt, v, attended_heads, lse, grad_heads, tables
    )
    grad_w_qkv = tn(grads, normed_full).astype(BF16).reshape(3, -1, width)
    grad_w_qkv, grad_w_up = lax.optimization_barrier((grad_w_qkv, grad_w_up))
    grad_w_qkv, grad_w_down, grad_w_out, grad_inputs, outputs, gains = finish(
        grad_w_qkv,
        grad_w_down,
        tn(grad_branch, mix_in).astype(BF16),
        nn(grads, w_heads).astype(BF16),
        part_outputs,
        x_low,
        grad_middle,
        middle,
        gain_attn,
        (grad_gain_mix, grad_gain_ffn, grad_gain_here),
        6,
    )
    grad_w_qkv, grad_w_up = widen([grad_w_qkv, grad_w_up])
    return (
        outputs[None],
        grad_inputs[None],
        grad_w_qkv,
        grad_w_out,
        grad_w_up,
        grad_w_down,
        *gains,
    )


def pick_part(turned, me, n, part):
    chosen = turned[0]
    home = part * n + me
    for j in (1, 2):
        chosen = jnp.where(lax.rem(home, 3) == j, turned[j], chosen)
    return chosen


def give_part(blocks, me, n, j):
    chosen = blocks[0]
    for part in (1, 2):
        chosen = jnp.where(lax.rem(part * n + me, 3) == j, blocks[part], chosen)
    return chosen


def solution(mesh):
    in_specs = (
        P("batch", "seq", None),
        P("batch", None),
        P("seq", None),
        P("seq", None),
        P("seq", None),
        P("seq", None),
        P(),
        P(),
        P(),
        P(),
        P("batch", "seq", None),
    )
    out_specs = (
        P("batch", "seq", None),
        P("batch", "seq", None),
        P("seq", None),
        P("seq", None),
        P("seq", None),
        P("seq", None),
        P(),
        P(),
        P(),
        P(),
    )
    return jax.shard_map(body, mesh=mesh, in_specs=in_specs, out_specs=out_specs, check_vma=False)
```

```python
import functools
import math

import jax
import jax.numpy as jnp
from jax import lax
from jax.experimental import pallas as pl
from jax.experimental.pallas import tpu as pltpu
from jax.sharding import PartitionSpec as P

HEADS = 32
HEAD_DIM = 64
LENGTH = 2048
XBASE = 512
DOCS = 4
EPSILON = 1e-05
MASKED = -1e30
TILE = 256
STEP = 32
VMEM_LIMIT = 60 * 1024 * 1024

MESH = pl.DeviceIdType.MESH
F32 = jnp.float32
BF16 = jnp.bfloat16
ANY = pl.BlockSpec(memory_space=pl.ANY)
INSIDE = pl.BlockSpec(memory_space=pltpu.VMEM)


def nn(a, b):
    return lax.dot_general(a, b, (((1,), (0,)), ((), ())), preferred_element_type=F32)


def nt(a, b):
    return lax.dot_general(a, b, (((1,), (1,)), ((), ())), preferred_element_type=F32)


def tn(a, b):
    return lax.dot_general(a, b, (((0,), (0,)), ((), ())), preferred_element_type=F32)


def norm_parts(values):
    average = jnp.mean(values, axis=-1, keepdims=True)
    centered = values - average
    spread = jnp.mean(centered * centered, axis=-1, keepdims=True)
    scale = lax.rsqrt(spread + EPSILON)
    return centered * scale, scale


def norm_back(grad, normal, scale, gain):
    part = grad * gain
    inner = (
        part
        - jnp.mean(part, axis=-1, keepdims=True)
        - normal * jnp.mean(part * normal, axis=-1, keepdims=True)
    )
    return scale * inner, jnp.sum(grad * normal, axis=0)


def places():
    me = lax.axis_index("seq")
    core = lax.rem(me, 2)
    along_x = lax.rem(me // 2, 2)
    along_y = me // 4
    twin = 1 - 2 * core
    near_x = me + 2 - 4 * along_x
    near_y = me + 4 - 8 * along_y
    across = near_x + 4 - 8 * along_y
    return me, twin, near_x, near_y, across


def remote(src, dst, send_sem, recv_sem, partner):
    return pltpu.make_async_remote_copy(
        src_ref=src,
        dst_ref=dst,
        send_sem=send_sem,
        recv_sem=recv_sem,
        device_id={"seq": partner},
        device_id_type=MESH,
    )


def meet(partners):
    barrier = pltpu.get_barrier_semaphore()
    for partner in partners:
        pl.semaphore_signal(
            barrier, inc=1, device_id={"seq": partner}, device_id_type=MESH
        )
    pl.semaphore_wait(barrier, len(partners))


def gather_copies(x_ref, o_ref, send_sem, recv_sem):
    me, twin, near_x, near_y, across = places()
    half = x_ref.shape[0] // 2
    low, high = pl.ds(0, half), pl.ds(half, half)

    def copy(k, src, dst, partner):
        return remote(src, dst, send_sem.at[k], recv_sem.at[k], partner)

    def relay(k, owner, rows, partner):
        place = o_ref.at[owner, rows]
        return copy(k, place, place, partner)

    return [
        copy(0, x_ref.at[low], o_ref.at[me, low], near_x),
        copy(1, x_ref.at[high], o_ref.at[me, high], near_y),
        copy(2, x_ref.at[high], o_ref.at[me, high], near_x),
        copy(3, x_ref.at[low], o_ref.at[me, low], near_y),
        copy(4, x_ref, o_ref.at[me], me + twin),
        relay(5, near_x, low, near_y),
        relay(6, near_y, high, near_x),
        relay(7, near_x, low, me + twin),
        relay(8, near_y, high, me + twin),
        relay(9, near_x, high, me + twin),
        relay(10, near_y, low, me + twin),
        relay(11, across, low, me + twin),
        relay(12, across, high, me + twin),
    ]


def gather_run(sends, *between):
    between = (*between, *([None] * 3))[:3]

    def pause(i):
        if between[i] is not None:
            between[i]()

    sends[0].wait_recv()
    sends[5].start()
    sends[7].start()
    sends[1].wait_recv()
    sends[6].start()
    sends[8].start()
    pause(0)
    sends[2].wait_recv()
    sends[9].start()
    sends[3].wait_recv()
    sends[10].start()
    pause(1)
    sends[5].wait_recv()
    sends[11].start()
    sends[6].wait_recv()
    sends[12].start()
    pause(2)
    for k in (4, 7, 8, 9, 10, 11, 12):
        sends[k].wait_recv()
    for send in sends:
        send.wait_send()


def meet_all(n, depth):
    me = lax.axis_index("seq")
    z = lax.axis_index("batch")
    barrier = pltpu.get_barrier_semaphore()
    for k in range(1, n):
        pl.semaphore_signal(
            barrier, inc=1, device_id={"seq": lax.rem(me + k, n)}, device_id_type=MESH
        )
    for k in range(1, depth):
        pl.semaphore_signal(
            barrier,
            inc=1,
            device_id={"batch": lax.rem(z + k, depth)},
            device_id_type=MESH,
        )
    pl.semaphore_wait(barrier, n + depth - 2)


def line_remote(src, dst, send_sem, recv_sem, partner):
    return pltpu.make_async_remote_copy(
        src_ref=src,
        dst_ref=dst,
        send_sem=send_sem,
        recv_sem=recv_sem,
        device_id={"batch": partner},
        device_id_type=MESH,
    )


class Line:
    def __init__(self, depth, source, target, send_sem, recv_sem):
        self.depth, self.source, self.target = depth, source, target
        self.send_sem, self.recv_sem = send_sem, recv_sem
        self.z = lax.axis_index("batch")

    def message(self, side, k):
        sign = 2 * side - 1
        owner = self.z - sign * k
        return line_remote(
            self.source(owner, k),
            self.target(owner),
            self.send_sem.at[side, k],
            self.recv_sem.at[side, k],
            self.z + sign,
        )

    def sends(self, side, k):
        sign = 2 * side - 1
        owner, target = self.z - sign * k, self.z + sign
        inside = (owner >= 0) & (owner < self.depth)
        return inside & (target >= 0) & (target < self.depth)

    def land(self, k):
        for side in (0, 1):
            sign = 2 * side - 1
            owner = self.z - sign * (k + 1)

            @pl.when((owner >= 0) & (owner < self.depth))
            def _():
                place = self.target(owner)
                line_remote(
                    place,
                    place,
                    self.send_sem.at[side, k],
                    self.recv_sem.at[side, k],
                    self.z - sign,
                ).wait_recv()

    def start(self, k):
        for side in (0, 1):

            @pl.when(self.sends(side, k))
            def _():
                self.message(side, k).start()

    def sent(self, k):
        for side in (0, 1):

            @pl.when(self.sends(side, k))
            def _():
                self.message(side, k).wait_send()


def lane_tables(place):
    half = HEAD_DIM // 2
    lane = lax.broadcasted_iota(jnp.int32, (1, 128), 1)
    channel = lax.rem(lane, half).astype(F32)
    inverse = jnp.exp(channel * (-math.log(10000.0) / half))
    zeta = (channel * (2.0 / HEAD_DIM) + 0.4) / 1.4
    sign = jnp.where(lax.rem(lane, HEAD_DIM) < half, -1.0, 1.0)
    angle = place * inverse
    growth = jnp.exp((place - 0.5 * LENGTH) * (1.0 / XBASE) * jnp.log(zeta))
    shrink = 1.0 / growth
    cosine = jnp.cos(angle)
    sine = jnp.sin(angle) * sign
    return cosine * growth, sine * growth, cosine * shrink, sine * shrink


def start_kernel(
    n, depth, x_ref, gain_ref, w_ref, wd_ref, pos_ref,
    o_ref, wt_ref, wc_ref, cq_ref, sq_ref, ck_ref, sk_ref,
    normed, keep_w, keep_c, local_sem, send_sem, recv_sem, hop_send, hop_recv, col_send, col_recv,
    line_send, line_recv,
):
    z = lax.axis_index("batch")
    rows_z = wc_ref.shape[2]
    cols = wc_ref.shape[3]
    me, twin, near_x, near_y, _ = places()
    own = pltpu.make_async_copy(normed, o_ref.at[me], local_sem.at[0])
    wd_rows = pl.ds(pl.multiple_of(z * rows_z, rows_z), rows_z)

    def column(k):
        return wd_ref.at[wd_rows, pl.ds(pl.multiple_of(k * cols, cols), cols)]

    load_column = pltpu.make_async_copy(column(me), keep_c, local_sem.at[4])
    own_column = pltpu.make_async_copy(keep_c, wc_ref.at[me, z], local_sem.at[5])
    load_column.start()
    meet_all(n, depth)
    load_column.wait()
    own_column.start()

    def hop(j, part, target):
        return remote(
            w_ref.at[j], wt_ref.at[part], hop_send.at[j], hop_recv.at[part], target
        )

    def load(j):
        return pltpu.make_async_copy(w_ref.at[j], keep_w, local_sem.at[6])

    def here(j, part):
        return pltpu.make_async_copy(keep_w, wt_ref.at[part], local_sem.at[1 + j])

    turns = [
        remote(
            column(lax.rem(me + k, n)),
            wc_ref.at[me, z],
            col_send.at[k],
            col_recv.at[k],
            lax.rem(me + k, n),
        )
        for k in range(1, n)
    ]
    for turn in turns:
        turn.start()

    @pl.loop(0, x_ref.shape[0] // STEP)
    def _(r):
        at = pl.ds(pl.multiple_of(r * STEP, STEP), STEP)
        normal, _ = norm_parts(x_ref[at].astype(F32))
        normed[at] = (normal * gain_ref[...]).astype(BF16)

    own.start()
    sends = gather_copies(normed, o_ref, send_sem, recv_sem)
    for k in range(5):
        sends[k].start()
    for j in range(3):
        block = 3 * me + j
        target = lax.rem(block, n)
        for part in range(3):
            inside = block // n == part

            @pl.when(inside & (target != me))
            def _():
                hop(j, part, target).start()

            @pl.when(inside & (target == me))
            def _():
                load(j).start()

    line = Line(
        depth,
        lambda owner, k: wc_ref.at[:, owner],
        lambda owner: wc_ref.at[:, owner],
        line_send,
        line_recv,
    )

    own_column.wait()
    for turn in turns:
        turn.wait_recv()
    line.start(0)
    for j in range(3):
        block = 3 * me + j
        target = lax.rem(block, n)
        for part in range(3):

            @pl.when((block // n == part) & (target == me))
            def _():
                load(j).wait()
                here(j, part).start()

    @pl.loop(0, pos_ref.shape[0])
    def _(r):
        at = pl.ds(pl.multiple_of(r * 128, 128), 128)
        places_here = jnp.broadcast_to(pos_ref[pl.ds(r, 1), :], (128, 128)).T
        tables = lane_tables(places_here)
        for ref, table in zip((cq_ref, sq_ref, ck_ref, sk_ref), tables, strict=True):
            ref[at] = table

    def hand_on(k):
        def step():
            line.land(k - 1)
            line.start(k)

        return step

    hand_on(1)()
    gather_run(sends, *[hand_on(k) for k in range(2, depth - 1)])
    line.land(depth - 2)
    for k in range(depth - 1):
        line.sent(k)
    for turn in turns:
        turn.wait_send()
    for j in range(3):
        block = 3 * me + j
        target = lax.rem(block, n)
        for part in range(3):
            inside = block // n == part

            @pl.when(inside & (target != me))
            def _():
                hop(j, part, target).wait_send()

            @pl.when(inside & (target == me))
            def _():
                here(j, part).wait()

    for part in range(3):
        source = (part * n + me) // 3

        @pl.when(source != me)
        def _():
            hop(0, part, source).wait_recv()

    own.wait()


def start_exchange(block, gain, w_qkv, w_down, positions, collective_id):
    n, depth = lax.axis_size("seq"), lax.axis_size("batch")
    rows, width = block.shape
    piece = w_qkv.shape[0] // 3
    w = w_qkv.reshape(3, piece, width)
    if n != 8:
        me = lax.axis_index("seq")
        turned = [
            lax.ppermute(w[j], "seq", [(d, (3 * d + j) % n) for d in range(n)])
            for j in range(3)
        ]
        parts = [pick_part(turned, me, n, part) for part in range(3)]
        place = jnp.broadcast_to(positions[:, None], (positions.shape[0], 128))
        normed = (norm_parts(block.astype(F32))[0] * gain).astype(BF16)
        return (
            lax.all_gather(normed, "seq", axis=0, tiled=True),
            jnp.concatenate(parts, axis=0),
            lax.all_to_all(w_down, "seq", split_axis=1, concat_axis=0, tiled=True),
            lane_tables(place),
        )
    rows_z, cols = w_down.shape[0] // depth, w_down.shape[1] // n
    inside = pl.BlockSpec(memory_space=pltpu.VMEM)
    table = jax.ShapeDtypeStruct((n * rows, 128), F32)
    gathered, turned, columns, *tables = pl.pallas_call(
        functools.partial(start_kernel, n, depth),
        out_shape=(
            jax.ShapeDtypeStruct((n, rows, width), block.dtype),
            jax.ShapeDtypeStruct((3, piece, width), w.dtype),
            jax.ShapeDtypeStruct((n, depth, rows_z, cols), w_down.dtype),
            *([table] * 4),
        ),
        in_specs=[INSIDE, INSIDE, ANY, ANY, INSIDE],
        out_specs=(ANY, ANY, ANY, *([INSIDE] * 4)),
        scratch_shapes=[
            pltpu.VMEM((rows, width), BF16),
            pltpu.VMEM((piece, width), BF16),
            pltpu.VMEM((rows_z, cols), BF16),
            pltpu.SemaphoreType.DMA((7,)),
            pltpu.SemaphoreType.DMA((13,)),
            pltpu.SemaphoreType.DMA((13,)),
            pltpu.SemaphoreType.DMA((3,)),
            pltpu.SemaphoreType.DMA((3,)),
            pltpu.SemaphoreType.DMA((n,)),
            pltpu.SemaphoreType.DMA((n,)),
            pltpu.SemaphoreType.DMA((2, depth)),
            pltpu.SemaphoreType.DMA((2, depth)),
        ],
        compiler_params=pltpu.CompilerParams(
            collective_id=collective_id, has_side_effects=True, vmem_limit_bytes=VMEM_LIMIT
        ),
        name="start_exchange",
    )(block, gain[None], w, w_down, positions.reshape(-1, 128))
    return (
        gathered.reshape(n * rows, width),
        turned.reshape(3 * piece, width),
        columns.reshape(-1, cols),
        tables,
    )


def scatter_seq(partial):
    return lax.psum_scatter(partial, "seq", scatter_dimension=0, tiled=True).astype(F32)


def heads_to_tokens_kernel(n, x_ref, o_ref, keep, local_sem, send_sem, recv_sem):
    me = lax.axis_index("seq")
    rows = o_ref.shape[0]
    cols = x_ref.shape[1]
    exchange(
        n,
        me,
        lambda k: x_ref.at[pl.ds(pl.multiple_of(k * rows, rows), rows)],
        o_ref.at[:, pl.ds(pl.multiple_of(me * cols, cols), cols)],
        keep,
        local_sem,
        send_sem,
        recv_sem,
    )


def exchange(n, me, source, target, keep, local_sem, send_sem, recv_sem):
    load = pltpu.make_async_copy(source(me), keep, local_sem.at[0])
    own = pltpu.make_async_copy(keep, target, local_sem.at[1])
    load.start()
    barrier = pltpu.get_barrier_semaphore()
    for k in range(1, n):
        pl.semaphore_signal(
            barrier,
            inc=1,
            device_id={"seq": lax.rem(me + k, n)},
            device_id_type=MESH,
        )
    pl.semaphore_wait(barrier, n - 1)
    copies = []
    for k in range(1, n):
        partner = lax.rem(me + k, n)
        copies.append(
            pltpu.make_async_remote_copy(
                src_ref=source(partner),
                dst_ref=target,
                send_sem=send_sem.at[k],
                recv_sem=recv_sem.at[k],
                device_id={"seq": partner},
                device_id_type=MESH,
            )
        )
        copies[-1].start()
    load.wait()
    own.start()
    for copy in copies:
        copy.wait()
    own.wait()


def heads_to_tokens(heads, collective_id):
    n = lax.axis_size("seq")
    total, cols = heads.shape
    rows = total // n
    return pl.pallas_call(
        functools.partial(heads_to_tokens_kernel, n),
        out_shape=jax.ShapeDtypeStruct((rows, n * cols), heads.dtype),
        in_specs=[ANY],
        out_specs=ANY,
        scratch_shapes=[
            pltpu.VMEM((rows, cols), heads.dtype),
            pltpu.SemaphoreType.DMA((2,)),
            pltpu.SemaphoreType.DMA((n,)),
            pltpu.SemaphoreType.DMA((n,)),
        ],
        compiler_params=pltpu.CompilerParams(
            collective_id=collective_id, has_side_effects=True, vmem_limit_bytes=VMEM_LIMIT
        ),
        name="heads_to_tokens",
    )(heads)


def tokens_to_heads_kernel(n, x_ref, o_ref, keep, local_sem, send_sem, recv_sem):
    me = lax.axis_index("seq")
    rows = x_ref.shape[0]
    cols = o_ref.shape[1]
    exchange(
        n,
        me,
        lambda k: x_ref.at[:, pl.ds(pl.multiple_of(k * cols, cols), cols)],
        o_ref.at[pl.ds(pl.multiple_of(me * rows, rows), rows)],
        keep,
        local_sem,
        send_sem,
        recv_sem,
    )


def tokens_to_heads(tokens, collective_id):
    n = lax.axis_size("seq")
    rows, total = tokens.shape
    return pl.pallas_call(
        functools.partial(tokens_to_heads_kernel, n),
        out_shape=jax.ShapeDtypeStruct((rows * n, total // n), tokens.dtype),
        in_specs=[ANY],
        out_specs=ANY,
        scratch_shapes=[
            pltpu.VMEM((rows, total // n), tokens.dtype),
            pltpu.SemaphoreType.DMA((2,)),
            pltpu.SemaphoreType.DMA((n,)),
            pltpu.SemaphoreType.DMA((n,)),
        ],
        compiler_params=pltpu.CompilerParams(
            collective_id=collective_id, has_side_effects=True, vmem_limit_bytes=VMEM_LIMIT
        ),
        name="tokens_to_heads",
    )(tokens)


def swap_halves(values):
    width = values.shape[-1]
    half = HEAD_DIM // 2
    lane = lax.broadcasted_iota(jnp.int32, values.shape, 1)
    ahead = pltpu.roll(values, width - half, 1)
    behind = pltpu.roll(values, half, 1)
    return jnp.where(lane % HEAD_DIM < half, ahead, behind)


def spread_lanes(table, width):
    return jnp.concatenate([table] * (width // table.shape[-1]), axis=-1)


def qkv_kernel(
    x_ref, w_ref, cq_ref, sq_ref, ck_ref, sk_ref,
    q_ref, k_ref, v_ref, kt_ref, vt_ref,
):
    x = x_ref[...]
    width = q_ref.shape[1]
    query = nt(x, w_ref[0:width])
    query = query * spread_lanes(cq_ref[...], width) + swap_halves(
        query
    ) * spread_lanes(sq_ref[...], width)
    q_ref[...] = query.astype(BF16) * (HEAD_DIM**-0.5)
    keys = nt(x, w_ref[width : 2 * width])
    keys = keys * spread_lanes(ck_ref[...], width) + swap_halves(
        keys
    ) * spread_lanes(sk_ref[...], width)
    k_ref[...] = keys.astype(BF16)
    kt_ref[...] = keys.T.astype(BF16)
    values = nt(x, w_ref[2 * width :])
    v_ref[...] = values.astype(BF16)
    vt_ref[...] = values.T.astype(BF16)


def project_qkv(x, w, tables):
    length, width = x.shape
    cols = w.shape[0] // 3
    steps = length // TILE
    weight = pl.BlockSpec((3 * cols, width), lambda i: (0, 0))
    table = pl.BlockSpec((TILE, tables[0].shape[1]), lambda i: (i, 0))
    row_out = pl.BlockSpec((TILE, cols), lambda i: (i, 0))
    col_out = pl.BlockSpec((cols, TILE), lambda i: (0, i))
    rows = jax.ShapeDtypeStruct((length, cols), BF16)
    columns = jax.ShapeDtypeStruct((cols, length), BF16)
    return pl.pallas_call(
        qkv_kernel,
        grid=(steps,),
        out_shape=(rows, rows, rows, columns, columns),
        in_specs=[pl.BlockSpec((TILE, width), lambda i: (i, 0))]
        + [weight]
        + [table] * 4,
        out_specs=(row_out, row_out, row_out, col_out, col_out),
        compiler_params=pltpu.CompilerParams(vmem_limit_bytes=VMEM_LIMIT),
        cost_estimate=pl.CostEstimate(
            flops=6 * length * width * cols,
            bytes_accessed=2 * length * width + 6 * width * cols + 10 * length * cols,
            transcendentals=0,
        ),
        name="project_qkv",
    )(x, w, *tables)


def pair_mask(start_row, i, j):
    key_place = j * TILE + lax.broadcasted_iota(jnp.int32, (TILE, TILE), 0)
    query_place = i * TILE + lax.broadcasted_iota(jnp.int32, (TILE, TILE), 1)
    return (key_place <= query_place) & (key_place >= start_row)


def head_rows(query, heads):
    lane = lax.broadcasted_iota(jnp.int32, query.shape, 1) // HEAD_DIM
    zero = jnp.zeros_like(query)
    return [jnp.where(lane == h, query, zero) for h in range(heads)]


def attend_kernel(
    heads, first_ref, start_ref, q_ref, k_ref, vt_ref, o_ref, lse_ref, peak, total, mixed
):
    i = pl.program_id(0)
    queries = head_rows(q_ref[...], heads)
    start_row = start_ref[...]

    def block(j, first):
        at = pl.ds(pl.multiple_of(j * TILE, TILE), TILE)
        keys = k_ref[at, :]
        mask = pair_mask(start_row, i, j)
        for h in range(heads):
            here = slice(h * HEAD_DIM, (h + 1) * HEAD_DIM)
            scores = jnp.where(mask, nt(keys, queries[h]), MASKED)
            if first:
                new_peak = jnp.max(scores, axis=0, keepdims=True)
                expo = jnp.exp(scores - new_peak)
                total[h : h + 1] = jnp.sum(expo, axis=0, keepdims=True)
                mixed[here] = nn(vt_ref[here, at], expo.astype(BF16))
            else:
                old_peak = peak[h : h + 1]
                new_peak = jnp.maximum(old_peak, jnp.max(scores, axis=0, keepdims=True))
                expo = jnp.exp(scores - new_peak)
                shrink = jnp.exp(old_peak - new_peak)
                total[h : h + 1] = total[h : h + 1] * shrink + jnp.sum(
                    expo, axis=0, keepdims=True
                )
                mixed[here] = mixed[here] * shrink + nn(
                    vt_ref[here, at], expo.astype(BF16)
                )
            peak[h : h + 1] = new_peak

    block(i, True)

    @pl.loop(0, i - first_ref[i])
    def _(t):
        block(i - 1 - t, False)

    for h in range(heads):
        here = slice(h * HEAD_DIM, (h + 1) * HEAD_DIM)
        mixed[here] = mixed[here] / total[h : h + 1]
    o_ref[...] = mixed[...].T.astype(BF16)
    lse_ref[0] = peak[...] + jnp.log(total[...])


def attend(first, start, q, k, vt):
    length, cols = q.shape
    heads = cols // HEAD_DIM
    steps = length // TILE
    row = pl.BlockSpec((TILE, cols), lambda i, *_: (i, 0))
    return pl.pallas_call(
        functools.partial(attend_kernel, heads),
        out_shape=(
            jax.ShapeDtypeStruct((length, cols), BF16),
            jax.ShapeDtypeStruct((steps, heads, TILE), F32),
        ),
        grid_spec=pltpu.PrefetchScalarGridSpec(
            num_scalar_prefetch=1,
            grid=(steps,),
            in_specs=[
                pl.BlockSpec((1, TILE), lambda i, *_: (0, i)),
                row,
                pl.BlockSpec((length, cols), lambda i, *_: (0, 0)),
                pl.BlockSpec((cols, length), lambda i, *_: (0, 0)),
            ],
            out_specs=(
                row,
                pl.BlockSpec((1, heads, TILE), lambda i, *_: (i, 0, 0)),
            ),
            scratch_shapes=[
                pltpu.VMEM((heads, TILE), F32),
                pltpu.VMEM((heads, TILE), F32),
                pltpu.VMEM((cols, TILE), F32),
            ],
        ),
        compiler_params=pltpu.CompilerParams(vmem_limit_bytes=VMEM_LIMIT),
        cost_estimate=pl.CostEstimate(
            flops=4 * length * 1024 * cols,
            bytes_accessed=8 * length * cols,
            transcendentals=length * 1024 * heads,
        ),
        name="attend",
    )(first, start, q, k, vt)


def attend_back_kernel(
    heads, first_ref, start_ref, q_ref, k_ref, kt_ref, v_ref, o_ref, lse_ref, do_ref,
    cq_ref, sq_ref, ck_ref, sk_ref, grad_ref, dqt, dk_sum, dv_sum,
):
    i = pl.program_id(0)
    steps = pl.num_programs(0)
    width = q_ref.shape[1]
    queries = head_rows(q_ref[...], heads)
    grads = head_rows(do_ref[...], heads)
    start_row = start_ref[...]
    product = (do_ref[...].astype(F32) * o_ref[...].astype(F32)).T
    inner = [
        jnp.sum(product[h * HEAD_DIM : (h + 1) * HEAD_DIM], axis=0, keepdims=True)
        for h in range(heads)
    ]

    def block(j, first):
        at = pl.ds(pl.multiple_of(j * TILE, TILE), TILE)
        keys = k_ref[at, :]
        values = v_ref[at, :]
        mask = pair_mask(start_row, i, j)
        key_term = None
        value_term = None
        for h in range(heads):
            here = slice(h * HEAD_DIM, (h + 1) * HEAD_DIM)
            scores = nt(keys, queries[h])
            weights = jnp.where(mask, jnp.exp(scores - lse_ref[0, h : h + 1]), 0.0)
            grad_weights = nt(values, grads[h])
            grad_scores = (weights * (grad_weights - inner[h])).astype(BF16)
            term = nn(weights.astype(BF16), grads[h])
            value_term = term if value_term is None else value_term + term
            term = nn(grad_scores, queries[h])
            key_term = term if key_term is None else key_term + term
            term = nn(kt_ref[here, at], grad_scores)
            if first:
                dqt[here] = term
            else:
                dqt[here] = dqt[here] + term
        if first:
            dk_sum[at] = key_term
            dv_sum[at] = value_term
        else:
            dk_sum[at] = dk_sum[at] + key_term
            dv_sum[at] = dv_sum[at] + value_term

    block(i, True)

    @pl.loop(0, i - first_ref[i])
    def _(t):
        block(i - 1 - t, False)

    def unturn(grad, cosine, sine):
        grad = grad.astype(BF16).astype(F32)
        cosine = spread_lanes(cosine, width)
        sine = spread_lanes(sine, width)
        return (grad * cosine - swap_halves(grad) * sine).astype(BF16)

    rows = pl.ds(pl.multiple_of(i * TILE, TILE), TILE)
    grad_ref[rows, 0:width] = unturn(
        dqt[...].T * (HEAD_DIM**-0.5), cq_ref[rows, :], sq_ref[rows, :]
    )

    @pl.when(i == steps - 1)
    def _():
        @pl.loop(0, steps)
        def _(j):
            at = pl.ds(pl.multiple_of(j * TILE, TILE), TILE)
            grad_ref[at, width : 2 * width] = unturn(
                dk_sum[at], ck_ref[at, :], sk_ref[at, :]
            )
            grad_ref[at, 2 * width :] = dv_sum[at].astype(BF16)


def attend_back(first, start, q, k, kt, v, o, lse, do, tables):
    length, cols = q.shape
    heads = cols // HEAD_DIM
    steps = length // TILE
    row = pl.BlockSpec((TILE, cols), lambda i, *_: (i, 0))
    whole = pl.BlockSpec((length, cols), lambda i, *_: (0, 0))
    table = pl.BlockSpec((length, tables[0].shape[1]), lambda i, *_: (0, 0))
    return pl.pallas_call(
        functools.partial(attend_back_kernel, heads),
        out_shape=jax.ShapeDtypeStruct((length, 3 * cols), BF16),
        grid_spec=pltpu.PrefetchScalarGridSpec(
            num_scalar_prefetch=1,
            grid=(steps,),
            in_specs=[
                pl.BlockSpec((1, TILE), lambda i, *_: (0, i)),
                row,
                whole,
                pl.BlockSpec((cols, length), lambda i, *_: (0, 0)),
                whole,
                row,
                pl.BlockSpec((1, heads, TILE), lambda i, *_: (i, 0, 0)),
                row,
            ]
            + [table] * 4,
            out_specs=pl.BlockSpec((length, 3 * cols), lambda i, *_: (0, 0)),
            scratch_shapes=[
                pltpu.VMEM((cols, TILE), F32),
                pltpu.VMEM((length, cols), F32),
                pltpu.VMEM((length, cols), F32),
            ],
        ),
        compiler_params=pltpu.CompilerParams(vmem_limit_bytes=VMEM_LIMIT),
        name="attend_back",
    )(first, start, q, k, kt, v, o, lse, do, *tables)


def upper_kernel(
    x_ref, wu_ref, c_ref, wd_ref, gain_ref, act_ref, slope_ref, grad_ref, stat_ref
):
    upper = nt(x_ref[...], wu_ref[...])
    grad = nn(c_ref[...], wd_ref[...])
    below = 0.5 * (1.0 + lax.erf(upper * (0.5**0.5)))
    act = upper * below
    slope = below + upper * (jnp.exp(-0.5 * upper * upper) * ((2.0 * math.pi) ** -0.5))
    act_ref[...] = act
    slope_ref[...] = slope.astype(BF16)
    grad_ref[...] = grad
    part = grad * gain_ref[...]
    average = jnp.mean(act, axis=-1, keepdims=True)
    centered = act - average
    spread = jnp.sum(centered * centered, axis=-1, keepdims=True)
    part_sum = jnp.sum(part, axis=-1, keepdims=True)
    cross = jnp.sum(part * centered, axis=-1, keepdims=True)
    lane = lax.broadcasted_iota(jnp.int32, (x_ref.shape[0], 128), 1)
    columns = jnp.where(
        lane == 0,
        average,
        jnp.where(lane == 1, spread, jnp.where(lane == 2, part_sum, cross)),
    )
    stat_ref[...] = columns.T[:8]


def upper_pass(x, w_up, cot, w_down, gain):
    length, width = x.shape
    feats = w_up.shape[0]
    rows = TILE
    row = pl.BlockSpec((rows, width), lambda i: (i, 0))
    out = pl.BlockSpec((rows, feats), lambda i: (i, 0))
    return pl.pallas_call(
        upper_kernel,
        grid=(length // rows,),
        out_shape=(
            jax.ShapeDtypeStruct((length, feats), F32),
            jax.ShapeDtypeStruct((length, feats), BF16),
            jax.ShapeDtypeStruct((length, feats), F32),
            jax.ShapeDtypeStruct((8, length), F32),
        ),
        in_specs=[
            row,
            pl.BlockSpec((feats, width), lambda i: (0, 0)),
            row,
            pl.BlockSpec((width, feats), lambda i: (0, 0)),
            pl.BlockSpec((1, feats), lambda i: (0, 0)),
        ],
        out_specs=(out, out, out, pl.BlockSpec((8, rows), lambda i: (0, i))),
        compiler_params=pltpu.CompilerParams(vmem_limit_bytes=VMEM_LIMIT),
        cost_estimate=pl.CostEstimate(
            flops=4 * length * width * feats,
            bytes_accessed=8 * length * width + 8 * length * feats,
            transcendentals=2 * length * feats,
        ),
        name="upper_pass",
    )(x, w_up, cot, w_down, gain)


def hidden_kernel(act_ref, slope_ref, grad_ref, stat_ref, gain_ref, hid_ref, gu_ref, gg_ref):
    i = pl.program_id(0)
    stats = stat_ref[...].T
    average = stats[:, 0:1]
    scale = stats[:, 1:2]
    part_mean = stats[:, 2:3]
    cross_mean = stats[:, 3:4]
    gain = gain_ref[...]
    normal = (act_ref[...] - average) * scale
    grad = grad_ref[...]
    hid_ref[...] = (normal * gain).astype(BF16)
    back = scale * (grad * gain - part_mean - normal * cross_mean)
    gu_ref[...] = (slope_ref[...].astype(F32) * back).astype(BF16)
    term = jnp.sum(grad * normal, axis=0, keepdims=True)

    @pl.when(i == 0)
    def _():
        gg_ref[...] = term

    @pl.when(i > 0)
    def _():
        gg_ref[...] = gg_ref[...] + term


def hidden_pass(act, slope, grad, stats, gain):
    length, feats = act.shape
    out = pl.BlockSpec((TILE, feats), lambda i: (i, 0))
    one = pl.BlockSpec((1, feats), lambda i: (0, 0))
    return pl.pallas_call(
        hidden_kernel,
        grid=(length // TILE,),
        out_shape=(
            jax.ShapeDtypeStruct((length, feats), BF16),
            jax.ShapeDtypeStruct((length, feats), BF16),
            jax.ShapeDtypeStruct((1, feats), F32),
        ),
        in_specs=[out, out, out, pl.BlockSpec((8, TILE), lambda i: (0, i)), one],
        out_specs=(out, out, one),
        compiler_params=pltpu.CompilerParams(vmem_limit_bytes=VMEM_LIMIT),
        cost_estimate=pl.CostEstimate(
            flops=12 * length * feats,
            bytes_accessed=14 * length * feats,
            transcendentals=0,
        ),
        name="hidden_pass",
    )(act, slope, grad, stats, gain)


def ffn_kernel(
    n, x_ref, wu_ref, cot_ref, wd_ref, gain_ref,
    full_ref, hid_ref, gu_ref, gg_ref,
    rows_in, wd, cot_in, act, slope, grad, stat, held, results,
    local_sem, cot_sem, out_sem, full_sem, send_sem, recv_sem, stat_send, stat_recv,
):
    me, twin, near_x, near_y, across = places()
    rows = x_ref.shape[0]
    feats = wu_ref.shape[0]

    def cut(i, size=rows):
        return pl.ds(pl.multiple_of(i * size, size), size)

    own = pltpu.make_async_copy(x_ref, rows_in.at[me], local_sem.at[0])
    own.start()
    load_wd = pltpu.make_async_copy(wd_ref, wd, local_sem.at[1])
    load_wd.start()

    def load_cot(i, slot):
        return pltpu.make_async_copy(
            cot_ref.at[cut(i)], cot_in.at[slot], cot_sem.at[slot]
        )

    load_cot(0, 0).start()
    meet([lax.rem(me + k, n) for k in range(1, n)])
    sends = gather_copies(x_ref, rows_in, send_sem, recv_sem)
    for k in range(5):
        sends[k].start()

    load_wd.wait()
    def incoming(first, last):
        @pl.loop(first, last)
        def _(i):
            slot = lax.rem(i, 2)

            @pl.when(i + 1 < n)
            def _():
                load_cot(i + 1, 1 - slot).start()

            load_cot(i, slot).wait()
            grad[cut(i)] = nn(cot_in[slot], wd[...])

    incoming(0, n - 2)
    sends[0].wait_recv()
    sends[5].start()
    sends[7].start()
    sends[1].wait_recv()
    sends[6].start()
    sends[8].start()
    incoming(n - 2, n)
    own.wait()

    def keep(b):
        return pltpu.make_async_copy(rows_in.at[b], full_ref.at[b], full_sem.at[b])

    @pl.loop(0, n)
    def _(i):
        @pl.when(i == 1)
        def _():
            sends[4].wait_recv()

        @pl.when(i == 2)
        def _():
            sends[2].wait_recv()
            sends[9].start()
            sends[3].wait_recv()
            sends[10].start()

        @pl.when(i == 4)
        def _():
            sends[7].wait_recv()
            sends[9].wait_recv()

        @pl.when(i == 5)
        def _():
            sends[8].wait_recv()
            sends[10].wait_recv()
            sends[5].wait_recv()
            sends[11].start()
            sends[6].wait_recv()
            sends[12].start()

        @pl.when(i == 7)
        def _():
            sends[11].wait_recv()
            sends[12].wait_recv()

        other = jnp.where((i == 1) | (i == 4) | (i == 5) | (i == 7), twin, 0)
        place = jnp.where(i < 2, me, jnp.where(i >= 6, across, jnp.where(lax.rem(i, 2) == 0, near_x, near_y)))
        b = place + other
        keep(b).start()
        at = cut(b)
        upper = nt(rows_in[b], wu_ref[...])
        below = 0.5 * (1.0 + lax.erf(upper * (0.5**0.5)))
        value = upper * below
        act[at] = value
        slope[at] = (
            below + upper * (jnp.exp(-0.5 * upper * upper) * ((2.0 * math.pi) ** -0.5))
        ).astype(BF16)
        part = grad[at] * gain_ref[...]
        average = jnp.mean(value, axis=-1, keepdims=True)
        centered = value - average
        spread = jnp.sum(centered * centered, axis=-1, keepdims=True)
        part_sum = jnp.sum(part, axis=-1, keepdims=True)
        cross = jnp.sum(part * centered, axis=-1, keepdims=True)
        lane = lax.broadcasted_iota(jnp.int32, (rows, 128), 1)
        columns = jnp.where(
            lane == 0,
            average,
            jnp.where(lane == 1, spread, jnp.where(lane == 2, part_sum, cross)),
        )
        stat[:, at] = columns.T[:8]

    held[me] = stat[...]
    rounds = [
        remote(
            stat, held.at[me], stat_send.at[k], stat_recv.at[k], lax.rem(me + k, n)
        )
        for k in range(1, n)
    ]
    for send in rounds:
        send.start()
    for send in rounds:
        send.wait()
    join_rows(n, feats, held, stat)

    def store(i, slot):
        return [
            pltpu.make_async_copy(
                results.at[slot, j], ref.at[cut(i)], out_sem.at[slot, j]
            )
            for j, ref in enumerate((hid_ref, gu_ref))
        ]

    gg_ref[...] = jnp.zeros_like(gg_ref)

    @pl.loop(0, n)
    def _(i):
        slot = lax.rem(i, 2)

        @pl.when(i >= 2)
        def _():
            for copy in store(i - 2, slot):
                copy.wait()

        at = cut(i)
        stats = stat[:, at].T
        gain = gain_ref[...]
        scale = stats[:, 1:2]
        normal = (act[at] - stats[:, 0:1]) * scale
        coming = grad[at]
        results[slot, 0] = (normal * gain).astype(BF16)
        back = scale * (coming * gain - stats[:, 2:3] - normal * stats[:, 3:4])
        results[slot, 1] = (slope[at].astype(F32) * back).astype(BF16)
        gg_ref[...] = gg_ref[...] + jnp.sum(coming * normal, axis=0, keepdims=True)
        for copy in store(i, slot):
            copy.start()

    for i in (n - 2, n - 1):
        for copy in store(i, i % 2):
            copy.wait()
    for b in range(n):
        keep(b).wait()
    for send in sends:
        send.wait_send()


def ffn_pass(ffn_in, w_up, cot, w_down, gain, collective_id):
    n = lax.axis_size("seq")
    rows, width = ffn_in.shape
    feats = w_up.shape[0]
    if n != 8:
        full = lax.all_gather(ffn_in, "seq", axis=0, tiled=True)
        act, slope, grad, stat = upper_pass(full, w_up, cot, w_down, gain)
        stats = join_stats(stat, feats, collective_id)
        return (full, *hidden_pass(act, slope, grad, stats, gain))
    length = n * rows
    dma = pltpu.SemaphoreType.DMA
    low = jax.ShapeDtypeStruct((length, feats), BF16)
    full, hidden, grad_upper, gain_grad = pl.pallas_call(
        functools.partial(ffn_kernel, n),
        out_shape=(
            jax.ShapeDtypeStruct((n, rows, width), BF16),
            low,
            low,
            jax.ShapeDtypeStruct((1, feats), F32),
        ),
        in_specs=[INSIDE, INSIDE, ANY, ANY, INSIDE],
        out_specs=(ANY, ANY, ANY, INSIDE),
        scratch_shapes=[
            pltpu.VMEM((n, rows, width), BF16),
            pltpu.VMEM((width, feats), BF16),
            pltpu.VMEM((2, rows, width), BF16),
            pltpu.VMEM((length, feats), F32),
            pltpu.VMEM((length, feats), BF16),
            pltpu.VMEM((length, feats), F32),
            pltpu.VMEM((8, length), F32),
            pltpu.VMEM((n, 8, length), F32),
            pltpu.VMEM((2, 2, rows, feats), BF16),
            dma((2,)),
            dma((2,)),
            dma((2, 2)),
            dma((n,)),
            dma((13,)),
            dma((13,)),
            dma((n,)),
            dma((n,)),
        ],
        compiler_params=pltpu.CompilerParams(
            collective_id=collective_id, has_side_effects=True, vmem_limit_bytes=VMEM_LIMIT
        ),
        name="ffn_pass",
    )(ffn_in, w_up, cot, w_down, gain)
    return full.reshape(length, width), hidden, grad_upper, gain_grad


def join_rows(n, feats, held, o_ref):
    average = held[0, 0:1]
    for d in range(1, n):
        average = average + held[d, 0:1]
    average = average * (1.0 / n)
    spread = jnp.zeros_like(average)
    part = jnp.zeros_like(average)
    cross = jnp.zeros_like(average)
    for d in range(n):
        shift = held[d, 0:1] - average
        spread = spread + held[d, 1:2] + feats * (shift * shift)
        part = part + held[d, 2:3]
        cross = cross + held[d, 3:4] + shift * held[d, 2:3]
    whole = 1.0 / (n * feats)
    scale = lax.rsqrt(spread * whole + EPSILON)
    o_ref[0:1] = average
    o_ref[1:2] = scale
    o_ref[2:3] = part * whole
    o_ref[3:4] = cross * scale * whole
    o_ref[4:8] = jnp.zeros((4, average.shape[1]), F32)


def stat_kernel(n, feats, x_ref, o_ref, held, send_sem, recv_sem):
    me = lax.axis_index("seq")
    held[me] = x_ref[...]
    meet([lax.rem(me + k, n) for k in range(1, n)])
    copies = [
        remote(x_ref, held.at[me], send_sem.at[k], recv_sem.at[k], lax.rem(me + k, n))
        for k in range(1, n)
    ]
    for copy in copies:
        copy.start()
    for copy in copies:
        copy.wait()
    join_rows(n, feats, held, o_ref)


def join_stats(stat, feats, collective_id):
    n = lax.axis_size("seq")
    inside = pl.BlockSpec(memory_space=pltpu.VMEM)
    return pl.pallas_call(
        functools.partial(stat_kernel, n, feats),
        out_shape=jax.ShapeDtypeStruct(stat.shape, F32),
        in_specs=[inside],
        out_specs=inside,
        scratch_shapes=[
            pltpu.VMEM((n, *stat.shape), F32),
            pltpu.SemaphoreType.DMA((n,)),
            pltpu.SemaphoreType.DMA((n,)),
        ],
        compiler_params=pltpu.CompilerParams(
            collective_id=collective_id, has_side_effects=True, vmem_limit_bytes=VMEM_LIMIT
        ),
        name="join_stats",
    )(stat)


def mix_kernel(att_ref, x_ref, w_ref, gm_ref, gf_ref, mix_ref, mid_ref, ffn_ref):
    j = pl.program_id(0)
    rows = att_ref.shape[0]
    cols = w_ref.shape[0]

    @pl.when(j == 0)
    def _():
        @pl.loop(0, rows // STEP)
        def _(r):
            at = pl.ds(pl.multiple_of(r * STEP, STEP), STEP)
            normal, _ = norm_parts(att_ref[at].astype(F32))
            mix_ref[at] = (normal * gm_ref[...]).astype(BF16)

    here = pl.ds(pl.multiple_of(j * cols, cols), cols)
    mid_ref[:, here] = x_ref[:, here].astype(F32) + nt(mix_ref[...], w_ref[...])

    @pl.when(j == pl.num_programs(0) - 1)
    def _():
        @pl.loop(0, rows // STEP)
        def _(r):
            at = pl.ds(pl.multiple_of(r * STEP, STEP), STEP)
            normal, _ = norm_parts(mid_ref[at])
            ffn_ref[at] = (normal * gf_ref[...]).astype(BF16)


def mix_pass(attended, x, w_out, gain_mix, gain_ffn):
    rows, width = x.shape
    cols = 2 * TILE
    n = width // cols
    whole = pl.BlockSpec((rows, width), lambda j: (0, 0))
    gain = pl.BlockSpec((1, width), lambda j: (0, 0))
    low = jax.ShapeDtypeStruct((rows, width), BF16)
    return pl.pallas_call(
        mix_kernel,
        grid=(n,),
        out_shape=(low, jax.ShapeDtypeStruct((rows, width), F32), low),
        in_specs=[
            whole,
            whole,
            pl.BlockSpec((cols, width), lambda j: (j, 0)),
            gain,
            gain,
        ],
        out_specs=(whole, whole, whole),
        compiler_params=pltpu.CompilerParams(vmem_limit_bytes=VMEM_LIMIT),
        cost_estimate=pl.CostEstimate(
            flops=2 * rows * width * width,
            bytes_accessed=2 * width * width + 12 * rows * width,
            transcendentals=0,
        ),
        name="mix_pass",
    )(attended, x, w_out, gain_mix[None], gain_ffn[None])


def branch_kernel(gbr_ref, att_ref, w_ref, gm_ref, gatt_ref, ggm_ref, total):
    j = pl.program_id(0)
    rows = att_ref.shape[0]
    cols = w_ref.shape[0]
    here = pl.ds(pl.multiple_of(j * cols, cols), cols)
    term = nn(gbr_ref[:, here], w_ref[...])

    @pl.when(j == 0)
    def _():
        total[...] = term

    @pl.when(j > 0)
    def _():
        total[...] = total[...] + term

    @pl.when(j == pl.num_programs(0) - 1)
    def _():
        ggm_ref[...] = jnp.zeros_like(ggm_ref)

        @pl.loop(0, rows // STEP)
        def _(r):
            at = pl.ds(pl.multiple_of(r * STEP, STEP), STEP)
            normal, scale = norm_parts(att_ref[at].astype(F32))
            part, gain_part = norm_back(total[at], normal, scale, gm_ref[...])
            ggm_ref[...] += gain_part[None]
            gatt_ref[at] = part.astype(BF16)


def branch_pass(grad_branch, attended, w_out, gain_mix):
    rows, width = grad_branch.shape
    cols = 2 * TILE
    n = width // cols
    whole = pl.BlockSpec((rows, width), lambda j: (0, 0))
    gain = pl.BlockSpec((1, width), lambda j: (0, 0))
    return pl.pallas_call(
        branch_kernel,
        grid=(n,),
        out_shape=(
            jax.ShapeDtypeStruct((rows, width), BF16),
            jax.ShapeDtypeStruct((1, width), F32),
        ),
        in_specs=[whole, whole, pl.BlockSpec((cols, width), lambda j: (j, 0)), gain],
        out_specs=(whole, gain),
        scratch_shapes=[pltpu.VMEM((rows, width), F32)],
        compiler_params=pltpu.CompilerParams(vmem_limit_bytes=VMEM_LIMIT),
        name="branch_pass",
    )(grad_branch, attended, w_out, gain_mix[None])


def ffn_back_kernel(
    n, gu_ref, wu_ref, hid_ref, wd_ref, all_ref, mid_ref, cot_ref, gf_ref,
    po_ref, gd_ref, gmid_ref, gbr_ref, ggf_ref,
    gu, hid, every, own, far, twin_in, held, made, made_grad,
    local_sem, made_sem, grad_sem, send_sem, recv_sem,
):
    me, twin, near_x, near_y, across = places()
    rows, width = mid_ref.shape
    half = rows // 2
    low, high = pl.ds(0, half), pl.ds(half, half)
    mine = (across, near_x, near_y, me)

    def cut(i, size=rows):
        return pl.ds(pl.multiple_of(i * size, size), size)

    load_gu = pltpu.make_async_copy(gu_ref, gu, local_sem.at[0])
    load_hid = pltpu.make_async_copy(hid_ref, hid, local_sem.at[1])
    load_all = pltpu.make_async_copy(all_ref, every, local_sem.at[2])
    for load in (load_gu, load_hid, load_all):
        load.start()
    meet((me + twin, near_x, near_y))
    load_gu.wait()

    def copy(k, src, dst, partner):
        return remote(src, dst, send_sem.at[k], recv_sem.at[k], partner)

    twins = [copy(i, far.at[i], twin_in.at[i], me + twin) for i in range(4)]
    sends = [
        copy(4, own.at[0, low], held.at[0], near_x),
        copy(5, own.at[0, high], held.at[1], near_y),
        copy(6, own.at[1, low], held.at[2], near_x),
        copy(7, own.at[2, high], held.at[3], near_y),
        copy(8, own.at[1, high], held.at[4], near_x),
        copy(9, own.at[2, low], held.at[5], near_y),
    ]

    def add(i, base, count, source):
        @pl.loop(0, count // STEP)
        def _(r):
            at = cut(r, STEP)
            to = pl.ds(pl.multiple_of(base + r * STEP, STEP), STEP)
            own[i, to] = (own[i, to].astype(F32) + source[at].astype(F32)).astype(BF16)

    for i, block in enumerate(mine):
        far[i] = nn(gu[cut(block + twin)], wu_ref[...]).astype(BF16)
        twins[i].start()
        own[i] = nn(gu[cut(block)], wu_ref[...]).astype(BF16)
        if i < 3:
            twins[i].wait_recv()
            add(i, 0, rows, twin_in.at[i])
        if i == 0:
            sends[0].start()
            sends[1].start()
        elif i < 3:
            sends[i + 1].start()

    def store(i, slot):
        return pltpu.make_async_copy(made.at[slot], po_ref.at[cut(i)], made_sem.at[slot])

    def outputs(first, last):
        @pl.loop(first, last)
        def _(i):
            slot = lax.rem(i, 2)

            @pl.when(i >= 2)
            def _():
                store(i - 2, slot).wait()

            made[slot] = nt(hid[cut(i)], wd_ref[...]).astype(BF16)
            store(i, slot).start()

    def store_grad(i, slot):
        return pltpu.make_async_copy(
            made_grad.at[slot], gd_ref.at[i], grad_sem.at[slot]
        )

    def weight_grads(first, last):
        for i in range(first, last):
            slot = i % 2
            if i >= 2:
                store_grad(i - 2, slot).wait()
            made_grad[slot] = tn(
                every[:, i * rows : (i + 1) * rows], hid[...]
            ).astype(BF16)
            store_grad(i, slot).start()

    load_hid.wait()
    load_all.wait()
    weight_grads(0, n // 2)
    sends[1].wait_recv()
    add(1, half, half, held.at[1])
    sends[4].start()
    sends[0].wait_recv()
    add(2, 0, half, held.at[0])
    sends[5].start()
    weight_grads(n // 2, n)
    outputs(0, n)
    twins[3].wait_recv()
    for k in (2, 3, 4, 5):
        sends[k].wait_recv()
    ggf_ref[...] = jnp.zeros_like(ggf_ref)
    for base, one, two in ((0, 2, 5), (half, 3, 4)):

        @pl.loop(0, half // STEP)
        def _(r):
            at = cut(r, STEP)
            to = pl.ds(pl.multiple_of(base + r * STEP, STEP), STEP)
            value = (
                own[3, to].astype(F32)
                + twin_in[3, to].astype(F32)
                + held[one, at].astype(F32)
                + held[two, at].astype(F32)
            )
            normal, scale = norm_parts(mid_ref[to])
            part, gain_part = norm_back(value, normal, scale, gf_ref[...])
            ggf_ref[...] = ggf_ref[...] + gain_part[None]
            grad = cot_ref[to].astype(F32) + part
            gmid_ref[to] = grad
            gbr_ref[to] = grad.astype(BF16)

    for i in (n - 2, n - 1):
        store(i, i % 2).wait()
        store_grad(i, i % 2).wait()
    for send in twins + sends:
        send.wait_send()


def ffn_back(grad_upper, w_up, hidden, w_down, cot_full, middle, cot, gain, collective_id):
    n = lax.axis_size("seq")
    rows, width = middle.shape
    feats = w_up.shape[0]
    if n != 8:
        normal, scale = norm_parts(middle)
        value = scatter_seq(nn(grad_upper, w_up).astype(BF16))
        part, gain_part = norm_back(value, normal, scale, gain)
        grad = cot.astype(F32) + part
        down = tn(cot_full, hidden).astype(BF16).reshape(n, rows, feats)
        outputs = nt(hidden, w_down).astype(BF16)
        return outputs, down, grad, grad.astype(BF16), gain_part[None]
    dma = pltpu.SemaphoreType.DMA
    block = pltpu.VMEM((4, rows, width), BF16)
    return pl.pallas_call(
        functools.partial(ffn_back_kernel, n),
        out_shape=(
            jax.ShapeDtypeStruct((n * rows, width), BF16),
            jax.ShapeDtypeStruct((n, rows, feats), BF16),
            jax.ShapeDtypeStruct((rows, width), F32),
            jax.ShapeDtypeStruct((rows, width), BF16),
            jax.ShapeDtypeStruct((1, width), F32),
        ),
        in_specs=[ANY, INSIDE, ANY, INSIDE, ANY, INSIDE, INSIDE, INSIDE],
        out_specs=(ANY, ANY, INSIDE, INSIDE, INSIDE),
        scratch_shapes=[
            pltpu.VMEM((n * rows, feats), BF16),
            pltpu.VMEM((n * rows, feats), BF16),
            pltpu.VMEM((n * rows, width), BF16),
            block,
            block,
            block,
            pltpu.VMEM((6, rows // 2, width), BF16),
            pltpu.VMEM((2, rows, width), BF16),
            pltpu.VMEM((2, rows, feats), BF16),
            dma((3,)),
            dma((2,)),
            dma((2,)),
            dma((10,)),
            dma((10,)),
        ],
        compiler_params=pltpu.CompilerParams(
            collective_id=collective_id, has_side_effects=True, vmem_limit_bytes=VMEM_LIMIT
        ),
        name="ffn_back",
    )(grad_upper, w_up, hidden, w_down, cot_full, middle, cot, gain[None])


CHUNK = 64


def finish_kernel(
    n, depth, gq_ref, gd_ref, pw_ref, pn_ref, po_ref, x_ref, grad_ref, mid_ref, ga_ref, gm_ref, gf_ref, gh_ref,
    oq_ref, od_ref, ow_ref, gi_ref, out_ref, sums_ref,
    own, twin_in, held, zown, zin, stage, gain_here, gain_row, gain_pack, gain_line,
    local_sem, load_sem, stage_sem, send_sem, recv_sem, keep_sem,
    up_send, up_recv, down_send, down_recv, home_send, home_recv, gain_send, gain_recv,
):
    me, twin, near_x, near_y, across = places()
    z = lax.axis_index("batch")
    rows, width = pn_ref.shape[1:]
    half = rows // 2
    low, high = pl.ds(0, half), pl.ds(half, half)
    mine = (across, near_x, near_y, me)
    _, chunk, cols = zown.shape
    across_width = width // cols
    per_part = (gq_ref.shape[1] // chunk) * across_width
    turned = gq_ref.shape[0] * per_part
    per_source = gd_ref.shape[1] // chunk
    outer = turned + gd_ref.shape[0] * per_source
    chunks = zown.shape[0]
    per_side = chunks // 2

    def cut(i, size):
        return pl.ds(pl.multiple_of(i * size, size), size)

    def wide(i):
        return cut(i // across_width, chunk), cut(lax.rem(i, across_width), cols)

    line_loads = []
    for g in range(turned):
        source = gq_ref.at[(g // per_part, *wide(g % per_part))]
        line_loads.append(pltpu.make_async_copy(source, zown.at[g], load_sem.at[g]))
    for g in range(turned, outer):
        source = gd_ref.at[
            (g - turned) // per_source, cut((g - turned) % per_source, chunk)
        ]
        line_loads.append(pltpu.make_async_copy(source, zown.at[g], load_sem.at[g]))
    for load in line_loads:
        load.start()
    partials = (pw_ref, pn_ref, po_ref)
    loads = [
        [
            pltpu.make_async_copy(p.at[block], own.at[m, i], local_sem.at[4 * m + i])
            for i, block in enumerate(mine)
        ]
        for m, p in enumerate(partials)
    ]
    for part in loads:
        for load in part:
            load.start()
    meet_all(n, depth)

    def copy(m, k, src, dst, partner):
        return remote(src, dst, send_sem.at[m, k], recv_sem.at[m, k], partner)

    twins = [
        [
            copy(m, i, p.at[block + twin], twin_in.at[m, i], me + twin)
            for i, block in enumerate(mine)
        ]
        for m, p in enumerate(partials)
    ]
    sends = [
        [
            copy(m, 4, own.at[m, 0, low], held.at[m, 0], near_x),
            copy(m, 5, own.at[m, 0, high], held.at[m, 1], near_y),
            copy(m, 6, own.at[m, 1, low], held.at[m, 2], near_x),
            copy(m, 7, own.at[m, 2, high], held.at[m, 3], near_y),
            copy(m, 8, own.at[m, 1, high], held.at[m, 4], near_x),
            copy(m, 9, own.at[m, 2, low], held.at[m, 5], near_y),
        ]
        for m in range(3)
    ]
    for part in twins:
        for send in part:
            send.start()

    def add_twin(m, i):
        loads[m][i].wait()
        twins[m][i].wait_recv()

        @pl.loop(0, rows // STEP)
        def _(r):
            at = cut(r, STEP)
            own[m, i, at] = (
                own[m, i, at].astype(F32) + twin_in[m, i, at].astype(F32)
            ).astype(BF16)

    def add_held(m, i, base, slot):
        @pl.loop(0, half // STEP)
        def _(r):
            at = cut(r, STEP)
            to = pl.ds(pl.multiple_of(base + r * STEP, STEP), STEP)
            own[m, i, to] = (
                own[m, i, to].astype(F32) + held[m, slot, at].astype(F32)
            ).astype(BF16)

    def first(m):
        add_twin(m, 0)
        sends[m][0].start()
        sends[m][1].start()
        add_twin(m, 1)
        sends[m][2].start()
        add_twin(m, 2)
        sends[m][3].start()

    def second(m):
        sends[m][1].wait_recv()
        add_held(m, 1, half, 1)
        sends[m][4].start()
        sends[m][0].wait_recv()
        add_held(m, 2, 0, 0)
        sends[m][5].start()

    def last(m, store):
        loads[m][3].wait()
        twins[m][3].wait_recv()
        for k in (2, 3, 4, 5):
            sends[m][k].wait_recv()
        for base, one, two in ((0, 2, 5), (half, 3, 4)):

            @pl.loop(0, half // STEP)
            def _(r):
                at = cut(r, STEP)
                place = base + r * STEP
                to = pl.ds(pl.multiple_of(place, STEP), STEP)
                store(
                    place,
                    to,
                    own[m, 3, to].astype(F32)
                    + twin_in[m, 3, to].astype(F32)
                    + held[m, one, at].astype(F32)
                    + held[m, two, at].astype(F32),
                )

    def store_line(place, to, value):
        value = value.astype(BF16)
        for side in range(across_width):
            zown[
                outer + (place // chunk) * across_width + side,
                pl.ds(pl.multiple_of(lax.rem(place, chunk), STEP), STEP),
            ] = value[:, side * cols : (side + 1) * cols]

    def store_inputs(place, to, value):
        normal, scale = norm_parts(x_ref[to].astype(F32))
        part, gain_part = norm_back(value, normal, scale, ga_ref[...])
        gi_ref[to] = grad_ref[to] + part
        gain_here[0:1] = gain_here[0:1] + gain_part[None]

    def store_outputs(place, to, value):
        out_ref[to] = (mid_ref[to] + value).astype(BF16)

    def home(part):
        block = part * n + me
        return block // 3, lax.rem(block, 3)

    def deliver_far(g):
        target, slot = home(g // per_part)
        piece = lax.rem(g, per_part)
        return remote(
            zin.at[g],
            oq_ref.at[(slot, *wide(piece))],
            home_send.at[g],
            home_recv.at[slot, piece],
            target,
        )

    def deliver_near(g):
        _, slot = home(g // per_part)
        return pltpu.make_async_copy(
            zin.at[g], oq_ref.at[(slot, *wide(lax.rem(g, per_part)))], keep_sem.at[g]
        )

    def widen(g):
        @pl.loop(0, chunk // STEP)
        def _(r):
            at = cut(r, STEP)
            stage[at] = zin[g, at].astype(F32)

    def deliver(g):
        target, _ = home(g // per_part)

        @pl.when((g < turned) & (target != me))
        def _():
            deliver_far(g).start()

        @pl.when((g < turned) & (target == me))
        def _():
            deliver_near(g).start()

        @pl.when((g >= turned) & (g < outer))
        def _():
            widen(g)
            at = g - turned
            place = cut(lax.rem(at, per_source), chunk), cut(at // per_source, cols)
            store = pltpu.make_async_copy(stage, od_ref.at[place], stage_sem)
            store.start()
            store.wait()

        @pl.when(g >= outer)
        def _():
            widen(g)
            store = pltpu.make_async_copy(
                stage, ow_ref.at[wide(g - outer)], stage_sem
            )
            store.start()
            store.wait()

    def delivered(g):
        target, _ = home(g // per_part)

        @pl.when(target != me)
        def _():
            deliver_far(g).wait_send()

        @pl.when(target == me)
        def _():
            deliver_near(g).wait()

    def go_up(g, ahead):
        return line_remote(zown.at[g], zin.at[g], up_send.at[g], up_recv.at[g], ahead)

    def go_down(g, behind):
        return line_remote(
            zin.at[g], zin.at[g], down_send.at[g], down_recv.at[g], behind
        )

    def ranks(side):
        if side == 0:
            return z, z + 1, z - 1
        return depth - 1 - z, z - 1, z + 1

    def add_line(g, target):
        @pl.loop(0, chunk // STEP)
        def _(r):
            at = cut(r, STEP)
            target[g, at] = (zown[g, at].astype(F32) + zin[g, at].astype(F32)).astype(
                BF16
            )

    lead = 1
    far = 2 * (depth - 1)
    steps = per_side + 2 * far

    def line_enter(c):
        for side in (0, 1):
            rank, ahead, _ = ranks(side)

            @pl.when(rank == 0)
            def _():
                go_up(2 * c + side, ahead).start()

    def line_step(t):
        @pl.when(t + lead < per_side)
        def _():
            line_enter(t + lead)

        back = []
        for side in (0, 1):
            rank, ahead, behind = ranks(side)
            c_back = t - 2 * far + 2 * rank
            g_back = 2 * c_back + side
            there = (c_back >= 0) & (c_back < per_side) & (rank < depth - 1)
            back.append((there, g_back))

            @pl.when(there)
            def _():
                go_down(g_back, ahead).wait_recv()

            @pl.when(there & (rank > 0))
            def _():
                go_down(g_back, behind).start()

        for side in (0, 1):
            rank, ahead, behind = ranks(side)
            c = t - 2 * rank
            g = 2 * c + side
            there = (c >= 0) & (c < per_side)

            @pl.when(there & (rank > 0) & (rank < depth - 1))
            def _():
                go_up(g, behind).wait_recv()
                add_line(g, zown)
                go_up(g, ahead).start()

            @pl.when(there & (rank == depth - 1))
            def _():
                go_up(g, behind).wait_recv()
                add_line(g, zin)
                go_down(g, behind).start()
                deliver(g)

        for there, g_back in back:

            @pl.when(there)
            def _():
                deliver(g_back)

    def line_steps(first_step, last_step):
        @pl.loop(first_step, last_step)
        def _(t):
            line_step(t)

    gain_here[...] = jnp.zeros_like(gain_here)
    for load in line_loads[:turned]:
        load.wait()
    for c in range(lead):
        line_enter(c)
    line_steps(0, 3)
    first(0)
    for load in line_loads[turned:]:
        load.wait()
    line_steps(3, 10)
    second(0)
    line_steps(10, 11)
    first(1)
    line_steps(11, 20)
    last(0, store_line)
    line_steps(20, 22)
    second(1)
    line_steps(22, 23)
    first(2)
    line_steps(23, 29)
    last(1, store_inputs)

    gain_here[1:2] = gm_ref[...]
    gain_here[2:3] = gf_ref[...]
    gain_here[3:4, 0 : gh_ref.shape[1]] = gh_ref[...]
    gain_row[me] = gain_here[...]
    rounds = [
        remote(
            gain_here,
            gain_row.at[me],
            gain_send.at[0, k],
            gain_recv.at[0, k],
            lax.rem(me + k, n),
        )
        for k in range(1, n)
    ]
    for send in rounds:
        send.start()
    line_steps(29, 33)
    second(2)
    line_steps(33, 41)
    last(2, store_outputs)
    line_steps(41, 42)
    for send in rounds:
        send.wait()
    total = gain_row[0]
    for d in range(1, n):
        total = total + gain_row[d]
    gain_pack[0:8] = total
    for d in range(n):
        gain_pack[8 + d : 9 + d] = gain_row[d, 3:4]
    gain_line[z] = gain_pack[...]
    rounds = [
        line_remote(
            gain_pack,
            gain_line.at[z],
            gain_send.at[1, k],
            gain_recv.at[1, k],
            lax.rem(z + k, depth),
        )
        for k in range(1, depth)
    ]
    for send in rounds:
        send.start()
    line_steps(42, steps)
    for send in rounds:
        send.wait()
    total = gain_line[0]
    for d in range(1, depth):
        total = total + gain_line[d]
    sums_ref[...] = total

    for m in range(3):
        for send in twins[m] + sends[m]:
            send.wait_send()
    for g in range(chunks):
        rank, ahead, behind = ranks(g % 2)

        @pl.when(rank < depth - 1)
        def _():
            go_up(g, ahead).wait_send()

        @pl.when(rank > 0)
        def _():
            go_down(g, behind).wait_send()

    for g in range(turned):
        delivered(g)
    for slot in range(3):
        block = 3 * me + slot
        source = lax.rem(block, n)

        @pl.when(source != me)
        def _():
            for piece in range(per_part):
                remote(
                    zin.at[0],
                    oq_ref.at[(slot, *wide(piece))],
                    home_send.at[0],
                    home_recv.at[slot, piece],
                    source,
                ).wait_recv()


def finish(
    grad_qkv, grad_down, part_out, part_normed, part_outputs, x, grad_middle, middle, gain, gains, collective_id
):
    n, depth = lax.axis_size("seq"), lax.axis_size("batch")
    rows, width = part_out.shape[0] // n, part_out.shape[1]
    cols = grad_qkv.shape[1]
    sources, _, feats = grad_down.shape
    if n != 8 or depth != 4:
        me = lax.axis_index("seq")
        blocks = lax.psum(grad_qkv, "batch")
        back = [
            lax.ppermute(
                give_part(blocks, me, n, j),
                "seq",
                [((3 * d + j) % n, d) for d in range(n)],
            )
            for j in range(3)
        ]
        w_out = lax.psum(scatter_seq(part_out).astype(BF16), "batch")
        normal, scale = norm_parts(x.astype(F32))
        part, gain_part = norm_back(scatter_seq(part_normed), normal, scale, gain)
        shared = [lax.psum(g, ("batch", "seq")) for g in (gain_part, gains[0][0], gains[1][0])]
        hidden = lax.all_gather(lax.psum(gains[2][0], "batch"), "seq", axis=0, tiled=True)
        down = lax.psum(grad_down, "batch")
        return (
            jnp.concatenate(back, axis=0),
            jnp.swapaxes(down, 0, 1).reshape(rows, sources * feats).astype(F32),
            w_out.astype(F32),
            grad_middle + part,
            (middle + scatter_seq(part_outputs)).astype(BF16),
            (*shared, hidden),
        )
    chunks = (
        3 * cols * width + rows * width + sources * rows * feats
    ) // (CHUNK * feats)
    dma = pltpu.SemaphoreType.DMA
    line = pltpu.VMEM((chunks, CHUNK, feats), BF16)
    w_qkv, w_down, w_out, grad_inputs, outputs, sums = pl.pallas_call(
        functools.partial(finish_kernel, n, depth),
        out_shape=(
            jax.ShapeDtypeStruct((3, cols, width), BF16),
            jax.ShapeDtypeStruct((rows, sources * feats), F32),
            jax.ShapeDtypeStruct((rows, width), F32),
            jax.ShapeDtypeStruct((rows, width), F32),
            jax.ShapeDtypeStruct((rows, width), BF16),
            jax.ShapeDtypeStruct((16, width), F32),
        ),
        in_specs=[ANY] * 5 + [INSIDE] * 7,
        out_specs=(ANY, ANY, ANY, INSIDE, INSIDE, INSIDE),
        scratch_shapes=[
            pltpu.VMEM((3, 4, rows, width), BF16),
            pltpu.VMEM((3, 4, rows, width), BF16),
            pltpu.VMEM((3, 6, rows // 2, width), BF16),
            line,
            line,
            pltpu.VMEM((CHUNK, feats), F32),
            pltpu.VMEM((8, width), F32),
            pltpu.VMEM((n, 8, width), F32),
            pltpu.VMEM((16, width), F32),
            pltpu.VMEM((depth, 16, width), F32),
            dma((12,)),
            dma((chunks,)),
            dma,
            dma((3, 10)),
            dma((3, 10)),
            dma((chunks,)),
            dma((chunks,)),
            dma((chunks,)),
            dma((chunks,)),
            dma((chunks,)),
            dma((chunks,)),
            dma((3, cols * width // (CHUNK * feats))),
            dma((2, n)),
            dma((2, n)),
        ],
        compiler_params=pltpu.CompilerParams(
            collective_id=collective_id,
            has_side_effects=True,
            vmem_limit_bytes=VMEM_LIMIT,
        ),
        name="finish",
    )(
        grad_qkv,
        grad_down,
        *[p.reshape(n, rows, width) for p in (part_out, part_normed, part_outputs)],
        x,
        grad_middle,
        middle,
        gain[None],
        *gains,
    )
    return (
        w_qkv.reshape(3 * cols, width),
        w_down,
        w_out,
        grad_inputs,
        outputs,
        (sums[0], sums[1], sums[2], sums[8:, :feats].reshape(-1)),
    )


def widen_kernel(*refs):
    half = len(refs) // 2
    for source, target in zip(refs[:half], refs[half:], strict=True):
        target[...] = source[...].astype(F32)


def widen(arrays):
    steps = 8
    specs = [pl.BlockSpec((x.shape[0] // steps, x.shape[1]), lambda i: (i, 0)) for x in arrays]
    return pl.pallas_call(
        widen_kernel,
        grid=(steps,),
        out_shape=[jax.ShapeDtypeStruct(x.shape, F32) for x in arrays],
        in_specs=specs,
        out_specs=specs,
        compiler_params=pltpu.CompilerParams(vmem_limit_bytes=VMEM_LIMIT),
        name="widen",
    )(*arrays)


def body(
    inputs,
    segment_ids,
    w_qkv,
    w_out,
    w_up,
    w_down,
    gain_attn,
    gain_mix,
    gain_ffn,
    gain_hidden,
    cotangent,
):
    _, local, width = inputs.shape
    n, depth = lax.axis_size("seq"), lax.axis_size("batch")
    me = lax.axis_index("seq")
    length = local * n
    feats = w_up.shape[0]
    x_low = inputs[0]
    cot = cotangent[0]
    segment = segment_ids[0]

    w_out_full = lax.all_gather(w_out, "seq", axis=0, tiled=True)
    before = [jnp.sum((segment < d).astype(jnp.int32)) for d in range(1, DOCS)]
    start = jnp.zeros_like(segment)
    for d in range(1, DOCS):
        start = jnp.where(segment == d, before[d - 1], start)
    positions = jnp.arange(length, dtype=jnp.int32) - start
    first = start[::TILE] // TILE
    start_row = start[None, :]

    normed_full, w_heads, w_down_cols, tables = start_exchange(
        x_low, gain_attn, w_qkv, w_down, positions.astype(F32), 1
    )
    cot_late, _ = lax.optimization_barrier((cot, w_heads))
    cot_full = lax.all_gather(cot_late, "seq", axis=0, tiled=True)

    q, k, v, kt, vt = project_qkv(normed_full, w_heads, tables)
    attended_heads, lse = attend(first, start_row, q, k, vt)
    attended = heads_to_tokens(attended_heads, 2)
    mix_in, middle, ffn_in = mix_pass(attended, x_low, w_out_full, gain_mix, gain_ffn)
    gain_here = lax.dynamic_slice_in_dim(gain_hidden, me * feats, feats, 0)[None, :]
    ffn_full, hidden, grad_upper, grad_gain_here = ffn_pass(
        ffn_in, w_up, cot_full, w_down_cols, gain_here, 3
    )

    grad_w_up = tn(grad_upper, ffn_full).astype(BF16)
    grad_upper, grad_w_up = lax.optimization_barrier((grad_upper, grad_w_up))
    grad_w_up = lax.psum(grad_w_up, "batch")
    part_outputs, grad_w_down, grad_middle, grad_branch, grad_gain_ffn = ffn_back(
        grad_upper, w_up, hidden, w_down_cols, cot_full, middle, cot, gain_ffn, 4
    )
    grad_att, grad_gain_mix = branch_pass(grad_branch, attended, w_out_full, gain_mix)
    grad_heads = tokens_to_heads(grad_att, 5)
    grad_w_down, grad_heads = lax.optimization_barrier((grad_w_down, grad_heads))
    grad_w_down = lax.all_to_all(grad_w_down, "seq", split_axis=0, concat_axis=0, tiled=True)
    grads = attend_back(
        first, start_row, q, k, kt, v, attended_heads, lse, grad_heads, tables
    )
    grad_w_qkv = tn(grads, normed_full).astype(BF16).reshape(3, -1, width)
    grad_w_qkv, grad_w_up = lax.optimization_barrier((grad_w_qkv, grad_w_up))
    grad_w_qkv, grad_w_down, grad_w_out, grad_inputs, outputs, gains = finish(
        grad_w_qkv,
        grad_w_down,
        tn(grad_branch, mix_in).astype(BF16),
        nn(grads, w_heads).astype(BF16),
        part_outputs,
        x_low,
        grad_middle,
        middle,
        gain_attn,
        (grad_gain_mix, grad_gain_ffn, grad_gain_here),
        6,
    )
    grad_w_qkv, grad_w_up = widen([grad_w_qkv, grad_w_up])
    return (
        outputs[None],
        grad_inputs[None],
        grad_w_qkv,
        grad_w_out,
        grad_w_up,
        grad_w_down,
        *gains,
    )


def pick_part(turned, me, n, part):
    chosen = turned[0]
    home = part * n + me
    for j in (1, 2):
        chosen = jnp.where(lax.rem(home, 3) == j, turned[j], chosen)
    return chosen


def give_part(blocks, me, n, j):
    chosen = blocks[0]
    for part in (1, 2):
        chosen = jnp.where(lax.rem(part * n + me, 3) == j, blocks[part], chosen)
    return chosen


def solution(mesh):
    in_specs = (
        P("batch", "seq", None),
        P("batch", None),
        P("seq", None),
        P("seq", None),
        P("seq", None),
        P("seq", None),
        P(),
        P(),
        P(),
        P(),
        P("batch", "seq", None),
    )
    out_specs = (
        P("batch", "seq", None),
        P("batch", "seq", None),
        P("seq", None),
        P("seq", None),
        P("seq", None),
        P("seq", None),
        P(),
        P(),
        P(),
        P(),
    )
    return jax.shard_map(body, mesh=mesh, in_specs=in_specs, out_specs=out_specs, check_vma=False)
```

```python
import functools
import math

import jax
import jax.numpy as jnp
from jax import lax
from jax.experimental import pallas as pl
from jax.experimental.pallas import tpu as pltpu
from jax.sharding import PartitionSpec as P

HEADS = 32
HEAD_DIM = 64
LENGTH = 2048
XBASE = 512
DOCS = 4
EPSILON = 1e-05
MASKED = -1e30
TILE = 256
STEP = 32
VMEM_LIMIT = 60 * 1024 * 1024

MESH = pl.DeviceIdType.MESH
F32 = jnp.float32
BF16 = jnp.bfloat16
ANY = pl.BlockSpec(memory_space=pl.ANY)
INSIDE = pl.BlockSpec(memory_space=pltpu.VMEM)


def nn(a, b):
    return lax.dot_general(a, b, (((1,), (0,)), ((), ())), preferred_element_type=F32)


def nt(a, b):
    return lax.dot_general(a, b, (((1,), (1,)), ((), ())), preferred_element_type=F32)


def tn(a, b):
    return lax.dot_general(a, b, (((0,), (0,)), ((), ())), preferred_element_type=F32)


def norm_parts(values):
    average = jnp.mean(values, axis=-1, keepdims=True)
    centered = values - average
    spread = jnp.mean(centered * centered, axis=-1, keepdims=True)
    scale = lax.rsqrt(spread + EPSILON)
    return centered * scale, scale


def norm_back(grad, normal, scale, gain):
    part = grad * gain
    inner = (
        part
        - jnp.mean(part, axis=-1, keepdims=True)
        - normal * jnp.mean(part * normal, axis=-1, keepdims=True)
    )
    return scale * inner, jnp.sum(grad * normal, axis=0)


def places():
    me = lax.axis_index("seq")
    core = lax.rem(me, 2)
    along_x = lax.rem(me // 2, 2)
    along_y = me // 4
    twin = 1 - 2 * core
    near_x = me + 2 - 4 * along_x
    near_y = me + 4 - 8 * along_y
    across = near_x + 4 - 8 * along_y
    return me, twin, near_x, near_y, across


def remote(src, dst, send_sem, recv_sem, partner):
    return pltpu.make_async_remote_copy(
        src_ref=src,
        dst_ref=dst,
        send_sem=send_sem,
        recv_sem=recv_sem,
        device_id={"seq": partner},
        device_id_type=MESH,
    )


def meet(partners):
    barrier = pltpu.get_barrier_semaphore()
    for partner in partners:
        pl.semaphore_signal(
            barrier, inc=1, device_id={"seq": partner}, device_id_type=MESH
        )
    pl.semaphore_wait(barrier, len(partners))


def gather_copies(x_ref, o_ref, send_sem, recv_sem):
    me, twin, near_x, near_y, across = places()
    half = x_ref.shape[0] // 2
    low, high = pl.ds(0, half), pl.ds(half, half)

    def copy(k, src, dst, partner):
        return remote(src, dst, send_sem.at[k], recv_sem.at[k], partner)

    def relay(k, owner, rows, partner):
        place = o_ref.at[owner, rows]
        return copy(k, place, place, partner)

    return [
        copy(0, x_ref.at[low], o_ref.at[me, low], near_x),
        copy(1, x_ref.at[high], o_ref.at[me, high], near_y),
        copy(2, x_ref.at[high], o_ref.at[me, high], near_x),
        copy(3, x_ref.at[low], o_ref.at[me, low], near_y),
        copy(4, x_ref, o_ref.at[me], me + twin),
        relay(5, near_x, low, near_y),
        relay(6, near_y, high, near_x),
        relay(7, near_x, low, me + twin),
        relay(8, near_y, high, me + twin),
        relay(9, near_x, high, me + twin),
        relay(10, near_y, low, me + twin),
        relay(11, across, low, me + twin),
        relay(12, across, high, me + twin),
    ]


def gather_run(sends, *between):
    between = (*between, *([None] * 3))[:3]

    def pause(i):
        if between[i] is not None:
            between[i]()

    sends[0].wait_recv()
    sends[5].start()
    sends[7].start()
    sends[1].wait_recv()
    sends[6].start()
    sends[8].start()
    pause(0)
    sends[2].wait_recv()
    sends[9].start()
    sends[3].wait_recv()
    sends[10].start()
    pause(1)
    sends[5].wait_recv()
    sends[11].start()
    sends[6].wait_recv()
    sends[12].start()
    pause(2)
    for k in (4, 7, 8, 9, 10, 11, 12):
        sends[k].wait_recv()
    for send in sends:
        send.wait_send()


def meet_all(n, depth):
    me = lax.axis_index("seq")
    z = lax.axis_index("batch")
    barrier = pltpu.get_barrier_semaphore()
    for k in range(1, n):
        pl.semaphore_signal(
            barrier, inc=1, device_id={"seq": lax.rem(me + k, n)}, device_id_type=MESH
        )
    for k in range(1, depth):
        pl.semaphore_signal(
            barrier,
            inc=1,
            device_id={"batch": lax.rem(z + k, depth)},
            device_id_type=MESH,
        )
    pl.semaphore_wait(barrier, n + depth - 2)


def line_remote(src, dst, send_sem, recv_sem, partner):
    return pltpu.make_async_remote_copy(
        src_ref=src,
        dst_ref=dst,
        send_sem=send_sem,
        recv_sem=recv_sem,
        device_id={"batch": partner},
        device_id_type=MESH,
    )


class Line:
    def __init__(self, depth, source, target, send_sem, recv_sem):
        self.depth, self.source, self.target = depth, source, target
        self.send_sem, self.recv_sem = send_sem, recv_sem
        self.z = lax.axis_index("batch")

    def message(self, side, k):
        sign = 2 * side - 1
        owner = self.z - sign * k
        return line_remote(
            self.source(owner, k),
            self.target(owner),
            self.send_sem.at[side, k],
            self.recv_sem.at[side, k],
            self.z + sign,
        )

    def sends(self, side, k):
        sign = 2 * side - 1
        owner, target = self.z - sign * k, self.z + sign
        inside = (owner >= 0) & (owner < self.depth)
        return inside & (target >= 0) & (target < self.depth)

    def land(self, k):
        for side in (0, 1):
            sign = 2 * side - 1
            owner = self.z - sign * (k + 1)

            @pl.when((owner >= 0) & (owner < self.depth))
            def _():
                place = self.target(owner)
                line_remote(
                    place,
                    place,
                    self.send_sem.at[side, k],
                    self.recv_sem.at[side, k],
                    self.z - sign,
                ).wait_recv()

    def start(self, k):
        for side in (0, 1):

            @pl.when(self.sends(side, k))
            def _():
                self.message(side, k).start()

    def sent(self, k):
        for side in (0, 1):

            @pl.when(self.sends(side, k))
            def _():
                self.message(side, k).wait_send()


def lane_tables(place):
    half = HEAD_DIM // 2
    lane = lax.broadcasted_iota(jnp.int32, (1, 128), 1)
    channel = lax.rem(lane, half).astype(F32)
    inverse = jnp.exp(channel * (-math.log(10000.0) / half))
    zeta = (channel * (2.0 / HEAD_DIM) + 0.4) / 1.4
    sign = jnp.where(lax.rem(lane, HEAD_DIM) < half, -1.0, 1.0)
    angle = place * inverse
    growth = jnp.exp((place - 0.5 * LENGTH) * (1.0 / XBASE) * jnp.log(zeta))
    shrink = 1.0 / growth
    cosine = jnp.cos(angle)
    sine = jnp.sin(angle) * sign
    return cosine * growth, sine * growth, cosine * shrink, sine * shrink


def start_kernel(
    n, depth, x_ref, gain_ref, w_ref, wd_ref, pos_ref,
    o_ref, wt_ref, wc_ref, cq_ref, sq_ref, ck_ref, sk_ref,
    normed, keep_w, keep_c, local_sem, send_sem, recv_sem, hop_send, hop_recv, col_send, col_recv,
    line_send, line_recv,
):
    z = lax.axis_index("batch")
    rows_z = wc_ref.shape[2]
    cols = wc_ref.shape[3]
    me, twin, near_x, near_y, _ = places()
    own = pltpu.make_async_copy(normed, o_ref.at[me], local_sem.at[0])
    wd_rows = pl.ds(pl.multiple_of(z * rows_z, rows_z), rows_z)

    def column(k):
        return wd_ref.at[wd_rows, pl.ds(pl.multiple_of(k * cols, cols), cols)]

    load_column = pltpu.make_async_copy(column(me), keep_c, local_sem.at[4])
    own_column = pltpu.make_async_copy(keep_c, wc_ref.at[me, z], local_sem.at[5])
    load_column.start()
    meet_all(n, depth)
    load_column.wait()
    own_column.start()

    def hop(j, part, target):
        return remote(
            w_ref.at[j], wt_ref.at[part], hop_send.at[j], hop_recv.at[part], target
        )

    def load(j):
        return pltpu.make_async_copy(w_ref.at[j], keep_w, local_sem.at[6])

    def here(j, part):
        return pltpu.make_async_copy(keep_w, wt_ref.at[part], local_sem.at[1 + j])

    turns = [
        remote(
            column(lax.rem(me + k, n)),
            wc_ref.at[me, z],
            col_send.at[k],
            col_recv.at[k],
            lax.rem(me + k, n),
        )
        for k in range(1, n)
    ]
    for turn in turns:
        turn.start()

    @pl.loop(0, x_ref.shape[0] // STEP)
    def _(r):
        at = pl.ds(pl.multiple_of(r * STEP, STEP), STEP)
        normal, _ = norm_parts(x_ref[at].astype(F32))
        normed[at] = (normal * gain_ref[...]).astype(BF16)

    own.start()
    sends = gather_copies(normed, o_ref, send_sem, recv_sem)
    for k in range(5):
        sends[k].start()
    for j in range(3):
        block = 3 * me + j
        target = lax.rem(block, n)
        for part in range(3):
            inside = block // n == part

            @pl.when(inside & (target != me))
            def _():
                hop(j, part, target).start()

            @pl.when(inside & (target == me))
            def _():
                load(j).start()

    line = Line(
        depth,
        lambda owner, k: wc_ref.at[:, owner],
        lambda owner: wc_ref.at[:, owner],
        line_send,
        line_recv,
    )

    own_column.wait()
    for turn in turns:
        turn.wait_recv()
    line.start(0)
    for j in range(3):
        block = 3 * me + j
        target = lax.rem(block, n)
        for part in range(3):

            @pl.when((block // n == part) & (target == me))
            def _():
                load(j).wait()
                here(j, part).start()

    @pl.loop(0, pos_ref.shape[0])
    def _(r):
        at = pl.ds(pl.multiple_of(r * 128, 128), 128)
        places_here = jnp.broadcast_to(pos_ref[pl.ds(r, 1), :], (128, 128)).T
        tables = lane_tables(places_here)
        for ref, table in zip((cq_ref, sq_ref, ck_ref, sk_ref), tables, strict=True):
            ref[at] = table

    def hand_on(k):
        def step():
            line.land(k - 1)
            line.start(k)

        return step

    hand_on(1)()
    gather_run(sends, *[hand_on(k) for k in range(2, depth - 1)])
    line.land(depth - 2)
    for k in range(depth - 1):
        line.sent(k)
    for turn in turns:
        turn.wait_send()
    for j in range(3):
        block = 3 * me + j
        target = lax.rem(block, n)
        for part in range(3):
            inside = block // n == part

            @pl.when(inside & (target != me))
            def _():
                hop(j, part, target).wait_send()

            @pl.when(inside & (target == me))
            def _():
                here(j, part).wait()

    for part in range(3):
        source = (part * n + me) // 3

        @pl.when(source != me)
        def _():
            hop(0, part, source).wait_recv()

    own.wait()


def start_exchange(block, gain, w_qkv, w_down, positions, collective_id):
    n, depth = lax.axis_size("seq"), lax.axis_size("batch")
    rows, width = block.shape
    piece = w_qkv.shape[0] // 3
    w = w_qkv.reshape(3, piece, width)
    if n != 8:
        me = lax.axis_index("seq")
        turned = [
            lax.ppermute(w[j], "seq", [(d, (3 * d + j) % n) for d in range(n)])
            for j in range(3)
        ]
        parts = [pick_part(turned, me, n, part) for part in range(3)]
        place = jnp.broadcast_to(positions[:, None], (positions.shape[0], 128))
        normed = (norm_parts(block.astype(F32))[0] * gain).astype(BF16)
        return (
            lax.all_gather(normed, "seq", axis=0, tiled=True),
            jnp.concatenate(parts, axis=0),
            lax.all_to_all(w_down, "seq", split_axis=1, concat_axis=0, tiled=True),
            lane_tables(place),
        )
    rows_z, cols = w_down.shape[0] // depth, w_down.shape[1] // n
    inside = pl.BlockSpec(memory_space=pltpu.VMEM)
    table = jax.ShapeDtypeStruct((n * rows, 128), F32)
    gathered, turned, columns, *tables = pl.pallas_call(
        functools.partial(start_kernel, n, depth),
        out_shape=(
            jax.ShapeDtypeStruct((n, rows, width), block.dtype),
            jax.ShapeDtypeStruct((3, piece, width), w.dtype),
            jax.ShapeDtypeStruct((n, depth, rows_z, cols), w_down.dtype),
            *([table] * 4),
        ),
        in_specs=[INSIDE, INSIDE, ANY, ANY, INSIDE],
        out_specs=(ANY, ANY, ANY, *([INSIDE] * 4)),
        scratch_shapes=[
            pltpu.VMEM((rows, width), BF16),
            pltpu.VMEM((piece, width), BF16),
            pltpu.VMEM((rows_z, cols), BF16),
            pltpu.SemaphoreType.DMA((7,)),
            pltpu.SemaphoreType.DMA((13,)),
            pltpu.SemaphoreType.DMA((13,)),
            pltpu.SemaphoreType.DMA((3,)),
            pltpu.SemaphoreType.DMA((3,)),
            pltpu.SemaphoreType.DMA((n,)),
            pltpu.SemaphoreType.DMA((n,)),
            pltpu.SemaphoreType.DMA((2, depth)),
            pltpu.SemaphoreType.DMA((2, depth)),
        ],
        compiler_params=pltpu.CompilerParams(
            collective_id=collective_id, has_side_effects=True, vmem_limit_bytes=VMEM_LIMIT
        ),
        name="start_exchange",
    )(block, gain[None], w, w_down, positions.reshape(-1, 128))
    return (
        gathered.reshape(n * rows, width),
        turned.reshape(3 * piece, width),
        columns.reshape(-1, cols),
        tables,
    )


def scatter_seq(partial):
    return lax.psum_scatter(partial, "seq", scatter_dimension=0, tiled=True).astype(F32)


def heads_to_tokens_kernel(n, x_ref, o_ref, keep, local_sem, send_sem, recv_sem):
    me = lax.axis_index("seq")
    rows = o_ref.shape[0]
    cols = x_ref.shape[1]
    exchange(
        n,
        me,
        lambda k: x_ref.at[pl.ds(pl.multiple_of(k * rows, rows), rows)],
        o_ref.at[:, pl.ds(pl.multiple_of(me * cols, cols), cols)],
        keep,
        local_sem,
        send_sem,
        recv_sem,
    )


def exchange(n, me, source, target, keep, local_sem, send_sem, recv_sem):
    load = pltpu.make_async_copy(source(me), keep, local_sem.at[0])
    own = pltpu.make_async_copy(keep, target, local_sem.at[1])
    load.start()
    barrier = pltpu.get_barrier_semaphore()
    for k in range(1, n):
        pl.semaphore_signal(
            barrier,
            inc=1,
            device_id={"seq": lax.rem(me + k, n)},
            device_id_type=MESH,
        )
    pl.semaphore_wait(barrier, n - 1)
    copies = []
    for k in range(1, n):
        partner = lax.rem(me + k, n)
        copies.append(
            pltpu.make_async_remote_copy(
                src_ref=source(partner),
                dst_ref=target,
                send_sem=send_sem.at[k],
                recv_sem=recv_sem.at[k],
                device_id={"seq": partner},
                device_id_type=MESH,
            )
        )
        copies[-1].start()
    load.wait()
    own.start()
    for copy in copies:
        copy.wait()
    own.wait()


def heads_to_tokens(heads, collective_id):
    n = lax.axis_size("seq")
    total, cols = heads.shape
    rows = total // n
    return pl.pallas_call(
        functools.partial(heads_to_tokens_kernel, n),
        out_shape=jax.ShapeDtypeStruct((rows, n * cols), heads.dtype),
        in_specs=[ANY],
        out_specs=ANY,
        scratch_shapes=[
            pltpu.VMEM((rows, cols), heads.dtype),
            pltpu.SemaphoreType.DMA((2,)),
            pltpu.SemaphoreType.DMA((n,)),
            pltpu.SemaphoreType.DMA((n,)),
        ],
        compiler_params=pltpu.CompilerParams(
            collective_id=collective_id, has_side_effects=True, vmem_limit_bytes=VMEM_LIMIT
        ),
        name="heads_to_tokens",
    )(heads)


def tokens_to_heads_kernel(n, x_ref, o_ref, keep, local_sem, send_sem, recv_sem):
    me = lax.axis_index("seq")
    rows = x_ref.shape[0]
    cols = o_ref.shape[1]
    exchange(
        n,
        me,
        lambda k: x_ref.at[:, pl.ds(pl.multiple_of(k * cols, cols), cols)],
        o_ref.at[pl.ds(pl.multiple_of(me * rows, rows), rows)],
        keep,
        local_sem,
        send_sem,
        recv_sem,
    )


def tokens_to_heads(tokens, collective_id):
    n = lax.axis_size("seq")
    rows, total = tokens.shape
    return pl.pallas_call(
        functools.partial(tokens_to_heads_kernel, n),
        out_shape=jax.ShapeDtypeStruct((rows * n, total // n), tokens.dtype),
        in_specs=[ANY],
        out_specs=ANY,
        scratch_shapes=[
            pltpu.VMEM((rows, total // n), tokens.dtype),
            pltpu.SemaphoreType.DMA((2,)),
            pltpu.SemaphoreType.DMA((n,)),
            pltpu.SemaphoreType.DMA((n,)),
        ],
        compiler_params=pltpu.CompilerParams(
            collective_id=collective_id, has_side_effects=True, vmem_limit_bytes=VMEM_LIMIT
        ),
        name="tokens_to_heads",
    )(tokens)


def swap_halves(values):
    width = values.shape[-1]
    half = HEAD_DIM // 2
    lane = lax.broadcasted_iota(jnp.int32, values.shape, 1)
    ahead = pltpu.roll(values, width - half, 1)
    behind = pltpu.roll(values, half, 1)
    return jnp.where(lane % HEAD_DIM < half, ahead, behind)


def spread_lanes(table, width):
    return jnp.concatenate([table] * (width // table.shape[-1]), axis=-1)


def qkv_kernel(
    x_ref, w_ref, cq_ref, sq_ref, ck_ref, sk_ref,
    q_ref, k_ref, v_ref, kt_ref, vt_ref,
):
    x = x_ref[...]
    width = q_ref.shape[1]
    query = nt(x, w_ref[0:width])
    query = query * spread_lanes(cq_ref[...], width) + swap_halves(
        query
    ) * spread_lanes(sq_ref[...], width)
    q_ref[...] = query.astype(BF16) * (HEAD_DIM**-0.5)
    keys = nt(x, w_ref[width : 2 * width])
    keys = keys * spread_lanes(ck_ref[...], width) + swap_halves(
        keys
    ) * spread_lanes(sk_ref[...], width)
    k_ref[...] = keys.astype(BF16)
    kt_ref[...] = keys.T.astype(BF16)
    values = nt(x, w_ref[2 * width :])
    v_ref[...] = values.astype(BF16)
    vt_ref[...] = values.T.astype(BF16)


def project_qkv(x, w, tables):
    length, width = x.shape
    cols = w.shape[0] // 3
    tile = 2 * TILE
    steps = length // tile
    weight = pl.BlockSpec((3 * cols, width), lambda i: (0, 0))
    table = pl.BlockSpec((tile, tables[0].shape[1]), lambda i: (i, 0))
    row_out = pl.BlockSpec((tile, cols), lambda i: (i, 0))
    col_out = pl.BlockSpec((cols, tile), lambda i: (0, i))
    rows = jax.ShapeDtypeStruct((length, cols), BF16)
    columns = jax.ShapeDtypeStruct((cols, length), BF16)
    return pl.pallas_call(
        qkv_kernel,
        grid=(steps,),
        out_shape=(rows, rows, rows, columns, columns),
        in_specs=[pl.BlockSpec((tile, width), lambda i: (i, 0))]
        + [weight]
        + [table] * 4,
        out_specs=(row_out, row_out, row_out, col_out, col_out),
        compiler_params=pltpu.CompilerParams(vmem_limit_bytes=VMEM_LIMIT),
        cost_estimate=pl.CostEstimate(
            flops=6 * length * width * cols,
            bytes_accessed=2 * length * width + 6 * width * cols + 10 * length * cols,
            transcendentals=0,
        ),
        name="project_qkv",
    )(x, w, *tables)


def pair_mask(start_row, i, j):
    key_place = j * TILE + lax.broadcasted_iota(jnp.int32, (TILE, TILE), 0)
    query_place = i * TILE + lax.broadcasted_iota(jnp.int32, (TILE, TILE), 1)
    return (key_place <= query_place) & (key_place >= start_row)


def head_rows(query, heads):
    lane = lax.broadcasted_iota(jnp.int32, query.shape, 1) // HEAD_DIM
    zero = jnp.zeros_like(query)
    return [jnp.where(lane == h, query, zero) for h in range(heads)]


def attend_kernel(
    heads, first_ref, start_ref, q_ref, k_ref, vt_ref, o_ref, lse_ref, peak, total, mixed
):
    i = pl.program_id(0)
    queries = head_rows(q_ref[...], heads)
    start_row = start_ref[...]

    def block(j, first):
        at = pl.ds(pl.multiple_of(j * TILE, TILE), TILE)
        keys = k_ref[at, :]
        mask = pair_mask(start_row, i, j)
        for h in range(heads):
            here = slice(h * HEAD_DIM, (h + 1) * HEAD_DIM)
            scores = jnp.where(mask, nt(keys, queries[h]), MASKED)
            if first:
                new_peak = jnp.max(scores, axis=0, keepdims=True)
                expo = jnp.exp(scores - new_peak)
                total[h : h + 1] = jnp.sum(expo, axis=0, keepdims=True)
                mixed[here] = nn(vt_ref[here, at], expo.astype(BF16))
            else:
                old_peak = peak[h : h + 1]
                new_peak = jnp.maximum(old_peak, jnp.max(scores, axis=0, keepdims=True))
                expo = jnp.exp(scores - new_peak)
                shrink = jnp.exp(old_peak - new_peak)
                total[h : h + 1] = total[h : h + 1] * shrink + jnp.sum(
                    expo, axis=0, keepdims=True
                )
                mixed[here] = mixed[here] * shrink + nn(
                    vt_ref[here, at], expo.astype(BF16)
                )
            peak[h : h + 1] = new_peak

    block(i, True)

    @pl.loop(0, i - first_ref[i])
    def _(t):
        block(i - 1 - t, False)

    for h in range(heads):
        here = slice(h * HEAD_DIM, (h + 1) * HEAD_DIM)
        mixed[here] = mixed[here] / total[h : h + 1]
    o_ref[...] = mixed[...].T.astype(BF16)
    lse_ref[0] = peak[...] + jnp.log(total[...])


def attend(first, start, q, k, vt):
    length, cols = q.shape
    heads = cols // HEAD_DIM
    steps = length // TILE
    row = pl.BlockSpec((TILE, cols), lambda i, *_: (i, 0))
    return pl.pallas_call(
        functools.partial(attend_kernel, heads),
        out_shape=(
            jax.ShapeDtypeStruct((length, cols), BF16),
            jax.ShapeDtypeStruct((steps, heads, TILE), F32),
        ),
        grid_spec=pltpu.PrefetchScalarGridSpec(
            num_scalar_prefetch=1,
            grid=(steps,),
            in_specs=[
                pl.BlockSpec((1, TILE), lambda i, *_: (0, i)),
                row,
                pl.BlockSpec((length, cols), lambda i, *_: (0, 0)),
                pl.BlockSpec((cols, length), lambda i, *_: (0, 0)),
            ],
            out_specs=(
                row,
                pl.BlockSpec((1, heads, TILE), lambda i, *_: (i, 0, 0)),
            ),
            scratch_shapes=[
                pltpu.VMEM((heads, TILE), F32),
                pltpu.VMEM((heads, TILE), F32),
                pltpu.VMEM((cols, TILE), F32),
            ],
        ),
        compiler_params=pltpu.CompilerParams(vmem_limit_bytes=VMEM_LIMIT),
        cost_estimate=pl.CostEstimate(
            flops=4 * length * 1024 * cols,
            bytes_accessed=8 * length * cols,
            transcendentals=length * 1024 * heads,
        ),
        name="attend",
    )(first, start, q, k, vt)


def attend_back_kernel(
    heads, first_ref, start_ref, q_ref, k_ref, kt_ref, v_ref, o_ref, lse_ref, do_ref,
    cq_ref, sq_ref, ck_ref, sk_ref, grad_ref, dqt, dk_sum, dv_sum,
):
    i = pl.program_id(0)
    steps = pl.num_programs(0)
    width = q_ref.shape[1]
    queries = head_rows(q_ref[...], heads)
    grads = head_rows(do_ref[...], heads)
    start_row = start_ref[...]
    product = (do_ref[...].astype(F32) * o_ref[...].astype(F32)).T
    inner = [
        jnp.sum(product[h * HEAD_DIM : (h + 1) * HEAD_DIM], axis=0, keepdims=True)
        for h in range(heads)
    ]

    def block(j, first):
        at = pl.ds(pl.multiple_of(j * TILE, TILE), TILE)
        keys = k_ref[at, :]
        values = v_ref[at, :]
        mask = pair_mask(start_row, i, j)
        key_term = None
        value_term = None
        for h in range(heads):
            here = slice(h * HEAD_DIM, (h + 1) * HEAD_DIM)
            scores = nt(keys, queries[h])
            weights = jnp.where(mask, jnp.exp(scores - lse_ref[0, h : h + 1]), 0.0)
            grad_weights = nt(values, grads[h])
            grad_scores = (weights * (grad_weights - inner[h])).astype(BF16)
            term = nn(weights.astype(BF16), grads[h])
            value_term = term if value_term is None else value_term + term
            term = nn(grad_scores, queries[h])
            key_term = term if key_term is None else key_term + term
            term = nn(kt_ref[here, at], grad_scores)
            if first:
                dqt[here] = term
            else:
                dqt[here] = dqt[here] + term
        if first:
            dk_sum[at] = key_term
            dv_sum[at] = value_term
        else:
            dk_sum[at] = dk_sum[at] + key_term
            dv_sum[at] = dv_sum[at] + value_term

    block(i, True)

    @pl.loop(0, i - first_ref[i])
    def _(t):
        block(i - 1 - t, False)

    def unturn(grad, cosine, sine):
        grad = grad.astype(BF16).astype(F32)
        cosine = spread_lanes(cosine, width)
        sine = spread_lanes(sine, width)
        return (grad * cosine - swap_halves(grad) * sine).astype(BF16)

    rows = pl.ds(pl.multiple_of(i * TILE, TILE), TILE)
    grad_ref[rows, 0:width] = unturn(
        dqt[...].T * (HEAD_DIM**-0.5), cq_ref[rows, :], sq_ref[rows, :]
    )

    @pl.when(i == steps - 1)
    def _():
        @pl.loop(0, steps)
        def _(j):
            at = pl.ds(pl.multiple_of(j * TILE, TILE), TILE)
            grad_ref[at, width : 2 * width] = unturn(
                dk_sum[at], ck_ref[at, :], sk_ref[at, :]
            )
            grad_ref[at, 2 * width :] = dv_sum[at].astype(BF16)


def attend_back(first, start, q, k, kt, v, o, lse, do, tables):
    length, cols = q.shape
    heads = cols // HEAD_DIM
    steps = length // TILE
    row = pl.BlockSpec((TILE, cols), lambda i, *_: (i, 0))
    whole = pl.BlockSpec((length, cols), lambda i, *_: (0, 0))
    table = pl.BlockSpec((length, tables[0].shape[1]), lambda i, *_: (0, 0))
    return pl.pallas_call(
        functools.partial(attend_back_kernel, heads),
        out_shape=jax.ShapeDtypeStruct((length, 3 * cols), BF16),
        grid_spec=pltpu.PrefetchScalarGridSpec(
            num_scalar_prefetch=1,
            grid=(steps,),
            in_specs=[
                pl.BlockSpec((1, TILE), lambda i, *_: (0, i)),
                row,
                whole,
                pl.BlockSpec((cols, length), lambda i, *_: (0, 0)),
                whole,
                row,
                pl.BlockSpec((1, heads, TILE), lambda i, *_: (i, 0, 0)),
                row,
            ]
            + [table] * 4,
            out_specs=pl.BlockSpec((length, 3 * cols), lambda i, *_: (0, 0)),
            scratch_shapes=[
                pltpu.VMEM((cols, TILE), F32),
                pltpu.VMEM((length, cols), F32),
                pltpu.VMEM((length, cols), F32),
            ],
        ),
        compiler_params=pltpu.CompilerParams(vmem_limit_bytes=VMEM_LIMIT),
        name="attend_back",
    )(first, start, q, k, kt, v, o, lse, do, *tables)


def upper_kernel(
    x_ref, wu_ref, c_ref, wd_ref, gain_ref, act_ref, slope_ref, grad_ref, stat_ref
):
    upper = nt(x_ref[...], wu_ref[...])
    grad = nn(c_ref[...], wd_ref[...])
    below = 0.5 * (1.0 + lax.erf(upper * (0.5**0.5)))
    act = upper * below
    slope = below + upper * (jnp.exp(-0.5 * upper * upper) * ((2.0 * math.pi) ** -0.5))
    act_ref[...] = act
    slope_ref[...] = slope.astype(BF16)
    grad_ref[...] = grad
    part = grad * gain_ref[...]
    average = jnp.mean(act, axis=-1, keepdims=True)
    centered = act - average
    spread = jnp.sum(centered * centered, axis=-1, keepdims=True)
    part_sum = jnp.sum(part, axis=-1, keepdims=True)
    cross = jnp.sum(part * centered, axis=-1, keepdims=True)
    lane = lax.broadcasted_iota(jnp.int32, (x_ref.shape[0], 128), 1)
    columns = jnp.where(
        lane == 0,
        average,
        jnp.where(lane == 1, spread, jnp.where(lane == 2, part_sum, cross)),
    )
    stat_ref[...] = columns.T[:8]


def upper_pass(x, w_up, cot, w_down, gain):
    length, width = x.shape
    feats = w_up.shape[0]
    rows = TILE
    row = pl.BlockSpec((rows, width), lambda i: (i, 0))
    out = pl.BlockSpec((rows, feats), lambda i: (i, 0))
    return pl.pallas_call(
        upper_kernel,
        grid=(length // rows,),
        out_shape=(
            jax.ShapeDtypeStruct((length, feats), F32),
            jax.ShapeDtypeStruct((length, feats), BF16),
            jax.ShapeDtypeStruct((length, feats), F32),
            jax.ShapeDtypeStruct((8, length), F32),
        ),
        in_specs=[
            row,
            pl.BlockSpec((feats, width), lambda i: (0, 0)),
            row,
            pl.BlockSpec((width, feats), lambda i: (0, 0)),
            pl.BlockSpec((1, feats), lambda i: (0, 0)),
        ],
        out_specs=(out, out, out, pl.BlockSpec((8, rows), lambda i: (0, i))),
        compiler_params=pltpu.CompilerParams(vmem_limit_bytes=VMEM_LIMIT),
        cost_estimate=pl.CostEstimate(
            flops=4 * length * width * feats,
            bytes_accessed=8 * length * width + 8 * length * feats,
            transcendentals=2 * length * feats,
        ),
        name="upper_pass",
    )(x, w_up, cot, w_down, gain)


def hidden_kernel(act_ref, slope_ref, grad_ref, stat_ref, gain_ref, hid_ref, gu_ref, gg_ref):
    i = pl.program_id(0)
    stats = stat_ref[...].T
    average = stats[:, 0:1]
    scale = stats[:, 1:2]
    part_mean = stats[:, 2:3]
    cross_mean = stats[:, 3:4]
    gain = gain_ref[...]
    normal = (act_ref[...] - average) * scale
    grad = grad_ref[...]
    hid_ref[...] = (normal * gain).astype(BF16)
    back = scale * (grad * gain - part_mean - normal * cross_mean)
    gu_ref[...] = (slope_ref[...].astype(F32) * back).astype(BF16)
    term = jnp.sum(grad * normal, axis=0, keepdims=True)

    @pl.when(i == 0)
    def _():
        gg_ref[...] = term

    @pl.when(i > 0)
    def _():
        gg_ref[...] = gg_ref[...] + term


def hidden_pass(act, slope, grad, stats, gain):
    length, feats = act.shape
    out = pl.BlockSpec((TILE, feats), lambda i: (i, 0))
    one = pl.BlockSpec((1, feats), lambda i: (0, 0))
    return pl.pallas_call(
        hidden_kernel,
        grid=(length // TILE,),
        out_shape=(
            jax.ShapeDtypeStruct((length, feats), BF16),
            jax.ShapeDtypeStruct((length, feats), BF16),
            jax.ShapeDtypeStruct((1, feats), F32),
        ),
        in_specs=[out, out, out, pl.BlockSpec((8, TILE), lambda i: (0, i)), one],
        out_specs=(out, out, one),
        compiler_params=pltpu.CompilerParams(vmem_limit_bytes=VMEM_LIMIT),
        cost_estimate=pl.CostEstimate(
            flops=12 * length * feats,
            bytes_accessed=14 * length * feats,
            transcendentals=0,
        ),
        name="hidden_pass",
    )(act, slope, grad, stats, gain)


def ffn_kernel(
    n, x_ref, wu_ref, cot_ref, wd_ref, gain_ref,
    full_ref, hid_ref, gu_ref, gg_ref,
    rows_in, wd, cot_in, act, slope, grad, stat, held, results,
    local_sem, cot_sem, out_sem, full_sem, send_sem, recv_sem, stat_send, stat_recv,
):
    me, twin, near_x, near_y, across = places()
    rows = x_ref.shape[0]
    feats = wu_ref.shape[0]

    def cut(i, size=rows):
        return pl.ds(pl.multiple_of(i * size, size), size)

    own = pltpu.make_async_copy(x_ref, rows_in.at[me], local_sem.at[0])
    own.start()
    load_wd = pltpu.make_async_copy(wd_ref, wd, local_sem.at[1])
    load_wd.start()

    def load_cot(i, slot):
        return pltpu.make_async_copy(
            cot_ref.at[cut(i, 2 * rows)], cot_in.at[slot], cot_sem.at[slot]
        )

    load_cot(0, 0).start()
    meet([lax.rem(me + k, n) for k in range(1, n)])
    sends = gather_copies(x_ref, rows_in, send_sem, recv_sem)
    for k in range(5):
        sends[k].start()

    load_wd.wait()
    def incoming(first, last):
        @pl.loop(first, last)
        def _(i):
            slot = lax.rem(i, 2)

            @pl.when(i + 1 < n // 2)
            def _():
                load_cot(i + 1, 1 - slot).start()

            load_cot(i, slot).wait()
            grad[cut(i, 2 * rows)] = nn(cot_in[slot], wd[...])

    incoming(0, n // 2 - 1)
    sends[0].wait_recv()
    sends[5].start()
    sends[7].start()
    sends[1].wait_recv()
    sends[6].start()
    sends[8].start()
    incoming(n // 2 - 1, n // 2)
    own.wait()

    def keep(b):
        return pltpu.make_async_copy(rows_in.at[b], full_ref.at[b], full_sem.at[b])

    @pl.loop(0, n)
    def _(i):
        @pl.when(i == 1)
        def _():
            sends[4].wait_recv()

        @pl.when(i == 2)
        def _():
            sends[2].wait_recv()
            sends[9].start()
            sends[3].wait_recv()
            sends[10].start()

        @pl.when(i == 4)
        def _():
            sends[7].wait_recv()
            sends[9].wait_recv()

        @pl.when(i == 5)
        def _():
            sends[8].wait_recv()
            sends[10].wait_recv()
            sends[5].wait_recv()
            sends[11].start()
            sends[6].wait_recv()
            sends[12].start()

        @pl.when(i == 7)
        def _():
            sends[11].wait_recv()
            sends[12].wait_recv()

        other = jnp.where((i == 1) | (i == 4) | (i == 5) | (i == 7), twin, 0)
        place = jnp.where(i < 2, me, jnp.where(i >= 6, across, jnp.where(lax.rem(i, 2) == 0, near_x, near_y)))
        b = place + other
        keep(b).start()
        at = cut(b)
        upper = nt(rows_in[b], wu_ref[...])
        below = 0.5 * (1.0 + lax.erf(upper * (0.5**0.5)))
        value = upper * below
        act[at] = value
        slope[at] = (
            below + upper * (jnp.exp(-0.5 * upper * upper) * ((2.0 * math.pi) ** -0.5))
        ).astype(BF16)
        part = grad[at] * gain_ref[...]
        average = jnp.mean(value, axis=-1, keepdims=True)
        centered = value - average
        spread = jnp.sum(centered * centered, axis=-1, keepdims=True)
        part_sum = jnp.sum(part, axis=-1, keepdims=True)
        cross = jnp.sum(part * centered, axis=-1, keepdims=True)
        lane = lax.broadcasted_iota(jnp.int32, (rows, 128), 1)
        columns = jnp.where(
            lane == 0,
            average,
            jnp.where(lane == 1, spread, jnp.where(lane == 2, part_sum, cross)),
        )
        stat[:, at] = columns.T[:8]

    held[me] = stat[...]
    rounds = [
        remote(
            stat, held.at[me], stat_send.at[k], stat_recv.at[k], lax.rem(me + k, n)
        )
        for k in range(1, n)
    ]
    for send in rounds:
        send.start()
    for send in rounds:
        send.wait()
    join_rows(n, feats, held, stat)

    def store(i, slot):
        return [
            pltpu.make_async_copy(
                results.at[slot, j], ref.at[cut(i)], out_sem.at[slot, j]
            )
            for j, ref in enumerate((hid_ref, gu_ref))
        ]

    gg_ref[...] = jnp.zeros_like(gg_ref)

    @pl.loop(0, n)
    def _(i):
        slot = lax.rem(i, 2)

        @pl.when(i >= 2)
        def _():
            for copy in store(i - 2, slot):
                copy.wait()

        at = cut(i)
        stats = stat[:, at].T
        gain = gain_ref[...]
        scale = stats[:, 1:2]
        normal = (act[at] - stats[:, 0:1]) * scale
        coming = grad[at]
        results[slot, 0] = (normal * gain).astype(BF16)
        back = scale * (coming * gain - stats[:, 2:3] - normal * stats[:, 3:4])
        results[slot, 1] = (slope[at].astype(F32) * back).astype(BF16)
        gg_ref[...] = gg_ref[...] + jnp.sum(coming * normal, axis=0, keepdims=True)
        for copy in store(i, slot):
            copy.start()

    for i in (n - 2, n - 1):
        for copy in store(i, i % 2):
            copy.wait()
    for b in range(n):
        keep(b).wait()
    for send in sends:
        send.wait_send()


def ffn_pass(ffn_in, w_up, cot, w_down, gain, collective_id):
    n = lax.axis_size("seq")
    rows, width = ffn_in.shape
    feats = w_up.shape[0]
    if n != 8:
        full = lax.all_gather(ffn_in, "seq", axis=0, tiled=True)
        act, slope, grad, stat = upper_pass(full, w_up, cot, w_down, gain)
        stats = join_stats(stat, feats, collective_id)
        return (full, *hidden_pass(act, slope, grad, stats, gain))
    length = n * rows
    dma = pltpu.SemaphoreType.DMA
    low = jax.ShapeDtypeStruct((length, feats), BF16)
    full, hidden, grad_upper, gain_grad = pl.pallas_call(
        functools.partial(ffn_kernel, n),
        out_shape=(
            jax.ShapeDtypeStruct((n, rows, width), BF16),
            low,
            low,
            jax.ShapeDtypeStruct((1, feats), F32),
        ),
        in_specs=[INSIDE, INSIDE, ANY, ANY, INSIDE],
        out_specs=(ANY, ANY, ANY, INSIDE),
        scratch_shapes=[
            pltpu.VMEM((n, rows, width), BF16),
            pltpu.VMEM((width, feats), BF16),
            pltpu.VMEM((2, 2 * rows, width), BF16),
            pltpu.VMEM((length, feats), F32),
            pltpu.VMEM((length, feats), BF16),
            pltpu.VMEM((length, feats), F32),
            pltpu.VMEM((8, length), F32),
            pltpu.VMEM((n, 8, length), F32),
            pltpu.VMEM((2, 2, rows, feats), BF16),
            dma((2,)),
            dma((2,)),
            dma((2, 2)),
            dma((n,)),
            dma((13,)),
            dma((13,)),
            dma((n,)),
            dma((n,)),
        ],
        compiler_params=pltpu.CompilerParams(
            collective_id=collective_id, has_side_effects=True, vmem_limit_bytes=VMEM_LIMIT
        ),
        name="ffn_pass",
    )(ffn_in, w_up, cot, w_down, gain)
    return full.reshape(length, width), hidden, grad_upper, gain_grad


def join_rows(n, feats, held, o_ref):
    average = held[0, 0:1]
    for d in range(1, n):
        average = average + held[d, 0:1]
    average = average * (1.0 / n)
    spread = jnp.zeros_like(average)
    part = jnp.zeros_like(average)
    cross = jnp.zeros_like(average)
    for d in range(n):
        shift = held[d, 0:1] - average
        spread = spread + held[d, 1:2] + feats * (shift * shift)
        part = part + held[d, 2:3]
        cross = cross + held[d, 3:4] + shift * held[d, 2:3]
    whole = 1.0 / (n * feats)
    scale = lax.rsqrt(spread * whole + EPSILON)
    o_ref[0:1] = average
    o_ref[1:2] = scale
    o_ref[2:3] = part * whole
    o_ref[3:4] = cross * scale * whole
    o_ref[4:8] = jnp.zeros((4, average.shape[1]), F32)


def stat_kernel(n, feats, x_ref, o_ref, held, send_sem, recv_sem):
    me = lax.axis_index("seq")
    held[me] = x_ref[...]
    meet([lax.rem(me + k, n) for k in range(1, n)])
    copies = [
        remote(x_ref, held.at[me], send_sem.at[k], recv_sem.at[k], lax.rem(me + k, n))
        for k in range(1, n)
    ]
    for copy in copies:
        copy.start()
    for copy in copies:
        copy.wait()
    join_rows(n, feats, held, o_ref)


def join_stats(stat, feats, collective_id):
    n = lax.axis_size("seq")
    inside = pl.BlockSpec(memory_space=pltpu.VMEM)
    return pl.pallas_call(
        functools.partial(stat_kernel, n, feats),
        out_shape=jax.ShapeDtypeStruct(stat.shape, F32),
        in_specs=[inside],
        out_specs=inside,
        scratch_shapes=[
            pltpu.VMEM((n, *stat.shape), F32),
            pltpu.SemaphoreType.DMA((n,)),
            pltpu.SemaphoreType.DMA((n,)),
        ],
        compiler_params=pltpu.CompilerParams(
            collective_id=collective_id, has_side_effects=True, vmem_limit_bytes=VMEM_LIMIT
        ),
        name="join_stats",
    )(stat)


def mix_kernel(att_ref, x_ref, w_ref, gm_ref, gf_ref, mix_ref, mid_ref, ffn_ref):
    j = pl.program_id(0)
    rows = att_ref.shape[0]
    cols = w_ref.shape[0]

    @pl.when(j == 0)
    def _():
        @pl.loop(0, rows // STEP)
        def _(r):
            at = pl.ds(pl.multiple_of(r * STEP, STEP), STEP)
            normal, _ = norm_parts(att_ref[at].astype(F32))
            mix_ref[at] = (normal * gm_ref[...]).astype(BF16)

    here = pl.ds(pl.multiple_of(j * cols, cols), cols)
    mid_ref[:, here] = x_ref[:, here].astype(F32) + nt(mix_ref[...], w_ref[...])

    @pl.when(j == pl.num_programs(0) - 1)
    def _():
        @pl.loop(0, rows // STEP)
        def _(r):
            at = pl.ds(pl.multiple_of(r * STEP, STEP), STEP)
            normal, _ = norm_parts(mid_ref[at])
            ffn_ref[at] = (normal * gf_ref[...]).astype(BF16)


def mix_pass(attended, x, w_out, gain_mix, gain_ffn):
    rows, width = x.shape
    cols = 2 * TILE
    n = width // cols
    whole = pl.BlockSpec((rows, width), lambda j: (0, 0))
    gain = pl.BlockSpec((1, width), lambda j: (0, 0))
    low = jax.ShapeDtypeStruct((rows, width), BF16)
    return pl.pallas_call(
        mix_kernel,
        grid=(n,),
        out_shape=(low, jax.ShapeDtypeStruct((rows, width), F32), low),
        in_specs=[
            whole,
            whole,
            pl.BlockSpec((cols, width), lambda j: (j, 0)),
            gain,
            gain,
        ],
        out_specs=(whole, whole, whole),
        compiler_params=pltpu.CompilerParams(vmem_limit_bytes=VMEM_LIMIT),
        cost_estimate=pl.CostEstimate(
            flops=2 * rows * width * width,
            bytes_accessed=2 * width * width + 12 * rows * width,
            transcendentals=0,
        ),
        name="mix_pass",
    )(attended, x, w_out, gain_mix[None], gain_ffn[None])


def branch_kernel(gbr_ref, att_ref, w_ref, gm_ref, gatt_ref, ggm_ref, total):
    j = pl.program_id(0)
    rows = att_ref.shape[0]
    cols = w_ref.shape[0]
    here = pl.ds(pl.multiple_of(j * cols, cols), cols)
    term = nn(gbr_ref[:, here], w_ref[...])

    @pl.when(j == 0)
    def _():
        total[...] = term

    @pl.when(j > 0)
    def _():
        total[...] = total[...] + term

    @pl.when(j == pl.num_programs(0) - 1)
    def _():
        ggm_ref[...] = jnp.zeros_like(ggm_ref)

        @pl.loop(0, rows // STEP)
        def _(r):
            at = pl.ds(pl.multiple_of(r * STEP, STEP), STEP)
            normal, scale = norm_parts(att_ref[at].astype(F32))
            part, gain_part = norm_back(total[at], normal, scale, gm_ref[...])
            ggm_ref[...] += gain_part[None]
            gatt_ref[at] = part.astype(BF16)


def branch_pass(grad_branch, attended, w_out, gain_mix):
    rows, width = grad_branch.shape
    cols = 2 * TILE
    n = width // cols
    whole = pl.BlockSpec((rows, width), lambda j: (0, 0))
    gain = pl.BlockSpec((1, width), lambda j: (0, 0))
    return pl.pallas_call(
        branch_kernel,
        grid=(n,),
        out_shape=(
            jax.ShapeDtypeStruct((rows, width), BF16),
            jax.ShapeDtypeStruct((1, width), F32),
        ),
        in_specs=[whole, whole, pl.BlockSpec((cols, width), lambda j: (j, 0)), gain],
        out_specs=(whole, gain),
        scratch_shapes=[pltpu.VMEM((rows, width), F32)],
        compiler_params=pltpu.CompilerParams(vmem_limit_bytes=VMEM_LIMIT),
        name="branch_pass",
    )(grad_branch, attended, w_out, gain_mix[None])


def ffn_back_kernel(
    n, gu_ref, wu_ref, hid_ref, wd_ref, all_ref, mid_ref, cot_ref, gf_ref,
    po_ref, gd_ref, gmid_ref, gbr_ref, ggf_ref,
    gu, hid, every, own, far, twin_in, held, made, made_grad,
    local_sem, made_sem, grad_sem, send_sem, recv_sem,
):
    me, twin, near_x, near_y, across = places()
    rows, width = mid_ref.shape
    half = rows // 2
    low, high = pl.ds(0, half), pl.ds(half, half)
    mine = (across, near_x, near_y, me)

    def cut(i, size=rows):
        return pl.ds(pl.multiple_of(i * size, size), size)

    load_gu = pltpu.make_async_copy(gu_ref, gu, local_sem.at[0])
    load_hid = pltpu.make_async_copy(hid_ref, hid, local_sem.at[1])
    load_all = pltpu.make_async_copy(all_ref, every, local_sem.at[2])
    for load in (load_gu, load_hid, load_all):
        load.start()
    meet((me + twin, near_x, near_y))
    load_gu.wait()

    def copy(k, src, dst, partner):
        return remote(src, dst, send_sem.at[k], recv_sem.at[k], partner)

    twins = [copy(i, far.at[i], twin_in.at[i], me + twin) for i in range(4)]
    sends = [
        copy(4, own.at[0, low], held.at[0], near_x),
        copy(5, own.at[0, high], held.at[1], near_y),
        copy(6, own.at[1, low], held.at[2], near_x),
        copy(7, own.at[2, high], held.at[3], near_y),
        copy(8, own.at[1, high], held.at[4], near_x),
        copy(9, own.at[2, low], held.at[5], near_y),
    ]

    def add(i, base, count, source):
        @pl.loop(0, count // STEP)
        def _(r):
            at = cut(r, STEP)
            to = pl.ds(pl.multiple_of(base + r * STEP, STEP), STEP)
            own[i, to] = (own[i, to].astype(F32) + source[at].astype(F32)).astype(BF16)

    for i, block in enumerate(mine):
        far[i] = nn(gu[cut(block + twin)], wu_ref[...]).astype(BF16)
        twins[i].start()
        own[i] = nn(gu[cut(block)], wu_ref[...]).astype(BF16)
        if i < 3:
            twins[i].wait_recv()
            add(i, 0, rows, twin_in.at[i])
        if i == 0:
            sends[0].start()
            sends[1].start()
        elif i < 3:
            sends[i + 1].start()

    def store(i, slot):
        return pltpu.make_async_copy(made.at[slot], po_ref.at[cut(i)], made_sem.at[slot])

    def outputs(first, last):
        @pl.loop(first, last)
        def _(i):
            slot = lax.rem(i, 2)

            @pl.when(i >= 2)
            def _():
                store(i - 2, slot).wait()

            made[slot] = nt(hid[cut(i)], wd_ref[...]).astype(BF16)
            store(i, slot).start()

    def store_grad(i, slot):
        return pltpu.make_async_copy(
            made_grad.at[slot], gd_ref.at[i], grad_sem.at[slot]
        )

    def weight_grads(first, last):
        for i in range(first, last):
            slot = i % 2
            if i >= 2:
                store_grad(i - 2, slot).wait()
            made_grad[slot] = tn(
                every[:, i * rows : (i + 1) * rows], hid[...]
            ).astype(BF16)
            store_grad(i, slot).start()

    load_hid.wait()
    load_all.wait()
    weight_grads(0, n // 2)
    sends[1].wait_recv()
    add(1, half, half, held.at[1])
    sends[4].start()
    sends[0].wait_recv()
    add(2, 0, half, held.at[0])
    sends[5].start()
    weight_grads(n // 2, n)
    outputs(0, n)
    twins[3].wait_recv()
    for k in (2, 3, 4, 5):
        sends[k].wait_recv()
    ggf_ref[...] = jnp.zeros_like(ggf_ref)
    for base, one, two in ((0, 2, 5), (half, 3, 4)):

        @pl.loop(0, half // STEP)
        def _(r):
            at = cut(r, STEP)
            to = pl.ds(pl.multiple_of(base + r * STEP, STEP), STEP)
            value = (
                own[3, to].astype(F32)
                + twin_in[3, to].astype(F32)
                + held[one, at].astype(F32)
                + held[two, at].astype(F32)
            )
            normal, scale = norm_parts(mid_ref[to])
            part, gain_part = norm_back(value, normal, scale, gf_ref[...])
            ggf_ref[...] = ggf_ref[...] + gain_part[None]
            grad = cot_ref[to].astype(F32) + part
            gmid_ref[to] = grad
            gbr_ref[to] = grad.astype(BF16)

    for i in (n - 2, n - 1):
        store(i, i % 2).wait()
        store_grad(i, i % 2).wait()
    for send in twins + sends:
        send.wait_send()


def ffn_back(grad_upper, w_up, hidden, w_down, cot_full, middle, cot, gain, collective_id):
    n = lax.axis_size("seq")
    rows, width = middle.shape
    feats = w_up.shape[0]
    if n != 8:
        normal, scale = norm_parts(middle)
        value = scatter_seq(nn(grad_upper, w_up).astype(BF16))
        part, gain_part = norm_back(value, normal, scale, gain)
        grad = cot.astype(F32) + part
        down = tn(cot_full, hidden).astype(BF16).reshape(n, rows, feats)
        outputs = nt(hidden, w_down).astype(BF16)
        return outputs, down, grad, grad.astype(BF16), gain_part[None]
    dma = pltpu.SemaphoreType.DMA
    block = pltpu.VMEM((4, rows, width), BF16)
    return pl.pallas_call(
        functools.partial(ffn_back_kernel, n),
        out_shape=(
            jax.ShapeDtypeStruct((n * rows, width), BF16),
            jax.ShapeDtypeStruct((n, rows, feats), BF16),
            jax.ShapeDtypeStruct((rows, width), F32),
            jax.ShapeDtypeStruct((rows, width), BF16),
            jax.ShapeDtypeStruct((1, width), F32),
        ),
        in_specs=[ANY, INSIDE, ANY, INSIDE, ANY, INSIDE, INSIDE, INSIDE],
        out_specs=(ANY, ANY, INSIDE, INSIDE, INSIDE),
        scratch_shapes=[
            pltpu.VMEM((n * rows, feats), BF16),
            pltpu.VMEM((n * rows, feats), BF16),
            pltpu.VMEM((n * rows, width), BF16),
            block,
            block,
            block,
            pltpu.VMEM((6, rows // 2, width), BF16),
            pltpu.VMEM((2, rows, width), BF16),
            pltpu.VMEM((2, rows, feats), BF16),
            dma((3,)),
            dma((2,)),
            dma((2,)),
            dma((10,)),
            dma((10,)),
        ],
        compiler_params=pltpu.CompilerParams(
            collective_id=collective_id, has_side_effects=True, vmem_limit_bytes=VMEM_LIMIT
        ),
        name="ffn_back",
    )(grad_upper, w_up, hidden, w_down, cot_full, middle, cot, gain[None])


CHUNK = 64


def finish_kernel(
    n, depth, gq_ref, gd_ref, pw_ref, pn_ref, po_ref, x_ref, grad_ref, mid_ref, ga_ref, gm_ref, gf_ref, gh_ref,
    oq_ref, od_ref, ow_ref, gi_ref, out_ref, sums_ref,
    own, twin_in, held, zown, zin, stage, gain_here, gain_row, gain_pack, gain_line,
    local_sem, load_sem, stage_sem, send_sem, recv_sem, keep_sem,
    up_send, up_recv, down_send, down_recv, home_send, home_recv, gain_send, gain_recv,
):
    me, twin, near_x, near_y, across = places()
    z = lax.axis_index("batch")
    rows, width = pn_ref.shape[1:]
    half = rows // 2
    low, high = pl.ds(0, half), pl.ds(half, half)
    mine = (across, near_x, near_y, me)
    _, chunk, cols = zown.shape
    across_width = width // cols
    per_part = (gq_ref.shape[1] // chunk) * across_width
    turned = gq_ref.shape[0] * per_part
    per_source = gd_ref.shape[1] // chunk
    outer = turned + gd_ref.shape[0] * per_source
    chunks = zown.shape[0]
    per_side = chunks // 2

    def cut(i, size):
        return pl.ds(pl.multiple_of(i * size, size), size)

    def wide(i):
        return cut(i // across_width, chunk), cut(lax.rem(i, across_width), cols)

    line_loads = []
    for g in range(turned):
        source = gq_ref.at[(g // per_part, *wide(g % per_part))]
        line_loads.append(pltpu.make_async_copy(source, zown.at[g], load_sem.at[g]))
    for g in range(turned, outer):
        source = gd_ref.at[
            (g - turned) // per_source, cut((g - turned) % per_source, chunk)
        ]
        line_loads.append(pltpu.make_async_copy(source, zown.at[g], load_sem.at[g]))
    for load in line_loads:
        load.start()
    partials = (pw_ref, pn_ref, po_ref)
    loads = [
        [
            pltpu.make_async_copy(p.at[block], own.at[m, i], local_sem.at[4 * m + i])
            for i, block in enumerate(mine)
        ]
        for m, p in enumerate(partials)
    ]
    for part in loads:
        for load in part:
            load.start()
    meet_all(n, depth)

    def copy(m, k, src, dst, partner):
        return remote(src, dst, send_sem.at[m, k], recv_sem.at[m, k], partner)

    twins = [
        [
            copy(m, i, p.at[block + twin], twin_in.at[m, i], me + twin)
            for i, block in enumerate(mine)
        ]
        for m, p in enumerate(partials)
    ]
    sends = [
        [
            copy(m, 4, own.at[m, 0, low], held.at[m, 0], near_x),
            copy(m, 5, own.at[m, 0, high], held.at[m, 1], near_y),
            copy(m, 6, own.at[m, 1, low], held.at[m, 2], near_x),
            copy(m, 7, own.at[m, 2, high], held.at[m, 3], near_y),
            copy(m, 8, own.at[m, 1, high], held.at[m, 4], near_x),
            copy(m, 9, own.at[m, 2, low], held.at[m, 5], near_y),
        ]
        for m in range(3)
    ]
    for part in twins:
        for send in part:
            send.start()

    def add_twin(m, i):
        loads[m][i].wait()
        twins[m][i].wait_recv()

        @pl.loop(0, rows // STEP)
        def _(r):
            at = cut(r, STEP)
            own[m, i, at] = (
                own[m, i, at].astype(F32) + twin_in[m, i, at].astype(F32)
            ).astype(BF16)

    def add_held(m, i, base, slot):
        @pl.loop(0, half // STEP)
        def _(r):
            at = cut(r, STEP)
            to = pl.ds(pl.multiple_of(base + r * STEP, STEP), STEP)
            own[m, i, to] = (
                own[m, i, to].astype(F32) + held[m, slot, at].astype(F32)
            ).astype(BF16)

    def first(m):
        add_twin(m, 0)
        sends[m][0].start()
        sends[m][1].start()
        add_twin(m, 1)
        sends[m][2].start()
        add_twin(m, 2)
        sends[m][3].start()

    def second(m):
        sends[m][1].wait_recv()
        add_held(m, 1, half, 1)
        sends[m][4].start()
        sends[m][0].wait_recv()
        add_held(m, 2, 0, 0)
        sends[m][5].start()

    def last(m, store):
        loads[m][3].wait()
        twins[m][3].wait_recv()
        for k in (2, 3, 4, 5):
            sends[m][k].wait_recv()
        for base, one, two in ((0, 2, 5), (half, 3, 4)):

            @pl.loop(0, half // STEP)
            def _(r):
                at = cut(r, STEP)
                place = base + r * STEP
                to = pl.ds(pl.multiple_of(place, STEP), STEP)
                store(
                    place,
                    to,
                    own[m, 3, to].astype(F32)
                    + twin_in[m, 3, to].astype(F32)
                    + held[m, one, at].astype(F32)
                    + held[m, two, at].astype(F32),
                )

    def store_line(place, to, value):
        value = value.astype(BF16)
        for side in range(across_width):
            zown[
                outer + (place // chunk) * across_width + side,
                pl.ds(pl.multiple_of(lax.rem(place, chunk), STEP), STEP),
            ] = value[:, side * cols : (side + 1) * cols]

    def store_inputs(place, to, value):
        normal, scale = norm_parts(x_ref[to].astype(F32))
        part, gain_part = norm_back(value, normal, scale, ga_ref[...])
        gi_ref[to] = grad_ref[to] + part
        gain_here[0:1] = gain_here[0:1] + gain_part[None]

    def store_outputs(place, to, value):
        out_ref[to] = (mid_ref[to] + value).astype(BF16)

    def home(part):
        block = part * n + me
        return block // 3, lax.rem(block, 3)

    def deliver_far(g):
        target, slot = home(g // per_part)
        piece = lax.rem(g, per_part)
        return remote(
            zin.at[g],
            oq_ref.at[(slot, *wide(piece))],
            home_send.at[g],
            home_recv.at[slot, piece],
            target,
        )

    def deliver_near(g):
        _, slot = home(g // per_part)
        return pltpu.make_async_copy(
            zin.at[g], oq_ref.at[(slot, *wide(lax.rem(g, per_part)))], keep_sem.at[g]
        )

    def widen(g):
        @pl.loop(0, chunk // STEP)
        def _(r):
            at = cut(r, STEP)
            stage[at] = zin[g, at].astype(F32)

    def deliver(g):
        target, _ = home(g // per_part)

        @pl.when((g < turned) & (target != me))
        def _():
            deliver_far(g).start()

        @pl.when((g < turned) & (target == me))
        def _():
            deliver_near(g).start()

        @pl.when((g >= turned) & (g < outer))
        def _():
            widen(g)
            at = g - turned
            place = cut(lax.rem(at, per_source), chunk), cut(at // per_source, cols)
            store = pltpu.make_async_copy(stage, od_ref.at[place], stage_sem)
            store.start()
            store.wait()

        @pl.when(g >= outer)
        def _():
            widen(g)
            store = pltpu.make_async_copy(
                stage, ow_ref.at[wide(g - outer)], stage_sem
            )
            store.start()
            store.wait()

    def delivered(g):
        target, _ = home(g // per_part)

        @pl.when(target != me)
        def _():
            deliver_far(g).wait_send()

        @pl.when(target == me)
        def _():
            deliver_near(g).wait()

    def go_up(g, ahead):
        return line_remote(zown.at[g], zin.at[g], up_send.at[g], up_recv.at[g], ahead)

    def go_down(g, behind):
        return line_remote(
            zin.at[g], zin.at[g], down_send.at[g], down_recv.at[g], behind
        )

    def ranks(side):
        if side == 0:
            return z, z + 1, z - 1
        return depth - 1 - z, z - 1, z + 1

    def add_line(g, target):
        @pl.loop(0, chunk // STEP)
        def _(r):
            at = cut(r, STEP)
            target[g, at] = (zown[g, at].astype(F32) + zin[g, at].astype(F32)).astype(
                BF16
            )

    lead = 1
    far = 2 * (depth - 1)
    steps = per_side + 2 * far

    def line_enter(c):
        for side in (0, 1):
            rank, ahead, _ = ranks(side)

            @pl.when(rank == 0)
            def _():
                go_up(2 * c + side, ahead).start()

    def line_step(t):
        @pl.when(t + lead < per_side)
        def _():
            line_enter(t + lead)

        back = []
        for side in (0, 1):
            rank, ahead, behind = ranks(side)
            c_back = t - 2 * far + 2 * rank
            g_back = 2 * c_back + side
            there = (c_back >= 0) & (c_back < per_side) & (rank < depth - 1)
            back.append((there, g_back))

            @pl.when(there)
            def _():
                go_down(g_back, ahead).wait_recv()

            @pl.when(there & (rank > 0))
            def _():
                go_down(g_back, behind).start()

        for side in (0, 1):
            rank, ahead, behind = ranks(side)
            c = t - 2 * rank
            g = 2 * c + side
            there = (c >= 0) & (c < per_side)

            @pl.when(there & (rank > 0) & (rank < depth - 1))
            def _():
                go_up(g, behind).wait_recv()
                add_line(g, zown)
                go_up(g, ahead).start()

            @pl.when(there & (rank == depth - 1))
            def _():
                go_up(g, behind).wait_recv()
                add_line(g, zin)
                go_down(g, behind).start()
                deliver(g)

        for there, g_back in back:

            @pl.when(there)
            def _():
                deliver(g_back)

    def line_steps(first_step, last_step):
        @pl.loop(first_step, last_step)
        def _(t):
            line_step(t)

    gain_here[...] = jnp.zeros_like(gain_here)
    for load in line_loads[:turned]:
        load.wait()
    for c in range(lead):
        line_enter(c)
    line_steps(0, 3)
    first(0)
    for load in line_loads[turned:]:
        load.wait()
    line_steps(3, 10)
    second(0)
    line_steps(10, 11)
    first(1)
    line_steps(11, 20)
    last(0, store_line)
    line_steps(20, 22)
    second(1)
    line_steps(22, 23)
    first(2)
    line_steps(23, 29)
    last(1, store_inputs)

    gain_here[1:2] = gm_ref[...]
    gain_here[2:3] = gf_ref[...]
    gain_here[3:4, 0 : gh_ref.shape[1]] = gh_ref[...]
    gain_row[me] = gain_here[...]
    rounds = [
        remote(
            gain_here,
            gain_row.at[me],
            gain_send.at[0, k],
            gain_recv.at[0, k],
            lax.rem(me + k, n),
        )
        for k in range(1, n)
    ]
    for send in rounds:
        send.start()
    line_steps(29, 33)
    second(2)
    line_steps(33, 41)
    last(2, store_outputs)
    line_steps(41, 42)
    for send in rounds:
        send.wait()
    total = gain_row[0]
    for d in range(1, n):
        total = total + gain_row[d]
    gain_pack[0:8] = total
    for d in range(n):
        gain_pack[8 + d : 9 + d] = gain_row[d, 3:4]
    gain_line[z] = gain_pack[...]
    rounds = [
        line_remote(
            gain_pack,
            gain_line.at[z],
            gain_send.at[1, k],
            gain_recv.at[1, k],
            lax.rem(z + k, depth),
        )
        for k in range(1, depth)
    ]
    for send in rounds:
        send.start()
    line_steps(42, steps)
    for send in rounds:
        send.wait()
    total = gain_line[0]
    for d in range(1, depth):
        total = total + gain_line[d]
    sums_ref[...] = total

    for m in range(3):
        for send in twins[m] + sends[m]:
            send.wait_send()
    for g in range(chunks):
        rank, ahead, behind = ranks(g % 2)

        @pl.when(rank < depth - 1)
        def _():
            go_up(g, ahead).wait_send()

        @pl.when(rank > 0)
        def _():
            go_down(g, behind).wait_send()

    for g in range(turned):
        delivered(g)
    for slot in range(3):
        block = 3 * me + slot
        source = lax.rem(block, n)

        @pl.when(source != me)
        def _():
            for piece in range(per_part):
                remote(
                    zin.at[0],
                    oq_ref.at[(slot, *wide(piece))],
                    home_send.at[0],
                    home_recv.at[slot, piece],
                    source,
                ).wait_recv()


def finish(
    grad_qkv, grad_down, part_out, part_normed, part_outputs, x, grad_middle, middle, gain, gains, collective_id
):
    n, depth = lax.axis_size("seq"), lax.axis_size("batch")
    rows, width = part_out.shape[0] // n, part_out.shape[1]
    cols = grad_qkv.shape[1]
    sources, _, feats = grad_down.shape
    if n != 8 or depth != 4:
        me = lax.axis_index("seq")
        blocks = lax.psum(grad_qkv, "batch")
        back = [
            lax.ppermute(
                give_part(blocks, me, n, j),
                "seq",
                [((3 * d + j) % n, d) for d in range(n)],
            )
            for j in range(3)
        ]
        w_out = lax.psum(scatter_seq(part_out).astype(BF16), "batch")
        normal, scale = norm_parts(x.astype(F32))
        part, gain_part = norm_back(scatter_seq(part_normed), normal, scale, gain)
        shared = [lax.psum(g, ("batch", "seq")) for g in (gain_part, gains[0][0], gains[1][0])]
        hidden = lax.all_gather(lax.psum(gains[2][0], "batch"), "seq", axis=0, tiled=True)
        down = lax.psum(grad_down, "batch")
        return (
            jnp.concatenate(back, axis=0),
            jnp.swapaxes(down, 0, 1).reshape(rows, sources * feats).astype(F32),
            w_out.astype(F32),
            grad_middle + part,
            (middle + scatter_seq(part_outputs)).astype(BF16),
            (*shared, hidden),
        )
    chunks = (
        3 * cols * width + rows * width + sources * rows * feats
    ) // (CHUNK * feats)
    dma = pltpu.SemaphoreType.DMA
    line = pltpu.VMEM((chunks, CHUNK, feats), BF16)
    w_qkv, w_down, w_out, grad_inputs, outputs, sums = pl.pallas_call(
        functools.partial(finish_kernel, n, depth),
        out_shape=(
            jax.ShapeDtypeStruct((3, cols, width), BF16),
            jax.ShapeDtypeStruct((rows, sources * feats), F32),
            jax.ShapeDtypeStruct((rows, width), F32),
            jax.ShapeDtypeStruct((rows, width), F32),
            jax.ShapeDtypeStruct((rows, width), BF16),
            jax.ShapeDtypeStruct((16, width), F32),
        ),
        in_specs=[ANY] * 5 + [INSIDE] * 7,
        out_specs=(ANY, ANY, ANY, INSIDE, INSIDE, INSIDE),
        scratch_shapes=[
            pltpu.VMEM((3, 4, rows, width), BF16),
            pltpu.VMEM((3, 4, rows, width), BF16),
            pltpu.VMEM((3, 6, rows // 2, width), BF16),
            line,
            line,
            pltpu.VMEM((CHUNK, feats), F32),
            pltpu.VMEM((8, width), F32),
            pltpu.VMEM((n, 8, width), F32),
            pltpu.VMEM((16, width), F32),
            pltpu.VMEM((depth, 16, width), F32),
            dma((12,)),
            dma((chunks,)),
            dma,
            dma((3, 10)),
            dma((3, 10)),
            dma((chunks,)),
            dma((chunks,)),
            dma((chunks,)),
            dma((chunks,)),
            dma((chunks,)),
            dma((chunks,)),
            dma((3, cols * width // (CHUNK * feats))),
            dma((2, n)),
            dma((2, n)),
        ],
        compiler_params=pltpu.CompilerParams(
            collective_id=collective_id,
            has_side_effects=True,
            vmem_limit_bytes=VMEM_LIMIT,
        ),
        name="finish",
    )(
        grad_qkv,
        grad_down,
        *[p.reshape(n, rows, width) for p in (part_out, part_normed, part_outputs)],
        x,
        grad_middle,
        middle,
        gain[None],
        *gains,
    )
    return (
        w_qkv.reshape(3 * cols, width),
        w_down,
        w_out,
        grad_inputs,
        outputs,
        (sums[0], sums[1], sums[2], sums[8:, :feats].reshape(-1)),
    )


def widen_kernel(*refs):
    half = len(refs) // 2
    for source, target in zip(refs[:half], refs[half:], strict=True):
        target[...] = source[...].astype(F32)


def widen(arrays):
    steps = 8
    specs = [pl.BlockSpec((x.shape[0] // steps, x.shape[1]), lambda i: (i, 0)) for x in arrays]
    return pl.pallas_call(
        widen_kernel,
        grid=(steps,),
        out_shape=[jax.ShapeDtypeStruct(x.shape, F32) for x in arrays],
        in_specs=specs,
        out_specs=specs,
        compiler_params=pltpu.CompilerParams(vmem_limit_bytes=VMEM_LIMIT),
        name="widen",
    )(*arrays)


def body(
    inputs,
    segment_ids,
    w_qkv,
    w_out,
    w_up,
    w_down,
    gain_attn,
    gain_mix,
    gain_ffn,
    gain_hidden,
    cotangent,
):
    _, local, width = inputs.shape
    n, depth = lax.axis_size("seq"), lax.axis_size("batch")
    me = lax.axis_index("seq")
    length = local * n
    feats = w_up.shape[0]
    x_low = inputs[0]
    cot = cotangent[0]
    segment = segment_ids[0]

    w_out_full = lax.all_gather(w_out, "seq", axis=0, tiled=True)
    before = [jnp.sum((segment < d).astype(jnp.int32)) for d in range(1, DOCS)]
    start = jnp.zeros_like(segment)
    for d in range(1, DOCS):
        start = jnp.where(segment == d, before[d - 1], start)
    positions = jnp.arange(length, dtype=jnp.int32) - start
    first = start[::TILE] // TILE
    start_row = start[None, :]

    normed_full, w_heads, w_down_cols, tables = start_exchange(
        x_low, gain_attn, w_qkv, w_down, positions.astype(F32), 1
    )
    cot_late, _ = lax.optimization_barrier((cot, w_heads))
    cot_full = lax.all_gather(cot_late, "seq", axis=0, tiled=True)

    q, k, v, kt, vt = project_qkv(normed_full, w_heads, tables)
    attended_heads, lse = attend(first, start_row, q, k, vt)
    attended = heads_to_tokens(attended_heads, 2)
    mix_in, middle, ffn_in = mix_pass(attended, x_low, w_out_full, gain_mix, gain_ffn)
    gain_here = lax.dynamic_slice_in_dim(gain_hidden, me * feats, feats, 0)[None, :]
    ffn_full, hidden, grad_upper, grad_gain_here = ffn_pass(
        ffn_in, w_up, cot_full, w_down_cols, gain_here, 3
    )

    grad_w_up = tn(grad_upper, ffn_full).astype(BF16)
    grad_upper, grad_w_up = lax.optimization_barrier((grad_upper, grad_w_up))
    grad_w_up = lax.psum(grad_w_up, "batch")
    part_outputs, grad_w_down, grad_middle, grad_branch, grad_gain_ffn = ffn_back(
        grad_upper, w_up, hidden, w_down_cols, cot_full, middle, cot, gain_ffn, 4
    )
    grad_att, grad_gain_mix = branch_pass(grad_branch, attended, w_out_full, gain_mix)
    grad_heads = tokens_to_heads(grad_att, 5)
    grad_w_down, grad_heads = lax.optimization_barrier((grad_w_down, grad_heads))
    grad_w_down = lax.all_to_all(grad_w_down, "seq", split_axis=0, concat_axis=0, tiled=True)
    grads = attend_back(
        first, start_row, q, k, kt, v, attended_heads, lse, grad_heads, tables
    )
    grad_w_qkv = tn(grads, normed_full).astype(BF16).reshape(3, -1, width)
    grad_w_qkv, grad_w_up = lax.optimization_barrier((grad_w_qkv, grad_w_up))
    grad_w_qkv, grad_w_down, grad_w_out, grad_inputs, outputs, gains = finish(
        grad_w_qkv,
        grad_w_down,
        tn(grad_branch, mix_in).astype(BF16),
        nn(grads, w_heads).astype(BF16),
        part_outputs,
        x_low,
        grad_middle,
        middle,
        gain_attn,
        (grad_gain_mix, grad_gain_ffn, grad_gain_here),
        6,
    )
    grad_w_qkv, grad_w_up = widen([grad_w_qkv, grad_w_up])
    return (
        outputs[None],
        grad_inputs[None],
        grad_w_qkv,
        grad_w_out,
        grad_w_up,
        grad_w_down,
        *gains,
    )


def pick_part(turned, me, n, part):
    chosen = turned[0]
    home = part * n + me
    for j in (1, 2):
        chosen = jnp.where(lax.rem(home, 3) == j, turned[j], chosen)
    return chosen


def give_part(blocks, me, n, j):
    chosen = blocks[0]
    for part in (1, 2):
        chosen = jnp.where(lax.rem(part * n + me, 3) == j, blocks[part], chosen)
    return chosen


def solution(mesh):
    in_specs = (
        P("batch", "seq", None),
        P("batch", None),
        P("seq", None),
        P("seq", None),
        P("seq", None),
        P("seq", None),
        P(),
        P(),
        P(),
        P(),
        P("batch", "seq", None),
    )
    out_specs = (
        P("batch", "seq", None),
        P("batch", "seq", None),
        P("seq", None),
        P("seq", None),
        P("seq", None),
        P("seq", None),
        P(),
        P(),
        P(),
        P(),
    )
    return jax.shard_map(body, mesh=mesh, in_specs=in_specs, out_specs=out_specs, check_vma=False)
```
